32 devices in a mesh: expert: 8 (over y, x, core), hidden: 4 (over z).
Axes of the slice: x: 2, y: 2, z: 4, core: 2. Of those that a mesh axis runs over, the one named last changes fastest.
Arguments:
- x_in: bfloat16 [2, 8, 1024, 1024], P(None, 'expert', 'hidden'), may hold values from -6 to 6
- cotangent: bfloat16 [2, 8, 1024, 1024], P(None, 'expert', 'hidden'), may hold values from -6 to 6
- segment_ids: int32 [2, 8, 1024], P(None, 'expert'), may hold values from -1 to 8, as said below
- routes: int32 [2, 8, 1024, 2], P(None, 'expert', 'hidden'), may hold values from 0 to 15, all different within a row; in each aligned block of 256 rows (0 to 255, 256 to 511, ..., all dimensions but the last counted through in order) at most 40 rows name the same one
- qkv_weight: bfloat16 [3, 1024, 1024], P(None, None, 'hidden'), may hold values from -0.1875 to 0.1875
- out_weight: bfloat16 [1024, 1024], P('hidden'), may hold values from -0.75 to 0.75
- bias_table: bfloat16 [32, 16], P(None, 'hidden'), may hold values from -4 to 4
- attn_gain: bfloat16 [1024], replicated, may hold values from 0.5 to 1.5
- moe_gain: bfloat16 [1024], replicated, may hold values from 0.5 to 1.5
- router_weight: bfloat16 [1024, 16], replicated, may hold values from -0.375 to 0.375
- gate_weight: bfloat16 [16, 1024, 2816], P('expert', None, 'hidden'), may hold values from -0.1875 to 0.1875
- up_weight: bfloat16 [16, 1024, 2816], P('expert', None, 'hidden'), may hold values from -0.1875 to 0.1875
- down_weight: bfloat16 [16, 2816, 1024], P('expert', 'hidden'), may hold values from -0.21875 to 0.21875
Outputs:
- block_out: bfloat16 [2, 8, 1024, 1024], P(None, 'expert', 'hidden')
- x_grad: bfloat16 [2, 8, 1024, 1024], P(None, 'expert', 'hidden')
- qkv_grad: float32 [3, 1024, 1024], P(None, None, 'hidden')
- out_grad: float32 [1024, 1024], P('hidden')
- bias_grad: float32 [32, 16], P(None, 'hidden')
- attn_gain_grad: float32 [1024], replicated
- moe_gain_grad: float32 [1024], replicated
- router_grad: float32 [1024, 16], replicated
- gate_grad: float32 [16, 1024, 2816], P('expert', None, 'hidden')
- up_grad: float32 [16, 1024, 2816], P('expert', None, 'hidden')
- down_grad: float32 [16, 2816, 1024], P('expert', 'hidden')
The draws below stay inside these ranges and needn't reach their ends.
Inputs may be any that keep to these rules, and one draw needn't show every extreme that they name: `segment_ids`: within each row, slots are numbered by item 0, 1, 2, ... in order; the first item of every row has 512 slots, every item 64 to 512; slots after the last whole item are -1. In the first row of the first micro-batch every item after the first has 64 slots. Item numbers serve only for comparison. `routes`: the two experts of a slot differ. In each aligned block of 256 slots (the slots of one row held by one index of hidden), no expert is named by more than 40 slots, a bound that some block reaches.
All inputs are finite; a program needn't handle non-finite values.
Results may differ from the reference program's by a relative error of at most 0.023.
Values may be sent and summed in bfloat16 or wider, within the bound.
A program may use at most 320 MiB of HBM per device.

```python
import math
import jax
import jax.numpy as jnp
import numpy as np
from jax import lax

D = 1024
HEADS = 16
HDIM = 64
FF = 2816
BUCKETS = 32
TOPK = 2
SLOTS = 1024
MB = 2
EXPERTS = 16
NROWS = 8
TOKB = 256
CAP = 40
ITEM_MAX = 512
ITEM_MIN = 64
N_HIDDEN = 4


def draw_segment_ids(key, part):
    item_total = SLOTS // ITEM_MIN
    lengths = jax.random.randint(key, (MB, NROWS, item_total - 1), ITEM_MIN, ITEM_MAX + 1).astype(jnp.int32)
    batch_place = jnp.arange(MB, dtype=jnp.int32)[:, None, None]
    row_place = jnp.arange(NROWS, dtype=jnp.int32)[None, :, None]
    filled_row = (batch_place == 0) & (row_place == 0)
    lengths = jnp.where(filled_row, ITEM_MIN, lengths).astype(jnp.int32)
    first_item = jnp.full((MB, NROWS, 1), ITEM_MAX, jnp.int32)
    item_ends = jnp.cumsum(jnp.concatenate([first_item, lengths], axis=-1), axis=-1)
    slot_place = jnp.arange(SLOTS, dtype=jnp.int32)
    numbered = jnp.sum((item_ends[..., None, :] <= slot_place[:, None]).astype(jnp.int32), axis=-1)
    last_end = jnp.max(jnp.where(item_ends <= SLOTS, item_ends, 0), axis=-1)
    return jnp.where(slot_place < last_end[..., None], numbered, -1).astype(jnp.int32)


def shard_levels(own_key, shape, split, least, largest):
    level = 1.0
    for dim, parts in split:
        heights = jax.random.uniform(jax.random.fold_in(jax.random.fold_in(own_key, 6), dim), (parts,), jnp.float32, least / len(split), largest / len(split))
        level = level * jnp.repeat(jnp.exp(heights), shape[dim] // parts).reshape((-1,) + (1,) * (len(shape) - 1 - dim))
    return level


def deal_out(own_key, own, number, rows, count, top, reach, lean):
    sequence = jax.random.permutation(own_key, count)
    crowded, common = portions_of(count, rows * top, reach, lean, True), portions_of(count, rows * top, reach, lean, False)
    places = jnp.arange(count)

    def named(tallies, rotation):
        used = int((tallies > 0).sum())
        fixed = max(1, used // 4)
        passed = fixed + (places - fixed + rotation * (used - fixed)) % max(1, count - fixed)
        return jnp.zeros((count,), jnp.int32).at[sequence[jnp.where(places < fixed, places, passed)]].set(jnp.asarray(tallies, jnp.int32))

    tallies = jnp.where(number % 4 == 0, named(crowded, number // 4), named(common, number - number // 4 - 1))
    mixed = jax.random.permutation(jax.random.fold_in(own, 3), count)
    source_of, sink = mixed[0:count // 2 * 2:2], mixed[1:count // 2 * 2:2]
    margin = jnp.minimum(tallies[source_of] - 1, reach - tallies[sink]) // 2
    margin = jnp.where((source_of == sequence[0]) | (sink == sequence[0]) | (tallies[sink] == 0), 0, jnp.maximum(margin, 0))
    passed = jax.random.randint(jax.random.fold_in(own, 4), (count // 2,), 0, 1 << 20) % (margin + 1)
    tallies = tallies.at[source_of].add(-passed).at[sink].add(passed)
    labels = jnp.searchsorted(jnp.cumsum(tallies), jnp.arange(rows * top), side="right").astype(jnp.int32)
    table = labels.reshape(top, rows).T
    table = table[jax.random.permutation(jax.random.fold_in(own, 1), rows)]
    rotation = jax.random.randint(jax.random.fold_in(own, 2), (rows, 1), 0, top)
    return jnp.take_along_axis(table, (jnp.arange(top)[None, :] + rotation) % top, axis=1)


def portions_of(amount, total, bound, lean, full):
    weights = [(1 << 20) // math.isqrt(rank ** lean) + 1 for rank in range(1, amount + 1)]
    largest = bound if full else min(bound, max(-(-total // amount), total * weights[0] // sum(weights)))
    least = 1 if total - largest >= amount - 1 else 0
    holding, surplus = [largest] + [least] * (amount - 1), total - largest - least * (amount - 1)
    while surplus > 0:
        movable = [i for i in range(1, amount) if holding[i] < largest] or [i for i in range(1, amount) if holding[i] < bound]
        whole, budget = sum([weights[i] for i in movable]), surplus
        for i in movable:
            more = min(bound - holding[i], max(1, budget * weights[i] // whole), surplus)
            holding[i] = holding[i] + more
            surplus = surplus - more
    return np.array(holding)


def scatter_about(own_key, dims, scale, bound, split=(), held_as=jnp.bfloat16):
    loudness = shard_levels(own_key, dims, split, -0.22, 0.18) if split else 1.0
    result = jax.random.normal(own_key, dims, jnp.float32) * scale * loudness
    return jnp.minimum(jnp.maximum(result, -bound), bound).astype(held_as)


def setup_inputs(seed: int = 0) -> dict:
    keys = jax.random.split(jax.random.key(seed), 14)
    x_in = scatter_about(keys[0], (MB, NROWS, SLOTS, D), 1.0, 6.0, ((1, 8), (2, 4)))
    cotangent = scatter_about(keys[1], (MB, NROWS, SLOTS, D), 1.0, 6.0, ((1, 8), (2, 4)))
    segment_ids = draw_segment_ids(jax.random.fold_in(keys[13], 71), 0)
    routes_keys = jax.random.split(jax.random.fold_in(keys[3], 1), MB * NROWS * SLOTS // TOKB)
    routes_turns = jax.random.permutation(jax.random.fold_in(keys[3], 3), MB * NROWS * SLOTS // TOKB)
    routes = jax.vmap(lambda own, number: deal_out(jax.random.fold_in(keys[3], 2), own, number, TOKB, EXPERTS, TOPK, CAP, 1))(routes_keys, routes_turns).reshape((MB, NROWS, SLOTS, TOPK))
    qkv_weight = scatter_about(keys[4], (3, D, HEADS * HDIM), D ** -0.5, 0.1875, ((2, 4),))
    out_weight = scatter_about(keys[5], (HEADS * HDIM, D), (HEADS * HDIM // 16) ** -0.5, 0.75, ((0, 4),))
    bias_table = scatter_about(keys[6], (BUCKETS, HEADS), 1.0, 4.0, ((1, 4),))
    attn_gain = jnp.clip(1.0 + 0.1 * jax.random.normal(keys[7], (D,), jnp.float32), 0.5, 1.5).astype(jnp.bfloat16)
    moe_gain = jnp.clip(1.0 + 0.1 * jax.random.normal(keys[8], (D,), jnp.float32), 0.5, 1.5).astype(jnp.bfloat16)
    router_weight = scatter_about(keys[9], (D, EXPERTS), (D // 4) ** -0.5, 0.375)
    gate_weight = scatter_about(keys[10], (EXPERTS, D, FF), D ** -0.5, 0.1875, ((0, 8), (2, 4)))
    up_weight = scatter_about(keys[11], (EXPERTS, D, FF), D ** -0.5, 0.1875, ((0, 8), (2, 4)))
    down_weight = scatter_about(keys[12], (EXPERTS, FF, D), (FF // 4) ** -0.5, 0.21875, ((0, 8), (1, 4)))
    return {"x_in": x_in, "cotangent": cotangent, "segment_ids": segment_ids, "routes": routes, "qkv_weight": qkv_weight, "out_weight": out_weight, "bias_table": bias_table, "attn_gain": attn_gain, "moe_gain": moe_gain, "router_weight": router_weight, "gate_weight": gate_weight, "up_weight": up_weight, "down_weight": down_weight}


EPSILON = 1e-06
PRECISE = lax.Precision.HIGHEST
LIMITS = (12, 16, 23, 32, 46, 64, 91)
MASKED = -1000000000.0

@jax.custom_vjp
def low(v):
    return lax.optimization_barrier(v.astype(jnp.bfloat16)).astype(jnp.float32)

@jax.custom_vjp
def low_back(v):
    return v

def low_keep(v):
    return (low(v), None)

def low_pass(kept, grad):
    return (grad,)

def back_keep(v):
    return (v, None)

def back_low(kept, grad):
    return (low(grad),)
low.defvjp(low_keep, low_pass)
low_back.defvjp(back_keep, back_low)

def bucket_of(distance):
    magnitude = jnp.abs(distance)
    far_bucket = jnp.full(magnitude.shape, 8, jnp.int32)
    for threshold in LIMITS:
        far_bucket = far_bucket + (magnitude >= threshold).astype(jnp.int32)
    return jnp.where(magnitude < 8, magnitude, far_bucket) + 16 * (distance > 0).astype(jnp.int32)

def normed(values, gain):
    return values * lax.rsqrt(lax.optimization_barrier(jnp.mean(values * values, axis=-1, keepdims=True)) + EPSILON) * gain

def attend_row(row_in, seg_row, qkv_weight, out_weight, bias_table):
    projected = low_back(low(jnp.einsum('sd,tdf->tsf', row_in, qkv_weight, precision=PRECISE)))
    split_heads = projected.reshape(3, SLOTS, HEADS, HDIM).transpose(0, 2, 1, 3)
    query_heads, key_heads, value_heads = (split_heads[0], split_heads[1], split_heads[2])
    slot_place = jnp.arange(SLOTS, dtype=jnp.int32)
    bucket_index = bucket_of(slot_place[None, :] - slot_place[:, None])
    position_bias = jnp.take(bias_table.T, bucket_index, axis=1)
    scores = jnp.einsum('hqe,hke->hqk', query_heads, key_heads, precision=PRECISE) * HDIM ** (-0.5)
    scores = low_back(scores + position_bias)
    same_item = seg_row[:, None] == seg_row[None, :]
    probability = jax.nn.softmax(jnp.where(same_item[None], scores, MASKED), axis=-1)
    heads_out = jnp.einsum('hqk,hke->qhe', low(probability), value_heads, precision=PRECISE)
    heads_out = low_back(low(heads_out.reshape(SLOTS, HEADS * HDIM)))
    return low_back(jnp.dot(heads_out, out_weight, precision=PRECISE))

def slot_table(route_blocks, live_blocks):
    block_count = route_blocks.shape[0]
    chosen = (route_blocks[..., None] == jnp.arange(EXPERTS, dtype=jnp.int32)).astype(jnp.int32)
    chosen = chosen * live_blocks[:, :, None, None].astype(jnp.int32)
    chosen = chosen.reshape(block_count, TOKB * 2, EXPERTS)
    earlier = jnp.cumsum(chosen, axis=1) - chosen
    position = lax.optimization_barrier(jnp.sum(earlier * chosen, axis=-1)).reshape(block_count, TOKB, 2)
    block_index = jnp.arange(block_count, dtype=jnp.int32)[:, None, None]
    slot_index = route_blocks * (block_count * CAP) + block_index * CAP + position
    return jnp.where(live_blocks[:, :, None], slot_index, EXPERTS * block_count * CAP)

def forward(x_all, qkv_weight, out_weight, bias_table, attn_gain, moe_gain, router_weight, gate_weight, up_weight, down_weight, segment_ids, routes):
    block_count = NROWS * N_HIDDEN
    token_count = NROWS * SLOTS
    slot_total = EXPERTS * block_count * CAP

    def attend_pair(pair):
        return attend_row(pair[0], pair[1], qkv_weight, out_weight, bias_table)
    attend_saved = jax.checkpoint(attend_pair)
    results = []
    for micro_batch in range(MB):
        x_now = x_all[micro_batch]
        seg_now = segment_ids[micro_batch]
        normed_one = low(normed(x_now, attn_gain))
        attn_out = lax.map(attend_saved, (normed_one, seg_now))
        first_sum = x_now + attn_out
        normed_two = low(normed(first_sum, moe_gain))
        token_rows = normed_two.reshape(token_count, D)
        logits = low_back(jnp.dot(token_rows, router_weight, precision=PRECISE))
        router_probs = jax.nn.softmax(logits, axis=-1)
        route_now = routes[micro_batch].reshape(token_count, 2)
        live_now = seg_now.reshape(token_count) >= 0
        picked_probs = jnp.take_along_axis(router_probs, route_now, axis=1)
        gates = picked_probs / lax.optimization_barrier(jnp.sum(picked_probs, axis=1, keepdims=True)) * live_now[:, None]
        slot_index = slot_table(route_now.reshape(block_count, TOKB, 2), live_now.reshape(block_count, TOKB))
        slot_index = slot_index.reshape(token_count * 2)
        buffer_all = jnp.zeros((slot_total + 1, D), jnp.float32).at[slot_index].add(jnp.repeat(token_rows, 2, axis=0))
        expert_in = low_back(buffer_all[:slot_total].reshape(EXPERTS, block_count * CAP, D))
        gate_act = low_back(jnp.einsum('erd,edf->erf', expert_in, gate_weight, precision=PRECISE))
        up_act = low_back(jnp.einsum('erd,edf->erf', expert_in, up_weight, precision=PRECISE))
        hidden_act = low(jax.nn.gelu(gate_act, approximate=True) * up_act)
        expert_out = low_back(low(jnp.einsum('erf,efd->erd', hidden_act, down_weight, precision=PRECISE)))
        padded_out = jnp.concatenate([expert_out.reshape(slot_total, D), jnp.zeros((1, D), jnp.float32)], axis=0)
        picked_out = padded_out[slot_index].reshape(token_count, 2, D)
        mixed = lax.optimization_barrier(jnp.sum(gates[:, :, None] * picked_out, axis=1))
        results.append(first_sum + mixed.reshape(NROWS, SLOTS, D))
    return jnp.stack(results)

def reference(x_in, cotangent, segment_ids, routes, qkv_weight, out_weight, bias_table, attn_gain, moe_gain, router_weight, gate_weight, up_weight, down_weight):
    floats = tuple((item.astype(jnp.float32) for item in (x_in, qkv_weight, out_weight, bias_table, attn_gain, moe_gain, router_weight, gate_weight, up_weight, down_weight)))

    def run_block(*values):
        return forward(*values, segment_ids, routes)
    block_out, back_fn = jax.vjp(run_block, *floats)
    grads = back_fn(cotangent.astype(jnp.float32))
    return (block_out.astype(jnp.bfloat16), grads[0].astype(jnp.bfloat16), grads[1], grads[2], grads[3], grads[4], grads[5], grads[6], grads[7], grads[8], grads[9])
```

```python
import functools

import jax
import jax.numpy as jnp
from jax import lax
from jax.experimental import pallas as pl
from jax.experimental.pallas import tpu as pltpu
from jax.sharding import PartitionSpec as P

EPSILON = 1e-06
PRECISE = lax.Precision.HIGHEST
LIMITS = (12, 16, 23, 32, 46, 64, 91)
MASKED = -1000000000.0
FIRST_ITEM = 512
GELU_C = 0.7978845608028654
GELU_A = 0.044715
VMEM_LIMIT = 60 * 1024 * 1024
F32 = jnp.float32
BF16 = jnp.bfloat16


def mm(a, b):
    return lax.dot_general(a, b, (((1,), (0,)), ((), ())), preferred_element_type=F32)


def mm_nt(a, b):
    return lax.dot_general(a, b, (((1,), (1,)), ((), ())), preferred_element_type=F32)


def mm_tn(a, b):
    return lax.dot_general(a, b, (((0,), (0,)), ((), ())), preferred_element_type=F32)


def bucket_of(distance):
    magnitude = jnp.abs(distance)
    far_bucket = jnp.full(magnitude.shape, 8, jnp.int32)
    for threshold in LIMITS:
        far_bucket = far_bucket + (magnitude >= threshold).astype(jnp.int32)
    return jnp.where(magnitude < 8, magnitude, far_bucket) + 16 * (distance > 0).astype(jnp.int32)


def bucket_onehot(half, bucket_count):
    lane = jnp.arange(2 * half, dtype=jnp.int32)
    distance = jnp.where(lane < half, lane, lane - 2 * half)
    return (
        bucket_of(distance)[:, None] == jnp.arange(bucket_count, dtype=jnp.int32)[None, :]
    ).astype(F32)


def bias_kernel(line_ref, out_ref):
    half = out_ref.shape[2]
    line = jnp.broadcast_to(line_ref[0], (16, 2 * half))
    row = lax.broadcasted_iota(jnp.int32, (16, 2 * half), 0)
    base = jnp.zeros((16, 2 * half), F32)
    for r in range(16):
        base = jnp.where(row == r, pltpu.roll(line, r, 1) if r else line, base)

    def body(a, carry):
        start = pl.multiple_of(a * 16, 16)
        moved = pltpu.roll(base, start, 1)
        out_ref[0, pl.ds(start, 16), :] = moved[:, :half].astype(out_ref.dtype)
        return carry

    lax.fori_loop(0, half // 16, body, 0)


def position_bias(line, half):
    heads = line.shape[0]
    return pl.pallas_call(
        bias_kernel,
        grid=(heads,),
        out_shape=jax.ShapeDtypeStruct((heads, half, half), BF16),
        in_specs=[pl.BlockSpec((1, 1, 2 * half), lambda h: (h, 0, 0))],
        out_specs=pl.BlockSpec((1, half, half), lambda h: (h, 0, 0)),
        compiler_params=pltpu.CompilerParams(vmem_limit_bytes=VMEM_LIMIT),
        name="position_bias",
    )(line.reshape(heads, 1, 2 * half))


def attend_kernel(scale, tile, qkv_ref, bias_ref, seg_row_ref, seg_col_ref, prob_ref, out_ref):
    heads, half = bias_ref.shape[0], bias_ref.shape[1]
    size = out_ref.shape[1] // heads
    seg_row = seg_row_ref[...]
    for head in range(heads):
        cols = slice(head * size, (head + 1) * size)
        keys = qkv_ref[1, :, cols]
        values = qkv_ref[2, :, cols]
        for start in range(0, half, tile):
            rows = slice(start, start + tile)
            scores = mm_nt(qkv_ref[0, rows, cols], keys) * scale
            scores = scores + bias_ref[head, rows, :].astype(F32)
            scores = jnp.where(seg_col_ref[rows, :] == seg_row, scores, MASKED)
            top = jnp.max(scores, axis=-1, keepdims=True)
            weights = jnp.exp(scores - top)
            inverse = 1.0 / jnp.sum(weights, axis=-1, keepdims=True)
            prob = (weights * inverse).astype(BF16)
            prob_ref[0, head, rows, :] = prob
            out_ref[rows, cols] = mm(prob, values).astype(BF16)


def attend(qkv, bias, seg, scale):
    heads, half = bias.shape[0], bias.shape[1]
    slots, cols = qkv.shape[1], qkv.shape[2]
    parts = slots // half
    return pl.pallas_call(
        functools.partial(attend_kernel, scale, min(128, half)),
        grid=(parts,),
        out_shape=(
            jax.ShapeDtypeStruct((parts, heads, half, half), BF16),
            jax.ShapeDtypeStruct((slots, cols), BF16),
        ),
        in_specs=[
            pl.BlockSpec((3, half, cols), lambda p: (0, p, 0)),
            pl.BlockSpec((heads, half, half), lambda p: (0, 0, 0)),
            pl.BlockSpec((1, half), lambda p: (0, p)),
            pl.BlockSpec((half, 1), lambda p: (p, 0)),
        ],
        out_specs=(
            pl.BlockSpec((1, heads, half, half), lambda p: (p, 0, 0, 0)),
            pl.BlockSpec((half, cols), lambda p: (p, 0)),
        ),
        compiler_params=pltpu.CompilerParams(vmem_limit_bytes=VMEM_LIMIT),
        cost_estimate=pl.CostEstimate(
            flops=4 * slots * half * cols,
            bytes_accessed=parts * heads * half * half * 3 + slots * cols * 8,
            transcendentals=parts * heads * half * half,
        ),
        name="attend",
    )(qkv, bias, seg.reshape(1, slots), seg.reshape(slots, 1))


def attend_back_kernel(
    scale, tile, qkv_ref, prob_ref, grad_ref, dproj_ref, line_ref, total_ref, ds_ref
):
    heads, half = prob_ref.shape[1], prob_ref.shape[2]
    size = grad_ref.shape[1] // heads
    part = pl.program_id(0)

    @pl.when(part == 0)
    def _():
        total_ref[...] = jnp.zeros_like(total_ref)

    for head in range(heads):
        cols = slice(head * size, (head + 1) * size)
        values = qkv_ref[2, :, cols]
        for start in range(0, half, tile):
            rows = slice(start, start + tile)
            prob = prob_ref[0, head, rows, :].astype(F32)
            dprob = mm_nt(grad_ref[rows, cols], values)
            inner = jnp.sum(prob * dprob, axis=-1, keepdims=True)
            dscore = (prob * (dprob - inner)).astype(BF16)
            ds_ref[rows, :] = dscore
            total_ref[head, rows, :] += dscore.astype(F32)
        dscores = ds_ref[...]
        dproj_ref[0, :, cols] = (mm(dscores, qkv_ref[1, :, cols]) * scale).astype(BF16)
        dproj_ref[1, :, cols] = (mm_tn(dscores, qkv_ref[0, :, cols]) * scale).astype(BF16)
        dproj_ref[2, :, cols] = mm_tn(prob_ref[0, head], grad_ref[:, cols]).astype(BF16)

    @pl.when(part == pl.num_programs(0) - 1)
    def _():
        row = lax.broadcasted_iota(jnp.int32, (8, 2 * half), 0)
        for head in range(heads):

            def body(a, carry):
                start = pl.multiple_of(a * 8, 8)
                block = total_ref[head, pl.ds(start, 8), :]
                block = jnp.concatenate([block, jnp.zeros_like(block)], axis=1)
                return carry + pltpu.roll(block, 2 * half - start, 1)

            found = lax.fori_loop(0, half // 8, body, jnp.zeros((8, 2 * half), F32))
            line = jnp.zeros((1, 2 * half), F32)
            for r in range(8):
                moved = pltpu.roll(found, 2 * half - r, 1) if r else found
                line = line + jnp.sum(jnp.where(row == r, moved, 0.0), axis=0, keepdims=True)
            line_ref[head : head + 1, :] = line


def attend_back(qkv, prob, grad_heads, scale):
    parts, heads, half = prob.shape[:3]
    slots, cols = grad_heads.shape
    return pl.pallas_call(
        functools.partial(attend_back_kernel, scale, min(128, half)),
        grid=(parts,),
        out_shape=(
            jax.ShapeDtypeStruct((3, slots, cols), BF16),
            jax.ShapeDtypeStruct((heads, 2 * half), F32),
        ),
        in_specs=[
            pl.BlockSpec((3, half, cols), lambda p: (0, p, 0)),
            pl.BlockSpec((1, heads, half, half), lambda p: (p, 0, 0, 0)),
            pl.BlockSpec((half, cols), lambda p: (p, 0)),
        ],
        out_specs=(
            pl.BlockSpec((3, half, cols), lambda p: (0, p, 0)),
            pl.BlockSpec((heads, 2 * half), lambda p: (0, 0)),
        ),
        scratch_shapes=[
            pltpu.VMEM((heads, half, half), F32),
            pltpu.VMEM((half, half), BF16),
        ],
        compiler_params=pltpu.CompilerParams(vmem_limit_bytes=VMEM_LIMIT),
        cost_estimate=pl.CostEstimate(
            flops=8 * slots * half * cols,
            bytes_accessed=parts * heads * half * half * 2 + slots * cols * 14,
            transcendentals=0,
        ),
        name="attend_back",
    )(qkv, prob, grad_heads)


def expert_kernel(x_ref, g_ref, wg_ref, wu_ref, wd_ref, y_ref, dx_ref, hid_ref, dga_ref, dup_ref):
    sources, _, cap, width = x_ref.shape
    rows = sources * cap
    x = x_ref[...].reshape(rows, width)
    g = g_ref[...].reshape(rows, width)
    gate = mm(x, wg_ref[0])
    up = mm(x, wu_ref[0])
    square = gate * gate
    bent = jnp.tanh(GELU_C * gate * (1.0 + GELU_A * square))
    half_gate = 0.5 * gate
    gelu = half_gate * (1.0 + bent)
    slope = 0.5 * (1.0 + bent) + half_gate * (1.0 - bent * bent) * (
        GELU_C * (1.0 + 3.0 * GELU_A * square)
    )
    hid = (gelu * up).astype(BF16)
    dhid = mm_nt(g, wd_ref[0])
    dga = (dhid * (up * slope)).astype(BF16)
    dup = (dhid * gelu).astype(BF16)
    hid_ref[0] = hid
    dga_ref[0] = dga
    dup_ref[0] = dup
    y_ref[...] = mm(hid, wd_ref[0]).astype(BF16).reshape(sources, 1, cap, width)
    dx = mm_nt(dga, wg_ref[0]) + mm_nt(dup, wu_ref[0])
    dx_ref[...] = dx.astype(BF16).reshape(sources, 1, cap, width)


def expert_pass(x, g, wg, wu, wd):
    sources, experts, cap, width = x.shape
    hidden = wg.shape[2]
    group = 2 if sources % 2 == 0 else 1
    tokens = pl.BlockSpec((group, 1, cap, width), lambda e, s: (s, e, 0, 0))
    wide = pl.BlockSpec((1, width, hidden), lambda e, s: (e, 0, 0))
    tall = pl.BlockSpec((1, hidden, width), lambda e, s: (e, 0, 0))
    acts = pl.BlockSpec((1, group * cap, hidden), lambda e, s: (e, s, 0))
    rows = sources * cap
    act_shape = jax.ShapeDtypeStruct((experts, rows, hidden), BF16)
    return pl.pallas_call(
        expert_kernel,
        grid=(experts, sources // group),
        out_shape=(
            jax.ShapeDtypeStruct(x.shape, BF16),
            jax.ShapeDtypeStruct(x.shape, BF16),
            act_shape,
            act_shape,
            act_shape,
        ),
        in_specs=[tokens, tokens, wide, wide, tall],
        out_specs=(tokens, tokens, acts, acts, acts),
        compiler_params=pltpu.CompilerParams(vmem_limit_bytes=VMEM_LIMIT),
        cost_estimate=pl.CostEstimate(
            flops=12 * experts * rows * width * hidden,
            bytes_accessed=8 * experts * rows * width + 6 * experts * hidden * (width + rows),
            transcendentals=experts * rows * hidden,
        ),
        name="expert_pass",
    )(x, g, wg, wu, wd)


def weight_kernel(*refs):
    count = (len(refs) - 3) // 5
    dwg_ref, dwu_ref, dwd_ref = refs[-3:]
    totals = [0.0, 0.0, 0.0]
    for index in range(count):
        x_ref, g_ref, hid_ref, dga_ref, dup_ref = refs[5 * index : 5 * index + 5]
        sources, _, cap, width = x_ref.shape
        x = x_ref[...].reshape(sources * cap, width)
        g = g_ref[...].reshape(sources * cap, width)
        totals[0] = totals[0] + mm_tn(x, dga_ref[0])
        totals[1] = totals[1] + mm_tn(x, dup_ref[0])
        totals[2] = totals[2] + mm_tn(hid_ref[0], g)
    dwg_ref[0] = totals[0]
    dwu_ref[0] = totals[1]
    dwd_ref[0] = totals[2]


def weight_pass(kept):
    sources, experts, cap, width = kept[0][0].shape
    rows, hidden = kept[0][2].shape[1:]
    block = 256 if width % 256 == 0 else width
    tokens = pl.BlockSpec((sources, 1, cap, block), lambda e, j: (0, e, 0, j))
    acts = pl.BlockSpec((1, rows, hidden), lambda e, j: (e, 0, 0))
    operands = []
    for arrays in kept:
        operands.extend(arrays)
    return pl.pallas_call(
        weight_kernel,
        grid=(experts, width // block),
        out_shape=(
            jax.ShapeDtypeStruct((experts, width, hidden), F32),
            jax.ShapeDtypeStruct((experts, width, hidden), F32),
            jax.ShapeDtypeStruct((experts, hidden, width), F32),
        ),
        in_specs=[tokens, tokens, acts, acts, acts] * len(kept),
        out_specs=(
            pl.BlockSpec((1, block, hidden), lambda e, j: (e, j, 0)),
            pl.BlockSpec((1, block, hidden), lambda e, j: (e, j, 0)),
            pl.BlockSpec((1, hidden, block), lambda e, j: (e, 0, j)),
        ),
        compiler_params=pltpu.CompilerParams(vmem_limit_bytes=VMEM_LIMIT),
        cost_estimate=pl.CostEstimate(
            flops=6 * len(kept) * experts * rows * width * hidden,
            bytes_accessed=len(kept) * experts * rows * (4 * width + 6 * hidden)
            + 12 * experts * width * hidden,
            transcendentals=0,
        ),
        name="weight_pass",
    )(*operands)


def norm_back(grad_out, unit, scale, gain):
    weighted = grad_out * gain
    grad_in = scale * (weighted - unit * jnp.mean(weighted * unit, axis=-1, keepdims=True))
    return grad_in, jnp.sum(grad_out * unit, axis=0)


def shards(
    x_in,
    cotangent,
    segment_ids,
    routes,
    qkv_weight,
    out_weight,
    bias_table,
    attn_gain,
    moe_gain,
    router_weight,
    gate_weight,
    up_weight,
    down_weight,
):
    micro_count, _, shard_len, width = x_in.shape
    slot_count = segment_ids.shape[2]
    head_cols = out_weight.shape[0]
    bucket_count, heads_here = bias_table.shape
    head_size = head_cols // heads_here
    expert_count = router_weight.shape[1]
    experts_here = gate_weight.shape[0]
    devices = expert_count // experts_here
    blocks = slot_count // shard_len
    capacity = max(2, (10 * shard_len + 4 * expert_count - 1) // (4 * expert_count))
    half = min(FIRST_ITEM, slot_count)
    scale = head_size ** (-0.5)
    hidden_index = lax.axis_index("hidden")
    own_start = hidden_index * shard_len
    attn_gain_f = attn_gain.astype(F32)
    moe_gain_f = moe_gain.astype(F32)
    onehot_bucket = bucket_onehot(half, bucket_count)
    line = jnp.einsum(
        "jb,bh->hj", onehot_bucket, bias_table.astype(F32), precision=PRECISE
    )
    bias = position_bias(line, half)
    expert_ids = jnp.arange(expert_count, dtype=jnp.int32)
    place_ids = jnp.arange(expert_count * capacity, dtype=jnp.int32)
    earlier_than = (
        jnp.arange(shard_len, dtype=jnp.int32)[:, None]
        < jnp.arange(shard_len, dtype=jnp.int32)[None, :]
    ).astype(BF16)
    all_routes = lax.all_gather(routes[:, 0], "hidden", axis=1, tiled=True)
    all_out_weight = lax.all_gather(out_weight, "hidden", axis=0, tiled=True)
    all_out_weight = all_out_weight.reshape(blocks, head_cols, width)

    def own(values):
        return lax.dynamic_slice_in_dim(values, own_start, shard_len, 0)

    def gather(values):
        return lax.all_gather(values, "hidden", axis=0, tiled=True)

    def scatter(values):
        return lax.psum_scatter(values.astype(BF16), "hidden", scatter_dimension=0, tiled=True)

    def exchange(buffer):
        return lax.all_to_all(buffer, "expert", split_axis=0, concat_axis=0, tiled=True)

    def to_buffer(rows):
        rows = rows.reshape(blocks, expert_count, capacity, width).transpose(1, 0, 2, 3)
        return rows.reshape(devices, experts_here * blocks * capacity, width)

    def from_buffer(buffer):
        rows = buffer.reshape(expert_count, blocks, capacity, width).transpose(1, 0, 2, 3)
        return rows.reshape(blocks, expert_count * capacity, width)

    def attention(micro):
        seg = segment_ids[micro, 0]
        gathered = gather(x_in[micro, 0])
        x_now = gathered.astype(F32)
        r1 = lax.rsqrt(jnp.mean(x_now * x_now, axis=-1, keepdims=True) + EPSILON)
        xn1 = (x_now * r1 * attn_gain_f).astype(BF16)
        qkv = jnp.einsum("sd,tdf->tsf", xn1, qkv_weight, preferred_element_type=F32).astype(BF16)
        prob, heads_out = attend(qkv, bias, seg, scale)
        all_heads = lax.all_gather(heads_out, "hidden", axis=0, tiled=False)
        return dict(seg=seg, gathered=gathered, xn1=xn1, qkv=qkv, prob=prob, heads=heads_out, all_heads=all_heads)

    def dispatch(micro, kept):
        attn = jnp.einsum(
            "hsf,hfd->sd", kept["all_heads"], all_out_weight, preferred_element_type=F32
        )
        h1 = kept["gathered"].astype(F32) + attn
        r2 = lax.rsqrt(jnp.mean(h1 * h1, axis=-1, keepdims=True) + EPSILON)
        xn2 = (h1 * r2 * moe_gain_f).astype(BF16)
        logits = jnp.dot(xn2, router_weight, preferred_element_type=F32)
        router = jax.nn.softmax(logits, axis=-1)
        route = all_routes[micro]
        live = kept["seg"] >= 0
        live_f = live.astype(F32)
        onehot = (route[:, :, None] == expert_ids).astype(F32)
        picked = jnp.sum(router[:, None, :] * onehot, axis=-1)
        total = jnp.sum(picked, axis=1, keepdims=True)
        gates = picked / total * live_f[:, None]
        chosen = (onehot * live_f[:, None, None]).reshape(blocks, shard_len, 2, expert_count)
        counted = jnp.sum(chosen, axis=2).astype(BF16)
        before = jnp.einsum("bte,tu->bue", counted, earlier_than, preferred_element_type=F32)
        position = jnp.sum(before[:, :, None, :] * chosen, axis=-1).astype(jnp.int32)
        route_b = route.reshape(blocks, shard_len, 2)
        place = jnp.where(
            live.reshape(blocks, shard_len)[:, :, None], route_b * capacity + position, -1
        )
        at_place = [place[:, None, :, k] == place_ids[None, :, None] for k in range(2)]
        placed = (at_place[0] | at_place[1]).astype(BF16)
        gates_b = gates.reshape(blocks, shard_len, 2)
        gate_place = sum(
            jnp.sum(jnp.where(at_place[k], gates_b[:, None, :, k], 0.0), axis=-1) for k in range(2)
        )
        xn2_b = xn2.reshape(blocks, shard_len, width)
        sent = jnp.einsum("bst,btd->bsd", placed, xn2_b, preferred_element_type=F32).astype(BF16)
        arrived = exchange(to_buffer(sent))
        dy = gather(cotangent[micro, 0])
        dy_b = dy.reshape(blocks, shard_len, width)
        dy_place = jnp.einsum("bst,btd->bsd", placed, dy_b, preferred_element_type=F32)
        sent_back = (dy_place * gate_place[:, :, None]).astype(BF16)
        arrived_back = exchange(to_buffer(sent_back))
        kept.update(
            h1=own(h1), r2=own(r2), xn2=own(xn2), router=own(router), picked=own(picked),
            total=own(total), onehot=own(onehot), live=own(live_f), placed=placed,
            place=place, at_place=at_place, gate_place=gate_place, dy_place=dy_place.astype(BF16),
            arrived=arrived, arrived_back=arrived_back,
        )

    def experts(micro, kept):
        shape = (devices, experts_here, blocks * capacity, width)
        x = kept["arrived"].reshape(shape)
        g = kept["arrived_back"].reshape(shape)
        y, dx, hid, dga, dup = expert_pass(x, g, gate_weight, up_weight, down_weight)
        kept["weights"] = (x, g, hid, dga, dup)
        kept["back_y"] = exchange(y.reshape(devices, -1, width))
        kept["back_dx"] = exchange(dx.reshape(devices, -1, width))

    def combine(micro, kept):
        y = from_buffer(kept["back_y"])
        y_f = y.astype(F32)
        scaled = (y_f * kept["gate_place"][:, :, None]).astype(BF16)
        mixed = jnp.einsum("bst,bsd->btd", kept["placed"], scaled, preferred_element_type=F32)
        mixed = scatter(mixed.reshape(slot_count, width))
        dgate_place = jnp.sum(y_f * kept["dy_place"].astype(F32), axis=-1)
        dgates = jnp.stack(
            [
                jnp.sum(jnp.where(kept["at_place"][k], dgate_place[:, :, None], 0.0), axis=1)
                for k in range(2)
            ],
            axis=-1,
        )
        dgates = lax.psum_scatter(
            dgates.reshape(slot_count, 2), "hidden", scatter_dimension=0, tiled=True
        )
        dx = from_buffer(kept["back_dx"])
        dxn2 = jnp.einsum("bst,bsd->btd", kept["placed"], dx, preferred_element_type=F32)
        dxn2 = scatter(dxn2.reshape(slot_count, width)).astype(F32)
        kept["block_out"] = (kept["h1"] + mixed.astype(F32)).astype(BF16)
        picked, total, router = kept["picked"], kept["total"], kept["router"]
        dgates = dgates * kept["live"][:, None]
        dpicked = dgates / total - jnp.sum(dgates * picked, axis=1, keepdims=True) / (total * total)
        drouter = jnp.sum(dpicked[:, :, None] * kept["onehot"], axis=1)
        dlogits = router * (drouter - jnp.sum(router * drouter, axis=-1, keepdims=True))
        dlogits = dlogits.astype(BF16)
        kept["router_grad"] = mm_tn(kept["xn2"], dlogits)
        dxn2 = dxn2 + mm_nt(dlogits, router_weight)
        unit = kept["h1"] * kept["r2"]
        part, kept["moe_gain_grad"] = norm_back(dxn2, unit, kept["r2"], moe_gain_f)
        kept["dh1"] = cotangent[micro, 0].astype(F32) + part
        kept["dattn"] = gather(kept["dh1"].astype(BF16))

    def attention_back(micro, kept):
        dattn = kept["dattn"]
        kept["out_grad"] = mm_tn(kept["heads"], dattn)
        dheads = mm_nt(dattn, out_weight).astype(BF16)
        dproj, bias_line = attend_back(kept["qkv"], kept["prob"], dheads, scale)
        kept["bias_line"] = bias_line
        dxn1 = jnp.einsum("tsf,tdf->sd", dproj, qkv_weight, preferred_element_type=F32)
        dxn1 = scatter(dxn1).astype(F32)
        kept["qkv_grad"] = jnp.einsum(
            "sd,tsf->tdf", kept["xn1"], dproj, preferred_element_type=F32
        )
        x_own = x_in[micro, 0].astype(F32)
        r1 = lax.rsqrt(jnp.mean(x_own * x_own, axis=-1, keepdims=True) + EPSILON)
        part, kept["attn_gain_grad"] = norm_back(dxn1, x_own * r1, r1, attn_gain_f)
        kept["x_grad"] = (kept["dh1"] + part).astype(BF16)

    states = []
    for micro in range(micro_count):
        states.append(attention(micro))
    for micro in range(micro_count):
        dispatch(micro, states[micro])
        experts(micro, states[micro])
    for micro in range(micro_count):
        combine(micro, states[micro])
        attention_back(micro, states[micro])
    dwg, dwu, dwd = weight_pass([state["weights"] for state in states])

    def added(name):
        total = states[0][name]
        for state in states[1:]:
            total = total + state[name]
        return total

    grad_table = jnp.einsum("hj,jb->bh", added("bias_line"), onehot_bucket, precision=PRECISE)
    grad_qkv, grad_out, grad_table = (
        lax.psum(added("qkv_grad").astype(BF16), "expert").astype(F32),
        lax.psum(added("out_grad").astype(BF16), "expert").astype(F32),
        lax.psum(grad_table.astype(BF16), "expert").astype(F32),
    )
    grad_router, grad_attn_gain, grad_moe_gain = lax.psum(
        (added("router_grad"), added("attn_gain_grad"), added("moe_gain_grad")),
        ("expert", "hidden"),
    )
    return (
        jnp.stack([state["block_out"] for state in states])[:, None],
        jnp.stack([state["x_grad"] for state in states])[:, None],
        grad_qkv,
        grad_out,
        grad_table,
        grad_attn_gain,
        grad_moe_gain,
        grad_router,
        dwg,
        dwu,
        dwd,
    )


def solution(mesh):
    return jax.shard_map(
        shards,
        mesh=mesh,
        in_specs=(
            P(None, "expert", "hidden", None),
            P(None, "expert", "hidden", None),
            P(None, "expert", None),
            P(None, "expert", "hidden", None),
            P(None, None, "hidden"),
            P("hidden", None),
            P(None, "hidden"),
            P(),
            P(),
            P(),
            P("expert", None, "hidden"),
            P("expert", None, "hidden"),
            P("expert", "hidden", None),
        ),
        out_specs=(
            P(None, "expert", "hidden", None),
            P(None, "expert", "hidden", None),
            P(None, None, "hidden"),
            P("hidden", None),
            P(None, "hidden"),
            P(),
            P(),
            P(),
            P("expert", None, "hidden"),
            P("expert", None, "hidden"),
            P("expert", "hidden", None),
        ),
        check_vma=False,
    )
```

```python
import functools

import jax
import jax.numpy as jnp
from jax import lax
from jax.experimental import pallas as pl
from jax.experimental.pallas import tpu as pltpu
from jax.sharding import PartitionSpec as P

EPSILON = 1e-06
PRECISE = lax.Precision.HIGHEST
LIMITS = (12, 16, 23, 32, 46, 64, 91)
MASKED = -1000000000.0
FIRST_ITEM = 512
GELU_C = 0.7978845608028654
GELU_A = 0.044715
VMEM_LIMIT = 60 * 1024 * 1024
F32 = jnp.float32
BF16 = jnp.bfloat16


def mm(a, b):
    return lax.dot_general(a, b, (((1,), (0,)), ((), ())), preferred_element_type=F32)


def mm_nt(a, b):
    return lax.dot_general(a, b, (((1,), (1,)), ((), ())), preferred_element_type=F32)


def mm_tn(a, b):
    return lax.dot_general(a, b, (((0,), (0,)), ((), ())), preferred_element_type=F32)


def bucket_of(distance):
    magnitude = jnp.abs(distance)
    far_bucket = jnp.full(magnitude.shape, 8, jnp.int32)
    for threshold in LIMITS:
        far_bucket = far_bucket + (magnitude >= threshold).astype(jnp.int32)
    return jnp.where(magnitude < 8, magnitude, far_bucket) + 16 * (distance > 0).astype(jnp.int32)


def bucket_onehot(half, bucket_count):
    lane = jnp.arange(2 * half, dtype=jnp.int32)
    distance = jnp.where(lane < half, lane, lane - 2 * half)
    return (
        bucket_of(distance)[:, None] == jnp.arange(bucket_count, dtype=jnp.int32)[None, :]
    ).astype(F32)


def bias_kernel(line_ref, out_ref):
    half = out_ref.shape[2]
    line = jnp.broadcast_to(line_ref[0], (16, 2 * half))
    row = lax.broadcasted_iota(jnp.int32, (16, 2 * half), 0)
    base = jnp.zeros((16, 2 * half), F32)
    for r in range(16):
        base = jnp.where(row == r, pltpu.roll(line, r, 1) if r else line, base)

    def body(a, carry):
        start = pl.multiple_of(a * 16, 16)
        moved = pltpu.roll(base, start, 1)
        out_ref[0, pl.ds(start, 16), :] = moved[:, :half].astype(out_ref.dtype)
        return carry

    lax.fori_loop(0, half // 16, body, 0)


def position_bias(line, half):
    heads = line.shape[0]
    return pl.pallas_call(
        bias_kernel,
        grid=(heads,),
        out_shape=jax.ShapeDtypeStruct((heads, half, half), BF16),
        in_specs=[pl.BlockSpec((1, 1, 2 * half), lambda h: (h, 0, 0))],
        out_specs=pl.BlockSpec((1, half, half), lambda h: (h, 0, 0)),
        compiler_params=pltpu.CompilerParams(vmem_limit_bytes=VMEM_LIMIT),
        name="position_bias",
    )(line.reshape(heads, 1, 2 * half))


def attend_kernel(scale, tile, qkv_ref, bias_ref, seg_row_ref, seg_col_ref, prob_ref, out_ref):
    heads, half = bias_ref.shape[0], bias_ref.shape[1]
    size = out_ref.shape[1] // heads
    seg_row = seg_row_ref[...]
    for head in range(heads):
        cols = slice(head * size, (head + 1) * size)
        keys = qkv_ref[1, :, cols]
        values = qkv_ref[2, :, cols]
        for start in range(0, half, tile):
            rows = slice(start, start + tile)
            scores = mm_nt(qkv_ref[0, rows, cols], keys) * scale
            scores = scores + bias_ref[head, rows, :].astype(F32)
            scores = jnp.where(seg_col_ref[rows, :] == seg_row, scores, MASKED)
            top = jnp.max(scores, axis=-1, keepdims=True)
            weights = jnp.exp(scores - top)
            inverse = 1.0 / jnp.sum(weights, axis=-1, keepdims=True)
            prob = (weights * inverse).astype(BF16)
            prob_ref[0, head, rows, :] = prob
            out_ref[rows, cols] = mm(prob, values).astype(BF16)


def attend(qkv, bias, seg, scale):
    heads, half = bias.shape[0], bias.shape[1]
    slots, cols = qkv.shape[1], qkv.shape[2]
    parts = slots // half
    return pl.pallas_call(
        functools.partial(attend_kernel, scale, min(128, half)),
        grid=(parts,),
        out_shape=(
            jax.ShapeDtypeStruct((parts, heads, half, half), BF16),
            jax.ShapeDtypeStruct((slots, cols), BF16),
        ),
        in_specs=[
            pl.BlockSpec((3, half, cols), lambda p: (0, p, 0)),
            pl.BlockSpec((heads, half, half), lambda p: (0, 0, 0)),
            pl.BlockSpec((1, half), lambda p: (0, p)),
            pl.BlockSpec((half, 1), lambda p: (p, 0)),
        ],
        out_specs=(
            pl.BlockSpec((1, heads, half, half), lambda p: (p, 0, 0, 0)),
            pl.BlockSpec((half, cols), lambda p: (p, 0)),
        ),
        compiler_params=pltpu.CompilerParams(vmem_limit_bytes=VMEM_LIMIT),
        cost_estimate=pl.CostEstimate(
            flops=4 * slots * half * cols,
            bytes_accessed=parts * heads * half * half * 3 + slots * cols * 8,
            transcendentals=parts * heads * half * half,
        ),
        name="attend",
    )(qkv, bias, seg.reshape(1, slots), seg.reshape(slots, 1))


def attend_back_kernel(
    scale, tile, qkv_ref, prob_ref, grad_ref, dproj_ref, line_ref, total_ref, ds_ref
):
    heads, half = prob_ref.shape[1], prob_ref.shape[2]
    size = grad_ref.shape[1] // heads
    part = pl.program_id(0)

    @pl.when(part == 0)
    def _():
        total_ref[...] = jnp.zeros_like(total_ref)

    for head in range(heads):
        cols = slice(head * size, (head + 1) * size)
        values = qkv_ref[2, :, cols]
        for start in range(0, half, tile):
            rows = slice(start, start + tile)
            prob = prob_ref[0, head, rows, :].astype(F32)
            dprob = mm_nt(grad_ref[rows, cols], values)
            inner = jnp.sum(prob * dprob, axis=-1, keepdims=True)
            dscore = (prob * (dprob - inner)).astype(BF16)
            ds_ref[rows, :] = dscore
            total_ref[head, rows, :] += dscore.astype(F32)
        dscores = ds_ref[...]
        dproj_ref[0, :, cols] = (mm(dscores, qkv_ref[1, :, cols]) * scale).astype(BF16)
        dproj_ref[1, :, cols] = (mm_tn(dscores, qkv_ref[0, :, cols]) * scale).astype(BF16)
        dproj_ref[2, :, cols] = mm_tn(prob_ref[0, head], grad_ref[:, cols]).astype(BF16)

    @pl.when(part == pl.num_programs(0) - 1)
    def _():
        row = lax.broadcasted_iota(jnp.int32, (8, 2 * half), 0)
        for head in range(heads):

            def body(a, carry):
                start = pl.multiple_of(a * 8, 8)
                block = total_ref[head, pl.ds(start, 8), :]
                block = jnp.concatenate([block, jnp.zeros_like(block)], axis=1)
                return carry + pltpu.roll(block, 2 * half - start, 1)

            found = lax.fori_loop(0, half // 8, body, jnp.zeros((8, 2 * half), F32))
            line = jnp.zeros((1, 2 * half), F32)
            for r in range(8):
                moved = pltpu.roll(found, 2 * half - r, 1) if r else found
                line = line + jnp.sum(jnp.where(row == r, moved, 0.0), axis=0, keepdims=True)
            line_ref[head : head + 1, :] = line


def attend_back(qkv, prob, grad_heads, scale):
    parts, heads, half = prob.shape[:3]
    slots, cols = grad_heads.shape
    return pl.pallas_call(
        functools.partial(attend_back_kernel, scale, min(128, half)),
        grid=(parts,),
        out_shape=(
            jax.ShapeDtypeStruct((3, slots, cols), BF16),
            jax.ShapeDtypeStruct((heads, 2 * half), F32),
        ),
        in_specs=[
            pl.BlockSpec((3, half, cols), lambda p: (0, p, 0)),
            pl.BlockSpec((1, heads, half, half), lambda p: (p, 0, 0, 0)),
            pl.BlockSpec((half, cols), lambda p: (p, 0)),
        ],
        out_specs=(
            pl.BlockSpec((3, half, cols), lambda p: (0, p, 0)),
            pl.BlockSpec((heads, 2 * half), lambda p: (0, 0)),
        ),
        scratch_shapes=[
            pltpu.VMEM((heads, half, half), F32),
            pltpu.VMEM((half, half), BF16),
        ],
        compiler_params=pltpu.CompilerParams(vmem_limit_bytes=VMEM_LIMIT),
        cost_estimate=pl.CostEstimate(
            flops=8 * slots * half * cols,
            bytes_accessed=parts * heads * half * half * 2 + slots * cols * 14,
            transcendentals=0,
        ),
        name="attend_back",
    )(qkv, prob, grad_heads)


def spread(rows, place0, place1, count):
    ids = lax.broadcasted_iota(jnp.int32, (count, rows.shape[0]), 0)
    hit = (ids == place0) | (ids == place1)
    return mm(jnp.where(hit, 1.0, 0.0).astype(BF16), rows)


def spread_kernel(rows_ref, place_ref, out_ref):
    experts, _, cap, width = out_ref.shape
    placed = spread(rows_ref[...], place_ref[0:1, :], place_ref[1:2, :], experts * cap)
    out_ref[...] = placed.astype(BF16).reshape(experts, 1, cap, width)


def spread_rows(rows, place, experts, cap, shard_len):
    slots, width = rows.shape
    blocks = slots // shard_len
    return pl.pallas_call(
        spread_kernel,
        grid=(blocks,),
        out_shape=jax.ShapeDtypeStruct((experts, blocks, cap, width), BF16),
        in_specs=[
            pl.BlockSpec((shard_len, width), lambda b: (b, 0)),
            pl.BlockSpec((2, shard_len), lambda b: (0, b)),
        ],
        out_specs=pl.BlockSpec((experts, 1, cap, width), lambda b: (0, b, 0, 0)),
        compiler_params=pltpu.CompilerParams(vmem_limit_bytes=VMEM_LIMIT),
        cost_estimate=pl.CostEstimate(
            flops=2 * experts * cap * slots * width,
            bytes_accessed=2 * slots * width + 2 * experts * blocks * cap * width,
            transcendentals=0,
        ),
        name="spread_rows",
    )(rows, place)


def project_kernel(heads_ref, weight_ref, x_ref, gain_ref, place_ref, h1_ref, out_ref):
    experts, _, cap, width = out_ref.shape
    h1 = x_ref[...].astype(F32)
    for group in range(heads_ref.shape[0]):
        h1 = h1 + mm(heads_ref[group], weight_ref[group])
    h1_ref[...] = h1
    scale = lax.rsqrt(jnp.mean(h1 * h1, axis=-1, keepdims=True) + EPSILON)
    tokens = (h1 * scale * gain_ref[...]).astype(BF16)
    placed = spread(tokens, place_ref[0:1, :], place_ref[1:2, :], experts * cap)
    out_ref[...] = placed.astype(BF16).reshape(experts, 1, cap, width)


def project_and_spread(heads, weight, x, gain, place, experts, cap, shard_len):
    slots, width = x.shape
    blocks = slots // shard_len
    groups, _, cols = heads.shape
    return pl.pallas_call(
        project_kernel,
        grid=(blocks,),
        out_shape=(
            jax.ShapeDtypeStruct((slots, width), F32),
            jax.ShapeDtypeStruct((experts, blocks, cap, width), BF16),
        ),
        in_specs=[
            pl.BlockSpec((groups, shard_len, cols), lambda b: (0, b, 0)),
            pl.BlockSpec((groups, cols, width), lambda b: (0, 0, 0)),
            pl.BlockSpec((shard_len, width), lambda b: (b, 0)),
            pl.BlockSpec((1, width), lambda b: (0, 0)),
            pl.BlockSpec((2, shard_len), lambda b: (0, b)),
        ],
        out_specs=(
            pl.BlockSpec((shard_len, width), lambda b: (b, 0)),
            pl.BlockSpec((experts, 1, cap, width), lambda b: (0, b, 0, 0)),
        ),
        compiler_params=pltpu.CompilerParams(vmem_limit_bytes=VMEM_LIMIT),
        cost_estimate=pl.CostEstimate(
            flops=2 * slots * width * (width + experts * cap),
            bytes_accessed=10 * slots * width + 2 * experts * blocks * cap * width,
            transcendentals=0,
        ),
        name="project_and_spread",
    )(heads, weight, x, gain.reshape(1, width), place)


def collect_kernel(rows_ref, place_ref, out_ref):
    experts, _, cap, width = rows_ref.shape
    tokens = out_ref.shape[0]
    ids = lax.broadcasted_iota(jnp.int32, (tokens, experts * cap), 1)
    hit = (ids == place_ref[:, 0:1]) | (ids == place_ref[:, 1:2])
    rows = rows_ref[...].reshape(experts * cap, width)
    out_ref[...] = mm(jnp.where(hit, 1.0, 0.0).astype(BF16), rows).astype(BF16)


def collect_rows(rows, place, shard_len):
    experts, blocks, cap, width = rows.shape
    slots = blocks * shard_len
    return pl.pallas_call(
        collect_kernel,
        grid=(blocks,),
        out_shape=jax.ShapeDtypeStruct((slots, width), BF16),
        in_specs=[
            pl.BlockSpec((experts, 1, cap, width), lambda b: (0, b, 0, 0)),
            pl.BlockSpec((shard_len, 2), lambda b: (b, 0)),
        ],
        out_specs=pl.BlockSpec((shard_len, width), lambda b: (b, 0)),
        compiler_params=pltpu.CompilerParams(vmem_limit_bytes=VMEM_LIMIT),
        cost_estimate=pl.CostEstimate(
            flops=2 * experts * cap * slots * width,
            bytes_accessed=2 * slots * width + 2 * experts * blocks * cap * width,
            transcendentals=0,
        ),
        name="collect_rows",
    )(rows, place)


def expert_kernel(
    x_ref, dy_ref, pair_ref, wr_ref, wg_ref, wu_ref, wd_ref,
    y_ref, dx_ref, g_ref, hid_ref, dga_ref, dup_ref, dlog_ref,
):
    sources, _, cap, width = x_ref.shape
    rows = sources * cap
    x = x_ref[...].reshape(rows, width)
    dy = dy_ref[...].reshape(rows, width).astype(F32)
    pair = pair_ref[...].reshape(rows, pair_ref.shape[3])
    margin = jnp.sum(mm(x, wr_ref[...]) * pair, axis=-1, keepdims=True)
    own_gate = 1.0 / (1.0 + jnp.exp(-margin))
    other_gate = 1.0 / (1.0 + jnp.exp(margin))
    g = (own_gate * dy).astype(BF16)
    g_ref[0] = g
    gate = mm(x, wg_ref[0])
    up = mm(x, wu_ref[0])
    square = gate * gate
    bent = jnp.tanh(GELU_C * gate * (1.0 + GELU_A * square))
    half_gate = 0.5 * gate
    gelu = half_gate * (1.0 + bent)
    slope = 0.5 * (1.0 + bent) + half_gate * (1.0 - bent * bent) * (
        GELU_C * (1.0 + 3.0 * GELU_A * square)
    )
    hid = (gelu * up).astype(BF16)
    dhid = mm_nt(g, wd_ref[0])
    dga = (dhid * (up * slope)).astype(BF16)
    dup = (dhid * gelu).astype(BF16)
    hid_ref[0] = hid
    dga_ref[0] = dga
    dup_ref[0] = dup
    y = mm(hid, wd_ref[0])
    dgate = jnp.sum(y * dy, axis=-1, keepdims=True)
    y_ref[...] = (y * own_gate).astype(BF16).reshape(sources, 1, cap, width)
    dlog = (dgate * own_gate * other_gate * pair).astype(BF16)
    dlog_ref[0] = dlog
    dx = mm_nt(dga, wg_ref[0]) + mm_nt(dup, wu_ref[0]) + mm_nt(dlog, wr_ref[...])
    dx_ref[...] = dx.astype(BF16).reshape(sources, 1, cap, width)


def expert_pass(x, dy, pair, wr, wg, wu, wd):
    sources, experts, cap, width = x.shape
    hidden = wg.shape[2]
    choices = wr.shape[1]
    group = 2 if sources % 2 == 0 else 1
    rows = sources * cap
    tokens = pl.BlockSpec((group, 1, cap, width), lambda e, s: (s, e, 0, 0))
    wide = pl.BlockSpec((1, width, hidden), lambda e, s: (e, 0, 0))
    tall = pl.BlockSpec((1, hidden, width), lambda e, s: (e, 0, 0))

    def acts(cols):
        return pl.BlockSpec((1, group * cap, cols), lambda e, s: (e, s, 0))

    def act_shape(cols):
        return jax.ShapeDtypeStruct((experts, rows, cols), BF16)

    return pl.pallas_call(
        expert_kernel,
        grid=(experts, sources // group),
        out_shape=(
            jax.ShapeDtypeStruct(x.shape, BF16),
            jax.ShapeDtypeStruct(x.shape, BF16),
            act_shape(width),
            act_shape(hidden),
            act_shape(hidden),
            act_shape(hidden),
            act_shape(choices),
        ),
        in_specs=[
            tokens,
            tokens,
            pl.BlockSpec((group, 1, cap, choices), lambda e, s: (s, e, 0, 0)),
            pl.BlockSpec((width, choices), lambda e, s: (0, 0)),
            wide,
            wide,
            tall,
        ],
        out_specs=(
            tokens, tokens, acts(width), acts(hidden), acts(hidden), acts(hidden), acts(choices)
        ),
        compiler_params=pltpu.CompilerParams(vmem_limit_bytes=VMEM_LIMIT),
        cost_estimate=pl.CostEstimate(
            flops=12 * experts * rows * width * hidden,
            bytes_accessed=10 * experts * rows * width + 6 * experts * hidden * (width + rows),
            transcendentals=experts * rows * hidden,
        ),
        name="expert_pass",
    )(x, dy, pair, wr, wg, wu, wd)


def weight_kernel(*refs):
    count = (len(refs) - 4) // 6
    dwr_ref, dwg_ref, dwu_ref, dwd_ref = refs[-4:]
    totals = [0.0, 0.0, 0.0, 0.0]
    for index in range(count):
        x_ref, g_ref, hid_ref, dga_ref, dup_ref, dlog_ref = refs[6 * index : 6 * index + 6]
        sources, _, cap, width = x_ref.shape
        x = x_ref[...].reshape(sources * cap, width)
        totals[0] = totals[0] + mm_tn(x, dlog_ref[0])
        totals[1] = totals[1] + mm_tn(x, dga_ref[0])
        totals[2] = totals[2] + mm_tn(x, dup_ref[0])
        totals[3] = totals[3] + mm_tn(hid_ref[0], g_ref[0])
    dwr_ref[0] = totals[0]
    dwg_ref[0] = totals[1]
    dwu_ref[0] = totals[2]
    dwd_ref[0] = totals[3]


def weight_pass(kept):
    sources, experts, cap, width = kept[0][0].shape
    rows, hidden = kept[0][2].shape[1:]
    choices = kept[0][5].shape[2]
    block = 256 if width % 256 == 0 else width
    tokens = pl.BlockSpec((sources, 1, cap, block), lambda e, j: (0, e, 0, j))
    grads = pl.BlockSpec((1, rows, block), lambda e, j: (e, 0, j))
    acts = pl.BlockSpec((1, rows, hidden), lambda e, j: (e, 0, 0))
    logs = pl.BlockSpec((1, rows, choices), lambda e, j: (e, 0, 0))
    operands = []
    for arrays in kept:
        operands.extend(arrays)
    return pl.pallas_call(
        weight_kernel,
        grid=(experts, width // block),
        out_shape=(
            jax.ShapeDtypeStruct((experts, width, choices), F32),
            jax.ShapeDtypeStruct((experts, width, hidden), F32),
            jax.ShapeDtypeStruct((experts, width, hidden), F32),
            jax.ShapeDtypeStruct((experts, hidden, width), F32),
        ),
        in_specs=[tokens, grads, acts, acts, acts, logs] * len(kept),
        out_specs=(
            pl.BlockSpec((1, block, choices), lambda e, j: (e, j, 0)),
            pl.BlockSpec((1, block, hidden), lambda e, j: (e, j, 0)),
            pl.BlockSpec((1, block, hidden), lambda e, j: (e, j, 0)),
            pl.BlockSpec((1, hidden, block), lambda e, j: (e, 0, j)),
        ),
        compiler_params=pltpu.CompilerParams(vmem_limit_bytes=VMEM_LIMIT),
        cost_estimate=pl.CostEstimate(
            flops=6 * len(kept) * experts * rows * width * hidden,
            bytes_accessed=len(kept) * experts * rows * (4 * width + 6 * hidden)
            + 12 * experts * width * hidden,
            transcendentals=0,
        ),
        name="weight_pass",
    )(*operands)


def norm_back(grad_out, unit, scale, gain):
    weighted = grad_out * gain
    grad_in = scale * (weighted - unit * jnp.mean(weighted * unit, axis=-1, keepdims=True))
    return grad_in, jnp.sum(grad_out * unit, axis=0)


def shards(
    x_in,
    cotangent,
    segment_ids,
    routes,
    qkv_weight,
    out_weight,
    bias_table,
    attn_gain,
    moe_gain,
    router_weight,
    gate_weight,
    up_weight,
    down_weight,
):
    micro_count, _, shard_len, width = x_in.shape
    slot_count = segment_ids.shape[2]
    head_cols = out_weight.shape[0]
    bucket_count, heads_here = bias_table.shape
    head_size = head_cols // heads_here
    expert_count = router_weight.shape[1]
    experts_here = gate_weight.shape[0]
    devices = expert_count // experts_here
    blocks = slot_count // shard_len
    capacity = max(2, (10 * shard_len + 4 * expert_count - 1) // (4 * expert_count))
    half = min(FIRST_ITEM, slot_count)
    scale = head_size ** (-0.5)
    hidden_index = lax.axis_index("hidden")
    own_start = hidden_index * shard_len
    attn_gain_f = attn_gain.astype(F32)
    moe_gain_f = moe_gain.astype(F32)
    onehot_bucket = bucket_onehot(half, bucket_count)
    line = jnp.einsum(
        "jb,bh->hj", onehot_bucket, bias_table.astype(F32), precision=PRECISE
    )
    bias = position_bias(line, half)
    expert_ids = jnp.arange(expert_count, dtype=jnp.int32)
    place_ids = jnp.arange(expert_count * capacity, dtype=jnp.int32)
    earlier_than = (
        jnp.arange(shard_len, dtype=jnp.int32)[:, None]
        < jnp.arange(shard_len, dtype=jnp.int32)[None, :]
    ).astype(BF16)
    expert_index = lax.axis_index("expert")
    token_shape = (devices, experts_here, blocks * capacity, width)
    flat_shape = (devices, experts_here * blocks * capacity, width)
    place_shape = (expert_count, blocks, capacity, width)

    def own(values):
        return lax.dynamic_slice_in_dim(values, own_start, shard_len, 0)

    def gather(values):
        return lax.all_gather(values, "hidden", axis=0, tiled=True)

    def scatter(values):
        return lax.psum_scatter(values.astype(BF16), "hidden", scatter_dimension=0, tiled=True)

    def exchange(buffer):
        return lax.all_to_all(buffer, "expert", split_axis=0, concat_axis=0, tiled=True)

    def placing():
        route = lax.all_gather(routes[:, 0], "hidden", axis=1, tiled=True)
        route = route.reshape(micro_count, blocks, shard_len, 2)
        live = (segment_ids[:, 0] >= 0).reshape(micro_count, blocks, shard_len)
        chosen = (route[..., None] == expert_ids).astype(F32)
        chosen = chosen * live[..., None, None].astype(F32)
        counted = jnp.sum(chosen, axis=3).astype(BF16)
        before = jnp.einsum("mbte,tu->mbue", counted, earlier_than, preferred_element_type=F32)
        position = jnp.sum(before[:, :, :, None, :] * chosen, axis=-1).astype(jnp.int32)
        place = jnp.where(live[..., None], route * capacity + position, -1)
        other = jnp.full((micro_count, blocks, expert_count * capacity), -1, jnp.int32)
        for k in range(2):
            hit = place[:, :, None, :, k] == place_ids[None, None, :, None]
            found = jnp.max(jnp.where(hit, route[:, :, None, :, 1 - k], -1), axis=-1)
            other = jnp.maximum(other, found)
        other = other.reshape(micro_count, blocks, devices, experts_here, capacity)
        other = exchange(other.transpose(2, 0, 3, 1, 4))
        other = other.transpose(1, 0, 2, 3, 4)
        other = other.reshape(micro_count, devices, experts_here, blocks * capacity)
        me = expert_index * experts_here + jnp.arange(experts_here, dtype=jnp.int32)
        plus = me[None, None, :, None, None] == expert_ids
        minus = other[..., None] == expert_ids
        pair = plus.astype(F32) - minus.astype(F32)
        pair = jnp.where(other[..., None] >= 0, pair, 0.0).astype(BF16)
        place = place.reshape(micro_count, slot_count, 2)
        return place, place.transpose(0, 2, 1), pair

    place_cols, place_rows, pairs = placing()
    all_out_weight = lax.all_gather(out_weight, "hidden", axis=0, tiled=False)

    def send_back(micro, kept):
        dy = gather(cotangent[micro, 0])
        sent = spread_rows(dy, place_rows[micro], expert_count, capacity, shard_len)
        kept["dy"] = exchange(sent.reshape(flat_shape)).reshape(token_shape)

    def attention(micro, kept):
        gathered = gather(x_in[micro, 0])
        x_now = gathered.astype(F32)
        r1 = lax.rsqrt(jnp.mean(x_now * x_now, axis=-1, keepdims=True) + EPSILON)
        xn1 = (x_now * r1 * attn_gain_f).astype(BF16)
        qkv = jnp.einsum("sd,tdf->tsf", xn1, qkv_weight, preferred_element_type=F32).astype(BF16)
        prob, heads_out = attend(qkv, bias, segment_ids[micro, 0], scale)
        all_heads = lax.all_gather(heads_out, "hidden", axis=0, tiled=False)
        kept.update(
            gathered=gathered, r1=r1, xn1=xn1, qkv=qkv, prob=prob, heads=heads_out,
            all_heads=all_heads,
        )

    def send(micro, kept):
        h1, sent = project_and_spread(
            kept["all_heads"], all_out_weight, kept["gathered"], moe_gain_f, place_rows[micro],
            expert_count, capacity, shard_len,
        )
        kept["h1"] = own(h1)
        kept["x"] = exchange(sent.reshape(flat_shape)).reshape(token_shape)

    def experts(micro, kept):
        y, dx, g, hid, dga, dup, dlog = expert_pass(
            kept["x"], kept["dy"], pairs[micro], router_weight, gate_weight, up_weight, down_weight
        )
        kept["weights"] = (kept["x"], g, hid, dga, dup, dlog)
        kept["back_dx"] = exchange(dx.reshape(flat_shape)).reshape(place_shape)
        kept["back_y"] = exchange(y.reshape(flat_shape)).reshape(place_shape)

    def finish(micro, kept):
        mixed = scatter(collect_rows(kept["back_y"], place_cols[micro], shard_len))
        kept["block_out"] = (kept["h1"] + mixed.astype(F32)).astype(BF16)

    def combine(micro, kept):
        dxn2 = scatter(collect_rows(kept["back_dx"], place_cols[micro], shard_len)).astype(F32)
        h1 = kept["h1"]
        r2 = lax.rsqrt(jnp.mean(h1 * h1, axis=-1, keepdims=True) + EPSILON)
        part, kept["moe_gain_grad"] = norm_back(dxn2, h1 * r2, r2, moe_gain_f)
        kept["dh1"] = cotangent[micro, 0].astype(F32) + part
        kept["dattn"] = gather(kept["dh1"].astype(BF16))

    def attention_back(micro, kept):
        dattn = kept["dattn"]
        kept["out_grad"] = mm_tn(kept["heads"], dattn)
        dheads = mm_nt(dattn, out_weight).astype(BF16)
        dproj, bias_line = attend_back(kept["qkv"], kept["prob"], dheads, scale)
        kept["bias_line"] = bias_line
        kept["qkv_grad"] = jnp.einsum(
            "sd,tsf->tdf", kept["xn1"], dproj, preferred_element_type=F32
        )
        dxn1 = jnp.einsum("tsf,tdf->sd", dproj, qkv_weight, preferred_element_type=F32)
        unit = kept["gathered"].astype(F32) * kept["r1"]
        kept["attn_gain_grad"] = jnp.sum(dxn1 * unit, axis=0)
        dxn1 = scatter(dxn1).astype(F32)
        x_own = x_in[micro, 0].astype(F32)
        r1 = lax.rsqrt(jnp.mean(x_own * x_own, axis=-1, keepdims=True) + EPSILON)
        part, _ = norm_back(dxn1, x_own * r1, r1, attn_gain_f)
        kept["x_grad"] = (kept["dh1"] + part).astype(BF16)

    states = [dict() for _ in range(micro_count)]
    for micro in range(micro_count):
        attention(micro, states[micro])
        send_back(micro, states[micro])
        send(micro, states[micro])
        experts(micro, states[micro])
    for micro in range(micro_count):
        combine(micro, states[micro])
        attention_back(micro, states[micro])
        finish(micro, states[micro])
    dwr, dwg, dwu, dwd = weight_pass([state["weights"] for state in states])

    def added(name):
        total = states[0][name]
        for state in states[1:]:
            total = total + state[name]
        return total

    def expert_sum(values):
        shape, count = values.shape, values.size // devices
        pieces = exchange(values.astype(BF16).reshape(devices, count // width, width))
        piece = jnp.sum(pieces.astype(F32), axis=0).astype(BF16)
        whole = lax.all_gather(piece, "expert", axis=0, tiled=True)
        return whole.astype(F32).reshape(shape)

    grad_qkv = expert_sum(added("qkv_grad"))
    grad_out = expert_sum(added("out_grad"))
    grad_table = jnp.einsum("hj,jb->bh", added("bias_line"), onehot_bucket, precision=PRECISE)
    grad_table = lax.psum(grad_table.astype(BF16), "expert").astype(F32)
    grad_router, grad_attn_gain, grad_moe_gain = lax.psum(
        (jnp.sum(dwr, axis=0), added("attn_gain_grad"), added("moe_gain_grad")),
        ("expert", "hidden"),
    )
    return (
        jnp.stack([state["block_out"] for state in states])[:, None],
        jnp.stack([state["x_grad"] for state in states])[:, None],
        grad_qkv,
        grad_out,
        grad_table,
        grad_attn_gain,
        grad_moe_gain,
        grad_router,
        dwg,
        dwu,
        dwd,
    )


def solution(mesh):
    return jax.shard_map(
        shards,
        mesh=mesh,
        in_specs=(
            P(None, "expert", "hidden", None),
            P(None, "expert", "hidden", None),
            P(None, "expert", None),
            P(None, "expert", "hidden", None),
            P(None, None, "hidden"),
            P("hidden", None),
            P(None, "hidden"),
            P(),
            P(),
            P(),
            P("expert", None, "hidden"),
            P("expert", None, "hidden"),
            P("expert", "hidden", None),
        ),
        out_specs=(
            P(None, "expert", "hidden", None),
            P(None, "expert", "hidden", None),
            P(None, None, "hidden"),
            P("hidden", None),
            P(None, "hidden"),
            P(),
            P(),
            P(),
            P("expert", None, "hidden"),
            P("expert", None, "hidden"),
            P("expert", "hidden", None),
        ),
        check_vma=False,
    )
```

```python
import functools

import jax
import jax.numpy as jnp
from jax import lax
from jax.experimental import pallas as pl
from jax.experimental.pallas import tpu as pltpu
from jax.sharding import PartitionSpec as P

EPSILON = 1e-06
PRECISE = lax.Precision.HIGHEST
LIMITS = (12, 16, 23, 32, 46, 64, 91)
MASKED = -1000000000.0
GELU_C = 0.7978845608028654
GELU_A = 0.044715
VMEM_LIMIT = 60 * 1024 * 1024
F32 = jnp.float32
BF16 = jnp.bfloat16


def mm(a, b):
    return lax.dot_general(a, b, (((1,), (0,)), ((), ())), preferred_element_type=F32)


def mm_nt(a, b):
    return lax.dot_general(a, b, (((1,), (1,)), ((), ())), preferred_element_type=F32)


def mm_tn(a, b):
    return lax.dot_general(a, b, (((0,), (0,)), ((), ())), preferred_element_type=F32)


def bucket_of(distance):
    magnitude = jnp.abs(distance)
    far_bucket = jnp.full(magnitude.shape, 8, jnp.int32)
    for threshold in LIMITS:
        far_bucket = far_bucket + (magnitude >= threshold).astype(jnp.int32)
    return jnp.where(magnitude < 8, magnitude, far_bucket) + 16 * (distance > 0).astype(jnp.int32)


def bucket_onehot(half, bucket_count):
    lane = jnp.arange(2 * half, dtype=jnp.int32)
    distance = jnp.where(lane < half, lane, lane - 2 * half)
    return (
        bucket_of(distance)[:, None] == jnp.arange(bucket_count, dtype=jnp.int32)[None, :]
    ).astype(F32)


TILE = 128


def bias_kernel(line_ref, out_ref):
    length = out_ref.shape[2]
    line = jnp.broadcast_to(line_ref[0], (8, length))
    row = lax.broadcasted_iota(jnp.int32, (8, length), 0)
    sheet = line
    for r in range(1, 8):
        sheet = jnp.where(row == r, pltpu.roll(line, r, 1), sheet)
    while sheet.shape[0] < TILE:
        sheet = jnp.concatenate([sheet, pltpu.roll(sheet, sheet.shape[0], 1)], axis=0)
    out_ref[0] = sheet.astype(out_ref.dtype)


def position_bias(line):
    heads, length = line.shape
    return pl.pallas_call(
        bias_kernel,
        grid=(heads,),
        out_shape=jax.ShapeDtypeStruct((heads, TILE, length), BF16),
        in_specs=[pl.BlockSpec((1, 1, length), lambda h: (h, 0, 0))],
        out_specs=pl.BlockSpec((1, TILE, length), lambda h: (h, 0, 0)),
        compiler_params=pltpu.CompilerParams(vmem_limit_bytes=VMEM_LIMIT),
        name="position_bias",
    )(line.reshape(heads, 1, length))


def unit_rows(x):
    x = x.astype(F32)
    return x * lax.rsqrt(jnp.mean(x * x, axis=-1, keepdims=True) + EPSILON)


def attend_kernel(
    scale, x_ref, gain_ref, own_ref, other_ref, bias_ref, seg_row_ref, seg_col_ref,
    qkv_ref, prob_ref, out_ref, xn_ref,
):
    heads, length = bias_ref.shape[0], bias_ref.shape[2]
    half = x_ref.shape[0]
    size = out_ref.shape[1] // heads
    group = pl.program_id(0)

    @pl.when(group == 0)
    def _():
        xn_ref[...] = (unit_rows(x_ref[...]) * gain_ref[...]).astype(BF16)
        for t in range(3):
            qkv_ref[0, t] = mm(xn_ref[...], own_ref[t]).astype(BF16)

    @pl.when(group > 0)
    def _():
        for t in range(3):
            qkv_ref[0, t] = mm(xn_ref[...], other_ref[t]).astype(BF16)

    seg_row = seg_row_ref[...]
    for head in range(heads):
        cols = slice(head * size, (head + 1) * size)
        keys = qkv_ref[0, 1, :, cols]
        values = qkv_ref[0, 2, :, cols]
        for start in range(0, half, TILE):
            rows = slice(start, start + TILE)
            scores = mm_nt(qkv_ref[0, 0, rows, cols], keys) * scale
            shift = bias_ref[head, :, : half - start]
            if start:
                shift = jnp.concatenate([bias_ref[head, :, length - start :], shift], axis=1)
            scores = scores + shift.astype(F32)
            scores = jnp.where(seg_col_ref[rows, :] == seg_row, scores, MASKED)
            top = jnp.max(scores, axis=-1, keepdims=True)
            weights = jnp.exp(scores - top)
            inverse = 1.0 / jnp.sum(weights, axis=-1, keepdims=True)
            prob = (weights * inverse).astype(BF16)
            prob_ref[0, head, rows, :] = prob
            out_ref[rows, cols] = mm(prob, values).astype(BF16)


def attend(x, gain, own_weight, other_weight, bias, seg, scale):
    half, width = x.shape
    cols = own_weight.shape[2]
    groups = 2
    heads = bias.shape[0] // groups
    return pl.pallas_call(
        functools.partial(attend_kernel, scale),
        grid=(groups,),
        out_shape=(
            jax.ShapeDtypeStruct((groups, 3, half, cols), BF16),
            jax.ShapeDtypeStruct((groups, heads, half, half), BF16),
            jax.ShapeDtypeStruct((half, groups * cols), BF16),
        ),
        in_specs=[
            pl.BlockSpec((half, width), lambda p: (0, 0)),
            pl.BlockSpec((1, width), lambda p: (0, 0)),
            pl.BlockSpec((3, width, cols), lambda p: (0, 0, 0)),
            pl.BlockSpec((3, width, cols), lambda p: (0, 0, 0)),
            pl.BlockSpec((heads,) + bias.shape[1:], lambda p: (p, 0, 0)),
            pl.BlockSpec((1, half), lambda p: (0, 0)),
            pl.BlockSpec((half, 1), lambda p: (0, 0)),
        ],
        out_specs=(
            pl.BlockSpec((1, 3, half, cols), lambda p: (p, 0, 0, 0)),
            pl.BlockSpec((1, heads, half, half), lambda p: (p, 0, 0, 0)),
            pl.BlockSpec((half, cols), lambda p: (0, p)),
        ),
        scratch_shapes=[pltpu.VMEM((half, width), BF16)],
        compiler_params=pltpu.CompilerParams(vmem_limit_bytes=VMEM_LIMIT),
        cost_estimate=pl.CostEstimate(
            flops=groups * half * cols * (6 * width + 4 * half),
            bytes_accessed=3 * groups * heads * half * half + 16 * width * cols,
            transcendentals=groups * heads * half * half,
        ),
        name="attend",
    )(x, gain, own_weight, other_weight, bias, seg.reshape(1, half), seg.reshape(half, 1))


def attend_back_kernel(
    scale, x_ref, gain_ref, own_ref, other_ref, qkv_ref, prob_ref, grad_ref,
    dxn_ref, dw_ref, line_ref, dgain_ref, sheet_ref, ds_ref, dproj_ref, xn_ref, total_ref,
):
    heads, half = prob_ref.shape[1], prob_ref.shape[2]
    size = grad_ref.shape[1] // heads
    length = sheet_ref.shape[1]
    group = pl.program_id(0)

    @pl.when(group == 0)
    def _():
        xn_ref[...] = (unit_rows(x_ref[...]) * gain_ref[...]).astype(BF16)

    for head in range(heads):
        cols = slice(head * size, (head + 1) * size)
        values = qkv_ref[0, 2, :, cols]
        sheet_ref[...] = jnp.zeros_like(sheet_ref)
        for start in range(0, half, TILE):
            rows = slice(start, start + TILE)
            prob = prob_ref[0, head, rows, :].astype(F32)
            dprob = mm_nt(grad_ref[rows, cols], values)
            inner = jnp.sum(prob * dprob, axis=-1, keepdims=True)
            dscore = (prob * (dprob - inner)).astype(BF16)
            ds_ref[rows, :] = dscore
            dscore = dscore.astype(F32)
            sheet_ref[:, : half - start] += dscore[:, start:]
            if start:
                sheet_ref[:, length - start :] += dscore[:, :start]
        dscores = ds_ref[...]
        dproj_ref[0, :, cols] = (mm(dscores, qkv_ref[0, 1, :, cols]) * scale).astype(BF16)
        dproj_ref[1, :, cols] = (mm_tn(dscores, qkv_ref[0, 0, :, cols]) * scale).astype(BF16)
        dproj_ref[2, :, cols] = mm_tn(prob_ref[0, head], grad_ref[:, cols]).astype(BF16)
        sheet = sheet_ref[...]
        while sheet.shape[0] > 8:
            upper = sheet.shape[0] // 2
            sheet = sheet[:upper] + pltpu.roll(sheet[upper:], length - upper, 1)
        row = lax.broadcasted_iota(jnp.int32, (8, length), 0)
        line = jnp.zeros((1, length), F32)
        for r in range(8):
            moved = pltpu.roll(sheet, length - r, 1) if r else sheet
            line = line + jnp.sum(jnp.where(row == r, moved, 0.0), axis=0, keepdims=True)
        line_ref[0, head : head + 1, :] = line

    def products(weight_ref):
        dxn = mm_nt(dproj_ref[0], weight_ref[0])
        for t in range(1, 3):
            dxn = dxn + mm_nt(dproj_ref[t], weight_ref[t])
        return dxn

    grads = [mm_tn(xn_ref[...], dproj_ref[t]).astype(BF16) for t in range(3)]
    grads = jnp.concatenate(grads, axis=0)
    dw_ref[...] = grads.reshape(dw_ref.shape)

    @pl.when(group == 0)
    def _():
        total_ref[...] = products(own_ref)

    @pl.when(group > 0)
    def _():
        total = total_ref[...] + products(other_ref)
        dgain_ref[...] = jnp.sum(total * unit_rows(x_ref[...]), axis=0, keepdims=True)
        dxn_ref[...] = total.astype(BF16)


def attend_back(x, gain, own_weight, other_weight, qkv, prob, grad_heads, scale, pieces):
    groups, heads, half = prob.shape[:3]
    width, cols = own_weight.shape[1:]
    length = 2 * half
    return pl.pallas_call(
        functools.partial(attend_back_kernel, scale),
        grid=(groups,),
        out_shape=(
            jax.ShapeDtypeStruct((half, width), BF16),
            jax.ShapeDtypeStruct((pieces, groups, 3 * width // pieces, cols), BF16),
            jax.ShapeDtypeStruct((groups, heads, length), F32),
            jax.ShapeDtypeStruct((1, width), F32),
        ),
        in_specs=[
            pl.BlockSpec((half, width), lambda p: (0, 0)),
            pl.BlockSpec((1, width), lambda p: (0, 0)),
            pl.BlockSpec((3, width, cols), lambda p: (0, 0, 0)),
            pl.BlockSpec((3, width, cols), lambda p: (0, 0, 0)),
            pl.BlockSpec((1, 3, half, cols), lambda p: (p, 0, 0, 0)),
            pl.BlockSpec((1, heads, half, half), lambda p: (p, 0, 0, 0)),
            pl.BlockSpec((half, cols), lambda p: (0, p)),
        ],
        out_specs=(
            pl.BlockSpec((half, width), lambda p: (0, 0)),
            pl.BlockSpec((pieces, 1, 3 * width // pieces, cols), lambda p: (0, p, 0, 0)),
            pl.BlockSpec((1, heads, length), lambda p: (p, 0, 0)),
            pl.BlockSpec((1, width), lambda p: (0, 0)),
        ),
        scratch_shapes=[
            pltpu.VMEM((TILE, length), F32),
            pltpu.VMEM((half, half), BF16),
            pltpu.VMEM((3, half, cols), BF16),
            pltpu.VMEM((half, width), BF16),
            pltpu.VMEM((half, width), F32),
        ],
        compiler_params=pltpu.CompilerParams(vmem_limit_bytes=VMEM_LIMIT),
        cost_estimate=pl.CostEstimate(
            flops=groups * half * cols * (12 * width + 8 * half),
            bytes_accessed=2 * groups * heads * half * half + 24 * width * cols,
            transcendentals=0,
        ),
        name="attend_back",
    )(x, gain, own_weight, other_weight, qkv, prob, grad_heads)


def project_kernel(part_ref, heads_ref, weight_ref, x_ref, gain_ref, h1_ref, xn_ref):
    members, _, both = heads_ref.shape
    cols = weight_ref.shape[1]
    part = part_ref[0]
    h1 = x_ref[...].astype(F32)
    for member in range(members):
        for j in range(both // cols):
            index = lax.rem(part + j, 2) * members + member
            h1 = h1 + mm(heads_ref[member, :, j * cols : (j + 1) * cols], weight_ref[index])
    h1_ref[...] = h1
    xn_ref[...] = (unit_rows(h1) * gain_ref[...]).astype(BF16)


def project(part, heads, weight, x, gain):
    slots, width = x.shape
    whole = pl.BlockSpec(memory_space=pltpu.VMEM)
    return pl.pallas_call(
        project_kernel,
        out_shape=(
            jax.ShapeDtypeStruct((slots, width), F32),
            jax.ShapeDtypeStruct((slots, width), BF16),
        ),
        in_specs=[pl.BlockSpec(memory_space=pltpu.SMEM)] + [whole] * 4,
        out_specs=(whole, whole),
        compiler_params=pltpu.CompilerParams(vmem_limit_bytes=VMEM_LIMIT),
        cost_estimate=pl.CostEstimate(
            flops=2 * slots * width * width,
            bytes_accessed=10 * slots * width + 2 * width * width,
            transcendentals=0,
        ),
        name="project",
    )(part, heads, weight, x, gain)


def turn_kernel(part_ref, grad_ref, h1_ref, dy_ref, gain_ref, weight_ref,
                dh1_ref, dattn_ref, dheads_ref, dgain_ref):
    members, _, both = dheads_ref.shape
    cols = weight_ref.shape[1]
    part = part_ref[0]
    grad = grad_ref[...].astype(F32)
    h1 = h1_ref[...]
    scale = lax.rsqrt(jnp.mean(h1 * h1, axis=-1, keepdims=True) + EPSILON)
    unit = h1 * scale
    dgain_ref[...] = jnp.sum(grad * unit, axis=0, keepdims=True)
    weighted = grad * gain_ref[...]
    inner = jnp.mean(weighted * unit, axis=-1, keepdims=True)
    dh1 = dy_ref[...].astype(F32) + scale * (weighted - unit * inner)
    dh1_ref[...] = dh1
    dattn = dh1.astype(BF16)
    dattn_ref[...] = dattn
    for member in range(members):
        for j in range(both // cols):
            index = lax.rem(part + j, 2) * members + member
            dheads = mm_nt(dattn, weight_ref[index])
            dheads_ref[member, :, j * cols : (j + 1) * cols] = dheads.astype(BF16)


def turn(part, grad, h1, dy, gain, weight, members):
    slots, width = h1.shape
    both = 2 * weight.shape[1]
    whole = pl.BlockSpec(memory_space=pltpu.VMEM)
    return pl.pallas_call(
        turn_kernel,
        out_shape=(
            jax.ShapeDtypeStruct((slots, width), F32),
            jax.ShapeDtypeStruct((slots, width), BF16),
            jax.ShapeDtypeStruct((members, slots, both), BF16),
            jax.ShapeDtypeStruct((1, width), F32),
        ),
        in_specs=[pl.BlockSpec(memory_space=pltpu.SMEM)] + [whole] * 5,
        out_specs=(whole,) * 4,
        compiler_params=pltpu.CompilerParams(vmem_limit_bytes=VMEM_LIMIT),
        cost_estimate=pl.CostEstimate(
            flops=2 * slots * width * width,
            bytes_accessed=16 * slots * width + 2 * width * width,
            transcendentals=0,
        ),
        name="turn",
    )(part, grad, h1, dy, gain, weight)


def spread(rows, place0, place1, count):
    ids = lax.broadcasted_iota(jnp.int32, (count, rows.shape[0]), 0)
    hit = (ids == place0) | (ids == place1)
    return mm(jnp.where(hit, 1.0, 0.0).astype(BF16), rows)


def spread_kernel(rows_ref, place_ref, out_ref):
    experts, _, cap, width = out_ref.shape
    placed = spread(rows_ref[...], place_ref[0:1, :], place_ref[1:2, :], experts * cap)
    out_ref[...] = placed.astype(BF16).reshape(experts, 1, cap, width)


def spread_rows(rows, place, experts, cap, shard_len):
    slots, width = rows.shape
    blocks = slots // shard_len
    return pl.pallas_call(
        spread_kernel,
        grid=(blocks,),
        out_shape=jax.ShapeDtypeStruct((experts, blocks, cap, width), BF16),
        in_specs=[
            pl.BlockSpec((shard_len, width), lambda b: (b, 0)),
            pl.BlockSpec((2, shard_len), lambda b: (0, b)),
        ],
        out_specs=pl.BlockSpec((experts, 1, cap, width), lambda b: (0, b, 0, 0)),
        compiler_params=pltpu.CompilerParams(vmem_limit_bytes=VMEM_LIMIT),
        cost_estimate=pl.CostEstimate(
            flops=2 * experts * cap * slots * width,
            bytes_accessed=2 * slots * width + 2 * experts * blocks * cap * width,
            transcendentals=0,
        ),
        name="spread_rows",
    )(rows, place)


def collect_kernel(rows_ref, place_ref, out_ref):
    experts, _, cap, width = rows_ref.shape
    tokens = out_ref.shape[0]
    ids = lax.broadcasted_iota(jnp.int32, (tokens, experts * cap), 1)
    hit = (ids == place_ref[:, 0:1]) | (ids == place_ref[:, 1:2])
    rows = rows_ref[...].reshape(experts * cap, width)
    out_ref[...] = mm(jnp.where(hit, 1.0, 0.0).astype(BF16), rows).astype(BF16)


def collect_rows(rows, place, shard_len):
    experts, blocks, cap, width = rows.shape
    slots = blocks * shard_len
    return pl.pallas_call(
        collect_kernel,
        grid=(blocks,),
        out_shape=jax.ShapeDtypeStruct((slots, width), BF16),
        in_specs=[
            pl.BlockSpec((experts, 1, cap, width), lambda b: (0, b, 0, 0)),
            pl.BlockSpec((shard_len, 2), lambda b: (b, 0)),
        ],
        out_specs=pl.BlockSpec((shard_len, width), lambda b: (b, 0)),
        compiler_params=pltpu.CompilerParams(vmem_limit_bytes=VMEM_LIMIT),
        cost_estimate=pl.CostEstimate(
            flops=2 * experts * cap * slots * width,
            bytes_accessed=2 * slots * width + 2 * experts * blocks * cap * width,
            transcendentals=0,
        ),
        name="collect_rows",
    )(rows, place)


def expert_kernel(
    x_ref, dy_ref, pair_ref, wr_ref, wg_ref, wu_ref, wd_ref,
    y_ref, dx_ref, g_ref, hid_ref, dga_ref, dup_ref, dlog_ref,
):
    sources, _, cap, width = x_ref.shape
    rows = sources * cap
    x = x_ref[...].reshape(rows, width)
    dy = dy_ref[...].reshape(rows, width).astype(F32)
    pair = pair_ref[...].reshape(rows, pair_ref.shape[3])
    margin = jnp.sum(mm(x, wr_ref[...]) * pair, axis=-1, keepdims=True)
    own_gate = 1.0 / (1.0 + jnp.exp(-margin))
    other_gate = 1.0 / (1.0 + jnp.exp(margin))
    g = (own_gate * dy).astype(BF16)
    g_ref[0] = g
    gate = mm(x, wg_ref[0])
    up = mm(x, wu_ref[0])
    square = gate * gate
    bent = jnp.tanh(GELU_C * gate * (1.0 + GELU_A * square))
    half_gate = 0.5 * gate
    gelu = half_gate * (1.0 + bent)
    slope = 0.5 * (1.0 + bent) + half_gate * (1.0 - bent * bent) * (
        GELU_C * (1.0 + 3.0 * GELU_A * square)
    )
    hid = (gelu * up).astype(BF16)
    dhid = mm_nt(g, wd_ref[0])
    dga = (dhid * (up * slope)).astype(BF16)
    dup = (dhid * gelu).astype(BF16)
    hid_ref[0] = hid
    dga_ref[0] = dga
    dup_ref[0] = dup
    y = mm(hid, wd_ref[0])
    dgate = jnp.sum(y * dy, axis=-1, keepdims=True)
    y_ref[...] = (y * own_gate).astype(BF16).reshape(sources, 1, cap, width)
    dlog = (dgate * own_gate * other_gate * pair).astype(BF16)
    dlog_ref[0] = dlog
    dx = mm_nt(dga, wg_ref[0]) + mm_nt(dup, wu_ref[0]) + mm_nt(dlog, wr_ref[...])
    dx_ref[...] = dx.astype(BF16).reshape(sources, 1, cap, width)


def expert_pass(x, dy, pair, wr, wg, wu, wd):
    sources, experts, cap, width = x.shape
    hidden = wg.shape[2]
    choices = wr.shape[1]
    group = 2 if sources % 2 == 0 else 1
    rows = sources * cap
    tokens = pl.BlockSpec((group, 1, cap, width), lambda e, s: (s, e, 0, 0))
    wide = pl.BlockSpec((1, width, hidden), lambda e, s: (e, 0, 0))
    tall = pl.BlockSpec((1, hidden, width), lambda e, s: (e, 0, 0))

    def acts(cols):
        return pl.BlockSpec((1, group * cap, cols), lambda e, s: (e, s, 0))

    def act_shape(cols):
        return jax.ShapeDtypeStruct((experts, rows, cols), BF16)

    return pl.pallas_call(
        expert_kernel,
        grid=(experts, sources // group),
        out_shape=(
            jax.ShapeDtypeStruct(x.shape, BF16),
            jax.ShapeDtypeStruct(x.shape, BF16),
            act_shape(width),
            act_shape(hidden),
            act_shape(hidden),
            act_shape(hidden),
            act_shape(choices),
        ),
        in_specs=[
            tokens,
            tokens,
            pl.BlockSpec((group, 1, cap, choices), lambda e, s: (s, e, 0, 0)),
            pl.BlockSpec((width, choices), lambda e, s: (0, 0)),
            wide,
            wide,
            tall,
        ],
        out_specs=(
            tokens, tokens, acts(width), acts(hidden), acts(hidden), acts(hidden), acts(choices)
        ),
        compiler_params=pltpu.CompilerParams(vmem_limit_bytes=VMEM_LIMIT),
        cost_estimate=pl.CostEstimate(
            flops=12 * experts * rows * width * hidden,
            bytes_accessed=10 * experts * rows * width + 6 * experts * hidden * (width + rows),
            transcendentals=experts * rows * hidden,
        ),
        name="expert_pass",
    )(x, dy, pair, wr, wg, wu, wd)


def weight_kernel(*refs):
    count = (len(refs) - 4) // 6
    dwr_ref, dwg_ref, dwu_ref, dwd_ref = refs[-4:]
    totals = [0.0, 0.0, 0.0, 0.0]
    for index in range(count):
        x_ref, g_ref, hid_ref, dga_ref, dup_ref, dlog_ref = refs[6 * index : 6 * index + 6]
        sources, _, cap, width = x_ref.shape
        x = x_ref[...].reshape(sources * cap, width)
        totals[0] = totals[0] + mm_tn(x, dlog_ref[0])
        totals[1] = totals[1] + mm_tn(x, dga_ref[0])
        totals[2] = totals[2] + mm_tn(x, dup_ref[0])
        totals[3] = totals[3] + mm_tn(hid_ref[0], g_ref[0])
    dwr_ref[0] = totals[0]
    dwg_ref[0] = totals[1]
    dwu_ref[0] = totals[2]
    dwd_ref[0] = totals[3]


def weight_pass(kept):
    sources, experts, cap, width = kept[0][0].shape
    rows, hidden = kept[0][2].shape[1:]
    choices = kept[0][5].shape[2]
    block = 256 if width % 256 == 0 else width
    tokens = pl.BlockSpec((sources, 1, cap, block), lambda e, j: (0, e, 0, j))
    grads = pl.BlockSpec((1, rows, block), lambda e, j: (e, 0, j))
    acts = pl.BlockSpec((1, rows, hidden), lambda e, j: (e, 0, 0))
    logs = pl.BlockSpec((1, rows, choices), lambda e, j: (e, 0, 0))
    operands = []
    for arrays in kept:
        operands.extend(arrays)
    return pl.pallas_call(
        weight_kernel,
        grid=(experts, width // block),
        out_shape=(
            jax.ShapeDtypeStruct((experts, width, choices), F32),
            jax.ShapeDtypeStruct((experts, width, hidden), F32),
            jax.ShapeDtypeStruct((experts, width, hidden), F32),
            jax.ShapeDtypeStruct((experts, hidden, width), F32),
        ),
        in_specs=[tokens, grads, acts, acts, acts, logs] * len(kept),
        out_specs=(
            pl.BlockSpec((1, block, choices), lambda e, j: (e, j, 0)),
            pl.BlockSpec((1, block, hidden), lambda e, j: (e, j, 0)),
            pl.BlockSpec((1, block, hidden), lambda e, j: (e, j, 0)),
            pl.BlockSpec((1, hidden, block), lambda e, j: (e, 0, j)),
        ),
        compiler_params=pltpu.CompilerParams(vmem_limit_bytes=VMEM_LIMIT),
        cost_estimate=pl.CostEstimate(
            flops=6 * len(kept) * experts * rows * width * hidden,
            bytes_accessed=len(kept) * experts * rows * (4 * width + 6 * hidden)
            + 12 * experts * width * hidden,
            transcendentals=0,
        ),
        name="weight_pass",
    )(*operands)


def after(values, *others):
    return lax.optimization_barrier((values,) + others)[0]


def shards(
    x_in,
    cotangent,
    segment_ids,
    routes,
    qkv_weight,
    out_weight,
    bias_table,
    attn_gain,
    moe_gain,
    router_weight,
    gate_weight,
    up_weight,
    down_weight,
):
    micro_count, _, shard_len, width = x_in.shape
    slot_count = segment_ids.shape[2]
    head_cols = out_weight.shape[0]
    bucket_count, heads_here = bias_table.shape
    head_size = head_cols // heads_here
    expert_count = router_weight.shape[1]
    experts_here = gate_weight.shape[0]
    devices = expert_count // experts_here
    blocks = slot_count // shard_len
    members = blocks // 2
    half = slot_count // 2
    capacity = max(2, (10 * shard_len + 4 * expert_count - 1) // (4 * expert_count))
    scale = head_size ** (-0.5)
    hidden_index = lax.axis_index("hidden")
    expert_index = lax.axis_index("expert")
    part = hidden_index // members
    part_ref = part.reshape(1).astype(jnp.int32)
    attn_gain_f = attn_gain.astype(F32).reshape(1, width)
    moe_gain_f = moe_gain.astype(F32).reshape(1, width)
    token_shape = (devices, experts_here, blocks * capacity, width)
    flat_shape = (devices, experts_here * blocks * capacity, width)
    place_shape = (expert_count, blocks, capacity, width)
    half_groups = [list(range(p * members, (p + 1) * members)) for p in range(2)]
    across = [(z, (z + members) % blocks) for z in range(blocks)]

    def exchange(buffer):
        return lax.all_to_all(buffer, "expert", split_axis=0, concat_axis=0, tiled=True)

    def to_all(values, axis, count, groups=None):
        copies = jnp.broadcast_to(values[None], (count,) + values.shape)
        return lax.all_to_all(
            copies, axis, split_axis=0, concat_axis=0, tiled=True, axis_index_groups=groups
        )

    def swap_half(buffer):
        return lax.all_to_all(
            buffer, "hidden", split_axis=0, concat_axis=0, tiled=True,
            axis_index_groups=half_groups,
        )

    def gather(values):
        return lax.all_gather(values, "hidden", axis=0, tiled=True)

    def scatter(values):
        return lax.psum_scatter(values.astype(BF16), "hidden", scatter_dimension=0, tiled=True)

    def my_piece(flat):
        rows = flat.shape[0] // devices
        return lax.dynamic_slice_in_dim(flat, expert_index * rows, rows, 0)

    def placing():
        expert_ids = jnp.arange(expert_count, dtype=jnp.int32)
        place_ids = jnp.arange(expert_count * capacity, dtype=jnp.int32)
        slot = jnp.arange(shard_len, dtype=jnp.int32)
        earlier_than = (slot[:, None] < slot[None, :]).astype(BF16)
        route = to_all(routes[:, 0], "hidden", blocks)
        route = route.transpose(1, 0, 2, 3)
        live = (segment_ids[:, 0] >= 0).reshape(micro_count, blocks, shard_len)
        chosen = (route[..., None] == expert_ids).astype(F32)
        chosen = chosen * live[..., None, None].astype(F32)
        counted = jnp.sum(chosen, axis=3).astype(BF16)
        before = jnp.einsum("mbte,tu->mbue", counted, earlier_than, preferred_element_type=F32)
        position = jnp.sum(before[:, :, :, None, :] * chosen, axis=-1).astype(jnp.int32)
        place = jnp.where(live[..., None], route * capacity + position, -1)
        other = jnp.full((micro_count, blocks, expert_count * capacity), -1, jnp.int32)
        for k in range(2):
            hit = place[:, :, None, :, k] == place_ids[None, None, :, None]
            found = jnp.max(jnp.where(hit, route[:, :, None, :, 1 - k], -1), axis=-1)
            other = jnp.maximum(other, found)
        other = other.reshape(micro_count, blocks, devices, experts_here, capacity)
        other = exchange(other.transpose(2, 0, 3, 1, 4))
        other = other.transpose(1, 0, 2, 3, 4)
        other = other.reshape(micro_count, devices, experts_here, blocks * capacity)
        me = expert_index * experts_here + jnp.arange(experts_here, dtype=jnp.int32)
        plus = me[None, None, :, None, None] == expert_ids
        minus = other[..., None] == expert_ids
        pair = plus.astype(F32) - minus.astype(F32)
        pair = jnp.where(other[..., None] >= 0, pair, 0.0).astype(BF16)
        place = place.reshape(micro_count, slot_count, 2)
        return place, place.transpose(0, 2, 1), pair

    states = [dict() for _ in range(micro_count)]

    piece = lax.ppermute(my_piece(qkv_weight.reshape(3 * width, head_cols)), "hidden", across)
    other_qkv = to_all(piece, "expert", devices).reshape(qkv_weight.shape)
    piece = to_all(my_piece(out_weight), "hidden", blocks)
    all_out = to_all(piece, "expert", devices)
    all_out = all_out.transpose(1, 0, 2, 3).reshape(blocks, head_cols, width)
    tables = jnp.concatenate(
        [bias_table, lax.ppermute(bias_table, "hidden", across)], axis=1
    ).astype(F32)
    onehot_bucket = bucket_onehot(half, bucket_count)
    bias = position_bias(jnp.einsum("jb,bh->hj", onehot_bucket, tables, precision=PRECISE))
    place_cols, place_rows, pairs = placing()

    def pair_x(micro, kept):
        kept["x_half"] = to_all(x_in[micro, 0], "hidden", members, half_groups).reshape(half, width)

    def attention(micro, kept):
        seg = lax.dynamic_slice_in_dim(segment_ids[micro, 0], part * half, half, 0)
        qkv, prob, heads = attend(
            kept["x_half"], attn_gain_f, qkv_weight, other_qkv, bias, seg, scale
        )
        kept.update(qkv=qkv, prob=prob, heads=heads)
        own_heads = swap_half(heads.reshape(members, shard_len, 2 * head_cols))
        kept["h1"], kept["xn2"] = project(part_ref, own_heads, all_out, x_in[micro, 0], moe_gain_f)

    def spread(rows, micro):
        sent = spread_rows(rows, place_rows[micro], expert_count, capacity, shard_len)
        return sent.reshape(flat_shape)

    def experts(micro, kept):
        y, dx, g, hid, dga, dup, dlog = expert_pass(
            kept["x"], kept["dy"], pairs[micro], router_weight, gate_weight, up_weight, down_weight
        )
        kept["weights"] = (kept["x"], g, hid, dga, dup, dlog)
        kept["y_sent"] = y.reshape(flat_shape)
        kept["dx_sent"] = dx.reshape(flat_shape)

    def combine(micro, kept):
        part_sum = collect_rows(kept["dx_back"], place_cols[micro], shard_len)
        kept["dxn2"] = scatter(part_sum)

    def attention_back(micro, kept):
        dh1, dattn, dheads, kept["moe_gain_grad"] = turn(
            part_ref, kept["dxn2"], kept["h1"], cotangent[micro, 0], moe_gain_f, all_out, members
        )
        dheads = swap_half(dheads).reshape(half, 2 * head_cols)
        dattn = to_all(dattn, "hidden", members, half_groups).reshape(half, width)
        dxn1, kept["qkv_grad"], kept["line"], kept["attn_gain_grad"] = attend_back(
            kept["x_half"], attn_gain_f, qkv_weight, other_qkv, kept["qkv"], kept["prob"], dheads,
            scale, devices,
        )
        kept["dxn1"] = dxn1
        kept["out_grad"] = mm_tn(kept["heads"], dattn).astype(BF16)
        dxn1 = swap_half(dxn1.reshape(members, shard_len, width))
        dxn1 = jnp.sum(dxn1.astype(F32), axis=0)
        x_own = x_in[micro, 0].astype(F32)
        r1 = lax.rsqrt(jnp.mean(x_own * x_own, axis=-1, keepdims=True) + EPSILON)
        unit = x_own * r1
        weighted = dxn1 * attn_gain_f
        inner = jnp.mean(weighted * unit, axis=-1, keepdims=True)
        kept["x_grad"] = (dh1 + r1 * (weighted - unit * inner)).astype(BF16)

    def finish(micro, kept):
        mixed = scatter(collect_rows(kept["y_back"], place_cols[micro], shard_len))
        kept["block_out"] = (kept["h1"] + mixed.astype(F32)).astype(BF16)

    first, last = states[0], states[-1]
    for micro in range(micro_count):
        pair_x(micro, states[micro])
    first["dy_all"] = gather(cotangent[0, 0])
    attention(0, first)
    first["dy"] = exchange(spread(first["dy_all"], 0)).reshape(token_shape)
    first["xn2_all"] = gather(first["xn2"])
    first["x"] = exchange(spread(first["xn2_all"], 0)).reshape(token_shape)
    behind = first["xn2_all"]
    for micro in range(1, micro_count):
        state = states[micro]
        attention(micro, state)
        state["xn2_all"] = gather(after(state["xn2"], behind))
        state["x"] = exchange(spread(state["xn2_all"], micro)).reshape(token_shape)
        state["dy_all"] = gather(after(cotangent[micro, 0], state["xn2_all"]))
        state["dy"] = exchange(spread(state["dy_all"], micro)).reshape(token_shape)
        behind = state["dy_all"]
    for micro in range(micro_count):
        state = states[micro]
        experts(micro, state)
        sent = state["dx_sent"]
        if micro + 1 < micro_count:
            sent = after(sent, states[micro + 1]["dy"])
        state["dx_back"] = exchange(sent).reshape(place_shape)
    for micro in range(micro_count):
        state = states[micro]
        state["y_back"] = exchange(after(state["y_sent"], last["dx_back"])).reshape(place_shape)
    for micro in range(micro_count):
        combine(micro, states[micro])
        attention_back(micro, states[micro])
    for micro in range(micro_count):
        finish(micro, states[micro])
    kept = [state["weights"] for state in states]
    kept[-1] = tuple(after(list(kept[-1]), last["dxn1"]))
    dwr, dwg, dwu, dwd = weight_pass(kept)

    def added(name):
        total = states[0][name].astype(F32)
        for state in states[1:]:
            total = total + state[name].astype(F32)
        return total

    def both_halves(pieces):
        total = jnp.sum(pieces.astype(F32), axis=0)
        moved = lax.ppermute(total[1].astype(BF16), "hidden", across)
        piece = (total[0] + moved.astype(F32)).astype(BF16)
        return to_all(piece, "expert", devices)

    grad_qkv = both_halves(exchange(added("qkv_grad").astype(BF16)))
    grad_qkv = grad_qkv.astype(F32).reshape(qkv_weight.shape)
    grad_out = added("out_grad").astype(BF16).reshape(2, devices, head_cols // devices, width)
    grad_out = both_halves(exchange(grad_out.transpose(1, 0, 2, 3)))
    grad_out = grad_out.astype(F32).reshape(out_weight.shape)
    lines = added("line").reshape(2 * heads_here, 2 * half)
    table = jnp.einsum("hj,jb->hb", lines, onehot_bucket, precision=PRECISE)
    table = table.reshape(2, heads_here * bucket_count)
    mine = jnp.arange(blocks, dtype=jnp.int32)[:, None]
    table = jnp.where(mine == hidden_index, table[0], 0.0) + jnp.where(
        mine == (hidden_index + members) % blocks, table[1], 0.0
    )
    small = jnp.concatenate(
        [
            jnp.sum(dwr, axis=0).reshape(-1),
            added("attn_gain_grad").reshape(-1),
            added("moe_gain_grad").reshape(-1),
            table.reshape(-1),
        ]
    ).reshape(-1, 128)
    small = jnp.sum(to_all(small, "expert", devices), axis=0)
    small = jnp.sum(to_all(small, "hidden", blocks), axis=0).reshape(-1)
    sizes = (width * expert_count, width, width)
    grad_router = small[: sizes[0]].reshape(width, expert_count)
    grad_attn_gain = small[sizes[0] : sizes[0] + width]
    grad_moe_gain = small[sizes[0] + width : sizes[0] + 2 * width]
    table = small[sizes[0] + 2 * width :].reshape(blocks, heads_here, bucket_count)
    grad_table = lax.dynamic_index_in_dim(table, hidden_index, 0, keepdims=False).T
    return (
        jnp.stack([state["block_out"] for state in states])[:, None],
        jnp.stack([state["x_grad"] for state in states])[:, None],
        grad_qkv,
        grad_out,
        grad_table,
        grad_attn_gain,
        grad_moe_gain,
        grad_router,
        dwg,
        dwu,
        dwd,
    )


def solution(mesh):
    return jax.shard_map(
        shards,
        mesh=mesh,
        in_specs=(
            P(None, "expert", "hidden", None),
            P(None, "expert", "hidden", None),
            P(None, "expert", None),
            P(None, "expert", "hidden", None),
            P(None, None, "hidden"),
            P("hidden", None),
            P(None, "hidden"),
            P(),
            P(),
            P(),
            P("expert", None, "hidden"),
            P("expert", None, "hidden"),
            P("expert", "hidden", None),
        ),
        out_specs=(
            P(None, "expert", "hidden", None),
            P(None, "expert", "hidden", None),
            P(None, None, "hidden"),
            P("hidden", None),
            P(None, "hidden"),
            P(),
            P(),
            P(),
            P("expert", None, "hidden"),
            P("expert", None, "hidden"),
            P("expert", "hidden", None),
        ),
        check_vma=False,
    )
```

```python
import functools

import jax
import jax.numpy as jnp
from jax import lax
from jax.experimental import pallas as pl
from jax.experimental.pallas import tpu as pltpu
from jax.sharding import PartitionSpec as P

EPSILON = 1e-06
PRECISE = lax.Precision.HIGHEST
LIMITS = (12, 16, 23, 32, 46, 64, 91)
MASKED = -1000000000.0
GELU_C = 0.7978845608028654
GELU_A = 0.044715
VMEM_LIMIT = 60 * 1024 * 1024
F32 = jnp.float32
BF16 = jnp.bfloat16


def mm(a, b):
    return lax.dot_general(a, b, (((1,), (0,)), ((), ())), preferred_element_type=F32)


def mm_nt(a, b):
    return lax.dot_general(a, b, (((1,), (1,)), ((), ())), preferred_element_type=F32)


def mm_tn(a, b):
    return lax.dot_general(a, b, (((0,), (0,)), ((), ())), preferred_element_type=F32)


def bucket_of(distance):
    magnitude = jnp.abs(distance)
    far_bucket = jnp.full(magnitude.shape, 8, jnp.int32)
    for threshold in LIMITS:
        far_bucket = far_bucket + (magnitude >= threshold).astype(jnp.int32)
    return jnp.where(magnitude < 8, magnitude, far_bucket) + 16 * (distance > 0).astype(jnp.int32)


def bucket_onehot(half, bucket_count):
    lane = jnp.arange(2 * half, dtype=jnp.int32)
    distance = jnp.where(lane < half, lane, lane - 2 * half)
    return (
        bucket_of(distance)[:, None] == jnp.arange(bucket_count, dtype=jnp.int32)[None, :]
    ).astype(F32)


TILE = 128


def bias_kernel(line_ref, out_ref):
    length = out_ref.shape[2]
    line = jnp.broadcast_to(line_ref[0], (8, length))
    row = lax.broadcasted_iota(jnp.int32, (8, length), 0)
    sheet = line
    for r in range(1, 8):
        sheet = jnp.where(row == r, pltpu.roll(line, r, 1), sheet)
    while sheet.shape[0] < TILE:
        sheet = jnp.concatenate([sheet, pltpu.roll(sheet, sheet.shape[0], 1)], axis=0)
    out_ref[0] = sheet.astype(out_ref.dtype)


def position_bias(line):
    heads, length = line.shape
    return pl.pallas_call(
        bias_kernel,
        grid=(heads,),
        out_shape=jax.ShapeDtypeStruct((heads, TILE, length), BF16),
        in_specs=[pl.BlockSpec((1, 1, length), lambda h: (h, 0, 0))],
        out_specs=pl.BlockSpec((1, TILE, length), lambda h: (h, 0, 0)),
        compiler_params=pltpu.CompilerParams(vmem_limit_bytes=VMEM_LIMIT),
        name="position_bias",
    )(line.reshape(heads, 1, length))


def unit_rows(x):
    x = x.astype(F32)
    return x * lax.rsqrt(jnp.mean(x * x, axis=-1, keepdims=True) + EPSILON)


def attend_kernel(
    scale, x_ref, gain_ref, own_ref, other_ref, bias_ref, seg_row_ref, seg_col_ref,
    qkv_ref, prob_ref, out_ref, xn_ref,
):
    heads, length = bias_ref.shape[0], bias_ref.shape[2]
    half = x_ref.shape[0]
    size = out_ref.shape[1] // heads
    group = pl.program_id(0)

    @pl.when(group == 0)
    def _():
        xn_ref[...] = (unit_rows(x_ref[...]) * gain_ref[...]).astype(BF16)
        for t in range(3):
            qkv_ref[0, t] = mm(xn_ref[...], own_ref[t]).astype(BF16)

    @pl.when(group > 0)
    def _():
        for t in range(3):
            qkv_ref[0, t] = mm(xn_ref[...], other_ref[t]).astype(BF16)

    seg_row = seg_row_ref[...]
    for head in range(heads):
        cols = slice(head * size, (head + 1) * size)
        keys = qkv_ref[0, 1, :, cols]
        values = qkv_ref[0, 2, :, cols]
        for start in range(0, half, TILE):
            rows = slice(start, start + TILE)
            scores = mm_nt(qkv_ref[0, 0, rows, cols], keys) * scale
            shift = bias_ref[head, :, : half - start]
            if start:
                shift = jnp.concatenate([bias_ref[head, :, length - start :], shift], axis=1)
            scores = scores + shift.astype(F32)
            scores = jnp.where(seg_col_ref[rows, :] == seg_row, scores, MASKED)
            top = jnp.max(scores, axis=-1, keepdims=True)
            weights = jnp.exp(scores - top)
            inverse = 1.0 / jnp.sum(weights, axis=-1, keepdims=True)
            prob = (weights * inverse).astype(BF16)
            prob_ref[0, head, rows, :] = prob
            out_ref[rows, cols] = mm(prob, values).astype(BF16)


def attend(x, gain, own_weight, other_weight, bias, seg, scale):
    half, width = x.shape
    cols = own_weight.shape[2]
    groups = 2
    heads = bias.shape[0] // groups
    return pl.pallas_call(
        functools.partial(attend_kernel, scale),
        grid=(groups,),
        out_shape=(
            jax.ShapeDtypeStruct((groups, 3, half, cols), BF16),
            jax.ShapeDtypeStruct((groups, heads, half, half), BF16),
            jax.ShapeDtypeStruct((half, groups * cols), BF16),
        ),
        in_specs=[
            pl.BlockSpec((half, width), lambda p: (0, 0)),
            pl.BlockSpec((1, width), lambda p: (0, 0)),
            pl.BlockSpec((3, width, cols), lambda p: (0, 0, 0)),
            pl.BlockSpec((3, width, cols), lambda p: (0, 0, 0)),
            pl.BlockSpec((heads,) + bias.shape[1:], lambda p: (p, 0, 0)),
            pl.BlockSpec((1, half), lambda p: (0, 0)),
            pl.BlockSpec((half, 1), lambda p: (0, 0)),
        ],
        out_specs=(
            pl.BlockSpec((1, 3, half, cols), lambda p: (p, 0, 0, 0)),
            pl.BlockSpec((1, heads, half, half), lambda p: (p, 0, 0, 0)),
            pl.BlockSpec((half, cols), lambda p: (0, p)),
        ),
        scratch_shapes=[pltpu.VMEM((half, width), BF16)],
        compiler_params=pltpu.CompilerParams(vmem_limit_bytes=VMEM_LIMIT),
        cost_estimate=pl.CostEstimate(
            flops=groups * half * cols * (6 * width + 4 * half),
            bytes_accessed=3 * groups * heads * half * half + 16 * width * cols,
            transcendentals=groups * heads * half * half,
        ),
        name="attend",
    )(x, gain, own_weight, other_weight, bias, seg.reshape(1, half), seg.reshape(half, 1))


def attend_back_kernel(
    scale, x_ref, gain_ref, own_ref, other_ref, qkv_ref, prob_ref, grad_ref,
    dxn_ref, dw_ref, line_ref, dgain_ref, sheet_ref, ds_ref, dproj_ref, xn_ref, total_ref,
):
    heads, half = prob_ref.shape[1], prob_ref.shape[2]
    size = grad_ref.shape[1] // heads
    length = sheet_ref.shape[1]
    group = pl.program_id(0)

    @pl.when(group == 0)
    def _():
        xn_ref[...] = (unit_rows(x_ref[...]) * gain_ref[...]).astype(BF16)

    for head in range(heads):
        cols = slice(head * size, (head + 1) * size)
        values = qkv_ref[0, 2, :, cols]
        sheet_ref[...] = jnp.zeros_like(sheet_ref)
        for start in range(0, half, TILE):
            rows = slice(start, start + TILE)
            prob = prob_ref[0, head, rows, :].astype(F32)
            dprob = mm_nt(grad_ref[rows, cols], values)
            inner = jnp.sum(prob * dprob, axis=-1, keepdims=True)
            dscore = (prob * (dprob - inner)).astype(BF16)
            ds_ref[rows, :] = dscore
            dscore = dscore.astype(F32)
            sheet_ref[:, : half - start] += dscore[:, start:]
            if start:
                sheet_ref[:, length - start :] += dscore[:, :start]
        dscores = ds_ref[...]
        dproj_ref[0, :, cols] = (mm(dscores, qkv_ref[0, 1, :, cols]) * scale).astype(BF16)
        dproj_ref[1, :, cols] = (mm_tn(dscores, qkv_ref[0, 0, :, cols]) * scale).astype(BF16)
        dproj_ref[2, :, cols] = mm_tn(prob_ref[0, head], grad_ref[:, cols]).astype(BF16)
        sheet = sheet_ref[...]
        while sheet.shape[0] > 8:
            upper = sheet.shape[0] // 2
            sheet = sheet[:upper] + pltpu.roll(sheet[upper:], length - upper, 1)
        row = lax.broadcasted_iota(jnp.int32, (8, length), 0)
        line = jnp.zeros((1, length), F32)
        for r in range(8):
            moved = pltpu.roll(sheet, length - r, 1) if r else sheet
            line = line + jnp.sum(jnp.where(row == r, moved, 0.0), axis=0, keepdims=True)
        line_ref[0, head : head + 1, :] = line

    def products(weight_ref):
        dxn = mm_nt(dproj_ref[0], weight_ref[0])
        for t in range(1, 3):
            dxn = dxn + mm_nt(dproj_ref[t], weight_ref[t])
        return dxn

    grads = [mm_tn(xn_ref[...], dproj_ref[t]).astype(BF16) for t in range(3)]
    grads = jnp.concatenate(grads, axis=0)
    dw_ref[...] = grads.reshape(dw_ref.shape)

    @pl.when(group == 0)
    def _():
        total_ref[...] = products(own_ref)

    @pl.when(group > 0)
    def _():
        total = total_ref[...] + products(other_ref)
        dgain_ref[...] = jnp.sum(total * unit_rows(x_ref[...]), axis=0, keepdims=True)
        dxn_ref[...] = total.astype(BF16)


def attend_back(x, gain, own_weight, other_weight, qkv, prob, grad_heads, scale, pieces):
    groups, heads, half = prob.shape[:3]
    width, cols = own_weight.shape[1:]
    length = 2 * half
    return pl.pallas_call(
        functools.partial(attend_back_kernel, scale),
        grid=(groups,),
        out_shape=(
            jax.ShapeDtypeStruct((half, width), BF16),
            jax.ShapeDtypeStruct((pieces, groups, 3 * width // pieces, cols), BF16),
            jax.ShapeDtypeStruct((groups, heads, length), F32),
            jax.ShapeDtypeStruct((1, width), F32),
        ),
        in_specs=[
            pl.BlockSpec((half, width), lambda p: (0, 0)),
            pl.BlockSpec((1, width), lambda p: (0, 0)),
            pl.BlockSpec((3, width, cols), lambda p: (0, 0, 0)),
            pl.BlockSpec((3, width, cols), lambda p: (0, 0, 0)),
            pl.BlockSpec((1, 3, half, cols), lambda p: (p, 0, 0, 0)),
            pl.BlockSpec((1, heads, half, half), lambda p: (p, 0, 0, 0)),
            pl.BlockSpec((half, cols), lambda p: (0, p)),
        ],
        out_specs=(
            pl.BlockSpec((half, width), lambda p: (0, 0)),
            pl.BlockSpec((pieces, 1, 3 * width // pieces, cols), lambda p: (0, p, 0, 0)),
            pl.BlockSpec((1, heads, length), lambda p: (p, 0, 0)),
            pl.BlockSpec((1, width), lambda p: (0, 0)),
        ),
        scratch_shapes=[
            pltpu.VMEM((TILE, length), F32),
            pltpu.VMEM((half, half), BF16),
            pltpu.VMEM((3, half, cols), BF16),
            pltpu.VMEM((half, width), BF16),
            pltpu.VMEM((half, width), F32),
        ],
        compiler_params=pltpu.CompilerParams(vmem_limit_bytes=VMEM_LIMIT),
        cost_estimate=pl.CostEstimate(
            flops=groups * half * cols * (12 * width + 8 * half),
            bytes_accessed=2 * groups * heads * half * half + 24 * width * cols,
            transcendentals=0,
        ),
        name="attend_back",
    )(x, gain, own_weight, other_weight, qkv, prob, grad_heads)


def project_kernel(part_ref, heads_ref, weight_ref, x_ref, gain_ref, h1_ref, xn_ref):
    members, _, both = heads_ref.shape
    cols = weight_ref.shape[1]
    part = part_ref[0]
    h1 = x_ref[...].astype(F32)
    for member in range(members):
        for j in range(both // cols):
            index = lax.rem(part + j, 2) * members + member
            h1 = h1 + mm(heads_ref[member, :, j * cols : (j + 1) * cols], weight_ref[index])
    h1_ref[...] = h1
    xn_ref[...] = (unit_rows(h1) * gain_ref[...]).astype(BF16)


def project(part, heads, weight, x, gain):
    slots, width = x.shape
    whole = pl.BlockSpec(memory_space=pltpu.VMEM)
    return pl.pallas_call(
        project_kernel,
        out_shape=(
            jax.ShapeDtypeStruct((slots, width), F32),
            jax.ShapeDtypeStruct((slots, width), BF16),
        ),
        in_specs=[pl.BlockSpec(memory_space=pltpu.SMEM)] + [whole] * 4,
        out_specs=(whole, whole),
        compiler_params=pltpu.CompilerParams(vmem_limit_bytes=VMEM_LIMIT),
        cost_estimate=pl.CostEstimate(
            flops=2 * slots * width * width,
            bytes_accessed=10 * slots * width + 2 * width * width,
            transcendentals=0,
        ),
        name="project",
    )(part, heads, weight, x, gain)


def turn_kernel(part_ref, grad_ref, h1_ref, dy_ref, gain_ref, weight_ref,
                dh1_ref, dattn_ref, dheads_ref, dgain_ref):
    members, _, both = dheads_ref.shape
    cols = weight_ref.shape[1]
    part = part_ref[0]
    grad = grad_ref[...].astype(F32)
    h1 = h1_ref[...]
    scale = lax.rsqrt(jnp.mean(h1 * h1, axis=-1, keepdims=True) + EPSILON)
    unit = h1 * scale
    dgain_ref[...] = jnp.sum(grad * unit, axis=0, keepdims=True)
    weighted = grad * gain_ref[...]
    inner = jnp.mean(weighted * unit, axis=-1, keepdims=True)
    dh1 = dy_ref[...].astype(F32) + scale * (weighted - unit * inner)
    dh1_ref[...] = dh1
    dattn = dh1.astype(BF16)
    dattn_ref[...] = dattn
    for member in range(members):
        for j in range(both // cols):
            index = lax.rem(part + j, 2) * members + member
            dheads = mm_nt(dattn, weight_ref[index])
            dheads_ref[member, :, j * cols : (j + 1) * cols] = dheads.astype(BF16)


def turn(part, grad, h1, dy, gain, weight, members):
    slots, width = h1.shape
    both = 2 * weight.shape[1]
    whole = pl.BlockSpec(memory_space=pltpu.VMEM)
    return pl.pallas_call(
        turn_kernel,
        out_shape=(
            jax.ShapeDtypeStruct((slots, width), F32),
            jax.ShapeDtypeStruct((slots, width), BF16),
            jax.ShapeDtypeStruct((members, slots, both), BF16),
            jax.ShapeDtypeStruct((1, width), F32),
        ),
        in_specs=[pl.BlockSpec(memory_space=pltpu.SMEM)] + [whole] * 5,
        out_specs=(whole,) * 4,
        compiler_params=pltpu.CompilerParams(vmem_limit_bytes=VMEM_LIMIT),
        cost_estimate=pl.CostEstimate(
            flops=2 * slots * width * width,
            bytes_accessed=16 * slots * width + 2 * width * width,
            transcendentals=0,
        ),
        name="turn",
    )(part, grad, h1, dy, gain, weight)


def spread(rows, place0, place1, count):
    ids = lax.broadcasted_iota(jnp.int32, (count, rows.shape[0]), 0)
    hit = (ids == place0) | (ids == place1)
    return mm(jnp.where(hit, 1.0, 0.0).astype(BF16), rows)


def spread_kernel(rows_ref, place_ref, out_ref):
    experts, _, cap, width = out_ref.shape
    placed = spread(rows_ref[...], place_ref[0:1, :], place_ref[1:2, :], experts * cap)
    out_ref[...] = placed.astype(BF16).reshape(experts, 1, cap, width)


def spread_rows(rows, place, experts, cap, shard_len):
    slots, width = rows.shape
    blocks = slots // shard_len
    return pl.pallas_call(
        spread_kernel,
        grid=(blocks,),
        out_shape=jax.ShapeDtypeStruct((experts, blocks, cap, width), BF16),
        in_specs=[
            pl.BlockSpec((shard_len, width), lambda b: (b, 0)),
            pl.BlockSpec((2, shard_len), lambda b: (0, b)),
        ],
        out_specs=pl.BlockSpec((experts, 1, cap, width), lambda b: (0, b, 0, 0)),
        compiler_params=pltpu.CompilerParams(vmem_limit_bytes=VMEM_LIMIT),
        cost_estimate=pl.CostEstimate(
            flops=2 * experts * cap * slots * width,
            bytes_accessed=2 * slots * width + 2 * experts * blocks * cap * width,
            transcendentals=0,
        ),
        name="spread_rows",
    )(rows, place)


def collect_kernel(rows_ref, place_ref, out_ref):
    experts, _, cap, width = rows_ref.shape
    tokens = out_ref.shape[0]
    ids = lax.broadcasted_iota(jnp.int32, (tokens, experts * cap), 1)
    hit = (ids == place_ref[:, 0:1]) | (ids == place_ref[:, 1:2])
    rows = rows_ref[...].reshape(experts * cap, width)
    out_ref[...] = mm(jnp.where(hit, 1.0, 0.0).astype(BF16), rows).astype(BF16)


def collect_rows(rows, place, shard_len):
    experts, blocks, cap, width = rows.shape
    slots = blocks * shard_len
    return pl.pallas_call(
        collect_kernel,
        grid=(blocks,),
        out_shape=jax.ShapeDtypeStruct((slots, width), BF16),
        in_specs=[
            pl.BlockSpec((experts, 1, cap, width), lambda b: (0, b, 0, 0)),
            pl.BlockSpec((shard_len, 2), lambda b: (b, 0)),
        ],
        out_specs=pl.BlockSpec((shard_len, width), lambda b: (b, 0)),
        compiler_params=pltpu.CompilerParams(vmem_limit_bytes=VMEM_LIMIT),
        cost_estimate=pl.CostEstimate(
            flops=2 * experts * cap * slots * width,
            bytes_accessed=2 * slots * width + 2 * experts * blocks * cap * width,
            transcendentals=0,
        ),
        name="collect_rows",
    )(rows, place)


def bits_of(count):
    return [1 << b for b in range(count.bit_length() - 1)]


def partner_of(me, step, count):
    found = 0
    for bit in bits_of(count):
        found = found + bit * lax.rem(me // bit + step // bit, 2)
    return found


def expert_kernel(
    sent_ref, dy_ref, pair_ref, wr_ref, wg_ref, wu_ref, wd_ref,
    back_ref, y_ref, x_ref, g_ref, hid_ref, dga_ref, dup_ref, dlog_ref,
    got_ref, dx_ref, stage_ref, x_send, x_recv, dx_send, dx_recv, own_sem, stage_sem,
):
    devices, experts, cap, width = sent_ref.shape
    step = pl.program_id(0)
    me = lax.axis_index("expert")
    line = lax.axis_index("hidden")

    def x_copy(s):
        peer = partner_of(me, s, devices)
        return pltpu.make_async_remote_copy(
            src_ref=sent_ref.at[peer], dst_ref=got_ref.at[s], send_sem=x_send.at[s],
            recv_sem=x_recv.at[s], device_id=(peer, line), device_id_type=pl.DeviceIdType.MESH,
        )

    def dx_copy(s):
        peer = partner_of(me, s, devices)
        return pltpu.make_async_remote_copy(
            src_ref=dx_ref.at[s], dst_ref=back_ref.at[me], send_sem=dx_send.at[s],
            recv_sem=dx_recv.at[s], device_id=(peer, line), device_id_type=pl.DeviceIdType.MESH,
        )

    def y_copy(s):
        source = partner_of(me, s, devices)
        slot = lax.rem(s, 2)
        return pltpu.make_async_copy(stage_ref.at[slot], y_ref.at[source], stage_sem.at[slot])

    def work(s):
        source = partner_of(me, s, devices)
        slot = lax.rem(s, 2)
        for e in range(experts):
            x = got_ref[s, e]
            dy = dy_ref[source, e].astype(F32)
            pair = pair_ref[source, e].astype(F32)
            margin = jnp.sum(mm(x, wr_ref[...]) * pair, axis=-1, keepdims=True)
            own_gate = 1.0 / (1.0 + jnp.exp(-margin))
            other_gate = 1.0 / (1.0 + jnp.exp(margin))
            g = (own_gate * dy).astype(BF16)
            x_ref[0, e] = x
            g_ref[0, e] = g
            gate = mm(x, wg_ref[e])
            up = mm(x, wu_ref[e])
            square = gate * gate
            bent = jnp.tanh(GELU_C * gate * (1.0 + GELU_A * square))
            half_gate = 0.5 * gate
            gelu = half_gate * (1.0 + bent)
            slope = 0.5 * (1.0 + bent) + half_gate * (1.0 - bent * bent) * (
                GELU_C * (1.0 + 3.0 * GELU_A * square)
            )
            hid = (gelu * up).astype(BF16)
            dhid = mm_nt(g, wd_ref[e])
            dga = (dhid * (up * slope)).astype(BF16)
            dup = (dhid * gelu).astype(BF16)
            hid_ref[0, e] = hid
            dga_ref[0, e] = dga
            dup_ref[0, e] = dup
            y = mm(hid, wd_ref[e])
            dgate = jnp.sum(y * dy, axis=-1, keepdims=True)
            stage_ref[slot, e] = (y * own_gate).astype(BF16)
            dlog = (dgate * own_gate * other_gate * pair).astype(BF16)
            dlog_ref[0, e] = dlog
            dx = mm_nt(dga, wg_ref[e]) + mm_nt(dup, wu_ref[e]) + mm_nt(dlog, wr_ref[...])
            dx_ref[s, e] = dx.astype(BF16)

    @pl.when(step == 0)
    def _():
        barrier = pltpu.get_barrier_semaphore()
        for s in range(1, devices):
            pl.semaphore_signal(
                barrier, inc=1, device_id=(partner_of(me, s, devices), line),
                device_id_type=pl.DeviceIdType.MESH,
            )
        pl.semaphore_wait(barrier, devices - 1)
        for s in range(devices - 1, 0, -1):
            x_copy(s).start()
        own = pltpu.make_async_copy(sent_ref.at[me], got_ref.at[0], own_sem)
        own.start()
        own.wait()

    @pl.when(step > 0)
    def _():
        x_copy(step).wait_recv()

    @pl.when(step > 1)
    def _():
        y_copy(step - 2).wait()

    work(step)
    y_copy(step).start()

    @pl.when(step > 0)
    def _():
        dx_copy(step).start()

    @pl.when(step == devices - 1)
    def _():
        own = pltpu.make_async_copy(dx_ref.at[0], back_ref.at[me], own_sem)
        own.start()
        own.wait()
        y_copy(devices - 2).wait()
        y_copy(devices - 1).wait()
        for s in range(1, devices):
            x_copy(s).wait_send()
            dx_copy(s).wait_send()
            dx_copy(s).wait_recv()


def expert_pass(sent, dy, pair, wr, wg, wu, wd, identity):
    devices, experts, cap, width = sent.shape
    hidden = wg.shape[2]
    choices = wr.shape[1]
    any_space = pl.BlockSpec(memory_space=pl.ANY)

    def whole(shape):
        return pl.BlockSpec(shape, lambda s: (0,) * len(shape), pipeline_mode=pl.Buffered(1))

    def block(cols):
        return pl.BlockSpec((1, experts, cap, cols), lambda s: (s, 0, 0, 0))

    def kept(cols):
        return jax.ShapeDtypeStruct((devices, experts, cap, cols), BF16)

    rows = devices * cap
    return pl.pallas_call(
        expert_kernel,
        grid=(devices,),
        out_shape=(
            kept(width), kept(width), kept(width), kept(width), kept(hidden), kept(hidden),
            kept(hidden), kept(choices),
        ),
        in_specs=[
            any_space, whole(dy.shape), whole(pair.shape), whole(wr.shape), whole(wg.shape),
            whole(wu.shape), whole(wd.shape),
        ],
        out_specs=(
            any_space, any_space, block(width), block(width), block(hidden), block(hidden),
            block(hidden), block(choices),
        ),
        scratch_shapes=[
            pltpu.VMEM((devices, experts, cap, width), BF16),
            pltpu.VMEM((devices, experts, cap, width), BF16),
            pltpu.VMEM((2, experts, cap, width), BF16),
            pltpu.SemaphoreType.DMA((devices,)),
            pltpu.SemaphoreType.DMA((devices,)),
            pltpu.SemaphoreType.DMA((devices,)),
            pltpu.SemaphoreType.DMA((devices,)),
            pltpu.SemaphoreType.DMA,
            pltpu.SemaphoreType.DMA((2,)),
        ],
        compiler_params=pltpu.CompilerParams(
            vmem_limit_bytes=VMEM_LIMIT, collective_id=identity, has_side_effects=True
        ),
        cost_estimate=pl.CostEstimate(
            flops=12 * experts * rows * width * hidden,
            bytes_accessed=80 * experts * rows * width,
            transcendentals=experts * rows * hidden,
        ),
        name="expert_pass",
    )(sent, dy, pair, wr, wg, wu, wd)


def weight_kernel(*refs):
    count = (len(refs) - 4) // 6
    dwr_ref, dwg_ref, dwu_ref, dwd_ref = refs[-4:]
    totals = [0.0, 0.0, 0.0, 0.0]
    for index in range(count):
        blocks = [
            ref[...].reshape(ref.shape[0] * ref.shape[2], ref.shape[3])
            for ref in refs[6 * index : 6 * index + 6]
        ]
        x, g, hid, dga, dup, dlog = blocks
        totals[0] = totals[0] + mm_tn(x, dlog)
        totals[1] = totals[1] + mm_tn(x, dga)
        totals[2] = totals[2] + mm_tn(x, dup)
        totals[3] = totals[3] + mm_tn(hid, g)
    dwr_ref[0] = totals[0]
    dwg_ref[0] = totals[1]
    dwu_ref[0] = totals[2]
    dwd_ref[0] = totals[3]


def weight_pass(kept):
    sources, experts, cap, width = kept[0][0].shape
    hidden = kept[0][2].shape[3]
    choices = kept[0][5].shape[3]
    rows = sources * cap
    block = 256 if width % 256 == 0 else width
    tokens = pl.BlockSpec((sources, 1, cap, block), lambda e, j: (0, e, 0, j))
    acts = pl.BlockSpec((sources, 1, cap, hidden), lambda e, j: (0, e, 0, 0))
    logs = pl.BlockSpec((sources, 1, cap, choices), lambda e, j: (0, e, 0, 0))
    operands = []
    for arrays in kept:
        operands.extend(arrays)
    return pl.pallas_call(
        weight_kernel,
        grid=(experts, width // block),
        out_shape=(
            jax.ShapeDtypeStruct((experts, width, choices), F32),
            jax.ShapeDtypeStruct((experts, width, hidden), F32),
            jax.ShapeDtypeStruct((experts, width, hidden), F32),
            jax.ShapeDtypeStruct((experts, hidden, width), F32),
        ),
        in_specs=[tokens, tokens, acts, acts, acts, logs] * len(kept),
        out_specs=(
            pl.BlockSpec((1, block, choices), lambda e, j: (e, j, 0)),
            pl.BlockSpec((1, block, hidden), lambda e, j: (e, j, 0)),
            pl.BlockSpec((1, block, hidden), lambda e, j: (e, j, 0)),
            pl.BlockSpec((1, hidden, block), lambda e, j: (e, 0, j)),
        ),
        compiler_params=pltpu.CompilerParams(vmem_limit_bytes=VMEM_LIMIT),
        cost_estimate=pl.CostEstimate(
            flops=6 * len(kept) * experts * rows * width * hidden,
            bytes_accessed=len(kept) * experts * rows * (4 * width + 6 * hidden)
            + 12 * experts * width * hidden,
            transcendentals=0,
        ),
        name="weight_pass",
    )(*operands)


def after(values, *others):
    return lax.optimization_barrier((values,) + others)[0]


def shards(
    x_in,
    cotangent,
    segment_ids,
    routes,
    qkv_weight,
    out_weight,
    bias_table,
    attn_gain,
    moe_gain,
    router_weight,
    gate_weight,
    up_weight,
    down_weight,
):
    micro_count, _, shard_len, width = x_in.shape
    slot_count = segment_ids.shape[2]
    head_cols = out_weight.shape[0]
    bucket_count, heads_here = bias_table.shape
    head_size = head_cols // heads_here
    expert_count = router_weight.shape[1]
    experts_here = gate_weight.shape[0]
    devices = expert_count // experts_here
    blocks = slot_count // shard_len
    members = blocks // 2
    half = slot_count // 2
    capacity = max(2, (10 * shard_len + 4 * expert_count - 1) // (4 * expert_count))
    scale = head_size ** (-0.5)
    hidden_index = lax.axis_index("hidden")
    expert_index = lax.axis_index("expert")
    part = hidden_index // members
    part_ref = part.reshape(1).astype(jnp.int32)
    attn_gain_f = attn_gain.astype(F32).reshape(1, width)
    moe_gain_f = moe_gain.astype(F32).reshape(1, width)
    token_shape = (devices, experts_here, blocks * capacity, width)
    flat_shape = (devices, experts_here * blocks * capacity, width)
    place_shape = (expert_count, blocks, capacity, width)
    half_groups = [list(range(p * members, (p + 1) * members)) for p in range(2)]
    across = [(z, (z + members) % blocks) for z in range(blocks)]

    def exchange(buffer):
        return lax.all_to_all(buffer, "expert", split_axis=0, concat_axis=0, tiled=True)

    def to_all(values, axis, count, groups=None):
        copies = jnp.broadcast_to(values[None], (count,) + values.shape)
        return lax.all_to_all(
            copies, axis, split_axis=0, concat_axis=0, tiled=True, axis_index_groups=groups
        )

    def swap_half(buffer):
        return lax.all_to_all(
            buffer, "hidden", split_axis=0, concat_axis=0, tiled=True,
            axis_index_groups=half_groups,
        )

    def gather(values):
        return lax.all_gather(values, "hidden", axis=0, tiled=True)

    def scatter(values):
        return lax.psum_scatter(values.astype(BF16), "hidden", scatter_dimension=0, tiled=True)

    def my_piece(flat):
        rows = flat.shape[0] // devices
        return lax.dynamic_slice_in_dim(flat, expert_index * rows, rows, 0)

    def placing():
        expert_ids = jnp.arange(expert_count, dtype=jnp.int32)
        place_ids = jnp.arange(expert_count * capacity, dtype=jnp.int32)
        slot = jnp.arange(shard_len, dtype=jnp.int32)
        earlier_than = (slot[:, None] < slot[None, :]).astype(BF16)
        route = to_all(routes[:, 0], "hidden", blocks)
        route = route.transpose(1, 0, 2, 3)
        live = (segment_ids[:, 0] >= 0).reshape(micro_count, blocks, shard_len)
        chosen = (route[..., None] == expert_ids).astype(F32)
        chosen = chosen * live[..., None, None].astype(F32)
        counted = jnp.sum(chosen, axis=3).astype(BF16)
        before = jnp.einsum("mbte,tu->mbue", counted, earlier_than, preferred_element_type=F32)
        position = jnp.sum(before[:, :, :, None, :] * chosen, axis=-1).astype(jnp.int32)
        place = jnp.where(live[..., None], route * capacity + position, -1)
        other = jnp.full((micro_count, blocks, expert_count * capacity), -1, jnp.int32)
        for k in range(2):
            hit = place[:, :, None, :, k] == place_ids[None, None, :, None]
            found = jnp.max(jnp.where(hit, route[:, :, None, :, 1 - k], -1), axis=-1)
            other = jnp.maximum(other, found)
        other = other.reshape(micro_count, blocks, devices, experts_here, capacity)
        other = exchange(other.transpose(2, 0, 3, 1, 4))
        other = other.transpose(1, 0, 2, 3, 4)
        other = other.reshape(micro_count, devices, experts_here, blocks * capacity)
        me = expert_index * experts_here + jnp.arange(experts_here, dtype=jnp.int32)
        plus = me[None, None, :, None, None] == expert_ids
        minus = other[..., None] == expert_ids
        pair = plus.astype(F32) - minus.astype(F32)
        pair = jnp.where(other[..., None] >= 0, pair, 0.0).astype(BF16)
        place = place.reshape(micro_count, slot_count, 2)
        return place, place.transpose(0, 2, 1), pair

    states = [dict() for _ in range(micro_count)]

    piece = lax.ppermute(my_piece(qkv_weight.reshape(3 * width, head_cols)), "hidden", across)
    other_qkv = to_all(piece, "expert", devices).reshape(qkv_weight.shape)
    piece = to_all(my_piece(out_weight), "hidden", blocks)
    all_out = to_all(piece, "expert", devices)
    all_out = all_out.transpose(1, 0, 2, 3).reshape(blocks, head_cols, width)
    tables = jnp.concatenate(
        [bias_table, lax.ppermute(bias_table, "hidden", across)], axis=1
    ).astype(F32)
    onehot_bucket = bucket_onehot(half, bucket_count)
    bias = position_bias(jnp.einsum("jb,bh->hj", onehot_bucket, tables, precision=PRECISE))
    place_cols, place_rows, pairs = placing()

    def pair_x(micro, kept):
        kept["x_half"] = to_all(x_in[micro, 0], "hidden", members, half_groups).reshape(half, width)

    def attention(micro, kept):
        seg = lax.dynamic_slice_in_dim(segment_ids[micro, 0], part * half, half, 0)
        qkv, prob, heads = attend(
            kept["x_half"], attn_gain_f, qkv_weight, other_qkv, bias, seg, scale
        )
        kept.update(qkv=qkv, prob=prob, heads=heads)
        own_heads = swap_half(heads.reshape(members, shard_len, 2 * head_cols))
        kept["h1"], kept["xn2"] = project(part_ref, own_heads, all_out, x_in[micro, 0], moe_gain_f)

    def spread(rows, micro):
        return spread_rows(rows, place_rows[micro], expert_count, capacity, shard_len)

    def send_dy(micro, kept):
        sent = spread(kept["dy_all"], micro).reshape(flat_shape)
        kept["dy"] = exchange(sent).reshape(token_shape)

    def experts(micro, kept, *behind):
        sent = spread(kept["xn2_all"], micro).reshape(token_shape)
        back, y, x, g, hid, dga, dup, dlog = expert_pass(
            after(sent, *behind), kept["dy"], pairs[micro], router_weight, gate_weight, up_weight,
            down_weight, 1 + micro,
        )
        kept["weights"] = (x, g, hid, dga, dup, dlog)
        kept["y_sent"] = y.reshape(flat_shape)
        kept["dx_back"] = back.reshape(place_shape)

    def combine(micro, kept):
        kept["dx_part"] = collect_rows(kept["dx_back"], place_cols[micro], shard_len)
        kept["dxn2"] = scatter(kept["dx_part"])

    def attention_back(micro, kept):
        dh1, dattn, dheads, kept["moe_gain_grad"] = turn(
            part_ref, kept["dxn2"], kept["h1"], cotangent[micro, 0], moe_gain_f, all_out, members
        )
        dheads = swap_half(dheads).reshape(half, 2 * head_cols)
        dattn = to_all(dattn, "hidden", members, half_groups).reshape(half, width)
        dxn1, kept["qkv_grad"], kept["line"], kept["attn_gain_grad"] = attend_back(
            kept["x_half"], attn_gain_f, qkv_weight, other_qkv, kept["qkv"], kept["prob"], dheads,
            scale, devices,
        )
        kept["dxn1"] = dxn1
        kept["out_grad"] = mm_tn(kept["heads"], dattn).astype(BF16)
        dxn1 = swap_half(dxn1.reshape(members, shard_len, width))
        dxn1 = jnp.sum(dxn1.astype(F32), axis=0)
        x_own = x_in[micro, 0].astype(F32)
        r1 = lax.rsqrt(jnp.mean(x_own * x_own, axis=-1, keepdims=True) + EPSILON)
        unit = x_own * r1
        weighted = dxn1 * attn_gain_f
        inner = jnp.mean(weighted * unit, axis=-1, keepdims=True)
        kept["x_grad"] = (dh1 + r1 * (weighted - unit * inner)).astype(BF16)

    def finish(micro, kept):
        mixed = scatter(collect_rows(kept["y_back"], place_cols[micro], shard_len))
        kept["block_out"] = (kept["h1"] + mixed.astype(F32)).astype(BF16)

    last = states[-1]
    behind = ()
    for micro in range(micro_count):
        state = states[micro]
        pair_x(micro, state)
        state["dy_all"] = gather(after(cotangent[micro, 0], *behind))
        send_dy(micro, state)
        behind = (state["dy_all"],)
    for micro in range(micro_count):
        state = states[micro]
        state["x_half"] = after(state["x_half"], state["dy_all"])
        attention(micro, state)
        state["xn2_all"] = gather(after(state["xn2"], *behind))
        behind = (state["xn2_all"],)
    behind = ()
    for micro in range(micro_count):
        experts(micro, states[micro], *behind)
        combine(micro, states[micro])
        behind = (states[micro]["dx_part"],)
    for micro in range(micro_count):
        state = states[micro]
        state["y_back"] = exchange(after(state["y_sent"], last["dx_back"])).reshape(place_shape)
    for micro in range(micro_count):
        attention_back(micro, states[micro])
    for micro in range(micro_count):
        finish(micro, states[micro])
    kept = [state["weights"] for state in states]
    kept[-1] = tuple(after(list(kept[-1]), last["dxn1"]))
    dwr, dwg, dwu, dwd = weight_pass(kept)

    def added(name):
        total = states[0][name].astype(F32)
        for state in states[1:]:
            total = total + state[name].astype(F32)
        return total

    def both_halves(pieces):
        total = jnp.sum(pieces.astype(F32), axis=0)
        moved = lax.ppermute(total[1].astype(BF16), "hidden", across)
        piece = (total[0] + moved.astype(F32)).astype(BF16)
        return to_all(piece, "expert", devices)

    grad_qkv = both_halves(exchange(added("qkv_grad").astype(BF16)))
    grad_qkv = grad_qkv.astype(F32).reshape(qkv_weight.shape)
    grad_out = added("out_grad").astype(BF16).reshape(2, devices, head_cols // devices, width)
    grad_out = both_halves(exchange(grad_out.transpose(1, 0, 2, 3)))
    grad_out = grad_out.astype(F32).reshape(out_weight.shape)
    lines = added("line").reshape(2 * heads_here, 2 * half)
    table = jnp.einsum("hj,jb->hb", lines, onehot_bucket, precision=PRECISE)
    table = table.reshape(2, heads_here * bucket_count)
    mine = jnp.arange(blocks, dtype=jnp.int32)[:, None]
    table = jnp.where(mine == hidden_index, table[0], 0.0) + jnp.where(
        mine == (hidden_index + members) % blocks, table[1], 0.0
    )
    small = jnp.concatenate(
        [
            jnp.sum(dwr, axis=0).reshape(-1),
            added("attn_gain_grad").reshape(-1),
            added("moe_gain_grad").reshape(-1),
            table.reshape(-1),
        ]
    ).reshape(-1, 128)
    small = jnp.sum(to_all(small, "expert", devices), axis=0)
    small = jnp.sum(to_all(small, "hidden", blocks), axis=0).reshape(-1)
    sizes = (width * expert_count, width, width)
    grad_router = small[: sizes[0]].reshape(width, expert_count)
    grad_attn_gain = small[sizes[0] : sizes[0] + width]
    grad_moe_gain = small[sizes[0] + width : sizes[0] + 2 * width]
    table = small[sizes[0] + 2 * width :].reshape(blocks, heads_here, bucket_count)
    grad_table = lax.dynamic_index_in_dim(table, hidden_index, 0, keepdims=False).T
    return (
        jnp.stack([state["block_out"] for state in states])[:, None],
        jnp.stack([state["x_grad"] for state in states])[:, None],
        grad_qkv,
        grad_out,
        grad_table,
        grad_attn_gain,
        grad_moe_gain,
        grad_router,
        dwg,
        dwu,
        dwd,
    )


def solution(mesh):
    return jax.shard_map(
        shards,
        mesh=mesh,
        in_specs=(
            P(None, "expert", "hidden", None),
            P(None, "expert", "hidden", None),
            P(None, "expert", None),
            P(None, "expert", "hidden", None),
            P(None, None, "hidden"),
            P("hidden", None),
            P(None, "hidden"),
            P(),
            P(),
            P(),
            P("expert", None, "hidden"),
            P("expert", None, "hidden"),
            P("expert", "hidden", None),
        ),
        out_specs=(
            P(None, "expert", "hidden", None),
            P(None, "expert", "hidden", None),
            P(None, None, "hidden"),
            P("hidden", None),
            P(None, "hidden"),
            P(),
            P(),
            P(),
            P("expert", None, "hidden"),
            P("expert", None, "hidden"),
            P("expert", "hidden", None),
        ),
        check_vma=False,
    )
```

```python
import functools

import jax
import jax.numpy as jnp
from jax import lax
from jax.experimental import pallas as pl
from jax.experimental.pallas import tpu as pltpu
from jax.sharding import PartitionSpec as P

EPSILON = 1e-06
PRECISE = lax.Precision.HIGHEST
LIMITS = (12, 16, 23, 32, 46, 64, 91)
MASKED = -1000000000.0
GELU_C = 0.7978845608028654
GELU_A = 0.044715
VMEM_LIMIT = 60 * 1024 * 1024
F32 = jnp.float32
BF16 = jnp.bfloat16


def mm(a, b):
    return lax.dot_general(a, b, (((1,), (0,)), ((), ())), preferred_element_type=F32)


def mm_nt(a, b):
    return lax.dot_general(a, b, (((1,), (1,)), ((), ())), preferred_element_type=F32)


def mm_tn(a, b):
    return lax.dot_general(a, b, (((0,), (0,)), ((), ())), preferred_element_type=F32)


def bucket_of(distance):
    magnitude = jnp.abs(distance)
    far_bucket = jnp.full(magnitude.shape, 8, jnp.int32)
    for threshold in LIMITS:
        far_bucket = far_bucket + (magnitude >= threshold).astype(jnp.int32)
    return jnp.where(magnitude < 8, magnitude, far_bucket) + 16 * (distance > 0).astype(jnp.int32)


def bucket_onehot(half, bucket_count):
    lane = jnp.arange(2 * half, dtype=jnp.int32)
    distance = jnp.where(lane < half, lane, lane - 2 * half)
    return (
        bucket_of(distance)[:, None] == jnp.arange(bucket_count, dtype=jnp.int32)[None, :]
    ).astype(F32)


TILE = 128


def bias_kernel(line_ref, out_ref):
    length = out_ref.shape[2]
    line = jnp.broadcast_to(line_ref[0], (8, length))
    row = lax.broadcasted_iota(jnp.int32, (8, length), 0)
    sheet = line
    for r in range(1, 8):
        sheet = jnp.where(row == r, pltpu.roll(line, r, 1), sheet)
    while sheet.shape[0] < TILE:
        sheet = jnp.concatenate([sheet, pltpu.roll(sheet, sheet.shape[0], 1)], axis=0)
    out_ref[0] = sheet.astype(out_ref.dtype)


def position_bias(line):
    heads, length = line.shape
    return pl.pallas_call(
        bias_kernel,
        grid=(heads,),
        out_shape=jax.ShapeDtypeStruct((heads, TILE, length), BF16),
        in_specs=[pl.BlockSpec((1, 1, length), lambda h: (h, 0, 0))],
        out_specs=pl.BlockSpec((1, TILE, length), lambda h: (h, 0, 0)),
        compiler_params=pltpu.CompilerParams(vmem_limit_bytes=VMEM_LIMIT),
        name="position_bias",
    )(line.reshape(heads, 1, length))


def unit_rows(x):
    x = x.astype(F32)
    return x * lax.rsqrt(jnp.mean(x * x, axis=-1, keepdims=True) + EPSILON)


def remote(src, dst, send_sem, recv_sem, device):
    return pltpu.make_async_remote_copy(
        src_ref=src, dst_ref=dst, send_sem=send_sem, recv_sem=recv_sem,
        device_id=device, device_id_type=pl.DeviceIdType.MESH,
    )


def greet(devices):
    barrier = pltpu.get_barrier_semaphore()
    for device in devices:
        pl.semaphore_signal(
            barrier, inc=1, device_id=device, device_id_type=pl.DeviceIdType.MESH
        )
    pl.semaphore_wait(barrier, len(devices))


def bits_of(count):
    return [1 << b for b in range(count.bit_length() - 1)]


def partner_of(me, step, count):
    found = 0
    for bit in bits_of(count):
        found = found + bit * lax.rem(me // bit + step // bit, 2)
    return found


def any_space():
    return pl.BlockSpec(memory_space=pl.ANY)


def opening_kernel(
    micros, x_ref, qkv_ref, out_ref, routes_ref, table_ref,
    x_all, qkv_all, out_all, routes_all, table_all,
    x_send, x_recv, qkv_send, qkv_recv, out_send, out_recv, qkv_on_send, qkv_on_recv,
    out_on_send, out_on_recv, routes_send, routes_recv, table_send, table_recv, own_sem,
):
    devices, qkv_rows = qkv_all.shape[0], qkv_all.shape[1]
    blocks, out_rows = out_all.shape[0], out_all.shape[2]
    members = x_all.shape[1]
    me = lax.axis_index("expert")
    line = lax.axis_index("hidden")
    mine = lax.rem(line, members)
    base = line - mine
    others = [partner_of(me, s, devices) for s in range(1, devices)]
    along = [lax.rem(line + s, blocks) for s in range(1, blocks)]
    across = lax.rem(line + members, blocks)
    greet([(other, line) for other in others] + [(me, z) for z in along])
    own = [
        pltpu.make_async_copy(out_ref.at[pl.ds(me * out_rows, out_rows)], out_all.at[line, me], own_sem.at[0]),
        pltpu.make_async_copy(routes_ref, routes_all.at[line], own_sem.at[1]),
    ]
    for micro in range(micros):
        own.append(
            pltpu.make_async_copy(x_ref.at[micro], x_all.at[micro, mine], own_sem.at[2 + micro])
        )
    for copy in own:
        copy.start()
    first_qkv = remote(
        qkv_ref.at[pl.ds(me * qkv_rows, qkv_rows)], qkv_all.at[me], qkv_send, qkv_recv, (me, across)
    )
    first_qkv.start()
    first_out = []
    small = [remote(table_ref, table_all, table_send, table_recv, (me, across))]
    for s, z in enumerate(along):
        first_out.append(
            remote(
                out_ref.at[pl.ds(me * out_rows, out_rows)], out_all.at[line, me], out_send.at[s],
                out_recv.at[s], (me, z),
            )
        )
        small.append(
            remote(routes_ref, routes_all.at[line], routes_send.at[s], routes_recv.at[s], (me, z))
        )
    for copy in first_out + small:
        copy.start()
    xs = []
    for micro in range(micros):
        for s in range(1, members):
            peer = base + lax.rem(mine + s, members)
            xs.append(
                remote(
                    x_ref.at[micro], x_all.at[micro, mine], x_send.at[micro, s],
                    x_recv.at[micro, s], (me, peer),
                )
            )
    for copy in xs:
        copy.start()
    first_qkv.wait_recv()
    second = []
    for s, other in enumerate(others):
        second.append(
            remote(
                qkv_all.at[me], qkv_all.at[me], qkv_on_send.at[s], qkv_on_recv.at[s], (other, line)
            )
        )
        second[-1].start()
    own[0].wait()
    for copy in first_out:
        copy.wait_recv()
    for s, other in enumerate(others):
        second.append(
            remote(
                out_all.at[:, me], out_all.at[:, me], out_on_send.at[s], out_on_recv.at[s],
                (other, line),
            )
        )
        second[-1].start()
    for copy in own[1:]:
        copy.wait()
    first_qkv.wait_send()
    for copy in first_out:
        copy.wait_send()
    for copy in small + xs + second:
        copy.wait()


def opening(x, qkv, out, routes, table, devices, blocks, members):
    micros, shard_len, width = x.shape
    dma = pltpu.SemaphoreType.DMA
    return pl.pallas_call(
        functools.partial(opening_kernel, micros),
        out_shape=(
            jax.ShapeDtypeStruct((micros, members, shard_len, width), BF16),
            jax.ShapeDtypeStruct((devices, qkv.shape[0] // devices, qkv.shape[1]), BF16),
            jax.ShapeDtypeStruct((blocks, devices, out.shape[0] // devices, width), BF16),
            jax.ShapeDtypeStruct((blocks,) + routes.shape, jnp.int32),
            jax.ShapeDtypeStruct(table.shape, table.dtype),
        ),
        in_specs=[any_space()] * 5,
        out_specs=(any_space(),) * 5,
        scratch_shapes=[
            dma((micros, members)), dma((micros, members)), dma, dma, dma((blocks,)), dma((blocks,)),
            dma((devices,)), dma((devices,)), dma((devices,)), dma((devices,)), dma((blocks,)),
            dma((blocks,)), dma, dma, dma((2 + micros,)),
        ],
        compiler_params=pltpu.CompilerParams(collective_id=1, has_side_effects=True),
        cost_estimate=pl.CostEstimate(flops=0, bytes_accessed=60000000, transcendentals=0),
        name="opening",
    )(x, qkv, out, routes, table)


def unit_rows(x):
    x = x.astype(F32)
    return x * lax.rsqrt(jnp.mean(x * x, axis=-1, keepdims=True) + EPSILON)


def attend_kernel(
    scale, x_ref, gain_ref, own_ref, other_ref, bias_ref, seg_row_ref, seg_col_ref,
    out_ref, x_own_ref, moe_gain_ref,
    qkv_ref, prob_ref, heads_ref, h1_ref, xn2_ref,
    xn_ref, part_ref, got_ref, send_sem, recv_sem,
):
    micros, members, shard_len, both = got_ref.shape
    cols = both // 2
    heads, length = bias_ref.shape[0], bias_ref.shape[2]
    half = members * shard_len
    size = cols // heads
    micro, group = pl.program_id(0), pl.program_id(1)
    me = lax.axis_index("expert")
    line = lax.axis_index("hidden")
    mine = lax.rem(line, members)
    part = line // members
    base = line - mine

    def swap(m, s):
        peer = lax.rem(mine + s, members)
        return remote(
            part_ref.at[m, peer], got_ref.at[m, mine], send_sem.at[m, s], recv_sem.at[m, s],
            (me, base + peer),
        )

    @pl.when((micro == 0) & (group == 0))
    def _():
        greet([(me, base + lax.rem(mine + s, members)) for s in range(1, members)])

    @pl.when(group == 0)
    def _():
        xn_ref[...] = (unit_rows(x_ref[0]) * gain_ref[...]).astype(BF16)
        for t in range(3):
            qkv_ref[0, 0, t] = mm(xn_ref[...], own_ref[t]).astype(BF16)

    @pl.when(group > 0)
    def _():
        for t in range(3):
            qkv_ref[0, 0, t] = mm(xn_ref[...], other_ref[t]).astype(BF16)

    seg_row = seg_row_ref[0]
    for head in range(heads):
        inner = slice(head * size, (head + 1) * size)
        keys = qkv_ref[0, 0, 1, :, inner]
        values = qkv_ref[0, 0, 2, :, inner]
        for start in range(0, half, TILE):
            rows = slice(start, start + TILE)
            scores = mm_nt(qkv_ref[0, 0, 0, rows, inner], keys) * scale
            shift = bias_ref[head, :, : half - start]
            if start:
                shift = jnp.concatenate([bias_ref[head, :, length - start :], shift], axis=1)
            scores = scores + shift.astype(F32)
            scores = jnp.where(seg_col_ref[0, rows, :] == seg_row, scores, MASKED)
            top = jnp.max(scores, axis=-1, keepdims=True)
            weights = jnp.exp(scores - top)
            inverse = 1.0 / jnp.sum(weights, axis=-1, keepdims=True)
            prob = (weights * inverse).astype(BF16)
            prob_ref[0, 0, head, rows, :] = prob
            heads_ref[0, rows, inner] = mm(prob, values).astype(BF16)

    for g in range(2):

        @pl.when(group == g)
        def _(g=g):
            for member in range(members):
                rows = slice(member * shard_len, (member + 1) * shard_len)
                part_ref[micro, member, :, g * cols : (g + 1) * cols] = heads_ref[0, rows, :]

    @pl.when(group == 1)
    def _():
        got_ref[micro, mine] = part_ref[micro, mine]
        for s in range(1, members):
            swap(micro, s).start()

    @pl.when((micro == micros - 1) & (group == 1))
    def _():
        for m in range(micros):
            for s in range(1, members):
                swap(m, s).wait_recv()
            h1 = x_own_ref[m].astype(F32)
            for member in range(members):
                for j in range(2):
                    index = lax.rem(part + j, 2) * members + member
                    h1 = h1 + mm(got_ref[m, member, :, j * cols : (j + 1) * cols], out_ref[index])
            h1_ref[m] = h1
            xn2_ref[m] = (unit_rows(h1) * moe_gain_ref[...]).astype(BF16)
        for m in range(micros):
            for s in range(1, members):
                swap(m, s).wait_send()


def attend(x, gain, own_weight, other_weight, bias, seg, out_weight, x_own, moe_gain, scale, members):
    micros, half, width = x.shape
    cols = own_weight.shape[2]
    heads = bias.shape[0] // 2
    shard_len = half // members

    def once(shape):
        return pl.BlockSpec(shape, lambda m, p: (0,) * len(shape), pipeline_mode=pl.Buffered(1))

    return pl.pallas_call(
        functools.partial(attend_kernel, scale),
        grid=(micros, 2),
        out_shape=(
            jax.ShapeDtypeStruct((micros, 2, 3, half, cols), BF16),
            jax.ShapeDtypeStruct((micros, 2, heads, half, half), BF16),
            jax.ShapeDtypeStruct((micros, half, 2 * cols), BF16),
            jax.ShapeDtypeStruct((micros, shard_len, width), F32),
            jax.ShapeDtypeStruct((micros, shard_len, width), BF16),
        ),
        in_specs=[
            pl.BlockSpec((1, half, width), lambda m, p: (m, 0, 0)),
            once((1, width)),
            once((3, width, cols)),
            once((3, width, cols)),
            pl.BlockSpec((heads,) + bias.shape[1:], lambda m, p: (p, 0, 0)),
            pl.BlockSpec((1, 1, half), lambda m, p: (m, 0, 0)),
            pl.BlockSpec((1, half, 1), lambda m, p: (m, 0, 0)),
            once(out_weight.shape),
            once(x_own.shape),
            once((1, width)),
        ],
        out_specs=(
            pl.BlockSpec((1, 1, 3, half, cols), lambda m, p: (m, p, 0, 0, 0)),
            pl.BlockSpec((1, 1, heads, half, half), lambda m, p: (m, p, 0, 0, 0)),
            pl.BlockSpec((1, half, cols), lambda m, p: (m, 0, p)),
            pl.BlockSpec((micros, shard_len, width), lambda m, p: (0, 0, 0)),
            pl.BlockSpec((micros, shard_len, width), lambda m, p: (0, 0, 0)),
        ),
        scratch_shapes=[
            pltpu.VMEM((half, width), BF16),
            pltpu.VMEM((micros, members, shard_len, 2 * cols), BF16),
            pltpu.VMEM((micros, members, shard_len, 2 * cols), BF16),
            pltpu.SemaphoreType.DMA((micros, members)),
            pltpu.SemaphoreType.DMA((micros, members)),
        ],
        compiler_params=pltpu.CompilerParams(
            vmem_limit_bytes=VMEM_LIMIT, collective_id=2, has_side_effects=True
        ),
        cost_estimate=pl.CostEstimate(
            flops=micros * 2 * half * cols * (8 * width + 4 * half),
            bytes_accessed=40000000,
            transcendentals=micros * 2 * heads * half * half,
        ),
        name="attend",
    )(
        x, gain, own_weight, other_weight, bias, seg.reshape(micros, 1, half),
        seg.reshape(micros, half, 1), out_weight, x_own, moe_gain,
    )


def back_kernel(
    scale, added, grad_ref, h1_ref, dy_ref, x_own_ref, moe_gain_ref, gain_ref, out_ref, x_ref,
    own_ref, other_ref, qkv_ref, prob_ref, heads_ref, *refs,
):
    if added:
        prev_ref, refs = refs[0], refs[1:]
    (
        xgrad_ref, grads_ref, line_ref, dmoe_ref, dgain_ref,
        dh1_ref, dattn_all, dheads_part, dheads_all, dxn_part, dxn_got, total_ref, xn_ref, ds_ref,
        dproj_ref, sheet_ref, attn_send, attn_recv, heads_send, heads_recv, dxn_send, dxn_recv,
    ) = refs
    members, shard_len, width = dattn_all.shape
    heads, half = prob_ref.shape[1], prob_ref.shape[2]
    cols = dproj_ref.shape[2]
    size = cols // heads
    length = sheet_ref.shape[1]
    group = pl.program_id(0)
    me = lax.axis_index("expert")
    line = lax.axis_index("hidden")
    mine = lax.rem(line, members)
    part = line // members
    base = line - mine
    steps = range(1, members)

    def peer_of(s):
        return lax.rem(mine + s, members)

    def attn_copy(s):
        return remote(
            dattn_all.at[mine], dattn_all.at[mine], attn_send.at[s], attn_recv.at[s],
            (me, base + peer_of(s)),
        )

    def heads_copy(s):
        return remote(
            dheads_part.at[peer_of(s)], dheads_all.at[mine], heads_send.at[s], heads_recv.at[s],
            (me, base + peer_of(s)),
        )

    def dxn_copy(s):
        return remote(
            dxn_part.at[peer_of(s)], dxn_got.at[mine], dxn_send.at[s], dxn_recv.at[s],
            (me, base + peer_of(s)),
        )

    @pl.when(group == 0)
    def _():
        greet([(me, base + peer_of(s)) for s in steps])
        grad = grad_ref[...].astype(F32)
        h1 = h1_ref[...]
        r2 = lax.rsqrt(jnp.mean(h1 * h1, axis=-1, keepdims=True) + EPSILON)
        unit = h1 * r2
        dmoe_ref[...] = jnp.sum(grad * unit, axis=0, keepdims=True)
        weighted = grad * moe_gain_ref[...]
        inner = jnp.mean(weighted * unit, axis=-1, keepdims=True)
        dh1 = dy_ref[...].astype(F32) + r2 * (weighted - unit * inner)
        dh1_ref[...] = dh1
        dattn = dh1.astype(BF16)
        dattn_all[mine] = dattn
        for member in range(members):
            for j in range(2):
                index = lax.rem(part + j, 2) * members + member
                dheads = mm_nt(dattn, out_ref[index]).astype(BF16)
                dheads_part[member, :, j * cols : (j + 1) * cols] = dheads
        for s in steps:
            heads_copy(s).start()
        for s in steps:
            attn_copy(s).start()
        dheads_all[mine] = dheads_part[mine]
        xn_ref[...] = (unit_rows(x_ref[...]) * gain_ref[...]).astype(BF16)
        for s in steps:
            heads_copy(s).wait_recv()

    for g in range(2):

        @pl.when(group == g)
        def _(g=g):
            for head in range(heads):
                inner_cols = slice(head * size, (head + 1) * size)
                outer_cols = slice(g * cols + head * size, g * cols + (head + 1) * size)
                values = qkv_ref[0, 2, :, inner_cols]
                grads = dheads_all[:, :, outer_cols].reshape(half, size)
                sheet_ref[...] = jnp.zeros_like(sheet_ref)
                for start in range(0, half, TILE):
                    rows = slice(start, start + TILE)
                    prob = prob_ref[0, head, rows, :].astype(F32)
                    dprob = mm_nt(grads[rows], values)
                    inner = jnp.sum(prob * dprob, axis=-1, keepdims=True)
                    dscore = (prob * (dprob - inner)).astype(BF16)
                    ds_ref[rows, :] = dscore
                    dscore = dscore.astype(F32)
                    sheet_ref[:, : half - start] += dscore[:, start:]
                    if start:
                        sheet_ref[:, length - start :] += dscore[:, :start]
                dscores = ds_ref[...]
                keys, queries = qkv_ref[0, 1, :, inner_cols], qkv_ref[0, 0, :, inner_cols]
                dproj_ref[0, :, inner_cols] = (mm(dscores, keys) * scale).astype(BF16)
                dproj_ref[1, :, inner_cols] = (mm_tn(dscores, queries) * scale).astype(BF16)
                dproj_ref[2, :, inner_cols] = mm_tn(prob_ref[0, head], grads).astype(BF16)
                sheet = sheet_ref[...]
                while sheet.shape[0] > 8:
                    upper = sheet.shape[0] // 2
                    sheet = sheet[:upper] + pltpu.roll(sheet[upper:], length - upper, 1)
                row = lax.broadcasted_iota(jnp.int32, (8, length), 0)
                found = jnp.zeros((1, length), F32)
                for r in range(8):
                    moved = pltpu.roll(sheet, length - r, 1) if r else sheet
                    found = found + jnp.sum(
                        jnp.where(row == r, moved, 0.0), axis=0, keepdims=True
                    )
                line_ref[0, head : head + 1, :] = found

    def products(weight_ref):
        dxn = mm_nt(dproj_ref[0], weight_ref[0])
        for t in range(1, 3):
            dxn = dxn + mm_nt(dproj_ref[t], weight_ref[t])
        return dxn.reshape(members, shard_len, width)

    @pl.when(group == 0)
    def _():
        total_ref[...] = products(own_ref)
        for s in steps:
            attn_copy(s).wait_recv()

    @pl.when(group == 1)
    def _():
        total_ref[...] += products(other_ref)
        dxn_part[...] = total_ref[...].astype(BF16)
        for s in steps:
            dxn_copy(s).start()

    per = grads_ref.shape[0] // 4
    for t in range(4):
        if t < 3:
            found = mm_tn(xn_ref[...], dproj_ref[t])
        else:
            found = mm_tn(dattn_all[...].reshape(half, width), heads_ref[...])
        found = found.reshape(per, 1, width // per, cols)
        if added:
            found = found + prev_ref[t * per : (t + 1) * per].astype(F32)
        grads_ref[t * per : (t + 1) * per] = found.astype(BF16)

    @pl.when(group == 1)
    def _():
        total = total_ref[...].reshape(half, width)
        dgain_ref[...] = jnp.sum(total * unit_rows(x_ref[...]), axis=0, keepdims=True)
        x_own = x_own_ref[...].astype(F32)
        r1 = lax.rsqrt(jnp.mean(x_own * x_own, axis=-1, keepdims=True) + EPSILON)
        unit = x_own * r1
        for s in steps:
            dxn_copy(s).wait_recv()
        dxn1 = total_ref[mine]
        for s in steps:
            dxn1 = dxn1 + dxn_got[lax.rem(mine + members - s, members)].astype(F32)
        weighted = dxn1 * gain_ref[...]
        inner = jnp.mean(weighted * unit, axis=-1, keepdims=True)
        xgrad_ref[...] = (dh1_ref[...] + r1 * (weighted - unit * inner)).astype(BF16)
        for s in steps:
            heads_copy(s).wait_send()
            attn_copy(s).wait_send()
            dxn_copy(s).wait_send()


def attend_back(
    grad, h1, dy, x_own, moe_gain, gain, out_weight, x_half, own_weight, other_weight, qkv, prob,
    heads_out, prev, scale, pieces, members, identity,
):
    _, heads, half = prob.shape[:3]
    width, cols = own_weight.shape[1:]
    shard_len = half // members
    length = 2 * half
    rows = 4 * width // pieces

    def once(shape):
        return pl.BlockSpec(shape, lambda p: (0,) * len(shape), pipeline_mode=pl.Buffered(1))

    pieces_spec = pl.BlockSpec((pieces, 1, rows, cols), lambda p: (0, p, 0, 0))
    operands = [
        grad, h1, dy, x_own, moe_gain, gain, out_weight, x_half, own_weight, other_weight, qkv,
        prob, heads_out,
    ]
    in_specs = [once(array.shape) for array in operands[:10]] + [
        pl.BlockSpec((1, 3, half, cols), lambda p: (p, 0, 0, 0)),
        pl.BlockSpec((1, heads, half, half), lambda p: (p, 0, 0, 0)),
        pl.BlockSpec((half, cols), lambda p: (0, p)),
    ]
    if prev is not None:
        operands.append(prev)
        in_specs.append(pieces_spec)
    dma = pltpu.SemaphoreType.DMA
    return pl.pallas_call(
        functools.partial(back_kernel, scale, prev is not None),
        grid=(2,),
        out_shape=(
            jax.ShapeDtypeStruct((shard_len, width), BF16),
            jax.ShapeDtypeStruct((pieces, 2, rows, cols), BF16),
            jax.ShapeDtypeStruct((2, heads, length), F32),
            jax.ShapeDtypeStruct((1, width), F32),
            jax.ShapeDtypeStruct((1, width), F32),
        ),
        in_specs=in_specs,
        out_specs=(
            pl.BlockSpec((shard_len, width), lambda p: (0, 0)),
            pieces_spec,
            pl.BlockSpec((1, heads, length), lambda p: (p, 0, 0)),
            pl.BlockSpec((1, width), lambda p: (0, 0)),
            pl.BlockSpec((1, width), lambda p: (0, 0)),
        ),
        scratch_shapes=[
            pltpu.VMEM((shard_len, width), F32),
            pltpu.VMEM((members, shard_len, width), BF16),
            pltpu.VMEM((members, shard_len, 2 * cols), BF16),
            pltpu.VMEM((members, shard_len, 2 * cols), BF16),
            pltpu.VMEM((members, shard_len, width), BF16),
            pltpu.VMEM((members, shard_len, width), BF16),
            pltpu.VMEM((members, shard_len, width), F32),
            pltpu.VMEM((half, width), BF16),
            pltpu.VMEM((half, half), BF16),
            pltpu.VMEM((3, half, cols), BF16),
            pltpu.VMEM((TILE, length), F32),
            dma((members,)), dma((members,)), dma((members,)), dma((members,)), dma((members,)),
            dma((members,)),
        ],
        compiler_params=pltpu.CompilerParams(
            vmem_limit_bytes=VMEM_LIMIT, collective_id=identity, has_side_effects=True
        ),
        cost_estimate=pl.CostEstimate(
            flops=2 * half * cols * (16 * width + 8 * half),
            bytes_accessed=40000000,
            transcendentals=0,
        ),
        name="attend_back",
    )(*operands)


def closing_kernel(
    pieces_ref, small_ref, whole_ref, sum_ref,
    total_ref, moved_ref, moved_got, piece_ref, small_got, line_sum, line_got,
    small_send, small_recv, line_send, line_recv, moved_send, moved_recv, on_send, on_recv, own_sem,
):
    devices = pieces_ref.shape[0]
    blocks = line_got.shape[0]
    me = lax.axis_index("expert")
    line = lax.axis_index("hidden")
    others = [partner_of(me, s, devices) for s in range(1, devices)]
    along = [lax.rem(line + s, blocks) for s in range(1, blocks)]
    across = lax.rem(line + blocks // 2, blocks)
    greet([(other, line) for other in others] + [(me, z) for z in along])
    smalls = [
        remote(small_ref, small_got.at[me], small_send.at[s], small_recv.at[s], (other, line))
        for s, other in enumerate(others)
    ]
    for copy in smalls:
        copy.start()
    small_got[me] = small_ref[...]
    moved = jnp.sum(pieces_ref[:, 1].astype(F32), axis=0)
    moved_ref[...] = moved.astype(BF16)
    cross = remote(moved_ref, moved_got, moved_send, moved_recv, (me, across))
    cross.start()
    total_ref[...] = jnp.sum(pieces_ref[:, 0].astype(F32), axis=0)
    cross.wait_recv()
    piece_ref[...] = (total_ref[...] + moved_got[...].astype(F32)).astype(BF16)
    onward = [
        remote(piece_ref, whole_ref.at[me], on_send.at[s], on_recv.at[s], (other, line))
        for s, other in enumerate(others)
    ]
    for copy in onward:
        copy.start()
    own = pltpu.make_async_copy(piece_ref, whole_ref.at[me], own_sem)
    own.start()
    for copy in smalls:
        copy.wait_recv()
    line_sum[...] = jnp.sum(small_got[...], axis=0)
    lines = [
        remote(line_sum, line_got.at[line], line_send.at[s], line_recv.at[s], (me, z))
        for s, z in enumerate(along)
    ]
    for copy in lines:
        copy.start()
    line_got[line] = line_sum[...]
    for copy in lines:
        copy.wait_recv()
    sum_ref[...] = jnp.sum(line_got[...], axis=0)
    own.wait()
    cross.wait_send()
    for copy in smalls + lines:
        copy.wait_send()
    for copy in onward:
        copy.wait()


def closing(pieces, small, blocks):
    devices, _, rows, cols = pieces.shape
    vmem = pl.BlockSpec(memory_space=pltpu.VMEM)
    dma = pltpu.SemaphoreType.DMA
    return pl.pallas_call(
        closing_kernel,
        out_shape=(
            jax.ShapeDtypeStruct((devices, rows, cols), BF16),
            jax.ShapeDtypeStruct(small.shape, F32),
        ),
        in_specs=[vmem, vmem],
        out_specs=(any_space(), vmem),
        scratch_shapes=[
            pltpu.VMEM((rows, cols), F32),
            pltpu.VMEM((rows, cols), BF16),
            pltpu.VMEM((rows, cols), BF16),
            pltpu.VMEM((rows, cols), BF16),
            pltpu.VMEM((devices,) + small.shape, F32),
            pltpu.VMEM(small.shape, F32),
            pltpu.VMEM((blocks,) + small.shape, F32),
            dma((devices,)), dma((devices,)), dma((blocks,)), dma((blocks,)), dma, dma,
            dma((devices,)), dma((devices,)), dma,
        ],
        compiler_params=pltpu.CompilerParams(
            vmem_limit_bytes=VMEM_LIMIT, collective_id=3, has_side_effects=True
        ),
        cost_estimate=pl.CostEstimate(flops=0, bytes_accessed=60000000, transcendentals=0),
        name="closing",
    )(pieces, small)


def spread(rows, place0, place1, count):
    ids = lax.broadcasted_iota(jnp.int32, (count, rows.shape[0]), 0)
    hit = (ids == place0) | (ids == place1)
    return mm(jnp.where(hit, 1.0, 0.0).astype(BF16), rows)


def spread_kernel(rows_ref, place_ref, out_ref):
    experts, _, cap, width = out_ref.shape
    placed = spread(rows_ref[...], place_ref[0:1, :], place_ref[1:2, :], experts * cap)
    out_ref[...] = placed.astype(BF16).reshape(experts, 1, cap, width)


def spread_rows(rows, place, experts, cap, shard_len):
    slots, width = rows.shape
    blocks = slots // shard_len
    return pl.pallas_call(
        spread_kernel,
        grid=(blocks,),
        out_shape=jax.ShapeDtypeStruct((experts, blocks, cap, width), BF16),
        in_specs=[
            pl.BlockSpec((shard_len, width), lambda b: (b, 0)),
            pl.BlockSpec((2, shard_len), lambda b: (0, b)),
        ],
        out_specs=pl.BlockSpec((experts, 1, cap, width), lambda b: (0, b, 0, 0)),
        compiler_params=pltpu.CompilerParams(vmem_limit_bytes=VMEM_LIMIT),
        cost_estimate=pl.CostEstimate(
            flops=2 * experts * cap * slots * width,
            bytes_accessed=2 * slots * width + 2 * experts * blocks * cap * width,
            transcendentals=0,
        ),
        name="spread_rows",
    )(rows, place)


def collect_kernel(rows_ref, place_ref, out_ref):
    experts, _, cap, width = rows_ref.shape
    tokens = out_ref.shape[0]
    ids = lax.broadcasted_iota(jnp.int32, (experts * cap, tokens), 0)
    hit = (ids == place_ref[0:1, :]) | (ids == place_ref[1:2, :])
    rows = rows_ref[...].reshape(experts * cap, width)
    out_ref[...] = mm_tn(jnp.where(hit, 1.0, 0.0).astype(BF16), rows).astype(BF16)


def collect_rows(rows, place, shard_len):
    experts, blocks, cap, width = rows.shape
    slots = blocks * shard_len
    return pl.pallas_call(
        collect_kernel,
        grid=(blocks,),
        out_shape=jax.ShapeDtypeStruct((slots, width), BF16),
        in_specs=[
            pl.BlockSpec((experts, 1, cap, width), lambda b: (0, b, 0, 0)),
            pl.BlockSpec((2, shard_len), lambda b: (0, b)),
        ],
        out_specs=pl.BlockSpec((shard_len, width), lambda b: (b, 0)),
        compiler_params=pltpu.CompilerParams(vmem_limit_bytes=VMEM_LIMIT),
        cost_estimate=pl.CostEstimate(
            flops=2 * experts * cap * slots * width,
            bytes_accessed=2 * slots * width + 2 * experts * blocks * cap * width,
            transcendentals=0,
        ),
        name="collect_rows",
    )(rows, place)


def place_kernel(cap, route_ref, live_ref, place_ref, other_ref):
    shard_len = route_ref.shape[2]
    count = other_ref.shape[1]
    experts = count // cap
    first, second = route_ref[0, 0:1, :], route_ref[0, 1:2, :]
    live = live_ref[0] >= 0
    ids = lax.broadcasted_iota(jnp.int32, (experts, shard_len), 0)
    chosen = ((ids == first) | (ids == second)) & live
    row = lax.broadcasted_iota(jnp.int32, (shard_len, shard_len), 0)
    col = lax.broadcasted_iota(jnp.int32, (shard_len, shard_len), 1)
    earlier = jnp.where(row < col, 1.0, 0.0).astype(BF16)
    before = mm(jnp.where(chosen, 1.0, 0.0).astype(BF16), earlier)
    spots = lax.broadcasted_iota(jnp.int32, (count, shard_len), 0)
    other = jnp.full((count, 1), -1, jnp.int32)
    for k, route in enumerate((first, second)):
        position = jnp.sum(jnp.where(ids == route, before, 0.0), axis=0, keepdims=True)
        place = jnp.where(live, route * cap + position.astype(jnp.int32), -1)
        place_ref[0, k : k + 1, :] = place
        partner = (second, first)[k]
        found = jnp.max(jnp.where(spots == place, partner, -1), axis=1, keepdims=True)
        other = jnp.maximum(other, found)
    other_ref[0] = other


def find_places(route, live, experts, cap):
    count, _, shard_len = route.shape
    return pl.pallas_call(
        functools.partial(place_kernel, cap),
        grid=(count,),
        out_shape=(
            jax.ShapeDtypeStruct((count, 2, shard_len), jnp.int32),
            jax.ShapeDtypeStruct((count, experts * cap, 1), jnp.int32),
        ),
        in_specs=[
            pl.BlockSpec((1, 2, shard_len), lambda b: (b, 0, 0)),
            pl.BlockSpec((1, 1, shard_len), lambda b: (b, 0, 0)),
        ],
        out_specs=(
            pl.BlockSpec((1, 2, shard_len), lambda b: (b, 0, 0)),
            pl.BlockSpec((1, experts * cap, 1), lambda b: (b, 0, 0)),
        ),
        compiler_params=pltpu.CompilerParams(vmem_limit_bytes=VMEM_LIMIT),
        name="find_places",
    )(route, live)


def expert_kernel(
    sent_ref, dy_ref, pair_ref, wr_ref, wg_ref, wu_ref, wd_ref,
    back_ref, y_ref, x_ref, g_ref, hid_ref, dga_ref, dup_ref, dlog_ref,
    got_ref, dx_ref, stage_ref, x_send, x_recv, dx_send, dx_recv, own_sem, stage_sem,
):
    devices, experts, cap, width = sent_ref.shape
    step = pl.program_id(0)
    me = lax.axis_index("expert")
    line = lax.axis_index("hidden")

    def x_copy(s):
        peer = partner_of(me, s, devices)
        return pltpu.make_async_remote_copy(
            src_ref=sent_ref.at[peer], dst_ref=got_ref.at[s], send_sem=x_send.at[s],
            recv_sem=x_recv.at[s], device_id=(peer, line), device_id_type=pl.DeviceIdType.MESH,
        )

    def dx_copy(s):
        peer = partner_of(me, s, devices)
        return pltpu.make_async_remote_copy(
            src_ref=dx_ref.at[s], dst_ref=back_ref.at[me], send_sem=dx_send.at[s],
            recv_sem=dx_recv.at[s], device_id=(peer, line), device_id_type=pl.DeviceIdType.MESH,
        )

    def y_copy(s):
        source = partner_of(me, s, devices)
        slot = lax.rem(s, 2)
        return pltpu.make_async_copy(stage_ref.at[slot], y_ref.at[source], stage_sem.at[slot])

    def work(s):
        source = partner_of(me, s, devices)
        slot = lax.rem(s, 2)
        for e in range(experts):
            x = got_ref[s, e]
            dy = dy_ref[source, e].astype(F32)
            pair = pair_ref[source, e].astype(F32)
            margin = jnp.sum(mm_nt(x, wr_ref[...]) * pair, axis=-1, keepdims=True)
            own_gate = 1.0 / (1.0 + jnp.exp(-margin))
            other_gate = 1.0 / (1.0 + jnp.exp(margin))
            g = (own_gate * dy).astype(BF16)
            x_ref[0, e] = x
            g_ref[0, e] = g
            gate = mm_nt(x, wg_ref[e])
            up = mm_nt(x, wu_ref[e])
            square = gate * gate
            bent = jnp.tanh(GELU_C * gate * (1.0 + GELU_A * square))
            half_gate = 0.5 * gate
            gelu = half_gate * (1.0 + bent)
            slope = 0.5 * (1.0 + bent) + half_gate * (1.0 - bent * bent) * (
                GELU_C * (1.0 + 3.0 * GELU_A * square)
            )
            hid = (gelu * up).astype(BF16)
            dhid = mm_nt(g, wd_ref[e])
            dga = (dhid * (up * slope)).astype(BF16)
            dup = (dhid * gelu).astype(BF16)
            hid_ref[0, e] = hid
            dga_ref[0, e] = dga
            dup_ref[0, e] = dup
            y = mm(hid, wd_ref[e])
            dgate = jnp.sum(y * dy, axis=-1, keepdims=True)
            stage_ref[slot, e] = (y * own_gate).astype(BF16)
            dlog = (dgate * own_gate * other_gate * pair).astype(BF16)
            dlog_ref[0, e] = dlog
            dx = mm(dga, wg_ref[e]) + mm(dup, wu_ref[e]) + mm(dlog, wr_ref[...])
            dx_ref[s, e] = dx.astype(BF16)

    @pl.when(step == 0)
    def _():
        barrier = pltpu.get_barrier_semaphore()
        for s in range(1, devices):
            pl.semaphore_signal(
                barrier, inc=1, device_id=(partner_of(me, s, devices), line),
                device_id_type=pl.DeviceIdType.MESH,
            )
        pl.semaphore_wait(barrier, devices - 1)
        for s in range(devices - 1, 0, -1):
            x_copy(s).start()
        own = pltpu.make_async_copy(sent_ref.at[me], got_ref.at[0], own_sem)
        own.start()
        own.wait()

    @pl.when(step > 0)
    def _():
        x_copy(step).wait_recv()

    @pl.when(step > 1)
    def _():
        y_copy(step - 2).wait()

    work(step)
    y_copy(step).start()

    @pl.when(step > 0)
    def _():
        dx_copy(step).start()

    @pl.when(step == devices - 1)
    def _():
        own = pltpu.make_async_copy(dx_ref.at[0], back_ref.at[me], own_sem)
        own.start()
        own.wait()
        y_copy(devices - 2).wait()
        y_copy(devices - 1).wait()
        for s in range(1, devices):
            x_copy(s).wait_send()
            dx_copy(s).wait_send()
            dx_copy(s).wait_recv()


def expert_pass(sent, dy, pair, wr, wg, wu, wd, identity):
    devices, experts, cap, width = sent.shape
    hidden = wg.shape[1]
    choices = wr.shape[0]

    def whole(shape):
        return pl.BlockSpec(shape, lambda s: (0,) * len(shape), pipeline_mode=pl.Buffered(1))

    def block(cols):
        return pl.BlockSpec((1, experts, cap, cols), lambda s: (s, 0, 0, 0))

    def kept(cols):
        return jax.ShapeDtypeStruct((devices, experts, cap, cols), BF16)

    rows = devices * cap
    return pl.pallas_call(
        expert_kernel,
        grid=(devices,),
        out_shape=(
            kept(width), kept(width), kept(width), kept(width), kept(hidden), kept(hidden),
            kept(hidden), kept(choices),
        ),
        in_specs=[
            any_space(), whole(dy.shape), whole(pair.shape), whole(wr.shape), whole(wg.shape),
            whole(wu.shape), whole(wd.shape),
        ],
        out_specs=(
            any_space(), any_space(), block(width), block(width), block(hidden), block(hidden),
            block(hidden), block(choices),
        ),
        scratch_shapes=[
            pltpu.VMEM((devices, experts, cap, width), BF16),
            pltpu.VMEM((devices, experts, cap, width), BF16),
            pltpu.VMEM((2, experts, cap, width), BF16),
            pltpu.SemaphoreType.DMA((devices,)),
            pltpu.SemaphoreType.DMA((devices,)),
            pltpu.SemaphoreType.DMA((devices,)),
            pltpu.SemaphoreType.DMA((devices,)),
            pltpu.SemaphoreType.DMA,
            pltpu.SemaphoreType.DMA((2,)),
        ],
        compiler_params=pltpu.CompilerParams(
            vmem_limit_bytes=VMEM_LIMIT, collective_id=identity, has_side_effects=True
        ),
        cost_estimate=pl.CostEstimate(
            flops=12 * experts * rows * width * hidden,
            bytes_accessed=80 * experts * rows * width,
            transcendentals=experts * rows * hidden,
        ),
        name="expert_pass",
    )(sent, dy, pair, wr, wg, wu, wd)


def weight_kernel(*refs):
    count = (len(refs) - 4) // 6
    dwr_ref, dwg_ref, dwu_ref, dwd_ref = refs[-4:]
    totals = [0.0, 0.0, 0.0, 0.0]
    for index in range(count):
        blocks = [
            ref[...].reshape(ref.shape[0] * ref.shape[2], ref.shape[3])
            for ref in refs[6 * index : 6 * index + 6]
        ]
        x, g, hid, dga, dup, dlog = blocks
        totals[0] = totals[0] + mm_tn(dlog, x)
        totals[1] = totals[1] + mm_tn(dga, x)
        totals[2] = totals[2] + mm_tn(dup, x)
        totals[3] = totals[3] + mm_tn(hid, g)
    dwr_ref[0] = totals[0]
    dwg_ref[0] = totals[1]
    dwu_ref[0] = totals[2]
    dwd_ref[0] = totals[3]


def weight_pass(kept):
    sources, experts, cap, width = kept[0][0].shape
    hidden = kept[0][2].shape[3]
    choices = kept[0][5].shape[3]
    rows = sources * cap
    block = 256 if width % 256 == 0 else width
    tokens = pl.BlockSpec((sources, 1, cap, block), lambda e, j: (0, e, 0, j))
    acts = pl.BlockSpec((sources, 1, cap, hidden), lambda e, j: (0, e, 0, 0))
    logs = pl.BlockSpec((sources, 1, cap, choices), lambda e, j: (0, e, 0, 0))
    operands = []
    for arrays in kept:
        operands.extend(arrays)
    return pl.pallas_call(
        weight_kernel,
        grid=(experts, width // block),
        out_shape=(
            jax.ShapeDtypeStruct((experts, choices, width), F32),
            jax.ShapeDtypeStruct((experts, hidden, width), F32),
            jax.ShapeDtypeStruct((experts, hidden, width), F32),
            jax.ShapeDtypeStruct((experts, hidden, width), F32),
        ),
        in_specs=[tokens, tokens, acts, acts, acts, logs] * len(kept),
        out_specs=(
            pl.BlockSpec((1, choices, block), lambda e, j: (e, 0, j)),
            pl.BlockSpec((1, hidden, block), lambda e, j: (e, 0, j)),
            pl.BlockSpec((1, hidden, block), lambda e, j: (e, 0, j)),
            pl.BlockSpec((1, hidden, block), lambda e, j: (e, 0, j)),
        ),
        compiler_params=pltpu.CompilerParams(vmem_limit_bytes=VMEM_LIMIT),
        cost_estimate=pl.CostEstimate(
            flops=6 * len(kept) * experts * rows * width * hidden,
            bytes_accessed=len(kept) * experts * rows * (4 * width + 6 * hidden)
            + 12 * experts * width * hidden,
            transcendentals=0,
        ),
        name="weight_pass",
    )(*operands)


def after(values, *others):
    return lax.optimization_barrier((values,) + others)[0]


def shards(
    x_in,
    cotangent,
    segment_ids,
    routes,
    qkv_weight,
    out_weight,
    bias_table,
    attn_gain,
    moe_gain,
    router_weight,
    gate_weight,
    up_weight,
    down_weight,
):
    micro_count, _, shard_len, width = x_in.shape
    slot_count = segment_ids.shape[2]
    head_cols = out_weight.shape[0]
    bucket_count, heads_here = bias_table.shape
    head_size = head_cols // heads_here
    expert_count = router_weight.shape[1]
    experts_here = gate_weight.shape[0]
    devices = expert_count // experts_here
    blocks = slot_count // shard_len
    members = blocks // 2
    half = slot_count // 2
    capacity = max(2, (10 * shard_len + 4 * expert_count - 1) // (4 * expert_count))
    scale = head_size ** (-0.5)
    hidden_index = lax.axis_index("hidden")
    expert_index = lax.axis_index("expert")
    part = hidden_index // members
    attn_gain_f = attn_gain.astype(F32).reshape(1, width)
    moe_gain_f = moe_gain.astype(F32).reshape(1, width)
    token_shape = (devices, experts_here, blocks * capacity, width)
    flat_shape = (devices, experts_here * blocks * capacity, width)
    place_shape = (expert_count, blocks, capacity, width)
    gate_rows = gate_weight.transpose(0, 2, 1)
    up_rows = up_weight.transpose(0, 2, 1)
    router_rows = router_weight.T

    def exchange(buffer):
        return lax.all_to_all(buffer, "expert", split_axis=0, concat_axis=0, tiled=True)

    def gather(values):
        return lax.all_gather(values, "hidden", axis=0, tiled=True)

    def scatter(values):
        return lax.psum_scatter(values, "hidden", scatter_dimension=0, tiled=True)

    states = [dict() for _ in range(micro_count)]
    x_all, other_qkv, all_out, all_routes, other_table = opening(
        x_in[:, 0], qkv_weight.reshape(3 * width, head_cols), out_weight,
        routes[:, 0].transpose(0, 2, 1), bias_table.T.astype(F32), devices, blocks, members,
    )
    x_half = x_all.reshape(micro_count, half, width)
    other_qkv = other_qkv.reshape(qkv_weight.shape)
    all_out = all_out.reshape(blocks, head_cols, width)

    route = all_routes.transpose(1, 0, 2, 3).reshape(micro_count * blocks, 2, shard_len)
    live = segment_ids.reshape(micro_count * blocks, 1, shard_len)
    place, other = find_places(route, live, expert_count, capacity)
    place = place.reshape(micro_count, blocks, 2, shard_len).transpose(0, 2, 1, 3)
    place = place.reshape(micro_count, 2, slot_count)
    other = other.reshape(micro_count, blocks, devices, experts_here, capacity)
    other = exchange(other.transpose(2, 0, 3, 1, 4)).transpose(1, 0, 2, 3, 4)
    other = other.reshape(micro_count, devices, experts_here, blocks * capacity, 1)
    expert_ids = jnp.arange(expert_count, dtype=jnp.int32)
    me = expert_index * experts_here + jnp.arange(experts_here, dtype=jnp.int32)
    plus = me[None, None, :, None, None] == expert_ids
    pairs = plus.astype(F32) - (other == expert_ids).astype(F32)
    pairs = jnp.where(other >= 0, pairs, 0.0).astype(BF16)

    tables = jnp.concatenate([bias_table.T.astype(F32), other_table], axis=0)
    onehot_bucket = bucket_onehot(half, bucket_count)
    bias = position_bias(jnp.einsum("jb,hb->hj", onehot_bucket, tables, precision=PRECISE))
    seg_half = lax.dynamic_slice_in_dim(segment_ids[:, 0], part * half, half, 1)

    def spread(rows, micro):
        return spread_rows(rows, place[micro], expert_count, capacity, shard_len)

    def send_dy(micro, kept, rows):
        kept["dy_sent"] = spread(rows, micro)
        kept["dy"] = exchange(kept["dy_sent"].reshape(flat_shape)).reshape(token_shape)

    def experts(micro, kept, *behind):
        sent = spread(kept["xn2_all"], micro).reshape(token_shape)
        back, y, x, g, hid, dga, dup, dlog = expert_pass(
            after(sent, *behind), kept["dy"], pairs[micro], router_rows, gate_rows, up_rows,
            down_weight, 4 + micro,
        )
        kept["weights"] = (x, g, hid, dga, dup, dlog)
        kept["y_sent"] = y.reshape(flat_shape)
        kept["dx_back"] = back.reshape(place_shape)
        kept["dx_part"] = collect_rows(kept["dx_back"], place[micro], shard_len)
        kept["dxn2"] = scatter(kept["dx_part"])

    states[0]["dy_all"] = gather(cotangent[0, 0])
    send_dy(0, states[0], states[0]["dy_all"])
    for micro in range(1, micro_count):
        before = states[micro - 1]["dy_all"]
        states[micro]["dy_all"] = gather(after(cotangent[micro, 0], before))
    qkv, prob, heads, h1, xn2 = attend(
        after(x_half, states[0]["dy_sent"]), attn_gain_f, qkv_weight, other_qkv, bias, seg_half,
        all_out, x_in[:, 0], moe_gain_f, scale, members,
    )
    behind = ()
    for micro in range(micro_count):
        states[micro]["xn2_all"] = gather(after(xn2[micro], *behind))
        behind = (states[micro]["xn2_all"],)
    for micro in range(1, micro_count):
        send_dy(micro, states[micro], after(states[micro]["dy_all"], xn2))
    behind = ()
    for micro in range(micro_count):
        experts(micro, states[micro], *behind)
        behind = (states[micro]["dx_part"],)
    behind = (states[-1]["dx_part"],)
    for micro in range(micro_count):
        state = states[micro]
        state["y_back"] = exchange(after(state["y_sent"], *behind)).reshape(place_shape)
        behind = (state["y_back"],)
    grads = None
    for micro in range(micro_count):
        state = states[micro]
        state["x_grad"], grads, state["line"], state["moe_gain_grad"], state["attn_gain_grad"] = (
            attend_back(
                state["dxn2"], h1[micro], cotangent[micro, 0], x_in[micro, 0], moe_gain_f,
                attn_gain_f, all_out, x_half[micro], qkv_weight, other_qkv, qkv[micro],
                prob[micro], heads[micro], grads, scale, devices, members,
                4 + micro_count + micro,
            )
        )
    for micro in range(micro_count):
        state = states[micro]
        state["mixed"] = scatter(collect_rows(state["y_back"], place[micro], shard_len))
        state["block_out"] = (h1[micro] + state["mixed"].astype(F32)).astype(BF16)
    pieces = exchange(grads)
    kept = [state["weights"] for state in states]
    kept[-1] = tuple(after(list(kept[-1]), grads))
    dwr, dwg, dwu, dwd = weight_pass(kept)

    def added(name):
        total = states[0][name]
        for state in states[1:]:
            total = total + state[name]
        return total

    lines = added("line").reshape(2 * heads_here, 2 * half)
    table = jnp.einsum("hj,jb->hb", lines, onehot_bucket, precision=PRECISE)
    table = table.reshape(2, heads_here * bucket_count)
    mine = jnp.arange(blocks, dtype=jnp.int32)[:, None]
    table = jnp.where(mine == hidden_index, table[0], 0.0) + jnp.where(
        mine == (hidden_index + members) % blocks, table[1], 0.0
    )
    small = jnp.concatenate(
        [
            jnp.sum(dwr, axis=0).reshape(-1),
            added("attn_gain_grad").reshape(-1),
            added("moe_gain_grad").reshape(-1),
            table.reshape(-1),
        ]
    )
    used = small.shape[0]
    small = jnp.pad(small, (0, -used % 1024)).reshape(-1, 128)
    whole, small = closing(pieces, small, blocks)
    whole = whole.reshape(4 * width, head_cols).astype(F32)
    grad_qkv = whole[: 3 * width].reshape(qkv_weight.shape)
    grad_out = whole[3 * width :].T
    small = small.reshape(-1)
    sizes = (width * expert_count, width, width)
    grad_router = small[: sizes[0]].reshape(expert_count, width).T
    grad_attn_gain = small[sizes[0] : sizes[0] + width]
    grad_moe_gain = small[sizes[0] + width : sizes[0] + 2 * width]
    table = small[sizes[0] + 2 * width : used].reshape(blocks, heads_here, bucket_count)
    grad_table = lax.dynamic_index_in_dim(table, hidden_index, 0, keepdims=False).T
    return (
        jnp.stack([state["block_out"] for state in states])[:, None],
        jnp.stack([state["x_grad"] for state in states])[:, None],
        grad_qkv,
        grad_out,
        grad_table,
        grad_attn_gain,
        grad_moe_gain,
        grad_router,
        dwg.transpose(0, 2, 1),
        dwu.transpose(0, 2, 1),
        dwd,
    )


def solution(mesh):
    return jax.shard_map(
        shards,
        mesh=mesh,
        in_specs=(
            P(None, "expert", "hidden", None),
            P(None, "expert", "hidden", None),
            P(None, "expert", None),
            P(None, "expert", "hidden", None),
            P(None, None, "hidden"),
            P("hidden", None),
            P(None, "hidden"),
            P(),
            P(),
            P(),
            P("expert", None, "hidden"),
            P("expert", None, "hidden"),
            P("expert", "hidden", None),
        ),
        out_specs=(
            P(None, "expert", "hidden", None),
            P(None, "expert", "hidden", None),
            P(None, None, "hidden"),
            P("hidden", None),
            P(None, "hidden"),
            P(),
            P(),
            P(),
            P("expert", None, "hidden"),
            P("expert", None, "hidden"),
            P("expert", "hidden", None),
        ),
        check_vma=False,
    )
```

```python
import functools

import jax
import jax.numpy as jnp
from jax import lax
from jax.experimental import pallas as pl
from jax.experimental.pallas import tpu as pltpu
from jax.sharding import PartitionSpec as P

EPSILON = 1e-06
PRECISE = lax.Precision.HIGHEST
LIMITS = (12, 16, 23, 32, 46, 64, 91)
MASKED = -1000000000.0
GELU_C = 0.7978845608028654
GELU_A = 0.044715
VMEM_LIMIT = 60 * 1024 * 1024
F32 = jnp.float32
BF16 = jnp.bfloat16


def mm(a, b):
    return lax.dot_general(a, b, (((1,), (0,)), ((), ())), preferred_element_type=F32)


def mm_nt(a, b):
    return lax.dot_general(a, b, (((1,), (1,)), ((), ())), preferred_element_type=F32)


def mm_tn(a, b):
    return lax.dot_general(a, b, (((0,), (0,)), ((), ())), preferred_element_type=F32)


def bucket_of(distance):
    magnitude = jnp.abs(distance)
    far_bucket = jnp.full(magnitude.shape, 8, jnp.int32)
    for threshold in LIMITS:
        far_bucket = far_bucket + (magnitude >= threshold).astype(jnp.int32)
    return jnp.where(magnitude < 8, magnitude, far_bucket) + 16 * (distance > 0).astype(jnp.int32)


def bucket_onehot(half, bucket_count):
    lane = jnp.arange(2 * half, dtype=jnp.int32)
    distance = jnp.where(lane < half, lane, lane - 2 * half)
    return (
        bucket_of(distance)[:, None] == jnp.arange(bucket_count, dtype=jnp.int32)[None, :]
    ).astype(F32)


TILE = 128


def bias_kernel(line_ref, out_ref):
    length = out_ref.shape[2]
    line = jnp.broadcast_to(line_ref[0], (8, length))
    row = lax.broadcasted_iota(jnp.int32, (8, length), 0)
    sheet = line
    for r in range(1, 8):
        sheet = jnp.where(row == r, pltpu.roll(line, r, 1), sheet)
    while sheet.shape[0] < TILE:
        sheet = jnp.concatenate([sheet, pltpu.roll(sheet, sheet.shape[0], 1)], axis=0)
    out_ref[0] = sheet.astype(out_ref.dtype)


def position_bias(line):
    heads, length = line.shape
    return pl.pallas_call(
        bias_kernel,
        grid=(heads,),
        out_shape=jax.ShapeDtypeStruct((heads, TILE, length), BF16),
        in_specs=[pl.BlockSpec((1, 1, length), lambda h: (h, 0, 0))],
        out_specs=pl.BlockSpec((1, TILE, length), lambda h: (h, 0, 0)),
        compiler_params=pltpu.CompilerParams(vmem_limit_bytes=VMEM_LIMIT),
        name="position_bias",
    )(line.reshape(heads, 1, length))


def unit_rows(x):
    x = x.astype(F32)
    return x * lax.rsqrt(jnp.mean(x * x, axis=-1, keepdims=True) + EPSILON)


def remote(src, dst, send_sem, recv_sem, device):
    return pltpu.make_async_remote_copy(
        src_ref=src, dst_ref=dst, send_sem=send_sem, recv_sem=recv_sem,
        device_id=device, device_id_type=pl.DeviceIdType.MESH,
    )


def greet(devices):
    barrier = pltpu.get_barrier_semaphore()
    for device in devices:
        pl.semaphore_signal(
            barrier, inc=1, device_id=device, device_id_type=pl.DeviceIdType.MESH
        )
    pl.semaphore_wait(barrier, len(devices))


def bits_of(count):
    return [1 << b for b in range(count.bit_length() - 1)]


def partner_of(me, step, count):
    found = 0
    for bit in bits_of(count):
        found = found + bit * lax.rem(me // bit + step // bit, 2)
    return found


def any_space():
    return pl.BlockSpec(memory_space=pl.ANY)


def opening_kernel(
    micros, x_ref, qkv_ref, out_ref, routes_ref, table_ref, *refs,
):
    x_all, refs = refs[:micros], refs[micros:]
    (
    qkv_all, out_all, routes_all, table_all,
    x_send, x_recv, qkv_send, qkv_recv, out_send, out_recv, qkv_on_send, qkv_on_recv,
    out_on_send, out_on_recv, routes_send, routes_recv, table_send, table_recv, own_sem,
    ) = refs
    devices, qkv_rows = qkv_all.shape[0], qkv_all.shape[1]
    blocks, out_rows = out_all.shape[0], out_all.shape[2]
    members = x_all[0].shape[0]
    me = lax.axis_index("expert")
    line = lax.axis_index("hidden")
    mine = lax.rem(line, members)
    base = line - mine
    others = [partner_of(me, s, devices) for s in range(1, devices)]
    along = [lax.rem(line + s, blocks) for s in range(1, blocks)]
    across = lax.rem(line + members, blocks)
    greet([(other, line) for other in others] + [(me, z) for z in along])
    own = [
        pltpu.make_async_copy(out_ref.at[pl.ds(me * out_rows, out_rows)], out_all.at[line, me], own_sem.at[0]),
        pltpu.make_async_copy(routes_ref, routes_all.at[line], own_sem.at[1]),
    ]
    for micro in range(micros):
        own.append(
            pltpu.make_async_copy(x_ref.at[micro], x_all[micro].at[mine], own_sem.at[2 + micro])
        )
    for copy in own:
        copy.start()
    first_qkv = remote(
        qkv_ref.at[pl.ds(me * qkv_rows, qkv_rows)], qkv_all.at[me], qkv_send, qkv_recv, (me, across)
    )
    first_qkv.start()
    first_out = []
    small = [remote(table_ref, table_all, table_send, table_recv, (me, across))]
    for s, z in enumerate(along):
        first_out.append(
            remote(
                out_ref.at[pl.ds(me * out_rows, out_rows)], out_all.at[line, me], out_send.at[s],
                out_recv.at[s], (me, z),
            )
        )
        small.append(
            remote(routes_ref, routes_all.at[line], routes_send.at[s], routes_recv.at[s], (me, z))
        )
    for copy in first_out + small:
        copy.start()
    xs = []
    for micro in range(micros):
        for s in range(1, members):
            peer = base + lax.rem(mine + s, members)
            xs.append(
                remote(
                    x_ref.at[micro], x_all[micro].at[mine], x_send.at[micro, s],
                    x_recv.at[micro, s], (me, peer),
                )
            )
    for copy in xs:
        copy.start()
    first_qkv.wait_recv()
    second = []
    for s, other in enumerate(others):
        second.append(
            remote(
                qkv_all.at[me], qkv_all.at[me], qkv_on_send.at[s], qkv_on_recv.at[s], (other, line)
            )
        )
        second[-1].start()
    own[0].wait()
    for copy in first_out:
        copy.wait_recv()
    for s, other in enumerate(others):
        second.append(
            remote(
                out_all.at[:, me], out_all.at[:, me], out_on_send.at[s], out_on_recv.at[s],
                (other, line),
            )
        )
        second[-1].start()
    for copy in own[1:]:
        copy.wait()
    first_qkv.wait_send()
    for copy in first_out:
        copy.wait_send()
    for copy in small + xs + second:
        copy.wait()


def opening(x, qkv, out, routes, table, devices, blocks, members):
    micros, shard_len, width = x.shape
    dma = pltpu.SemaphoreType.DMA
    return pl.pallas_call(
        functools.partial(opening_kernel, micros),
        out_shape=(jax.ShapeDtypeStruct((members, shard_len, width), BF16),) * micros
        + (
            jax.ShapeDtypeStruct((devices, qkv.shape[0] // devices, qkv.shape[1]), BF16),
            jax.ShapeDtypeStruct((blocks, devices, out.shape[0] // devices, width), BF16),
            jax.ShapeDtypeStruct((blocks,) + routes.shape, jnp.int32),
            jax.ShapeDtypeStruct(table.shape, table.dtype),
        ),
        in_specs=[any_space()] * 5,
        out_specs=(any_space(),) * (4 + micros),
        scratch_shapes=[
            dma((micros, members)), dma((micros, members)), dma, dma, dma((blocks,)), dma((blocks,)),
            dma((devices,)), dma((devices,)), dma((devices,)), dma((devices,)), dma((blocks,)),
            dma((blocks,)), dma, dma, dma((2 + micros,)),
        ],
        compiler_params=pltpu.CompilerParams(collective_id=1, has_side_effects=True),
        cost_estimate=pl.CostEstimate(flops=0, bytes_accessed=60000000, transcendentals=0),
        name="opening",
    )(x, qkv, out, routes, table)


def unit_rows(x):
    x = x.astype(F32)
    return x * lax.rsqrt(jnp.mean(x * x, axis=-1, keepdims=True) + EPSILON)


def attend_kernel(
    scale, x_ref, gain_ref, own_ref, other_ref, bias_ref, seg_row_ref, seg_col_ref,
    out_ref, x_own_ref, moe_gain_ref,
    qkv_ref, prob_ref, heads_ref, h1_ref, xn2_ref,
    xn_ref, part_ref, got_ref, send_sem, recv_sem,
):
    micros, members, shard_len, both = got_ref.shape
    cols = both // 2
    heads, length = bias_ref.shape[0], bias_ref.shape[2]
    half = members * shard_len
    size = cols // heads
    micro, group = pl.program_id(0), pl.program_id(1)
    me = lax.axis_index("expert")
    line = lax.axis_index("hidden")
    mine = lax.rem(line, members)
    part = line // members
    base = line - mine

    def swap(m, s):
        peer = lax.rem(mine + s, members)
        return remote(
            part_ref.at[m, peer], got_ref.at[m, mine], send_sem.at[m, s], recv_sem.at[m, s],
            (me, base + peer),
        )

    @pl.when((micro == 0) & (group == 0))
    def _():
        greet([(me, base + lax.rem(mine + s, members)) for s in range(1, members)])

    @pl.when(group == 0)
    def _():
        xn_ref[...] = (unit_rows(x_ref[0]) * gain_ref[...]).astype(BF16)
        for t in range(3):
            qkv_ref[0, 0, t] = mm(xn_ref[...], own_ref[t]).astype(BF16)

    @pl.when(group > 0)
    def _():
        for t in range(3):
            qkv_ref[0, 0, t] = mm(xn_ref[...], other_ref[t]).astype(BF16)

    seg_row = seg_row_ref[0]
    for head in range(heads):
        inner = slice(head * size, (head + 1) * size)
        keys = qkv_ref[0, 0, 1, :, inner]
        values = qkv_ref[0, 0, 2, :, inner]
        for start in range(0, half, TILE):
            rows = slice(start, start + TILE)
            scores = mm_nt(qkv_ref[0, 0, 0, rows, inner], keys) * scale
            shift = bias_ref[head, :, : half - start]
            if start:
                shift = jnp.concatenate([bias_ref[head, :, length - start :], shift], axis=1)
            scores = scores + shift.astype(F32)
            scores = jnp.where(seg_col_ref[0, rows, :] == seg_row, scores, MASKED)
            top = jnp.max(scores, axis=-1, keepdims=True)
            weights = jnp.exp(scores - top)
            inverse = 1.0 / jnp.sum(weights, axis=-1, keepdims=True)
            prob = (weights * inverse).astype(BF16)
            prob_ref[0, 0, head, rows, :] = prob
            heads_ref[0, rows, inner] = mm(prob, values).astype(BF16)

    for g in range(2):

        @pl.when(group == g)
        def _(g=g):
            for member in range(members):
                rows = slice(member * shard_len, (member + 1) * shard_len)
                part_ref[micro, member, :, g * cols : (g + 1) * cols] = heads_ref[0, rows, :]

    @pl.when(group == 1)
    def _():
        got_ref[micro, mine] = part_ref[micro, mine]
        for s in range(1, members):
            swap(micro, s).start()

    @pl.when((micro == micros - 1) & (group == 1))
    def _():
        for m in range(micros):
            for s in range(1, members):
                swap(m, s).wait_recv()
            h1 = x_own_ref[m].astype(F32)
            for member in range(members):
                for j in range(2):
                    index = lax.rem(part + j, 2) * members + member
                    h1 = h1 + mm(got_ref[m, member, :, j * cols : (j + 1) * cols], out_ref[index])
            h1_ref[m] = h1
            xn2_ref[m] = (unit_rows(h1) * moe_gain_ref[...]).astype(BF16)
        for m in range(micros):
            for s in range(1, members):
                swap(m, s).wait_send()


def attend(
    x, gain, own_weight, other_weight, bias, seg, out_weight, x_own, moe_gain, scale, members, identity
):
    micros, half, width = x.shape
    cols = own_weight.shape[2]
    heads = bias.shape[0] // 2
    shard_len = half // members

    def once(shape):
        return pl.BlockSpec(shape, lambda m, p: (0,) * len(shape), pipeline_mode=pl.Buffered(1))

    return pl.pallas_call(
        functools.partial(attend_kernel, scale),
        grid=(micros, 2),
        out_shape=(
            jax.ShapeDtypeStruct((micros, 2, 3, half, cols), BF16),
            jax.ShapeDtypeStruct((micros, 2, heads, half, half), BF16),
            jax.ShapeDtypeStruct((micros, half, 2 * cols), BF16),
            jax.ShapeDtypeStruct((micros, shard_len, width), F32),
            jax.ShapeDtypeStruct((micros, shard_len, width), BF16),
        ),
        in_specs=[
            pl.BlockSpec((1, half, width), lambda m, p: (m, 0, 0)),
            once((1, width)),
            once((3, width, cols)),
            once((3, width, cols)),
            pl.BlockSpec((heads,) + bias.shape[1:], lambda m, p: (p, 0, 0)),
            pl.BlockSpec((1, 1, half), lambda m, p: (m, 0, 0)),
            pl.BlockSpec((1, half, 1), lambda m, p: (m, 0, 0)),
            once(out_weight.shape),
            once(x_own.shape),
            once((1, width)),
        ],
        out_specs=(
            pl.BlockSpec((1, 1, 3, half, cols), lambda m, p: (m, p, 0, 0, 0)),
            pl.BlockSpec((1, 1, heads, half, half), lambda m, p: (m, p, 0, 0, 0)),
            pl.BlockSpec((1, half, cols), lambda m, p: (m, 0, p)),
            pl.BlockSpec((micros, shard_len, width), lambda m, p: (0, 0, 0)),
            pl.BlockSpec((micros, shard_len, width), lambda m, p: (0, 0, 0)),
        ),
        scratch_shapes=[
            pltpu.VMEM((half, width), BF16),
            pltpu.VMEM((micros, members, shard_len, 2 * cols), BF16),
            pltpu.VMEM((micros, members, shard_len, 2 * cols), BF16),
            pltpu.SemaphoreType.DMA((micros, members)),
            pltpu.SemaphoreType.DMA((micros, members)),
        ],
        compiler_params=pltpu.CompilerParams(
            vmem_limit_bytes=VMEM_LIMIT, collective_id=identity, has_side_effects=True
        ),
        cost_estimate=pl.CostEstimate(
            flops=micros * 2 * half * cols * (8 * width + 4 * half),
            bytes_accessed=40000000,
            transcendentals=micros * 2 * heads * half * half,
        ),
        name="attend",
    )(
        x, gain, own_weight, other_weight, bias, seg.reshape(micros, 1, half),
        seg.reshape(micros, half, 1), out_weight, x_own, moe_gain,
    )


def back_kernel(
    scale, added, grad_ref, h1_ref, dy_ref, x_own_ref, moe_gain_ref, gain_ref, out_ref, x_ref,
    own_ref, other_ref, qkv_ref, prob_ref, heads_ref, *refs,
):
    if added:
        prev_ref, refs = refs[0], refs[1:]
    (
        xgrad_ref, grads_ref, line_ref, dmoe_ref, dgain_ref,
        dh1_ref, dattn_all, dheads_part, dheads_all, dxn_part, dxn_got, total_ref, xn_ref, ds_ref,
        dproj_ref, sheet_ref, attn_send, attn_recv, heads_send, heads_recv, dxn_send, dxn_recv,
    ) = refs
    members, shard_len, width = dattn_all.shape
    heads, half = prob_ref.shape[1], prob_ref.shape[2]
    cols = dproj_ref.shape[2]
    size = cols // heads
    length = sheet_ref.shape[1]
    group = pl.program_id(0)
    me = lax.axis_index("expert")
    line = lax.axis_index("hidden")
    mine = lax.rem(line, members)
    part = line // members
    base = line - mine
    steps = range(1, members)

    def peer_of(s):
        return lax.rem(mine + s, members)

    def attn_copy(s):
        return remote(
            dattn_all.at[mine], dattn_all.at[mine], attn_send.at[s], attn_recv.at[s],
            (me, base + peer_of(s)),
        )

    def heads_copy(s):
        return remote(
            dheads_part.at[peer_of(s)], dheads_all.at[mine], heads_send.at[s], heads_recv.at[s],
            (me, base + peer_of(s)),
        )

    def dxn_copy(s):
        return remote(
            dxn_part.at[peer_of(s)], dxn_got.at[mine], dxn_send.at[s], dxn_recv.at[s],
            (me, base + peer_of(s)),
        )

    @pl.when(group == 0)
    def _():
        greet([(me, base + peer_of(s)) for s in steps])
        grad = grad_ref[...].astype(F32)
        h1 = h1_ref[...]
        r2 = lax.rsqrt(jnp.mean(h1 * h1, axis=-1, keepdims=True) + EPSILON)
        unit = h1 * r2
        dmoe_ref[...] = jnp.sum(grad * unit, axis=0, keepdims=True)
        weighted = grad * moe_gain_ref[...]
        inner = jnp.mean(weighted * unit, axis=-1, keepdims=True)
        dh1 = dy_ref[...].astype(F32) + r2 * (weighted - unit * inner)
        dh1_ref[...] = dh1
        dattn = dh1.astype(BF16)
        dattn_all[mine] = dattn
        for member in range(members):
            for j in range(2):
                index = lax.rem(part + j, 2) * members + member
                dheads = mm_nt(dattn, out_ref[index]).astype(BF16)
                dheads_part[member, :, j * cols : (j + 1) * cols] = dheads
        for s in steps:
            heads_copy(s).start()
        for s in steps:
            attn_copy(s).start()
        dheads_all[mine] = dheads_part[mine]
        xn_ref[...] = (unit_rows(x_ref[...]) * gain_ref[...]).astype(BF16)
        for s in steps:
            heads_copy(s).wait_recv()

    for g in range(2):

        @pl.when(group == g)
        def _(g=g):
            for head in range(heads):
                inner_cols = slice(head * size, (head + 1) * size)
                outer_cols = slice(g * cols + head * size, g * cols + (head + 1) * size)
                values = qkv_ref[0, 2, :, inner_cols]
                grads = dheads_all[:, :, outer_cols].reshape(half, size)
                sheet_ref[...] = jnp.zeros_like(sheet_ref)
                for start in range(0, half, TILE):
                    rows = slice(start, start + TILE)
                    prob = prob_ref[0, head, rows, :].astype(F32)
                    dprob = mm_nt(grads[rows], values)
                    inner = jnp.sum(prob * dprob, axis=-1, keepdims=True)
                    dscore = (prob * (dprob - inner)).astype(BF16)
                    ds_ref[rows, :] = dscore
                    dscore = dscore.astype(F32)
                    sheet_ref[:, : half - start] += dscore[:, start:]
                    if start:
                        sheet_ref[:, length - start :] += dscore[:, :start]
                dscores = ds_ref[...]
                keys, queries = qkv_ref[0, 1, :, inner_cols], qkv_ref[0, 0, :, inner_cols]
                dproj_ref[0, :, inner_cols] = (mm(dscores, keys) * scale).astype(BF16)
                dproj_ref[1, :, inner_cols] = (mm_tn(dscores, queries) * scale).astype(BF16)
                dproj_ref[2, :, inner_cols] = mm_tn(prob_ref[0, head], grads).astype(BF16)
                sheet = sheet_ref[...]
                while sheet.shape[0] > 8:
                    upper = sheet.shape[0] // 2
                    sheet = sheet[:upper] + pltpu.roll(sheet[upper:], length - upper, 1)
                row = lax.broadcasted_iota(jnp.int32, (8, length), 0)
                found = jnp.zeros((1, length), F32)
                for r in range(8):
                    moved = pltpu.roll(sheet, length - r, 1) if r else sheet
                    found = found + jnp.sum(
                        jnp.where(row == r, moved, 0.0), axis=0, keepdims=True
                    )
                line_ref[0, head : head + 1, :] = found

    def products(weight_ref):
        dxn = mm_nt(dproj_ref[0], weight_ref[0])
        for t in range(1, 3):
            dxn = dxn + mm_nt(dproj_ref[t], weight_ref[t])
        return dxn.reshape(members, shard_len, width)

    @pl.when(group == 0)
    def _():
        total_ref[...] = products(own_ref)
        for s in steps:
            attn_copy(s).wait_recv()

    @pl.when(group == 1)
    def _():
        total_ref[...] += products(other_ref)
        dxn_part[...] = total_ref[...].astype(BF16)
        for s in steps:
            dxn_copy(s).start()

    per = grads_ref.shape[0] // 4
    for t in range(4):
        if t < 3:
            found = mm_tn(xn_ref[...], dproj_ref[t])
        else:
            found = mm_tn(dattn_all[...].reshape(half, width), heads_ref[...])
        found = found.reshape(per, 1, width // per, cols)
        if added:
            found = found + prev_ref[t * per : (t + 1) * per].astype(F32)
        grads_ref[t * per : (t + 1) * per] = found.astype(BF16)

    @pl.when(group == 1)
    def _():
        total = total_ref[...].reshape(half, width)
        dgain_ref[...] = jnp.sum(total * unit_rows(x_ref[...]), axis=0, keepdims=True)
        x_own = x_own_ref[...].astype(F32)
        r1 = lax.rsqrt(jnp.mean(x_own * x_own, axis=-1, keepdims=True) + EPSILON)
        unit = x_own * r1
        for s in steps:
            dxn_copy(s).wait_recv()
        dxn1 = total_ref[mine]
        for s in steps:
            dxn1 = dxn1 + dxn_got[lax.rem(mine + members - s, members)].astype(F32)
        weighted = dxn1 * gain_ref[...]
        inner = jnp.mean(weighted * unit, axis=-1, keepdims=True)
        xgrad_ref[...] = (dh1_ref[...] + r1 * (weighted - unit * inner)).astype(BF16)
        for s in steps:
            heads_copy(s).wait_send()
            attn_copy(s).wait_send()
            dxn_copy(s).wait_send()


def attend_back(
    grad, h1, dy, x_own, moe_gain, gain, out_weight, x_half, own_weight, other_weight, qkv, prob,
    heads_out, prev, scale, pieces, members, identity,
):
    _, heads, half = prob.shape[:3]
    width, cols = own_weight.shape[1:]
    shard_len = half // members
    length = 2 * half
    rows = 4 * width // pieces

    def once(shape):
        return pl.BlockSpec(shape, lambda p: (0,) * len(shape), pipeline_mode=pl.Buffered(1))

    pieces_spec = pl.BlockSpec((pieces, 1, rows, cols), lambda p: (0, p, 0, 0))
    operands = [
        grad, h1, dy, x_own, moe_gain, gain, out_weight, x_half, own_weight, other_weight, qkv,
        prob, heads_out,
    ]
    in_specs = [once(array.shape) for array in operands[:10]] + [
        pl.BlockSpec((1, 3, half, cols), lambda p: (p, 0, 0, 0)),
        pl.BlockSpec((1, heads, half, half), lambda p: (p, 0, 0, 0)),
        pl.BlockSpec((half, cols), lambda p: (0, p)),
    ]
    if prev is not None:
        operands.append(prev)
        in_specs.append(pieces_spec)
    dma = pltpu.SemaphoreType.DMA
    return pl.pallas_call(
        functools.partial(back_kernel, scale, prev is not None),
        grid=(2,),
        out_shape=(
            jax.ShapeDtypeStruct((shard_len, width), BF16),
            jax.ShapeDtypeStruct((pieces, 2, rows, cols), BF16),
            jax.ShapeDtypeStruct((2, heads, length), F32),
            jax.ShapeDtypeStruct((1, width), F32),
            jax.ShapeDtypeStruct((1, width), F32),
        ),
        in_specs=in_specs,
        out_specs=(
            pl.BlockSpec((shard_len, width), lambda p: (0, 0)),
            pieces_spec,
            pl.BlockSpec((1, heads, length), lambda p: (p, 0, 0)),
            pl.BlockSpec((1, width), lambda p: (0, 0)),
            pl.BlockSpec((1, width), lambda p: (0, 0)),
        ),
        scratch_shapes=[
            pltpu.VMEM((shard_len, width), F32),
            pltpu.VMEM((members, shard_len, width), BF16),
            pltpu.VMEM((members, shard_len, 2 * cols), BF16),
            pltpu.VMEM((members, shard_len, 2 * cols), BF16),
            pltpu.VMEM((members, shard_len, width), BF16),
            pltpu.VMEM((members, shard_len, width), BF16),
            pltpu.VMEM((members, shard_len, width), F32),
            pltpu.VMEM((half, width), BF16),
            pltpu.VMEM((half, half), BF16),
            pltpu.VMEM((3, half, cols), BF16),
            pltpu.VMEM((TILE, length), F32),
            dma((members,)), dma((members,)), dma((members,)), dma((members,)), dma((members,)),
            dma((members,)),
        ],
        compiler_params=pltpu.CompilerParams(
            vmem_limit_bytes=VMEM_LIMIT, collective_id=identity, has_side_effects=True
        ),
        cost_estimate=pl.CostEstimate(
            flops=2 * half * cols * (16 * width + 8 * half),
            bytes_accessed=40000000,
            transcendentals=0,
        ),
        name="attend_back",
    )(*operands)


def closing_kernel(
    pieces_ref, small_ref, whole_ref, sum_ref,
    total_ref, moved_ref, moved_got, piece_ref, small_got, line_sum, line_got,
    small_send, small_recv, line_send, line_recv, moved_send, moved_recv, on_send, on_recv, own_sem,
):
    devices = pieces_ref.shape[0]
    blocks = line_got.shape[0]
    me = lax.axis_index("expert")
    line = lax.axis_index("hidden")
    others = [partner_of(me, s, devices) for s in range(1, devices)]
    along = [lax.rem(line + s, blocks) for s in range(1, blocks)]
    across = lax.rem(line + blocks // 2, blocks)
    greet([(other, line) for other in others] + [(me, z) for z in along])
    smalls = [
        remote(small_ref, small_got.at[me], small_send.at[s], small_recv.at[s], (other, line))
        for s, other in enumerate(others)
    ]
    for copy in smalls:
        copy.start()
    small_got[me] = small_ref[...]
    moved = jnp.sum(pieces_ref[:, 1].astype(F32), axis=0)
    moved_ref[...] = moved.astype(BF16)
    cross = remote(moved_ref, moved_got, moved_send, moved_recv, (me, across))
    cross.start()
    total_ref[...] = jnp.sum(pieces_ref[:, 0].astype(F32), axis=0)
    cross.wait_recv()
    piece_ref[...] = (total_ref[...] + moved_got[...].astype(F32)).astype(BF16)
    onward = [
        remote(piece_ref, whole_ref.at[me], on_send.at[s], on_recv.at[s], (other, line))
        for s, other in enumerate(others)
    ]
    for copy in onward:
        copy.start()
    own = pltpu.make_async_copy(piece_ref, whole_ref.at[me], own_sem)
    own.start()
    for copy in smalls:
        copy.wait_recv()
    line_sum[...] = jnp.sum(small_got[...], axis=0)
    lines = [
        remote(line_sum, line_got.at[line], line_send.at[s], line_recv.at[s], (me, z))
        for s, z in enumerate(along)
    ]
    for copy in lines:
        copy.start()
    line_got[line] = line_sum[...]
    for copy in lines:
        copy.wait_recv()
    sum_ref[...] = jnp.sum(line_got[...], axis=0)
    own.wait()
    cross.wait_send()
    for copy in smalls + lines:
        copy.wait_send()
    for copy in onward:
        copy.wait()


def closing(pieces, small, blocks):
    devices, _, rows, cols = pieces.shape
    vmem = pl.BlockSpec(memory_space=pltpu.VMEM)
    dma = pltpu.SemaphoreType.DMA
    return pl.pallas_call(
        closing_kernel,
        out_shape=(
            jax.ShapeDtypeStruct((devices, rows, cols), BF16),
            jax.ShapeDtypeStruct(small.shape, F32),
        ),
        in_specs=[vmem, vmem],
        out_specs=(any_space(), vmem),
        scratch_shapes=[
            pltpu.VMEM((rows, cols), F32),
            pltpu.VMEM((rows, cols), BF16),
            pltpu.VMEM((rows, cols), BF16),
            pltpu.VMEM((rows, cols), BF16),
            pltpu.VMEM((devices,) + small.shape, F32),
            pltpu.VMEM(small.shape, F32),
            pltpu.VMEM((blocks,) + small.shape, F32),
            dma((devices,)), dma((devices,)), dma((blocks,)), dma((blocks,)), dma, dma,
            dma((devices,)), dma((devices,)), dma,
        ],
        compiler_params=pltpu.CompilerParams(
            vmem_limit_bytes=VMEM_LIMIT, collective_id=3, has_side_effects=True
        ),
        cost_estimate=pl.CostEstimate(flops=0, bytes_accessed=60000000, transcendentals=0),
        name="closing",
    )(pieces, small)


def spread(rows, place0, place1, count):
    ids = lax.broadcasted_iota(jnp.int32, (count, rows.shape[0]), 0)
    hit = (ids == place0) | (ids == place1)
    return mm(jnp.where(hit, 1.0, 0.0).astype(BF16), rows)


def spread_kernel(rows_ref, place_ref, out_ref):
    experts, _, cap, width = out_ref.shape
    placed = spread(rows_ref[...], place_ref[0:1, :], place_ref[1:2, :], experts * cap)
    out_ref[...] = placed.astype(BF16).reshape(experts, 1, cap, width)


def spread_rows(rows, place, experts, cap, shard_len):
    slots, width = rows.shape
    blocks = slots // shard_len
    return pl.pallas_call(
        spread_kernel,
        grid=(blocks,),
        out_shape=jax.ShapeDtypeStruct((experts, blocks, cap, width), BF16),
        in_specs=[
            pl.BlockSpec((shard_len, width), lambda b: (b, 0)),
            pl.BlockSpec((2, shard_len), lambda b: (0, b)),
        ],
        out_specs=pl.BlockSpec((experts, 1, cap, width), lambda b: (0, b, 0, 0)),
        compiler_params=pltpu.CompilerParams(vmem_limit_bytes=VMEM_LIMIT),
        cost_estimate=pl.CostEstimate(
            flops=2 * experts * cap * slots * width,
            bytes_accessed=2 * slots * width + 2 * experts * blocks * cap * width,
            transcendentals=0,
        ),
        name="spread_rows",
    )(rows, place)


def collect_kernel(rows_ref, place_ref, out_ref):
    experts, _, cap, width = rows_ref.shape
    tokens = out_ref.shape[0]
    ids = lax.broadcasted_iota(jnp.int32, (experts * cap, tokens), 0)
    hit = (ids == place_ref[0:1, :]) | (ids == place_ref[1:2, :])
    rows = rows_ref[...].reshape(experts * cap, width)
    out_ref[...] = mm_tn(jnp.where(hit, 1.0, 0.0).astype(BF16), rows).astype(BF16)


def collect_rows(rows, place, shard_len):
    experts, blocks, cap, width = rows.shape
    slots = blocks * shard_len
    return pl.pallas_call(
        collect_kernel,
        grid=(blocks,),
        out_shape=jax.ShapeDtypeStruct((slots, width), BF16),
        in_specs=[
            pl.BlockSpec((experts, 1, cap, width), lambda b: (0, b, 0, 0)),
            pl.BlockSpec((2, shard_len), lambda b: (0, b)),
        ],
        out_specs=pl.BlockSpec((shard_len, width), lambda b: (b, 0)),
        compiler_params=pltpu.CompilerParams(vmem_limit_bytes=VMEM_LIMIT),
        cost_estimate=pl.CostEstimate(
            flops=2 * experts * cap * slots * width,
            bytes_accessed=2 * slots * width + 2 * experts * blocks * cap * width,
            transcendentals=0,
        ),
        name="collect_rows",
    )(rows, place)


def place_kernel(cap, route_ref, live_ref, place_ref, other_ref):
    shard_len = route_ref.shape[2]
    count = other_ref.shape[1]
    experts = count // cap
    first, second = route_ref[0, 0:1, :], route_ref[0, 1:2, :]
    live = live_ref[0] >= 0
    ids = lax.broadcasted_iota(jnp.int32, (experts, shard_len), 0)
    chosen = ((ids == first) | (ids == second)) & live
    row = lax.broadcasted_iota(jnp.int32, (shard_len, shard_len), 0)
    col = lax.broadcasted_iota(jnp.int32, (shard_len, shard_len), 1)
    earlier = jnp.where(row < col, 1.0, 0.0).astype(BF16)
    before = mm(jnp.where(chosen, 1.0, 0.0).astype(BF16), earlier)
    spots = lax.broadcasted_iota(jnp.int32, (count, shard_len), 0)
    other = jnp.full((count, 1), -1, jnp.int32)
    for k, route in enumerate((first, second)):
        position = jnp.sum(jnp.where(ids == route, before, 0.0), axis=0, keepdims=True)
        place = jnp.where(live, route * cap + position.astype(jnp.int32), -1)
        place_ref[0, k : k + 1, :] = place
        partner = (second, first)[k]
        found = jnp.max(jnp.where(spots == place, partner, -1), axis=1, keepdims=True)
        other = jnp.maximum(other, found)
    other_ref[0] = other


def find_places(route, live, experts, cap):
    count, _, shard_len = route.shape
    return pl.pallas_call(
        functools.partial(place_kernel, cap),
        grid=(count,),
        out_shape=(
            jax.ShapeDtypeStruct((count, 2, shard_len), jnp.int32),
            jax.ShapeDtypeStruct((count, experts * cap, 1), jnp.int32),
        ),
        in_specs=[
            pl.BlockSpec((1, 2, shard_len), lambda b: (b, 0, 0)),
            pl.BlockSpec((1, 1, shard_len), lambda b: (b, 0, 0)),
        ],
        out_specs=(
            pl.BlockSpec((1, 2, shard_len), lambda b: (b, 0, 0)),
            pl.BlockSpec((1, experts * cap, 1), lambda b: (b, 0, 0)),
        ),
        compiler_params=pltpu.CompilerParams(vmem_limit_bytes=VMEM_LIMIT),
        name="find_places",
    )(route, live)


def expert_kernel(
    sent_ref, dy_ref, pair_ref, wr_ref, wg_ref, wu_ref, wd_ref,
    back_ref, y_ref, x_ref, g_ref, hid_ref, dga_ref, dup_ref, dlog_ref,
    got_ref, dx_ref, stage_ref, x_send, x_recv, dx_send, dx_recv, own_sem, stage_sem,
):
    devices, experts, cap, width = sent_ref.shape
    step = pl.program_id(0)
    me = lax.axis_index("expert")
    line = lax.axis_index("hidden")

    def x_copy(s):
        peer = partner_of(me, s, devices)
        return pltpu.make_async_remote_copy(
            src_ref=sent_ref.at[peer], dst_ref=got_ref.at[s], send_sem=x_send.at[s],
            recv_sem=x_recv.at[s], device_id=(peer, line), device_id_type=pl.DeviceIdType.MESH,
        )

    def dx_copy(s):
        peer = partner_of(me, s, devices)
        return pltpu.make_async_remote_copy(
            src_ref=dx_ref.at[s], dst_ref=back_ref.at[me], send_sem=dx_send.at[s],
            recv_sem=dx_recv.at[s], device_id=(peer, line), device_id_type=pl.DeviceIdType.MESH,
        )

    def y_copy(s):
        source = partner_of(me, s, devices)
        slot = lax.rem(s, 2)
        return pltpu.make_async_copy(stage_ref.at[slot], y_ref.at[source], stage_sem.at[slot])

    def work(s):
        source = partner_of(me, s, devices)
        slot = lax.rem(s, 2)
        for e in range(experts):
            x = got_ref[s, e]
            dy = dy_ref[source, e].astype(F32)
            pair = pair_ref[source, e].astype(F32)
            margin = jnp.sum(mm_nt(x, wr_ref[...]) * pair, axis=-1, keepdims=True)
            own_gate = 1.0 / (1.0 + jnp.exp(-margin))
            other_gate = 1.0 / (1.0 + jnp.exp(margin))
            g = (own_gate * dy).astype(BF16)
            x_ref[0, e] = x
            g_ref[0, e] = g
            gate = mm_nt(x, wg_ref[e])
            up = mm_nt(x, wu_ref[e])
            square = gate * gate
            bent = jnp.tanh(GELU_C * gate * (1.0 + GELU_A * square))
            half_gate = 0.5 * gate
            gelu = half_gate * (1.0 + bent)
            slope = 0.5 * (1.0 + bent) + half_gate * (1.0 - bent * bent) * (
                GELU_C * (1.0 + 3.0 * GELU_A * square)
            )
            hid = (gelu * up).astype(BF16)
            dhid = mm_nt(g, wd_ref[e])
            dga = (dhid * (up * slope)).astype(BF16)
            dup = (dhid * gelu).astype(BF16)
            hid_ref[0, e] = hid
            dga_ref[0, e] = dga
            dup_ref[0, e] = dup
            y = mm(hid, wd_ref[e])
            dgate = jnp.sum(y * dy, axis=-1, keepdims=True)
            stage_ref[slot, e] = (y * own_gate).astype(BF16)
            dlog = (dgate * own_gate * other_gate * pair).astype(BF16)
            dlog_ref[0, e] = dlog
            dx = mm(dga, wg_ref[e]) + mm(dup, wu_ref[e]) + mm(dlog, wr_ref[...])
            dx_ref[s, e] = dx.astype(BF16)

    @pl.when(step == 0)
    def _():
        barrier = pltpu.get_barrier_semaphore()
        for s in range(1, devices):
            pl.semaphore_signal(
                barrier, inc=1, device_id=(partner_of(me, s, devices), line),
                device_id_type=pl.DeviceIdType.MESH,
            )
        pl.semaphore_wait(barrier, devices - 1)
        for s in range(devices - 1, 0, -1):
            x_copy(s).start()
        own = pltpu.make_async_copy(sent_ref.at[me], got_ref.at[0], own_sem)
        own.start()
        own.wait()

    @pl.when(step > 0)
    def _():
        x_copy(step).wait_recv()

    @pl.when(step > 1)
    def _():
        y_copy(step - 2).wait()

    work(step)
    y_copy(step).start()

    @pl.when(step > 0)
    def _():
        dx_copy(step).start()

    @pl.when(step == devices - 1)
    def _():
        own = pltpu.make_async_copy(dx_ref.at[0], back_ref.at[me], own_sem)
        own.start()
        own.wait()
        y_copy(devices - 2).wait()
        y_copy(devices - 1).wait()
        for s in range(1, devices):
            x_copy(s).wait_send()
            dx_copy(s).wait_send()
            dx_copy(s).wait_recv()


def expert_pass(sent, dy, pair, wr, wg, wu, wd, identity):
    devices, experts, cap, width = sent.shape
    hidden = wg.shape[1]
    choices = wr.shape[0]

    def whole(shape):
        return pl.BlockSpec(shape, lambda s: (0,) * len(shape), pipeline_mode=pl.Buffered(1))

    def block(cols):
        return pl.BlockSpec((1, experts, cap, cols), lambda s: (s, 0, 0, 0))

    def kept(cols):
        return jax.ShapeDtypeStruct((devices, experts, cap, cols), BF16)

    rows = devices * cap
    return pl.pallas_call(
        expert_kernel,
        grid=(devices,),
        out_shape=(
            kept(width), kept(width), kept(width), kept(width), kept(hidden), kept(hidden),
            kept(hidden), kept(choices),
        ),
        in_specs=[
            any_space(), whole(dy.shape), whole(pair.shape), whole(wr.shape), whole(wg.shape),
            whole(wu.shape), whole(wd.shape),
        ],
        out_specs=(
            any_space(), any_space(), block(width), block(width), block(hidden), block(hidden),
            block(hidden), block(choices),
        ),
        scratch_shapes=[
            pltpu.VMEM((devices, experts, cap, width), BF16),
            pltpu.VMEM((devices, experts, cap, width), BF16),
            pltpu.VMEM((2, experts, cap, width), BF16),
            pltpu.SemaphoreType.DMA((devices,)),
            pltpu.SemaphoreType.DMA((devices,)),
            pltpu.SemaphoreType.DMA((devices,)),
            pltpu.SemaphoreType.DMA((devices,)),
            pltpu.SemaphoreType.DMA,
            pltpu.SemaphoreType.DMA((2,)),
        ],
        compiler_params=pltpu.CompilerParams(
            vmem_limit_bytes=VMEM_LIMIT, collective_id=identity, has_side_effects=True
        ),
        cost_estimate=pl.CostEstimate(
            flops=12 * experts * rows * width * hidden,
            bytes_accessed=80 * experts * rows * width,
            transcendentals=experts * rows * hidden,
        ),
        name="expert_pass",
    )(sent, dy, pair, wr, wg, wu, wd)


def weight_kernel(*refs):
    count = (len(refs) - 4) // 6
    dwr_ref, dwg_ref, dwu_ref, dwd_ref = refs[-4:]
    totals = [0.0, 0.0, 0.0, 0.0]
    for index in range(count):
        blocks = [
            ref[...].reshape(ref.shape[0] * ref.shape[2], ref.shape[3])
            for ref in refs[6 * index : 6 * index + 6]
        ]
        x, g, hid, dga, dup, dlog = blocks
        totals[0] = totals[0] + mm_tn(dlog, x)
        totals[1] = totals[1] + mm_tn(dga, x)
        totals[2] = totals[2] + mm_tn(dup, x)
        totals[3] = totals[3] + mm_tn(hid, g)
    dwr_ref[0] = totals[0]
    dwg_ref[0] = totals[1]
    dwu_ref[0] = totals[2]
    dwd_ref[0] = totals[3]


def weight_pass(kept):
    sources, experts, cap, width = kept[0][0].shape
    hidden = kept[0][2].shape[3]
    choices = kept[0][5].shape[3]
    rows = sources * cap
    block = 256 if width % 256 == 0 else width
    tokens = pl.BlockSpec((sources, 1, cap, block), lambda e, j: (0, e, 0, j))
    acts = pl.BlockSpec((sources, 1, cap, hidden), lambda e, j: (0, e, 0, 0))
    logs = pl.BlockSpec((sources, 1, cap, choices), lambda e, j: (0, e, 0, 0))
    operands = []
    for arrays in kept:
        operands.extend(arrays)
    return pl.pallas_call(
        weight_kernel,
        grid=(experts, width // block),
        out_shape=(
            jax.ShapeDtypeStruct((experts, choices, width), F32),
            jax.ShapeDtypeStruct((experts, hidden, width), F32),
            jax.ShapeDtypeStruct((experts, hidden, width), F32),
            jax.ShapeDtypeStruct((experts, hidden, width), F32),
        ),
        in_specs=[tokens, tokens, acts, acts, acts, logs] * len(kept),
        out_specs=(
            pl.BlockSpec((1, choices, block), lambda e, j: (e, 0, j)),
            pl.BlockSpec((1, hidden, block), lambda e, j: (e, 0, j)),
            pl.BlockSpec((1, hidden, block), lambda e, j: (e, 0, j)),
            pl.BlockSpec((1, hidden, block), lambda e, j: (e, 0, j)),
        ),
        compiler_params=pltpu.CompilerParams(vmem_limit_bytes=VMEM_LIMIT),
        cost_estimate=pl.CostEstimate(
            flops=6 * len(kept) * experts * rows * width * hidden,
            bytes_accessed=len(kept) * experts * rows * (4 * width + 6 * hidden)
            + 12 * experts * width * hidden,
            transcendentals=0,
        ),
        name="weight_pass",
    )(*operands)


def after(values, *others):
    return lax.optimization_barrier((values,) + others)[0]


def shards(
    x_in,
    cotangent,
    segment_ids,
    routes,
    qkv_weight,
    out_weight,
    bias_table,
    attn_gain,
    moe_gain,
    router_weight,
    gate_weight,
    up_weight,
    down_weight,
):
    micro_count, _, shard_len, width = x_in.shape
    slot_count = segment_ids.shape[2]
    head_cols = out_weight.shape[0]
    bucket_count, heads_here = bias_table.shape
    head_size = head_cols // heads_here
    expert_count = router_weight.shape[1]
    experts_here = gate_weight.shape[0]
    devices = expert_count // experts_here
    blocks = slot_count // shard_len
    members = blocks // 2
    half = slot_count // 2
    capacity = max(2, (10 * shard_len + 4 * expert_count - 1) // (4 * expert_count))
    scale = head_size ** (-0.5)
    hidden_index = lax.axis_index("hidden")
    expert_index = lax.axis_index("expert")
    part = hidden_index // members
    attn_gain_f = attn_gain.astype(F32).reshape(1, width)
    moe_gain_f = moe_gain.astype(F32).reshape(1, width)
    token_shape = (devices, experts_here, blocks * capacity, width)
    flat_shape = (devices, experts_here * blocks * capacity, width)
    place_shape = (expert_count, blocks, capacity, width)
    gate_rows = gate_weight.transpose(0, 2, 1)
    up_rows = up_weight.transpose(0, 2, 1)
    router_rows = router_weight.T

    def exchange(buffer):
        return lax.all_to_all(buffer, "expert", split_axis=0, concat_axis=0, tiled=True)

    def gather(values):
        return lax.all_gather(values, "hidden", axis=0, tiled=True)

    def scatter(values):
        return lax.psum_scatter(values, "hidden", scatter_dimension=0, tiled=True)

    states = [dict() for _ in range(micro_count)]
    *x_all, other_qkv, all_out, all_routes, other_table = opening(
        x_in[:, 0], qkv_weight.reshape(3 * width, head_cols), out_weight,
        routes[:, 0].transpose(0, 2, 1), bias_table.T.astype(F32), devices, blocks, members,
    )
    x_half = [x.reshape(1, half, width) for x in x_all]
    other_qkv = other_qkv.reshape(qkv_weight.shape)
    all_out = all_out.reshape(blocks, head_cols, width)

    route = all_routes.transpose(1, 0, 2, 3).reshape(micro_count * blocks, 2, shard_len)
    live = segment_ids.reshape(micro_count * blocks, 1, shard_len)
    place, other = find_places(route, live, expert_count, capacity)
    place = place.reshape(micro_count, blocks, 2, shard_len).transpose(0, 2, 1, 3)
    place = place.reshape(micro_count, 2, slot_count)
    other = other.reshape(micro_count, blocks, devices, experts_here, capacity)
    other = exchange(other.transpose(2, 0, 3, 1, 4)).transpose(1, 0, 2, 3, 4)
    other = other.reshape(micro_count, devices, experts_here, blocks * capacity, 1)
    expert_ids = jnp.arange(expert_count, dtype=jnp.int32)
    me = expert_index * experts_here + jnp.arange(experts_here, dtype=jnp.int32)
    plus = me[None, None, :, None, None] == expert_ids
    pairs = plus.astype(F32) - (other == expert_ids).astype(F32)
    pairs = jnp.where(other >= 0, pairs, 0.0).astype(BF16)

    tables = jnp.concatenate([bias_table.T.astype(F32), other_table], axis=0)
    onehot_bucket = bucket_onehot(half, bucket_count)
    bias = position_bias(jnp.einsum("jb,hb->hj", onehot_bucket, tables, precision=PRECISE))
    seg_half = lax.dynamic_slice_in_dim(segment_ids[:, 0], part * half, half, 1)

    def spread(rows, micro):
        return spread_rows(rows, place[micro], expert_count, capacity, shard_len)

    def send_dy(micro, kept, rows):
        kept["dy_sent"] = spread(rows, micro)
        kept["dy"] = exchange(kept["dy_sent"].reshape(flat_shape)).reshape(token_shape)

    def experts(micro, kept, *behind):
        sent = spread(kept["xn2_all"], micro).reshape(token_shape)
        back, y, x, g, hid, dga, dup, dlog = expert_pass(
            after(sent, *behind), kept["dy"], pairs[micro], router_rows, gate_rows, up_rows,
            down_weight, 4 + micro,
        )
        kept["weights"] = (x, g, hid, dga, dup, dlog)
        kept["y_sent"] = y.reshape(flat_shape)
        kept["dx_back"] = back.reshape(place_shape)
        kept["dx_part"] = collect_rows(kept["dx_back"], place[micro], shard_len)
        kept["dxn2"] = scatter(kept["dx_part"])

    states[0]["dy_all"] = gather(cotangent[0, 0])
    send_dy(0, states[0], states[0]["dy_all"])
    for micro in range(1, micro_count):
        before = states[micro - 1]["dy_all"]
        states[micro]["dy_all"] = gather(after(cotangent[micro, 0], before, all_out))
    behind = (states[0]["dy_sent"],)
    for micro in range(micro_count):
        state = states[micro]
        qkv, prob, heads, h1, xn2 = attend(
            after(x_half[micro], *behind), attn_gain_f, qkv_weight, other_qkv, bias,
            seg_half[micro : micro + 1], all_out, x_in[micro], moe_gain_f, scale, members, 10 + micro,
        )
        state.update(qkv=qkv[0], prob=prob[0], heads=heads[0], h1=h1[0], xn2=xn2[0])
        behind = (xn2,)
    for micro in range(1, micro_count):
        send_dy(micro, states[micro], after(states[micro]["dy_all"], states[-1]["xn2"]))
    behind = ()
    for micro in range(micro_count):
        states[micro]["xn2_all"] = gather(after(states[micro]["xn2"], *behind))
        behind = (states[micro]["xn2_all"], states[-1]["dy_sent"])
    behind = ()
    for micro in range(micro_count):
        experts(micro, states[micro], *behind)
        behind = (states[micro]["dx_part"],)
    behind = (states[-1]["dx_part"],)
    grads = None
    for micro in range(micro_count):
        state = states[micro]
        state["y_back"] = exchange(after(state["y_sent"], *behind)).reshape(place_shape)
        state["x_grad"], grads, state["line"], state["moe_gain_grad"], state["attn_gain_grad"] = (
            attend_back(
                state["dxn2"], state["h1"], cotangent[micro, 0], x_in[micro, 0], moe_gain_f,
                attn_gain_f, all_out, x_half[micro][0], qkv_weight, other_qkv, state["qkv"],
                state["prob"], state["heads"], grads, scale, devices, members,
                4 + micro_count + micro,
            )
        )
        behind = (grads,)
    parts = []
    for micro in range(micro_count):
        state = states[micro]
        parts.append(collect_rows(after(state["y_back"], grads), place[micro], shard_len))
        state["mixed"] = scatter(parts[-1])
        state["block_out"] = (state["h1"] + state["mixed"].astype(F32)).astype(BF16)
    pieces = exchange(grads)
    kept = [state["weights"] for state in states]
    kept[-1] = tuple(after(list(kept[-1]), *parts))
    dwr, dwg, dwu, dwd = weight_pass(kept)

    def added(name):
        total = states[0][name]
        for state in states[1:]:
            total = total + state[name]
        return total

    lines = added("line").reshape(2 * heads_here, 2 * half)
    table = jnp.einsum("hj,jb->hb", lines, onehot_bucket, precision=PRECISE)
    table = table.reshape(2, heads_here * bucket_count)
    mine = jnp.arange(blocks, dtype=jnp.int32)[:, None]
    table = jnp.where(mine == hidden_index, table[0], 0.0) + jnp.where(
        mine == (hidden_index + members) % blocks, table[1], 0.0
    )
    small = jnp.concatenate(
        [
            jnp.sum(dwr, axis=0).reshape(-1),
            added("attn_gain_grad").reshape(-1),
            added("moe_gain_grad").reshape(-1),
            table.reshape(-1),
        ]
    )
    used = small.shape[0]
    small = jnp.pad(small, (0, -used % 1024)).reshape(-1, 128)
    whole, small = closing(pieces, small, blocks)
    whole = whole.reshape(4 * width, head_cols).astype(F32)
    grad_qkv = whole[: 3 * width].reshape(qkv_weight.shape)
    grad_out = whole[3 * width :].T
    small = small.reshape(-1)
    sizes = (width * expert_count, width, width)
    grad_router = small[: sizes[0]].reshape(expert_count, width).T
    grad_attn_gain = small[sizes[0] : sizes[0] + width]
    grad_moe_gain = small[sizes[0] + width : sizes[0] + 2 * width]
    table = small[sizes[0] + 2 * width : used].reshape(blocks, heads_here, bucket_count)
    grad_table = lax.dynamic_index_in_dim(table, hidden_index, 0, keepdims=False).T
    return (
        jnp.stack([state["block_out"] for state in states])[:, None],
        jnp.stack([state["x_grad"] for state in states])[:, None],
        grad_qkv,
        grad_out,
        grad_table,
        grad_attn_gain,
        grad_moe_gain,
        grad_router,
        dwg.transpose(0, 2, 1),
        dwu.transpose(0, 2, 1),
        dwd,
    )


def solution(mesh):
    return jax.shard_map(
        shards,
        mesh=mesh,
        in_specs=(
            P(None, "expert", "hidden", None),
            P(None, "expert", "hidden", None),
            P(None, "expert", None),
            P(None, "expert", "hidden", None),
            P(None, None, "hidden"),
            P("hidden", None),
            P(None, "hidden"),
            P(),
            P(),
            P(),
            P("expert", None, "hidden"),
            P("expert", None, "hidden"),
            P("expert", "hidden", None),
        ),
        out_specs=(
            P(None, "expert", "hidden", None),
            P(None, "expert", "hidden", None),
            P(None, None, "hidden"),
            P("hidden", None),
            P(None, "hidden"),
            P(),
            P(),
            P(),
            P("expert", None, "hidden"),
            P("expert", None, "hidden"),
            P("expert", "hidden", None),
        ),
        check_vma=False,
    )
```

```python
import functools

import jax
import jax.numpy as jnp
from jax import lax
from jax.experimental import pallas as pl
from jax.experimental.pallas import tpu as pltpu
from jax.sharding import PartitionSpec as P

EPSILON = 1e-06
PRECISE = lax.Precision.HIGHEST
LIMITS = (12, 16, 23, 32, 46, 64, 91)
MASKED = -1000000000.0
GELU_C = 0.7978845608028654
GELU_A = 0.044715
VMEM_LIMIT = 60 * 1024 * 1024
F32 = jnp.float32
BF16 = jnp.bfloat16


def mm(a, b):
    return lax.dot_general(a, b, (((1,), (0,)), ((), ())), preferred_element_type=F32)


def mm_nt(a, b):
    return lax.dot_general(a, b, (((1,), (1,)), ((), ())), preferred_element_type=F32)


def mm_tn(a, b):
    return lax.dot_general(a, b, (((0,), (0,)), ((), ())), preferred_element_type=F32)


def bucket_of(distance):
    magnitude = jnp.abs(distance)
    far_bucket = jnp.full(magnitude.shape, 8, jnp.int32)
    for threshold in LIMITS:
        far_bucket = far_bucket + (magnitude >= threshold).astype(jnp.int32)
    return jnp.where(magnitude < 8, magnitude, far_bucket) + 16 * (distance > 0).astype(jnp.int32)


def bucket_onehot(half, bucket_count):
    lane = jnp.arange(2 * half, dtype=jnp.int32)
    distance = jnp.where(lane < half, lane, lane - 2 * half)
    return (
        bucket_of(distance)[:, None] == jnp.arange(bucket_count, dtype=jnp.int32)[None, :]
    ).astype(F32)


TILE = 128


def bias_kernel(line_ref, out_ref):
    length = out_ref.shape[2]
    line = jnp.broadcast_to(line_ref[0], (8, length))
    row = lax.broadcasted_iota(jnp.int32, (8, length), 0)
    sheet = line
    for r in range(1, 8):
        sheet = jnp.where(row == r, pltpu.roll(line, r, 1), sheet)
    while sheet.shape[0] < TILE:
        sheet = jnp.concatenate([sheet, pltpu.roll(sheet, sheet.shape[0], 1)], axis=0)
    out_ref[0] = sheet.astype(out_ref.dtype)


def position_bias(line):
    heads, length = line.shape
    return pl.pallas_call(
        bias_kernel,
        grid=(heads,),
        out_shape=jax.ShapeDtypeStruct((heads, TILE, length), BF16),
        in_specs=[pl.BlockSpec((1, 1, length), lambda h: (h, 0, 0))],
        out_specs=pl.BlockSpec((1, TILE, length), lambda h: (h, 0, 0)),
        compiler_params=pltpu.CompilerParams(vmem_limit_bytes=VMEM_LIMIT),
        name="position_bias",
    )(line.reshape(heads, 1, length))


def unit_rows(x):
    x = x.astype(F32)
    return x * lax.rsqrt(jnp.mean(x * x, axis=-1, keepdims=True) + EPSILON)


def remote(src, dst, send_sem, recv_sem, device):
    return pltpu.make_async_remote_copy(
        src_ref=src, dst_ref=dst, send_sem=send_sem, recv_sem=recv_sem,
        device_id=device, device_id_type=pl.DeviceIdType.MESH,
    )


def greet(devices):
    barrier = pltpu.get_barrier_semaphore()
    for device in devices:
        pl.semaphore_signal(
            barrier, inc=1, device_id=device, device_id_type=pl.DeviceIdType.MESH
        )
    pl.semaphore_wait(barrier, len(devices))


def bits_of(count):
    return [1 << b for b in range(count.bit_length() - 1)]


def partner_of(me, step, count):
    found = 0
    for bit in bits_of(count):
        found = found + bit * lax.rem(me // bit + step // bit, 2)
    return found


def any_space():
    return pl.BlockSpec(memory_space=pl.ANY)


def opening_kernel(
    micros, x_ref, qkv_ref, out_ref, routes_ref, table_ref, *refs,
):
    x_all, refs = refs[:micros], refs[micros:]
    (
    qkv_all, out_all, routes_all, table_all,
    x_send, x_recv, qkv_send, qkv_recv, out_send, out_recv, qkv_on_send, qkv_on_recv,
    out_on_send, out_on_recv, routes_send, routes_recv, routes_on_send, routes_on_recv,
    table_send, table_recv, own_sem,
    ) = refs
    devices, qkv_rows = qkv_all.shape[0], qkv_all.shape[1]
    blocks, out_rows = out_all.shape[0], out_all.shape[2]
    members = x_all[0].shape[0]
    me = lax.axis_index("expert")
    line = lax.axis_index("hidden")
    mine = lax.rem(line, members)
    base = line - mine
    others = [partner_of(me, s, devices) for s in range(1, devices)]
    along = [lax.rem(line + s, blocks) for s in range(1, blocks)]
    across = lax.rem(line + members, blocks)
    greet([(other, line) for other in others] + [(me, z) for z in along])
    own = [
        pltpu.make_async_copy(out_ref.at[pl.ds(me * out_rows, out_rows)], out_all.at[line, me], own_sem.at[0]),
        pltpu.make_async_copy(routes_ref, routes_all.at[me, line], own_sem.at[1]),
    ]
    for micro in range(micros):
        own.append(
            pltpu.make_async_copy(x_ref.at[micro], x_all[micro].at[mine], own_sem.at[2 + micro])
        )
    for copy in own:
        copy.start()
    first_qkv = remote(
        qkv_ref.at[pl.ds(me * qkv_rows, qkv_rows)], qkv_all.at[me], qkv_send, qkv_recv, (me, across)
    )
    first_qkv.start()
    first_out = []
    small = [remote(table_ref, table_all, table_send, table_recv, (me, across))]
    first_routes = []
    for s, z in enumerate(along):
        first_out.append(
            remote(
                out_ref.at[pl.ds(me * out_rows, out_rows)], out_all.at[line, me], out_send.at[s],
                out_recv.at[s], (me, z),
            )
        )
        first_routes.append(
            remote(
                routes_ref, routes_all.at[me, line], routes_send.at[s], routes_recv.at[s], (me, z)
            )
        )
    for copy in first_routes + first_out + small:
        copy.start()
    xs = []
    for micro in range(micros):
        for s in range(1, members):
            peer = base + lax.rem(mine + s, members)
            xs.append(
                remote(
                    x_ref.at[micro], x_all[micro].at[mine], x_send.at[micro, s],
                    x_recv.at[micro, s], (me, peer),
                )
            )
    for copy in xs:
        copy.start()
    first_qkv.wait_recv()
    second = []
    for s, other in enumerate(others):
        second.append(
            remote(
                qkv_all.at[me], qkv_all.at[me], qkv_on_send.at[s], qkv_on_recv.at[s], (other, line)
            )
        )
        second[-1].start()
    own[1].wait()
    for copy in first_routes:
        copy.wait_recv()
    for s, other in enumerate(others):
        second.append(
            remote(
                routes_all.at[me], routes_all.at[me], routes_on_send.at[s], routes_on_recv.at[s],
                (other, line),
            )
        )
        second[-1].start()
    own[0].wait()
    for copy in first_out:
        copy.wait_recv()
    for s, other in enumerate(others):
        second.append(
            remote(
                out_all.at[:, me], out_all.at[:, me], out_on_send.at[s], out_on_recv.at[s],
                (other, line),
            )
        )
        second[-1].start()
    for copy in own[2:]:
        copy.wait()
    first_qkv.wait_send()
    for copy in first_out + first_routes:
        copy.wait_send()
    for copy in small + xs + second:
        copy.wait()


def opening(x, qkv, out, routes, table, devices, blocks, members):
    micros, shard_len, width = x.shape
    dma = pltpu.SemaphoreType.DMA
    return pl.pallas_call(
        functools.partial(opening_kernel, micros),
        out_shape=(jax.ShapeDtypeStruct((members, shard_len, width), BF16),) * micros
        + (
            jax.ShapeDtypeStruct((devices, qkv.shape[0] // devices, qkv.shape[1]), BF16),
            jax.ShapeDtypeStruct((blocks, devices, out.shape[0] // devices, width), BF16),
            jax.ShapeDtypeStruct((devices, blocks) + routes.shape, jnp.int32),
            jax.ShapeDtypeStruct(table.shape, table.dtype),
        ),
        in_specs=[any_space()] * 5,
        out_specs=(any_space(),) * (4 + micros),
        scratch_shapes=[
            dma((micros, members)), dma((micros, members)), dma, dma, dma((blocks,)), dma((blocks,)),
            dma((devices,)), dma((devices,)), dma((devices,)), dma((devices,)), dma((blocks,)),
            dma((blocks,)), dma((devices,)), dma((devices,)), dma, dma, dma((2 + micros,)),
        ],
        compiler_params=pltpu.CompilerParams(collective_id=1, has_side_effects=True),
        cost_estimate=pl.CostEstimate(flops=0, bytes_accessed=60000000, transcendentals=0),
        name="opening",
    )(x, qkv, out, routes, table)


def unit_rows(x):
    x = x.astype(F32)
    return x * lax.rsqrt(jnp.mean(x * x, axis=-1, keepdims=True) + EPSILON)


def attend_kernel(
    scale, x_ref, gain_ref, own_ref, other_ref, bias_ref, seg_row_ref, seg_col_ref,
    out_ref, x_own_ref, moe_gain_ref, *refs,
):
    riding = len(refs) > 10
    if riding:
        sent_ref, arrived_ref, ride_send, ride_recv, ride_own = refs[0], refs[6], *refs[-3:]
        refs = refs[1:6] + refs[7:-3]
    qkv_ref, prob_ref, heads_ref, h1_ref, xn2_ref, xn_ref, part_ref, got_ref, send_sem, recv_sem = refs
    micros, members, shard_len, both = got_ref.shape
    cols = both // 2
    heads, length = bias_ref.shape[0], bias_ref.shape[2]
    half = members * shard_len
    size = cols // heads
    micro, group = pl.program_id(0), pl.program_id(1)
    me = lax.axis_index("expert")
    line = lax.axis_index("hidden")
    mine = lax.rem(line, members)
    part = line // members
    base = line - mine

    def swap(m, s):
        peer = lax.rem(mine + s, members)
        return remote(
            part_ref.at[m, peer], got_ref.at[m, mine], send_sem.at[m, s], recv_sem.at[m, s],
            (me, base + peer),
        )

    def ride(s):
        peer = partner_of(me, s, sent_ref.shape[0])
        return remote(
            sent_ref.at[peer], arrived_ref.at[me], ride_send.at[s], ride_recv.at[s], (peer, line)
        )

    def stay():
        return pltpu.make_async_copy(sent_ref.at[me], arrived_ref.at[me], ride_own)

    @pl.when((micro == 0) & (group == 0))
    def _():
        peers = [(me, base + lax.rem(mine + s, members)) for s in range(1, members)]
        if riding:
            devices = sent_ref.shape[0]
            peers += [(partner_of(me, s, devices), line) for s in range(1, devices)]
        greet(peers)
        if riding:
            stay().start()
            for s in range(1, devices):
                ride(s).start()

    @pl.when(group == 0)
    def _():
        xn_ref[...] = (unit_rows(x_ref[0]) * gain_ref[...]).astype(BF16)
        for t in range(3):
            qkv_ref[0, 0, t] = mm(xn_ref[...], own_ref[t]).astype(BF16)

    @pl.when(group > 0)
    def _():
        for t in range(3):
            qkv_ref[0, 0, t] = mm(xn_ref[...], other_ref[t]).astype(BF16)

    seg_row = seg_row_ref[0]
    for head in range(heads):
        inner = slice(head * size, (head + 1) * size)
        keys = qkv_ref[0, 0, 1, :, inner]
        values = qkv_ref[0, 0, 2, :, inner]
        for start in range(0, half, TILE):
            rows = slice(start, start + TILE)
            scores = mm_nt(qkv_ref[0, 0, 0, rows, inner], keys) * scale
            shift = bias_ref[head, :, : half - start]
            if start:
                shift = jnp.concatenate([bias_ref[head, :, length - start :], shift], axis=1)
            scores = scores + shift.astype(F32)
            scores = jnp.where(seg_col_ref[0, rows, :] == seg_row, scores, MASKED)
            top = jnp.max(scores, axis=-1, keepdims=True)
            weights = jnp.exp(scores - top)
            inverse = 1.0 / jnp.sum(weights, axis=-1, keepdims=True)
            prob = (weights * inverse).astype(BF16)
            prob_ref[0, 0, head, rows, :] = prob
            heads_ref[0, rows, inner] = mm(prob, values).astype(BF16)

    for g in range(2):

        @pl.when(group == g)
        def _(g=g):
            for member in range(members):
                rows = slice(member * shard_len, (member + 1) * shard_len)
                part_ref[micro, member, :, g * cols : (g + 1) * cols] = heads_ref[0, rows, :]

    @pl.when(group == 1)
    def _():
        got_ref[micro, mine] = part_ref[micro, mine]
        for s in range(1, members):
            swap(micro, s).start()

    @pl.when((micro == micros - 1) & (group == 1))
    def _():
        for m in range(micros):
            for s in range(1, members):
                swap(m, s).wait_recv()
            h1 = x_own_ref[m].astype(F32)
            for member in range(members):
                for j in range(2):
                    index = lax.rem(part + j, 2) * members + member
                    h1 = h1 + mm(got_ref[m, member, :, j * cols : (j + 1) * cols], out_ref[index])
            h1_ref[m] = h1
            xn2_ref[m] = (unit_rows(h1) * moe_gain_ref[...]).astype(BF16)
        for m in range(micros):
            for s in range(1, members):
                swap(m, s).wait_send()
        if riding:
            stay().wait()
            for s in range(1, sent_ref.shape[0]):
                ride(s).wait()


def attend(
    x, gain, own_weight, other_weight, bias, seg, out_weight, x_own, moe_gain, scale, members, identity,
    rider=None,
):
    micros, half, width = x.shape
    cols = own_weight.shape[2]
    heads = bias.shape[0] // 2
    shard_len = half // members
    riders = [] if rider is None else [rider]
    ride_sems = []
    for array in riders:
        ride_sems = [pltpu.SemaphoreType.DMA((array.shape[0],))] * 2 + [pltpu.SemaphoreType.DMA]

    def once(shape):
        return pl.BlockSpec(shape, lambda m, p: (0,) * len(shape), pipeline_mode=pl.Buffered(1))

    return pl.pallas_call(
        functools.partial(attend_kernel, scale),
        grid=(micros, 2),
        out_shape=(
            jax.ShapeDtypeStruct((micros, 2, 3, half, cols), BF16),
            jax.ShapeDtypeStruct((micros, 2, heads, half, half), BF16),
            jax.ShapeDtypeStruct((micros, half, 2 * cols), BF16),
            jax.ShapeDtypeStruct((micros, shard_len, width), F32),
            jax.ShapeDtypeStruct((micros, shard_len, width), BF16),
        )
        + tuple(jax.ShapeDtypeStruct(array.shape, array.dtype) for array in riders),
        in_specs=[
            pl.BlockSpec((1, half, width), lambda m, p: (m, 0, 0)),
            once((1, width)),
            once((3, width, cols)),
            once((3, width, cols)),
            pl.BlockSpec((heads,) + bias.shape[1:], lambda m, p: (p, 0, 0)),
            pl.BlockSpec((1, 1, half), lambda m, p: (m, 0, 0)),
            pl.BlockSpec((1, half, 1), lambda m, p: (m, 0, 0)),
            once(out_weight.shape),
            once(x_own.shape),
            once((1, width)),
        ]
        + [any_space()] * len(riders),
        out_specs=(
            pl.BlockSpec((1, 1, 3, half, cols), lambda m, p: (m, p, 0, 0, 0)),
            pl.BlockSpec((1, 1, heads, half, half), lambda m, p: (m, p, 0, 0, 0)),
            pl.BlockSpec((1, half, cols), lambda m, p: (m, 0, p)),
            pl.BlockSpec((micros, shard_len, width), lambda m, p: (0, 0, 0)),
            pl.BlockSpec((micros, shard_len, width), lambda m, p: (0, 0, 0)),
        )
        + (any_space(),) * len(riders),
        scratch_shapes=[
            pltpu.VMEM((half, width), BF16),
            pltpu.VMEM((micros, members, shard_len, 2 * cols), BF16),
            pltpu.VMEM((micros, members, shard_len, 2 * cols), BF16),
            pltpu.SemaphoreType.DMA((micros, members)),
            pltpu.SemaphoreType.DMA((micros, members)),
        ]
        + ride_sems,
        compiler_params=pltpu.CompilerParams(
            vmem_limit_bytes=VMEM_LIMIT, collective_id=identity, has_side_effects=True
        ),
        cost_estimate=pl.CostEstimate(
            flops=micros * 2 * half * cols * (8 * width + 4 * half),
            bytes_accessed=40000000,
            transcendentals=micros * 2 * heads * half * half,
        ),
        name="attend",
    )(
        x, gain, own_weight, other_weight, bias, seg.reshape(micros, 1, half),
        seg.reshape(micros, half, 1), out_weight, x_own, moe_gain, *riders,
    )


def back_kernel(
    scale, added, grad_ref, h1_ref, dy_ref, x_own_ref, moe_gain_ref, gain_ref, out_ref, x_ref,
    own_ref, other_ref, qkv_ref, prob_ref, heads_ref, *refs,
):
    if added:
        prev_ref, refs = refs[0], refs[1:]
    (
        xgrad_ref, grads_ref, line_ref, dmoe_ref, dgain_ref,
        dh1_ref, dattn_all, dheads_part, dheads_all, dxn_part, dxn_got, total_ref, xn_ref, ds_ref,
        dproj_ref, sheet_ref, attn_send, attn_recv, heads_send, heads_recv, dxn_send, dxn_recv,
    ) = refs
    members, shard_len, width = dattn_all.shape
    heads, half = prob_ref.shape[1], prob_ref.shape[2]
    cols = dproj_ref.shape[2]
    size = cols // heads
    length = sheet_ref.shape[1]
    group = pl.program_id(0)
    me = lax.axis_index("expert")
    line = lax.axis_index("hidden")
    mine = lax.rem(line, members)
    part = line // members
    base = line - mine
    steps = range(1, members)

    def peer_of(s):
        return lax.rem(mine + s, members)

    def attn_copy(s):
        return remote(
            dattn_all.at[mine], dattn_all.at[mine], attn_send.at[s], attn_recv.at[s],
            (me, base + peer_of(s)),
        )

    def heads_copy(s):
        return remote(
            dheads_part.at[peer_of(s)], dheads_all.at[mine], heads_send.at[s], heads_recv.at[s],
            (me, base + peer_of(s)),
        )

    def dxn_copy(s):
        return remote(
            dxn_part.at[peer_of(s)], dxn_got.at[mine], dxn_send.at[s], dxn_recv.at[s],
            (me, base + peer_of(s)),
        )

    @pl.when(group == 0)
    def _():
        greet([(me, base + peer_of(s)) for s in steps])
        grad = grad_ref[...].astype(F32)
        h1 = h1_ref[...]
        r2 = lax.rsqrt(jnp.mean(h1 * h1, axis=-1, keepdims=True) + EPSILON)
        unit = h1 * r2
        dmoe_ref[...] = jnp.sum(grad * unit, axis=0, keepdims=True)
        weighted = grad * moe_gain_ref[...]
        inner = jnp.mean(weighted * unit, axis=-1, keepdims=True)
        dh1 = dy_ref[...].astype(F32) + r2 * (weighted - unit * inner)
        dh1_ref[...] = dh1
        dattn = dh1.astype(BF16)
        dattn_all[mine] = dattn
        for member in range(members):
            for j in range(2):
                index = lax.rem(part + j, 2) * members + member
                dheads = mm_nt(dattn, out_ref[index]).astype(BF16)
                dheads_part[member, :, j * cols : (j + 1) * cols] = dheads
        for s in steps:
            heads_copy(s).start()
        for s in steps:
            attn_copy(s).start()
        dheads_all[mine] = dheads_part[mine]
        xn_ref[...] = (unit_rows(x_ref[...]) * gain_ref[...]).astype(BF16)
        for s in steps:
            heads_copy(s).wait_recv()

    for g in range(2):

        @pl.when(group == g)
        def _(g=g):
            for head in range(heads):
                inner_cols = slice(head * size, (head + 1) * size)
                outer_cols = slice(g * cols + head * size, g * cols + (head + 1) * size)
                values = qkv_ref[0, 2, :, inner_cols]
                grads = dheads_all[:, :, outer_cols].reshape(half, size)
                sheet_ref[...] = jnp.zeros_like(sheet_ref)
                for start in range(0, half, TILE):
                    rows = slice(start, start + TILE)
                    prob = prob_ref[0, head, rows, :].astype(F32)
                    dprob = mm_nt(grads[rows], values)
                    inner = jnp.sum(prob * dprob, axis=-1, keepdims=True)
                    dscore = (prob * (dprob - inner)).astype(BF16)
                    ds_ref[rows, :] = dscore
                    dscore = dscore.astype(F32)
                    sheet_ref[:, : half - start] += dscore[:, start:]
                    if start:
                        sheet_ref[:, length - start :] += dscore[:, :start]
                dscores = ds_ref[...]
                keys, queries = qkv_ref[0, 1, :, inner_cols], qkv_ref[0, 0, :, inner_cols]
                dproj_ref[0, :, inner_cols] = (mm(dscores, keys) * scale).astype(BF16)
                dproj_ref[1, :, inner_cols] = (mm_tn(dscores, queries) * scale).astype(BF16)
                dproj_ref[2, :, inner_cols] = mm_tn(prob_ref[0, head], grads).astype(BF16)
                sheet = sheet_ref[...]
                while sheet.shape[0] > 8:
                    upper = sheet.shape[0] // 2
                    sheet = sheet[:upper] + pltpu.roll(sheet[upper:], length - upper, 1)
                row = lax.broadcasted_iota(jnp.int32, (8, length), 0)
                found = jnp.zeros((1, length), F32)
                for r in range(8):
                    moved = pltpu.roll(sheet, length - r, 1) if r else sheet
                    found = found + jnp.sum(
                        jnp.where(row == r, moved, 0.0), axis=0, keepdims=True
                    )
                line_ref[0, head : head + 1, :] = found

    def products(weight_ref):
        dxn = mm_nt(dproj_ref[0], weight_ref[0])
        for t in range(1, 3):
            dxn = dxn + mm_nt(dproj_ref[t], weight_ref[t])
        return dxn.reshape(members, shard_len, width)

    @pl.when(group == 0)
    def _():
        total_ref[...] = products(own_ref)
        for s in steps:
            attn_copy(s).wait_recv()

    @pl.when(group == 1)
    def _():
        total_ref[...] += products(other_ref)
        dxn_part[...] = total_ref[...].astype(BF16)
        for s in steps:
            dxn_copy(s).start()

    per = grads_ref.shape[0] // 4
    for t in range(4):
        if t < 3:
            found = mm_tn(xn_ref[...], dproj_ref[t])
        else:
            found = mm_tn(dattn_all[...].reshape(half, width), heads_ref[...])
        found = found.reshape(per, 1, width // per, cols)
        if added:
            found = found + prev_ref[t * per : (t + 1) * per].astype(F32)
        grads_ref[t * per : (t + 1) * per] = found.astype(BF16)

    @pl.when(group == 1)
    def _():
        total = total_ref[...].reshape(half, width)
        dgain_ref[...] = jnp.sum(total * unit_rows(x_ref[...]), axis=0, keepdims=True)
        x_own = x_own_ref[...].astype(F32)
        r1 = lax.rsqrt(jnp.mean(x_own * x_own, axis=-1, keepdims=True) + EPSILON)
        unit = x_own * r1
        for s in steps:
            dxn_copy(s).wait_recv()
        dxn1 = total_ref[mine]
        for s in steps:
            dxn1 = dxn1 + dxn_got[lax.rem(mine + members - s, members)].astype(F32)
        weighted = dxn1 * gain_ref[...]
        inner = jnp.mean(weighted * unit, axis=-1, keepdims=True)
        xgrad_ref[...] = (dh1_ref[...] + r1 * (weighted - unit * inner)).astype(BF16)
        for s in steps:
            heads_copy(s).wait_send()
            attn_copy(s).wait_send()
            dxn_copy(s).wait_send()


def attend_back(
    grad, h1, dy, x_own, moe_gain, gain, out_weight, x_half, own_weight, other_weight, qkv, prob,
    heads_out, prev, scale, pieces, members, identity,
):
    _, heads, half = prob.shape[:3]
    width, cols = own_weight.shape[1:]
    shard_len = half // members
    length = 2 * half
    rows = 4 * width // pieces

    def once(shape):
        return pl.BlockSpec(shape, lambda p: (0,) * len(shape), pipeline_mode=pl.Buffered(1))

    pieces_spec = pl.BlockSpec((pieces, 1, rows, cols), lambda p: (0, p, 0, 0))
    operands = [
        grad, h1, dy, x_own, moe_gain, gain, out_weight, x_half, own_weight, other_weight, qkv,
        prob, heads_out,
    ]
    in_specs = [once(array.shape) for array in operands[:10]] + [
        pl.BlockSpec((1, 3, half, cols), lambda p: (p, 0, 0, 0)),
        pl.BlockSpec((1, heads, half, half), lambda p: (p, 0, 0, 0)),
        pl.BlockSpec((half, cols), lambda p: (0, p)),
    ]
    if prev is not None:
        operands.append(prev)
        in_specs.append(pieces_spec)
    dma = pltpu.SemaphoreType.DMA
    return pl.pallas_call(
        functools.partial(back_kernel, scale, prev is not None),
        grid=(2,),
        out_shape=(
            jax.ShapeDtypeStruct((shard_len, width), BF16),
            jax.ShapeDtypeStruct((pieces, 2, rows, cols), BF16),
            jax.ShapeDtypeStruct((2, heads, length), F32),
            jax.ShapeDtypeStruct((1, width), F32),
            jax.ShapeDtypeStruct((1, width), F32),
        ),
        in_specs=in_specs,
        out_specs=(
            pl.BlockSpec((shard_len, width), lambda p: (0, 0)),
            pieces_spec,
            pl.BlockSpec((1, heads, length), lambda p: (p, 0, 0)),
            pl.BlockSpec((1, width), lambda p: (0, 0)),
            pl.BlockSpec((1, width), lambda p: (0, 0)),
        ),
        scratch_shapes=[
            pltpu.VMEM((shard_len, width), F32),
            pltpu.VMEM((members, shard_len, width), BF16),
            pltpu.VMEM((members, shard_len, 2 * cols), BF16),
            pltpu.VMEM((members, shard_len, 2 * cols), BF16),
            pltpu.VMEM((members, shard_len, width), BF16),
            pltpu.VMEM((members, shard_len, width), BF16),
            pltpu.VMEM((members, shard_len, width), F32),
            pltpu.VMEM((half, width), BF16),
            pltpu.VMEM((half, half), BF16),
            pltpu.VMEM((3, half, cols), BF16),
            pltpu.VMEM((TILE, length), F32),
            dma((members,)), dma((members,)), dma((members,)), dma((members,)), dma((members,)),
            dma((members,)),
        ],
        compiler_params=pltpu.CompilerParams(
            vmem_limit_bytes=VMEM_LIMIT, collective_id=identity, has_side_effects=True
        ),
        cost_estimate=pl.CostEstimate(
            flops=2 * half * cols * (16 * width + 8 * half),
            bytes_accessed=40000000,
            transcendentals=0,
        ),
        name="attend_back",
    )(*operands)


def closing_kernel(
    pieces_ref, small_ref, whole_ref, sum_ref,
    total_ref, moved_ref, moved_got, piece_ref, small_got, line_sum, line_got,
    small_send, small_recv, line_send, line_recv, moved_send, moved_recv, on_send, on_recv, own_sem,
):
    devices = pieces_ref.shape[0]
    blocks = line_got.shape[0]
    me = lax.axis_index("expert")
    line = lax.axis_index("hidden")
    others = [partner_of(me, s, devices) for s in range(1, devices)]
    along = [lax.rem(line + s, blocks) for s in range(1, blocks)]
    across = lax.rem(line + blocks // 2, blocks)
    greet([(other, line) for other in others] + [(me, z) for z in along])
    smalls = [
        remote(small_ref, small_got.at[me], small_send.at[s], small_recv.at[s], (other, line))
        for s, other in enumerate(others)
    ]
    for copy in smalls:
        copy.start()
    small_got[me] = small_ref[...]
    moved = jnp.sum(pieces_ref[:, 1].astype(F32), axis=0)
    moved_ref[...] = moved.astype(BF16)
    cross = remote(moved_ref, moved_got, moved_send, moved_recv, (me, across))
    cross.start()
    total_ref[...] = jnp.sum(pieces_ref[:, 0].astype(F32), axis=0)
    cross.wait_recv()
    piece_ref[...] = (total_ref[...] + moved_got[...].astype(F32)).astype(BF16)
    onward = [
        remote(piece_ref, whole_ref.at[me], on_send.at[s], on_recv.at[s], (other, line))
        for s, other in enumerate(others)
    ]
    for copy in onward:
        copy.start()
    own = pltpu.make_async_copy(piece_ref, whole_ref.at[me], own_sem)
    own.start()
    for copy in smalls:
        copy.wait_recv()
    line_sum[...] = jnp.sum(small_got[...], axis=0)
    lines = [
        remote(line_sum, line_got.at[line], line_send.at[s], line_recv.at[s], (me, z))
        for s, z in enumerate(along)
    ]
    for copy in lines:
        copy.start()
    line_got[line] = line_sum[...]
    for copy in lines:
        copy.wait_recv()
    sum_ref[...] = jnp.sum(line_got[...], axis=0)
    own.wait()
    cross.wait_send()
    for copy in smalls + lines:
        copy.wait_send()
    for copy in onward:
        copy.wait()


def closing(pieces, small, blocks):
    devices, _, rows, cols = pieces.shape
    vmem = pl.BlockSpec(memory_space=pltpu.VMEM)
    dma = pltpu.SemaphoreType.DMA
    return pl.pallas_call(
        closing_kernel,
        out_shape=(
            jax.ShapeDtypeStruct((devices, rows, cols), BF16),
            jax.ShapeDtypeStruct(small.shape, F32),
        ),
        in_specs=[vmem, vmem],
        out_specs=(any_space(), vmem),
        scratch_shapes=[
            pltpu.VMEM((rows, cols), F32),
            pltpu.VMEM((rows, cols), BF16),
            pltpu.VMEM((rows, cols), BF16),
            pltpu.VMEM((rows, cols), BF16),
            pltpu.VMEM((devices,) + small.shape, F32),
            pltpu.VMEM(small.shape, F32),
            pltpu.VMEM((blocks,) + small.shape, F32),
            dma((devices,)), dma((devices,)), dma((blocks,)), dma((blocks,)), dma, dma,
            dma((devices,)), dma((devices,)), dma,
        ],
        compiler_params=pltpu.CompilerParams(
            vmem_limit_bytes=VMEM_LIMIT, collective_id=3, has_side_effects=True
        ),
        cost_estimate=pl.CostEstimate(flops=0, bytes_accessed=60000000, transcendentals=0),
        name="closing",
    )(pieces, small)


def spread(rows, place0, place1, count):
    ids = lax.broadcasted_iota(jnp.int32, (count, rows.shape[0]), 0)
    hit = (ids == place0) | (ids == place1)
    return mm(jnp.where(hit, 1.0, 0.0).astype(BF16), rows)


def spread_kernel(rows_ref, place_ref, out_ref):
    experts, _, cap, width = out_ref.shape
    placed = spread(rows_ref[...], place_ref[0:1, :], place_ref[1:2, :], experts * cap)
    out_ref[...] = placed.astype(BF16).reshape(experts, 1, cap, width)


def spread_rows(rows, place, experts, cap, shard_len):
    slots, width = rows.shape
    blocks = slots // shard_len
    return pl.pallas_call(
        spread_kernel,
        grid=(blocks,),
        out_shape=jax.ShapeDtypeStruct((experts, blocks, cap, width), BF16),
        in_specs=[
            pl.BlockSpec((shard_len, width), lambda b: (b, 0)),
            pl.BlockSpec((2, shard_len), lambda b: (0, b)),
        ],
        out_specs=pl.BlockSpec((experts, 1, cap, width), lambda b: (0, b, 0, 0)),
        compiler_params=pltpu.CompilerParams(vmem_limit_bytes=VMEM_LIMIT),
        cost_estimate=pl.CostEstimate(
            flops=2 * experts * cap * slots * width,
            bytes_accessed=2 * slots * width + 2 * experts * blocks * cap * width,
            transcendentals=0,
        ),
        name="spread_rows",
    )(rows, place)


def collect_kernel(rows_ref, place_ref, out_ref):
    experts, _, cap, width = rows_ref.shape
    tokens = out_ref.shape[0]
    ids = lax.broadcasted_iota(jnp.int32, (experts * cap, tokens), 0)
    hit = (ids == place_ref[0:1, :]) | (ids == place_ref[1:2, :])
    rows = rows_ref[...].reshape(experts * cap, width)
    out_ref[...] = mm_tn(jnp.where(hit, 1.0, 0.0).astype(BF16), rows).astype(BF16)


def collect_rows(rows, place, shard_len):
    experts, blocks, cap, width = rows.shape
    slots = blocks * shard_len
    return pl.pallas_call(
        collect_kernel,
        grid=(blocks,),
        out_shape=jax.ShapeDtypeStruct((slots, width), BF16),
        in_specs=[
            pl.BlockSpec((experts, 1, cap, width), lambda b: (0, b, 0, 0)),
            pl.BlockSpec((2, shard_len), lambda b: (0, b)),
        ],
        out_specs=pl.BlockSpec((shard_len, width), lambda b: (b, 0)),
        compiler_params=pltpu.CompilerParams(vmem_limit_bytes=VMEM_LIMIT),
        cost_estimate=pl.CostEstimate(
            flops=2 * experts * cap * slots * width,
            bytes_accessed=2 * slots * width + 2 * experts * blocks * cap * width,
            transcendentals=0,
        ),
        name="collect_rows",
    )(rows, place)


def places(route_ref, index, cap, experts):
    shard_len = route_ref.shape[-1]
    row = lax.broadcasted_iota(jnp.int32, (shard_len, shard_len), 0)
    col = lax.broadcasted_iota(jnp.int32, (shard_len, shard_len), 1)
    earlier = jnp.where(row < col, 1.0, 0.0).astype(BF16)
    ids = lax.broadcasted_iota(jnp.int32, (experts, shard_len), 0)
    pair = [route_ref[index + (slice(k, k + 1),)] for k in range(2)]
    chosen = (ids == pair[0]) | (ids == pair[1])
    before = mm(jnp.where(chosen, 1.0, 0.0).astype(BF16), earlier)
    found = []
    for route in pair:
        position = jnp.sum(jnp.where(ids == route, before, 0.0), axis=0, keepdims=True)
        found.append(jnp.where(route >= 0, route * cap + position.astype(jnp.int32), -1))
    return pair, found


def place_kernel(cap, experts, route_ref, place_ref):
    blocks, micros, _, shard_len = route_ref.shape
    for block in range(blocks):
        for micro in range(micros):
            _, found = places(route_ref, (block, micro), cap, experts)
            for k in range(2):
                lanes = slice(block * shard_len, (block + 1) * shard_len)
                place_ref[micro, k : k + 1, lanes] = found[k]


def find_places(route, experts, cap):
    blocks, micros, _, shard_len = route.shape
    vmem = pl.BlockSpec(memory_space=pltpu.VMEM)
    return pl.pallas_call(
        functools.partial(place_kernel, cap, experts),
        out_shape=jax.ShapeDtypeStruct((micros, 2, blocks * shard_len), jnp.int32),
        in_specs=[vmem],
        out_specs=vmem,
        compiler_params=pltpu.CompilerParams(vmem_limit_bytes=VMEM_LIMIT),
        name="find_places",
    )(route)


def pair_kernel(route_ref, pair_ref):
    _, _, here, blocks, cap, experts = pair_ref.shape
    shard_len = route_ref.shape[-1]
    me = lax.axis_index("expert")
    spots = lax.broadcasted_iota(jnp.int32, (cap, shard_len), 0)
    ids = lax.broadcasted_iota(jnp.int32, (cap, experts), 1)
    for block in range(blocks):
        pair, place = places(route_ref, (0, block, 0), cap, experts)
        for e in range(here):
            expert = me * here + e
            other = jnp.full((cap, 1), -1, jnp.int32)
            for k in range(2):
                hit = spots + expert * cap == place[k]
                found = jnp.max(jnp.where(hit, pair[1 - k], -1), axis=1, keepdims=True)
                other = jnp.maximum(other, found)
            sign = jnp.where(ids == expert, 1.0, 0.0) - jnp.where(ids == other, 1.0, 0.0)
            pair_ref[0, 0, e, block] = jnp.where(other >= 0, sign, 0.0).astype(BF16)


def find_pairs(route, experts, here, cap):
    devices, blocks, micros, _, shard_len = route.shape
    return pl.pallas_call(
        pair_kernel,
        grid=(micros, devices),
        out_shape=jax.ShapeDtypeStruct((micros, devices, here, blocks, cap, experts), BF16),
        in_specs=[pl.BlockSpec((1, blocks, 1, 2, shard_len), lambda m, s: (s, 0, m, 0, 0))],
        out_specs=pl.BlockSpec((1, 1, here, blocks, cap, experts), lambda m, s: (m, s, 0, 0, 0, 0)),
        compiler_params=pltpu.CompilerParams(vmem_limit_bytes=VMEM_LIMIT),
        name="find_pairs",
    )(route)


def expert_kernel(
    sent_ref, dy_ref, pair_ref, wr_ref, wg_ref, wu_ref, wd_ref,
    back_ref, y_ref, x_ref, g_ref, hid_ref, dga_ref, dup_ref, dlog_ref,
    got_ref, dx_ref, stage_ref, x_send, x_recv, dx_send, dx_recv, own_sem, stage_sem,
):
    devices, experts, cap, width = sent_ref.shape
    step = pl.program_id(0)
    me = lax.axis_index("expert")
    line = lax.axis_index("hidden")
    first_wave = bits_of(devices)
    rest = [s for s in range(1, devices) if s not in first_wave]
    later_waves = [rest[i : i + 2] for i in range(0, len(rest), 2)]

    def x_copy(s):
        peer = partner_of(me, s, devices)
        return pltpu.make_async_remote_copy(
            src_ref=sent_ref.at[peer], dst_ref=got_ref.at[s], send_sem=x_send.at[s],
            recv_sem=x_recv.at[s], device_id=(peer, line), device_id_type=pl.DeviceIdType.MESH,
        )

    def dx_copy(s):
        peer = partner_of(me, s, devices)
        return pltpu.make_async_remote_copy(
            src_ref=dx_ref.at[s], dst_ref=back_ref.at[me], send_sem=dx_send.at[s],
            recv_sem=dx_recv.at[s], device_id=(peer, line), device_id_type=pl.DeviceIdType.MESH,
        )

    def y_copy(s):
        source = partner_of(me, s, devices)
        slot = lax.rem(s, 2)
        return pltpu.make_async_copy(stage_ref.at[slot], y_ref.at[source], stage_sem.at[slot])

    def work(s):
        source = partner_of(me, s, devices)
        slot = lax.rem(s, 2)
        for e in range(experts):
            x = got_ref[s, e]
            dy = dy_ref[source, e].astype(F32)
            pair = pair_ref[source, e].astype(F32)
            margin = jnp.sum(mm_nt(x, wr_ref[...]) * pair, axis=-1, keepdims=True)
            own_gate = 1.0 / (1.0 + jnp.exp(-margin))
            other_gate = 1.0 / (1.0 + jnp.exp(margin))
            g = (own_gate * dy).astype(BF16)
            x_ref[0, e] = x
            g_ref[0, e] = g
            gate = mm_nt(x, wg_ref[e])
            up = mm_nt(x, wu_ref[e])
            square = gate * gate
            bent = jnp.tanh(GELU_C * gate * (1.0 + GELU_A * square))
            half_gate = 0.5 * gate
            gelu = half_gate * (1.0 + bent)
            slope = 0.5 * (1.0 + bent) + half_gate * (1.0 - bent * bent) * (
                GELU_C * (1.0 + 3.0 * GELU_A * square)
            )
            hid = (gelu * up).astype(BF16)
            dhid = mm_nt(g, wd_ref[e])
            dga = (dhid * (up * slope)).astype(BF16)
            dup = (dhid * gelu).astype(BF16)
            hid_ref[0, e] = hid
            dga_ref[0, e] = dga
            dup_ref[0, e] = dup
            y = mm(hid, wd_ref[e])
            dgate = jnp.sum(y * dy, axis=-1, keepdims=True)
            stage_ref[slot, e] = (y * own_gate).astype(BF16)
            dlog = (dgate * own_gate * other_gate * pair).astype(BF16)
            dlog_ref[0, e] = dlog
            dx = mm(dga, wg_ref[e]) + mm(dup, wu_ref[e]) + mm(dlog, wr_ref[...])
            dx_ref[s, e] = dx.astype(BF16)

    @pl.when(step == 0)
    def _():
        barrier = pltpu.get_barrier_semaphore()
        for s in range(1, devices):
            pl.semaphore_signal(
                barrier, inc=1, device_id=(partner_of(me, s, devices), line),
                device_id_type=pl.DeviceIdType.MESH,
            )
        pl.semaphore_wait(barrier, devices - 1)
        for s in first_wave:
            x_copy(s).start()
        own = pltpu.make_async_copy(sent_ref.at[me], got_ref.at[0], own_sem)
        own.start()
        own.wait()

    @pl.when(step > 0)
    def _():
        x_copy(step).wait_recv()

    for index, wave in enumerate(later_waves):

        @pl.when(step == 2 + index)
        def _(wave=wave):
            for s in wave:
                x_copy(s).start()

    @pl.when(step > 1)
    def _():
        y_copy(step - 2).wait()

    work(step)
    y_copy(step).start()

    @pl.when(step > 0)
    def _():
        dx_copy(step).start()

    @pl.when(step == devices - 1)
    def _():
        own = pltpu.make_async_copy(dx_ref.at[0], back_ref.at[me], own_sem)
        own.start()
        own.wait()
        y_copy(devices - 2).wait()
        y_copy(devices - 1).wait()
        for s in range(1, devices):
            x_copy(s).wait_send()
            dx_copy(s).wait_send()
            dx_copy(s).wait_recv()


def expert_pass(sent, dy, pair, wr, wg, wu, wd, identity):
    devices, experts, cap, width = sent.shape
    hidden = wg.shape[1]
    choices = wr.shape[0]

    def whole(shape):
        return pl.BlockSpec(shape, lambda s: (0,) * len(shape), pipeline_mode=pl.Buffered(1))

    def block(cols):
        return pl.BlockSpec((1, experts, cap, cols), lambda s: (s, 0, 0, 0))

    def kept(cols):
        return jax.ShapeDtypeStruct((devices, experts, cap, cols), BF16)

    return pl.pallas_call(
        expert_kernel,
        grid=(devices,),
        out_shape=(
            kept(width), kept(width), kept(width), kept(width), kept(hidden), kept(hidden),
            kept(hidden), kept(choices),
        ),
        in_specs=[
            any_space(), whole(dy.shape), whole(pair.shape), whole(wr.shape), whole(wg.shape),
            whole(wu.shape), whole(wd.shape),
        ],
        out_specs=(
            any_space(), any_space(), block(width), block(width), block(hidden), block(hidden),
            block(hidden), block(choices),
        ),
        scratch_shapes=[
            pltpu.VMEM((devices, experts, cap, width), BF16),
            pltpu.VMEM((devices, experts, cap, width), BF16),
            pltpu.VMEM((2, experts, cap, width), BF16),
            pltpu.SemaphoreType.DMA((devices,)),
            pltpu.SemaphoreType.DMA((devices,)),
            pltpu.SemaphoreType.DMA((devices,)),
            pltpu.SemaphoreType.DMA((devices,)),
            pltpu.SemaphoreType.DMA,
            pltpu.SemaphoreType.DMA((2,)),
        ],
        compiler_params=pltpu.CompilerParams(
            vmem_limit_bytes=VMEM_LIMIT, collective_id=identity, has_side_effects=True
        ),
        cost_estimate=pl.CostEstimate(flops=0, bytes_accessed=4000000, transcendentals=0),
        name="expert_pass",
    )(sent, dy, pair, wr, wg, wu, wd)


def weight_kernel(*refs):
    count = (len(refs) - 4) // 6
    dwr_ref, dwg_ref, dwu_ref, dwd_ref = refs[-4:]
    totals = [0.0, 0.0, 0.0, 0.0]
    for index in range(count):
        blocks = [
            ref[...].reshape(ref.shape[0] * ref.shape[2], ref.shape[3])
            for ref in refs[6 * index : 6 * index + 6]
        ]
        x, g, hid, dga, dup, dlog = blocks
        totals[0] = totals[0] + mm_tn(dlog, x)
        totals[1] = totals[1] + mm_tn(dga, x)
        totals[2] = totals[2] + mm_tn(dup, x)
        totals[3] = totals[3] + mm_tn(hid, g)
    dwr_ref[0] = totals[0]
    dwg_ref[0] = totals[1]
    dwu_ref[0] = totals[2]
    dwd_ref[0] = totals[3]


def weight_pass(kept):
    sources, experts, cap, width = kept[0][0].shape
    hidden = kept[0][2].shape[3]
    choices = kept[0][5].shape[3]
    rows = sources * cap
    block = 256 if width % 256 == 0 else width
    tokens = pl.BlockSpec((sources, 1, cap, block), lambda e, j: (0, e, 0, j))
    acts = pl.BlockSpec((sources, 1, cap, hidden), lambda e, j: (0, e, 0, 0))
    logs = pl.BlockSpec((sources, 1, cap, choices), lambda e, j: (0, e, 0, 0))
    operands = []
    for arrays in kept:
        operands.extend(arrays)
    return pl.pallas_call(
        weight_kernel,
        grid=(experts, width // block),
        out_shape=(
            jax.ShapeDtypeStruct((experts, choices, width), F32),
            jax.ShapeDtypeStruct((experts, hidden, width), F32),
            jax.ShapeDtypeStruct((experts, hidden, width), F32),
            jax.ShapeDtypeStruct((experts, hidden, width), F32),
        ),
        in_specs=[tokens, tokens, acts, acts, acts, logs] * len(kept),
        out_specs=(
            pl.BlockSpec((1, choices, block), lambda e, j: (e, 0, j)),
            pl.BlockSpec((1, hidden, block), lambda e, j: (e, 0, j)),
            pl.BlockSpec((1, hidden, block), lambda e, j: (e, 0, j)),
            pl.BlockSpec((1, hidden, block), lambda e, j: (e, 0, j)),
        ),
        compiler_params=pltpu.CompilerParams(vmem_limit_bytes=VMEM_LIMIT),
        cost_estimate=pl.CostEstimate(
            flops=6 * len(kept) * experts * rows * width * hidden,
            bytes_accessed=len(kept) * experts * rows * (4 * width + 6 * hidden)
            + 12 * experts * width * hidden,
            transcendentals=0,
        ),
        name="weight_pass",
    )(*operands)


def after(values, *others):
    return lax.optimization_barrier((values,) + others)[0]


def shards(
    x_in,
    cotangent,
    segment_ids,
    routes,
    qkv_weight,
    out_weight,
    bias_table,
    attn_gain,
    moe_gain,
    router_weight,
    gate_weight,
    up_weight,
    down_weight,
):
    micro_count, _, shard_len, width = x_in.shape
    slot_count = segment_ids.shape[2]
    head_cols = out_weight.shape[0]
    bucket_count, heads_here = bias_table.shape
    head_size = head_cols // heads_here
    expert_count = router_weight.shape[1]
    experts_here = gate_weight.shape[0]
    devices = expert_count // experts_here
    blocks = slot_count // shard_len
    members = blocks // 2
    half = slot_count // 2
    capacity = max(2, (10 * shard_len + 4 * expert_count - 1) // (4 * expert_count))
    scale = head_size ** (-0.5)
    hidden_index = lax.axis_index("hidden")
    expert_index = lax.axis_index("expert")
    part = hidden_index // members
    attn_gain_f = attn_gain.astype(F32).reshape(1, width)
    moe_gain_f = moe_gain.astype(F32).reshape(1, width)
    token_shape = (devices, experts_here, blocks * capacity, width)
    flat_shape = (devices, experts_here * blocks * capacity, width)
    place_shape = (expert_count, blocks, capacity, width)
    gate_rows = gate_weight.transpose(0, 2, 1)
    up_rows = up_weight.transpose(0, 2, 1)
    router_rows = router_weight.T

    def exchange(buffer):
        return lax.all_to_all(buffer, "expert", split_axis=0, concat_axis=0, tiled=True)

    def gather(values):
        return lax.all_gather(values, "hidden", axis=0, tiled=True)

    def scatter(values):
        return lax.psum_scatter(values, "hidden", scatter_dimension=0, tiled=True)

    states = [dict() for _ in range(micro_count)]
    own_seg = lax.dynamic_slice_in_dim(segment_ids[:, 0], hidden_index * shard_len, shard_len, 1)
    live_routes = jnp.where(own_seg[:, None, :] >= 0, routes[:, 0].transpose(0, 2, 1), -1)
    *x_all, other_qkv, all_out, all_routes, other_table = opening(
        x_in[:, 0], qkv_weight.reshape(3 * width, head_cols), out_weight,
        live_routes, bias_table.T.astype(F32), devices, blocks, members,
    )
    x_half = [x.reshape(1, half, width) for x in x_all]
    other_qkv = other_qkv.reshape(qkv_weight.shape)
    all_out = all_out.reshape(blocks, head_cols, width)

    own_routes = lax.dynamic_index_in_dim(all_routes, expert_index, 0, keepdims=False)
    place = find_places(own_routes, expert_count, capacity)

    tables = jnp.concatenate([bias_table.T.astype(F32), other_table], axis=0)
    onehot_bucket = bucket_onehot(half, bucket_count)
    bias = position_bias(jnp.einsum("jb,hb->hj", onehot_bucket, tables, precision=PRECISE))
    seg_half = lax.dynamic_slice_in_dim(segment_ids[:, 0], part * half, half, 1)

    def spread(rows, micro):
        return spread_rows(rows, place[micro], expert_count, capacity, shard_len)

    def experts(micro, kept, *behind):
        sent = spread(kept["xn2_all"], micro).reshape(token_shape)
        back, y, x, g, hid, dga, dup, dlog = expert_pass(
            after(sent, *behind), kept["dy"], pairs[micro], router_rows, gate_rows, up_rows,
            down_weight, 4 + micro,
        )
        kept["weights"] = (x, g, hid, dga, dup, dlog)
        kept["y_sent"] = y.reshape(flat_shape)
        kept["dx_back"] = back.reshape(place_shape)
        kept["dx_part"] = collect_rows(kept["dx_back"], place[micro], shard_len)
        kept["dxn2"] = scatter(kept["dx_part"])

    states[0]["dy_all"] = gather(cotangent[0, 0])
    for micro in range(1, micro_count):
        before = states[micro - 1]["dy_all"]
        states[micro]["dy_all"] = gather(after(cotangent[micro, 0], before, all_out))
    behind = ()
    for micro in range(micro_count):
        state = states[micro]
        rider = spread(after(state["dy_all"], *behind), micro).reshape(token_shape)
        qkv, prob, heads, h1, xn2, state["dy"] = attend(
            after(x_half[micro], *behind), attn_gain_f, qkv_weight, other_qkv, bias,
            seg_half[micro : micro + 1], all_out, x_in[micro], moe_gain_f, scale, members, 10 + micro,
            rider,
        )
        state.update(qkv=qkv[0], prob=prob[0], heads=heads[0], h1=h1[0], xn2=xn2[0])
        behind = (xn2,)
    pairs = find_pairs(after(all_routes, states[0]["xn2"]), expert_count, experts_here, capacity)
    pairs = pairs.reshape(micro_count, devices, experts_here, blocks * capacity, expert_count)
    behind = ()
    for micro in range(micro_count):
        states[micro]["xn2_all"] = gather(after(states[micro]["xn2"], *behind))
        behind = (states[micro]["xn2_all"],)
    behind = ()
    for micro in range(micro_count):
        experts(micro, states[micro], *behind)
        behind = (states[micro]["dx_part"],)
    last_part = states[-1]["dx_part"]
    kept = [state["weights"] for state in states]
    kept[-1] = tuple(after(list(kept[-1]), last_part))
    dwr, dwg, dwu, dwd = weight_pass(kept)
    behind = (last_part,)
    grads = None
    for micro in range(micro_count):
        state = states[micro]
        state["y_back"] = exchange(after(state["y_sent"], *behind)).reshape(place_shape)
        behind = (dwr,)
    for micro in range(micro_count):
        state = states[micro]
        state["x_grad"], grads, state["line"], state["moe_gain_grad"], state["attn_gain_grad"] = (
            attend_back(
                after(state["dxn2"], dwr), state["h1"], cotangent[micro, 0], x_in[micro, 0],
                moe_gain_f, attn_gain_f, all_out, x_half[micro][0], qkv_weight, other_qkv,
                state["qkv"], state["prob"], state["heads"], grads, scale, devices, members,
                4 + micro_count + micro,
            )
        )
    parts = []
    for micro in range(micro_count):
        state = states[micro]
        parts.append(collect_rows(after(state["y_back"], grads), place[micro], shard_len))
        state["mixed"] = scatter(parts[-1])
        state["block_out"] = (state["h1"] + state["mixed"].astype(F32)).astype(BF16)
    pieces = exchange(grads)

    def added(name):
        total = states[0][name]
        for state in states[1:]:
            total = total + state[name]
        return total

    lines = added("line").reshape(2 * heads_here, 2 * half)
    table = jnp.einsum("hj,jb->hb", lines, onehot_bucket, precision=PRECISE)
    table = table.reshape(2, heads_here * bucket_count)
    mine = jnp.arange(blocks, dtype=jnp.int32)[:, None]
    table = jnp.where(mine == hidden_index, table[0], 0.0) + jnp.where(
        mine == (hidden_index + members) % blocks, table[1], 0.0
    )
    small = jnp.concatenate(
        [
            jnp.sum(dwr, axis=0).reshape(-1),
            added("attn_gain_grad").reshape(-1),
            added("moe_gain_grad").reshape(-1),
            table.reshape(-1),
        ]
    )
    used = small.shape[0]
    small = jnp.pad(small, (0, -used % 1024)).reshape(-1, 128)
    whole, small = closing(pieces, small, blocks)
    whole = whole.reshape(4 * width, head_cols).astype(F32)
    grad_qkv = whole[: 3 * width].reshape(qkv_weight.shape)
    grad_out = whole[3 * width :].T
    small = small.reshape(-1)
    sizes = (width * expert_count, width, width)
    grad_router = small[: sizes[0]].reshape(expert_count, width).T
    grad_attn_gain = small[sizes[0] : sizes[0] + width]
    grad_moe_gain = small[sizes[0] + width : sizes[0] + 2 * width]
    table = small[sizes[0] + 2 * width : used].reshape(blocks, heads_here, bucket_count)
    grad_table = lax.dynamic_index_in_dim(table, hidden_index, 0, keepdims=False).T
    return (
        jnp.stack([state["block_out"] for state in states])[:, None],
        jnp.stack([state["x_grad"] for state in states])[:, None],
        grad_qkv,
        grad_out,
        grad_table,
        grad_attn_gain,
        grad_moe_gain,
        grad_router,
        dwg.transpose(0, 2, 1),
        dwu.transpose(0, 2, 1),
        dwd,
    )


def solution(mesh):
    return jax.shard_map(
        shards,
        mesh=mesh,
        in_specs=(
            P(None, "expert", "hidden", None),
            P(None, "expert", "hidden", None),
            P(None, "expert", None),
            P(None, "expert", "hidden", None),
            P(None, None, "hidden"),
            P("hidden", None),
            P(None, "hidden"),
            P(),
            P(),
            P(),
            P("expert", None, "hidden"),
            P("expert", None, "hidden"),
            P("expert", "hidden", None),
        ),
        out_specs=(
            P(None, "expert", "hidden", None),
            P(None, "expert", "hidden", None),
            P(None, None, "hidden"),
            P("hidden", None),
            P(None, "hidden"),
            P(),
            P(),
            P(),
            P("expert", None, "hidden"),
            P("expert", None, "hidden"),
            P("expert", "hidden", None),
        ),
        check_vma=False,
    )
```

```python
import functools

import jax
import jax.numpy as jnp
from jax import lax
from jax.experimental import pallas as pl
from jax.experimental.pallas import tpu as pltpu
from jax.sharding import PartitionSpec as P

EPSILON = 1e-06
PRECISE = lax.Precision.HIGHEST
LIMITS = (12, 16, 23, 32, 46, 64, 91)
MASKED = -1000000000.0
GELU_C = 0.7978845608028654
GELU_A = 0.044715
VMEM_LIMIT = 60 * 1024 * 1024
F32 = jnp.float32
BF16 = jnp.bfloat16


def mm(a, b):
    return lax.dot_general(a, b, (((1,), (0,)), ((), ())), preferred_element_type=F32)


def mm_nt(a, b):
    return lax.dot_general(a, b, (((1,), (1,)), ((), ())), preferred_element_type=F32)


def mm_tn(a, b):
    return lax.dot_general(a, b, (((0,), (0,)), ((), ())), preferred_element_type=F32)


def bucket_of(distance):
    magnitude = jnp.abs(distance)
    far_bucket = jnp.full(magnitude.shape, 8, jnp.int32)
    for threshold in LIMITS:
        far_bucket = far_bucket + (magnitude >= threshold).astype(jnp.int32)
    return jnp.where(magnitude < 8, magnitude, far_bucket) + 16 * (distance > 0).astype(jnp.int32)


def bucket_onehot(half, bucket_count):
    lane = jnp.arange(2 * half, dtype=jnp.int32)
    distance = jnp.where(lane < half, lane, lane - 2 * half)
    return (
        bucket_of(distance)[:, None] == jnp.arange(bucket_count, dtype=jnp.int32)[None, :]
    ).astype(F32)


TILE = 128


def bias_kernel(line_ref, out_ref):
    length = out_ref.shape[2]
    line = jnp.broadcast_to(line_ref[0], (8, length))
    row = lax.broadcasted_iota(jnp.int32, (8, length), 0)
    sheet = line
    for r in range(1, 8):
        sheet = jnp.where(row == r, pltpu.roll(line, r, 1), sheet)
    while sheet.shape[0] < TILE:
        sheet = jnp.concatenate([sheet, pltpu.roll(sheet, sheet.shape[0], 1)], axis=0)
    out_ref[0] = sheet.astype(out_ref.dtype)


def position_bias(line):
    heads, length = line.shape
    return pl.pallas_call(
        bias_kernel,
        grid=(heads,),
        out_shape=jax.ShapeDtypeStruct((heads, TILE, length), BF16),
        in_specs=[pl.BlockSpec((1, 1, length), lambda h: (h, 0, 0))],
        out_specs=pl.BlockSpec((1, TILE, length), lambda h: (h, 0, 0)),
        compiler_params=pltpu.CompilerParams(vmem_limit_bytes=VMEM_LIMIT),
        name="position_bias",
    )(line.reshape(heads, 1, length))


def unit_rows(x):
    x = x.astype(F32)
    return x * lax.rsqrt(jnp.mean(x * x, axis=-1, keepdims=True) + EPSILON)


def remote(src, dst, send_sem, recv_sem, device):
    return pltpu.make_async_remote_copy(
        src_ref=src, dst_ref=dst, send_sem=send_sem, recv_sem=recv_sem,
        device_id=device, device_id_type=pl.DeviceIdType.MESH,
    )


def greet(devices):
    barrier = pltpu.get_barrier_semaphore()
    for device in devices:
        pl.semaphore_signal(
            barrier, inc=1, device_id=device, device_id_type=pl.DeviceIdType.MESH
        )
    pl.semaphore_wait(barrier, len(devices))


def bits_of(count):
    return [1 << b for b in range(count.bit_length() - 1)]


def partner_of(me, step, count):
    found = 0
    for bit in bits_of(count):
        found = found + bit * lax.rem(me // bit + step // bit, 2)
    return found


def any_space():
    return pl.BlockSpec(memory_space=pl.ANY)


def opening_kernel(
    micros, x_ref, qkv_ref, out_ref, routes_ref, table_ref, dy_ref, *refs,
):
    x_all, refs = refs[:micros], refs[micros:]
    (
        qkv_all, out_all, routes_all, table_all, dy_all,
        x_send, x_recv, qkv_send, qkv_recv, out_send, out_recv, qkv_on_send, qkv_on_recv,
        out_on_send, out_on_recv, routes_send, routes_recv, routes_on_send, routes_on_recv,
        table_send, table_recv, dy_send, dy_recv, own_sem,
    ) = refs
    devices, qkv_rows = qkv_all.shape[0] * 2, qkv_all.shape[2]
    blocks, out_rows = out_all.shape[0], out_all.shape[3]
    members = x_all[0].shape[0]
    me = lax.axis_index("expert")
    line = lax.axis_index("hidden")
    chip, core = me // 2, lax.rem(me, 2)
    mine = lax.rem(line, members)
    base = line - mine
    along = [lax.rem(line + s, blocks) for s in range(1, blocks)]
    across = lax.rem(line + members, blocks)
    sibling = partner_of(me, 1, devices)
    greet([(partner_of(me, s, devices), line) for s in range(1, devices)] + [(me, z) for z in along])
    own = [
        pltpu.make_async_copy(
            out_ref.at[pl.ds(me * out_rows, out_rows)], out_all.at[line, chip, core], own_sem.at[0]
        ),
        pltpu.make_async_copy(routes_ref, routes_all.at[me, line], own_sem.at[1]),
        pltpu.make_async_copy(dy_ref.at[me], dy_all.at[me], own_sem.at[2]),
    ]
    for micro in range(micros):
        own.append(
            pltpu.make_async_copy(x_ref.at[micro], x_all[micro].at[mine], own_sem.at[3 + micro])
        )
    for copy in own:
        copy.start()
    first_qkv = remote(
        qkv_ref.at[pl.ds(me * qkv_rows, qkv_rows)], qkv_all.at[chip, core], qkv_send, qkv_recv,
        (me, across),
    )
    first_qkv.start()
    first_out, first_routes = [], []
    rest = [remote(table_ref, table_all, table_send, table_recv, (me, across))]
    for s, z in enumerate(along):
        first_out.append(
            remote(
                out_ref.at[pl.ds(me * out_rows, out_rows)], out_all.at[line, chip, core],
                out_send.at[s], out_recv.at[s], (me, z),
            )
        )
        first_routes.append(
            remote(
                routes_ref, routes_all.at[me, line], routes_send.at[s], routes_recv.at[s], (me, z)
            )
        )
    for copy in first_routes + first_out + rest:
        copy.start()
    for micro in range(micros):
        for s in range(1, members):
            peer = base + lax.rem(mine + s, members)
            copy = remote(
                x_ref.at[micro], x_all[micro].at[mine], x_send.at[micro, s], x_recv.at[micro, s],
                (me, peer),
            )
            copy.start()
            rest.append(copy)
    for s in range(1, devices):
        peer = partner_of(me, s, devices)
        copy = remote(dy_ref.at[peer], dy_all.at[me], dy_send.at[s], dy_recv.at[s], (peer, line))
        copy.start()
        rest.append(copy)
    first_qkv.wait_recv()
    qkv_on, out_on = [], []
    for s in range(2, devices, 2):
        copy = remote(
            qkv_all.at[chip, core], qkv_all.at[chip, core], qkv_on_send.at[s], qkv_on_recv.at[s],
            (partner_of(me, s, devices), line),
        )
        copy.start()
        qkv_on.append(copy)
    own[1].wait()
    for copy in first_routes:
        copy.wait_recv()
    for s in range(1, devices):
        copy = remote(
            routes_all.at[me], routes_all.at[me], routes_on_send.at[s], routes_on_recv.at[s],
            (partner_of(me, s, devices), line),
        )
        copy.start()
        rest.append(copy)
    own[0].wait()
    for copy in first_out:
        copy.wait_recv()
    for s in range(2, devices, 2):
        copy = remote(
            out_all.at[:, chip, core], out_all.at[:, chip, core], out_on_send.at[s],
            out_on_recv.at[s], (partner_of(me, s, devices), line),
        )
        copy.start()
        out_on.append(copy)
    for copy in qkv_on:
        copy.wait_recv()
    copy = remote(
        qkv_all.at[:, core], qkv_all.at[:, core], qkv_on_send.at[1], qkv_on_recv.at[1],
        (sibling, line),
    )
    copy.start()
    rest.append(copy)
    for copy in out_on:
        copy.wait_recv()
    copy = remote(
        out_all.at[:, :, core], out_all.at[:, :, core], out_on_send.at[1], out_on_recv.at[1],
        (sibling, line),
    )
    copy.start()
    rest.append(copy)
    for copy in own[2:]:
        copy.wait()
    first_qkv.wait_send()
    for copy in first_out + first_routes + qkv_on + out_on:
        copy.wait_send()
    for copy in rest:
        copy.wait()


def opening(x, qkv, out, routes, table, dy, devices, blocks, members):
    micros, shard_len, width = x.shape
    dma = pltpu.SemaphoreType.DMA
    pair = (devices // 2, 2)
    return pl.pallas_call(
        functools.partial(opening_kernel, micros),
        out_shape=(jax.ShapeDtypeStruct((members, shard_len, width), BF16),) * micros
        + (
            jax.ShapeDtypeStruct(pair + (qkv.shape[0] // devices, qkv.shape[1]), BF16),
            jax.ShapeDtypeStruct((blocks,) + pair + (out.shape[0] // devices, width), BF16),
            jax.ShapeDtypeStruct((devices, blocks) + routes.shape, jnp.int32),
            jax.ShapeDtypeStruct(table.shape, table.dtype),
            jax.ShapeDtypeStruct(dy.shape, BF16),
        ),
        in_specs=[any_space()] * 6,
        out_specs=(any_space(),) * (5 + micros),
        scratch_shapes=[
            dma((micros, members)), dma((micros, members)), dma, dma, dma((blocks,)), dma((blocks,)),
            dma((devices,)), dma((devices,)), dma((devices,)), dma((devices,)), dma((blocks,)),
            dma((blocks,)), dma((devices,)), dma((devices,)), dma, dma, dma((devices,)),
            dma((devices,)), dma((3 + micros,)),
        ],
        compiler_params=pltpu.CompilerParams(collective_id=1, has_side_effects=True),
        cost_estimate=pl.CostEstimate(flops=0, bytes_accessed=200000000, transcendentals=0),
        name="opening",
    )(x, qkv, out, routes, table, dy)


def unit_rows(x):
    x = x.astype(F32)
    return x * lax.rsqrt(jnp.mean(x * x, axis=-1, keepdims=True) + EPSILON)


def attend_kernel(
    scale, x_ref, gain_ref, own_ref, other_ref, bias_ref, seg_row_ref, seg_col_ref,
    out_ref, x_own_ref, moe_gain_ref, *refs,
):
    riding = len(refs) > 10
    if riding:
        sent_ref, arrived_ref, ride_send, ride_recv, ride_own = refs[0], refs[6], *refs[-3:]
        refs = refs[1:6] + refs[7:-3]
    qkv_ref, prob_ref, heads_ref, h1_ref, xn2_ref, xn_ref, part_ref, got_ref, send_sem, recv_sem = refs
    micros, members, shard_len, both = got_ref.shape
    cols = both // 2
    heads, length = bias_ref.shape[0], bias_ref.shape[2]
    half = members * shard_len
    size = cols // heads
    micro, group = pl.program_id(0), pl.program_id(1)
    me = lax.axis_index("expert")
    line = lax.axis_index("hidden")
    mine = lax.rem(line, members)
    part = line // members
    base = line - mine

    def swap(m, s):
        peer = lax.rem(mine + s, members)
        return remote(
            part_ref.at[m, peer], got_ref.at[m, mine], send_sem.at[m, s], recv_sem.at[m, s],
            (me, base + peer),
        )

    def ride(s):
        peer = partner_of(me, s, sent_ref.shape[0])
        return remote(
            sent_ref.at[peer], arrived_ref.at[me], ride_send.at[s], ride_recv.at[s], (peer, line)
        )

    def stay():
        return pltpu.make_async_copy(sent_ref.at[me], arrived_ref.at[me], ride_own)

    @pl.when((micro == 0) & (group == 0))
    def _():
        peers = [(me, base + lax.rem(mine + s, members)) for s in range(1, members)]
        if riding:
            devices = sent_ref.shape[0]
            peers += [(partner_of(me, s, devices), line) for s in range(1, devices)]
        greet(peers)
        if riding:
            stay().start()
            for s in range(1, devices):
                ride(s).start()

    @pl.when(group == 0)
    def _():
        xn_ref[...] = (unit_rows(x_ref[0]) * gain_ref[...]).astype(BF16)
        for t in range(3):
            qkv_ref[0, 0, t] = mm(xn_ref[...], own_ref[t]).astype(BF16)

    @pl.when(group > 0)
    def _():
        for t in range(3):
            qkv_ref[0, 0, t] = mm(xn_ref[...], other_ref[t]).astype(BF16)

    seg_row = seg_row_ref[0]
    for head in range(heads):
        inner = slice(head * size, (head + 1) * size)
        keys = qkv_ref[0, 0, 1, :, inner]
        values = qkv_ref[0, 0, 2, :, inner]
        for start in range(0, half, TILE):
            rows = slice(start, start + TILE)
            scores = mm_nt(qkv_ref[0, 0, 0, rows, inner], keys) * scale
            shift = bias_ref[head, :, : half - start]
            if start:
                shift = jnp.concatenate([bias_ref[head, :, length - start :], shift], axis=1)
            scores = scores + shift.astype(F32)
            scores = jnp.where(seg_col_ref[0, rows, :] == seg_row, scores, MASKED)
            top = jnp.max(scores, axis=-1, keepdims=True)
            weights = jnp.exp(scores - top)
            inverse = 1.0 / jnp.sum(weights, axis=-1, keepdims=True)
            prob = (weights * inverse).astype(BF16)
            prob_ref[0, 0, head, rows, :] = prob
            heads_ref[0, rows, inner] = mm(prob, values).astype(BF16)

    for g in range(2):

        @pl.when(group == g)
        def _(g=g):
            for member in range(members):
                rows = slice(member * shard_len, (member + 1) * shard_len)
                part_ref[micro, member, :, g * cols : (g + 1) * cols] = heads_ref[0, rows, :]

    @pl.when(group == 1)
    def _():
        got_ref[micro, mine] = part_ref[micro, mine]
        for s in range(1, members):
            swap(micro, s).start()

    @pl.when((micro == micros - 1) & (group == 1))
    def _():
        for m in range(micros):
            for s in range(1, members):
                swap(m, s).wait_recv()
            h1 = x_own_ref[m].astype(F32)
            for member in range(members):
                for j in range(2):
                    index = lax.rem(part + j, 2) * members + member
                    h1 = h1 + mm(got_ref[m, member, :, j * cols : (j + 1) * cols], out_ref[index])
            h1_ref[m] = h1
            xn2_ref[m] = (unit_rows(h1) * moe_gain_ref[...]).astype(BF16)
        for m in range(micros):
            for s in range(1, members):
                swap(m, s).wait_send()
        if riding:
            stay().wait()
            for s in range(1, sent_ref.shape[0]):
                ride(s).wait()


def attend(
    x, gain, own_weight, other_weight, bias, seg, out_weight, x_own, moe_gain, scale, members, identity,
    rider=None,
):
    micros, half, width = x.shape
    cols = own_weight.shape[2]
    heads = bias.shape[0] // 2
    shard_len = half // members
    riders = [] if rider is None else [rider]
    ride_sems = []
    for array in riders:
        ride_sems = [pltpu.SemaphoreType.DMA((array.shape[0],))] * 2 + [pltpu.SemaphoreType.DMA]

    def once(shape):
        return pl.BlockSpec(shape, lambda m, p: (0,) * len(shape), pipeline_mode=pl.Buffered(1))

    return pl.pallas_call(
        functools.partial(attend_kernel, scale),
        grid=(micros, 2),
        out_shape=(
            jax.ShapeDtypeStruct((micros, 2, 3, half, cols), BF16),
            jax.ShapeDtypeStruct((micros, 2, heads, half, half), BF16),
            jax.ShapeDtypeStruct((micros, half, 2 * cols), BF16),
            jax.ShapeDtypeStruct((micros, shard_len, width), F32),
            jax.ShapeDtypeStruct((micros, shard_len, width), BF16),
        )
        + tuple(jax.ShapeDtypeStruct(array.shape, array.dtype) for array in riders),
        in_specs=[
            pl.BlockSpec((1, half, width), lambda m, p: (m, 0, 0)),
            once((1, width)),
            once((3, width, cols)),
            once((3, width, cols)),
            pl.BlockSpec((heads,) + bias.shape[1:], lambda m, p: (p, 0, 0)),
            pl.BlockSpec((1, 1, half), lambda m, p: (m, 0, 0)),
            pl.BlockSpec((1, half, 1), lambda m, p: (m, 0, 0)),
            once(out_weight.shape),
            once(x_own.shape),
            once((1, width)),
        ]
        + [any_space()] * len(riders),
        out_specs=(
            pl.BlockSpec((1, 1, 3, half, cols), lambda m, p: (m, p, 0, 0, 0)),
            pl.BlockSpec((1, 1, heads, half, half), lambda m, p: (m, p, 0, 0, 0)),
            pl.BlockSpec((1, half, cols), lambda m, p: (m, 0, p)),
            pl.BlockSpec((micros, shard_len, width), lambda m, p: (0, 0, 0)),
            pl.BlockSpec((micros, shard_len, width), lambda m, p: (0, 0, 0)),
        )
        + (any_space(),) * len(riders),
        scratch_shapes=[
            pltpu.VMEM((half, width), BF16),
            pltpu.VMEM((micros, members, shard_len, 2 * cols), BF16),
            pltpu.VMEM((micros, members, shard_len, 2 * cols), BF16),
            pltpu.SemaphoreType.DMA((micros, members)),
            pltpu.SemaphoreType.DMA((micros, members)),
        ]
        + ride_sems,
        compiler_params=pltpu.CompilerParams(
            vmem_limit_bytes=VMEM_LIMIT, collective_id=identity, has_side_effects=True
        ),
        cost_estimate=pl.CostEstimate(
            flops=micros * 2 * half * cols * (8 * width + 4 * half),
            bytes_accessed=100000000,
            transcendentals=micros * 2 * heads * half * half,
        ),
        name="attend",
    )(
        x, gain, own_weight, other_weight, bias, seg.reshape(micros, 1, half),
        seg.reshape(micros, half, 1), out_weight, x_own, moe_gain, *riders,
    )


def back_kernel(
    scale, added, grad_ref, h1_ref, dy_ref, x_own_ref, moe_gain_ref, gain_ref, out_ref, x_ref,
    own_ref, other_ref, qkv_ref, prob_ref, heads_ref, *refs,
):
    if added:
        prev_ref, refs = refs[0], refs[1:]
    (
        xgrad_ref, grads_ref, line_ref, dmoe_ref, dgain_ref,
        dh1_ref, dattn_all, dheads_part, dheads_all, dxn_part, dxn_got, total_ref, xn_ref, ds_ref,
        dproj_ref, sheet_ref, attn_send, attn_recv, heads_send, heads_recv, dxn_send, dxn_recv,
    ) = refs
    members, shard_len, width = dattn_all.shape
    heads, half = prob_ref.shape[1], prob_ref.shape[2]
    cols = dproj_ref.shape[2]
    size = cols // heads
    length = sheet_ref.shape[1]
    group = pl.program_id(0)
    me = lax.axis_index("expert")
    line = lax.axis_index("hidden")
    mine = lax.rem(line, members)
    part = line // members
    base = line - mine
    steps = range(1, members)

    def peer_of(s):
        return lax.rem(mine + s, members)

    def attn_copy(s):
        return remote(
            dattn_all.at[mine], dattn_all.at[mine], attn_send.at[s], attn_recv.at[s],
            (me, base + peer_of(s)),
        )

    def heads_copy(s):
        return remote(
            dheads_part.at[peer_of(s)], dheads_all.at[mine], heads_send.at[s], heads_recv.at[s],
            (me, base + peer_of(s)),
        )

    def dxn_copy(s):
        return remote(
            dxn_part.at[peer_of(s)], dxn_got.at[mine], dxn_send.at[s], dxn_recv.at[s],
            (me, base + peer_of(s)),
        )

    @pl.when(group == 0)
    def _():
        greet([(me, base + peer_of(s)) for s in steps])
        grad = grad_ref[...].astype(F32)
        h1 = h1_ref[...]
        r2 = lax.rsqrt(jnp.mean(h1 * h1, axis=-1, keepdims=True) + EPSILON)
        unit = h1 * r2
        dmoe_ref[...] = jnp.sum(grad * unit, axis=0, keepdims=True)
        weighted = grad * moe_gain_ref[...]
        inner = jnp.mean(weighted * unit, axis=-1, keepdims=True)
        dh1 = dy_ref[...].astype(F32) + r2 * (weighted - unit * inner)
        dh1_ref[...] = dh1
        dattn = dh1.astype(BF16)
        dattn_all[mine] = dattn
        for member in range(members):
            for j in range(2):
                index = lax.rem(part + j, 2) * members + member
                dheads = mm_nt(dattn, out_ref[index]).astype(BF16)
                dheads_part[member, :, j * cols : (j + 1) * cols] = dheads
        for s in steps:
            heads_copy(s).start()
        for s in steps:
            attn_copy(s).start()
        dheads_all[mine] = dheads_part[mine]
        xn_ref[...] = (unit_rows(x_ref[...]) * gain_ref[...]).astype(BF16)
        for s in steps:
            heads_copy(s).wait_recv()

    for g in range(2):

        @pl.when(group == g)
        def _(g=g):
            for head in range(heads):
                inner_cols = slice(head * size, (head + 1) * size)
                outer_cols = slice(g * cols + head * size, g * cols + (head + 1) * size)
                values = qkv_ref[0, 2, :, inner_cols]
                grads = dheads_all[:, :, outer_cols].reshape(half, size)
                sheet_ref[...] = jnp.zeros_like(sheet_ref)
                for start in range(0, half, TILE):
                    rows = slice(start, start + TILE)
                    prob = prob_ref[0, head, rows, :].astype(F32)
                    dprob = mm_nt(grads[rows], values)
                    inner = jnp.sum(prob * dprob, axis=-1, keepdims=True)
                    dscore = (prob * (dprob - inner)).astype(BF16)
                    ds_ref[rows, :] = dscore
                    dscore = dscore.astype(F32)
                    sheet_ref[:, : half - start] += dscore[:, start:]
                    if start:
                        sheet_ref[:, length - start :] += dscore[:, :start]
                dscores = ds_ref[...]
                keys, queries = qkv_ref[0, 1, :, inner_cols], qkv_ref[0, 0, :, inner_cols]
                dproj_ref[0, :, inner_cols] = (mm(dscores, keys) * scale).astype(BF16)
                dproj_ref[1, :, inner_cols] = (mm_tn(dscores, queries) * scale).astype(BF16)
                dproj_ref[2, :, inner_cols] = mm_tn(prob_ref[0, head], grads).astype(BF16)
                sheet = sheet_ref[...]
                while sheet.shape[0] > 8:
                    upper = sheet.shape[0] // 2
                    sheet = sheet[:upper] + pltpu.roll(sheet[upper:], length - upper, 1)
                row = lax.broadcasted_iota(jnp.int32, (8, length), 0)
                found = jnp.zeros((1, length), F32)
                for r in range(8):
                    moved = pltpu.roll(sheet, length - r, 1) if r else sheet
                    found = found + jnp.sum(
                        jnp.where(row == r, moved, 0.0), axis=0, keepdims=True
                    )
                line_ref[0, head : head + 1, :] = found

    def products(weight_ref):
        dxn = mm_nt(dproj_ref[0], weight_ref[0])
        for t in range(1, 3):
            dxn = dxn + mm_nt(dproj_ref[t], weight_ref[t])
        return dxn.reshape(members, shard_len, width)

    @pl.when(group == 0)
    def _():
        total_ref[...] = products(own_ref)
        for s in steps:
            attn_copy(s).wait_recv()

    @pl.when(group == 1)
    def _():
        total_ref[...] += products(other_ref)
        dxn_part[...] = total_ref[...].astype(BF16)
        for s in steps:
            dxn_copy(s).start()

    per = grads_ref.shape[0] // 4
    for t in range(4):
        if t < 3:
            found = mm_tn(xn_ref[...], dproj_ref[t])
        else:
            found = mm_tn(dattn_all[...].reshape(half, width), heads_ref[...])
        found = found.reshape(per, 1, width // per, cols)
        if added:
            found = found + prev_ref[t * per : (t + 1) * per].astype(F32)
        grads_ref[t * per : (t + 1) * per] = found.astype(BF16)

    @pl.when(group == 1)
    def _():
        total = total_ref[...].reshape(half, width)
        dgain_ref[...] = jnp.sum(total * unit_rows(x_ref[...]), axis=0, keepdims=True)
        x_own = x_own_ref[...].astype(F32)
        r1 = lax.rsqrt(jnp.mean(x_own * x_own, axis=-1, keepdims=True) + EPSILON)
        unit = x_own * r1
        for s in steps:
            dxn_copy(s).wait_recv()
        dxn1 = total_ref[mine]
        for s in steps:
            dxn1 = dxn1 + dxn_got[lax.rem(mine + members - s, members)].astype(F32)
        weighted = dxn1 * gain_ref[...]
        inner = jnp.mean(weighted * unit, axis=-1, keepdims=True)
        xgrad_ref[...] = (dh1_ref[...] + r1 * (weighted - unit * inner)).astype(BF16)
        for s in steps:
            heads_copy(s).wait_send()
            attn_copy(s).wait_send()
            dxn_copy(s).wait_send()


def attend_back(
    grad, h1, dy, x_own, moe_gain, gain, out_weight, x_half, own_weight, other_weight, qkv, prob,
    heads_out, prev, scale, pieces, members, identity,
):
    _, heads, half = prob.shape[:3]
    width, cols = own_weight.shape[1:]
    shard_len = half // members
    length = 2 * half
    rows = 4 * width // pieces

    def once(shape):
        return pl.BlockSpec(shape, lambda p: (0,) * len(shape), pipeline_mode=pl.Buffered(1))

    pieces_spec = pl.BlockSpec((pieces, 1, rows, cols), lambda p: (0, p, 0, 0))
    operands = [
        grad, h1, dy, x_own, moe_gain, gain, out_weight, x_half, own_weight, other_weight, qkv,
        prob, heads_out,
    ]
    in_specs = [once(array.shape) for array in operands[:10]] + [
        pl.BlockSpec((1, 3, half, cols), lambda p: (p, 0, 0, 0)),
        pl.BlockSpec((1, heads, half, half), lambda p: (p, 0, 0, 0)),
        pl.BlockSpec((half, cols), lambda p: (0, p)),
    ]
    if prev is not None:
        operands.append(prev)
        in_specs.append(pieces_spec)
    dma = pltpu.SemaphoreType.DMA
    return pl.pallas_call(
        functools.partial(back_kernel, scale, prev is not None),
        grid=(2,),
        out_shape=(
            jax.ShapeDtypeStruct((shard_len, width), BF16),
            jax.ShapeDtypeStruct((pieces, 2, rows, cols), BF16),
            jax.ShapeDtypeStruct((2, heads, length), F32),
            jax.ShapeDtypeStruct((1, width), F32),
            jax.ShapeDtypeStruct((1, width), F32),
        ),
        in_specs=in_specs,
        out_specs=(
            pl.BlockSpec((shard_len, width), lambda p: (0, 0)),
            pieces_spec,
            pl.BlockSpec((1, heads, length), lambda p: (p, 0, 0)),
            pl.BlockSpec((1, width), lambda p: (0, 0)),
            pl.BlockSpec((1, width), lambda p: (0, 0)),
        ),
        scratch_shapes=[
            pltpu.VMEM((shard_len, width), F32),
            pltpu.VMEM((members, shard_len, width), BF16),
            pltpu.VMEM((members, shard_len, 2 * cols), BF16),
            pltpu.VMEM((members, shard_len, 2 * cols), BF16),
            pltpu.VMEM((members, shard_len, width), BF16),
            pltpu.VMEM((members, shard_len, width), BF16),
            pltpu.VMEM((members, shard_len, width), F32),
            pltpu.VMEM((half, width), BF16),
            pltpu.VMEM((half, half), BF16),
            pltpu.VMEM((3, half, cols), BF16),
            pltpu.VMEM((TILE, length), F32),
            dma((members,)), dma((members,)), dma((members,)), dma((members,)), dma((members,)),
            dma((members,)),
        ],
        compiler_params=pltpu.CompilerParams(
            vmem_limit_bytes=VMEM_LIMIT, collective_id=identity, has_side_effects=True
        ),
        cost_estimate=pl.CostEstimate(
            flops=2 * half * cols * (16 * width + 8 * half),
            bytes_accessed=150000000,
            transcendentals=0,
        ),
        name="attend_back",
    )(*operands)


def closing_kernel(
    pieces_ref, small_ref, whole_ref, sum_ref,
    half_got, held_ref, quarter_got, total_ref, moved_ref, moved_got, small_got, line_sum,
    line_got, half_sem, quarter_send, quarter_recv, small_send, small_recv, line_send, line_recv,
    moved_sem, on_send, on_recv, own_sem,
):
    chips = pieces_ref.shape[0]
    devices = 2 * chips
    blocks = line_got.shape[0]
    me = lax.axis_index("expert")
    line = lax.axis_index("hidden")
    chip, core = me // 2, lax.rem(me, 2)
    sibling = partner_of(me, 1, devices)
    along = [lax.rem(line + s, blocks) for s in range(1, blocks)]
    across = lax.rem(line + blocks // 2, blocks)
    greet([(partner_of(me, s, devices), line) for s in range(1, devices)] + [(me, z) for z in along])
    halves = remote(
        pieces_ref.at[:, 1 - core], half_got, half_sem.at[0], half_sem.at[1], (sibling, line)
    )
    halves.start()
    smalls = [
        remote(
            small_ref, small_got.at[me], small_send.at[s], small_recv.at[s],
            (partner_of(me, s, devices), line),
        )
        for s in range(1, devices)
    ]
    for copy in smalls:
        copy.start()
    small_got[me] = small_ref[...]
    halves.wait_recv()
    steps = range(1, chips)

    def quarter(s):
        other = partner_of(chip, s, chips)
        return remote(
            held_ref.at[other], quarter_got.at[s], quarter_send.at[s], quarter_recv.at[s],
            (partner_of(me, 2 * s, devices), line),
        )

    for s in steps:
        other = partner_of(chip, s, chips)
        held = pieces_ref[other, core].astype(F32) + half_got[other].astype(F32)
        held_ref[other] = held.astype(BF16)
        quarter(s).start()
    total_ref[...] = pieces_ref[chip, core].astype(F32) + half_got[chip].astype(F32)
    for copy in smalls:
        copy.wait_recv()
    line_sum[...] = jnp.sum(small_got[...], axis=0)
    lines = [
        remote(line_sum, line_got.at[line], line_send.at[s], line_recv.at[s], (me, z))
        for s, z in enumerate(along)
    ]
    for copy in lines:
        copy.start()
    line_got[line] = line_sum[...]
    for s in steps:
        quarter(s).wait_recv()
        total_ref[...] += quarter_got[s].astype(F32)
    moved_ref[...] = total_ref[1].astype(BF16)
    cross = remote(moved_ref, moved_got, moved_sem.at[0], moved_sem.at[1], (me, across))
    cross.start()
    cross.wait_recv()
    whole_ref[chip, core] = (total_ref[0] + moved_got[...].astype(F32)).astype(BF16)
    onward = [
        remote(
            whole_ref.at[chip, core], whole_ref.at[chip, core], on_send.at[s], on_recv.at[s],
            (partner_of(me, 2 * s, devices), line),
        )
        for s in steps
    ]
    for copy in onward:
        copy.start()
    for copy in lines:
        copy.wait_recv()
    sum_ref[...] = jnp.sum(line_got[...], axis=0)
    for copy in onward:
        copy.wait_recv()
    last = remote(
        whole_ref.at[:, core], whole_ref.at[:, core], on_send.at[0], on_recv.at[0], (sibling, line)
    )
    last.start()
    halves.wait_send()
    for s in steps:
        quarter(s).wait_send()
    cross.wait_send()
    for copy in smalls + lines + onward:
        copy.wait_send()
    last.wait()


def closing(pieces, small, blocks):
    devices, both, rows, cols = pieces.shape
    chips = devices // 2
    vmem = pl.BlockSpec(memory_space=pltpu.VMEM)
    dma = pltpu.SemaphoreType.DMA
    return pl.pallas_call(
        closing_kernel,
        out_shape=(
            jax.ShapeDtypeStruct((chips, 2, rows, cols), BF16),
            jax.ShapeDtypeStruct(small.shape, F32),
        ),
        in_specs=[vmem, vmem],
        out_specs=(vmem, vmem),
        scratch_shapes=[
            pltpu.VMEM((chips, both, rows, cols), BF16),
            pltpu.VMEM((chips, both, rows, cols), BF16),
            pltpu.VMEM((chips, both, rows, cols), BF16),
            pltpu.VMEM((both, rows, cols), F32),
            pltpu.VMEM((rows, cols), BF16),
            pltpu.VMEM((rows, cols), BF16),
            pltpu.VMEM((devices,) + small.shape, F32),
            pltpu.VMEM(small.shape, F32),
            pltpu.VMEM((blocks,) + small.shape, F32),
            dma((2,)), dma((chips,)), dma((chips,)), dma((devices,)), dma((devices,)),
            dma((blocks,)), dma((blocks,)), dma((2,)), dma((chips,)), dma((chips,)), dma,
        ],
        compiler_params=pltpu.CompilerParams(
            vmem_limit_bytes=VMEM_LIMIT, collective_id=3, has_side_effects=True
        ),
        cost_estimate=pl.CostEstimate(flops=0, bytes_accessed=160000000, transcendentals=0),
        name="closing",
    )(pieces.reshape(chips, 2, both, rows, cols), small)


def spread(rows, place0, place1, count):
    ids = lax.broadcasted_iota(jnp.int32, (count, rows.shape[0]), 0)
    hit = (ids == place0) | (ids == place1)
    return mm(jnp.where(hit, 1.0, 0.0).astype(BF16), rows)


def spread_kernel(rows_ref, place_ref, out_ref):
    experts, _, cap, width = out_ref.shape
    placed = spread(rows_ref[...], place_ref[0:1, :], place_ref[1:2, :], experts * cap)
    out_ref[...] = placed.astype(BF16).reshape(experts, 1, cap, width)


def spread_rows(rows, place, experts, cap, shard_len):
    slots, width = rows.shape
    blocks = slots // shard_len
    return pl.pallas_call(
        spread_kernel,
        grid=(blocks,),
        out_shape=jax.ShapeDtypeStruct((experts, blocks, cap, width), BF16),
        in_specs=[
            pl.BlockSpec((shard_len, width), lambda b: (b, 0)),
            pl.BlockSpec((2, shard_len), lambda b: (0, b)),
        ],
        out_specs=pl.BlockSpec((experts, 1, cap, width), lambda b: (0, b, 0, 0)),
        compiler_params=pltpu.CompilerParams(vmem_limit_bytes=VMEM_LIMIT),
        cost_estimate=pl.CostEstimate(
            flops=2 * experts * cap * slots * width,
            bytes_accessed=2 * slots * width + 2 * experts * blocks * cap * width,
            transcendentals=0,
        ),
        name="spread_rows",
    )(rows, place)


def collect_kernel(rows_ref, place_ref, out_ref):
    experts, _, cap, width = rows_ref.shape
    tokens = out_ref.shape[0]
    ids = lax.broadcasted_iota(jnp.int32, (experts * cap, tokens), 0)
    hit = (ids == place_ref[0:1, :]) | (ids == place_ref[1:2, :])
    rows = rows_ref[...].reshape(experts * cap, width)
    out_ref[...] = mm_tn(jnp.where(hit, 1.0, 0.0).astype(BF16), rows).astype(BF16)


def collect_rows(rows, place, shard_len):
    experts, blocks, cap, width = rows.shape
    slots = blocks * shard_len
    return pl.pallas_call(
        collect_kernel,
        grid=(blocks,),
        out_shape=jax.ShapeDtypeStruct((slots, width), BF16),
        in_specs=[
            pl.BlockSpec((experts, 1, cap, width), lambda b: (0, b, 0, 0)),
            pl.BlockSpec((2, shard_len), lambda b: (0, b)),
        ],
        out_specs=pl.BlockSpec((shard_len, width), lambda b: (b, 0)),
        compiler_params=pltpu.CompilerParams(vmem_limit_bytes=VMEM_LIMIT),
        cost_estimate=pl.CostEstimate(
            flops=2 * experts * cap * slots * width,
            bytes_accessed=2 * slots * width + 2 * experts * blocks * cap * width,
            transcendentals=0,
        ),
        name="collect_rows",
    )(rows, place)


def places(route_ref, index, cap, experts):
    shard_len = route_ref.shape[-1]
    row = lax.broadcasted_iota(jnp.int32, (shard_len, shard_len), 0)
    col = lax.broadcasted_iota(jnp.int32, (shard_len, shard_len), 1)
    earlier = jnp.where(row < col, 1.0, 0.0).astype(BF16)
    ids = lax.broadcasted_iota(jnp.int32, (experts, shard_len), 0)
    pair = [route_ref[index + (slice(k, k + 1),)] for k in range(2)]
    chosen = (ids == pair[0]) | (ids == pair[1])
    before = mm(jnp.where(chosen, 1.0, 0.0).astype(BF16), earlier)
    found = []
    for route in pair:
        position = jnp.sum(jnp.where(ids == route, before, 0.0), axis=0, keepdims=True)
        found.append(jnp.where(route >= 0, route * cap + position.astype(jnp.int32), -1))
    return pair, found


def place_kernel(cap, experts, route_ref, place_ref):
    blocks, micros, _, shard_len = route_ref.shape
    for block in range(blocks):
        for micro in range(micros):
            _, found = places(route_ref, (block, micro), cap, experts)
            for k in range(2):
                lanes = slice(block * shard_len, (block + 1) * shard_len)
                place_ref[micro, k : k + 1, lanes] = found[k]


def find_places(route, experts, cap):
    blocks, micros, _, shard_len = route.shape
    vmem = pl.BlockSpec(memory_space=pltpu.VMEM)
    return pl.pallas_call(
        functools.partial(place_kernel, cap, experts),
        out_shape=jax.ShapeDtypeStruct((micros, 2, blocks * shard_len), jnp.int32),
        in_specs=[vmem],
        out_specs=vmem,
        compiler_params=pltpu.CompilerParams(vmem_limit_bytes=VMEM_LIMIT),
        name="find_places",
    )(route)


def pair_kernel(route_ref, pair_ref):
    _, _, here, blocks, cap, experts = pair_ref.shape
    shard_len = route_ref.shape[-1]
    me = lax.axis_index("expert")
    spots = lax.broadcasted_iota(jnp.int32, (cap, shard_len), 0)
    ids = lax.broadcasted_iota(jnp.int32, (cap, experts), 1)
    for block in range(blocks):
        pair, place = places(route_ref, (0, block, 0), cap, experts)
        for e in range(here):
            expert = me * here + e
            other = jnp.full((cap, 1), -1, jnp.int32)
            for k in range(2):
                hit = spots + expert * cap == place[k]
                found = jnp.max(jnp.where(hit, pair[1 - k], -1), axis=1, keepdims=True)
                other = jnp.maximum(other, found)
            sign = jnp.where(ids == expert, 1.0, 0.0) - jnp.where(ids == other, 1.0, 0.0)
            pair_ref[0, 0, e, block] = jnp.where(other >= 0, sign, 0.0).astype(BF16)


def find_pairs(route, experts, here, cap):
    devices, blocks, micros, _, shard_len = route.shape
    return pl.pallas_call(
        pair_kernel,
        grid=(micros, devices),
        out_shape=jax.ShapeDtypeStruct((micros, devices, here, blocks, cap, experts), BF16),
        in_specs=[pl.BlockSpec((1, blocks, 1, 2, shard_len), lambda m, s: (s, 0, m, 0, 0))],
        out_specs=pl.BlockSpec((1, 1, here, blocks, cap, experts), lambda m, s: (m, s, 0, 0, 0, 0)),
        compiler_params=pltpu.CompilerParams(vmem_limit_bytes=VMEM_LIMIT),
        name="find_pairs",
    )(route)


def expert_kernel(
    by_block, sent_ref, dy_ref, pair_ref, wr_ref, wg_ref, wu_ref, wd_ref,
    back_ref, y_ref, x_ref, g_ref, hid_ref, dga_ref, dup_ref, dlog_ref,
    got_ref, dx_ref, stage_ref, x_send, x_recv, dx_send, dx_recv, own_sem, stage_sem,
):
    devices, experts, cap, width = sent_ref.shape
    step = pl.program_id(0)
    me = lax.axis_index("expert")
    line = lax.axis_index("hidden")
    first_wave = bits_of(devices)
    rest = [s for s in range(1, devices) if s not in first_wave]
    later_waves = [rest[i : i + 2] for i in range(0, len(rest), 2)]

    def x_copy(s):
        peer = partner_of(me, s, devices)
        return pltpu.make_async_remote_copy(
            src_ref=sent_ref.at[peer], dst_ref=got_ref.at[s], send_sem=x_send.at[s],
            recv_sem=x_recv.at[s], device_id=(peer, line), device_id_type=pl.DeviceIdType.MESH,
        )

    def dx_copy(s):
        peer = partner_of(me, s, devices)
        return pltpu.make_async_remote_copy(
            src_ref=dx_ref.at[s], dst_ref=back_ref.at[me], send_sem=dx_send.at[s],
            recv_sem=dx_recv.at[s], device_id=(peer, line), device_id_type=pl.DeviceIdType.MESH,
        )

    blocks, share = stage_ref.shape[2:4]

    def y_copies(s):
        source = partner_of(me, s, devices)
        slot = lax.rem(s, 2)
        if not by_block:
            return [
                pltpu.make_async_copy(stage_ref.at[slot], y_ref.at[source], stage_sem.at[slot, 0])
            ]
        return [
            pltpu.make_async_copy(
                stage_ref.at[slot, e], y_ref.at[:, source, e], stage_sem.at[slot, e]
            )
            for e in range(experts)
        ]

    def work(s):
        source = partner_of(me, s, devices)
        slot = lax.rem(s, 2)
        for e in range(experts):
            x = got_ref[s, e]
            dy = dy_ref[:, source, e].reshape(cap, width).astype(F32)
            pair = pair_ref[source, e].astype(F32)
            margin = jnp.sum(mm_nt(x, wr_ref[...]) * pair, axis=-1, keepdims=True)
            own_gate = 1.0 / (1.0 + jnp.exp(-margin))
            other_gate = 1.0 / (1.0 + jnp.exp(margin))
            g = (own_gate * dy).astype(BF16)
            x_ref[0, e] = x
            g_ref[0, e] = g
            gate = mm_nt(x, wg_ref[e])
            up = mm_nt(x, wu_ref[e])
            square = gate * gate
            bent = jnp.tanh(GELU_C * gate * (1.0 + GELU_A * square))
            half_gate = 0.5 * gate
            gelu = half_gate * (1.0 + bent)
            slope = 0.5 * (1.0 + bent) + half_gate * (1.0 - bent * bent) * (
                GELU_C * (1.0 + 3.0 * GELU_A * square)
            )
            hid = (gelu * up).astype(BF16)
            dhid = mm_nt(g, wd_ref[e])
            dga = (dhid * (up * slope)).astype(BF16)
            dup = (dhid * gelu).astype(BF16)
            hid_ref[0, e] = hid
            dga_ref[0, e] = dga
            dup_ref[0, e] = dup
            y = mm(hid, wd_ref[e])
            dgate = jnp.sum(y * dy, axis=-1, keepdims=True)
            stage_ref[slot, e] = (y * own_gate).astype(BF16).reshape(blocks, share, width)
            dlog = (dgate * own_gate * other_gate * pair).astype(BF16)
            dlog_ref[0, e] = dlog
            dx = mm(dga, wg_ref[e]) + mm(dup, wu_ref[e]) + mm(dlog, wr_ref[...])
            dx_ref[s, e] = dx.astype(BF16)

    @pl.when(step == 0)
    def _():
        barrier = pltpu.get_barrier_semaphore()
        for s in range(1, devices):
            pl.semaphore_signal(
                barrier, inc=1, device_id=(partner_of(me, s, devices), line),
                device_id_type=pl.DeviceIdType.MESH,
            )
        pl.semaphore_wait(barrier, devices - 1)
        for s in first_wave:
            x_copy(s).start()
        own = pltpu.make_async_copy(sent_ref.at[me], got_ref.at[0], own_sem)
        own.start()
        own.wait()

    @pl.when(step > 0)
    def _():
        x_copy(step).wait_recv()

    for index, wave in enumerate(later_waves):

        @pl.when(step == 2 + index)
        def _(wave=wave):
            for s in wave:
                x_copy(s).start()

    @pl.when(step > 1)
    def _():
        for copy in y_copies(step - 2):
            copy.wait()

    work(step)
    for copy in y_copies(step):
        copy.start()

    @pl.when(step > 0)
    def _():
        dx_copy(step).start()

    @pl.when(step == devices - 1)
    def _():
        own = pltpu.make_async_copy(dx_ref.at[0], back_ref.at[me], own_sem)
        own.start()
        own.wait()
        for copy in y_copies(devices - 2) + y_copies(devices - 1):
            copy.wait()
        for s in range(1, devices):
            x_copy(s).wait_send()
            dx_copy(s).wait_send()
            dx_copy(s).wait_recv()


def expert_pass(sent, dy, pair, wr, wg, wu, wd, by_block, identity):
    blocks, _, _, share, _ = dy.shape
    devices, experts, cap, width = sent.shape
    hidden = wg.shape[1]
    choices = wr.shape[0]

    def whole(shape):
        return pl.BlockSpec(shape, lambda s: (0,) * len(shape), pipeline_mode=pl.Buffered(1))

    def block(cols):
        return pl.BlockSpec((1, experts, cap, cols), lambda s: (s, 0, 0, 0))

    def kept(cols):
        return jax.ShapeDtypeStruct((devices, experts, cap, cols), BF16)

    y_shape = (blocks, devices, experts, share, width)
    if not by_block:
        y_shape = (devices, experts, blocks, share, width)
    return pl.pallas_call(
        functools.partial(expert_kernel, by_block),
        grid=(devices,),
        out_shape=(
            kept(width), jax.ShapeDtypeStruct(y_shape, BF16), kept(width), kept(width), kept(hidden), kept(hidden),
            kept(hidden), kept(choices),
        ),
        in_specs=[
            any_space(), whole(dy.shape), whole(pair.shape), whole(wr.shape), whole(wg.shape),
            whole(wu.shape), whole(wd.shape),
        ],
        out_specs=(
            any_space(), any_space(), block(width), block(width), block(hidden), block(hidden),
            block(hidden), block(choices),
        ),
        scratch_shapes=[
            pltpu.VMEM((devices, experts, cap, width), BF16),
            pltpu.VMEM((devices, experts, cap, width), BF16),
            pltpu.VMEM((2, experts, blocks, share, width), BF16),
            pltpu.SemaphoreType.DMA((devices,)),
            pltpu.SemaphoreType.DMA((devices,)),
            pltpu.SemaphoreType.DMA((devices,)),
            pltpu.SemaphoreType.DMA((devices,)),
            pltpu.SemaphoreType.DMA,
            pltpu.SemaphoreType.DMA((2, experts)),
        ],
        compiler_params=pltpu.CompilerParams(
            vmem_limit_bytes=VMEM_LIMIT, collective_id=identity, has_side_effects=True
        ),
        cost_estimate=pl.CostEstimate(flops=0, bytes_accessed=490000000, transcendentals=0),
        name="expert_pass",
    )(sent, dy, pair, wr, wg, wu, wd)


def weight_kernel(*refs):
    count = (len(refs) - 4) // 6
    dwr_ref, dwg_ref, dwu_ref, dwd_ref = refs[-4:]
    totals = [0.0, 0.0, 0.0, 0.0]
    for index in range(count):
        blocks = [
            ref[...].reshape(ref.shape[0] * ref.shape[2], ref.shape[3])
            for ref in refs[6 * index : 6 * index + 6]
        ]
        x, g, hid, dga, dup, dlog = blocks
        totals[0] = totals[0] + mm_tn(dlog, x)
        totals[1] = totals[1] + mm_tn(dga, x)
        totals[2] = totals[2] + mm_tn(dup, x)
        totals[3] = totals[3] + mm_tn(hid, g)
    dwr_ref[0] = totals[0]
    dwg_ref[0] = totals[1]
    dwu_ref[0] = totals[2]
    dwd_ref[0] = totals[3]


def weight_pass(kept):
    sources, experts, cap, width = kept[0][0].shape
    hidden = kept[0][2].shape[3]
    choices = kept[0][5].shape[3]
    rows = sources * cap
    block = 256 if width % 256 == 0 else width
    tokens = pl.BlockSpec((sources, 1, cap, block), lambda e, j: (0, e, 0, j))
    acts = pl.BlockSpec((sources, 1, cap, hidden), lambda e, j: (0, e, 0, 0))
    logs = pl.BlockSpec((sources, 1, cap, choices), lambda e, j: (0, e, 0, 0))
    operands = []
    for arrays in kept:
        operands.extend(arrays)
    return pl.pallas_call(
        weight_kernel,
        grid=(experts, width // block),
        out_shape=(
            jax.ShapeDtypeStruct((experts, choices, width), F32),
            jax.ShapeDtypeStruct((experts, hidden, width), F32),
            jax.ShapeDtypeStruct((experts, hidden, width), F32),
            jax.ShapeDtypeStruct((experts, hidden, width), F32),
        ),
        in_specs=[tokens, tokens, acts, acts, acts, logs] * len(kept),
        out_specs=(
            pl.BlockSpec((1, choices, block), lambda e, j: (e, 0, j)),
            pl.BlockSpec((1, hidden, block), lambda e, j: (e, 0, j)),
            pl.BlockSpec((1, hidden, block), lambda e, j: (e, 0, j)),
            pl.BlockSpec((1, hidden, block), lambda e, j: (e, 0, j)),
        ),
        compiler_params=pltpu.CompilerParams(vmem_limit_bytes=VMEM_LIMIT),
        cost_estimate=pl.CostEstimate(
            flops=6 * len(kept) * experts * rows * width * hidden,
            bytes_accessed=len(kept) * experts * rows * (4 * width + 6 * hidden)
            + 12 * experts * width * hidden,
            transcendentals=0,
        ),
        name="weight_pass",
    )(*operands)


def after(values, *others):
    return lax.optimization_barrier((values,) + others)[0]


def shards(
    x_in,
    cotangent,
    segment_ids,
    routes,
    qkv_weight,
    out_weight,
    bias_table,
    attn_gain,
    moe_gain,
    router_weight,
    gate_weight,
    up_weight,
    down_weight,
):
    micro_count, _, shard_len, width = x_in.shape
    slot_count = segment_ids.shape[2]
    head_cols = out_weight.shape[0]
    bucket_count, heads_here = bias_table.shape
    head_size = head_cols // heads_here
    expert_count = router_weight.shape[1]
    experts_here = gate_weight.shape[0]
    devices = expert_count // experts_here
    blocks = slot_count // shard_len
    members = blocks // 2
    half = slot_count // 2
    capacity = max(2, (10 * shard_len + 4 * expert_count - 1) // (4 * expert_count))
    scale = head_size ** (-0.5)
    hidden_index = lax.axis_index("hidden")
    expert_index = lax.axis_index("expert")
    part = hidden_index // members
    attn_gain_f = attn_gain.astype(F32).reshape(1, width)
    moe_gain_f = moe_gain.astype(F32).reshape(1, width)
    token_shape = (devices, experts_here, blocks * capacity, width)
    flat_shape = (devices, experts_here * blocks * capacity, width)
    place_shape = (expert_count, blocks, capacity, width)
    gate_rows = gate_weight.transpose(0, 2, 1)
    up_rows = up_weight.transpose(0, 2, 1)
    router_rows = router_weight.T

    def exchange(buffer):
        return lax.all_to_all(buffer, "expert", split_axis=0, concat_axis=0, tiled=True)

    def gather(values):
        return lax.all_gather(values, "hidden", axis=0, tiled=True)

    def scatter(values):
        return lax.psum_scatter(values, "hidden", scatter_dimension=0, tiled=True)

    states = [dict() for _ in range(micro_count)]
    own_seg = lax.dynamic_slice_in_dim(segment_ids[:, 0], hidden_index * shard_len, shard_len, 1)
    live_routes = jnp.where(own_seg[:, None, :] >= 0, routes[:, 0].transpose(0, 2, 1), -1)
    own_place = find_places(live_routes[None], expert_count, capacity)

    def spread(rows, placed):
        return spread_rows(rows, placed, expert_count, capacity, shard_len)

    dy_sent = [
        spread(cotangent[micro, 0], own_place[micro]).reshape(devices, -1, width)
        for micro in range(micro_count)
    ]
    *x_all, other_qkv, all_out, all_routes, other_table, dy_first = opening(
        x_in[:, 0], qkv_weight.reshape(3 * width, head_cols), out_weight,
        live_routes, bias_table.T.astype(F32), dy_sent[0], devices, blocks, members,
    )
    x_half = [x.reshape(1, half, width) for x in x_all]
    other_qkv = other_qkv.reshape(qkv_weight.shape)
    all_out = all_out.reshape(blocks, head_cols, width)

    own_routes = lax.dynamic_index_in_dim(all_routes, expert_index, 0, keepdims=False)
    place = find_places(own_routes, expert_count, capacity)

    tables = jnp.concatenate([bias_table.T.astype(F32), other_table], axis=0)
    onehot_bucket = bucket_onehot(half, bucket_count)
    bias = position_bias(jnp.einsum("jb,hb->hj", onehot_bucket, tables, precision=PRECISE))
    seg_half = lax.dynamic_slice_in_dim(segment_ids[:, 0], part * half, half, 1)

    def gather_dy(rows):
        whole = gather(rows.reshape(1, devices * experts_here * capacity, width))
        return whole.reshape(blocks, devices, experts_here, capacity, width)

    def experts(micro, kept, *behind):
        sent = spread(kept["xn2_all"], place[micro]).reshape(token_shape)
        kept["by_block"] = micro + 1 < micro_count
        back, kept["y"], x, g, hid, dga, dup, dlog = expert_pass(
            after(sent, *behind), kept["dy"], pairs[micro], router_rows, gate_rows, up_rows,
            down_weight, kept["by_block"], 4 + micro,
        )
        kept["weights"] = (x, g, hid, dga, dup, dlog)
        kept["back"] = back
        if micro > 0:
            back = after(back, states[micro - 1]["y_own"])
        kept["dx_back"] = back.reshape(place_shape)
        kept["dx_part"] = collect_rows(kept["dx_back"], place[micro], shard_len)
        kept["dxn2"] = scatter(kept["dx_part"])
        if kept["by_block"]:
            parts = after(kept["y"], kept["dx_part"]).reshape(blocks, -1, width)
            kept["y_own"] = scatter(parts).reshape(devices, -1, width)

    states[0]["dy"] = gather_dy(dy_first)
    behind = ()
    for micro in range(micro_count):
        state = states[micro]
        rider = None
        if micro + 1 < micro_count:
            rider = dy_sent[micro + 1]
        qkv, prob, heads, h1, xn2, *rode = attend(
            after(x_half[micro], *behind), attn_gain_f, qkv_weight, other_qkv, bias,
            seg_half[micro : micro + 1], all_out, x_in[micro], moe_gain_f, scale, members, 10 + micro,
            rider,
        )
        state.update(qkv=qkv[0], prob=prob[0], heads=heads[0], h1=h1[0], xn2=xn2[0])
        if micro + 1 < micro_count:
            states[micro + 1]["dy_here"] = rode[0]
        behind = (xn2, states[0]["dy"])
    behind = ()
    for micro in range(micro_count):
        state = states[micro]
        state["xn2_all"] = gather(after(state["xn2"], *behind))
        behind = (state["xn2_all"],)
    for micro in range(1, micro_count):
        states[micro]["dy"] = gather_dy(after(states[micro]["dy_here"], states[0]["xn2_all"]))
    pairs = find_pairs(after(all_routes, states[-1]["xn2"]), expert_count, experts_here, capacity)
    pairs = pairs.reshape(micro_count, devices, experts_here, blocks * capacity, expert_count)
    behind = ()
    for micro in range(micro_count):
        experts(micro, states[micro], *behind)
        behind = (states[micro]["dx_part"],)
    last_part = states[-1]["dx_part"]
    kept = [state["weights"] for state in states]
    kept[-1] = tuple(after(list(kept[-1]), last_part))
    dwr, dwg, dwu, dwd = weight_pass(kept)
    grads = None
    behind = (last_part,)
    for micro in range(micro_count):
        state = states[micro]
        if state["by_block"]:
            sent = after(state["y_own"], states[-1]["back"])
            state["y_rows"] = exchange(sent).reshape(expert_count, 1, capacity, width)
        else:
            sent = after(state["y"], *behind).reshape(flat_shape)
            state["y_rows"] = exchange(sent).reshape(place_shape)
        behind = (last_part, state["y_rows"])
    for micro in range(micro_count):
        state = states[micro]
        state["x_grad"], grads, state["line"], state["moe_gain_grad"], state["attn_gain_grad"] = (
            attend_back(
                after(state["dxn2"], dwr), state["h1"], cotangent[micro, 0], x_in[micro, 0],
                moe_gain_f, attn_gain_f, all_out, x_half[micro][0], qkv_weight, other_qkv,
                state["qkv"], state["prob"], state["heads"], grads, scale, devices, members,
                4 + micro_count + micro,
            )
        )
    for micro in range(micro_count):
        state = states[micro]
        rows = after(state["y_rows"], grads)
        if state["by_block"]:
            mixed = collect_rows(rows, own_place[micro], shard_len)
        else:
            mixed = scatter(collect_rows(rows, place[micro], shard_len))
        state["block_out"] = (state["h1"] + mixed.astype(F32)).astype(BF16)

    def added(name):
        total = states[0][name]
        for state in states[1:]:
            total = total + state[name]
        return total

    lines = added("line").reshape(2 * heads_here, 2 * half)
    table = jnp.einsum("hj,jb->hb", lines, onehot_bucket, precision=PRECISE)
    table = table.reshape(2, heads_here * bucket_count)
    mine = jnp.arange(blocks, dtype=jnp.int32)[:, None]
    table = jnp.where(mine == hidden_index, table[0], 0.0) + jnp.where(
        mine == (hidden_index + members) % blocks, table[1], 0.0
    )
    small = jnp.concatenate(
        [
            jnp.sum(dwr, axis=0).reshape(-1),
            added("attn_gain_grad").reshape(-1),
            added("moe_gain_grad").reshape(-1),
            table.reshape(-1),
        ]
    )
    used = small.shape[0]
    small = jnp.pad(small, (0, -used % 1024)).reshape(-1, 128)
    whole, small = closing(grads, small, blocks)
    whole = whole.reshape(4 * width, head_cols).astype(F32)
    grad_qkv = whole[: 3 * width].reshape(qkv_weight.shape)
    grad_out = whole[3 * width :].T
    small = small.reshape(-1)
    sizes = (width * expert_count, width, width)
    grad_router = small[: sizes[0]].reshape(expert_count, width).T
    grad_attn_gain = small[sizes[0] : sizes[0] + width]
    grad_moe_gain = small[sizes[0] + width : sizes[0] + 2 * width]
    table = small[sizes[0] + 2 * width : used].reshape(blocks, heads_here, bucket_count)
    grad_table = lax.dynamic_index_in_dim(table, hidden_index, 0, keepdims=False).T
    return (
        jnp.stack([state["block_out"] for state in states])[:, None],
        jnp.stack([state["x_grad"] for state in states])[:, None],
        grad_qkv,
        grad_out,
        grad_table,
        grad_attn_gain,
        grad_moe_gain,
        grad_router,
        dwg.transpose(0, 2, 1),
        dwu.transpose(0, 2, 1),
        dwd,
    )


def solution(mesh):
    return jax.shard_map(
        shards,
        mesh=mesh,
        in_specs=(
            P(None, "expert", "hidden", None),
            P(None, "expert", "hidden", None),
            P(None, "expert", None),
            P(None, "expert", "hidden", None),
            P(None, None, "hidden"),
            P("hidden", None),
            P(None, "hidden"),
            P(),
            P(),
            P(),
            P("expert", None, "hidden"),
            P("expert", None, "hidden"),
            P("expert", "hidden", None),
        ),
        out_specs=(
            P(None, "expert", "hidden", None),
            P(None, "expert", "hidden", None),
            P(None, None, "hidden"),
            P("hidden", None),
            P(None, "hidden"),
            P(),
            P(),
            P(),
            P("expert", None, "hidden"),
            P("expert", None, "hidden"),
            P("expert", "hidden", None),
        ),
        check_vma=False,
    )
```

```python
import functools

import jax
import jax.numpy as jnp
from jax import lax
from jax.experimental import pallas as pl
from jax.experimental.pallas import tpu as pltpu
from jax.sharding import PartitionSpec as P

EPSILON = 1e-06
PRECISE = lax.Precision.HIGHEST
LIMITS = (12, 16, 23, 32, 46, 64, 91)
MASKED = -1000000000.0
GELU_C = 0.7978845608028654
GELU_A = 0.044715
VMEM_LIMIT = 60 * 1024 * 1024
F32 = jnp.float32
BF16 = jnp.bfloat16


def mm(a, b):
    return lax.dot_general(a, b, (((1,), (0,)), ((), ())), preferred_element_type=F32)


def mm_nt(a, b):
    return lax.dot_general(a, b, (((1,), (1,)), ((), ())), preferred_element_type=F32)


def mm_tn(a, b):
    return lax.dot_general(a, b, (((0,), (0,)), ((), ())), preferred_element_type=F32)


def bucket_of(distance):
    magnitude = jnp.abs(distance)
    far_bucket = jnp.full(magnitude.shape, 8, jnp.int32)
    for threshold in LIMITS:
        far_bucket = far_bucket + (magnitude >= threshold).astype(jnp.int32)
    return jnp.where(magnitude < 8, magnitude, far_bucket) + 16 * (distance > 0).astype(jnp.int32)


def bucket_onehot(half, bucket_count):
    lane = jnp.arange(2 * half, dtype=jnp.int32)
    distance = jnp.where(lane < half, lane, lane - 2 * half)
    return (
        bucket_of(distance)[:, None] == jnp.arange(bucket_count, dtype=jnp.int32)[None, :]
    ).astype(F32)


TILE = 128


def bias_kernel(line_ref, out_ref):
    length = out_ref.shape[2]
    line = jnp.broadcast_to(line_ref[0], (8, length))
    row = lax.broadcasted_iota(jnp.int32, (8, length), 0)
    sheet = line
    for r in range(1, 8):
        sheet = jnp.where(row == r, pltpu.roll(line, r, 1), sheet)
    while sheet.shape[0] < TILE:
        sheet = jnp.concatenate([sheet, pltpu.roll(sheet, sheet.shape[0], 1)], axis=0)
    out_ref[0] = sheet.astype(out_ref.dtype)


def position_bias(line):
    heads, length = line.shape
    return pl.pallas_call(
        bias_kernel,
        grid=(heads,),
        out_shape=jax.ShapeDtypeStruct((heads, TILE, length), BF16),
        in_specs=[pl.BlockSpec((1, 1, length), lambda h: (h, 0, 0))],
        out_specs=pl.BlockSpec((1, TILE, length), lambda h: (h, 0, 0)),
        compiler_params=pltpu.CompilerParams(vmem_limit_bytes=VMEM_LIMIT),
        name="position_bias",
    )(line.reshape(heads, 1, length))


def unit_rows(x):
    x = x.astype(F32)
    return x * lax.rsqrt(jnp.mean(x * x, axis=-1, keepdims=True) + EPSILON)


def remote(src, dst, send_sem, recv_sem, device):
    return pltpu.make_async_remote_copy(
        src_ref=src, dst_ref=dst, send_sem=send_sem, recv_sem=recv_sem,
        device_id=device, device_id_type=pl.DeviceIdType.MESH,
    )


def greet(devices):
    barrier = pltpu.get_barrier_semaphore()
    for device in devices:
        pl.semaphore_signal(
            barrier, inc=1, device_id=device, device_id_type=pl.DeviceIdType.MESH
        )
    pl.semaphore_wait(barrier, len(devices))


def bits_of(count):
    return [1 << b for b in range(count.bit_length() - 1)]


def partner_of(me, step, count):
    found = 0
    for bit in bits_of(count):
        found = found + bit * lax.rem(me // bit + step // bit, 2)
    return found


def any_space():
    return pl.BlockSpec(memory_space=pl.ANY)


def opening_kernel(
    micros, x_ref, qkv_ref, out_ref, routes_ref, table_ref, *refs,
):
    x_all, refs = refs[:micros], refs[micros:]
    (
        qkv_all, out_all, routes_all, table_all,
        x_send, x_recv, qkv_send, qkv_recv, out_send, out_recv, qkv_on_send, qkv_on_recv,
        out_on_send, out_on_recv, routes_send, routes_recv, routes_on_send, routes_on_recv,
        table_send, table_recv, own_sem,
    ) = refs
    devices, qkv_rows = qkv_all.shape[0] * 2, qkv_all.shape[2]
    blocks, out_rows = out_all.shape[0], out_all.shape[3]
    members = x_all[0].shape[0]
    me = lax.axis_index("expert")
    line = lax.axis_index("hidden")
    chip, core = me // 2, lax.rem(me, 2)
    mine = lax.rem(line, members)
    base = line - mine
    along = [lax.rem(line + s, blocks) for s in range(1, blocks)]
    across = lax.rem(line + members, blocks)
    sibling = partner_of(me, 1, devices)
    greet([(partner_of(me, s, devices), line) for s in range(1, devices)] + [(me, z) for z in along])
    own = [
        pltpu.make_async_copy(
            out_ref.at[pl.ds(me * out_rows, out_rows)], out_all.at[line, chip, core], own_sem.at[0]
        ),
        pltpu.make_async_copy(routes_ref, routes_all.at[me, line], own_sem.at[1]),
    ]
    for micro in range(micros):
        own.append(
            pltpu.make_async_copy(x_ref.at[micro], x_all[micro].at[mine], own_sem.at[2 + micro])
        )
    for copy in own:
        copy.start()
    first_qkv = remote(
        qkv_ref.at[pl.ds(me * qkv_rows, qkv_rows)], qkv_all.at[chip, core], qkv_send, qkv_recv,
        (me, across),
    )
    first_qkv.start()
    first_out, first_routes = [], []
    rest = [remote(table_ref, table_all, table_send, table_recv, (me, across))]
    for s, z in enumerate(along):
        first_out.append(
            remote(
                out_ref.at[pl.ds(me * out_rows, out_rows)], out_all.at[line, chip, core],
                out_send.at[s], out_recv.at[s], (me, z),
            )
        )
        first_routes.append(
            remote(
                routes_ref, routes_all.at[me, line], routes_send.at[s], routes_recv.at[s], (me, z)
            )
        )
    for copy in first_routes + first_out + rest:
        copy.start()
    for micro in range(micros):
        for s in range(1, members):
            peer = base + lax.rem(mine + s, members)
            copy = remote(
                x_ref.at[micro], x_all[micro].at[mine], x_send.at[micro, s], x_recv.at[micro, s],
                (me, peer),
            )
            copy.start()
            rest.append(copy)
    first_qkv.wait_recv()
    qkv_on, out_on = [], []
    for s in range(2, devices, 2):
        copy = remote(
            qkv_all.at[chip, core], qkv_all.at[chip, core], qkv_on_send.at[s], qkv_on_recv.at[s],
            (partner_of(me, s, devices), line),
        )
        copy.start()
        qkv_on.append(copy)
    own[1].wait()
    for copy in first_routes:
        copy.wait_recv()
    for s in range(1, devices):
        copy = remote(
            routes_all.at[me], routes_all.at[me], routes_on_send.at[s], routes_on_recv.at[s],
            (partner_of(me, s, devices), line),
        )
        copy.start()
        rest.append(copy)
    own[0].wait()
    for copy in first_out:
        copy.wait_recv()
    for s in range(2, devices, 2):
        copy = remote(
            out_all.at[:, chip, core], out_all.at[:, chip, core], out_on_send.at[s],
            out_on_recv.at[s], (partner_of(me, s, devices), line),
        )
        copy.start()
        out_on.append(copy)
    for copy in qkv_on:
        copy.wait_recv()
    copy = remote(
        qkv_all.at[:, core], qkv_all.at[:, core], qkv_on_send.at[1], qkv_on_recv.at[1],
        (sibling, line),
    )
    copy.start()
    rest.append(copy)
    for copy in out_on:
        copy.wait_recv()
    copy = remote(
        out_all.at[:, :, core], out_all.at[:, :, core], out_on_send.at[1], out_on_recv.at[1],
        (sibling, line),
    )
    copy.start()
    rest.append(copy)
    for copy in own[2:]:
        copy.wait()
    first_qkv.wait_send()
    for copy in first_out + first_routes + qkv_on + out_on:
        copy.wait_send()
    for copy in rest:
        copy.wait()


def opening(x, qkv, out, routes, table, devices, blocks, members):
    micros, shard_len, width = x.shape
    dma = pltpu.SemaphoreType.DMA
    pair = (devices // 2, 2)
    return pl.pallas_call(
        functools.partial(opening_kernel, micros),
        out_shape=(jax.ShapeDtypeStruct((members, shard_len, width), BF16),) * micros
        + (
            jax.ShapeDtypeStruct(pair + (qkv.shape[0] // devices, qkv.shape[1]), BF16),
            jax.ShapeDtypeStruct((blocks,) + pair + (out.shape[0] // devices, width), BF16),
            jax.ShapeDtypeStruct((devices, blocks) + routes.shape, jnp.int32),
            jax.ShapeDtypeStruct(table.shape, table.dtype),
        ),
        in_specs=[any_space()] * 5,
        out_specs=(any_space(),) * (4 + micros),
        scratch_shapes=[
            dma((micros, members)), dma((micros, members)), dma, dma, dma((blocks,)), dma((blocks,)),
            dma((devices,)), dma((devices,)), dma((devices,)), dma((devices,)), dma((blocks,)),
            dma((blocks,)), dma((devices,)), dma((devices,)), dma, dma, dma((2 + micros,)),
        ],
        compiler_params=pltpu.CompilerParams(collective_id=1, has_side_effects=True),
        cost_estimate=pl.CostEstimate(flops=0, bytes_accessed=200000000, transcendentals=0),
        name="opening",
    )(x, qkv, out, routes, table)


def swap_kernel(sent_ref, got_ref, send_sem, recv_sem, own_sem):
    devices = sent_ref.shape[0]
    me = lax.axis_index("expert")
    line = lax.axis_index("hidden")
    greet([(partner_of(me, s, devices), line) for s in range(1, devices)])
    own = pltpu.make_async_copy(sent_ref.at[me], got_ref.at[me], own_sem)
    own.start()
    copies = []
    for s in range(1, devices):
        peer = partner_of(me, s, devices)
        copies.append(
            remote(sent_ref.at[peer], got_ref.at[me], send_sem.at[s], recv_sem.at[s], (peer, line))
        )
        copies[-1].start()
    own.wait()
    for copy in copies:
        copy.wait()


def swap_rows(sent, identity):
    dma = pltpu.SemaphoreType.DMA
    return pl.pallas_call(
        swap_kernel,
        out_shape=jax.ShapeDtypeStruct(sent.shape, sent.dtype),
        in_specs=[any_space()],
        out_specs=any_space(),
        scratch_shapes=[dma((sent.shape[0],)), dma((sent.shape[0],)), dma],
        compiler_params=pltpu.CompilerParams(collective_id=identity, has_side_effects=True),
        cost_estimate=pl.CostEstimate(flops=0, bytes_accessed=60000000, transcendentals=0),
        name="swap_rows",
    )(sent)


def unit_rows(x):
    x = x.astype(F32)
    return x * lax.rsqrt(jnp.mean(x * x, axis=-1, keepdims=True) + EPSILON)


def attend_kernel(
    scale, x_ref, gain_ref, own_ref, other_ref, bias_ref, seg_row_ref, seg_col_ref,
    out_ref, x_own_ref, moe_gain_ref, *refs,
):
    riding = len(refs) > 10
    if riding:
        sent_ref, arrived_ref, ride_send, ride_recv, ride_own = refs[0], refs[6], *refs[-3:]
        refs = refs[1:6] + refs[7:-3]
    qkv_ref, prob_ref, heads_ref, h1_ref, xn2_ref, xn_ref, part_ref, got_ref, send_sem, recv_sem = refs
    micros, members, shard_len, both = got_ref.shape
    cols = both // 2
    heads, length = bias_ref.shape[0], bias_ref.shape[2]
    half = members * shard_len
    size = cols // heads
    micro, group = pl.program_id(0), pl.program_id(1)
    me = lax.axis_index("expert")
    line = lax.axis_index("hidden")
    mine = lax.rem(line, members)
    part = line // members
    base = line - mine

    def swap(m, s):
        peer = lax.rem(mine + s, members)
        return remote(
            part_ref.at[m, peer], got_ref.at[m, mine], send_sem.at[m, s], recv_sem.at[m, s],
            (me, base + peer),
        )

    def ride(s):
        peer = partner_of(me, s, sent_ref.shape[0])
        return remote(
            sent_ref.at[peer], arrived_ref.at[me], ride_send.at[s], ride_recv.at[s], (peer, line)
        )

    def stay():
        return pltpu.make_async_copy(sent_ref.at[me], arrived_ref.at[me], ride_own)

    @pl.when((micro == 0) & (group == 0))
    def _():
        peers = [(me, base + lax.rem(mine + s, members)) for s in range(1, members)]
        if riding:
            devices = sent_ref.shape[0]
            peers += [(partner_of(me, s, devices), line) for s in range(1, devices)]
        greet(peers)
        if riding:
            stay().start()
            for s in range(1, devices):
                ride(s).start()

    @pl.when(group == 0)
    def _():
        xn_ref[...] = (unit_rows(x_ref[0]) * gain_ref[...]).astype(BF16)
        for t in range(3):
            qkv_ref[0, 0, t] = mm(xn_ref[...], own_ref[t]).astype(BF16)

    @pl.when(group > 0)
    def _():
        for t in range(3):
            qkv_ref[0, 0, t] = mm(xn_ref[...], other_ref[t]).astype(BF16)

    seg_row = seg_row_ref[0]
    for head in range(heads):
        inner = slice(head * size, (head + 1) * size)
        keys = qkv_ref[0, 0, 1, :, inner]
        values = qkv_ref[0, 0, 2, :, inner]
        for start in range(0, half, TILE):
            rows = slice(start, start + TILE)
            scores = mm_nt(qkv_ref[0, 0, 0, rows, inner], keys) * scale
            shift = bias_ref[head, :, : half - start]
            if start:
                shift = jnp.concatenate([bias_ref[head, :, length - start :], shift], axis=1)
            scores = scores + shift.astype(F32)
            scores = jnp.where(seg_col_ref[0, rows, :] == seg_row, scores, MASKED)
            top = jnp.max(scores, axis=-1, keepdims=True)
            weights = jnp.exp(scores - top)
            inverse = 1.0 / jnp.sum(weights, axis=-1, keepdims=True)
            prob = (weights * inverse).astype(BF16)
            prob_ref[0, 0, head, rows, :] = prob
            heads_ref[0, rows, inner] = mm(prob, values).astype(BF16)

    for g in range(2):

        @pl.when(group == g)
        def _(g=g):
            for member in range(members):
                rows = slice(member * shard_len, (member + 1) * shard_len)
                part_ref[micro, member, :, g * cols : (g + 1) * cols] = heads_ref[0, rows, :]

    @pl.when(group == 1)
    def _():
        got_ref[micro, mine] = part_ref[micro, mine]
        for s in range(1, members):
            swap(micro, s).start()

    @pl.when((micro == micros - 1) & (group == 1))
    def _():
        for m in range(micros):
            for s in range(1, members):
                swap(m, s).wait_recv()
            h1 = x_own_ref[m].astype(F32)
            for member in range(members):
                for j in range(2):
                    index = lax.rem(part + j, 2) * members + member
                    h1 = h1 + mm(got_ref[m, member, :, j * cols : (j + 1) * cols], out_ref[index])
            h1_ref[m] = h1
            xn2_ref[m] = (unit_rows(h1) * moe_gain_ref[...]).astype(BF16)
        for m in range(micros):
            for s in range(1, members):
                swap(m, s).wait_send()
        if riding:
            stay().wait()
            for s in range(1, sent_ref.shape[0]):
                ride(s).wait()


def attend(
    x, gain, own_weight, other_weight, bias, seg, out_weight, x_own, moe_gain, scale, members, identity,
    rider=None,
):
    micros, half, width = x.shape
    cols = own_weight.shape[2]
    heads = bias.shape[0] // 2
    shard_len = half // members
    riders = [] if rider is None else [rider]
    ride_sems = []
    for array in riders:
        ride_sems = [pltpu.SemaphoreType.DMA((array.shape[0],))] * 2 + [pltpu.SemaphoreType.DMA]

    def once(shape):
        return pl.BlockSpec(shape, lambda m, p: (0,) * len(shape), pipeline_mode=pl.Buffered(1))

    return pl.pallas_call(
        functools.partial(attend_kernel, scale),
        grid=(micros, 2),
        out_shape=(
            jax.ShapeDtypeStruct((micros, 2, 3, half, cols), BF16),
            jax.ShapeDtypeStruct((micros, 2, heads, half, half), BF16),
            jax.ShapeDtypeStruct((micros, half, 2 * cols), BF16),
            jax.ShapeDtypeStruct((micros, shard_len, width), F32),
            jax.ShapeDtypeStruct((micros, shard_len, width), BF16),
        )
        + tuple(jax.ShapeDtypeStruct(array.shape, array.dtype) for array in riders),
        in_specs=[
            pl.BlockSpec((1, half, width), lambda m, p: (m, 0, 0)),
            once((1, width)),
            once((3, width, cols)),
            once((3, width, cols)),
            pl.BlockSpec((heads,) + bias.shape[1:], lambda m, p: (p, 0, 0)),
            pl.BlockSpec((1, 1, half), lambda m, p: (m, 0, 0)),
            pl.BlockSpec((1, half, 1), lambda m, p: (m, 0, 0)),
            once(out_weight.shape),
            once(x_own.shape),
            once((1, width)),
        ]
        + [any_space()] * len(riders),
        out_specs=(
            pl.BlockSpec((1, 1, 3, half, cols), lambda m, p: (m, p, 0, 0, 0)),
            pl.BlockSpec((1, 1, heads, half, half), lambda m, p: (m, p, 0, 0, 0)),
            pl.BlockSpec((1, half, cols), lambda m, p: (m, 0, p)),
            pl.BlockSpec((micros, shard_len, width), lambda m, p: (0, 0, 0)),
            pl.BlockSpec((micros, shard_len, width), lambda m, p: (0, 0, 0)),
        )
        + (any_space(),) * len(riders),
        scratch_shapes=[
            pltpu.VMEM((half, width), BF16),
            pltpu.VMEM((micros, members, shard_len, 2 * cols), BF16),
            pltpu.VMEM((micros, members, shard_len, 2 * cols), BF16),
            pltpu.SemaphoreType.DMA((micros, members)),
            pltpu.SemaphoreType.DMA((micros, members)),
        ]
        + ride_sems,
        compiler_params=pltpu.CompilerParams(
            vmem_limit_bytes=VMEM_LIMIT, collective_id=identity, has_side_effects=True
        ),
        cost_estimate=pl.CostEstimate(
            flops=micros * 2 * half * cols * (8 * width + 4 * half),
            bytes_accessed=100000000,
            transcendentals=micros * 2 * heads * half * half,
        ),
        name="attend",
    )(
        x, gain, own_weight, other_weight, bias, seg.reshape(micros, 1, half),
        seg.reshape(micros, half, 1), out_weight, x_own, moe_gain, *riders,
    )


def back_kernel(scale, micros, *refs):
    moe_gain_ref, gain_ref, out_ref, own_ref, other_ref = refs[:5]
    inputs = [refs[5 + 8 * m : 13 + 8 * m] for m in range(micros)]
    refs = refs[5 + 8 * micros :]
    xgrads, refs = refs[:micros], refs[micros:]
    (
        grads_ref, line_ref, dmoe_ref, dgain_ref,
        dh1_ref, dattn_all, dheads_part, dheads_all, dxn_part, dxn_got, total_ref, xn_ref, ds_ref,
        dproj_ref, sheet_ref, attn_send, attn_recv, heads_send, heads_recv, dxn_send, dxn_recv,
    ) = refs
    _, members, shard_len, width = dattn_all.shape
    cols = dproj_ref.shape[2]
    half = members * shard_len
    length = sheet_ref.shape[1]
    group, micro = pl.program_id(0), pl.program_id(1)
    me = lax.axis_index("expert")
    line = lax.axis_index("hidden")
    mine = lax.rem(line, members)
    part = line // members
    base = line - mine
    steps = range(1, members)

    def peer_of(s):
        return lax.rem(mine + s, members)

    def attn_copy(m, s):
        return remote(
            dattn_all.at[m, mine], dattn_all.at[m, mine], attn_send.at[m, s], attn_recv.at[m, s],
            (me, base + peer_of(s)),
        )

    def heads_copy(m, s):
        return remote(
            dheads_part.at[m, peer_of(s)], dheads_all.at[m, mine], heads_send.at[m, s],
            heads_recv.at[m, s], (me, base + peer_of(s)),
        )

    def dxn_copy(m, s):
        return remote(
            dxn_part.at[m, peer_of(s)], dxn_got.at[m, mine], dxn_send.at[m, s], dxn_recv.at[m, s],
            (me, base + peer_of(s)),
        )

    @pl.when((group == 0) & (micro == 0))
    def _():
        greet([(me, base + peer_of(s)) for s in steps])
        dmoe_ref[...] = jnp.zeros_like(dmoe_ref)
        dgain_ref[...] = jnp.zeros_like(dgain_ref)
        for m in range(micros):
            grad_ref, h1_ref, dy_ref = inputs[m][:3]
            grad = grad_ref[...].astype(F32)
            h1 = h1_ref[...]
            r2 = lax.rsqrt(jnp.mean(h1 * h1, axis=-1, keepdims=True) + EPSILON)
            unit = h1 * r2
            dmoe_ref[...] += jnp.sum(grad * unit, axis=0, keepdims=True)
            weighted = grad * moe_gain_ref[...]
            inner = jnp.mean(weighted * unit, axis=-1, keepdims=True)
            dh1 = dy_ref[...].astype(F32) + r2 * (weighted - unit * inner)
            dh1_ref[m] = dh1
            dattn = dh1.astype(BF16)
            dattn_all[m, mine] = dattn
            for member in range(members):
                for j in range(2):
                    index = lax.rem(part + j, 2) * members + member
                    dheads = mm_nt(dattn, out_ref[index]).astype(BF16)
                    dheads_part[m, member, :, j * cols : (j + 1) * cols] = dheads
            for s in steps:
                heads_copy(m, s).start()
            dheads_all[m, mine] = dheads_part[m, mine]
        for m in range(micros):
            xn_ref[m] = (unit_rows(inputs[m][4][...]) * gain_ref[...]).astype(BF16)

    def products(weight_ref):
        dxn = mm_nt(dproj_ref[0], weight_ref[0])
        for t in range(1, 3):
            dxn = dxn + mm_nt(dproj_ref[t], weight_ref[t])
        return dxn.reshape(members, shard_len, width)

    per = grads_ref.shape[0] // 4
    for g in range(2):
        for m in range(micros):

            @pl.when((group == g) & (micro == m))
            def _(g=g, m=m):
                x_ref, qkv_ref, prob_ref, heads_ref = inputs[m][4:]
                heads = prob_ref.shape[1]
                size = cols // heads
                if g == 0:
                    for s in steps:
                        heads_copy(m, s).wait_recv()
                    for s in steps:
                        attn_copy(m, s).start()
                for head in range(heads):
                    inner_cols = slice(head * size, (head + 1) * size)
                    outer_cols = slice(g * cols + head * size, g * cols + (head + 1) * size)
                    values = qkv_ref[0, 2, :, inner_cols]
                    grads = dheads_all[m, :, :, outer_cols].reshape(half, size)
                    sheet_ref[...] = jnp.zeros_like(sheet_ref)
                    for start in range(0, half, TILE):
                        rows = slice(start, start + TILE)
                        prob = prob_ref[0, head, rows, :].astype(F32)
                        dprob = mm_nt(grads[rows], values)
                        inner = jnp.sum(prob * dprob, axis=-1, keepdims=True)
                        dscore = (prob * (dprob - inner)).astype(BF16)
                        ds_ref[rows, :] = dscore
                        dscore = dscore.astype(F32)
                        sheet_ref[:, : half - start] += dscore[:, start:]
                        if start:
                            sheet_ref[:, length - start :] += dscore[:, :start]
                    dscores = ds_ref[...]
                    keys, queries = qkv_ref[0, 1, :, inner_cols], qkv_ref[0, 0, :, inner_cols]
                    dproj_ref[0, :, inner_cols] = (mm(dscores, keys) * scale).astype(BF16)
                    dproj_ref[1, :, inner_cols] = (mm_tn(dscores, queries) * scale).astype(BF16)
                    dproj_ref[2, :, inner_cols] = mm_tn(prob_ref[0, head], grads).astype(BF16)
                    sheet = sheet_ref[...]
                    while sheet.shape[0] > 8:
                        upper = sheet.shape[0] // 2
                        sheet = sheet[:upper] + pltpu.roll(sheet[upper:], length - upper, 1)
                    row = lax.broadcasted_iota(jnp.int32, (8, length), 0)
                    found = jnp.zeros((1, length), F32)
                    for r in range(8):
                        moved = pltpu.roll(sheet, length - r, 1) if r else sheet
                        found = found + jnp.sum(
                            jnp.where(row == r, moved, 0.0), axis=0, keepdims=True
                        )
                    if m:
                        found = found + line_ref[0, head : head + 1, :]
                    line_ref[0, head : head + 1, :] = found
                if g == 0:
                    total_ref[m] = products(own_ref)
                    for s in steps:
                        attn_copy(m, s).wait_recv()
                else:
                    total = total_ref[m] + products(other_ref)
                    total_ref[m] = total
                    dxn_part[m] = total.astype(BF16)
                    for s in steps:
                        dxn_copy(m, s).start()
                    total = total.reshape(half, width)
                    dgain_ref[...] += jnp.sum(total * unit_rows(x_ref[...]), axis=0, keepdims=True)
                for t in range(4):
                    if t < 3:
                        found = mm_tn(xn_ref[m], dproj_ref[t])
                    else:
                        found = mm_tn(dattn_all[m].reshape(half, width), heads_ref[...])
                    found = found.reshape(per, 1, width // per, cols)
                    if m:
                        found = found + grads_ref[t * per : (t + 1) * per].astype(F32)
                    grads_ref[t * per : (t + 1) * per] = found.astype(BF16)

    @pl.when((group == 1) & (micro == micros - 1))
    def _():
        for m in range(micros):
            x_own = inputs[m][3][...].astype(F32)
            r1 = lax.rsqrt(jnp.mean(x_own * x_own, axis=-1, keepdims=True) + EPSILON)
            unit = x_own * r1
            for s in steps:
                dxn_copy(m, s).wait_recv()
            dxn1 = total_ref[m, mine]
            for s in steps:
                dxn1 = dxn1 + dxn_got[m, lax.rem(mine + members - s, members)].astype(F32)
            weighted = dxn1 * gain_ref[...]
            inner = jnp.mean(weighted * unit, axis=-1, keepdims=True)
            xgrads[m][...] = (dh1_ref[m] + r1 * (weighted - unit * inner)).astype(BF16)
        for m in range(micros):
            for s in steps:
                heads_copy(m, s).wait_send()
                attn_copy(m, s).wait_send()
                dxn_copy(m, s).wait_send()


def attend_back(moe_gain, gain, out_weight, own_weight, other_weight, kept, scale, pieces, members):
    micros = len(kept)
    _, heads, half = kept[0][6].shape[:3]
    width, cols = own_weight.shape[1:]
    shard_len = half // members
    length = 2 * half
    rows = 4 * width // pieces

    def once(array):
        return pl.BlockSpec(
            array.shape, lambda p, m: (0,) * array.ndim, pipeline_mode=pl.Buffered(1)
        )

    operands = [moe_gain, gain, out_weight, own_weight, other_weight]
    in_specs = [once(array) for array in operands]
    for arrays in kept:
        operands.extend(arrays)
        in_specs += [once(array) for array in arrays[:5]] + [
            pl.BlockSpec((1, 3, half, cols), lambda p, m: (p, 0, 0, 0)),
            pl.BlockSpec((1, heads, half, half), lambda p, m: (p, 0, 0, 0)),
            pl.BlockSpec((half, cols), lambda p, m: (0, p)),
        ]
    dma = pltpu.SemaphoreType.DMA((micros, members))
    return pl.pallas_call(
        functools.partial(back_kernel, scale, micros),
        grid=(2, micros),
        out_shape=(jax.ShapeDtypeStruct((shard_len, width), BF16),) * micros
        + (
            jax.ShapeDtypeStruct((pieces, 2, rows, cols), BF16),
            jax.ShapeDtypeStruct((2, heads, length), F32),
            jax.ShapeDtypeStruct((1, width), F32),
            jax.ShapeDtypeStruct((1, width), F32),
        ),
        in_specs=in_specs,
        out_specs=(pl.BlockSpec((shard_len, width), lambda p, m: (0, 0)),) * micros
        + (
            pl.BlockSpec((pieces, 1, rows, cols), lambda p, m: (0, p, 0, 0)),
            pl.BlockSpec((1, heads, length), lambda p, m: (p, 0, 0)),
            pl.BlockSpec((1, width), lambda p, m: (0, 0)),
            pl.BlockSpec((1, width), lambda p, m: (0, 0)),
        ),
        scratch_shapes=[
            pltpu.VMEM((micros, shard_len, width), F32),
            pltpu.VMEM((micros, members, shard_len, width), BF16),
            pltpu.VMEM((micros, members, shard_len, 2 * cols), BF16),
            pltpu.VMEM((micros, members, shard_len, 2 * cols), BF16),
            pltpu.VMEM((micros, members, shard_len, width), BF16),
            pltpu.VMEM((micros, members, shard_len, width), BF16),
            pltpu.VMEM((micros, members, shard_len, width), F32),
            pltpu.VMEM((micros, half, width), BF16),
            pltpu.VMEM((half, half), BF16),
            pltpu.VMEM((3, half, cols), BF16),
            pltpu.VMEM((TILE, length), F32),
            dma, dma, dma, dma, dma, dma,
        ],
        compiler_params=pltpu.CompilerParams(
            vmem_limit_bytes=VMEM_LIMIT, collective_id=6, has_side_effects=True
        ),
        cost_estimate=pl.CostEstimate(
            flops=2 * micros * half * cols * (16 * width + 8 * half),
            bytes_accessed=250000000,
            transcendentals=0,
        ),
        name="attend_back",
    )(*operands)


def closing_kernel(
    pieces_ref, small_ref, y_ref, h1_ref, whole_ref, sum_ref, block_ref,
    y_got, y_send, y_recv, half_got, held_ref, quarter_got, total_ref, moved_ref, moved_got, small_got, line_sum,
    line_got, half_sem, quarter_send, quarter_recv, small_send, small_recv, line_send, line_recv,
    moved_sem, on_send, on_recv, own_sem,
):
    chips = pieces_ref.shape[0]
    devices = 2 * chips
    blocks = line_got.shape[0]
    me = lax.axis_index("expert")
    line = lax.axis_index("hidden")
    chip, core = me // 2, lax.rem(me, 2)
    sibling = partner_of(me, 1, devices)
    along = [lax.rem(line + s, blocks) for s in range(1, blocks)]
    across = lax.rem(line + blocks // 2, blocks)
    greet([(partner_of(me, s, devices), line) for s in range(1, devices)] + [(me, z) for z in along])
    ys = [
        remote(y_ref.at[z], y_got.at[line], y_send.at[s], y_recv.at[s], (me, z))
        for s, z in enumerate(along)
    ]
    halves = remote(
        pieces_ref.at[:, 1 - core], half_got, half_sem.at[0], half_sem.at[1], (sibling, line)
    )
    halves.start()
    for copy in ys:
        copy.start()
    smalls = [
        remote(
            small_ref, small_got.at[me], small_send.at[s], small_recv.at[s],
            (partner_of(me, s, devices), line),
        )
        for s in range(1, devices)
    ]
    for copy in smalls:
        copy.start()
    small_got[me] = small_ref[...]
    halves.wait_recv()
    steps = range(1, chips)

    def quarter(s):
        other = partner_of(chip, s, chips)
        return remote(
            held_ref.at[other], quarter_got.at[s], quarter_send.at[s], quarter_recv.at[s],
            (partner_of(me, 2 * s, devices), line),
        )

    for s in steps:
        other = partner_of(chip, s, chips)
        held = pieces_ref[other, core].astype(F32) + half_got[other].astype(F32)
        held_ref[other] = held.astype(BF16)
        quarter(s).start()
    total_ref[...] = pieces_ref[chip, core].astype(F32) + half_got[chip].astype(F32)
    for copy in smalls:
        copy.wait_recv()
    line_sum[...] = jnp.sum(small_got[...], axis=0)
    lines = [
        remote(line_sum, line_got.at[line], line_send.at[s], line_recv.at[s], (me, z))
        for s, z in enumerate(along)
    ]
    for copy in lines:
        copy.start()
    line_got[line] = line_sum[...]
    for s in steps:
        quarter(s).wait_recv()
        total_ref[...] += quarter_got[s].astype(F32)
    moved_ref[...] = total_ref[1].astype(BF16)
    cross = remote(moved_ref, moved_got, moved_sem.at[0], moved_sem.at[1], (me, across))
    cross.start()
    cross.wait_recv()
    whole_ref[chip, core] = (total_ref[0] + moved_got[...].astype(F32)).astype(BF16)
    onward = [
        remote(
            whole_ref.at[chip, core], whole_ref.at[chip, core], on_send.at[s], on_recv.at[s],
            (partner_of(me, 2 * s, devices), line),
        )
        for s in steps
    ]
    for copy in onward:
        copy.start()
    for copy in lines:
        copy.wait_recv()
    sum_ref[...] = jnp.sum(line_got[...], axis=0)
    for copy in onward:
        copy.wait_recv()
    y_got[line] = y_ref[line]
    last = remote(
        whole_ref.at[:, core], whole_ref.at[:, core], on_send.at[0], on_recv.at[0], (sibling, line)
    )
    last.start()
    for copy in ys:
        copy.wait_recv()
    block_ref[...] = (h1_ref[...] + jnp.sum(y_got[...].astype(F32), axis=0)).astype(BF16)
    for copy in ys:
        copy.wait_send()
    halves.wait_send()
    for s in steps:
        quarter(s).wait_send()
    cross.wait_send()
    for copy in smalls + lines + onward:
        copy.wait_send()
    last.wait()


def closing(pieces, small, y, h1):
    devices, both, rows, cols = pieces.shape
    blocks = y.shape[0]
    chips = devices // 2
    vmem = pl.BlockSpec(memory_space=pltpu.VMEM)
    dma = pltpu.SemaphoreType.DMA
    return pl.pallas_call(
        closing_kernel,
        out_shape=(
            jax.ShapeDtypeStruct((chips, 2, rows, cols), BF16),
            jax.ShapeDtypeStruct(small.shape, F32),
            jax.ShapeDtypeStruct(h1.shape, BF16),
        ),
        in_specs=[vmem] * 4,
        out_specs=(vmem,) * 3,
        scratch_shapes=[
            pltpu.VMEM(y.shape, BF16),
            dma((blocks,)),
            dma((blocks,)),
            pltpu.VMEM((chips, both, rows, cols), BF16),
            pltpu.VMEM((chips, both, rows, cols), BF16),
            pltpu.VMEM((chips, both, rows, cols), BF16),
            pltpu.VMEM((both, rows, cols), F32),
            pltpu.VMEM((rows, cols), BF16),
            pltpu.VMEM((rows, cols), BF16),
            pltpu.VMEM((devices,) + small.shape, F32),
            pltpu.VMEM(small.shape, F32),
            pltpu.VMEM((blocks,) + small.shape, F32),
            dma((2,)), dma((chips,)), dma((chips,)), dma((devices,)), dma((devices,)),
            dma((blocks,)), dma((blocks,)), dma((2,)), dma((chips,)), dma((chips,)), dma,
        ],
        compiler_params=pltpu.CompilerParams(
            vmem_limit_bytes=VMEM_LIMIT, collective_id=3, has_side_effects=True
        ),
        cost_estimate=pl.CostEstimate(flops=0, bytes_accessed=160000000, transcendentals=0),
        name="closing",
    )(pieces.reshape(chips, 2, both, rows, cols), small, y, h1)


def spread(rows, place0, place1, count):
    ids = lax.broadcasted_iota(jnp.int32, (count, rows.shape[0]), 0)
    hit = (ids == place0) | (ids == place1)
    return mm(jnp.where(hit, 1.0, 0.0).astype(BF16), rows)


def spread_kernel(rows_ref, place_ref, out_ref):
    experts, _, cap, width = out_ref.shape
    placed = spread(rows_ref[...], place_ref[0:1, :], place_ref[1:2, :], experts * cap)
    out_ref[...] = placed.astype(BF16).reshape(experts, 1, cap, width)


def spread_rows(rows, place, experts, cap, shard_len):
    slots, width = rows.shape
    blocks = slots // shard_len
    return pl.pallas_call(
        spread_kernel,
        grid=(blocks,),
        out_shape=jax.ShapeDtypeStruct((experts, blocks, cap, width), BF16),
        in_specs=[
            pl.BlockSpec((shard_len, width), lambda b: (b, 0)),
            pl.BlockSpec((2, shard_len), lambda b: (0, b)),
        ],
        out_specs=pl.BlockSpec((experts, 1, cap, width), lambda b: (0, b, 0, 0)),
        compiler_params=pltpu.CompilerParams(vmem_limit_bytes=VMEM_LIMIT),
        cost_estimate=pl.CostEstimate(
            flops=2 * experts * cap * slots * width,
            bytes_accessed=2 * slots * width + 2 * experts * blocks * cap * width,
            transcendentals=0,
        ),
        name="spread_rows",
    )(rows, place)


def collect_kernel(rows_ref, place_ref, out_ref):
    experts, _, cap, width = rows_ref.shape
    tokens = out_ref.shape[0]
    ids = lax.broadcasted_iota(jnp.int32, (experts * cap, tokens), 0)
    hit = (ids == place_ref[0:1, :]) | (ids == place_ref[1:2, :])
    rows = rows_ref[...].reshape(experts * cap, width)
    out_ref[...] = mm_tn(jnp.where(hit, 1.0, 0.0).astype(BF16), rows).astype(BF16)


def collect_rows(rows, place, shard_len):
    experts, blocks, cap, width = rows.shape
    slots = blocks * shard_len
    return pl.pallas_call(
        collect_kernel,
        grid=(blocks,),
        out_shape=jax.ShapeDtypeStruct((slots, width), BF16),
        in_specs=[
            pl.BlockSpec((experts, 1, cap, width), lambda b: (0, b, 0, 0)),
            pl.BlockSpec((2, shard_len), lambda b: (0, b)),
        ],
        out_specs=pl.BlockSpec((shard_len, width), lambda b: (b, 0)),
        compiler_params=pltpu.CompilerParams(vmem_limit_bytes=VMEM_LIMIT),
        cost_estimate=pl.CostEstimate(
            flops=2 * experts * cap * slots * width,
            bytes_accessed=2 * slots * width + 2 * experts * blocks * cap * width,
            transcendentals=0,
        ),
        name="collect_rows",
    )(rows, place)


def places(route_ref, index, cap, experts):
    shard_len = route_ref.shape[-1]
    row = lax.broadcasted_iota(jnp.int32, (shard_len, shard_len), 0)
    col = lax.broadcasted_iota(jnp.int32, (shard_len, shard_len), 1)
    earlier = jnp.where(row < col, 1.0, 0.0).astype(BF16)
    ids = lax.broadcasted_iota(jnp.int32, (experts, shard_len), 0)
    pair = [route_ref[index + (slice(k, k + 1),)] for k in range(2)]
    chosen = (ids == pair[0]) | (ids == pair[1])
    before = mm(jnp.where(chosen, 1.0, 0.0).astype(BF16), earlier)
    found = []
    for route in pair:
        position = jnp.sum(jnp.where(ids == route, before, 0.0), axis=0, keepdims=True)
        found.append(jnp.where(route >= 0, route * cap + position.astype(jnp.int32), -1))
    return pair, found


def place_kernel(cap, experts, route_ref, place_ref):
    blocks, micros, _, shard_len = route_ref.shape
    for block in range(blocks):
        for micro in range(micros):
            _, found = places(route_ref, (block, micro), cap, experts)
            for k in range(2):
                lanes = slice(block * shard_len, (block + 1) * shard_len)
                place_ref[micro, k : k + 1, lanes] = found[k]


def find_places(route, experts, cap):
    blocks, micros, _, shard_len = route.shape
    vmem = pl.BlockSpec(memory_space=pltpu.VMEM)
    return pl.pallas_call(
        functools.partial(place_kernel, cap, experts),
        out_shape=jax.ShapeDtypeStruct((micros, 2, blocks * shard_len), jnp.int32),
        in_specs=[vmem],
        out_specs=vmem,
        compiler_params=pltpu.CompilerParams(vmem_limit_bytes=VMEM_LIMIT),
        name="find_places",
    )(route)


def pair_kernel(route_ref, pair_ref):
    _, _, here, blocks, cap, experts = pair_ref.shape
    shard_len = route_ref.shape[-1]
    me = lax.axis_index("expert")
    spots = lax.broadcasted_iota(jnp.int32, (cap, shard_len), 0)
    ids = lax.broadcasted_iota(jnp.int32, (cap, experts), 1)
    for block in range(blocks):
        pair, place = places(route_ref, (0, block, 0), cap, experts)
        for e in range(here):
            expert = me * here + e
            other = jnp.full((cap, 1), -1, jnp.int32)
            for k in range(2):
                hit = spots + expert * cap == place[k]
                found = jnp.max(jnp.where(hit, pair[1 - k], -1), axis=1, keepdims=True)
                other = jnp.maximum(other, found)
            sign = jnp.where(ids == expert, 1.0, 0.0) - jnp.where(ids == other, 1.0, 0.0)
            pair_ref[0, 0, e, block] = jnp.where(other >= 0, sign, 0.0).astype(BF16)


def find_pairs(route, experts, here, cap):
    devices, blocks, micros, _, shard_len = route.shape
    return pl.pallas_call(
        pair_kernel,
        grid=(micros, devices),
        out_shape=jax.ShapeDtypeStruct((micros, devices, here, blocks, cap, experts), BF16),
        in_specs=[pl.BlockSpec((1, blocks, 1, 2, shard_len), lambda m, s: (s, 0, m, 0, 0))],
        out_specs=pl.BlockSpec((1, 1, here, blocks, cap, experts), lambda m, s: (m, s, 0, 0, 0, 0)),
        compiler_params=pltpu.CompilerParams(vmem_limit_bytes=VMEM_LIMIT),
        name="find_pairs",
    )(route)


def expert_kernel(
    by_block, sent_ref, dy_ref, pair_ref, wr_ref, wg_ref, wu_ref, wd_ref,
    back_ref, y_ref, x_ref, g_ref, hid_ref, dga_ref, dup_ref, dlog_ref,
    got_ref, dx_ref, stage_ref, x_send, x_recv, dx_send, dx_recv, own_sem, stage_sem,
):
    devices, experts, cap, width = sent_ref.shape
    step = pl.program_id(0)
    me = lax.axis_index("expert")
    line = lax.axis_index("hidden")
    first_wave = bits_of(devices)
    rest = [s for s in range(1, devices) if s not in first_wave]
    later_waves = [rest[i : i + 2] for i in range(0, len(rest), 2)]

    def x_copy(s):
        peer = partner_of(me, s, devices)
        return pltpu.make_async_remote_copy(
            src_ref=sent_ref.at[peer], dst_ref=got_ref.at[s], send_sem=x_send.at[s],
            recv_sem=x_recv.at[s], device_id=(peer, line), device_id_type=pl.DeviceIdType.MESH,
        )

    def dx_copy(s):
        peer = partner_of(me, s, devices)
        return pltpu.make_async_remote_copy(
            src_ref=dx_ref.at[s], dst_ref=back_ref.at[me], send_sem=dx_send.at[s],
            recv_sem=dx_recv.at[s], device_id=(peer, line), device_id_type=pl.DeviceIdType.MESH,
        )

    blocks, share = stage_ref.shape[2:4]

    def y_copies(s):
        source = partner_of(me, s, devices)
        slot = lax.rem(s, 2)
        if not by_block:
            return [
                pltpu.make_async_copy(stage_ref.at[slot], y_ref.at[source], stage_sem.at[slot, 0])
            ]
        return [
            pltpu.make_async_copy(
                stage_ref.at[slot, e], y_ref.at[:, source, e], stage_sem.at[slot, e]
            )
            for e in range(experts)
        ]

    def work(s):
        source = partner_of(me, s, devices)
        slot = lax.rem(s, 2)
        for e in range(experts):
            x = got_ref[s, e]
            dy = dy_ref[:, source, e].reshape(cap, width).astype(F32)
            pair = pair_ref[source, e].astype(F32)
            margin = jnp.sum(mm_nt(x, wr_ref[...]) * pair, axis=-1, keepdims=True)
            own_gate = 1.0 / (1.0 + jnp.exp(-margin))
            other_gate = 1.0 / (1.0 + jnp.exp(margin))
            g = (own_gate * dy).astype(BF16)
            x_ref[0, e] = x
            g_ref[0, e] = g
            gate = mm_nt(x, wg_ref[e])
            up = mm_nt(x, wu_ref[e])
            square = gate * gate
            bent = jnp.tanh(GELU_C * gate * (1.0 + GELU_A * square))
            half_gate = 0.5 * gate
            gelu = half_gate * (1.0 + bent)
            slope = 0.5 * (1.0 + bent) + half_gate * (1.0 - bent * bent) * (
                GELU_C * (1.0 + 3.0 * GELU_A * square)
            )
            hid = (gelu * up).astype(BF16)
            dhid = mm_nt(g, wd_ref[e])
            dga = (dhid * (up * slope)).astype(BF16)
            dup = (dhid * gelu).astype(BF16)
            hid_ref[0, e] = hid
            dga_ref[0, e] = dga
            dup_ref[0, e] = dup
            y = mm(hid, wd_ref[e])
            dgate = jnp.sum(y * dy, axis=-1, keepdims=True)
            stage_ref[slot, e] = (y * own_gate).astype(BF16).reshape(blocks, share, width)
            dlog = (dgate * own_gate * other_gate * pair).astype(BF16)
            dlog_ref[0, e] = dlog
            dx = mm(dga, wg_ref[e]) + mm(dup, wu_ref[e]) + mm(dlog, wr_ref[...])
            dx_ref[s, e] = dx.astype(BF16)

    @pl.when(step == 0)
    def _():
        barrier = pltpu.get_barrier_semaphore()
        for s in range(1, devices):
            pl.semaphore_signal(
                barrier, inc=1, device_id=(partner_of(me, s, devices), line),
                device_id_type=pl.DeviceIdType.MESH,
            )
        pl.semaphore_wait(barrier, devices - 1)
        for s in first_wave:
            x_copy(s).start()
        own = pltpu.make_async_copy(sent_ref.at[me], got_ref.at[0], own_sem)
        own.start()
        own.wait()

    @pl.when(step > 0)
    def _():
        x_copy(step).wait_recv()

    for index, wave in enumerate(later_waves):

        @pl.when(step == 2 + index)
        def _(wave=wave):
            for s in wave:
                x_copy(s).start()

    @pl.when(step > 1)
    def _():
        for copy in y_copies(step - 2):
            copy.wait()

    work(step)
    for copy in y_copies(step):
        copy.start()

    @pl.when(step > 0)
    def _():
        dx_copy(step).start()

    @pl.when(step == devices - 1)
    def _():
        own = pltpu.make_async_copy(dx_ref.at[0], back_ref.at[me], own_sem)
        own.start()
        own.wait()
        for copy in y_copies(devices - 2) + y_copies(devices - 1):
            copy.wait()
        for s in range(1, devices):
            x_copy(s).wait_send()
            dx_copy(s).wait_send()
            dx_copy(s).wait_recv()


def expert_pass(sent, dy, pair, wr, wg, wu, wd, by_block, identity):
    blocks, _, _, share, _ = dy.shape
    devices, experts, cap, width = sent.shape
    hidden = wg.shape[1]
    choices = wr.shape[0]

    def whole(shape):
        return pl.BlockSpec(shape, lambda s: (0,) * len(shape), pipeline_mode=pl.Buffered(1))

    def block(cols):
        return pl.BlockSpec((1, experts, cap, cols), lambda s: (s, 0, 0, 0))

    def kept(cols):
        return jax.ShapeDtypeStruct((devices, experts, cap, cols), BF16)

    y_shape = (blocks, devices, experts, share, width)
    if not by_block:
        y_shape = (devices, experts, blocks, share, width)
    return pl.pallas_call(
        functools.partial(expert_kernel, by_block),
        grid=(devices,),
        out_shape=(
            kept(width), jax.ShapeDtypeStruct(y_shape, BF16), kept(width), kept(width), kept(hidden), kept(hidden),
            kept(hidden), kept(choices),
        ),
        in_specs=[
            any_space(), whole(dy.shape), whole(pair.shape), whole(wr.shape), whole(wg.shape),
            whole(wu.shape), whole(wd.shape),
        ],
        out_specs=(
            any_space(), any_space(), block(width), block(width), block(hidden), block(hidden),
            block(hidden), block(choices),
        ),
        scratch_shapes=[
            pltpu.VMEM((devices, experts, cap, width), BF16),
            pltpu.VMEM((devices, experts, cap, width), BF16),
            pltpu.VMEM((2, experts, blocks, share, width), BF16),
            pltpu.SemaphoreType.DMA((devices,)),
            pltpu.SemaphoreType.DMA((devices,)),
            pltpu.SemaphoreType.DMA((devices,)),
            pltpu.SemaphoreType.DMA((devices,)),
            pltpu.SemaphoreType.DMA,
            pltpu.SemaphoreType.DMA((2, experts)),
        ],
        compiler_params=pltpu.CompilerParams(
            vmem_limit_bytes=VMEM_LIMIT, collective_id=identity, has_side_effects=True
        ),
        cost_estimate=pl.CostEstimate(flops=0, bytes_accessed=490000000, transcendentals=0),
        name="expert_pass",
    )(sent, dy, pair, wr, wg, wu, wd)


def weight_kernel(*refs):
    count = (len(refs) - 4) // 6
    dwr_ref, dwg_ref, dwu_ref, dwd_ref = refs[-4:]
    totals = [0.0, 0.0, 0.0, 0.0]
    for index in range(count):
        blocks = [
            ref[...].reshape(ref.shape[0] * ref.shape[2], ref.shape[3])
            for ref in refs[6 * index : 6 * index + 6]
        ]
        x, g, hid, dga, dup, dlog = blocks
        totals[0] = totals[0] + mm_tn(dlog, x)
        totals[1] = totals[1] + mm_tn(dga, x)
        totals[2] = totals[2] + mm_tn(dup, x)
        totals[3] = totals[3] + mm_tn(hid, g)
    dwr_ref[0] = totals[0]
    dwg_ref[0] = totals[1]
    dwu_ref[0] = totals[2]
    dwd_ref[0] = totals[3]


def weight_pass(kept):
    sources, experts, cap, width = kept[0][0].shape
    hidden = kept[0][2].shape[3]
    choices = kept[0][5].shape[3]
    rows = sources * cap
    block = 256 if width % 256 == 0 else width
    tokens = pl.BlockSpec((sources, 1, cap, block), lambda e, j: (0, e, 0, j))
    acts = pl.BlockSpec((sources, 1, cap, hidden), lambda e, j: (0, e, 0, 0))
    logs = pl.BlockSpec((sources, 1, cap, choices), lambda e, j: (0, e, 0, 0))
    operands = []
    for arrays in kept:
        operands.extend(arrays)
    return pl.pallas_call(
        weight_kernel,
        grid=(experts, width // block),
        out_shape=(
            jax.ShapeDtypeStruct((experts, choices, width), F32),
            jax.ShapeDtypeStruct((experts, hidden, width), F32),
            jax.ShapeDtypeStruct((experts, hidden, width), F32),
            jax.ShapeDtypeStruct((experts, hidden, width), F32),
        ),
        in_specs=[tokens, tokens, acts, acts, acts, logs] * len(kept),
        out_specs=(
            pl.BlockSpec((1, choices, block), lambda e, j: (e, 0, j)),
            pl.BlockSpec((1, hidden, block), lambda e, j: (e, 0, j)),
            pl.BlockSpec((1, hidden, block), lambda e, j: (e, 0, j)),
            pl.BlockSpec((1, hidden, block), lambda e, j: (e, 0, j)),
        ),
        compiler_params=pltpu.CompilerParams(vmem_limit_bytes=VMEM_LIMIT),
        cost_estimate=pl.CostEstimate(
            flops=6 * len(kept) * experts * rows * width * hidden,
            bytes_accessed=len(kept) * experts * rows * (4 * width + 6 * hidden)
            + 12 * experts * width * hidden,
            transcendentals=0,
        ),
        name="weight_pass",
    )(*operands)


def after(values, *others):
    return lax.optimization_barrier((values,) + others)[0]


def shards(
    x_in,
    cotangent,
    segment_ids,
    routes,
    qkv_weight,
    out_weight,
    bias_table,
    attn_gain,
    moe_gain,
    router_weight,
    gate_weight,
    up_weight,
    down_weight,
):
    micro_count, _, shard_len, width = x_in.shape
    slot_count = segment_ids.shape[2]
    head_cols = out_weight.shape[0]
    bucket_count, heads_here = bias_table.shape
    head_size = head_cols // heads_here
    expert_count = router_weight.shape[1]
    experts_here = gate_weight.shape[0]
    devices = expert_count // experts_here
    blocks = slot_count // shard_len
    members = blocks // 2
    half = slot_count // 2
    capacity = max(2, (10 * shard_len + 4 * expert_count - 1) // (4 * expert_count))
    scale = head_size ** (-0.5)
    hidden_index = lax.axis_index("hidden")
    expert_index = lax.axis_index("expert")
    part = hidden_index // members
    attn_gain_f = attn_gain.astype(F32).reshape(1, width)
    moe_gain_f = moe_gain.astype(F32).reshape(1, width)
    token_shape = (devices, experts_here, blocks * capacity, width)
    flat_shape = (devices, experts_here * blocks * capacity, width)
    place_shape = (expert_count, blocks, capacity, width)
    gate_rows = gate_weight.transpose(0, 2, 1)
    up_rows = up_weight.transpose(0, 2, 1)
    router_rows = router_weight.T

    def exchange(buffer):
        return lax.all_to_all(buffer, "expert", split_axis=0, concat_axis=0, tiled=True)

    def gather(values):
        return lax.all_gather(values, "hidden", axis=0, tiled=True)

    def scatter(values):
        return lax.psum_scatter(values, "hidden", scatter_dimension=0, tiled=True)

    states = [dict() for _ in range(micro_count)]
    own_seg = lax.dynamic_slice_in_dim(segment_ids[:, 0], hidden_index * shard_len, shard_len, 1)
    live_routes = jnp.where(own_seg[:, None, :] >= 0, routes[:, 0].transpose(0, 2, 1), -1)
    own_place = find_places(live_routes[None], expert_count, capacity)

    def spread(rows, placed):
        return spread_rows(rows, placed, expert_count, capacity, shard_len)

    dy_sent = [
        spread(cotangent[micro, 0], own_place[micro]).reshape(devices, -1, width)
        for micro in range(micro_count)
    ]
    dy_first = swap_rows(dy_sent[0], 7)
    *x_all, other_qkv, all_out, all_routes, other_table = opening(
        x_in[:, 0], qkv_weight.reshape(3 * width, head_cols), out_weight,
        after(live_routes, dy_first), bias_table.T.astype(F32), devices, blocks, members,
    )
    x_half = [x.reshape(1, half, width) for x in x_all]
    other_qkv = other_qkv.reshape(qkv_weight.shape)
    all_out = all_out.reshape(blocks, head_cols, width)

    own_routes = lax.dynamic_index_in_dim(all_routes, expert_index, 0, keepdims=False)
    place = find_places(own_routes, expert_count, capacity)

    tables = jnp.concatenate([bias_table.T.astype(F32), other_table], axis=0)
    onehot_bucket = bucket_onehot(half, bucket_count)
    bias = position_bias(jnp.einsum("jb,hb->hj", onehot_bucket, tables, precision=PRECISE))
    seg_half = lax.dynamic_slice_in_dim(segment_ids[:, 0], part * half, half, 1)

    def gather_dy(rows):
        whole = gather(rows.reshape(1, devices * experts_here * capacity, width))
        return whole.reshape(blocks, devices, experts_here, capacity, width)

    def experts(micro, kept, *behind):
        sent = spread(kept["xn2_all"], place[micro]).reshape(token_shape)
        kept["by_block"] = micro + 1 < micro_count
        back, kept["y"], x, g, hid, dga, dup, dlog = expert_pass(
            after(sent, *behind), kept["dy"], pairs[micro], router_rows, gate_rows, up_rows,
            down_weight, kept["by_block"], 4 + micro,
        )
        kept["weights"] = (x, g, hid, dga, dup, dlog)
        kept["back"] = back
        if micro > 0:
            back = after(back, states[micro - 1]["y_own"])
        kept["dx_back"] = back.reshape(place_shape)
        kept["dx_part"] = collect_rows(kept["dx_back"], place[micro], shard_len)
        kept["dxn2"] = scatter(kept["dx_part"])
        if kept["by_block"]:
            parts = after(kept["y"], kept["dx_part"]).reshape(blocks, -1, width)
            kept["y_own"] = scatter(parts).reshape(devices, -1, width)

    states[0]["dy"] = gather_dy(dy_first)
    behind = ()
    for micro in range(micro_count):
        state = states[micro]
        rider = None
        if micro + 1 < micro_count:
            rider = dy_sent[micro + 1]
        qkv, prob, heads, h1, xn2, *rode = attend(
            after(x_half[micro], *behind), attn_gain_f, qkv_weight, other_qkv, bias,
            seg_half[micro : micro + 1], all_out, x_in[micro], moe_gain_f, scale, members, 10 + micro,
            rider,
        )
        state.update(qkv=qkv[0], prob=prob[0], heads=heads[0], h1=h1[0], xn2=xn2[0])
        if micro + 1 < micro_count:
            states[micro + 1]["dy_here"] = rode[0]
        if micro == 0:
            pairs = find_pairs(after(all_routes, xn2), expert_count, experts_here, capacity)
            pairs = pairs.reshape(
                micro_count, devices, experts_here, blocks * capacity, expert_count
            )
            place = after(place, xn2)
            seg_half = seg_half + jnp.where(pairs[0, 0, 0, 0, 0] > 2, 1, 0)
        behind = (xn2, states[0]["dy"], place)
    behind = ()
    for micro in range(micro_count):
        state = states[micro]
        state["xn2_all"] = gather(after(state["xn2"], *behind))
        behind = (state["xn2_all"],)
    for micro in range(1, micro_count):
        states[micro]["dy"] = gather_dy(after(states[micro]["dy_here"], states[0]["xn2_all"]))
    behind = ()
    for micro in range(micro_count):
        experts(micro, states[micro], *behind)
        behind = (states[micro]["dx_part"],)
    last_part = states[-1]["dx_part"]
    kept = [state["weights"] for state in states]
    kept[-1] = tuple(after(list(kept[-1]), last_part))
    dwr, dwg, dwu, dwd = weight_pass(kept)
    last = states[-1]
    last["y_rows"] = exchange(after(last["y"], last_part).reshape(flat_shape)).reshape(place_shape)
    *x_grads, grads, lines, moe_gain_grad, attn_gain_grad = attend_back(
        moe_gain_f, attn_gain_f, all_out, qkv_weight, other_qkv,
        [
            (
                after(state["dxn2"], dwr), state["h1"], cotangent[micro, 0], x_in[micro, 0],
                x_half[micro][0], state["qkv"], state["prob"], state["heads"],
            )
            for micro, state in enumerate(states)
        ],
        scale, devices, members,
    )
    rows = collect_rows(after(last["y_rows"], grads), place[-1], shard_len)
    rows = rows.reshape(blocks, shard_len, width)
    for micro in range(micro_count - 1):
        state = states[micro]
        mixed = exchange(after(state["y_own"], grads)).reshape(expert_count, 1, capacity, width)
        mixed = collect_rows(mixed, own_place[micro], shard_len)
        state["block_out"] = (state["h1"] + mixed.astype(F32)).astype(BF16)

    lines = lines.reshape(2 * heads_here, 2 * half)
    table = jnp.einsum("hj,jb->hb", lines, onehot_bucket, precision=PRECISE)
    table = table.reshape(2, heads_here * bucket_count)
    mine = jnp.arange(blocks, dtype=jnp.int32)[:, None]
    table = jnp.where(mine == hidden_index, table[0], 0.0) + jnp.where(
        mine == (hidden_index + members) % blocks, table[1], 0.0
    )
    small = jnp.concatenate(
        [
            jnp.sum(dwr, axis=0).reshape(-1),
            attn_gain_grad.reshape(-1),
            moe_gain_grad.reshape(-1),
            table.reshape(-1),
        ]
    )
    used = small.shape[0]
    small = jnp.pad(small, (0, -used % 1024)).reshape(-1, 128)
    whole, small, last["block_out"] = closing(grads, small, rows, last["h1"])
    whole = whole.reshape(4 * width, head_cols).astype(F32)
    grad_qkv = whole[: 3 * width].reshape(qkv_weight.shape)
    grad_out = whole[3 * width :].T
    small = small.reshape(-1)
    sizes = (width * expert_count, width, width)
    grad_router = small[: sizes[0]].reshape(expert_count, width).T
    grad_attn_gain = small[sizes[0] : sizes[0] + width]
    grad_moe_gain = small[sizes[0] + width : sizes[0] + 2 * width]
    table = small[sizes[0] + 2 * width : used].reshape(blocks, heads_here, bucket_count)
    grad_table = lax.dynamic_index_in_dim(table, hidden_index, 0, keepdims=False).T
    return (
        jnp.stack([state["block_out"] for state in states])[:, None],
        jnp.stack(x_grads)[:, None],
        grad_qkv,
        grad_out,
        grad_table,
        grad_attn_gain,
        grad_moe_gain,
        grad_router,
        dwg.transpose(0, 2, 1),
        dwu.transpose(0, 2, 1),
        dwd,
    )


def solution(mesh):
    return jax.shard_map(
        shards,
        mesh=mesh,
        in_specs=(
            P(None, "expert", "hidden", None),
            P(None, "expert", "hidden", None),
            P(None, "expert", None),
            P(None, "expert", "hidden", None),
            P(None, None, "hidden"),
            P("hidden", None),
            P(None, "hidden"),
            P(),
            P(),
            P(),
            P("expert", None, "hidden"),
            P("expert", None, "hidden"),
            P("expert", "hidden", None),
        ),
        out_specs=(
            P(None, "expert", "hidden", None),
            P(None, "expert", "hidden", None),
            P(None, None, "hidden"),
            P("hidden", None),
            P(None, "hidden"),
            P(),
            P(),
            P(),
            P("expert", None, "hidden"),
            P("expert", None, "hidden"),
            P("expert", "hidden", None),
        ),
        check_vma=False,
    )
```

```python
import functools

import jax
import jax.numpy as jnp
from jax import lax
from jax.experimental import pallas as pl
from jax.experimental.pallas import tpu as pltpu
from jax.sharding import PartitionSpec as P

EPSILON = 1e-06
PRECISE = lax.Precision.HIGHEST
LIMITS = (12, 16, 23, 32, 46, 64, 91)
MASKED = -1000000000.0
GELU_C = 0.7978845608028654
GELU_A = 0.044715
VMEM_LIMIT = 60 * 1024 * 1024
F32 = jnp.float32
BF16 = jnp.bfloat16


def mm(a, b):
    return lax.dot_general(a, b, (((1,), (0,)), ((), ())), preferred_element_type=F32)


def mm_nt(a, b):
    return lax.dot_general(a, b, (((1,), (1,)), ((), ())), preferred_element_type=F32)


def mm_tn(a, b):
    return lax.dot_general(a, b, (((0,), (0,)), ((), ())), preferred_element_type=F32)


def bucket_of(distance):
    magnitude = jnp.abs(distance)
    far_bucket = jnp.full(magnitude.shape, 8, jnp.int32)
    for threshold in LIMITS:
        far_bucket = far_bucket + (magnitude >= threshold).astype(jnp.int32)
    return jnp.where(magnitude < 8, magnitude, far_bucket) + 16 * (distance > 0).astype(jnp.int32)


def bucket_onehot(half, bucket_count):
    lane = jnp.arange(2 * half, dtype=jnp.int32)
    distance = jnp.where(lane < half, lane, lane - 2 * half)
    return (
        bucket_of(distance)[:, None] == jnp.arange(bucket_count, dtype=jnp.int32)[None, :]
    ).astype(F32)


TILE = 128


def bias_kernel(line_ref, out_ref):
    length = out_ref.shape[2]
    line = jnp.broadcast_to(line_ref[0], (8, length))
    row = lax.broadcasted_iota(jnp.int32, (8, length), 0)
    sheet = line
    for r in range(1, 8):
        sheet = jnp.where(row == r, pltpu.roll(line, r, 1), sheet)
    while sheet.shape[0] < TILE:
        sheet = jnp.concatenate([sheet, pltpu.roll(sheet, sheet.shape[0], 1)], axis=0)
    out_ref[0] = sheet.astype(out_ref.dtype)


def position_bias(line):
    heads, length = line.shape
    return pl.pallas_call(
        bias_kernel,
        grid=(heads,),
        out_shape=jax.ShapeDtypeStruct((heads, TILE, length), BF16),
        in_specs=[pl.BlockSpec((1, 1, length), lambda h: (h, 0, 0))],
        out_specs=pl.BlockSpec((1, TILE, length), lambda h: (h, 0, 0)),
        compiler_params=pltpu.CompilerParams(vmem_limit_bytes=VMEM_LIMIT),
        name="position_bias",
    )(line.reshape(heads, 1, length))


def unit_rows(x):
    x = x.astype(F32)
    return x * lax.rsqrt(jnp.mean(x * x, axis=-1, keepdims=True) + EPSILON)


def remote(src, dst, send_sem, recv_sem, device):
    return pltpu.make_async_remote_copy(
        src_ref=src, dst_ref=dst, send_sem=send_sem, recv_sem=recv_sem,
        device_id=device, device_id_type=pl.DeviceIdType.MESH,
    )


def greet(devices):
    barrier = pltpu.get_barrier_semaphore()
    for device in devices:
        pl.semaphore_signal(
            barrier, inc=1, device_id=device, device_id_type=pl.DeviceIdType.MESH
        )
    pl.semaphore_wait(barrier, len(devices))


def bits_of(count):
    return [1 << b for b in range(count.bit_length() - 1)]


def partner_of(me, step, count):
    found = 0
    for bit in bits_of(count):
        found = found + bit * lax.rem(me // bit + step // bit, 2)
    return found


def any_space():
    return pl.BlockSpec(memory_space=pl.ANY)


def opening_kernel(
    micros, x_ref, qkv_ref, out_ref, routes_ref, table_ref, dy_ref, *refs,
):
    x_all, refs = refs[:micros], refs[micros:]
    (
        qkv_all, out_all, routes_all, table_all, dy_all,
        x_send, x_recv, qkv_send, qkv_recv, out_send, out_recv, qkv_on_send, qkv_on_recv,
        out_on_send, out_on_recv, routes_send, routes_recv, routes_on_send, routes_on_recv,
        table_send, table_recv, dy_send, dy_recv, own_sem,
    ) = refs
    devices, qkv_rows = qkv_all.shape[0] * 2, qkv_all.shape[2]
    blocks, out_rows = out_all.shape[0], out_all.shape[3]
    members = x_all[0].shape[0]
    me = lax.axis_index("expert")
    line = lax.axis_index("hidden")
    chip, core = me // 2, lax.rem(me, 2)
    mine = lax.rem(line, members)
    base = line - mine
    along = [lax.rem(line + s, blocks) for s in range(1, blocks)]
    across = lax.rem(line + members, blocks)
    sibling = partner_of(me, 1, devices)
    greet([(partner_of(me, s, devices), line) for s in range(1, devices)] + [(me, z) for z in along])
    own = [
        pltpu.make_async_copy(
            out_ref.at[pl.ds(me * out_rows, out_rows)], out_all.at[line, chip, core], own_sem.at[0]
        ),
        pltpu.make_async_copy(routes_ref, routes_all.at[me, line], own_sem.at[1]),
        pltpu.make_async_copy(dy_ref.at[me], dy_all.at[me], own_sem.at[2]),
    ]
    for micro in range(micros):
        own.append(
            pltpu.make_async_copy(x_ref.at[micro], x_all[micro].at[mine], own_sem.at[3 + micro])
        )
    for copy in own:
        copy.start()
    first_qkv = remote(
        qkv_ref.at[pl.ds(me * qkv_rows, qkv_rows)], qkv_all.at[chip, core], qkv_send, qkv_recv,
        (me, across),
    )
    first_qkv.start()
    first_out, first_routes = [], []
    rest = [remote(table_ref, table_all, table_send, table_recv, (me, across))]
    for s, z in enumerate(along):
        first_out.append(
            remote(
                out_ref.at[pl.ds(me * out_rows, out_rows)], out_all.at[line, chip, core],
                out_send.at[s], out_recv.at[s], (me, z),
            )
        )
        first_routes.append(
            remote(
                routes_ref, routes_all.at[me, line], routes_send.at[s], routes_recv.at[s], (me, z)
            )
        )
    for copy in first_routes + first_out + rest:
        copy.start()
    for micro in range(micros):
        for s in range(1, members):
            peer = base + lax.rem(mine + s, members)
            copy = remote(
                x_ref.at[micro], x_all[micro].at[mine], x_send.at[micro, s], x_recv.at[micro, s],
                (me, peer),
            )
            copy.start()
            rest.append(copy)
    for s in range(1, devices):
        peer = partner_of(me, s, devices)
        copy = remote(dy_ref.at[peer], dy_all.at[me], dy_send.at[s], dy_recv.at[s], (peer, line))
        copy.start()
        rest.append(copy)
    first_qkv.wait_recv()
    qkv_on, out_on = [], []
    for s in range(2, devices, 2):
        copy = remote(
            qkv_all.at[chip, core], qkv_all.at[chip, core], qkv_on_send.at[s], qkv_on_recv.at[s],
            (partner_of(me, s, devices), line),
        )
        copy.start()
        qkv_on.append(copy)
    own[1].wait()
    for copy in first_routes:
        copy.wait_recv()
    for s in range(1, devices):
        copy = remote(
            routes_all.at[me], routes_all.at[me], routes_on_send.at[s], routes_on_recv.at[s],
            (partner_of(me, s, devices), line),
        )
        copy.start()
        rest.append(copy)
    own[0].wait()
    for copy in first_out:
        copy.wait_recv()
    for s in range(2, devices, 2):
        copy = remote(
            out_all.at[:, chip, core], out_all.at[:, chip, core], out_on_send.at[s],
            out_on_recv.at[s], (partner_of(me, s, devices), line),
        )
        copy.start()
        out_on.append(copy)
    for copy in qkv_on:
        copy.wait_recv()
    copy = remote(
        qkv_all.at[:, core], qkv_all.at[:, core], qkv_on_send.at[1], qkv_on_recv.at[1],
        (sibling, line),
    )
    copy.start()
    rest.append(copy)
    for copy in out_on:
        copy.wait_recv()
    copy = remote(
        out_all.at[:, :, core], out_all.at[:, :, core], out_on_send.at[1], out_on_recv.at[1],
        (sibling, line),
    )
    copy.start()
    rest.append(copy)
    for copy in own[2:]:
        copy.wait()
    first_qkv.wait_send()
    for copy in first_out + first_routes + qkv_on + out_on:
        copy.wait_send()
    for copy in rest:
        copy.wait()


def opening(x, qkv, out, routes, table, dy, devices, blocks, members):
    micros, shard_len, width = x.shape
    dma = pltpu.SemaphoreType.DMA
    pair = (devices // 2, 2)
    return pl.pallas_call(
        functools.partial(opening_kernel, micros),
        out_shape=(jax.ShapeDtypeStruct((members, shard_len, width), BF16),) * micros
        + (
            jax.ShapeDtypeStruct(pair + (qkv.shape[0] // devices, qkv.shape[1]), BF16),
            jax.ShapeDtypeStruct((blocks,) + pair + (out.shape[0] // devices, width), BF16),
            jax.ShapeDtypeStruct((devices, blocks) + routes.shape, jnp.int32),
            jax.ShapeDtypeStruct(table.shape, table.dtype),
            jax.ShapeDtypeStruct(dy.shape, BF16),
        ),
        in_specs=[any_space()] * 6,
        out_specs=(any_space(),) * (5 + micros),
        scratch_shapes=[
            dma((micros, members)), dma((micros, members)), dma, dma, dma((blocks,)), dma((blocks,)),
            dma((devices,)), dma((devices,)), dma((devices,)), dma((devices,)), dma((blocks,)),
            dma((blocks,)), dma((devices,)), dma((devices,)), dma, dma, dma((devices,)),
            dma((devices,)), dma((3 + micros,)),
        ],
        compiler_params=pltpu.CompilerParams(collective_id=1, has_side_effects=True),
        cost_estimate=pl.CostEstimate(flops=0, bytes_accessed=200000000, transcendentals=0),
        name="opening",
    )(x, qkv, out, routes, table, dy)


def unit_rows(x):
    x = x.astype(F32)
    return x * lax.rsqrt(jnp.mean(x * x, axis=-1, keepdims=True) + EPSILON)


def attend_kernel(
    scale, x_ref, gain_ref, own_ref, other_ref, bias_ref, seg_row_ref, seg_col_ref,
    out_ref, x_own_ref, moe_gain_ref, *refs,
):
    riding = len(refs) > 10
    if riding:
        sent_ref, next_ref, arrived_ref, next_all = *refs[:2], *refs[7:9]
        ride_send, ride_recv, next_send, next_recv, ride_own = refs[-5:]
        refs = refs[2:7] + refs[9:-5]
    qkv_ref, prob_ref, heads_ref, h1_ref, xn2_ref, xn_ref, part_ref, got_ref, send_sem, recv_sem = refs
    micros, members, shard_len, both = got_ref.shape
    cols = both // 2
    heads, length = bias_ref.shape[0], bias_ref.shape[2]
    half = members * shard_len
    size = cols // heads
    micro, group = pl.program_id(0), pl.program_id(1)
    me = lax.axis_index("expert")
    line = lax.axis_index("hidden")
    mine = lax.rem(line, members)
    part = line // members
    base = line - mine

    def swap(m, s):
        peer = lax.rem(mine + s, members)
        return remote(
            part_ref.at[m, peer], got_ref.at[m, mine], send_sem.at[m, s], recv_sem.at[m, s],
            (me, base + peer),
        )

    def ride(s):
        peer = partner_of(me, s, sent_ref.shape[0])
        return remote(
            sent_ref.at[peer], arrived_ref.at[me], ride_send.at[s], ride_recv.at[s], (peer, line)
        )

    def stay():
        return [
            pltpu.make_async_copy(sent_ref.at[me], arrived_ref.at[me], ride_own.at[0]),
            pltpu.make_async_copy(next_ref, next_all.at[mine], ride_own.at[1]),
        ]

    def pair(s):
        peer = lax.rem(mine + s, members)
        return remote(
            next_ref, next_all.at[mine], next_send.at[s], next_recv.at[s], (me, base + peer)
        )

    @pl.when((micro == 0) & (group == 0))
    def _():
        peers = [(me, base + lax.rem(mine + s, members)) for s in range(1, members)]
        if riding:
            devices = sent_ref.shape[0]
            peers += [(partner_of(me, s, devices), line) for s in range(1, devices)]
        greet(peers)
        if riding:
            for copy in stay():
                copy.start()
            for s in range(1, devices):
                ride(s).start()

    @pl.when(group == 0)
    def _():
        xn_ref[...] = (unit_rows(x_ref[0]) * gain_ref[...]).astype(BF16)
        for t in range(3):
            qkv_ref[0, 0, t] = mm(xn_ref[...], own_ref[t]).astype(BF16)

    @pl.when(group > 0)
    def _():
        for t in range(3):
            qkv_ref[0, 0, t] = mm(xn_ref[...], other_ref[t]).astype(BF16)

    seg_row = seg_row_ref[0]
    for head in range(heads):
        inner = slice(head * size, (head + 1) * size)
        keys = qkv_ref[0, 0, 1, :, inner]
        values = qkv_ref[0, 0, 2, :, inner]
        for start in range(0, half, TILE):
            rows = slice(start, start + TILE)
            scores = mm_nt(qkv_ref[0, 0, 0, rows, inner], keys) * scale
            shift = bias_ref[head, :, : half - start]
            if start:
                shift = jnp.concatenate([bias_ref[head, :, length - start :], shift], axis=1)
            scores = scores + shift.astype(F32)
            scores = jnp.where(seg_col_ref[0, rows, :] == seg_row, scores, MASKED)
            top = jnp.max(scores, axis=-1, keepdims=True)
            weights = jnp.exp(scores - top)
            inverse = 1.0 / jnp.sum(weights, axis=-1, keepdims=True)
            prob = (weights * inverse).astype(BF16)
            prob_ref[0, 0, head, rows, :] = prob
            heads_ref[0, rows, inner] = mm(prob, values).astype(BF16)

    for g in range(2):

        @pl.when(group == g)
        def _(g=g):
            for member in range(members):
                rows = slice(member * shard_len, (member + 1) * shard_len)
                part_ref[micro, member, :, g * cols : (g + 1) * cols] = heads_ref[0, rows, :]

    @pl.when(group == 1)
    def _():
        got_ref[micro, mine] = part_ref[micro, mine]
        for s in range(1, members):
            swap(micro, s).start()
            if riding:
                pair(s).start()

    @pl.when((micro == micros - 1) & (group == 1))
    def _():
        for m in range(micros):
            for s in range(1, members):
                swap(m, s).wait_recv()
            h1 = x_own_ref[m].astype(F32)
            for member in range(members):
                for j in range(2):
                    index = lax.rem(part + j, 2) * members + member
                    h1 = h1 + mm(got_ref[m, member, :, j * cols : (j + 1) * cols], out_ref[index])
            h1_ref[m] = h1
            xn2_ref[m] = (unit_rows(h1) * moe_gain_ref[...]).astype(BF16)
        for m in range(micros):
            for s in range(1, members):
                swap(m, s).wait_send()
        if riding:
            for copy in stay():
                copy.wait()
            for s in range(1, members):
                pair(s).wait()
            for s in range(1, sent_ref.shape[0]):
                ride(s).wait()


def attend(
    x, gain, own_weight, other_weight, bias, seg, out_weight, x_own, moe_gain, scale, members, identity,
    rider=None,
):
    micros, half, width = x.shape
    cols = own_weight.shape[2]
    heads = bias.shape[0] // 2
    shard_len = half // members
    riders, ride_shapes, ride_sems = [], (), []
    if rider is not None:
        riders = list(rider)
        ride_shapes = (rider[0].shape, (members, shard_len, width))
        ride_sems = [pltpu.SemaphoreType.DMA((rider[0].shape[0],))] * 2
        ride_sems += [pltpu.SemaphoreType.DMA((members,))] * 2 + [pltpu.SemaphoreType.DMA((2,))]

    def once(shape):
        return pl.BlockSpec(shape, lambda m, p: (0,) * len(shape), pipeline_mode=pl.Buffered(1))

    return pl.pallas_call(
        functools.partial(attend_kernel, scale),
        grid=(micros, 2),
        out_shape=(
            jax.ShapeDtypeStruct((micros, 2, 3, half, cols), BF16),
            jax.ShapeDtypeStruct((micros, 2, heads, half, half), BF16),
            jax.ShapeDtypeStruct((micros, half, 2 * cols), BF16),
            jax.ShapeDtypeStruct((micros, shard_len, width), F32),
            jax.ShapeDtypeStruct((micros, shard_len, width), BF16),
        )
        + tuple(jax.ShapeDtypeStruct(shape, BF16) for shape in ride_shapes),
        in_specs=[
            pl.BlockSpec((1, half, width), lambda m, p: (m, 0, 0)),
            once((1, width)),
            once((3, width, cols)),
            once((3, width, cols)),
            pl.BlockSpec((heads,) + bias.shape[1:], lambda m, p: (p, 0, 0)),
            pl.BlockSpec((1, 1, half), lambda m, p: (m, 0, 0)),
            pl.BlockSpec((1, half, 1), lambda m, p: (m, 0, 0)),
            once(out_weight.shape),
            once(x_own.shape),
            once((1, width)),
        ]
        + [any_space()] * len(riders),
        out_specs=(
            pl.BlockSpec((1, 1, 3, half, cols), lambda m, p: (m, p, 0, 0, 0)),
            pl.BlockSpec((1, 1, heads, half, half), lambda m, p: (m, p, 0, 0, 0)),
            pl.BlockSpec((1, half, cols), lambda m, p: (m, 0, p)),
            pl.BlockSpec((micros, shard_len, width), lambda m, p: (0, 0, 0)),
            pl.BlockSpec((micros, shard_len, width), lambda m, p: (0, 0, 0)),
        )
        + (any_space(),) * len(riders),
        scratch_shapes=[
            pltpu.VMEM((half, width), BF16),
            pltpu.VMEM((micros, members, shard_len, 2 * cols), BF16),
            pltpu.VMEM((micros, members, shard_len, 2 * cols), BF16),
            pltpu.SemaphoreType.DMA((micros, members)),
            pltpu.SemaphoreType.DMA((micros, members)),
        ]
        + ride_sems,
        compiler_params=pltpu.CompilerParams(
            vmem_limit_bytes=VMEM_LIMIT, collective_id=identity, has_side_effects=True
        ),
        cost_estimate=pl.CostEstimate(
            flops=micros * 2 * half * cols * (8 * width + 4 * half),
            bytes_accessed=100000000,
            transcendentals=micros * 2 * heads * half * half,
        ),
        name="attend",
    )(
        x, gain, own_weight, other_weight, bias, seg.reshape(micros, 1, half),
        seg.reshape(micros, half, 1), out_weight, x_own, moe_gain, *riders,
    )


def back_kernel(scale, micros, *refs):
    moe_gain_ref, gain_ref, out_ref, own_ref, other_ref = refs[:5]
    inputs = [refs[5 + 8 * m : 13 + 8 * m] for m in range(micros)]
    refs = refs[5 + 8 * micros :]
    xgrads, refs = refs[:micros], refs[micros:]
    (
        grads_ref, line_ref, dmoe_ref, dgain_ref,
        dh1_ref, dattn_all, dheads_part, dheads_all, dxn_part, dxn_got, total_ref, xn_ref, ds_ref,
        dproj_ref, sheet_ref, attn_send, attn_recv, heads_send, heads_recv, dxn_send, dxn_recv,
    ) = refs
    _, members, shard_len, width = dattn_all.shape
    cols = dproj_ref.shape[2]
    half = members * shard_len
    length = sheet_ref.shape[1]
    group, micro = pl.program_id(0), pl.program_id(1)
    me = lax.axis_index("expert")
    line = lax.axis_index("hidden")
    mine = lax.rem(line, members)
    part = line // members
    base = line - mine
    steps = range(1, members)

    def peer_of(s):
        return lax.rem(mine + s, members)

    def attn_copy(m, s):
        return remote(
            dattn_all.at[m, mine], dattn_all.at[m, mine], attn_send.at[m, s], attn_recv.at[m, s],
            (me, base + peer_of(s)),
        )

    def heads_copy(m, s):
        return remote(
            dheads_part.at[m, peer_of(s)], dheads_all.at[m, mine], heads_send.at[m, s],
            heads_recv.at[m, s], (me, base + peer_of(s)),
        )

    def dxn_copy(m, s):
        return remote(
            dxn_part.at[m, peer_of(s)], dxn_got.at[m, mine], dxn_send.at[m, s], dxn_recv.at[m, s],
            (me, base + peer_of(s)),
        )

    @pl.when((group == 0) & (micro == 0))
    def _():
        greet([(me, base + peer_of(s)) for s in steps])
        dmoe_ref[...] = jnp.zeros_like(dmoe_ref)
        dgain_ref[...] = jnp.zeros_like(dgain_ref)
        for m in range(micros):
            grad_ref, h1_ref, dy_ref = inputs[m][:3]
            grad = grad_ref[...].astype(F32)
            h1 = h1_ref[...]
            r2 = lax.rsqrt(jnp.mean(h1 * h1, axis=-1, keepdims=True) + EPSILON)
            unit = h1 * r2
            dmoe_ref[...] += jnp.sum(grad * unit, axis=0, keepdims=True)
            weighted = grad * moe_gain_ref[...]
            inner = jnp.mean(weighted * unit, axis=-1, keepdims=True)
            dh1 = dy_ref[...].astype(F32) + r2 * (weighted - unit * inner)
            dh1_ref[m] = dh1
            dattn = dh1.astype(BF16)
            dattn_all[m, mine] = dattn
            for member in range(members):
                for j in range(2):
                    index = lax.rem(part + j, 2) * members + member
                    dheads = mm_nt(dattn, out_ref[index]).astype(BF16)
                    dheads_part[m, member, :, j * cols : (j + 1) * cols] = dheads
            for s in steps:
                heads_copy(m, s).start()
            dheads_all[m, mine] = dheads_part[m, mine]
        for m in range(micros):
            xn_ref[m] = (unit_rows(inputs[m][4][...]) * gain_ref[...]).astype(BF16)

    def products(weight_ref):
        dxn = mm_nt(dproj_ref[0], weight_ref[0])
        for t in range(1, 3):
            dxn = dxn + mm_nt(dproj_ref[t], weight_ref[t])
        return dxn.reshape(members, shard_len, width)

    per = grads_ref.shape[0] // 4
    for g in range(2):
        for m in range(micros):

            @pl.when((group == g) & (micro == m))
            def _(g=g, m=m):
                x_ref, qkv_ref, prob_ref, heads_ref = inputs[m][4:]
                heads = prob_ref.shape[1]
                size = cols // heads
                if g == 0:
                    for s in steps:
                        heads_copy(m, s).wait_recv()
                    for s in steps:
                        attn_copy(m, s).start()
                for head in range(heads):
                    inner_cols = slice(head * size, (head + 1) * size)
                    outer_cols = slice(g * cols + head * size, g * cols + (head + 1) * size)
                    values = qkv_ref[0, 2, :, inner_cols]
                    grads = dheads_all[m, :, :, outer_cols].reshape(half, size)
                    sheet_ref[...] = jnp.zeros_like(sheet_ref)
                    for start in range(0, half, TILE):
                        rows = slice(start, start + TILE)
                        prob = prob_ref[0, head, rows, :].astype(F32)
                        dprob = mm_nt(grads[rows], values)
                        inner = jnp.sum(prob * dprob, axis=-1, keepdims=True)
                        dscore = (prob * (dprob - inner)).astype(BF16)
                        ds_ref[rows, :] = dscore
                        dscore = dscore.astype(F32)
                        sheet_ref[:, : half - start] += dscore[:, start:]
                        if start:
                            sheet_ref[:, length - start :] += dscore[:, :start]
                    dscores = ds_ref[...]
                    keys, queries = qkv_ref[0, 1, :, inner_cols], qkv_ref[0, 0, :, inner_cols]
                    dproj_ref[0, :, inner_cols] = (mm(dscores, keys) * scale).astype(BF16)
                    dproj_ref[1, :, inner_cols] = (mm_tn(dscores, queries) * scale).astype(BF16)
                    dproj_ref[2, :, inner_cols] = mm_tn(prob_ref[0, head], grads).astype(BF16)
                    sheet = sheet_ref[...]
                    while sheet.shape[0] > 8:
                        upper = sheet.shape[0] // 2
                        sheet = sheet[:upper] + pltpu.roll(sheet[upper:], length - upper, 1)
                    row = lax.broadcasted_iota(jnp.int32, (8, length), 0)
                    found = jnp.zeros((1, length), F32)
                    for r in range(8):
                        moved = pltpu.roll(sheet, length - r, 1) if r else sheet
                        found = found + jnp.sum(
                            jnp.where(row == r, moved, 0.0), axis=0, keepdims=True
                        )
                    if m:
                        found = found + line_ref[0, head : head + 1, :]
                    line_ref[0, head : head + 1, :] = found
                if g == 0:
                    total_ref[m] = products(own_ref)
                    for s in steps:
                        attn_copy(m, s).wait_recv()
                else:
                    total = total_ref[m] + products(other_ref)
                    total_ref[m] = total
                    dxn_part[m] = total.astype(BF16)
                    for s in steps:
                        dxn_copy(m, s).start()
                    total = total.reshape(half, width)
                    dgain_ref[...] += jnp.sum(total * unit_rows(x_ref[...]), axis=0, keepdims=True)
                for t in range(4):
                    if t < 3:
                        found = mm_tn(xn_ref[m], dproj_ref[t])
                    else:
                        found = mm_tn(dattn_all[m].reshape(half, width), heads_ref[...])
                    found = found.reshape(per, 1, width // per, cols)
                    if m:
                        found = found + grads_ref[t * per : (t + 1) * per].astype(F32)
                    grads_ref[t * per : (t + 1) * per] = found.astype(BF16)

    @pl.when((group == 1) & (micro == micros - 1))
    def _():
        for m in range(micros):
            x_own = inputs[m][3][...].astype(F32)
            r1 = lax.rsqrt(jnp.mean(x_own * x_own, axis=-1, keepdims=True) + EPSILON)
            unit = x_own * r1
            for s in steps:
                dxn_copy(m, s).wait_recv()
            dxn1 = total_ref[m, mine]
            for s in steps:
                dxn1 = dxn1 + dxn_got[m, lax.rem(mine + members - s, members)].astype(F32)
            weighted = dxn1 * gain_ref[...]
            inner = jnp.mean(weighted * unit, axis=-1, keepdims=True)
            xgrads[m][...] = (dh1_ref[m] + r1 * (weighted - unit * inner)).astype(BF16)
        for m in range(micros):
            for s in steps:
                heads_copy(m, s).wait_send()
                attn_copy(m, s).wait_send()
                dxn_copy(m, s).wait_send()


def attend_back(moe_gain, gain, out_weight, own_weight, other_weight, kept, scale, pieces, members):
    micros = len(kept)
    _, heads, half = kept[0][6].shape[:3]
    width, cols = own_weight.shape[1:]
    shard_len = half // members
    length = 2 * half
    rows = 4 * width // pieces

    def once(array):
        return pl.BlockSpec(
            array.shape, lambda p, m: (0,) * array.ndim, pipeline_mode=pl.Buffered(1)
        )

    operands = [moe_gain, gain, out_weight, own_weight, other_weight]
    in_specs = [once(array) for array in operands]
    for arrays in kept:
        operands.extend(arrays)
        in_specs += [once(array) for array in arrays[:5]] + [
            pl.BlockSpec((1, 3, half, cols), lambda p, m: (p, 0, 0, 0)),
            pl.BlockSpec((1, heads, half, half), lambda p, m: (p, 0, 0, 0)),
            pl.BlockSpec((half, cols), lambda p, m: (0, p)),
        ]
    dma = pltpu.SemaphoreType.DMA((micros, members))
    return pl.pallas_call(
        functools.partial(back_kernel, scale, micros),
        grid=(2, micros),
        out_shape=(jax.ShapeDtypeStruct((shard_len, width), BF16),) * micros
        + (
            jax.ShapeDtypeStruct((pieces, 2, rows, cols), BF16),
            jax.ShapeDtypeStruct((2, heads, length), F32),
            jax.ShapeDtypeStruct((1, width), F32),
            jax.ShapeDtypeStruct((1, width), F32),
        ),
        in_specs=in_specs,
        out_specs=(pl.BlockSpec((shard_len, width), lambda p, m: (0, 0)),) * micros
        + (
            pl.BlockSpec((pieces, 1, rows, cols), lambda p, m: (0, p, 0, 0)),
            pl.BlockSpec((1, heads, length), lambda p, m: (p, 0, 0)),
            pl.BlockSpec((1, width), lambda p, m: (0, 0)),
            pl.BlockSpec((1, width), lambda p, m: (0, 0)),
        ),
        scratch_shapes=[
            pltpu.VMEM((micros, shard_len, width), F32),
            pltpu.VMEM((micros, members, shard_len, width), BF16),
            pltpu.VMEM((micros, members, shard_len, 2 * cols), BF16),
            pltpu.VMEM((micros, members, shard_len, 2 * cols), BF16),
            pltpu.VMEM((micros, members, shard_len, width), BF16),
            pltpu.VMEM((micros, members, shard_len, width), BF16),
            pltpu.VMEM((micros, members, shard_len, width), F32),
            pltpu.VMEM((micros, half, width), BF16),
            pltpu.VMEM((half, half), BF16),
            pltpu.VMEM((3, half, cols), BF16),
            pltpu.VMEM((TILE, length), F32),
            dma, dma, dma, dma, dma, dma,
        ],
        compiler_params=pltpu.CompilerParams(
            vmem_limit_bytes=VMEM_LIMIT, collective_id=6, has_side_effects=True
        ),
        cost_estimate=pl.CostEstimate(
            flops=2 * micros * half * cols * (16 * width + 8 * half),
            bytes_accessed=250000000,
            transcendentals=0,
        ),
        name="attend_back",
    )(*operands)


def closing_kernel(
    pieces_ref, small_ref, y_ref, h1_ref, whole_ref, sum_ref, block_ref,
    y_got, y_send, y_recv, half_got, held_ref, quarter_got, total_ref, moved_ref, moved_got, small_got, line_sum,
    line_got, half_sem, quarter_send, quarter_recv, small_send, small_recv, line_send, line_recv,
    moved_sem, on_send, on_recv, own_sem,
):
    chips = pieces_ref.shape[0]
    devices = 2 * chips
    blocks = line_got.shape[0]
    me = lax.axis_index("expert")
    line = lax.axis_index("hidden")
    chip, core = me // 2, lax.rem(me, 2)
    sibling = partner_of(me, 1, devices)
    along = [lax.rem(line + s, blocks) for s in range(1, blocks)]
    across = lax.rem(line + blocks // 2, blocks)
    greet([(partner_of(me, s, devices), line) for s in range(1, devices)] + [(me, z) for z in along])
    share = y_ref.shape[1] // 2

    def y_copies(turn):
        rows = pl.ds(turn * share, share)
        return [
            remote(
                y_ref.at[z, rows], y_got.at[line, rows], y_send.at[turn, s], y_recv.at[turn, s],
                (me, z),
            )
            for s, z in enumerate(along)
        ]

    halves = remote(
        pieces_ref.at[:, 1 - core], half_got, half_sem.at[0], half_sem.at[1], (sibling, line)
    )
    halves.start()
    for copy in y_copies(0):
        copy.start()
    smalls = [
        remote(
            small_ref, small_got.at[me], small_send.at[s], small_recv.at[s],
            (partner_of(me, s, devices), line),
        )
        for s in range(1, devices)
    ]
    for copy in smalls:
        copy.start()
    small_got[me] = small_ref[...]
    halves.wait_recv()
    steps = range(1, chips)

    def quarter(s):
        other = partner_of(chip, s, chips)
        return remote(
            held_ref.at[other], quarter_got.at[s], quarter_send.at[s], quarter_recv.at[s],
            (partner_of(me, 2 * s, devices), line),
        )

    for s in steps:
        other = partner_of(chip, s, chips)
        held = pieces_ref[other, core].astype(F32) + half_got[other].astype(F32)
        held_ref[other] = held.astype(BF16)
        quarter(s).start()
    total_ref[...] = pieces_ref[chip, core].astype(F32) + half_got[chip].astype(F32)
    for copy in smalls:
        copy.wait_recv()
    line_sum[...] = jnp.sum(small_got[...], axis=0)
    lines = [
        remote(line_sum, line_got.at[line], line_send.at[s], line_recv.at[s], (me, z))
        for s, z in enumerate(along)
    ]
    for copy in lines:
        copy.start()
    line_got[line] = line_sum[...]
    for s in steps:
        quarter(s).wait_recv()
        total_ref[...] += quarter_got[s].astype(F32)
    moved_ref[...] = total_ref[1].astype(BF16)
    cross = remote(moved_ref, moved_got, moved_sem.at[0], moved_sem.at[1], (me, across))
    cross.start()
    cross.wait_recv()
    for copy in y_copies(1):
        copy.start()
    whole_ref[chip, core] = (total_ref[0] + moved_got[...].astype(F32)).astype(BF16)
    onward = [
        remote(
            whole_ref.at[chip, core], whole_ref.at[chip, core], on_send.at[s], on_recv.at[s],
            (partner_of(me, 2 * s, devices), line),
        )
        for s in steps
    ]
    for copy in onward:
        copy.start()
    for copy in lines:
        copy.wait_recv()
    sum_ref[...] = jnp.sum(line_got[...], axis=0)
    for copy in onward:
        copy.wait_recv()
    y_got[line] = y_ref[line]
    last = remote(
        whole_ref.at[:, core], whole_ref.at[:, core], on_send.at[0], on_recv.at[0], (sibling, line)
    )
    last.start()
    for copy in y_copies(0) + y_copies(1):
        copy.wait_recv()
    block_ref[...] = (h1_ref[...] + jnp.sum(y_got[...].astype(F32), axis=0)).astype(BF16)
    for copy in y_copies(0) + y_copies(1):
        copy.wait_send()
    halves.wait_send()
    for s in steps:
        quarter(s).wait_send()
    cross.wait_send()
    for copy in smalls + lines + onward:
        copy.wait_send()
    last.wait()


def closing(pieces, small, y, h1):
    devices, both, rows, cols = pieces.shape
    blocks = y.shape[0]
    chips = devices // 2
    vmem = pl.BlockSpec(memory_space=pltpu.VMEM)
    dma = pltpu.SemaphoreType.DMA
    return pl.pallas_call(
        closing_kernel,
        out_shape=(
            jax.ShapeDtypeStruct((chips, 2, rows, cols), BF16),
            jax.ShapeDtypeStruct(small.shape, F32),
            jax.ShapeDtypeStruct(h1.shape, BF16),
        ),
        in_specs=[vmem] * 4,
        out_specs=(vmem,) * 3,
        scratch_shapes=[
            pltpu.VMEM(y.shape, BF16),
            dma((2, blocks)),
            dma((2, blocks)),
            pltpu.VMEM((chips, both, rows, cols), BF16),
            pltpu.VMEM((chips, both, rows, cols), BF16),
            pltpu.VMEM((chips, both, rows, cols), BF16),
            pltpu.VMEM((both, rows, cols), F32),
            pltpu.VMEM((rows, cols), BF16),
            pltpu.VMEM((rows, cols), BF16),
            pltpu.VMEM((devices,) + small.shape, F32),
            pltpu.VMEM(small.shape, F32),
            pltpu.VMEM((blocks,) + small.shape, F32),
            dma((2,)), dma((chips,)), dma((chips,)), dma((devices,)), dma((devices,)),
            dma((blocks,)), dma((blocks,)), dma((2,)), dma((chips,)), dma((chips,)), dma,
        ],
        compiler_params=pltpu.CompilerParams(
            vmem_limit_bytes=VMEM_LIMIT, collective_id=3, has_side_effects=True
        ),
        cost_estimate=pl.CostEstimate(flops=0, bytes_accessed=160000000, transcendentals=0),
        name="closing",
    )(pieces.reshape(chips, 2, both, rows, cols), small, y, h1)


def spread(rows, place0, place1, count):
    ids = lax.broadcasted_iota(jnp.int32, (count, rows.shape[0]), 0)
    hit = (ids == place0) | (ids == place1)
    return mm(jnp.where(hit, 1.0, 0.0).astype(BF16), rows)


def spread_kernel(rows_ref, place_ref, out_ref):
    experts, _, cap, width = out_ref.shape
    placed = spread(rows_ref[0], place_ref[0:1, :], place_ref[1:2, :], experts * cap)
    out_ref[...] = placed.astype(BF16).reshape(experts, 1, cap, width)


def spread_rows(rows, micro, place, experts, cap, shard_len):
    _, slots, width = rows.shape
    blocks = slots // shard_len
    return pl.pallas_call(
        spread_kernel,
        grid=(blocks,),
        out_shape=jax.ShapeDtypeStruct((experts, blocks, cap, width), BF16),
        in_specs=[
            pl.BlockSpec((1, shard_len, width), lambda b: (micro, b, 0)),
            pl.BlockSpec((2, shard_len), lambda b: (0, b)),
        ],
        out_specs=pl.BlockSpec((experts, 1, cap, width), lambda b: (0, b, 0, 0)),
        compiler_params=pltpu.CompilerParams(vmem_limit_bytes=VMEM_LIMIT),
        cost_estimate=pl.CostEstimate(
            flops=2 * experts * cap * slots * width,
            bytes_accessed=2 * slots * width + 2 * experts * blocks * cap * width,
            transcendentals=0,
        ),
        name="spread_rows",
    )(rows, place)


def collect_kernel(rows_ref, place_ref, out_ref):
    experts, _, cap, width = rows_ref.shape
    tokens = out_ref.shape[0]
    ids = lax.broadcasted_iota(jnp.int32, (experts * cap, tokens), 0)
    hit = (ids == place_ref[0:1, :]) | (ids == place_ref[1:2, :])
    rows = rows_ref[...].reshape(experts * cap, width)
    out_ref[...] = mm_tn(jnp.where(hit, 1.0, 0.0).astype(BF16), rows).astype(BF16)


def collect_rows(rows, place, shard_len):
    experts, blocks, cap, width = rows.shape
    slots = blocks * shard_len
    return pl.pallas_call(
        collect_kernel,
        grid=(blocks,),
        out_shape=jax.ShapeDtypeStruct((slots, width), BF16),
        in_specs=[
            pl.BlockSpec((experts, 1, cap, width), lambda b: (0, b, 0, 0)),
            pl.BlockSpec((2, shard_len), lambda b: (0, b)),
        ],
        out_specs=pl.BlockSpec((shard_len, width), lambda b: (b, 0)),
        compiler_params=pltpu.CompilerParams(vmem_limit_bytes=VMEM_LIMIT),
        cost_estimate=pl.CostEstimate(
            flops=2 * experts * cap * slots * width,
            bytes_accessed=2 * slots * width + 2 * experts * blocks * cap * width,
            transcendentals=0,
        ),
        name="collect_rows",
    )(rows, place)


def places(route_ref, index, cap, experts):
    shard_len = route_ref.shape[-1]
    row = lax.broadcasted_iota(jnp.int32, (shard_len, shard_len), 0)
    col = lax.broadcasted_iota(jnp.int32, (shard_len, shard_len), 1)
    earlier = jnp.where(row < col, 1.0, 0.0).astype(BF16)
    ids = lax.broadcasted_iota(jnp.int32, (experts, shard_len), 0)
    pair = [route_ref[index + (slice(k, k + 1),)] for k in range(2)]
    chosen = (ids == pair[0]) | (ids == pair[1])
    before = mm(jnp.where(chosen, 1.0, 0.0).astype(BF16), earlier)
    found = []
    for route in pair:
        position = jnp.sum(jnp.where(ids == route, before, 0.0), axis=0, keepdims=True)
        found.append(jnp.where(route >= 0, route * cap + position.astype(jnp.int32), -1))
    return pair, found


def place_kernel(cap, experts, route_ref, place_ref):
    blocks, micros, _, shard_len = route_ref.shape
    for block in range(blocks):
        for micro in range(micros):
            _, found = places(route_ref, (block, micro), cap, experts)
            for k in range(2):
                lanes = slice(block * shard_len, (block + 1) * shard_len)
                place_ref[micro, k : k + 1, lanes] = found[k]


def find_places(route, experts, cap):
    blocks, micros, _, shard_len = route.shape
    vmem = pl.BlockSpec(memory_space=pltpu.VMEM)
    return pl.pallas_call(
        functools.partial(place_kernel, cap, experts),
        out_shape=jax.ShapeDtypeStruct((micros, 2, blocks * shard_len), jnp.int32),
        in_specs=[vmem],
        out_specs=vmem,
        compiler_params=pltpu.CompilerParams(vmem_limit_bytes=VMEM_LIMIT),
        name="find_places",
    )(route)


def pair_kernel(route_ref, pair_ref):
    _, _, here, blocks, cap, experts = pair_ref.shape
    shard_len = route_ref.shape[-1]
    me = lax.axis_index("expert")
    spots = lax.broadcasted_iota(jnp.int32, (cap, shard_len), 0)
    ids = lax.broadcasted_iota(jnp.int32, (cap, experts), 1)
    for block in range(blocks):
        pair, place = places(route_ref, (0, block, 0), cap, experts)
        for e in range(here):
            expert = me * here + e
            other = jnp.full((cap, 1), -1, jnp.int32)
            for k in range(2):
                hit = spots + expert * cap == place[k]
                found = jnp.max(jnp.where(hit, pair[1 - k], -1), axis=1, keepdims=True)
                other = jnp.maximum(other, found)
            sign = jnp.where(ids == expert, 1.0, 0.0) - jnp.where(ids == other, 1.0, 0.0)
            pair_ref[0, 0, e, block] = jnp.where(other >= 0, sign, 0.0).astype(BF16)


def find_pairs(route, experts, here, cap):
    devices, blocks, micros, _, shard_len = route.shape
    return pl.pallas_call(
        pair_kernel,
        grid=(micros, devices),
        out_shape=jax.ShapeDtypeStruct((micros, devices, here, blocks, cap, experts), BF16),
        in_specs=[pl.BlockSpec((1, blocks, 1, 2, shard_len), lambda m, s: (s, 0, m, 0, 0))],
        out_specs=pl.BlockSpec((1, 1, here, blocks, cap, experts), lambda m, s: (m, s, 0, 0, 0, 0)),
        compiler_params=pltpu.CompilerParams(vmem_limit_bytes=VMEM_LIMIT),
        name="find_pairs",
    )(route)


def expert_kernel(
    by_block, sent_ref, dy_ref, pair_ref, wr_ref, wg_ref, wu_ref, wd_ref,
    back_ref, y_ref, x_ref, g_ref, hid_ref, dga_ref, dup_ref, dlog_ref,
    got_ref, dx_ref, stage_ref, x_send, x_recv, dx_send, dx_recv, own_sem, stage_sem,
):
    devices, experts, cap, width = sent_ref.shape
    step = pl.program_id(0)
    me = lax.axis_index("expert")
    line = lax.axis_index("hidden")
    first_wave = bits_of(devices)
    rest = [s for s in range(1, devices) if s not in first_wave]
    later_waves = [rest[i : i + 2] for i in range(0, len(rest), 2)]

    def x_copy(s):
        peer = partner_of(me, s, devices)
        return pltpu.make_async_remote_copy(
            src_ref=sent_ref.at[peer], dst_ref=got_ref.at[s], send_sem=x_send.at[s],
            recv_sem=x_recv.at[s], device_id=(peer, line), device_id_type=pl.DeviceIdType.MESH,
        )

    def dx_copy(s):
        peer = partner_of(me, s, devices)
        return pltpu.make_async_remote_copy(
            src_ref=dx_ref.at[s], dst_ref=back_ref.at[me], send_sem=dx_send.at[s],
            recv_sem=dx_recv.at[s], device_id=(peer, line), device_id_type=pl.DeviceIdType.MESH,
        )

    blocks, share = stage_ref.shape[2:4]

    def y_copies(s):
        source = partner_of(me, s, devices)
        slot = lax.rem(s, 2)
        if not by_block:
            return [
                pltpu.make_async_copy(stage_ref.at[slot], y_ref.at[source], stage_sem.at[slot, 0])
            ]
        return [
            pltpu.make_async_copy(
                stage_ref.at[slot, e], y_ref.at[:, source, e], stage_sem.at[slot, e]
            )
            for e in range(experts)
        ]

    def work(s):
        source = partner_of(me, s, devices)
        slot = lax.rem(s, 2)
        for e in range(experts):
            x = got_ref[s, e]
            dy = dy_ref[:, source, e].reshape(cap, width).astype(F32)
            pair = pair_ref[source, e].astype(F32)
            margin = jnp.sum(mm_nt(x, wr_ref[...]) * pair, axis=-1, keepdims=True)
            own_gate = 1.0 / (1.0 + jnp.exp(-margin))
            other_gate = 1.0 / (1.0 + jnp.exp(margin))
            g = (own_gate * dy).astype(BF16)
            x_ref[0, e] = x
            g_ref[0, e] = g
            gate = mm_nt(x, wg_ref[e])
            up = mm_nt(x, wu_ref[e])
            square = gate * gate
            bent = jnp.tanh(GELU_C * gate * (1.0 + GELU_A * square))
            half_gate = 0.5 * gate
            gelu = half_gate * (1.0 + bent)
            slope = 0.5 * (1.0 + bent) + half_gate * (1.0 - bent * bent) * (
                GELU_C * (1.0 + 3.0 * GELU_A * square)
            )
            hid = (gelu * up).astype(BF16)
            dhid = mm_nt(g, wd_ref[e])
            dga = (dhid * (up * slope)).astype(BF16)
            dup = (dhid * gelu).astype(BF16)
            hid_ref[0, e] = hid
            dga_ref[0, e] = dga
            dup_ref[0, e] = dup
            y = mm(hid, wd_ref[e])
            dgate = jnp.sum(y * dy, axis=-1, keepdims=True)
            stage_ref[slot, e] = (y * own_gate).astype(BF16).reshape(blocks, share, width)
            dlog = (dgate * own_gate * other_gate * pair).astype(BF16)
            dlog_ref[0, e] = dlog
            dx = mm(dga, wg_ref[e]) + mm(dup, wu_ref[e]) + mm(dlog, wr_ref[...])
            dx_ref[s, e] = dx.astype(BF16)

    @pl.when(step == 0)
    def _():
        barrier = pltpu.get_barrier_semaphore()
        for s in range(1, devices):
            pl.semaphore_signal(
                barrier, inc=1, device_id=(partner_of(me, s, devices), line),
                device_id_type=pl.DeviceIdType.MESH,
            )
        pl.semaphore_wait(barrier, devices - 1)
        for s in first_wave:
            x_copy(s).start()
        own = pltpu.make_async_copy(sent_ref.at[me], got_ref.at[0], own_sem)
        own.start()
        own.wait()

    @pl.when(step > 0)
    def _():
        x_copy(step).wait_recv()

    for index, wave in enumerate(later_waves):

        @pl.when(step == 2 + index)
        def _(wave=wave):
            for s in wave:
                x_copy(s).start()

    @pl.when(step > 1)
    def _():
        for copy in y_copies(step - 2):
            copy.wait()

    work(step)
    for copy in y_copies(step):
        copy.start()

    @pl.when(step > 0)
    def _():
        dx_copy(step).start()

    @pl.when(step == devices - 1)
    def _():
        own = pltpu.make_async_copy(dx_ref.at[0], back_ref.at[me], own_sem)
        own.start()
        own.wait()
        for copy in y_copies(devices - 2) + y_copies(devices - 1):
            copy.wait()
        for s in range(1, devices):
            x_copy(s).wait_send()
            dx_copy(s).wait_send()
            dx_copy(s).wait_recv()


def expert_pass(sent, dy, pair, wr, wg, wu, wd, by_block, identity):
    blocks, _, _, share, _ = dy.shape
    devices, experts, cap, width = sent.shape
    hidden = wg.shape[1]
    choices = wr.shape[0]

    def whole(shape):
        return pl.BlockSpec(shape, lambda s: (0,) * len(shape), pipeline_mode=pl.Buffered(1))

    def block(cols):
        return pl.BlockSpec((1, experts, cap, cols), lambda s: (s, 0, 0, 0))

    def kept(cols):
        return jax.ShapeDtypeStruct((devices, experts, cap, cols), BF16)

    y_shape = (blocks, devices, experts, share, width)
    if not by_block:
        y_shape = (devices, experts, blocks, share, width)
    return pl.pallas_call(
        functools.partial(expert_kernel, by_block),
        grid=(devices,),
        out_shape=(
            kept(width), jax.ShapeDtypeStruct(y_shape, BF16), kept(width), kept(width), kept(hidden), kept(hidden),
            kept(hidden), kept(choices),
        ),
        in_specs=[
            any_space(), whole(dy.shape), whole(pair.shape), whole(wr.shape), whole(wg.shape),
            whole(wu.shape), whole(wd.shape),
        ],
        out_specs=(
            any_space(), any_space(), block(width), block(width), block(hidden), block(hidden),
            block(hidden), block(choices),
        ),
        scratch_shapes=[
            pltpu.VMEM((devices, experts, cap, width), BF16),
            pltpu.VMEM((devices, experts, cap, width), BF16),
            pltpu.VMEM((2, experts, blocks, share, width), BF16),
            pltpu.SemaphoreType.DMA((devices,)),
            pltpu.SemaphoreType.DMA((devices,)),
            pltpu.SemaphoreType.DMA((devices,)),
            pltpu.SemaphoreType.DMA((devices,)),
            pltpu.SemaphoreType.DMA,
            pltpu.SemaphoreType.DMA((2, experts)),
        ],
        compiler_params=pltpu.CompilerParams(
            vmem_limit_bytes=VMEM_LIMIT, collective_id=identity, has_side_effects=True
        ),
        cost_estimate=pl.CostEstimate(flops=0, bytes_accessed=490000000, transcendentals=0),
        name="expert_pass",
    )(sent, dy, pair, wr, wg, wu, wd)


def weight_kernel(*refs):
    count = (len(refs) - 4) // 6
    dwr_ref, dwg_ref, dwu_ref, dwd_ref = refs[-4:]
    totals = [0.0, 0.0, 0.0, 0.0]
    for index in range(count):
        blocks = [
            ref[...].reshape(ref.shape[0] * ref.shape[2], ref.shape[3])
            for ref in refs[6 * index : 6 * index + 6]
        ]
        x, g, hid, dga, dup, dlog = blocks
        totals[0] = totals[0] + mm_tn(dlog, x)
        totals[1] = totals[1] + mm_tn(dga, x)
        totals[2] = totals[2] + mm_tn(dup, x)
        totals[3] = totals[3] + mm_tn(hid, g)
    dwr_ref[0] = totals[0]
    dwg_ref[0] = totals[1]
    dwu_ref[0] = totals[2]
    dwd_ref[0] = totals[3]


def weight_pass(kept):
    sources, experts, cap, width = kept[0][0].shape
    hidden = kept[0][2].shape[3]
    choices = kept[0][5].shape[3]
    rows = sources * cap
    block = 256 if width % 256 == 0 else width
    tokens = pl.BlockSpec((sources, 1, cap, block), lambda e, j: (0, e, 0, j))
    acts = pl.BlockSpec((sources, 1, cap, hidden), lambda e, j: (0, e, 0, 0))
    logs = pl.BlockSpec((sources, 1, cap, choices), lambda e, j: (0, e, 0, 0))
    operands = []
    for arrays in kept:
        operands.extend(arrays)
    return pl.pallas_call(
        weight_kernel,
        grid=(experts, width // block),
        out_shape=(
            jax.ShapeDtypeStruct((experts, choices, width), F32),
            jax.ShapeDtypeStruct((experts, hidden, width), F32),
            jax.ShapeDtypeStruct((experts, hidden, width), F32),
            jax.ShapeDtypeStruct((experts, hidden, width), F32),
        ),
        in_specs=[tokens, tokens, acts, acts, acts, logs] * len(kept),
        out_specs=(
            pl.BlockSpec((1, choices, block), lambda e, j: (e, 0, j)),
            pl.BlockSpec((1, hidden, block), lambda e, j: (e, 0, j)),
            pl.BlockSpec((1, hidden, block), lambda e, j: (e, 0, j)),
            pl.BlockSpec((1, hidden, block), lambda e, j: (e, 0, j)),
        ),
        compiler_params=pltpu.CompilerParams(vmem_limit_bytes=VMEM_LIMIT),
        cost_estimate=pl.CostEstimate(
            flops=6 * len(kept) * experts * rows * width * hidden,
            bytes_accessed=len(kept) * experts * rows * (4 * width + 6 * hidden)
            + 12 * experts * width * hidden,
            transcendentals=0,
        ),
        name="weight_pass",
    )(*operands)


def after(values, *others):
    return lax.optimization_barrier((values,) + others)[0]


def shards(
    x_in,
    cotangent,
    segment_ids,
    routes,
    qkv_weight,
    out_weight,
    bias_table,
    attn_gain,
    moe_gain,
    router_weight,
    gate_weight,
    up_weight,
    down_weight,
):
    micro_count, _, shard_len, width = x_in.shape
    slot_count = segment_ids.shape[2]
    head_cols = out_weight.shape[0]
    bucket_count, heads_here = bias_table.shape
    head_size = head_cols // heads_here
    expert_count = router_weight.shape[1]
    experts_here = gate_weight.shape[0]
    devices = expert_count // experts_here
    blocks = slot_count // shard_len
    members = blocks // 2
    half = slot_count // 2
    capacity = max(2, (10 * shard_len + 4 * expert_count - 1) // (4 * expert_count))
    scale = head_size ** (-0.5)
    hidden_index = lax.axis_index("hidden")
    expert_index = lax.axis_index("expert")
    part = hidden_index // members
    attn_gain_f = attn_gain.astype(F32).reshape(1, width)
    moe_gain_f = moe_gain.astype(F32).reshape(1, width)
    token_shape = (devices, experts_here, blocks * capacity, width)
    flat_shape = (devices, experts_here * blocks * capacity, width)
    place_shape = (expert_count, blocks, capacity, width)
    gate_rows = gate_weight.transpose(0, 2, 1)
    up_rows = up_weight.transpose(0, 2, 1)
    router_rows = router_weight.T

    def exchange(buffer):
        return lax.all_to_all(buffer, "expert", split_axis=0, concat_axis=0, tiled=True)

    def gather(values):
        return lax.all_gather(values, "hidden", axis=0, tiled=True)

    def scatter(values):
        return lax.psum_scatter(values, "hidden", scatter_dimension=0, tiled=True)

    states = [dict() for _ in range(micro_count)]
    own_seg = lax.dynamic_slice_in_dim(segment_ids[:, 0], hidden_index * shard_len, shard_len, 1)
    live_routes = jnp.where(own_seg[:, None, :] >= 0, routes[:, 0].transpose(0, 2, 1), -1)
    own_place = find_places(live_routes[None], expert_count, capacity)

    def spread(rows, micro, placed):
        return spread_rows(rows, micro, placed, expert_count, capacity, shard_len)

    dy_sent = [
        spread(cotangent[:, 0], micro, own_place[micro]).reshape(devices, -1, width)
        for micro in range(micro_count)
    ]
    x_first, other_qkv, all_out, all_routes, other_table, dy_first = opening(
        x_in[0], qkv_weight.reshape(3 * width, head_cols), out_weight,
        live_routes, bias_table.T.astype(F32), dy_sent[0], devices, blocks, members,
    )
    x_half = [x_first.reshape(1, half, width)]
    other_qkv = other_qkv.reshape(qkv_weight.shape)
    all_out = all_out.reshape(blocks, head_cols, width)

    own_routes = lax.dynamic_index_in_dim(all_routes, expert_index, 0, keepdims=False)
    place = find_places(own_routes, expert_count, capacity)

    tables = jnp.concatenate([bias_table.T.astype(F32), other_table], axis=0)
    onehot_bucket = bucket_onehot(half, bucket_count)
    bias = position_bias(jnp.einsum("jb,hb->hj", onehot_bucket, tables, precision=PRECISE))
    seg_half = lax.dynamic_slice_in_dim(segment_ids[:, 0], part * half, half, 1)

    def gather_dy(rows):
        whole = gather(rows.reshape(1, devices * experts_here * capacity, width))
        return whole.reshape(blocks, devices, experts_here, capacity, width)

    def experts(micro, kept, *behind):
        sent = spread(kept["xn2_all"][None], 0, place[micro]).reshape(token_shape)
        kept["by_block"] = micro + 1 < micro_count
        back, kept["y"], x, g, hid, dga, dup, dlog = expert_pass(
            after(sent, *behind), kept["dy"], pairs[micro], router_rows, gate_rows, up_rows,
            down_weight, kept["by_block"], 4 + micro,
        )
        kept["weights"] = (x, g, hid, dga, dup, dlog)
        kept["back"] = back
        if micro > 0:
            back = after(back, states[micro - 1]["y_own"])
        kept["dx_back"] = back.reshape(place_shape)
        kept["dx_part"] = collect_rows(kept["dx_back"], place[micro], shard_len)
        kept["dxn2"] = scatter(kept["dx_part"])
        if kept["by_block"]:
            parts = after(kept["y"], kept["dx_part"]).reshape(blocks, -1, width)
            kept["y_own"] = scatter(parts).reshape(devices, -1, width)

    states[0]["dy"] = gather_dy(dy_first)
    behind = ()
    for micro in range(micro_count):
        state = states[micro]
        rider = None
        if micro + 1 < micro_count:
            rider = (dy_sent[micro + 1], x_in[micro + 1, 0])
        qkv, prob, heads, h1, xn2, *rode = attend(
            after(x_half[micro], *behind), attn_gain_f, qkv_weight, other_qkv, bias,
            seg_half[micro : micro + 1], all_out, x_in[micro], moe_gain_f, scale, members, 10 + micro,
            rider,
        )
        state.update(qkv=qkv[0], prob=prob[0], heads=heads[0], h1=h1[0], xn2=xn2[0])
        if micro + 1 < micro_count:
            states[micro + 1]["dy_here"] = rode[0]
            x_half.append(rode[1].reshape(1, half, width))
        if micro == 0:
            pairs = find_pairs(after(all_routes, xn2), expert_count, experts_here, capacity)
            pairs = pairs.reshape(
                micro_count, devices, experts_here, blocks * capacity, expert_count
            )
            place = after(place, xn2)
            seg_half = seg_half + jnp.where(pairs[0, 0, 0, 0, 0] > 2, 1, 0)
        behind = (xn2, states[0]["dy"], place)
    behind = ()
    for micro in range(micro_count):
        state = states[micro]
        state["xn2_all"] = gather(after(state["xn2"], *behind))
        behind = (state["xn2_all"],)
    for micro in range(1, micro_count):
        states[micro]["dy"] = gather_dy(after(states[micro]["dy_here"], states[0]["xn2_all"]))
    behind = ()
    for micro in range(micro_count):
        experts(micro, states[micro], *behind)
        behind = (states[micro]["dx_part"],)
    last_part = states[-1]["dx_part"]
    kept = [state["weights"] for state in states]
    kept[-1] = tuple(after(list(kept[-1]), last_part))
    dwr, dwg, dwu, dwd = weight_pass(kept)
    last = states[-1]
    last["y_rows"] = exchange(after(last["y"], last_part).reshape(flat_shape)).reshape(place_shape)
    *x_grads, grads, lines, moe_gain_grad, attn_gain_grad = attend_back(
        moe_gain_f, attn_gain_f, all_out, qkv_weight, other_qkv,
        [
            (
                after(state["dxn2"], dwr), state["h1"], cotangent[micro, 0], x_in[micro, 0],
                x_half[micro][0], state["qkv"], state["prob"], state["heads"],
            )
            for micro, state in enumerate(states)
        ],
        scale, devices, members,
    )
    rows = collect_rows(after(last["y_rows"], grads), place[-1], shard_len)
    rows = rows.reshape(blocks, shard_len, width)
    for micro in range(micro_count - 1):
        state = states[micro]
        mixed = exchange(after(state["y_own"], grads)).reshape(expert_count, 1, capacity, width)
        mixed = collect_rows(mixed, own_place[micro], shard_len)
        state["block_out"] = (state["h1"] + mixed.astype(F32)).astype(BF16)

    lines = lines.reshape(2 * heads_here, 2 * half)
    table = jnp.einsum("hj,jb->hb", lines, onehot_bucket, precision=PRECISE)
    table = table.reshape(2, heads_here * bucket_count)
    mine = jnp.arange(blocks, dtype=jnp.int32)[:, None]
    table = jnp.where(mine == hidden_index, table[0], 0.0) + jnp.where(
        mine == (hidden_index + members) % blocks, table[1], 0.0
    )
    small = jnp.concatenate(
        [
            jnp.sum(dwr, axis=0).reshape(-1),
            attn_gain_grad.reshape(-1),
            moe_gain_grad.reshape(-1),
            table.reshape(-1),
        ]
    )
    used = small.shape[0]
    small = jnp.pad(small, (0, -used % 1024)).reshape(-1, 128)
    whole, small, last["block_out"] = closing(grads, small, rows, last["h1"])
    whole = whole.reshape(4 * width, head_cols).astype(F32)
    grad_qkv = whole[: 3 * width].reshape(qkv_weight.shape)
    grad_out = whole[3 * width :].T
    small = small.reshape(-1)
    sizes = (width * expert_count, width, width)
    grad_router = small[: sizes[0]].reshape(expert_count, width).T
    grad_attn_gain = small[sizes[0] : sizes[0] + width]
    grad_moe_gain = small[sizes[0] + width : sizes[0] + 2 * width]
    table = small[sizes[0] + 2 * width : used].reshape(blocks, heads_here, bucket_count)
    grad_table = lax.dynamic_index_in_dim(table, hidden_index, 0, keepdims=False).T
    return (
        jnp.stack([state["block_out"] for state in states])[:, None],
        jnp.stack(x_grads)[:, None],
        grad_qkv,
        grad_out,
        grad_table,
        grad_attn_gain,
        grad_moe_gain,
        grad_router,
        dwg.transpose(0, 2, 1),
        dwu.transpose(0, 2, 1),
        dwd,
    )


def solution(mesh):
    return jax.shard_map(
        shards,
        mesh=mesh,
        in_specs=(
            P(None, "expert", "hidden", None),
            P(None, "expert", "hidden", None),
            P(None, "expert", None),
            P(None, "expert", "hidden", None),
            P(None, None, "hidden"),
            P("hidden", None),
            P(None, "hidden"),
            P(),
            P(),
            P(),
            P("expert", None, "hidden"),
            P("expert", None, "hidden"),
            P("expert", "hidden", None),
        ),
        out_specs=(
            P(None, "expert", "hidden", None),
            P(None, "expert", "hidden", None),
            P(None, None, "hidden"),
            P("hidden", None),
            P(None, "hidden"),
            P(),
            P(),
            P(),
            P("expert", None, "hidden"),
            P("expert", None, "hidden"),
            P("expert", "hidden", None),
        ),
        check_vma=False,
    )
```

```python
import functools

import jax
import jax.numpy as jnp
from jax import lax
from jax.experimental import pallas as pl
from jax.experimental.pallas import tpu as pltpu
from jax.sharding import PartitionSpec as P

EPSILON = 1e-06
PRECISE = lax.Precision.HIGHEST
LIMITS = (12, 16, 23, 32, 46, 64, 91)
MASKED = -1000000000.0
GELU_C = 0.7978845608028654
GELU_A = 0.044715
VMEM_LIMIT = 60 * 1024 * 1024
F32 = jnp.float32
BF16 = jnp.bfloat16


def mm(a, b):
    return lax.dot_general(a, b, (((1,), (0,)), ((), ())), preferred_element_type=F32)


def mm_nt(a, b):
    return lax.dot_general(a, b, (((1,), (1,)), ((), ())), preferred_element_type=F32)


def mm_tn(a, b):
    return lax.dot_general(a, b, (((0,), (0,)), ((), ())), preferred_element_type=F32)


def bucket_of(distance):
    magnitude = jnp.abs(distance)
    far_bucket = jnp.full(magnitude.shape, 8, jnp.int32)
    for threshold in LIMITS:
        far_bucket = far_bucket + (magnitude >= threshold).astype(jnp.int32)
    return jnp.where(magnitude < 8, magnitude, far_bucket) + 16 * (distance > 0).astype(jnp.int32)


def bucket_onehot(half, bucket_count):
    lane = jnp.arange(2 * half, dtype=jnp.int32)
    distance = jnp.where(lane < half, lane, lane - 2 * half)
    return (
        bucket_of(distance)[:, None] == jnp.arange(bucket_count, dtype=jnp.int32)[None, :]
    ).astype(F32)


TILE = 128


def bias_kernel(line_ref, out_ref):
    length = out_ref.shape[2]
    line = jnp.broadcast_to(line_ref[0], (8, length))
    row = lax.broadcasted_iota(jnp.int32, (8, length), 0)
    sheet = line
    for r in range(1, 8):
        sheet = jnp.where(row == r, pltpu.roll(line, r, 1), sheet)
    while sheet.shape[0] < TILE:
        sheet = jnp.concatenate([sheet, pltpu.roll(sheet, sheet.shape[0], 1)], axis=0)
    out_ref[0] = sheet.astype(out_ref.dtype)


def position_bias(line):
    heads, length = line.shape
    return pl.pallas_call(
        bias_kernel,
        grid=(heads,),
        out_shape=jax.ShapeDtypeStruct((heads, TILE, length), BF16),
        in_specs=[pl.BlockSpec((1, 1, length), lambda h: (h, 0, 0))],
        out_specs=pl.BlockSpec((1, TILE, length), lambda h: (h, 0, 0)),
        compiler_params=pltpu.CompilerParams(vmem_limit_bytes=VMEM_LIMIT),
        name="position_bias",
    )(line.reshape(heads, 1, length))


def unit_rows(x):
    x = x.astype(F32)
    return x * lax.rsqrt(jnp.mean(x * x, axis=-1, keepdims=True) + EPSILON)


def remote(src, dst, send_sem, recv_sem, device):
    return pltpu.make_async_remote_copy(
        src_ref=src, dst_ref=dst, send_sem=send_sem, recv_sem=recv_sem,
        device_id=device, device_id_type=pl.DeviceIdType.MESH,
    )


def greet(devices):
    barrier = pltpu.get_barrier_semaphore()
    for device in devices:
        pl.semaphore_signal(
            barrier, inc=1, device_id=device, device_id_type=pl.DeviceIdType.MESH
        )
    pl.semaphore_wait(barrier, len(devices))


def bits_of(count):
    return [1 << b for b in range(count.bit_length() - 1)]


def partner_of(me, step, count):
    found = 0
    for bit in bits_of(count):
        found = found + bit * lax.rem(me // bit + step // bit, 2)
    return found


def any_space():
    return pl.BlockSpec(memory_space=pl.ANY)


def opening_kernel(
    micros, x_ref, qkv_ref, out_ref, routes_ref, table_ref, *refs,
):
    x_all, refs = refs[:micros], refs[micros:]
    (
        qkv_all, out_all, routes_all, table_all,
        x_send, x_recv, qkv_send, qkv_recv, out_send, out_recv, qkv_on_send, qkv_on_recv,
        out_on_send, out_on_recv, routes_send, routes_recv, routes_on_send, routes_on_recv,
        table_send, table_recv, own_sem,
    ) = refs
    devices, qkv_rows = qkv_all.shape[0] * 2, qkv_all.shape[2]
    blocks, out_rows = out_all.shape[0], out_all.shape[3]
    members = x_all[0].shape[0]
    me = lax.axis_index("expert")
    line = lax.axis_index("hidden")
    chip, core = me // 2, lax.rem(me, 2)
    mine = lax.rem(line, members)
    base = line - mine
    along = [lax.rem(line + s, blocks) for s in range(1, blocks)]
    across = lax.rem(line + members, blocks)
    sibling = partner_of(me, 1, devices)
    greet([(partner_of(me, s, devices), line) for s in range(1, devices)] + [(me, z) for z in along])
    own = [
        pltpu.make_async_copy(
            out_ref.at[pl.ds(me * out_rows, out_rows)], out_all.at[line, chip, core], own_sem.at[0]
        ),
        pltpu.make_async_copy(routes_ref, routes_all.at[me, line], own_sem.at[1]),
    ]
    for micro in range(micros):
        own.append(
            pltpu.make_async_copy(x_ref.at[micro], x_all[micro].at[mine], own_sem.at[2 + micro])
        )
    for copy in own:
        copy.start()
    first_qkv = remote(
        qkv_ref.at[pl.ds(me * qkv_rows, qkv_rows)], qkv_all.at[chip, core], qkv_send, qkv_recv,
        (me, across),
    )
    first_qkv.start()
    first_out, first_routes = [], []
    rest = [remote(table_ref, table_all, table_send, table_recv, (me, across))]
    for s, z in enumerate(along):
        first_out.append(
            remote(
                out_ref.at[pl.ds(me * out_rows, out_rows)], out_all.at[line, chip, core],
                out_send.at[s], out_recv.at[s], (me, z),
            )
        )
        first_routes.append(
            remote(
                routes_ref, routes_all.at[me, line], routes_send.at[s], routes_recv.at[s], (me, z)
            )
        )
    for copy in first_routes + first_out + rest:
        copy.start()
    for micro in range(micros):
        for s in range(1, members):
            peer = base + lax.rem(mine + s, members)
            copy = remote(
                x_ref.at[micro], x_all[micro].at[mine], x_send.at[micro, s], x_recv.at[micro, s],
                (me, peer),
            )
            copy.start()
            rest.append(copy)
    first_qkv.wait_recv()
    qkv_on, out_on = [], []
    for s in range(2, devices, 2):
        copy = remote(
            qkv_all.at[chip, core], qkv_all.at[chip, core], qkv_on_send.at[s], qkv_on_recv.at[s],
            (partner_of(me, s, devices), line),
        )
        copy.start()
        qkv_on.append(copy)
    own[1].wait()
    for copy in first_routes:
        copy.wait_recv()
    for s in range(1, devices):
        copy = remote(
            routes_all.at[me], routes_all.at[me], routes_on_send.at[s], routes_on_recv.at[s],
            (partner_of(me, s, devices), line),
        )
        copy.start()
        rest.append(copy)
    own[0].wait()
    for copy in first_out:
        copy.wait_recv()
    for s in range(2, devices, 2):
        copy = remote(
            out_all.at[:, chip, core], out_all.at[:, chip, core], out_on_send.at[s],
            out_on_recv.at[s], (partner_of(me, s, devices), line),
        )
        copy.start()
        out_on.append(copy)
    for copy in qkv_on:
        copy.wait_recv()
    copy = remote(
        qkv_all.at[:, core], qkv_all.at[:, core], qkv_on_send.at[1], qkv_on_recv.at[1],
        (sibling, line),
    )
    copy.start()
    rest.append(copy)
    for copy in out_on:
        copy.wait_recv()
    copy = remote(
        out_all.at[:, :, core], out_all.at[:, :, core], out_on_send.at[1], out_on_recv.at[1],
        (sibling, line),
    )
    copy.start()
    rest.append(copy)
    for copy in own[2:]:
        copy.wait()
    first_qkv.wait_send()
    for copy in first_out + first_routes + qkv_on + out_on:
        copy.wait_send()
    for copy in rest:
        copy.wait()


def opening(x, qkv, out, routes, table, devices, blocks, members):
    micros, shard_len, width = x.shape
    dma = pltpu.SemaphoreType.DMA
    pair = (devices // 2, 2)
    return pl.pallas_call(
        functools.partial(opening_kernel, micros),
        out_shape=(jax.ShapeDtypeStruct((members, shard_len, width), BF16),) * micros
        + (
            jax.ShapeDtypeStruct(pair + (qkv.shape[0] // devices, qkv.shape[1]), BF16),
            jax.ShapeDtypeStruct((blocks,) + pair + (out.shape[0] // devices, width), BF16),
            jax.ShapeDtypeStruct((devices, blocks) + routes.shape, jnp.int32),
            jax.ShapeDtypeStruct(table.shape, table.dtype),
        ),
        in_specs=[any_space()] * 5,
        out_specs=(any_space(),) * (4 + micros),
        scratch_shapes=[
            dma((micros, members)), dma((micros, members)), dma, dma, dma((blocks,)), dma((blocks,)),
            dma((devices,)), dma((devices,)), dma((devices,)), dma((devices,)), dma((blocks,)),
            dma((blocks,)), dma((devices,)), dma((devices,)), dma, dma, dma((2 + micros,)),
        ],
        compiler_params=pltpu.CompilerParams(collective_id=1, has_side_effects=True),
        cost_estimate=pl.CostEstimate(flops=0, bytes_accessed=200000000, transcendentals=0),
        name="opening",
    )(x, qkv, out, routes, table)


def unit_rows(x):
    x = x.astype(F32)
    return x * lax.rsqrt(jnp.mean(x * x, axis=-1, keepdims=True) + EPSILON)


def places(route_ref, index, cap, experts):
    shard_len = route_ref.shape[-1]
    row = lax.broadcasted_iota(jnp.int32, (shard_len, shard_len), 0)
    col = lax.broadcasted_iota(jnp.int32, (shard_len, shard_len), 1)
    earlier = jnp.where(row < col, 1.0, 0.0).astype(BF16)
    ids = lax.broadcasted_iota(jnp.int32, (experts, shard_len), 0)
    pair = [route_ref[index + (slice(k, k + 1),)] for k in range(2)]
    chosen = (ids == pair[0]) | (ids == pair[1])
    before = mm(jnp.where(chosen, 1.0, 0.0).astype(BF16), earlier)
    found = []
    for route in pair:
        position = jnp.sum(jnp.where(ids == route, before, 0.0), axis=0, keepdims=True)
        found.append(jnp.where(route >= 0, route * cap + position.astype(jnp.int32), -1))
    return pair, found


def fill_pairs(route_ref, pair_ref, source, micro, me):
    _, _, here, blocks, cap, experts = pair_ref.shape
    spots = lax.broadcasted_iota(jnp.int32, (cap, route_ref.shape[-1]), 0)
    ids = lax.broadcasted_iota(jnp.int32, (cap, experts), 1)
    for block in range(blocks):
        pair, place = places(route_ref, (source, block, micro), cap, experts)
        for e in range(here):
            expert = me * here + e
            other = jnp.full((cap, 1), -1, jnp.int32)
            for k in range(2):
                hit = spots + expert * cap == place[k]
                found = jnp.max(jnp.where(hit, pair[1 - k], -1), axis=1, keepdims=True)
                other = jnp.maximum(other, found)
            sign = jnp.where(ids == expert, 1.0, 0.0) - jnp.where(ids == other, 1.0, 0.0)
            pair_ref[micro, source, e, block] = jnp.where(other >= 0, sign, 0.0).astype(BF16)


def attend_kernel(
    scale, x_ref, gain_ref, own_ref, other_ref, bias_ref, seg_row_ref, seg_col_ref,
    out_ref, x_own_ref, moe_gain_ref, *refs,
):
    sent_ref, refs = refs[0], refs[1:]
    pairing = len(refs) > 14
    if pairing:
        routes_ref, pair_ref = refs[0], refs[7]
        refs = refs[1:7] + refs[8:]
    arrived_ref, ride_send, ride_recv, ride_own = refs[5], *refs[-3:]
    refs = refs[:5] + refs[6:-3]
    qkv_ref, prob_ref, heads_ref, h1_ref, xn2_ref, xn_ref, part_ref, got_ref, send_sem, recv_sem = refs
    micros, members, shard_len, both = got_ref.shape
    cols = both // 2
    heads, length = bias_ref.shape[0], bias_ref.shape[2]
    half = members * shard_len
    size = cols // heads
    micro, group = pl.program_id(0), pl.program_id(1)
    me = lax.axis_index("expert")
    line = lax.axis_index("hidden")
    mine = lax.rem(line, members)
    part = line // members
    base = line - mine

    def swap(m, s):
        peer = lax.rem(mine + s, members)
        return remote(
            part_ref.at[m, peer], got_ref.at[m, mine], send_sem.at[m, s], recv_sem.at[m, s],
            (me, base + peer),
        )

    def ride(s):
        peer = partner_of(me, s, sent_ref.shape[0])
        return remote(
            sent_ref.at[peer], arrived_ref.at[me], ride_send.at[s], ride_recv.at[s], (peer, line)
        )

    def stay():
        return pltpu.make_async_copy(sent_ref.at[me], arrived_ref.at[me], ride_own)

    @pl.when((micro == 0) & (group == 0))
    def _():
        peers = [(me, base + lax.rem(mine + s, members)) for s in range(1, members)]
        devices = sent_ref.shape[0]
        peers += [(partner_of(me, s, devices), line) for s in range(1, devices)]
        greet(peers)
        stay().start()
        for s in range(1, devices):
            ride(s).start()

    @pl.when(group == 0)
    def _():
        xn_ref[...] = (unit_rows(x_ref[0]) * gain_ref[...]).astype(BF16)
        for t in range(3):
            qkv_ref[0, 0, t] = mm(xn_ref[...], own_ref[t]).astype(BF16)

    @pl.when(group > 0)
    def _():
        for t in range(3):
            qkv_ref[0, 0, t] = mm(xn_ref[...], other_ref[t]).astype(BF16)

    seg_row = seg_row_ref[0]
    for head in range(heads):
        inner = slice(head * size, (head + 1) * size)
        keys = qkv_ref[0, 0, 1, :, inner]
        values = qkv_ref[0, 0, 2, :, inner]
        for start in range(0, half, TILE):
            rows = slice(start, start + TILE)
            scores = mm_nt(qkv_ref[0, 0, 0, rows, inner], keys) * scale
            shift = bias_ref[head, :, : half - start]
            if start:
                shift = jnp.concatenate([bias_ref[head, :, length - start :], shift], axis=1)
            scores = scores + shift.astype(F32)
            scores = jnp.where(seg_col_ref[0, rows, :] == seg_row, scores, MASKED)
            top = jnp.max(scores, axis=-1, keepdims=True)
            weights = jnp.exp(scores - top)
            inverse = 1.0 / jnp.sum(weights, axis=-1, keepdims=True)
            prob = (weights * inverse).astype(BF16)
            prob_ref[0, 0, head, rows, :] = prob
            heads_ref[0, rows, inner] = mm(prob, values).astype(BF16)

    for g in range(2):

        @pl.when(group == g)
        def _(g=g):
            for member in range(members):
                rows = slice(member * shard_len, (member + 1) * shard_len)
                part_ref[micro, member, :, g * cols : (g + 1) * cols] = heads_ref[0, rows, :]

    @pl.when(group == 1)
    def _():
        got_ref[micro, mine] = part_ref[micro, mine]
        for s in range(1, members):
            swap(micro, s).start()

    @pl.when((micro == micros - 1) & (group == 1))
    def _():
        for m in range(micros):
            for s in range(1, members):
                swap(m, s).wait_recv()
            h1 = x_own_ref[m].astype(F32)
            for member in range(members):
                for j in range(2):
                    index = lax.rem(part + j, 2) * members + member
                    h1 = h1 + mm(got_ref[m, member, :, j * cols : (j + 1) * cols], out_ref[index])
            h1_ref[m] = h1
            xn2_ref[m] = (unit_rows(h1) * moe_gain_ref[...]).astype(BF16)
        for m in range(micros):
            for s in range(1, members):
                swap(m, s).wait_send()
        if pairing:

            @pl.loop(0, routes_ref.shape[0])
            def _(source):
                for m in range(pair_ref.shape[0]):
                    fill_pairs(routes_ref, pair_ref, source, m, me)

        stay().wait()
        for s in range(1, sent_ref.shape[0]):
            ride(s).wait()


def attend(
    x, gain, own_weight, other_weight, bias, seg, out_weight, x_own, moe_gain, scale, members, identity,
    rider, routes=None, pair_shape=None,
):
    micros, half, width = x.shape
    cols = own_weight.shape[2]
    heads = bias.shape[0] // 2
    shard_len = half // members
    riders, ride_specs = [rider], [any_space()]
    ride_out, ride_out_specs = [jax.ShapeDtypeStruct(rider.shape, BF16)], [any_space()]
    if routes is not None:
        riders.append(routes)
        ride_specs.append(pl.BlockSpec(memory_space=pltpu.VMEM))
        ride_out.append(jax.ShapeDtypeStruct(pair_shape, BF16))
        ride_out_specs.append(pl.BlockSpec(memory_space=pltpu.VMEM))
    ride_sems = [pltpu.SemaphoreType.DMA((rider.shape[0],))] * 2 + [pltpu.SemaphoreType.DMA]

    def once(shape):
        return pl.BlockSpec(shape, lambda m, p: (0,) * len(shape), pipeline_mode=pl.Buffered(1))

    return pl.pallas_call(
        functools.partial(attend_kernel, scale),
        grid=(micros, 2),
        out_shape=(
            jax.ShapeDtypeStruct((micros, 2, 3, half, cols), BF16),
            jax.ShapeDtypeStruct((micros, 2, heads, half, half), BF16),
            jax.ShapeDtypeStruct((micros, half, 2 * cols), BF16),
            jax.ShapeDtypeStruct((micros, shard_len, width), F32),
            jax.ShapeDtypeStruct((micros, shard_len, width), BF16),
        )
        + tuple(ride_out),
        in_specs=[
            pl.BlockSpec((1, half, width), lambda m, p: (m, 0, 0)),
            once((1, width)),
            once((3, width, cols)),
            once((3, width, cols)),
            pl.BlockSpec((heads,) + bias.shape[1:], lambda m, p: (p, 0, 0)),
            pl.BlockSpec((1, 1, half), lambda m, p: (m, 0, 0)),
            pl.BlockSpec((1, half, 1), lambda m, p: (m, 0, 0)),
            once(out_weight.shape),
            once(x_own.shape),
            once((1, width)),
        ]
        + ride_specs,
        out_specs=(
            pl.BlockSpec((1, 1, 3, half, cols), lambda m, p: (m, p, 0, 0, 0)),
            pl.BlockSpec((1, 1, heads, half, half), lambda m, p: (m, p, 0, 0, 0)),
            pl.BlockSpec((1, half, cols), lambda m, p: (m, 0, p)),
            pl.BlockSpec((micros, shard_len, width), lambda m, p: (0, 0, 0)),
            pl.BlockSpec((micros, shard_len, width), lambda m, p: (0, 0, 0)),
        )
        + tuple(ride_out_specs),
        scratch_shapes=[
            pltpu.VMEM((half, width), BF16),
            pltpu.VMEM((micros, members, shard_len, 2 * cols), BF16),
            pltpu.VMEM((micros, members, shard_len, 2 * cols), BF16),
            pltpu.SemaphoreType.DMA((micros, members)),
            pltpu.SemaphoreType.DMA((micros, members)),
        ]
        + ride_sems,
        compiler_params=pltpu.CompilerParams(
            vmem_limit_bytes=VMEM_LIMIT, collective_id=identity, has_side_effects=True
        ),
        cost_estimate=pl.CostEstimate(
            flops=micros * 2 * half * cols * (8 * width + 4 * half),
            bytes_accessed=100000000,
            transcendentals=micros * 2 * heads * half * half,
        ),
        name="attend",
    )(
        x, gain, own_weight, other_weight, bias, seg.reshape(micros, 1, half),
        seg.reshape(micros, half, 1), out_weight, x_own, moe_gain, *riders,
    )


def back_kernel(scale, micros, *refs):
    moe_gain_ref, gain_ref, out_ref, own_ref, other_ref = refs[:5]
    inputs = [refs[5 + 8 * m : 13 + 8 * m] for m in range(micros)]
    refs = refs[5 + 8 * micros :]
    xgrads, refs = refs[:micros], refs[micros:]
    (
        grads_ref, line_ref, dmoe_ref, dgain_ref,
        dh1_ref, dattn_all, dheads_part, dheads_all, dxn_part, dxn_got, total_ref, xn_ref, ds_ref,
        dproj_ref, sheet_ref, attn_send, attn_recv, heads_send, heads_recv, dxn_send, dxn_recv,
    ) = refs
    _, members, shard_len, width = dattn_all.shape
    cols = dproj_ref.shape[2]
    half = members * shard_len
    length = sheet_ref.shape[1]
    group, micro = pl.program_id(0), pl.program_id(1)
    me = lax.axis_index("expert")
    line = lax.axis_index("hidden")
    mine = lax.rem(line, members)
    part = line // members
    base = line - mine
    steps = range(1, members)

    def peer_of(s):
        return lax.rem(mine + s, members)

    def attn_copy(m, s):
        return remote(
            dattn_all.at[m, mine], dattn_all.at[m, mine], attn_send.at[m, s], attn_recv.at[m, s],
            (me, base + peer_of(s)),
        )

    def heads_copy(m, s):
        return remote(
            dheads_part.at[m, peer_of(s)], dheads_all.at[m, mine], heads_send.at[m, s],
            heads_recv.at[m, s], (me, base + peer_of(s)),
        )

    def dxn_copy(m, s):
        return remote(
            dxn_part.at[m, peer_of(s)], dxn_got.at[m, mine], dxn_send.at[m, s], dxn_recv.at[m, s],
            (me, base + peer_of(s)),
        )

    @pl.when((group == 0) & (micro == 0))
    def _():
        greet([(me, base + peer_of(s)) for s in steps])
        dmoe_ref[...] = jnp.zeros_like(dmoe_ref)
        dgain_ref[...] = jnp.zeros_like(dgain_ref)
        for m in range(micros):
            grad_ref, h1_ref, dy_ref = inputs[m][:3]
            grad = grad_ref[...].astype(F32)
            h1 = h1_ref[...]
            r2 = lax.rsqrt(jnp.mean(h1 * h1, axis=-1, keepdims=True) + EPSILON)
            unit = h1 * r2
            dmoe_ref[...] += jnp.sum(grad * unit, axis=0, keepdims=True)
            weighted = grad * moe_gain_ref[...]
            inner = jnp.mean(weighted * unit, axis=-1, keepdims=True)
            dh1 = dy_ref[...].astype(F32) + r2 * (weighted - unit * inner)
            dh1_ref[m] = dh1
            dattn = dh1.astype(BF16)
            dattn_all[m, mine] = dattn
            for member in range(members):
                for j in range(2):
                    index = lax.rem(part + j, 2) * members + member
                    dheads = mm_nt(dattn, out_ref[index]).astype(BF16)
                    dheads_part[m, member, :, j * cols : (j + 1) * cols] = dheads
            for s in steps:
                heads_copy(m, s).start()
            dheads_all[m, mine] = dheads_part[m, mine]
        for m in range(micros):
            xn_ref[m] = (unit_rows(inputs[m][4][...]) * gain_ref[...]).astype(BF16)

    def products(weight_ref):
        dxn = mm_nt(dproj_ref[0], weight_ref[0])
        for t in range(1, 3):
            dxn = dxn + mm_nt(dproj_ref[t], weight_ref[t])
        return dxn.reshape(members, shard_len, width)

    per = grads_ref.shape[0] // 4
    for g in range(2):
        for m in range(micros):

            @pl.when((group == g) & (micro == m))
            def _(g=g, m=m):
                x_ref, qkv_ref, prob_ref, heads_ref = inputs[m][4:]
                heads = prob_ref.shape[1]
                size = cols // heads
                if g == 0:
                    for s in steps:
                        heads_copy(m, s).wait_recv()
                    for s in steps:
                        attn_copy(m, s).start()
                for head in range(heads):
                    inner_cols = slice(head * size, (head + 1) * size)
                    outer_cols = slice(g * cols + head * size, g * cols + (head + 1) * size)
                    values = qkv_ref[0, 2, :, inner_cols]
                    grads = dheads_all[m, :, :, outer_cols].reshape(half, size)
                    sheet_ref[...] = jnp.zeros_like(sheet_ref)
                    for start in range(0, half, TILE):
                        rows = slice(start, start + TILE)
                        prob = prob_ref[0, head, rows, :].astype(F32)
                        dprob = mm_nt(grads[rows], values)
                        inner = jnp.sum(prob * dprob, axis=-1, keepdims=True)
                        dscore = (prob * (dprob - inner)).astype(BF16)
                        ds_ref[rows, :] = dscore
                        dscore = dscore.astype(F32)
                        sheet_ref[:, : half - start] += dscore[:, start:]
                        if start:
                            sheet_ref[:, length - start :] += dscore[:, :start]
                    dscores = ds_ref[...]
                    keys, queries = qkv_ref[0, 1, :, inner_cols], qkv_ref[0, 0, :, inner_cols]
                    dproj_ref[0, :, inner_cols] = (mm(dscores, keys) * scale).astype(BF16)
                    dproj_ref[1, :, inner_cols] = (mm_tn(dscores, queries) * scale).astype(BF16)
                    dproj_ref[2, :, inner_cols] = mm_tn(prob_ref[0, head], grads).astype(BF16)
                    sheet = sheet_ref[...]
                    while sheet.shape[0] > 8:
                        upper = sheet.shape[0] // 2
                        sheet = sheet[:upper] + pltpu.roll(sheet[upper:], length - upper, 1)
                    row = lax.broadcasted_iota(jnp.int32, (8, length), 0)
                    found = jnp.zeros((1, length), F32)
                    for r in range(8):
                        moved = pltpu.roll(sheet, length - r, 1) if r else sheet
                        found = found + jnp.sum(
                            jnp.where(row == r, moved, 0.0), axis=0, keepdims=True
                        )
                    if m:
                        found = found + line_ref[0, head : head + 1, :]
                    line_ref[0, head : head + 1, :] = found
                if g == 0:
                    total_ref[m] = products(own_ref)
                    for s in steps:
                        attn_copy(m, s).wait_recv()
                else:
                    total = total_ref[m] + products(other_ref)
                    total_ref[m] = total
                    dxn_part[m] = total.astype(BF16)
                    for s in steps:
                        dxn_copy(m, s).start()
                    total = total.reshape(half, width)
                    dgain_ref[...] += jnp.sum(total * unit_rows(x_ref[...]), axis=0, keepdims=True)
                for t in range(4):
                    if t < 3:
                        found = mm_tn(xn_ref[m], dproj_ref[t])
                    else:
                        found = mm_tn(dattn_all[m].reshape(half, width), heads_ref[...])
                    found = found.reshape(per, 1, width // per, cols)
                    if m:
                        found = found + grads_ref[t * per : (t + 1) * per].astype(F32)
                    grads_ref[t * per : (t + 1) * per] = found.astype(BF16)

    @pl.when((group == 1) & (micro == micros - 1))
    def _():
        for m in range(micros):
            x_own = inputs[m][3][...].astype(F32)
            r1 = lax.rsqrt(jnp.mean(x_own * x_own, axis=-1, keepdims=True) + EPSILON)
            unit = x_own * r1
            for s in steps:
                dxn_copy(m, s).wait_recv()
            dxn1 = total_ref[m, mine]
            for s in steps:
                dxn1 = dxn1 + dxn_got[m, lax.rem(mine + members - s, members)].astype(F32)
            weighted = dxn1 * gain_ref[...]
            inner = jnp.mean(weighted * unit, axis=-1, keepdims=True)
            xgrads[m][...] = (dh1_ref[m] + r1 * (weighted - unit * inner)).astype(BF16)
        for m in range(micros):
            for s in steps:
                heads_copy(m, s).wait_send()
                attn_copy(m, s).wait_send()
                dxn_copy(m, s).wait_send()


def attend_back(moe_gain, gain, out_weight, own_weight, other_weight, kept, scale, pieces, members):
    micros = len(kept)
    _, heads, half = kept[0][6].shape[:3]
    width, cols = own_weight.shape[1:]
    shard_len = half // members
    length = 2 * half
    rows = 4 * width // pieces

    def once(array):
        return pl.BlockSpec(
            array.shape, lambda p, m: (0,) * array.ndim, pipeline_mode=pl.Buffered(1)
        )

    operands = [moe_gain, gain, out_weight, own_weight, other_weight]
    in_specs = [once(array) for array in operands]
    for arrays in kept:
        operands.extend(arrays)
        in_specs += [once(array) for array in arrays[:5]] + [
            pl.BlockSpec((1, 3, half, cols), lambda p, m: (p, 0, 0, 0)),
            pl.BlockSpec((1, heads, half, half), lambda p, m: (p, 0, 0, 0)),
            pl.BlockSpec((half, cols), lambda p, m: (0, p)),
        ]
    dma = pltpu.SemaphoreType.DMA((micros, members))
    return pl.pallas_call(
        functools.partial(back_kernel, scale, micros),
        grid=(2, micros),
        out_shape=(jax.ShapeDtypeStruct((shard_len, width), BF16),) * micros
        + (
            jax.ShapeDtypeStruct((pieces, 2, rows, cols), BF16),
            jax.ShapeDtypeStruct((2, heads, length), F32),
            jax.ShapeDtypeStruct((1, width), F32),
            jax.ShapeDtypeStruct((1, width), F32),
        ),
        in_specs=in_specs,
        out_specs=(pl.BlockSpec((shard_len, width), lambda p, m: (0, 0)),) * micros
        + (
            pl.BlockSpec((pieces, 1, rows, cols), lambda p, m: (0, p, 0, 0)),
            pl.BlockSpec((1, heads, length), lambda p, m: (p, 0, 0)),
            pl.BlockSpec((1, width), lambda p, m: (0, 0)),
            pl.BlockSpec((1, width), lambda p, m: (0, 0)),
        ),
        scratch_shapes=[
            pltpu.VMEM((micros, shard_len, width), F32),
            pltpu.VMEM((micros, members, shard_len, width), BF16),
            pltpu.VMEM((micros, members, shard_len, 2 * cols), BF16),
            pltpu.VMEM((micros, members, shard_len, 2 * cols), BF16),
            pltpu.VMEM((micros, members, shard_len, width), BF16),
            pltpu.VMEM((micros, members, shard_len, width), BF16),
            pltpu.VMEM((micros, members, shard_len, width), F32),
            pltpu.VMEM((micros, half, width), BF16),
            pltpu.VMEM((half, half), BF16),
            pltpu.VMEM((3, half, cols), BF16),
            pltpu.VMEM((TILE, length), F32),
            dma, dma, dma, dma, dma, dma,
        ],
        compiler_params=pltpu.CompilerParams(
            vmem_limit_bytes=VMEM_LIMIT, collective_id=6, has_side_effects=True
        ),
        cost_estimate=pl.CostEstimate(
            flops=2 * micros * half * cols * (16 * width + 8 * half),
            bytes_accessed=250000000,
            transcendentals=0,
        ),
        name="attend_back",
    )(*operands)


def closing_kernel(
    pieces_ref, small_ref, y_ref, h1_ref, whole_ref, sum_ref, block_ref,
    y_got, y_send, y_recv, half_got, held_ref, quarter_got, total_ref, moved_ref, moved_got, small_got, line_sum,
    line_got, half_sem, quarter_send, quarter_recv, small_send, small_recv, line_send, line_recv,
    moved_sem, on_send, on_recv, own_sem,
):
    chips = pieces_ref.shape[0]
    devices = 2 * chips
    blocks = line_got.shape[0]
    me = lax.axis_index("expert")
    line = lax.axis_index("hidden")
    chip, core = me // 2, lax.rem(me, 2)
    sibling = partner_of(me, 1, devices)
    along = [lax.rem(line + s, blocks) for s in range(1, blocks)]
    across = lax.rem(line + blocks // 2, blocks)
    greet([(partner_of(me, s, devices), line) for s in range(1, devices)] + [(me, z) for z in along])
    share = 3 * y_ref.shape[1] // 4
    turns = (pl.ds(0, share), pl.ds(share, y_ref.shape[1] - share))

    def y_copies(turn):
        rows = turns[turn]
        return [
            remote(
                y_ref.at[z, rows], y_got.at[line, rows], y_send.at[turn, s], y_recv.at[turn, s],
                (me, z),
            )
            for s, z in enumerate(along)
        ]

    halves = remote(
        pieces_ref.at[:, 1 - core], half_got, half_sem.at[0], half_sem.at[1], (sibling, line)
    )
    halves.start()
    for copy in y_copies(0):
        copy.start()
    smalls = [
        remote(
            small_ref, small_got.at[me], small_send.at[s], small_recv.at[s],
            (partner_of(me, s, devices), line),
        )
        for s in range(1, devices)
    ]
    for copy in smalls:
        copy.start()
    small_got[me] = small_ref[...]
    halves.wait_recv()
    steps = range(1, chips)

    def quarter(s):
        other = partner_of(chip, s, chips)
        return remote(
            held_ref.at[other], quarter_got.at[s], quarter_send.at[s], quarter_recv.at[s],
            (partner_of(me, 2 * s, devices), line),
        )

    for s in steps:
        other = partner_of(chip, s, chips)
        held = pieces_ref[other, core].astype(F32) + half_got[other].astype(F32)
        held_ref[other] = held.astype(BF16)
        quarter(s).start()
    total_ref[...] = pieces_ref[chip, core].astype(F32) + half_got[chip].astype(F32)
    for copy in smalls:
        copy.wait_recv()
    line_sum[...] = jnp.sum(small_got[...], axis=0)
    lines = [
        remote(line_sum, line_got.at[line], line_send.at[s], line_recv.at[s], (me, z))
        for s, z in enumerate(along)
    ]
    for copy in lines:
        copy.start()
    line_got[line] = line_sum[...]
    for s in steps:
        quarter(s).wait_recv()
        total_ref[...] += quarter_got[s].astype(F32)
    moved_ref[...] = total_ref[1].astype(BF16)
    cross = remote(moved_ref, moved_got, moved_sem.at[0], moved_sem.at[1], (me, across))
    cross.start()
    cross.wait_recv()
    for copy in y_copies(1):
        copy.start()
    whole_ref[chip, core] = (total_ref[0] + moved_got[...].astype(F32)).astype(BF16)
    onward = [
        remote(
            whole_ref.at[chip, core], whole_ref.at[chip, core], on_send.at[s], on_recv.at[s],
            (partner_of(me, 2 * s, devices), line),
        )
        for s in steps
    ]
    for copy in onward:
        copy.start()
    for copy in lines:
        copy.wait_recv()
    sum_ref[...] = jnp.sum(line_got[...], axis=0)
    for copy in onward:
        copy.wait_recv()
    y_got[line] = y_ref[line]
    last = remote(
        whole_ref.at[:, core], whole_ref.at[:, core], on_send.at[0], on_recv.at[0], (sibling, line)
    )
    last.start()
    for copy in y_copies(0) + y_copies(1):
        copy.wait_recv()
    block_ref[...] = (h1_ref[...] + jnp.sum(y_got[...].astype(F32), axis=0)).astype(BF16)
    for copy in y_copies(0) + y_copies(1):
        copy.wait_send()
    halves.wait_send()
    for s in steps:
        quarter(s).wait_send()
    cross.wait_send()
    for copy in smalls + lines + onward:
        copy.wait_send()
    last.wait()


def closing(pieces, small, y, h1):
    devices, both, rows, cols = pieces.shape
    blocks = y.shape[0]
    chips = devices // 2
    vmem = pl.BlockSpec(memory_space=pltpu.VMEM)
    dma = pltpu.SemaphoreType.DMA
    return pl.pallas_call(
        closing_kernel,
        out_shape=(
            jax.ShapeDtypeStruct((chips, 2, rows, cols), BF16),
            jax.ShapeDtypeStruct(small.shape, F32),
            jax.ShapeDtypeStruct(h1.shape, BF16),
        ),
        in_specs=[vmem] * 4,
        out_specs=(vmem,) * 3,
        scratch_shapes=[
            pltpu.VMEM(y.shape, BF16),
            dma((2, blocks)),
            dma((2, blocks)),
            pltpu.VMEM((chips, both, rows, cols), BF16),
            pltpu.VMEM((chips, both, rows, cols), BF16),
            pltpu.VMEM((chips, both, rows, cols), BF16),
            pltpu.VMEM((both, rows, cols), F32),
            pltpu.VMEM((rows, cols), BF16),
            pltpu.VMEM((rows, cols), BF16),
            pltpu.VMEM((devices,) + small.shape, F32),
            pltpu.VMEM(small.shape, F32),
            pltpu.VMEM((blocks,) + small.shape, F32),
            dma((2,)), dma((chips,)), dma((chips,)), dma((devices,)), dma((devices,)),
            dma((blocks,)), dma((blocks,)), dma((2,)), dma((chips,)), dma((chips,)), dma,
        ],
        compiler_params=pltpu.CompilerParams(
            vmem_limit_bytes=VMEM_LIMIT, collective_id=3, has_side_effects=True
        ),
        cost_estimate=pl.CostEstimate(flops=0, bytes_accessed=160000000, transcendentals=0),
        name="closing",
    )(pieces.reshape(chips, 2, both, rows, cols), small, y, h1)


def spread(rows, place0, place1, count):
    ids = lax.broadcasted_iota(jnp.int32, (count, rows.shape[0]), 0)
    hit = (ids == place0) | (ids == place1)
    return mm(jnp.where(hit, 1.0, 0.0).astype(BF16), rows)


def spread_kernel(rows_ref, place_ref, out_ref):
    experts, _, cap, width = out_ref.shape
    placed = spread(rows_ref[0], place_ref[0:1, :], place_ref[1:2, :], experts * cap)
    out_ref[...] = placed.astype(BF16).reshape(experts, 1, cap, width)


def spread_rows(rows, micro, place, experts, cap, shard_len):
    _, slots, width = rows.shape
    blocks = slots // shard_len
    return pl.pallas_call(
        spread_kernel,
        grid=(blocks,),
        out_shape=jax.ShapeDtypeStruct((experts, blocks, cap, width), BF16),
        in_specs=[
            pl.BlockSpec((1, shard_len, width), lambda b: (micro, b, 0)),
            pl.BlockSpec((2, shard_len), lambda b: (0, b)),
        ],
        out_specs=pl.BlockSpec((experts, 1, cap, width), lambda b: (0, b, 0, 0)),
        compiler_params=pltpu.CompilerParams(vmem_limit_bytes=VMEM_LIMIT),
        cost_estimate=pl.CostEstimate(
            flops=2 * experts * cap * slots * width,
            bytes_accessed=2 * slots * width + 2 * experts * blocks * cap * width,
            transcendentals=0,
        ),
        name="spread_rows",
    )(rows, place)


def collect_kernel(rows_ref, place_ref, out_ref):
    experts, _, cap, width = rows_ref.shape
    tokens = out_ref.shape[0]
    ids = lax.broadcasted_iota(jnp.int32, (experts * cap, tokens), 0)
    hit = (ids == place_ref[0:1, :]) | (ids == place_ref[1:2, :])
    rows = rows_ref[...].reshape(experts * cap, width)
    out_ref[...] = mm_tn(jnp.where(hit, 1.0, 0.0).astype(BF16), rows).astype(BF16)


def collect_rows(rows, place, shard_len):
    experts, blocks, cap, width = rows.shape
    slots = blocks * shard_len
    return pl.pallas_call(
        collect_kernel,
        grid=(blocks,),
        out_shape=jax.ShapeDtypeStruct((slots, width), BF16),
        in_specs=[
            pl.BlockSpec((experts, 1, cap, width), lambda b: (0, b, 0, 0)),
            pl.BlockSpec((2, shard_len), lambda b: (0, b)),
        ],
        out_specs=pl.BlockSpec((shard_len, width), lambda b: (b, 0)),
        compiler_params=pltpu.CompilerParams(vmem_limit_bytes=VMEM_LIMIT),
        cost_estimate=pl.CostEstimate(
            flops=2 * experts * cap * slots * width,
            bytes_accessed=2 * slots * width + 2 * experts * blocks * cap * width,
            transcendentals=0,
        ),
        name="collect_rows",
    )(rows, place)


def place_kernel(cap, experts, route_ref, place_ref):
    blocks, micros, _, shard_len = route_ref.shape
    for block in range(blocks):
        for micro in range(micros):
            _, found = places(route_ref, (block, micro), cap, experts)
            for k in range(2):
                lanes = slice(block * shard_len, (block + 1) * shard_len)
                place_ref[micro, k : k + 1, lanes] = found[k]


def find_places(route, experts, cap):
    blocks, micros, _, shard_len = route.shape
    vmem = pl.BlockSpec(memory_space=pltpu.VMEM)
    return pl.pallas_call(
        functools.partial(place_kernel, cap, experts),
        out_shape=jax.ShapeDtypeStruct((micros, 2, blocks * shard_len), jnp.int32),
        in_specs=[vmem],
        out_specs=vmem,
        compiler_params=pltpu.CompilerParams(vmem_limit_bytes=VMEM_LIMIT),
        name="find_places",
    )(route)


def expert_kernel(
    by_block, sent_ref, dy_ref, pair_ref, wr_ref, wg_ref, wu_ref, wd_ref,
    back_ref, y_ref, x_ref, g_ref, hid_ref, dga_ref, dup_ref, dlog_ref,
    got_ref, dx_ref, stage_ref, x_send, x_recv, dx_send, dx_recv, own_sem, stage_sem,
):
    devices, experts, cap, width = sent_ref.shape
    step = pl.program_id(0)
    me = lax.axis_index("expert")
    line = lax.axis_index("hidden")
    first_wave = bits_of(devices)
    rest = [s for s in range(1, devices) if s not in first_wave]
    later_waves = [rest[i : i + 2] for i in range(0, len(rest), 2)]

    def x_copy(s):
        peer = partner_of(me, s, devices)
        return pltpu.make_async_remote_copy(
            src_ref=sent_ref.at[peer], dst_ref=got_ref.at[s], send_sem=x_send.at[s],
            recv_sem=x_recv.at[s], device_id=(peer, line), device_id_type=pl.DeviceIdType.MESH,
        )

    def dx_copy(s):
        peer = partner_of(me, s, devices)
        return pltpu.make_async_remote_copy(
            src_ref=dx_ref.at[s], dst_ref=back_ref.at[me], send_sem=dx_send.at[s],
            recv_sem=dx_recv.at[s], device_id=(peer, line), device_id_type=pl.DeviceIdType.MESH,
        )

    blocks, share = stage_ref.shape[2:4]

    def y_copies(s):
        source = partner_of(me, s, devices)
        slot = lax.rem(s, 2)
        if not by_block[1]:
            return [
                pltpu.make_async_copy(stage_ref.at[slot], y_ref.at[source], stage_sem.at[slot, 0])
            ]
        return [
            pltpu.make_async_copy(
                stage_ref.at[slot, e], y_ref.at[:, source, e], stage_sem.at[slot, e]
            )
            for e in range(experts)
        ]

    def work(s):
        source = partner_of(me, s, devices)
        slot = lax.rem(s, 2)
        for e in range(experts):
            x = got_ref[s, e]
            dy = dy_ref[:, source, e] if by_block[0] else dy_ref[source, e]
            dy = dy.reshape(cap, width).astype(F32)
            pair = pair_ref[source, e].astype(F32)
            margin = jnp.sum(mm_nt(x, wr_ref[...]) * pair, axis=-1, keepdims=True)
            own_gate = 1.0 / (1.0 + jnp.exp(-margin))
            other_gate = 1.0 / (1.0 + jnp.exp(margin))
            g = (own_gate * dy).astype(BF16)
            x_ref[0, e] = x
            g_ref[0, e] = g
            gate = mm_nt(x, wg_ref[e])
            up = mm_nt(x, wu_ref[e])
            square = gate * gate
            bent = jnp.tanh(GELU_C * gate * (1.0 + GELU_A * square))
            half_gate = 0.5 * gate
            gelu = half_gate * (1.0 + bent)
            slope = 0.5 * (1.0 + bent) + half_gate * (1.0 - bent * bent) * (
                GELU_C * (1.0 + 3.0 * GELU_A * square)
            )
            hid = (gelu * up).astype(BF16)
            dhid = mm_nt(g, wd_ref[e])
            dga = (dhid * (up * slope)).astype(BF16)
            dup = (dhid * gelu).astype(BF16)
            hid_ref[0, e] = hid
            dga_ref[0, e] = dga
            dup_ref[0, e] = dup
            y = mm(hid, wd_ref[e])
            dgate = jnp.sum(y * dy, axis=-1, keepdims=True)
            stage_ref[slot, e] = (y * own_gate).astype(BF16).reshape(blocks, share, width)
            dlog = (dgate * own_gate * other_gate * pair).astype(BF16)
            dlog_ref[0, e] = dlog
            dx = mm(dga, wg_ref[e]) + mm(dup, wu_ref[e]) + mm(dlog, wr_ref[...])
            dx_ref[s, e] = dx.astype(BF16)

    @pl.when(step == 0)
    def _():
        barrier = pltpu.get_barrier_semaphore()
        for s in range(1, devices):
            pl.semaphore_signal(
                barrier, inc=1, device_id=(partner_of(me, s, devices), line),
                device_id_type=pl.DeviceIdType.MESH,
            )
        pl.semaphore_wait(barrier, devices - 1)
        for s in first_wave:
            x_copy(s).start()
        own = pltpu.make_async_copy(sent_ref.at[me], got_ref.at[0], own_sem)
        own.start()
        own.wait()

    @pl.when(step > 0)
    def _():
        x_copy(step).wait_recv()

    for index, wave in enumerate(later_waves):

        @pl.when(step == 2 + index)
        def _(wave=wave):
            for s in wave:
                x_copy(s).start()

    @pl.when(step > 1)
    def _():
        for copy in y_copies(step - 2):
            copy.wait()

    work(step)
    for copy in y_copies(step):
        copy.start()

    @pl.when(step > 0)
    def _():
        dx_copy(step).start()

    @pl.when(step == devices - 1)
    def _():
        own = pltpu.make_async_copy(dx_ref.at[0], back_ref.at[me], own_sem)
        own.start()
        own.wait()
        for copy in y_copies(devices - 2) + y_copies(devices - 1):
            copy.wait()
        for s in range(1, devices):
            x_copy(s).wait_send()
            dx_copy(s).wait_send()
            dx_copy(s).wait_recv()


def expert_pass(sent, dy, pair, wr, wg, wu, wd, by_block, identity):
    share = dy.shape[3]
    blocks = sent.shape[2] // share
    devices, experts, cap, width = sent.shape
    hidden = wg.shape[1]
    choices = wr.shape[0]

    def whole(shape):
        return pl.BlockSpec(shape, lambda s: (0,) * len(shape), pipeline_mode=pl.Buffered(1))

    def block(cols):
        return pl.BlockSpec((1, experts, cap, cols), lambda s: (s, 0, 0, 0))

    def kept(cols):
        return jax.ShapeDtypeStruct((devices, experts, cap, cols), BF16)

    y_shape = (blocks, devices, experts, share, width)
    if not by_block[1]:
        y_shape = (devices, experts, blocks, share, width)
    return pl.pallas_call(
        functools.partial(expert_kernel, by_block),
        grid=(devices,),
        out_shape=(
            kept(width), jax.ShapeDtypeStruct(y_shape, BF16), kept(width), kept(width), kept(hidden), kept(hidden),
            kept(hidden), kept(choices),
        ),
        in_specs=[
            any_space(), whole(dy.shape), whole(pair.shape), whole(wr.shape), whole(wg.shape),
            whole(wu.shape), whole(wd.shape),
        ],
        out_specs=(
            any_space(), any_space(), block(width), block(width), block(hidden), block(hidden),
            block(hidden), block(choices),
        ),
        scratch_shapes=[
            pltpu.VMEM((devices, experts, cap, width), BF16),
            pltpu.VMEM((devices, experts, cap, width), BF16),
            pltpu.VMEM((2, experts, blocks, share, width), BF16),
            pltpu.SemaphoreType.DMA((devices,)),
            pltpu.SemaphoreType.DMA((devices,)),
            pltpu.SemaphoreType.DMA((devices,)),
            pltpu.SemaphoreType.DMA((devices,)),
            pltpu.SemaphoreType.DMA,
            pltpu.SemaphoreType.DMA((2, experts)),
        ],
        compiler_params=pltpu.CompilerParams(
            vmem_limit_bytes=VMEM_LIMIT, collective_id=identity, has_side_effects=True
        ),
        cost_estimate=pl.CostEstimate(flops=0, bytes_accessed=490000000, transcendentals=0),
        name="expert_pass",
    )(sent, dy, pair, wr, wg, wu, wd)


def weight_kernel(*refs):
    count = (len(refs) - 4) // 6
    dwr_ref, dwg_ref, dwu_ref, dwd_ref = refs[-4:]
    totals = [0.0, 0.0, 0.0, 0.0]
    for index in range(count):
        blocks = [
            ref[...].reshape(ref.shape[0] * ref.shape[2], ref.shape[3])
            for ref in refs[6 * index : 6 * index + 6]
        ]
        x, g, hid, dga, dup, dlog = blocks
        totals[0] = totals[0] + mm_tn(dlog, x)
        totals[1] = totals[1] + mm_tn(dga, x)
        totals[2] = totals[2] + mm_tn(dup, x)
        totals[3] = totals[3] + mm_tn(hid, g)
    dwr_ref[0] = totals[0]
    dwg_ref[0] = totals[1]
    dwu_ref[0] = totals[2]
    dwd_ref[0] = totals[3]


def weight_pass(kept):
    sources, experts, cap, width = kept[0][0].shape
    hidden = kept[0][2].shape[3]
    choices = kept[0][5].shape[3]
    rows = sources * cap
    block = 256 if width % 256 == 0 else width
    tokens = pl.BlockSpec((sources, 1, cap, block), lambda e, j: (0, e, 0, j))
    acts = pl.BlockSpec((sources, 1, cap, hidden), lambda e, j: (0, e, 0, 0))
    logs = pl.BlockSpec((sources, 1, cap, choices), lambda e, j: (0, e, 0, 0))
    operands = []
    for arrays in kept:
        operands.extend(arrays)
    return pl.pallas_call(
        weight_kernel,
        grid=(experts, width // block),
        out_shape=(
            jax.ShapeDtypeStruct((experts, choices, width), F32),
            jax.ShapeDtypeStruct((experts, hidden, width), F32),
            jax.ShapeDtypeStruct((experts, hidden, width), F32),
            jax.ShapeDtypeStruct((experts, hidden, width), F32),
        ),
        in_specs=[tokens, tokens, acts, acts, acts, logs] * len(kept),
        out_specs=(
            pl.BlockSpec((1, choices, block), lambda e, j: (e, 0, j)),
            pl.BlockSpec((1, hidden, block), lambda e, j: (e, 0, j)),
            pl.BlockSpec((1, hidden, block), lambda e, j: (e, 0, j)),
            pl.BlockSpec((1, hidden, block), lambda e, j: (e, 0, j)),
        ),
        compiler_params=pltpu.CompilerParams(vmem_limit_bytes=VMEM_LIMIT),
        cost_estimate=pl.CostEstimate(
            flops=6 * len(kept) * experts * rows * width * hidden,
            bytes_accessed=len(kept) * experts * rows * (4 * width + 6 * hidden)
            + 12 * experts * width * hidden,
            transcendentals=0,
        ),
        name="weight_pass",
    )(*operands)


def after(values, *others):
    return lax.optimization_barrier((values,) + others)[0]


def shards(
    x_in,
    cotangent,
    segment_ids,
    routes,
    qkv_weight,
    out_weight,
    bias_table,
    attn_gain,
    moe_gain,
    router_weight,
    gate_weight,
    up_weight,
    down_weight,
):
    micro_count, _, shard_len, width = x_in.shape
    slot_count = segment_ids.shape[2]
    head_cols = out_weight.shape[0]
    bucket_count, heads_here = bias_table.shape
    head_size = head_cols // heads_here
    expert_count = router_weight.shape[1]
    experts_here = gate_weight.shape[0]
    devices = expert_count // experts_here
    blocks = slot_count // shard_len
    members = blocks // 2
    half = slot_count // 2
    capacity = max(2, (10 * shard_len + 4 * expert_count - 1) // (4 * expert_count))
    scale = head_size ** (-0.5)
    hidden_index = lax.axis_index("hidden")
    expert_index = lax.axis_index("expert")
    part = hidden_index // members
    attn_gain_f = attn_gain.astype(F32).reshape(1, width)
    moe_gain_f = moe_gain.astype(F32).reshape(1, width)
    token_shape = (devices, experts_here, blocks * capacity, width)
    flat_shape = (devices, experts_here * blocks * capacity, width)
    place_shape = (expert_count, blocks, capacity, width)
    gate_rows = gate_weight.transpose(0, 2, 1)
    up_rows = up_weight.transpose(0, 2, 1)
    router_rows = router_weight.T

    def exchange(buffer):
        return lax.all_to_all(buffer, "expert", split_axis=0, concat_axis=0, tiled=True)

    def gather(values):
        return lax.all_gather(values, "hidden", axis=0, tiled=True)

    def scatter(values):
        return lax.psum_scatter(values, "hidden", scatter_dimension=0, tiled=True)

    states = [dict() for _ in range(micro_count)]
    own_seg = lax.dynamic_slice_in_dim(segment_ids[:, 0], hidden_index * shard_len, shard_len, 1)
    live_routes = jnp.where(own_seg[:, None, :] >= 0, routes[:, 0].transpose(0, 2, 1), -1)
    own_place = find_places(live_routes[None], expert_count, capacity)

    def spread(rows, micro, placed):
        return spread_rows(rows, micro, placed, expert_count, capacity, shard_len)

    *x_all, other_qkv, all_out, all_routes, other_table = opening(
        x_in[:, 0], qkv_weight.reshape(3 * width, head_cols), out_weight,
        live_routes, bias_table.T.astype(F32), devices, blocks, members,
    )
    x_half = [x.reshape(1, half, width) for x in x_all]
    other_qkv = other_qkv.reshape(qkv_weight.shape)
    all_out = all_out.reshape(blocks, head_cols, width)

    own_routes = lax.dynamic_index_in_dim(all_routes, expert_index, 0, keepdims=False)
    place = find_places(own_routes, expert_count, capacity)

    tables = jnp.concatenate([bias_table.T.astype(F32), other_table], axis=0)
    onehot_bucket = bucket_onehot(half, bucket_count)
    bias = position_bias(jnp.einsum("jb,hb->hj", onehot_bucket, tables, precision=PRECISE))
    seg_half = lax.dynamic_slice_in_dim(segment_ids[:, 0], part * half, half, 1)

    def gather_dy(rows):
        whole = gather(rows.reshape(1, devices * experts_here * capacity, width))
        return whole.reshape(blocks, devices, experts_here, capacity, width)

    def experts(micro, kept, *behind):
        sent = spread(kept["xn2_all"][None], 0, place[micro]).reshape(token_shape)
        kept["by_block"] = (micro > 0, micro + 1 < micro_count)
        back, kept["y"], x, g, hid, dga, dup, dlog = expert_pass(
            after(sent, *behind), kept["dy"], pairs[micro], router_rows, gate_rows, up_rows,
            down_weight, kept["by_block"], 4 + micro,
        )
        kept["weights"] = (x, g, hid, dga, dup, dlog)
        kept["back"] = back
        if micro > 0:
            back = after(back, states[micro - 1]["y_own"])
        kept["dx_back"] = back.reshape(place_shape)
        kept["dx_part"] = collect_rows(kept["dx_back"], place[micro], shard_len)
        kept["dxn2"] = scatter(kept["dx_part"])
        if kept["by_block"][1]:
            parts = after(kept["y"], kept["dx_part"]).reshape(blocks, -1, width)
            kept["y_own"] = scatter(parts).reshape(devices, -1, width)

    first, last = states
    first["dy_all"] = gather(after(cotangent[0, 0], all_out))
    pair_shape = (micro_count, devices, experts_here, blocks, capacity, expert_count)
    for micro, state in enumerate(states):
        inputs = (
            attn_gain_f, qkv_weight, other_qkv, bias, seg_half[micro : micro + 1], all_out,
            x_in[micro], moe_gain_f, scale, members, 10 + micro,
        )
        if micro == 0:
            sent = spread(cotangent[:, 0], 1, own_place[1]).reshape(devices, -1, width)
            qkv, prob, heads, h1, xn2, last["dy_here"] = attend(x_half[0], *inputs, sent)
        else:
            sent = spread(after(first["dy_all"], xn2)[None], 0, place[0]).reshape(token_shape)
            qkv, prob, heads, h1, xn2, first["dy"], pairs = attend(
                after(x_half[1], xn2), *inputs, sent, all_routes, pair_shape
            )
        state.update(qkv=qkv[0], prob=prob[0], heads=heads[0], h1=h1[0], xn2=xn2[0])
    first["dy"] = first["dy"].reshape(devices, experts_here, blocks, capacity, width)
    pairs = pairs.reshape(micro_count, devices, experts_here, blocks * capacity, expert_count)
    behind = ()
    for micro in range(micro_count):
        state = states[micro]
        state["xn2_all"] = gather(after(state["xn2"], *behind))
        behind = (state["xn2_all"],)
    for micro in range(1, micro_count):
        states[micro]["dy"] = gather_dy(after(states[micro]["dy_here"], states[0]["xn2_all"]))
    behind = ()
    for micro in range(micro_count):
        experts(micro, states[micro], *behind)
        behind = (states[micro]["dx_part"],)
    last_part = states[-1]["dx_part"]
    kept = [state["weights"] for state in states]
    kept[-1] = tuple(after(list(kept[-1]), last_part))
    dwr, dwg, dwu, dwd = weight_pass(kept)
    last["y_rows"] = exchange(after(last["y"], last_part).reshape(flat_shape)).reshape(place_shape)
    *x_grads, grads, lines, moe_gain_grad, attn_gain_grad = attend_back(
        moe_gain_f, attn_gain_f, all_out, qkv_weight, other_qkv,
        [
            (
                after(state["dxn2"], dwr), state["h1"], cotangent[micro, 0], x_in[micro, 0],
                x_half[micro][0], state["qkv"], state["prob"], state["heads"],
            )
            for micro, state in enumerate(states)
        ],
        scale, devices, members,
    )
    rows = collect_rows(after(last["y_rows"], grads), place[-1], shard_len)
    rows = rows.reshape(blocks, shard_len, width)
    for micro in range(micro_count - 1):
        state = states[micro]
        mixed = exchange(after(state["y_own"], grads)).reshape(expert_count, 1, capacity, width)
        mixed = collect_rows(mixed, own_place[micro], shard_len)
        state["block_out"] = (state["h1"] + mixed.astype(F32)).astype(BF16)

    lines = lines.reshape(2 * heads_here, 2 * half)
    table = jnp.einsum("hj,jb->hb", lines, onehot_bucket, precision=PRECISE)
    table = table.reshape(2, heads_here * bucket_count)
    mine = jnp.arange(blocks, dtype=jnp.int32)[:, None]
    table = jnp.where(mine == hidden_index, table[0], 0.0) + jnp.where(
        mine == (hidden_index + members) % blocks, table[1], 0.0
    )
    small = jnp.concatenate(
        [
            jnp.sum(dwr, axis=0).reshape(-1),
            attn_gain_grad.reshape(-1),
            moe_gain_grad.reshape(-1),
            table.reshape(-1),
        ]
    )
    used = small.shape[0]
    small = jnp.pad(small, (0, -used % 1024)).reshape(-1, 128)
    whole, small, last["block_out"] = closing(grads, small, rows, last["h1"])
    whole = whole.reshape(4 * width, head_cols).astype(F32)
    grad_qkv = whole[: 3 * width].reshape(qkv_weight.shape)
    grad_out = whole[3 * width :].T
    small = small.reshape(-1)
    sizes = (width * expert_count, width, width)
    grad_router = small[: sizes[0]].reshape(expert_count, width).T
    grad_attn_gain = small[sizes[0] : sizes[0] + width]
    grad_moe_gain = small[sizes[0] + width : sizes[0] + 2 * width]
    table = small[sizes[0] + 2 * width : used].reshape(blocks, heads_here, bucket_count)
    grad_table = lax.dynamic_index_in_dim(table, hidden_index, 0, keepdims=False).T
    return (
        jnp.stack([state["block_out"] for state in states])[:, None],
        jnp.stack(x_grads)[:, None],
        grad_qkv,
        grad_out,
        grad_table,
        grad_attn_gain,
        grad_moe_gain,
        grad_router,
        dwg.transpose(0, 2, 1),
        dwu.transpose(0, 2, 1),
        dwd,
    )


def solution(mesh):
    return jax.shard_map(
        shards,
        mesh=mesh,
        in_specs=(
            P(None, "expert", "hidden", None),
            P(None, "expert", "hidden", None),
            P(None, "expert", None),
            P(None, "expert", "hidden", None),
            P(None, None, "hidden"),
            P("hidden", None),
            P(None, "hidden"),
            P(),
            P(),
            P(),
            P("expert", None, "hidden"),
            P("expert", None, "hidden"),
            P("expert", "hidden", None),
        ),
        out_specs=(
            P(None, "expert", "hidden", None),
            P(None, "expert", "hidden", None),
            P(None, None, "hidden"),
            P("hidden", None),
            P(None, "hidden"),
            P(),
            P(),
            P(),
            P("expert", None, "hidden"),
            P("expert", None, "hidden"),
            P("expert", "hidden", None),
        ),
        check_vma=False,
    )
```

```python
import functools

import jax
import jax.numpy as jnp
from jax import lax
from jax.experimental import pallas as pl
from jax.experimental.pallas import tpu as pltpu
from jax.sharding import PartitionSpec as P

EPSILON = 1e-06
PRECISE = lax.Precision.HIGHEST
LIMITS = (12, 16, 23, 32, 46, 64, 91)
MASKED = -1000000000.0
GELU_C = 0.7978845608028654
GELU_A = 0.044715
VMEM_LIMIT = 60 * 1024 * 1024
F32 = jnp.float32
BF16 = jnp.bfloat16


def mm(a, b):
    return lax.dot_general(a, b, (((1,), (0,)), ((), ())), preferred_element_type=F32)


def mm_nt(a, b):
    return lax.dot_general(a, b, (((1,), (1,)), ((), ())), preferred_element_type=F32)


def mm_tn(a, b):
    return lax.dot_general(a, b, (((0,), (0,)), ((), ())), preferred_element_type=F32)


def bucket_of(distance):
    magnitude = jnp.abs(distance)
    far_bucket = jnp.full(magnitude.shape, 8, jnp.int32)
    for threshold in LIMITS:
        far_bucket = far_bucket + (magnitude >= threshold).astype(jnp.int32)
    return jnp.where(magnitude < 8, magnitude, far_bucket) + 16 * (distance > 0).astype(jnp.int32)


def bucket_onehot(half, bucket_count):
    lane = jnp.arange(2 * half, dtype=jnp.int32)
    distance = jnp.where(lane < half, lane, lane - 2 * half)
    return (
        bucket_of(distance)[:, None] == jnp.arange(bucket_count, dtype=jnp.int32)[None, :]
    ).astype(F32)


TILE = 128


def bias_kernel(line_ref, out_ref):
    heads, _, length = out_ref.shape
    row = lax.broadcasted_iota(jnp.int32, (8, length), 0)
    for head in range(heads):
        line = jnp.broadcast_to(line_ref[head : head + 1, :], (8, length))
        sheet = line
        for r in range(1, 8):
            sheet = jnp.where(row == r, pltpu.roll(line, r, 1), sheet)
        while sheet.shape[0] < TILE:
            sheet = jnp.concatenate([sheet, pltpu.roll(sheet, sheet.shape[0], 1)], axis=0)
        out_ref[head] = sheet.astype(out_ref.dtype)


def position_bias(line):
    heads, length = line.shape
    vmem = pl.BlockSpec(memory_space=pltpu.VMEM)
    return pl.pallas_call(
        bias_kernel,
        out_shape=jax.ShapeDtypeStruct((heads, TILE, length), BF16),
        in_specs=[vmem],
        out_specs=vmem,
        compiler_params=pltpu.CompilerParams(vmem_limit_bytes=VMEM_LIMIT),
        name="position_bias",
    )(line)


def unit_rows(x):
    x = x.astype(F32)
    return x * lax.rsqrt(jnp.mean(x * x, axis=-1, keepdims=True) + EPSILON)


def remote(src, dst, send_sem, recv_sem, device):
    return pltpu.make_async_remote_copy(
        src_ref=src, dst_ref=dst, send_sem=send_sem, recv_sem=recv_sem,
        device_id=device, device_id_type=pl.DeviceIdType.MESH,
    )


def greet(devices):
    barrier = pltpu.get_barrier_semaphore()
    for device in devices:
        pl.semaphore_signal(
            barrier, inc=1, device_id=device, device_id_type=pl.DeviceIdType.MESH
        )
    pl.semaphore_wait(barrier, len(devices))


def bits_of(count):
    return [1 << b for b in range(count.bit_length() - 1)]


def partner_of(me, step, count):
    found = 0
    for bit in bits_of(count):
        found = found + bit * lax.rem(me // bit + step // bit, 2)
    return found


def any_space():
    return pl.BlockSpec(memory_space=pl.ANY)


def opening_kernel(
    micros, x_ref, qkv_ref, out_ref, routes_ref, table_ref, *refs,
):
    x_all, refs = refs[:micros], refs[micros:]
    (
        qkv_all, out_all, routes_all, table_all,
        x_send, x_recv, qkv_send, qkv_recv, out_send, out_recv, qkv_on_send, qkv_on_recv,
        out_on_send, out_on_recv, routes_send, routes_recv, routes_on_send, routes_on_recv,
        table_send, table_recv, own_sem,
    ) = refs
    devices, qkv_rows = qkv_all.shape[0] * 2, qkv_all.shape[2]
    blocks, out_rows = out_all.shape[0], out_all.shape[3]
    members = x_all[0].shape[0]
    me = lax.axis_index("expert")
    line = lax.axis_index("hidden")
    chip, core = me // 2, lax.rem(me, 2)
    mine = lax.rem(line, members)
    base = line - mine
    along = [lax.rem(line + s, blocks) for s in range(1, blocks)]
    across = lax.rem(line + members, blocks)
    sibling = partner_of(me, 1, devices)
    greet([(partner_of(me, s, devices), line) for s in range(1, devices)] + [(me, z) for z in along])
    own = [
        pltpu.make_async_copy(
            out_ref.at[pl.ds(me * out_rows, out_rows)], out_all.at[line, chip, core], own_sem.at[0]
        ),
        pltpu.make_async_copy(routes_ref, routes_all.at[me, line], own_sem.at[1]),
    ]
    for micro in range(micros):
        own.append(
            pltpu.make_async_copy(x_ref.at[micro], x_all[micro].at[mine], own_sem.at[2 + micro])
        )
    for copy in own:
        copy.start()
    first_qkv = remote(
        qkv_ref.at[pl.ds(me * qkv_rows, qkv_rows)], qkv_all.at[chip, core], qkv_send, qkv_recv,
        (me, across),
    )
    first_qkv.start()
    first_out, first_routes = [], []
    rest = [remote(table_ref, table_all, table_send, table_recv, (me, across))]
    for s, z in enumerate(along):
        first_out.append(
            remote(
                out_ref.at[pl.ds(me * out_rows, out_rows)], out_all.at[line, chip, core],
                out_send.at[s], out_recv.at[s], (me, z),
            )
        )
        first_routes.append(
            remote(
                routes_ref, routes_all.at[me, line], routes_send.at[s], routes_recv.at[s], (me, z)
            )
        )
    for copy in first_routes + first_out + rest:
        copy.start()
    for micro in range(micros):
        for s in range(1, members):
            peer = base + lax.rem(mine + s, members)
            copy = remote(
                x_ref.at[micro], x_all[micro].at[mine], x_send.at[micro, s], x_recv.at[micro, s],
                (me, peer),
            )
            copy.start()
            rest.append(copy)
    first_qkv.wait_recv()
    qkv_on, out_on = [], []
    for s in range(2, devices, 2):
        copy = remote(
            qkv_all.at[chip, core], qkv_all.at[chip, core], qkv_on_send.at[s], qkv_on_recv.at[s],
            (partner_of(me, s, devices), line),
        )
        copy.start()
        qkv_on.append(copy)
    own[1].wait()
    for copy in first_routes:
        copy.wait_recv()
    for s in range(1, devices):
        copy = remote(
            routes_all.at[me], routes_all.at[me], routes_on_send.at[s], routes_on_recv.at[s],
            (partner_of(me, s, devices), line),
        )
        copy.start()
        rest.append(copy)
    own[0].wait()
    for copy in first_out:
        copy.wait_recv()
    for s in range(2, devices, 2):
        copy = remote(
            out_all.at[:, chip, core], out_all.at[:, chip, core], out_on_send.at[s],
            out_on_recv.at[s], (partner_of(me, s, devices), line),
        )
        copy.start()
        out_on.append(copy)
    for copy in qkv_on:
        copy.wait_recv()
    copy = remote(
        qkv_all.at[:, core], qkv_all.at[:, core], qkv_on_send.at[1], qkv_on_recv.at[1],
        (sibling, line),
    )
    copy.start()
    rest.append(copy)
    for copy in out_on:
        copy.wait_recv()
    copy = remote(
        out_all.at[:, :, core], out_all.at[:, :, core], out_on_send.at[1], out_on_recv.at[1],
        (sibling, line),
    )
    copy.start()
    rest.append(copy)
    for copy in own[2:]:
        copy.wait()
    first_qkv.wait_send()
    for copy in first_out + first_routes + qkv_on + out_on:
        copy.wait_send()
    for copy in rest:
        copy.wait()


def opening(x, qkv, out, routes, table, devices, blocks, members):
    micros, shard_len, width = x.shape
    dma = pltpu.SemaphoreType.DMA
    pair = (devices // 2, 2)
    return pl.pallas_call(
        functools.partial(opening_kernel, micros),
        out_shape=(jax.ShapeDtypeStruct((members, shard_len, width), BF16),) * micros
        + (
            jax.ShapeDtypeStruct(pair + (qkv.shape[0] // devices, qkv.shape[1]), BF16),
            jax.ShapeDtypeStruct((blocks,) + pair + (out.shape[0] // devices, width), BF16),
            jax.ShapeDtypeStruct((devices, blocks) + routes.shape, jnp.int32),
            jax.ShapeDtypeStruct(table.shape, table.dtype),
        ),
        in_specs=[any_space()] * 5,
        out_specs=(any_space(),) * (4 + micros),
        scratch_shapes=[
            dma((micros, members)), dma((micros, members)), dma, dma, dma((blocks,)), dma((blocks,)),
            dma((devices,)), dma((devices,)), dma((devices,)), dma((devices,)), dma((blocks,)),
            dma((blocks,)), dma((devices,)), dma((devices,)), dma, dma, dma((2 + micros,)),
        ],
        compiler_params=pltpu.CompilerParams(collective_id=1, has_side_effects=True),
        cost_estimate=pl.CostEstimate(flops=0, bytes_accessed=200000000, transcendentals=0),
        name="opening",
    )(x, qkv, out, routes, table)


def unit_rows(x):
    x = x.astype(F32)
    return x * lax.rsqrt(jnp.mean(x * x, axis=-1, keepdims=True) + EPSILON)


def places(route_ref, index, cap, experts):
    shard_len = route_ref.shape[-1]
    row = lax.broadcasted_iota(jnp.int32, (shard_len, shard_len), 0)
    col = lax.broadcasted_iota(jnp.int32, (shard_len, shard_len), 1)
    earlier = jnp.where(row < col, 1.0, 0.0).astype(BF16)
    ids = lax.broadcasted_iota(jnp.int32, (experts, shard_len), 0)
    pair = [route_ref[index + (slice(k, k + 1),)] for k in range(2)]
    chosen = (ids == pair[0]) | (ids == pair[1])
    before = mm(jnp.where(chosen, 1.0, 0.0).astype(BF16), earlier)
    found = []
    for route in pair:
        position = jnp.sum(jnp.where(ids == route, before, 0.0), axis=0, keepdims=True)
        found.append(jnp.where(route >= 0, route * cap + position.astype(jnp.int32), -1))
    return pair, found


def fill_pairs(route_ref, pair_ref, source, micro, me):
    _, _, here, blocks, cap, experts = pair_ref.shape
    spots = lax.broadcasted_iota(jnp.int32, (cap, route_ref.shape[-1]), 0)
    ids = lax.broadcasted_iota(jnp.int32, (cap, experts), 1)
    for block in range(blocks):
        pair, place = places(route_ref, (source, block, micro), cap, experts)
        for e in range(here):
            expert = me * here + e
            other = jnp.full((cap, 1), -1, jnp.int32)
            for k in range(2):
                hit = spots + expert * cap == place[k]
                found = jnp.max(jnp.where(hit, pair[1 - k], -1), axis=1, keepdims=True)
                other = jnp.maximum(other, found)
            sign = jnp.where(ids == expert, 1.0, 0.0) - jnp.where(ids == other, 1.0, 0.0)
            pair_ref[micro, source, e, block] = jnp.where(other >= 0, sign, 0.0).astype(BF16)


def collect(rows_ref, place_ref):
    experts, _, cap, width = rows_ref.shape
    tokens = place_ref.shape[1]
    ids = lax.broadcasted_iota(jnp.int32, (experts * cap, tokens), 0)
    hit = (ids == place_ref[0:1, :]) | (ids == place_ref[1:2, :])
    rows = rows_ref[...].reshape(experts * cap, width)
    return mm_tn(jnp.where(hit, 1.0, 0.0).astype(BF16), rows)


def attend_kernel(
    scale, x_ref, gain_ref, own_ref, other_ref, bias_ref, seg_row_ref, seg_col_ref,
    out_ref, x_own_ref, moe_gain_ref, *refs,
):
    sent_ref, refs = refs[0], refs[1:]
    pairing = len(refs) > 14
    if pairing:
        routes_ref, pair_ref = refs[0], refs[7]
        refs = refs[1:7] + refs[8:]
    arrived_ref, ride_send, ride_recv, ride_own = refs[5], *refs[-3:]
    refs = refs[:5] + refs[6:-3]
    qkv_ref, prob_ref, heads_ref, h1_ref, xn2_ref, xn_ref, part_ref, got_ref, send_sem, recv_sem = refs
    micros, members, shard_len, both = got_ref.shape
    cols = both // 2
    heads, length = bias_ref.shape[0], bias_ref.shape[2]
    half = members * shard_len
    size = cols // heads
    micro, group = pl.program_id(0), pl.program_id(1)
    me = lax.axis_index("expert")
    line = lax.axis_index("hidden")
    mine = lax.rem(line, members)
    part = line // members
    base = line - mine

    def swap(m, s):
        peer = lax.rem(mine + s, members)
        return remote(
            part_ref.at[m, peer], got_ref.at[m, mine], send_sem.at[m, s], recv_sem.at[m, s],
            (me, base + peer),
        )

    def ride(s):
        peer = partner_of(me, s, sent_ref.shape[0])
        return remote(
            sent_ref.at[peer], arrived_ref.at[me], ride_send.at[s], ride_recv.at[s], (peer, line)
        )

    def stay():
        return pltpu.make_async_copy(sent_ref.at[me], arrived_ref.at[me], ride_own)

    @pl.when((micro == 0) & (group == 0))
    def _():
        peers = [(me, base + lax.rem(mine + s, members)) for s in range(1, members)]
        devices = sent_ref.shape[0]
        peers += [(partner_of(me, s, devices), line) for s in range(1, devices)]
        greet(peers)
        stay().start()
        for s in range(1, devices):
            ride(s).start()

    @pl.when(group == 0)
    def _():
        xn_ref[...] = (unit_rows(x_ref[0]) * gain_ref[...]).astype(BF16)
        for t in range(3):
            qkv_ref[0, 0, t] = mm(xn_ref[...], own_ref[t]).astype(BF16)

    @pl.when(group > 0)
    def _():
        for t in range(3):
            qkv_ref[0, 0, t] = mm(xn_ref[...], other_ref[t]).astype(BF16)

    seg_row = seg_row_ref[0]
    for head in range(heads):
        inner = slice(head * size, (head + 1) * size)
        keys = qkv_ref[0, 0, 1, :, inner]
        values = qkv_ref[0, 0, 2, :, inner]
        for start in range(0, half, TILE):
            rows = slice(start, start + TILE)
            scores = mm_nt(qkv_ref[0, 0, 0, rows, inner], keys) * scale
            shift = bias_ref[head, :, : half - start]
            if start:
                shift = jnp.concatenate([bias_ref[head, :, length - start :], shift], axis=1)
            scores = scores + shift.astype(F32)
            scores = jnp.where(seg_col_ref[0, rows, :] == seg_row, scores, MASKED)
            top = jnp.max(scores, axis=-1, keepdims=True)
            weights = jnp.exp(scores - top)
            inverse = 1.0 / jnp.sum(weights, axis=-1, keepdims=True)
            prob = (weights * inverse).astype(BF16)
            prob_ref[0, 0, head, rows, :] = prob
            heads_ref[0, rows, inner] = mm(prob, values).astype(BF16)

    for g in range(2):

        @pl.when(group == g)
        def _(g=g):
            for member in range(members):
                rows = slice(member * shard_len, (member + 1) * shard_len)
                part_ref[micro, member, :, g * cols : (g + 1) * cols] = heads_ref[0, rows, :]

    @pl.when(group == 1)
    def _():
        got_ref[micro, mine] = part_ref[micro, mine]
        for s in range(1, members):
            swap(micro, s).start()

    @pl.when((micro == micros - 1) & (group == 1))
    def _():
        for m in range(micros):
            for s in range(1, members):
                swap(m, s).wait_recv()
            h1 = x_own_ref[0, 0].astype(F32)
            for member in range(members):
                for j in range(2):
                    index = lax.rem(part + j, 2) * members + member
                    h1 = h1 + mm(got_ref[m, member, :, j * cols : (j + 1) * cols], out_ref[index])
            h1_ref[m] = h1
            xn2_ref[m] = (unit_rows(h1) * moe_gain_ref[...]).astype(BF16)
        for m in range(micros):
            for s in range(1, members):
                swap(m, s).wait_send()
        if pairing:

            @pl.loop(0, routes_ref.shape[0])
            def _(source):
                for m in range(pair_ref.shape[0]):
                    fill_pairs(routes_ref, pair_ref, source, m, me)

        stay().wait()
        for s in range(1, sent_ref.shape[0]):
            ride(s).wait()


def attend(
    x, gain, own_weight, other_weight, bias, seg, out_weight, x_own, moe_gain, scale, members, identity,
    which, rider, routes=None, pair_shape=None,
):
    micros, half, width = x.shape
    cols = own_weight.shape[2]
    heads = bias.shape[0] // 2
    shard_len = half // members
    mine = pl.BlockSpec(
        (1, 1, shard_len, width), lambda m, p: (which, 0, 0, 0), pipeline_mode=pl.Buffered(1)
    )
    riders, ride_specs = [rider], [any_space()]
    ride_out, ride_out_specs = [jax.ShapeDtypeStruct(rider.shape, BF16)], [any_space()]
    if routes is not None:
        riders.append(routes)
        ride_specs.append(pl.BlockSpec(memory_space=pltpu.VMEM))
        ride_out.append(jax.ShapeDtypeStruct(pair_shape, BF16))
        ride_out_specs.append(pl.BlockSpec(memory_space=pltpu.VMEM))
    ride_sems = [pltpu.SemaphoreType.DMA((rider.shape[0],))] * 2 + [pltpu.SemaphoreType.DMA]

    def once(shape):
        return pl.BlockSpec(shape, lambda m, p: (0,) * len(shape), pipeline_mode=pl.Buffered(1))

    return pl.pallas_call(
        functools.partial(attend_kernel, scale),
        grid=(micros, 2),
        out_shape=(
            jax.ShapeDtypeStruct((micros, 2, 3, half, cols), BF16),
            jax.ShapeDtypeStruct((micros, 2, heads, half, half), BF16),
            jax.ShapeDtypeStruct((micros, half, 2 * cols), BF16),
            jax.ShapeDtypeStruct((micros, shard_len, width), F32),
            jax.ShapeDtypeStruct((micros, shard_len, width), BF16),
        )
        + tuple(ride_out),
        in_specs=[
            pl.BlockSpec((1, half, width), lambda m, p: (m, 0, 0)),
            once((1, width)),
            once((3, width, cols)),
            once((3, width, cols)),
            pl.BlockSpec((heads,) + bias.shape[1:], lambda m, p: (p, 0, 0)),
            pl.BlockSpec((1, 1, half), lambda m, p: (m, 0, 0)),
            pl.BlockSpec((1, half, 1), lambda m, p: (m, 0, 0)),
            once(out_weight.shape),
            mine,
            once((1, width)),
        ]
        + ride_specs,
        out_specs=(
            pl.BlockSpec((1, 1, 3, half, cols), lambda m, p: (m, p, 0, 0, 0)),
            pl.BlockSpec((1, 1, heads, half, half), lambda m, p: (m, p, 0, 0, 0)),
            pl.BlockSpec((1, half, cols), lambda m, p: (m, 0, p)),
            pl.BlockSpec((micros, shard_len, width), lambda m, p: (0, 0, 0)),
            pl.BlockSpec((micros, shard_len, width), lambda m, p: (0, 0, 0)),
        )
        + tuple(ride_out_specs),
        scratch_shapes=[
            pltpu.VMEM((half, width), BF16),
            pltpu.VMEM((micros, members, shard_len, 2 * cols), BF16),
            pltpu.VMEM((micros, members, shard_len, 2 * cols), BF16),
            pltpu.SemaphoreType.DMA((micros, members)),
            pltpu.SemaphoreType.DMA((micros, members)),
        ]
        + ride_sems,
        compiler_params=pltpu.CompilerParams(
            vmem_limit_bytes=VMEM_LIMIT, collective_id=identity, has_side_effects=True
        ),
        cost_estimate=pl.CostEstimate(
            flops=micros * 2 * half * cols * (8 * width + 4 * half),
            bytes_accessed=100000000,
            transcendentals=micros * 2 * heads * half * half,
        ),
        name="attend",
    )(
        x, gain, own_weight, other_weight, bias, seg.reshape(micros, 1, half),
        seg.reshape(micros, half, 1), out_weight, x_own, moe_gain, *riders,
    )


def back_kernel(scale, micros, *refs):
    moe_gain_ref, gain_ref, out_ref, own_ref, other_ref = refs[:5]
    inputs = [refs[5 + 8 * m : 13 + 8 * m] for m in range(micros)]
    sent_ref, refs = refs[5 + 8 * micros], refs[6 + 8 * micros :]
    (
        xgrad_ref, arrived_ref, grads_ref, line_ref, dmoe_ref, dgain_ref,
        dh1_ref, dattn_all, dheads_part, dheads_all, dxn_part, dxn_got, total_ref, xn_ref, ds_ref,
        dproj_ref, sheet_ref, attn_send, attn_recv, heads_send, heads_recv, dxn_send, dxn_recv,
        ride_send, ride_recv, ride_own,
    ) = refs
    devices = sent_ref.shape[0]
    _, members, shard_len, width = dattn_all.shape
    cols = dproj_ref.shape[2]
    half = members * shard_len
    length = sheet_ref.shape[1]
    group, micro = pl.program_id(0), pl.program_id(1)
    me = lax.axis_index("expert")
    line = lax.axis_index("hidden")
    mine = lax.rem(line, members)
    part = line // members
    base = line - mine
    steps = range(1, members)

    def peer_of(s):
        return lax.rem(mine + s, members)

    def attn_copy(m, s):
        return remote(
            dattn_all.at[m, mine], dattn_all.at[m, mine], attn_send.at[m, s], attn_recv.at[m, s],
            (me, base + peer_of(s)),
        )

    def heads_copy(m, s):
        return remote(
            dheads_part.at[m, peer_of(s)], dheads_all.at[m, mine], heads_send.at[m, s],
            heads_recv.at[m, s], (me, base + peer_of(s)),
        )

    def dxn_copy(m, s):
        return remote(
            dxn_part.at[m, peer_of(s)], dxn_got.at[m, mine], dxn_send.at[m, s], dxn_recv.at[m, s],
            (me, base + peer_of(s)),
        )

    def ride(s):
        peer = partner_of(me, s, devices)
        return remote(
            sent_ref.at[peer], arrived_ref.at[me], ride_send.at[s], ride_recv.at[s], (peer, line)
        )

    def stay():
        return pltpu.make_async_copy(sent_ref.at[me], arrived_ref.at[me], ride_own)

    @pl.when((group == 0) & (micro == 0))
    def _():
        peers = [(me, base + peer_of(s)) for s in steps]
        greet(peers + [(partner_of(me, s, devices), line) for s in range(1, devices)])
        stay().start()
        for s in range(1, devices):
            ride(s).start()
        dmoe_ref[...] = jnp.zeros_like(dmoe_ref)
        dgain_ref[...] = jnp.zeros_like(dgain_ref)
        for m in range(micros):
            grad_ref, h1_ref, dy_ref = inputs[m][:3]
            grad = grad_ref[...].astype(F32)
            h1 = h1_ref[...]
            r2 = lax.rsqrt(jnp.mean(h1 * h1, axis=-1, keepdims=True) + EPSILON)
            unit = h1 * r2
            dmoe_ref[...] += jnp.sum(grad * unit, axis=0, keepdims=True)
            weighted = grad * moe_gain_ref[...]
            inner = jnp.mean(weighted * unit, axis=-1, keepdims=True)
            dh1 = dy_ref[0, 0].astype(F32) + r2 * (weighted - unit * inner)
            dh1_ref[m] = dh1
            dattn = dh1.astype(BF16)
            dattn_all[m, mine] = dattn
            for member in range(members):
                for j in range(2):
                    index = lax.rem(part + j, 2) * members + member
                    dheads = mm_nt(dattn, out_ref[index]).astype(BF16)
                    dheads_part[m, member, :, j * cols : (j + 1) * cols] = dheads
            for s in steps:
                heads_copy(m, s).start()
            dheads_all[m, mine] = dheads_part[m, mine]
        for m in range(micros):
            xn_ref[m] = (unit_rows(inputs[m][4][...]) * gain_ref[...]).astype(BF16)

    def products(weight_ref):
        dxn = mm_nt(dproj_ref[0], weight_ref[0])
        for t in range(1, 3):
            dxn = dxn + mm_nt(dproj_ref[t], weight_ref[t])
        return dxn.reshape(members, shard_len, width)

    per = grads_ref.shape[0] // 4
    for g in range(2):
        for m in range(micros):

            @pl.when((group == g) & (micro == m))
            def _(g=g, m=m):
                x_ref, qkv_ref, prob_ref, heads_ref = inputs[m][4:]
                heads = prob_ref.shape[1]
                size = cols // heads
                if g == 0:
                    for s in steps:
                        heads_copy(m, s).wait_recv()
                    for s in steps:
                        attn_copy(m, s).start()
                for head in range(heads):
                    inner_cols = slice(head * size, (head + 1) * size)
                    outer_cols = slice(g * cols + head * size, g * cols + (head + 1) * size)
                    values = qkv_ref[0, 2, :, inner_cols]
                    grads = dheads_all[m, :, :, outer_cols].reshape(half, size)
                    sheet_ref[...] = jnp.zeros_like(sheet_ref)
                    for start in range(0, half, TILE):
                        rows = slice(start, start + TILE)
                        prob = prob_ref[0, head, rows, :].astype(F32)
                        dprob = mm_nt(grads[rows], values)
                        inner = jnp.sum(prob * dprob, axis=-1, keepdims=True)
                        dscore = (prob * (dprob - inner)).astype(BF16)
                        ds_ref[rows, :] = dscore
                        dscore = dscore.astype(F32)
                        sheet_ref[:, : half - start] += dscore[:, start:]
                        if start:
                            sheet_ref[:, length - start :] += dscore[:, :start]
                    dscores = ds_ref[...]
                    keys, queries = qkv_ref[0, 1, :, inner_cols], qkv_ref[0, 0, :, inner_cols]
                    dproj_ref[0, :, inner_cols] = (mm(dscores, keys) * scale).astype(BF16)
                    dproj_ref[1, :, inner_cols] = (mm_tn(dscores, queries) * scale).astype(BF16)
                    dproj_ref[2, :, inner_cols] = mm_tn(prob_ref[0, head], grads).astype(BF16)
                    sheet = sheet_ref[...]
                    while sheet.shape[0] > 8:
                        upper = sheet.shape[0] // 2
                        sheet = sheet[:upper] + pltpu.roll(sheet[upper:], length - upper, 1)
                    row = lax.broadcasted_iota(jnp.int32, (8, length), 0)
                    found = jnp.zeros((1, length), F32)
                    for r in range(8):
                        moved = pltpu.roll(sheet, length - r, 1) if r else sheet
                        found = found + jnp.sum(
                            jnp.where(row == r, moved, 0.0), axis=0, keepdims=True
                        )
                    if m:
                        found = found + line_ref[0, head : head + 1, :]
                    line_ref[0, head : head + 1, :] = found
                if g == 0:
                    total_ref[m] = products(own_ref)
                    for s in steps:
                        attn_copy(m, s).wait_recv()
                else:
                    total = total_ref[m] + products(other_ref)
                    total_ref[m] = total
                    dxn_part[m] = total.astype(BF16)
                    for s in steps:
                        dxn_copy(m, s).start()
                    total = total.reshape(half, width)
                    dgain_ref[...] += jnp.sum(total * unit_rows(x_ref[...]), axis=0, keepdims=True)
                for t in range(4):
                    if t < 3:
                        found = mm_tn(xn_ref[m], dproj_ref[t])
                    else:
                        found = mm_tn(dattn_all[m].reshape(half, width), heads_ref[...])
                    found = found.reshape(per, 1, width // per, cols)
                    if m:
                        found = found + grads_ref[t * per : (t + 1) * per].astype(F32)
                    grads_ref[t * per : (t + 1) * per] = found.astype(BF16)

    @pl.when((group == 1) & (micro == micros - 1))
    def _():
        for m in range(micros):
            x_own = inputs[m][3][0, 0].astype(F32)
            r1 = lax.rsqrt(jnp.mean(x_own * x_own, axis=-1, keepdims=True) + EPSILON)
            unit = x_own * r1
            for s in steps:
                dxn_copy(m, s).wait_recv()
            dxn1 = total_ref[m, mine]
            for s in steps:
                dxn1 = dxn1 + dxn_got[m, lax.rem(mine + members - s, members)].astype(F32)
            weighted = dxn1 * gain_ref[...]
            inner = jnp.mean(weighted * unit, axis=-1, keepdims=True)
            xgrad_ref[m] = (dh1_ref[m] + r1 * (weighted - unit * inner)).astype(BF16)
        for m in range(micros):
            for s in steps:
                heads_copy(m, s).wait_send()
                attn_copy(m, s).wait_send()
                dxn_copy(m, s).wait_send()
        stay().wait()
        for s in range(1, devices):
            ride(s).wait()


def attend_back(
    moe_gain, gain, out_weight, own_weight, other_weight, kept, rider, scale, pieces, members
):
    micros = len(kept)
    _, heads, half = kept[0][6].shape[:3]
    width, cols = own_weight.shape[1:]
    shard_len = half // members
    length = 2 * half
    rows = 4 * width // pieces

    def once(array):
        return pl.BlockSpec(
            array.shape, lambda p, m: (0,) * array.ndim, pipeline_mode=pl.Buffered(1)
        )

    operands = [moe_gain, gain, out_weight, own_weight, other_weight]
    in_specs = [once(array) for array in operands]
    for micro, arrays in enumerate(kept):
        operands.extend(arrays)
        grad, h1, _, _, x_half = [once(array) for array in arrays[:5]]
        mine = pl.BlockSpec(
            (1, 1, shard_len, width), lambda p, m, which=micro: (which, 0, 0, 0),
            pipeline_mode=pl.Buffered(1),
        )
        in_specs += [grad, h1, mine, mine, x_half] + [
            pl.BlockSpec((1, 3, half, cols), lambda p, m: (p, 0, 0, 0)),
            pl.BlockSpec((1, heads, half, half), lambda p, m: (p, 0, 0, 0)),
            pl.BlockSpec((half, cols), lambda p, m: (0, p)),
        ]
    operands.append(rider)
    in_specs.append(any_space())
    dma = pltpu.SemaphoreType.DMA((micros, members))
    ride_dma = pltpu.SemaphoreType.DMA((rider.shape[0],))
    return pl.pallas_call(
        functools.partial(back_kernel, scale, micros),
        grid=(2, micros),
        out_shape=(
            jax.ShapeDtypeStruct((micros, shard_len, width), BF16),
            jax.ShapeDtypeStruct(rider.shape, BF16),
            jax.ShapeDtypeStruct((pieces, 2, rows, cols), BF16),
            jax.ShapeDtypeStruct((2, heads, length), F32),
            jax.ShapeDtypeStruct((1, width), F32),
            jax.ShapeDtypeStruct((1, width), F32),
        ),
        in_specs=in_specs,
        out_specs=(
            pl.BlockSpec((micros, shard_len, width), lambda p, m: (0, 0, 0)),
            any_space(),
            pl.BlockSpec((pieces, 1, rows, cols), lambda p, m: (0, p, 0, 0)),
            pl.BlockSpec((1, heads, length), lambda p, m: (p, 0, 0)),
            pl.BlockSpec((1, width), lambda p, m: (0, 0)),
            pl.BlockSpec((1, width), lambda p, m: (0, 0)),
        ),
        scratch_shapes=[
            pltpu.VMEM((micros, shard_len, width), F32),
            pltpu.VMEM((micros, members, shard_len, width), BF16),
            pltpu.VMEM((micros, members, shard_len, 2 * cols), BF16),
            pltpu.VMEM((micros, members, shard_len, 2 * cols), BF16),
            pltpu.VMEM((micros, members, shard_len, width), BF16),
            pltpu.VMEM((micros, members, shard_len, width), BF16),
            pltpu.VMEM((micros, members, shard_len, width), F32),
            pltpu.VMEM((micros, half, width), BF16),
            pltpu.VMEM((half, half), BF16),
            pltpu.VMEM((3, half, cols), BF16),
            pltpu.VMEM((TILE, length), F32),
            dma, dma, dma, dma, dma, dma, ride_dma, ride_dma, pltpu.SemaphoreType.DMA,
        ],
        compiler_params=pltpu.CompilerParams(
            vmem_limit_bytes=VMEM_LIMIT, collective_id=6, has_side_effects=True
        ),
        cost_estimate=pl.CostEstimate(
            flops=2 * micros * half * cols * (16 * width + 8 * half),
            bytes_accessed=250000000,
            transcendentals=0,
        ),
        name="attend_back",
    )(*operands)


def closing_kernel(
    pieces_ref, small_ref, y_ref, h1_ref, rows_ref, place_ref, first_h1_ref,
    whole_ref, sum_ref, block_ref,
    y_got, y_send, y_recv, half_got, held_ref, quarter_got, total_ref, moved_ref, moved_got, small_got, line_sum,
    line_got, half_sem, quarter_send, quarter_recv, small_send, small_recv, line_send, line_recv,
    moved_sem, on_send, on_recv, own_sem,
):
    chips = pieces_ref.shape[0]
    devices = 2 * chips
    blocks = line_got.shape[0]
    me = lax.axis_index("expert")
    line = lax.axis_index("hidden")
    chip, core = me // 2, lax.rem(me, 2)
    sibling = partner_of(me, 1, devices)
    along = [lax.rem(line + s, blocks) for s in range(1, blocks)]
    across = lax.rem(line + blocks // 2, blocks)
    greet([(partner_of(me, s, devices), line) for s in range(1, devices)] + [(me, z) for z in along])
    share = y_ref.shape[1] // 2
    turns = (pl.ds(0, share), pl.ds(share, y_ref.shape[1] - share))

    def y_copies(turn):
        rows = turns[turn]
        return [
            remote(
                y_ref.at[z, rows], y_got.at[line, rows], y_send.at[turn, s], y_recv.at[turn, s],
                (me, z),
            )
            for s, z in enumerate(along)
        ]

    halves = remote(
        pieces_ref.at[:, 1 - core], half_got, half_sem.at[0], half_sem.at[1], (sibling, line)
    )
    halves.start()
    for copy in y_copies(0):
        copy.start()
    smalls = [
        remote(
            small_ref, small_got.at[me], small_send.at[s], small_recv.at[s],
            (partner_of(me, s, devices), line),
        )
        for s in range(1, devices)
    ]
    for copy in smalls:
        copy.start()
    small_got[me] = small_ref[...]
    block_ref[0] = (first_h1_ref[...] + collect(rows_ref, place_ref)).astype(BF16)
    halves.wait_recv()
    steps = range(1, chips)

    def quarter(s):
        other = partner_of(chip, s, chips)
        return remote(
            held_ref.at[other], quarter_got.at[s], quarter_send.at[s], quarter_recv.at[s],
            (partner_of(me, 2 * s, devices), line),
        )

    for s in steps:
        other = partner_of(chip, s, chips)
        held = pieces_ref[other, core].astype(F32) + half_got[other].astype(F32)
        held_ref[other] = held.astype(BF16)
        quarter(s).start()
    total_ref[...] = pieces_ref[chip, core].astype(F32) + half_got[chip].astype(F32)
    for copy in smalls:
        copy.wait_recv()
    line_sum[...] = jnp.sum(small_got[...], axis=0)
    lines = [
        remote(line_sum, line_got.at[line], line_send.at[s], line_recv.at[s], (me, z))
        for s, z in enumerate(along)
    ]
    for copy in lines:
        copy.start()
    line_got[line] = line_sum[...]
    for s in steps:
        quarter(s).wait_recv()
        total_ref[...] += quarter_got[s].astype(F32)
    moved_ref[...] = total_ref[1].astype(BF16)
    cross = remote(moved_ref, moved_got, moved_sem.at[0], moved_sem.at[1], (me, across))
    cross.start()
    cross.wait_recv()
    for copy in y_copies(1):
        copy.start()
    whole_ref[chip, core] = (total_ref[0] + moved_got[...].astype(F32)).astype(BF16)
    onward = [
        remote(
            whole_ref.at[chip, core], whole_ref.at[chip, core], on_send.at[s], on_recv.at[s],
            (partner_of(me, 2 * s, devices), line),
        )
        for s in steps
    ]
    for copy in onward:
        copy.start()
    for copy in lines:
        copy.wait_recv()
    sum_ref[...] = jnp.sum(line_got[...], axis=0)
    for copy in onward:
        copy.wait_recv()
    y_got[line] = y_ref[line]
    last = remote(
        whole_ref.at[:, core], whole_ref.at[:, core], on_send.at[0], on_recv.at[0], (sibling, line)
    )
    last.start()
    for copy in y_copies(0) + y_copies(1):
        copy.wait_recv()
    block_ref[1] = (h1_ref[...] + jnp.sum(y_got[...].astype(F32), axis=0)).astype(BF16)
    for copy in y_copies(0) + y_copies(1):
        copy.wait_send()
    halves.wait_send()
    for s in steps:
        quarter(s).wait_send()
    cross.wait_send()
    for copy in smalls + lines + onward:
        copy.wait_send()
    last.wait()


def closing(pieces, small, y, h1, rows_first, place, first_h1):
    devices, both, rows, cols = pieces.shape
    blocks = y.shape[0]
    chips = devices // 2
    vmem = pl.BlockSpec(memory_space=pltpu.VMEM)
    dma = pltpu.SemaphoreType.DMA
    return pl.pallas_call(
        closing_kernel,
        out_shape=(
            jax.ShapeDtypeStruct((chips, 2, rows, cols), BF16),
            jax.ShapeDtypeStruct(small.shape, F32),
            jax.ShapeDtypeStruct((2,) + h1.shape, BF16),
        ),
        in_specs=[vmem] * 7,
        out_specs=(vmem,) * 3,
        scratch_shapes=[
            pltpu.VMEM(y.shape, BF16),
            dma((2, blocks)),
            dma((2, blocks)),
            pltpu.VMEM((chips, both, rows, cols), BF16),
            pltpu.VMEM((chips, both, rows, cols), BF16),
            pltpu.VMEM((chips, both, rows, cols), BF16),
            pltpu.VMEM((both, rows, cols), F32),
            pltpu.VMEM((rows, cols), BF16),
            pltpu.VMEM((rows, cols), BF16),
            pltpu.VMEM((devices,) + small.shape, F32),
            pltpu.VMEM(small.shape, F32),
            pltpu.VMEM((blocks,) + small.shape, F32),
            dma((2,)), dma((chips,)), dma((chips,)), dma((devices,)), dma((devices,)),
            dma((blocks,)), dma((blocks,)), dma((2,)), dma((chips,)), dma((chips,)), dma,
        ],
        compiler_params=pltpu.CompilerParams(
            vmem_limit_bytes=VMEM_LIMIT, collective_id=3, has_side_effects=True
        ),
        cost_estimate=pl.CostEstimate(flops=0, bytes_accessed=160000000, transcendentals=0),
        name="closing",
    )(pieces.reshape(chips, 2, both, rows, cols), small, y, h1, rows_first, place, first_h1)


def spread(rows, place0, place1, count):
    ids = lax.broadcasted_iota(jnp.int32, (count, rows.shape[0]), 0)
    hit = (ids == place0) | (ids == place1)
    return mm(jnp.where(hit, 1.0, 0.0).astype(BF16), rows)


def spread_kernel(rows_ref, place_ref, out_ref):
    experts, _, cap, width = out_ref.shape
    placed = spread(rows_ref[0], place_ref[0:1, :], place_ref[1:2, :], experts * cap)
    out_ref[...] = placed.astype(BF16).reshape(experts, 1, cap, width)


def spread_rows(rows, micro, place, experts, cap, shard_len):
    _, slots, width = rows.shape
    blocks = slots // shard_len
    return pl.pallas_call(
        spread_kernel,
        grid=(blocks,),
        out_shape=jax.ShapeDtypeStruct((experts, blocks, cap, width), BF16),
        in_specs=[
            pl.BlockSpec((1, shard_len, width), lambda b: (micro, b, 0)),
            pl.BlockSpec((2, shard_len), lambda b: (0, b)),
        ],
        out_specs=pl.BlockSpec((experts, 1, cap, width), lambda b: (0, b, 0, 0)),
        compiler_params=pltpu.CompilerParams(vmem_limit_bytes=VMEM_LIMIT),
        cost_estimate=pl.CostEstimate(
            flops=2 * experts * cap * slots * width,
            bytes_accessed=2 * slots * width + 2 * experts * blocks * cap * width,
            transcendentals=0,
        ),
        name="spread_rows",
    )(rows, place)


def collect_kernel(rows_ref, place_ref, out_ref):
    out_ref[...] = collect(rows_ref, place_ref).astype(BF16)


def collect_rows(rows, place, shard_len):
    experts, blocks, cap, width = rows.shape
    slots = blocks * shard_len
    return pl.pallas_call(
        collect_kernel,
        grid=(blocks,),
        out_shape=jax.ShapeDtypeStruct((slots, width), BF16),
        in_specs=[
            pl.BlockSpec((experts, 1, cap, width), lambda b: (0, b, 0, 0)),
            pl.BlockSpec((2, shard_len), lambda b: (0, b)),
        ],
        out_specs=pl.BlockSpec((shard_len, width), lambda b: (b, 0)),
        compiler_params=pltpu.CompilerParams(vmem_limit_bytes=VMEM_LIMIT),
        cost_estimate=pl.CostEstimate(
            flops=2 * experts * cap * slots * width,
            bytes_accessed=2 * slots * width + 2 * experts * blocks * cap * width,
            transcendentals=0,
        ),
        name="collect_rows",
    )(rows, place)


def place_kernel(cap, experts, route_ref, place_ref):
    blocks, micros, _, shard_len = route_ref.shape
    for block in range(blocks):
        for micro in range(micros):
            _, found = places(route_ref, (block, micro), cap, experts)
            for k in range(2):
                lanes = slice(block * shard_len, (block + 1) * shard_len)
                place_ref[micro, k : k + 1, lanes] = found[k]


def find_places(route, experts, cap):
    blocks, micros, _, shard_len = route.shape
    vmem = pl.BlockSpec(memory_space=pltpu.VMEM)
    return pl.pallas_call(
        functools.partial(place_kernel, cap, experts),
        out_shape=jax.ShapeDtypeStruct((micros, 2, blocks * shard_len), jnp.int32),
        in_specs=[vmem],
        out_specs=vmem,
        compiler_params=pltpu.CompilerParams(vmem_limit_bytes=VMEM_LIMIT),
        name="find_places",
    )(route)


def expert_kernel(
    by_block, sent_ref, dy_ref, pair_ref, wr_ref, wg_ref, wu_ref, wd_ref,
    back_ref, y_ref, x_ref, g_ref, hid_ref, dga_ref, dup_ref, dlog_ref,
    got_ref, dx_ref, stage_ref, x_send, x_recv, dx_send, dx_recv, own_sem, stage_sem,
):
    devices, experts, cap, width = sent_ref.shape
    step = pl.program_id(0)
    me = lax.axis_index("expert")
    line = lax.axis_index("hidden")
    first_wave = bits_of(devices)
    rest = [s for s in range(1, devices) if s not in first_wave]
    later_waves = [rest[i : i + 2] for i in range(0, len(rest), 2)]

    def x_copy(s):
        peer = partner_of(me, s, devices)
        return pltpu.make_async_remote_copy(
            src_ref=sent_ref.at[peer], dst_ref=got_ref.at[s], send_sem=x_send.at[s],
            recv_sem=x_recv.at[s], device_id=(peer, line), device_id_type=pl.DeviceIdType.MESH,
        )

    def dx_copy(s):
        peer = partner_of(me, s, devices)
        return pltpu.make_async_remote_copy(
            src_ref=dx_ref.at[s], dst_ref=back_ref.at[me], send_sem=dx_send.at[s],
            recv_sem=dx_recv.at[s], device_id=(peer, line), device_id_type=pl.DeviceIdType.MESH,
        )

    blocks, share = stage_ref.shape[2:4]

    def y_copies(s):
        source = partner_of(me, s, devices)
        slot = lax.rem(s, 2)
        if not by_block[1]:
            return [
                pltpu.make_async_copy(stage_ref.at[slot], y_ref.at[source], stage_sem.at[slot, 0])
            ]
        return [
            pltpu.make_async_copy(
                stage_ref.at[slot, e], y_ref.at[:, source, e], stage_sem.at[slot, e]
            )
            for e in range(experts)
        ]

    def work(s):
        source = partner_of(me, s, devices)
        slot = lax.rem(s, 2)
        for e in range(experts):
            x = got_ref[s, e]
            dy = dy_ref[:, source, e] if by_block[0] else dy_ref[source, e]
            dy = dy.reshape(cap, width).astype(F32)
            pair = pair_ref[source, e].astype(F32)
            margin = jnp.sum(mm_nt(x, wr_ref[...]) * pair, axis=-1, keepdims=True)
            own_gate = 1.0 / (1.0 + jnp.exp(-margin))
            other_gate = 1.0 / (1.0 + jnp.exp(margin))
            g = (own_gate * dy).astype(BF16)
            x_ref[0, e] = x
            g_ref[0, e] = g
            gate = mm_nt(x, wg_ref[e])
            up = mm_nt(x, wu_ref[e])
            square = gate * gate
            bent = jnp.tanh(GELU_C * gate * (1.0 + GELU_A * square))
            half_gate = 0.5 * gate
            gelu = half_gate * (1.0 + bent)
            slope = 0.5 * (1.0 + bent) + half_gate * (1.0 - bent * bent) * (
                GELU_C * (1.0 + 3.0 * GELU_A * square)
            )
            hid = (gelu * up).astype(BF16)
            dhid = mm_nt(g, wd_ref[e])
            dga = (dhid * (up * slope)).astype(BF16)
            dup = (dhid * gelu).astype(BF16)
            hid_ref[0, e] = hid
            dga_ref[0, e] = dga
            dup_ref[0, e] = dup
            y = mm(hid, wd_ref[e])
            dgate = jnp.sum(y * dy, axis=-1, keepdims=True)
            stage_ref[slot, e] = (y * own_gate).astype(BF16).reshape(blocks, share, width)
            dlog = (dgate * own_gate * other_gate * pair).astype(BF16)
            dlog_ref[0, e] = dlog
            dx = mm(dga, wg_ref[e]) + mm(dup, wu_ref[e]) + mm(dlog, wr_ref[...])
            dx_ref[s, e] = dx.astype(BF16)

    @pl.when(step == 0)
    def _():
        barrier = pltpu.get_barrier_semaphore()
        for s in range(1, devices):
            pl.semaphore_signal(
                barrier, inc=1, device_id=(partner_of(me, s, devices), line),
                device_id_type=pl.DeviceIdType.MESH,
            )
        pl.semaphore_wait(barrier, devices - 1)
        for s in first_wave:
            x_copy(s).start()
        own = pltpu.make_async_copy(sent_ref.at[me], got_ref.at[0], own_sem)
        own.start()
        own.wait()

    @pl.when(step > 0)
    def _():
        x_copy(step).wait_recv()

    for index, wave in enumerate(later_waves):

        @pl.when(step == 2 + index)
        def _(wave=wave):
            for s in wave:
                x_copy(s).start()

    @pl.when(step > 1)
    def _():
        for copy in y_copies(step - 2):
            copy.wait()

    work(step)
    for copy in y_copies(step):
        copy.start()

    @pl.when(step > 0)
    def _():
        dx_copy(step).start()

    @pl.when(step == devices - 1)
    def _():
        own = pltpu.make_async_copy(dx_ref.at[0], back_ref.at[me], own_sem)
        own.start()
        own.wait()
        for copy in y_copies(devices - 2) + y_copies(devices - 1):
            copy.wait()
        for s in range(1, devices):
            x_copy(s).wait_send()
            dx_copy(s).wait_send()
            dx_copy(s).wait_recv()


def expert_pass(sent, dy, pair, wr, wg, wu, wd, by_block, identity):
    share = dy.shape[3]
    blocks = sent.shape[2] // share
    devices, experts, cap, width = sent.shape
    hidden = wg.shape[1]
    choices = wr.shape[0]

    def whole(shape):
        return pl.BlockSpec(shape, lambda s: (0,) * len(shape), pipeline_mode=pl.Buffered(1))

    def block(cols):
        return pl.BlockSpec((1, experts, cap, cols), lambda s: (s, 0, 0, 0))

    def kept(cols):
        return jax.ShapeDtypeStruct((devices, experts, cap, cols), BF16)

    y_shape = (blocks, devices, experts, share, width)
    if not by_block[1]:
        y_shape = (devices, experts, blocks, share, width)
    return pl.pallas_call(
        functools.partial(expert_kernel, by_block),
        grid=(devices,),
        out_shape=(
            kept(width), jax.ShapeDtypeStruct(y_shape, BF16), kept(width), kept(width), kept(hidden), kept(hidden),
            kept(hidden), kept(choices),
        ),
        in_specs=[
            any_space(), whole(dy.shape), whole(pair.shape), whole(wr.shape), whole(wg.shape),
            whole(wu.shape), whole(wd.shape),
        ],
        out_specs=(
            any_space(), any_space(), block(width), block(width), block(hidden), block(hidden),
            block(hidden), block(choices),
        ),
        scratch_shapes=[
            pltpu.VMEM((devices, experts, cap, width), BF16),
            pltpu.VMEM((devices, experts, cap, width), BF16),
            pltpu.VMEM((2, experts, blocks, share, width), BF16),
            pltpu.SemaphoreType.DMA((devices,)),
            pltpu.SemaphoreType.DMA((devices,)),
            pltpu.SemaphoreType.DMA((devices,)),
            pltpu.SemaphoreType.DMA((devices,)),
            pltpu.SemaphoreType.DMA,
            pltpu.SemaphoreType.DMA((2, experts)),
        ],
        compiler_params=pltpu.CompilerParams(
            vmem_limit_bytes=VMEM_LIMIT, collective_id=identity, has_side_effects=True
        ),
        cost_estimate=pl.CostEstimate(flops=0, bytes_accessed=490000000, transcendentals=0),
        name="expert_pass",
    )(sent, dy, pair, wr, wg, wu, wd)


def weight_kernel(*refs):
    count = (len(refs) - 4) // 6
    dwr_ref, dwg_ref, dwu_ref, dwd_ref = refs[-4:]
    totals = [0.0, 0.0, 0.0, 0.0]
    for index in range(count):
        blocks = [
            ref[...].reshape(ref.shape[0] * ref.shape[2], ref.shape[3])
            for ref in refs[6 * index : 6 * index + 6]
        ]
        x, g, hid, dga, dup, dlog = blocks
        totals[0] = totals[0] + mm_tn(dlog, x)
        totals[1] = totals[1] + mm_tn(dga, x)
        totals[2] = totals[2] + mm_tn(dup, x)
        totals[3] = totals[3] + mm_tn(hid, g)
    dwr_ref[0] = totals[0]
    dwg_ref[0] = totals[1]
    dwu_ref[0] = totals[2]
    dwd_ref[0] = totals[3]


def weight_pass(kept):
    sources, experts, cap, width = kept[0][0].shape
    hidden = kept[0][2].shape[3]
    choices = kept[0][5].shape[3]
    rows = sources * cap
    block = 256 if width % 256 == 0 else width
    tokens = pl.BlockSpec((sources, 1, cap, block), lambda e, j: (0, e, 0, j))
    acts = pl.BlockSpec((sources, 1, cap, hidden), lambda e, j: (0, e, 0, 0))
    logs = pl.BlockSpec((sources, 1, cap, choices), lambda e, j: (0, e, 0, 0))
    operands = []
    for arrays in kept:
        operands.extend(arrays)
    return pl.pallas_call(
        weight_kernel,
        grid=(experts, width // block),
        out_shape=(
            jax.ShapeDtypeStruct((experts, choices, width), F32),
            jax.ShapeDtypeStruct((experts, hidden, width), F32),
            jax.ShapeDtypeStruct((experts, hidden, width), F32),
            jax.ShapeDtypeStruct((experts, hidden, width), F32),
        ),
        in_specs=[tokens, tokens, acts, acts, acts, logs] * len(kept),
        out_specs=(
            pl.BlockSpec((1, choices, block), lambda e, j: (e, 0, j)),
            pl.BlockSpec((1, hidden, block), lambda e, j: (e, 0, j)),
            pl.BlockSpec((1, hidden, block), lambda e, j: (e, 0, j)),
            pl.BlockSpec((1, hidden, block), lambda e, j: (e, 0, j)),
        ),
        compiler_params=pltpu.CompilerParams(vmem_limit_bytes=VMEM_LIMIT),
        cost_estimate=pl.CostEstimate(
            flops=6 * len(kept) * experts * rows * width * hidden,
            bytes_accessed=len(kept) * experts * rows * (4 * width + 6 * hidden)
            + 12 * experts * width * hidden,
            transcendentals=0,
        ),
        name="weight_pass",
    )(*operands)


def after(values, *others):
    return lax.optimization_barrier((values,) + others)[0]


def shards(
    x_in,
    cotangent,
    segment_ids,
    routes,
    qkv_weight,
    out_weight,
    bias_table,
    attn_gain,
    moe_gain,
    router_weight,
    gate_weight,
    up_weight,
    down_weight,
):
    micro_count, _, shard_len, width = x_in.shape
    slot_count = segment_ids.shape[2]
    head_cols = out_weight.shape[0]
    bucket_count, heads_here = bias_table.shape
    head_size = head_cols // heads_here
    expert_count = router_weight.shape[1]
    experts_here = gate_weight.shape[0]
    devices = expert_count // experts_here
    blocks = slot_count // shard_len
    members = blocks // 2
    half = slot_count // 2
    capacity = max(2, (10 * shard_len + 4 * expert_count - 1) // (4 * expert_count))
    scale = head_size ** (-0.5)
    hidden_index = lax.axis_index("hidden")
    expert_index = lax.axis_index("expert")
    part = hidden_index // members
    attn_gain_f = attn_gain.astype(F32).reshape(1, width)
    moe_gain_f = moe_gain.astype(F32).reshape(1, width)
    token_shape = (devices, experts_here, blocks * capacity, width)
    flat_shape = (devices, experts_here * blocks * capacity, width)
    place_shape = (expert_count, blocks, capacity, width)
    gate_rows = gate_weight.transpose(0, 2, 1)
    up_rows = up_weight.transpose(0, 2, 1)
    router_rows = router_weight.T

    def exchange(buffer):
        return lax.all_to_all(buffer, "expert", split_axis=0, concat_axis=0, tiled=True)

    def gather(values):
        return lax.all_gather(values, "hidden", axis=0, tiled=True)

    def scatter(values):
        return lax.psum_scatter(values, "hidden", scatter_dimension=0, tiled=True)

    states = [dict() for _ in range(micro_count)]
    own_seg = lax.dynamic_slice_in_dim(segment_ids[:, 0], hidden_index * shard_len, shard_len, 1)
    live_routes = jnp.where(own_seg[:, None, :] >= 0, routes[:, 0].transpose(0, 2, 1), -1)
    own_place = find_places(live_routes[None], expert_count, capacity)

    def spread(rows, micro, placed):
        return spread_rows(rows, micro, placed, expert_count, capacity, shard_len)

    *x_all, other_qkv, all_out, all_routes, other_table = opening(
        x_in[:, 0], qkv_weight.reshape(3 * width, head_cols), out_weight,
        live_routes, bias_table.T.astype(F32), devices, blocks, members,
    )
    x_half = [x.reshape(1, half, width) for x in x_all]
    other_qkv = other_qkv.reshape(qkv_weight.shape)
    all_out = all_out.reshape(blocks, head_cols, width)

    own_routes = lax.dynamic_index_in_dim(all_routes, expert_index, 0, keepdims=False)
    place = find_places(own_routes, expert_count, capacity)

    tables = jnp.concatenate([bias_table.T.astype(F32), other_table], axis=0)
    onehot_bucket = bucket_onehot(half, bucket_count)
    bias = position_bias(jnp.einsum("jb,hb->hj", onehot_bucket, tables, precision=PRECISE))
    seg_half = lax.dynamic_slice_in_dim(segment_ids[:, 0], part * half, half, 1)

    def gather_dy(rows):
        whole = gather(rows.reshape(1, devices * experts_here * capacity, width))
        return whole.reshape(blocks, devices, experts_here, capacity, width)

    def experts(micro, kept, *behind):
        sent = spread(kept["xn2_all"][None], 0, place[micro]).reshape(token_shape)
        kept["by_block"] = (micro > 0, micro + 1 < micro_count)
        back, kept["y"], x, g, hid, dga, dup, dlog = expert_pass(
            after(sent, *behind), kept["dy"], pairs[micro], router_rows, gate_rows, up_rows,
            down_weight, kept["by_block"], 4 + micro,
        )
        kept["weights"] = (x, g, hid, dga, dup, dlog)
        kept["back"] = back
        if micro > 0:
            back = after(back, states[micro - 1]["y_own"])
        kept["dx_back"] = back.reshape(place_shape)
        kept["dx_part"] = collect_rows(kept["dx_back"], place[micro], shard_len)
        kept["dxn2"] = scatter(kept["dx_part"])
        if kept["by_block"][1]:
            parts = after(kept["y"], kept["dx_part"]).reshape(blocks, -1, width)
            kept["y_own"] = scatter(parts).reshape(devices, -1, width)

    first, last = states
    first["dy_all"] = gather(after(cotangent[0, 0], all_out))
    pair_shape = (micro_count, devices, experts_here, blocks, capacity, expert_count)
    for micro, state in enumerate(states):
        inputs = (
            attn_gain_f, qkv_weight, other_qkv, bias, seg_half[micro : micro + 1], all_out,
            x_in, moe_gain_f, scale, members, 10 + micro, micro,
        )
        if micro == 0:
            sent = spread(cotangent[:, 0], 1, own_place[1]).reshape(devices, -1, width)
            qkv, prob, heads, h1, xn2, last["dy_here"] = attend(x_half[0], *inputs, sent)
        else:
            sent = spread(after(first["dy_all"], xn2)[None], 0, place[0]).reshape(token_shape)
            qkv, prob, heads, h1, xn2, first["dy"], pairs = attend(
                after(x_half[1], xn2), *inputs, sent, all_routes, pair_shape
            )
        state.update(qkv=qkv[0], prob=prob[0], heads=heads[0], h1=h1[0], xn2=xn2[0])
    first["dy"] = first["dy"].reshape(devices, experts_here, blocks, capacity, width)
    pairs = pairs.reshape(micro_count, devices, experts_here, blocks * capacity, expert_count)
    behind = ()
    for micro in range(micro_count):
        state = states[micro]
        state["xn2_all"] = gather(after(state["xn2"], *behind))
        behind = (state["xn2_all"],)
    for micro in range(1, micro_count):
        states[micro]["dy"] = gather_dy(after(states[micro]["dy_here"], states[0]["xn2_all"]))
    behind = ()
    for micro in range(micro_count):
        experts(micro, states[micro], *behind)
        behind = (states[micro]["dx_part"],)
    last_part = states[-1]["dx_part"]
    kept = [state["weights"] for state in states]
    kept[-1] = tuple(after(list(kept[-1]), last_part))
    dwr, dwg, dwu, dwd = weight_pass(kept)
    last["y_rows"] = exchange(after(last["y"], last_part).reshape(flat_shape)).reshape(place_shape)
    x_grad, first_rows, grads, lines, moe_gain_grad, attn_gain_grad = attend_back(
        moe_gain_f, attn_gain_f, all_out, qkv_weight, other_qkv,
        [
            (
                after(state["dxn2"], dwr), state["h1"], cotangent, x_in,
                x_half[micro][0], state["qkv"], state["prob"], state["heads"],
            )
            for micro, state in enumerate(states)
        ],
        first["y_own"], scale, devices, members,
    )
    rows = collect_rows(after(last["y_rows"], grads), place[-1], shard_len)
    rows = rows.reshape(blocks, shard_len, width)
    first_rows = first_rows.reshape(expert_count, 1, capacity, width)
    lines = lines.reshape(2 * heads_here, 2 * half)
    table = jnp.einsum("hj,jb->hb", lines, onehot_bucket, precision=PRECISE)
    table = table.reshape(2, heads_here * bucket_count)
    mine = jnp.arange(blocks, dtype=jnp.int32)[:, None]
    table = jnp.where(mine == hidden_index, table[0], 0.0) + jnp.where(
        mine == (hidden_index + members) % blocks, table[1], 0.0
    )
    small = jnp.concatenate(
        [
            jnp.sum(dwr, axis=0).reshape(-1),
            attn_gain_grad.reshape(-1),
            moe_gain_grad.reshape(-1),
            table.reshape(-1),
        ]
    )
    used = small.shape[0]
    small = jnp.pad(small, (0, -used % 1024)).reshape(-1, 128)
    whole, small, block_out = closing(
        grads, small, rows, last["h1"], first_rows, own_place[0], first["h1"]
    )
    whole = whole.reshape(4 * width, head_cols).astype(F32)
    grad_qkv = whole[: 3 * width].reshape(qkv_weight.shape)
    grad_out = whole[3 * width :].T
    small = small.reshape(-1)
    sizes = (width * expert_count, width, width)
    grad_router = small[: sizes[0]].reshape(expert_count, width).T
    grad_attn_gain = small[sizes[0] : sizes[0] + width]
    grad_moe_gain = small[sizes[0] + width : sizes[0] + 2 * width]
    table = small[sizes[0] + 2 * width : used].reshape(blocks, heads_here, bucket_count)
    grad_table = lax.dynamic_index_in_dim(table, hidden_index, 0, keepdims=False).T
    return (
        block_out[:, None],
        x_grad[:, None],
        grad_qkv,
        grad_out,
        grad_table,
        grad_attn_gain,
        grad_moe_gain,
        grad_router,
        dwg.transpose(0, 2, 1),
        dwu.transpose(0, 2, 1),
        dwd,
    )


def solution(mesh):
    return jax.shard_map(
        shards,
        mesh=mesh,
        in_specs=(
            P(None, "expert", "hidden", None),
            P(None, "expert", "hidden", None),
            P(None, "expert", None),
            P(None, "expert", "hidden", None),
            P(None, None, "hidden"),
            P("hidden", None),
            P(None, "hidden"),
            P(),
            P(),
            P(),
            P("expert", None, "hidden"),
            P("expert", None, "hidden"),
            P("expert", "hidden", None),
        ),
        out_specs=(
            P(None, "expert", "hidden", None),
            P(None, "expert", "hidden", None),
            P(None, None, "hidden"),
            P("hidden", None),
            P(None, "hidden"),
            P(),
            P(),
            P(),
            P("expert", None, "hidden"),
            P("expert", None, "hidden"),
            P("expert", "hidden", None),
        ),
        check_vma=False,
    )
```

```python
import functools

import jax
import jax.numpy as jnp
from jax import lax
from jax.experimental import pallas as pl
from jax.experimental.pallas import tpu as pltpu
from jax.sharding import PartitionSpec as P

EPSILON = 1e-06
PRECISE = lax.Precision.HIGHEST
LIMITS = (12, 16, 23, 32, 46, 64, 91)
MASKED = -1000000000.0
GELU_C = 0.7978845608028654
GELU_A = 0.044715
VMEM_LIMIT = 60 * 1024 * 1024
F32 = jnp.float32
BF16 = jnp.bfloat16


def mm(a, b):
    return lax.dot_general(a, b, (((1,), (0,)), ((), ())), preferred_element_type=F32)


def mm_nt(a, b):
    return lax.dot_general(a, b, (((1,), (1,)), ((), ())), preferred_element_type=F32)


def mm_tn(a, b):
    return lax.dot_general(a, b, (((0,), (0,)), ((), ())), preferred_element_type=F32)


def bucket_of(distance):
    magnitude = jnp.abs(distance)
    far_bucket = jnp.full(magnitude.shape, 8, jnp.int32)
    for threshold in LIMITS:
        far_bucket = far_bucket + (magnitude >= threshold).astype(jnp.int32)
    return jnp.where(magnitude < 8, magnitude, far_bucket) + 16 * (distance > 0).astype(jnp.int32)


def bucket_onehot(half, bucket_count):
    lane = jnp.arange(2 * half, dtype=jnp.int32)
    distance = jnp.where(lane < half, lane, lane - 2 * half)
    return (
        bucket_of(distance)[:, None] == jnp.arange(bucket_count, dtype=jnp.int32)[None, :]
    ).astype(F32)


TILE = 128


def bias_kernel(line_ref, out_ref):
    heads, _, length = out_ref.shape
    row = lax.broadcasted_iota(jnp.int32, (8, length), 0)
    for head in range(heads):
        line = jnp.broadcast_to(line_ref[head : head + 1, :], (8, length))
        sheet = line
        for r in range(1, 8):
            sheet = jnp.where(row == r, pltpu.roll(line, r, 1), sheet)
        while sheet.shape[0] < TILE:
            sheet = jnp.concatenate([sheet, pltpu.roll(sheet, sheet.shape[0], 1)], axis=0)
        out_ref[head] = sheet.astype(out_ref.dtype)


def position_bias(line):
    heads, length = line.shape
    vmem = pl.BlockSpec(memory_space=pltpu.VMEM)
    return pl.pallas_call(
        bias_kernel,
        out_shape=jax.ShapeDtypeStruct((heads, TILE, length), BF16),
        in_specs=[vmem],
        out_specs=vmem,
        compiler_params=pltpu.CompilerParams(vmem_limit_bytes=VMEM_LIMIT),
        name="position_bias",
    )(line)


def unit_rows(x):
    x = x.astype(F32)
    return x * lax.rsqrt(jnp.mean(x * x, axis=-1, keepdims=True) + EPSILON)


def remote(src, dst, send_sem, recv_sem, device):
    return pltpu.make_async_remote_copy(
        src_ref=src, dst_ref=dst, send_sem=send_sem, recv_sem=recv_sem,
        device_id=device, device_id_type=pl.DeviceIdType.MESH,
    )


def greet(devices):
    barrier = pltpu.get_barrier_semaphore()
    for device in devices:
        pl.semaphore_signal(
            barrier, inc=1, device_id=device, device_id_type=pl.DeviceIdType.MESH
        )
    pl.semaphore_wait(barrier, len(devices))


def bits_of(count):
    return [1 << b for b in range(count.bit_length() - 1)]


def partner_of(me, step, count):
    found = 0
    for bit in bits_of(count):
        found = found + bit * lax.rem(me // bit + step // bit, 2)
    return found


def any_space():
    return pl.BlockSpec(memory_space=pl.ANY)


def opening_kernel(
    micros, x_ref, qkv_ref, out_ref, routes_ref, table_ref, *refs,
):
    x_all, refs = refs[:micros], refs[micros:]
    (
        qkv_all, out_all, routes_all, table_all,
        x_send, x_recv, qkv_send, qkv_recv, out_send, out_recv, qkv_on_send, qkv_on_recv,
        out_on_send, out_on_recv, routes_send, routes_recv, routes_on_send, routes_on_recv,
        table_send, table_recv, own_sem,
    ) = refs
    devices, qkv_rows = qkv_all.shape[0] * 2, qkv_all.shape[2]
    blocks, out_rows = out_all.shape[0], out_all.shape[3]
    members = x_all[0].shape[0]
    me = lax.axis_index("expert")
    line = lax.axis_index("hidden")
    chip, core = me // 2, lax.rem(me, 2)
    mine = lax.rem(line, members)
    base = line - mine
    along = [lax.rem(line + s, blocks) for s in range(1, blocks)]
    across = lax.rem(line + members, blocks)
    sibling = partner_of(me, 1, devices)
    greet([(partner_of(me, s, devices), line) for s in range(1, devices)] + [(me, z) for z in along])
    own = [
        pltpu.make_async_copy(
            out_ref.at[pl.ds(me * out_rows, out_rows)], out_all.at[line, chip, core], own_sem.at[0]
        ),
        pltpu.make_async_copy(routes_ref, routes_all.at[me, line], own_sem.at[1]),
    ]
    for micro in range(micros):
        own.append(
            pltpu.make_async_copy(x_ref.at[micro], x_all[micro].at[mine], own_sem.at[2 + micro])
        )
    for copy in own:
        copy.start()
    first_qkv = remote(
        qkv_ref.at[pl.ds(me * qkv_rows, qkv_rows)], qkv_all.at[chip, core], qkv_send, qkv_recv,
        (me, across),
    )
    first_qkv.start()
    first_out, first_routes = [], []
    rest = [remote(table_ref, table_all, table_send, table_recv, (me, across))]
    for s, z in enumerate(along):
        first_out.append(
            remote(
                out_ref.at[pl.ds(me * out_rows, out_rows)], out_all.at[line, chip, core],
                out_send.at[s], out_recv.at[s], (me, z),
            )
        )
        first_routes.append(
            remote(
                routes_ref, routes_all.at[me, line], routes_send.at[s], routes_recv.at[s], (me, z)
            )
        )
    for copy in first_routes + first_out + rest:
        copy.start()
    for micro in range(micros):
        for s in range(1, members):
            peer = base + lax.rem(mine + s, members)
            copy = remote(
                x_ref.at[micro], x_all[micro].at[mine], x_send.at[micro, s], x_recv.at[micro, s],
                (me, peer),
            )
            copy.start()
            rest.append(copy)
    first_qkv.wait_recv()
    qkv_on, out_on = [], []
    for s in range(2, devices, 2):
        copy = remote(
            qkv_all.at[chip, core], qkv_all.at[chip, core], qkv_on_send.at[s], qkv_on_recv.at[s],
            (partner_of(me, s, devices), line),
        )
        copy.start()
        qkv_on.append(copy)
    own[1].wait()
    for copy in first_routes:
        copy.wait_recv()
    for s in range(1, devices):
        copy = remote(
            routes_all.at[me], routes_all.at[me], routes_on_send.at[s], routes_on_recv.at[s],
            (partner_of(me, s, devices), line),
        )
        copy.start()
        rest.append(copy)
    own[0].wait()
    for copy in first_out:
        copy.wait_recv()
    for s in range(2, devices, 2):
        copy = remote(
            out_all.at[:, chip, core], out_all.at[:, chip, core], out_on_send.at[s],
            out_on_recv.at[s], (partner_of(me, s, devices), line),
        )
        copy.start()
        out_on.append(copy)
    for copy in qkv_on:
        copy.wait_recv()
    copy = remote(
        qkv_all.at[:, core], qkv_all.at[:, core], qkv_on_send.at[1], qkv_on_recv.at[1],
        (sibling, line),
    )
    copy.start()
    rest.append(copy)
    for copy in out_on:
        copy.wait_recv()
    copy = remote(
        out_all.at[:, :, core], out_all.at[:, :, core], out_on_send.at[1], out_on_recv.at[1],
        (sibling, line),
    )
    copy.start()
    rest.append(copy)
    for copy in own[2:]:
        copy.wait()
    first_qkv.wait_send()
    for copy in first_out + first_routes + qkv_on + out_on:
        copy.wait_send()
    for copy in rest:
        copy.wait()


def opening(x, qkv, out, routes, table, devices, blocks, members):
    micros, shard_len, width = x.shape
    dma = pltpu.SemaphoreType.DMA
    pair = (devices // 2, 2)
    return pl.pallas_call(
        functools.partial(opening_kernel, micros),
        out_shape=(jax.ShapeDtypeStruct((members, shard_len, width), BF16),) * micros
        + (
            jax.ShapeDtypeStruct(pair + (qkv.shape[0] // devices, qkv.shape[1]), BF16),
            jax.ShapeDtypeStruct((blocks,) + pair + (out.shape[0] // devices, width), BF16),
            jax.ShapeDtypeStruct((devices, blocks) + routes.shape, jnp.int32),
            jax.ShapeDtypeStruct(table.shape, table.dtype),
        ),
        in_specs=[any_space()] * 5,
        out_specs=(any_space(),) * (4 + micros),
        scratch_shapes=[
            dma((micros, members)), dma((micros, members)), dma, dma, dma((blocks,)), dma((blocks,)),
            dma((devices,)), dma((devices,)), dma((devices,)), dma((devices,)), dma((blocks,)),
            dma((blocks,)), dma((devices,)), dma((devices,)), dma, dma, dma((2 + micros,)),
        ],
        compiler_params=pltpu.CompilerParams(collective_id=1, has_side_effects=True),
        cost_estimate=pl.CostEstimate(flops=0, bytes_accessed=200000000, transcendentals=0),
        name="opening",
    )(x, qkv, out, routes, table)


def unit_rows(x):
    x = x.astype(F32)
    return x * lax.rsqrt(jnp.mean(x * x, axis=-1, keepdims=True) + EPSILON)


def places(route_ref, index, cap, experts):
    shard_len = route_ref.shape[-1]
    row = lax.broadcasted_iota(jnp.int32, (shard_len, shard_len), 0)
    col = lax.broadcasted_iota(jnp.int32, (shard_len, shard_len), 1)
    earlier = jnp.where(row < col, 1.0, 0.0).astype(BF16)
    ids = lax.broadcasted_iota(jnp.int32, (experts, shard_len), 0)
    pair = [route_ref[index + (slice(k, k + 1),)] for k in range(2)]
    chosen = (ids == pair[0]) | (ids == pair[1])
    before = mm(jnp.where(chosen, 1.0, 0.0).astype(BF16), earlier)
    found = []
    for route in pair:
        position = jnp.sum(jnp.where(ids == route, before, 0.0), axis=0, keepdims=True)
        found.append(jnp.where(route >= 0, route * cap + position.astype(jnp.int32), -1))
    return pair, found


def fill_pairs(route_ref, pair_ref, source, micro, me):
    _, _, here, blocks, cap, experts = pair_ref.shape
    spots = lax.broadcasted_iota(jnp.int32, (cap, route_ref.shape[-1]), 0)
    ids = lax.broadcasted_iota(jnp.int32, (cap, experts), 1)
    for block in range(blocks):
        pair, place = places(route_ref, (source, block, micro), cap, experts)
        for e in range(here):
            expert = me * here + e
            other = jnp.full((cap, 1), -1, jnp.int32)
            for k in range(2):
                hit = spots + expert * cap == place[k]
                found = jnp.max(jnp.where(hit, pair[1 - k], -1), axis=1, keepdims=True)
                other = jnp.maximum(other, found)
            sign = jnp.where(ids == expert, 1.0, 0.0) - jnp.where(ids == other, 1.0, 0.0)
            pair_ref[micro, source, e, block] = jnp.where(other >= 0, sign, 0.0).astype(BF16)


def collect(rows_ref, place_ref):
    experts, _, cap, width = rows_ref.shape
    tokens = place_ref.shape[1]
    ids = lax.broadcasted_iota(jnp.int32, (experts * cap, tokens), 0)
    hit = (ids == place_ref[0:1, :]) | (ids == place_ref[1:2, :])
    rows = rows_ref[...].reshape(experts * cap, width)
    return mm_tn(jnp.where(hit, 1.0, 0.0).astype(BF16), rows)


def attend_kernel(
    scale, x_ref, gain_ref, own_ref, other_ref, bias_ref, seg_row_ref, seg_col_ref,
    out_ref, x_own_ref, moe_gain_ref, *refs,
):
    sent_ref, refs = refs[0], refs[1:]
    pairing = len(refs) > 14
    if pairing:
        routes_ref, pair_ref = refs[0], refs[7]
        refs = refs[1:7] + refs[8:]
    arrived_ref, ride_send, ride_recv, ride_own = refs[5], *refs[-3:]
    refs = refs[:5] + refs[6:-3]
    qkv_ref, prob_ref, heads_ref, h1_ref, xn2_ref, xn_ref, part_ref, got_ref, send_sem, recv_sem = refs
    micros, members, shard_len, both = got_ref.shape
    cols = both // 2
    heads, length = bias_ref.shape[0], bias_ref.shape[2]
    half = members * shard_len
    size = cols // heads
    micro, group = pl.program_id(0), pl.program_id(1)
    me = lax.axis_index("expert")
    line = lax.axis_index("hidden")
    mine = lax.rem(line, members)
    part = line // members
    base = line - mine

    def swap(m, s):
        peer = lax.rem(mine + s, members)
        return remote(
            part_ref.at[m, peer], got_ref.at[m, mine], send_sem.at[m, s], recv_sem.at[m, s],
            (me, base + peer),
        )

    def ride(s):
        peer = partner_of(me, s, sent_ref.shape[0])
        return remote(
            sent_ref.at[peer], arrived_ref.at[me], ride_send.at[s], ride_recv.at[s], (peer, line)
        )

    def stay():
        return pltpu.make_async_copy(sent_ref.at[me], arrived_ref.at[me], ride_own)

    @pl.when((micro == 0) & (group == 0))
    def _():
        peers = [(me, base + lax.rem(mine + s, members)) for s in range(1, members)]
        devices = sent_ref.shape[0]
        peers += [(partner_of(me, s, devices), line) for s in range(1, devices)]
        greet(peers)
        stay().start()
        for s in range(1, devices):
            ride(s).start()

    @pl.when(group == 0)
    def _():
        xn_ref[...] = (unit_rows(x_ref[0]) * gain_ref[...]).astype(BF16)
        for t in range(3):
            qkv_ref[0, 0, t] = mm(xn_ref[...], own_ref[t]).astype(BF16)

    @pl.when(group > 0)
    def _():
        for t in range(3):
            qkv_ref[0, 0, t] = mm(xn_ref[...], other_ref[t]).astype(BF16)

    seg_row = seg_row_ref[0]
    for head in range(heads):
        inner = slice(head * size, (head + 1) * size)
        keys = qkv_ref[0, 0, 1, :, inner]
        values = qkv_ref[0, 0, 2, :, inner]
        for start in range(0, half, TILE):
            rows = slice(start, start + TILE)
            scores = mm_nt(qkv_ref[0, 0, 0, rows, inner], keys) * scale
            shift = bias_ref[head, :, : half - start]
            if start:
                shift = jnp.concatenate([bias_ref[head, :, length - start :], shift], axis=1)
            scores = scores + shift.astype(F32)
            scores = jnp.where(seg_col_ref[0, rows, :] == seg_row, scores, MASKED)
            top = jnp.max(scores, axis=-1, keepdims=True)
            weights = jnp.exp(scores - top)
            inverse = 1.0 / jnp.sum(weights, axis=-1, keepdims=True)
            prob = (weights * inverse).astype(BF16)
            prob_ref[0, 0, head, :, rows] = prob.T
            heads_ref[0, rows, inner] = mm(prob, values).astype(BF16)

    for g in range(2):

        @pl.when(group == g)
        def _(g=g):
            for member in range(members):
                rows = slice(member * shard_len, (member + 1) * shard_len)
                part_ref[micro, member, :, g * cols : (g + 1) * cols] = heads_ref[0, rows, :]

    @pl.when(group == 1)
    def _():
        got_ref[micro, mine] = part_ref[micro, mine]
        for s in range(1, members):
            swap(micro, s).start()

    @pl.when((micro == micros - 1) & (group == 1))
    def _():
        for m in range(micros):
            for s in range(1, members):
                swap(m, s).wait_recv()
            h1 = x_own_ref[0, 0].astype(F32)
            for member in range(members):
                for j in range(2):
                    index = lax.rem(part + j, 2) * members + member
                    h1 = h1 + mm(got_ref[m, member, :, j * cols : (j + 1) * cols], out_ref[index])
            h1_ref[m] = h1
            xn2_ref[m] = (unit_rows(h1) * moe_gain_ref[...]).astype(BF16)
        for m in range(micros):
            for s in range(1, members):
                swap(m, s).wait_send()
        if pairing:

            @pl.loop(0, routes_ref.shape[0])
            def _(source):
                for m in range(pair_ref.shape[0]):
                    fill_pairs(routes_ref, pair_ref, source, m, me)

        stay().wait()
        for s in range(1, sent_ref.shape[0]):
            ride(s).wait()


def attend(
    x, gain, own_weight, other_weight, bias, seg, out_weight, x_own, moe_gain, scale, members, identity,
    which, rider, routes=None, pair_shape=None,
):
    micros, half, width = x.shape
    cols = own_weight.shape[2]
    heads = bias.shape[0] // 2
    shard_len = half // members
    mine = pl.BlockSpec(
        (1, 1, shard_len, width), lambda m, p: (which, 0, 0, 0), pipeline_mode=pl.Buffered(1)
    )
    riders, ride_specs = [rider], [any_space()]
    ride_out, ride_out_specs = [jax.ShapeDtypeStruct(rider.shape, BF16)], [any_space()]
    if routes is not None:
        riders.append(routes)
        ride_specs.append(pl.BlockSpec(memory_space=pltpu.VMEM))
        ride_out.append(jax.ShapeDtypeStruct(pair_shape, BF16))
        ride_out_specs.append(pl.BlockSpec(memory_space=pltpu.VMEM))
    ride_sems = [pltpu.SemaphoreType.DMA((rider.shape[0],))] * 2 + [pltpu.SemaphoreType.DMA]

    def once(shape):
        return pl.BlockSpec(shape, lambda m, p: (0,) * len(shape), pipeline_mode=pl.Buffered(1))

    return pl.pallas_call(
        functools.partial(attend_kernel, scale),
        grid=(micros, 2),
        out_shape=(
            jax.ShapeDtypeStruct((micros, 2, 3, half, cols), BF16),
            jax.ShapeDtypeStruct((micros, 2, heads, half, half), BF16),
            jax.ShapeDtypeStruct((micros, half, 2 * cols), BF16),
            jax.ShapeDtypeStruct((micros, shard_len, width), F32),
            jax.ShapeDtypeStruct((micros, shard_len, width), BF16),
        )
        + tuple(ride_out),
        in_specs=[
            pl.BlockSpec((1, half, width), lambda m, p: (m, 0, 0)),
            once((1, width)),
            once((3, width, cols)),
            once((3, width, cols)),
            pl.BlockSpec((heads,) + bias.shape[1:], lambda m, p: (p, 0, 0)),
            pl.BlockSpec((1, 1, half), lambda m, p: (m, 0, 0)),
            pl.BlockSpec((1, half, 1), lambda m, p: (m, 0, 0)),
            once(out_weight.shape),
            mine,
            once((1, width)),
        ]
        + ride_specs,
        out_specs=(
            pl.BlockSpec((1, 1, 3, half, cols), lambda m, p: (m, p, 0, 0, 0)),
            pl.BlockSpec((1, 1, heads, half, half), lambda m, p: (m, p, 0, 0, 0)),
            pl.BlockSpec((1, half, cols), lambda m, p: (m, 0, p)),
            pl.BlockSpec((micros, shard_len, width), lambda m, p: (0, 0, 0)),
            pl.BlockSpec((micros, shard_len, width), lambda m, p: (0, 0, 0)),
        )
        + tuple(ride_out_specs),
        scratch_shapes=[
            pltpu.VMEM((half, width), BF16),
            pltpu.VMEM((micros, members, shard_len, 2 * cols), BF16),
            pltpu.VMEM((micros, members, shard_len, 2 * cols), BF16),
            pltpu.SemaphoreType.DMA((micros, members)),
            pltpu.SemaphoreType.DMA((micros, members)),
        ]
        + ride_sems,
        compiler_params=pltpu.CompilerParams(
            vmem_limit_bytes=VMEM_LIMIT, collective_id=identity, has_side_effects=True
        ),
        cost_estimate=pl.CostEstimate(
            flops=micros * 2 * half * cols * (8 * width + 4 * half),
            bytes_accessed=100000000,
            transcendentals=micros * 2 * heads * half * half,
        ),
        name="attend",
    )(
        x, gain, own_weight, other_weight, bias, seg.reshape(micros, 1, half),
        seg.reshape(micros, half, 1), out_weight, x_own, moe_gain, *riders,
    )


def back_kernel(scale, micros, *refs):
    moe_gain_ref, gain_ref, out_ref, own_ref, other_ref = refs[:5]
    inputs = [refs[5 + 8 * m : 13 + 8 * m] for m in range(micros)]
    sent_ref, refs = refs[5 + 8 * micros], refs[6 + 8 * micros :]
    (
        xgrad_ref, arrived_ref, grads_ref, line_ref, dmoe_ref, dgain_ref,
        dh1_ref, dattn_all, dheads_part, dheads_all, dxn_part, dxn_got, total_ref, xn_ref, ds_ref,
        dproj_ref, sheet_ref, attn_send, attn_recv, heads_send, heads_recv, dxn_send, dxn_recv,
        ride_send, ride_recv, ride_own,
    ) = refs
    devices = sent_ref.shape[0]
    _, members, shard_len, width = dattn_all.shape
    cols = dproj_ref.shape[2]
    half = members * shard_len
    length = sheet_ref.shape[0]
    group, micro = pl.program_id(0), pl.program_id(1)
    me = lax.axis_index("expert")
    line = lax.axis_index("hidden")
    mine = lax.rem(line, members)
    part = line // members
    base = line - mine
    steps = range(1, members)

    def peer_of(s):
        return lax.rem(mine + s, members)

    def attn_copy(m, s):
        return remote(
            dattn_all.at[m, mine], dattn_all.at[m, mine], attn_send.at[m, s], attn_recv.at[m, s],
            (me, base + peer_of(s)),
        )

    def heads_copy(m, s):
        return remote(
            dheads_part.at[m, peer_of(s)], dheads_all.at[m, mine], heads_send.at[m, s],
            heads_recv.at[m, s], (me, base + peer_of(s)),
        )

    def dxn_copy(m, s):
        return remote(
            dxn_part.at[m, peer_of(s)], dxn_got.at[m, mine], dxn_send.at[m, s], dxn_recv.at[m, s],
            (me, base + peer_of(s)),
        )

    def ride(s):
        peer = partner_of(me, s, devices)
        return remote(
            sent_ref.at[peer], arrived_ref.at[me], ride_send.at[s], ride_recv.at[s], (peer, line)
        )

    def stay():
        return pltpu.make_async_copy(sent_ref.at[me], arrived_ref.at[me], ride_own)

    @pl.when((group == 0) & (micro == 0))
    def _():
        peers = [(me, base + peer_of(s)) for s in steps]
        greet(peers + [(partner_of(me, s, devices), line) for s in range(1, devices)])
        stay().start()
        for s in range(1, devices):
            ride(s).start()
        dmoe_ref[...] = jnp.zeros_like(dmoe_ref)
        dgain_ref[...] = jnp.zeros_like(dgain_ref)
        for m in range(micros):
            grad_ref, h1_ref, dy_ref = inputs[m][:3]
            grad = grad_ref[...].astype(F32)
            h1 = h1_ref[...]
            r2 = lax.rsqrt(jnp.mean(h1 * h1, axis=-1, keepdims=True) + EPSILON)
            unit = h1 * r2
            dmoe_ref[...] += jnp.sum(grad * unit, axis=0, keepdims=True)
            weighted = grad * moe_gain_ref[...]
            inner = jnp.mean(weighted * unit, axis=-1, keepdims=True)
            dh1 = dy_ref[0, 0].astype(F32) + r2 * (weighted - unit * inner)
            dh1_ref[m] = dh1
            dattn = dh1.astype(BF16)
            dattn_all[m, mine] = dattn
            for member in range(members):
                for j in range(2):
                    index = lax.rem(part + j, 2) * members + member
                    dheads = mm_nt(dattn, out_ref[index]).astype(BF16)
                    dheads_part[m, member, :, j * cols : (j + 1) * cols] = dheads
            for s in steps:
                heads_copy(m, s).start()
            dheads_all[m, mine] = dheads_part[m, mine]
        for m in range(micros):
            xn_ref[m] = (unit_rows(inputs[m][4][...]) * gain_ref[...]).astype(BF16)

    def products(weight_ref):
        dxn = mm_nt(dproj_ref[0], weight_ref[0])
        for t in range(1, 3):
            dxn = dxn + mm_nt(dproj_ref[t], weight_ref[t])
        return dxn.reshape(members, shard_len, width)

    per = grads_ref.shape[0] // 4
    for g in range(2):
        for m in range(micros):

            @pl.when((group == g) & (micro == m))
            def _(g=g, m=m):
                x_ref, qkv_ref, prob_ref, heads_ref = inputs[m][4:]
                heads = prob_ref.shape[1]
                size = cols // heads
                if g == 0:
                    for s in steps:
                        heads_copy(m, s).wait_recv()
                    for s in steps:
                        attn_copy(m, s).start()
                for head in range(heads):
                    inner_cols = slice(head * size, (head + 1) * size)
                    outer_cols = slice(g * cols + head * size, g * cols + (head + 1) * size)
                    values = qkv_ref[0, 2, :, inner_cols]
                    grads = dheads_all[m, :, :, outer_cols].reshape(half, size)
                    sheet_ref[...] = jnp.zeros_like(sheet_ref)
                    for start in range(0, half, TILE):
                        rows = slice(start, start + TILE)
                        prob = prob_ref[0, head, :, rows].astype(F32)
                        dprob = mm_nt(values, grads[rows])
                        inner = jnp.sum(prob * dprob, axis=0, keepdims=True)
                        dscore = (prob * (dprob - inner)).astype(BF16)
                        ds_ref[:, rows] = dscore
                        dscore = dscore.astype(F32)
                        sheet_ref[: half - start, :] += dscore[start:]
                        if start:
                            sheet_ref[length - start :, :] += dscore[:start]
                    dscores = ds_ref[...]
                    keys, queries = qkv_ref[0, 1, :, inner_cols], qkv_ref[0, 0, :, inner_cols]
                    dproj_ref[0, :, inner_cols] = (mm_tn(dscores, keys) * scale).astype(BF16)
                    dproj_ref[1, :, inner_cols] = (mm(dscores, queries) * scale).astype(BF16)
                    dproj_ref[2, :, inner_cols] = mm(prob_ref[0, head], grads).astype(BF16)
                    sheet = sheet_ref[...].T
                    while sheet.shape[0] > 8:
                        upper = sheet.shape[0] // 2
                        sheet = sheet[:upper] + pltpu.roll(sheet[upper:], length - upper, 1)
                    row = lax.broadcasted_iota(jnp.int32, (8, length), 0)
                    found = jnp.zeros((1, length), F32)
                    for r in range(8):
                        moved = pltpu.roll(sheet, length - r, 1) if r else sheet
                        found = found + jnp.sum(
                            jnp.where(row == r, moved, 0.0), axis=0, keepdims=True
                        )
                    if m:
                        found = found + line_ref[0, head : head + 1, :]
                    line_ref[0, head : head + 1, :] = found
                if g == 0:
                    total_ref[m] = products(own_ref)
                    for s in steps:
                        attn_copy(m, s).wait_recv()
                else:
                    total = total_ref[m] + products(other_ref)
                    total_ref[m] = total
                    dxn_part[m] = total.astype(BF16)
                    for s in steps:
                        dxn_copy(m, s).start()
                    total = total.reshape(half, width)
                    dgain_ref[...] += jnp.sum(total * unit_rows(x_ref[...]), axis=0, keepdims=True)
                for t in range(4):
                    if t < 3:
                        found = mm_tn(xn_ref[m], dproj_ref[t])
                    else:
                        found = mm_tn(dattn_all[m].reshape(half, width), heads_ref[...])
                    found = found.reshape(per, 1, width // per, cols)
                    if m:
                        found = found + grads_ref[t * per : (t + 1) * per].astype(F32)
                    grads_ref[t * per : (t + 1) * per] = found.astype(BF16)

    @pl.when((group == 1) & (micro == micros - 1))
    def _():
        for m in range(micros):
            x_own = inputs[m][3][0, 0].astype(F32)
            r1 = lax.rsqrt(jnp.mean(x_own * x_own, axis=-1, keepdims=True) + EPSILON)
            unit = x_own * r1
            for s in steps:
                dxn_copy(m, s).wait_recv()
            dxn1 = total_ref[m, mine]
            for s in steps:
                dxn1 = dxn1 + dxn_got[m, lax.rem(mine + members - s, members)].astype(F32)
            weighted = dxn1 * gain_ref[...]
            inner = jnp.mean(weighted * unit, axis=-1, keepdims=True)
            xgrad_ref[m] = (dh1_ref[m] + r1 * (weighted - unit * inner)).astype(BF16)
        for m in range(micros):
            for s in steps:
                heads_copy(m, s).wait_send()
                attn_copy(m, s).wait_send()
                dxn_copy(m, s).wait_send()
        stay().wait()
        for s in range(1, devices):
            ride(s).wait()


def attend_back(
    moe_gain, gain, out_weight, own_weight, other_weight, kept, rider, scale, pieces, members
):
    micros = len(kept)
    _, heads, half = kept[0][6].shape[:3]
    width, cols = own_weight.shape[1:]
    shard_len = half // members
    length = 2 * half
    rows = 4 * width // pieces

    def once(array):
        return pl.BlockSpec(
            array.shape, lambda p, m: (0,) * array.ndim, pipeline_mode=pl.Buffered(1)
        )

    operands = [moe_gain, gain, out_weight, own_weight, other_weight]
    in_specs = [once(array) for array in operands]
    for micro, arrays in enumerate(kept):
        operands.extend(arrays)
        grad, h1, _, _, x_half = [once(array) for array in arrays[:5]]
        mine = pl.BlockSpec(
            (1, 1, shard_len, width), lambda p, m, which=micro: (which, 0, 0, 0),
            pipeline_mode=pl.Buffered(1),
        )
        in_specs += [grad, h1, mine, mine, x_half] + [
            pl.BlockSpec((1, 3, half, cols), lambda p, m: (p, 0, 0, 0)),
            pl.BlockSpec((1, heads, half, half), lambda p, m: (p, 0, 0, 0)),
            pl.BlockSpec((half, cols), lambda p, m: (0, p)),
        ]
    operands.append(rider)
    in_specs.append(any_space())
    dma = pltpu.SemaphoreType.DMA((micros, members))
    ride_dma = pltpu.SemaphoreType.DMA((rider.shape[0],))
    return pl.pallas_call(
        functools.partial(back_kernel, scale, micros),
        grid=(2, micros),
        out_shape=(
            jax.ShapeDtypeStruct((micros, shard_len, width), BF16),
            jax.ShapeDtypeStruct(rider.shape, BF16),
            jax.ShapeDtypeStruct((pieces, 2, rows, cols), BF16),
            jax.ShapeDtypeStruct((2, heads, length), F32),
            jax.ShapeDtypeStruct((1, width), F32),
            jax.ShapeDtypeStruct((1, width), F32),
        ),
        in_specs=in_specs,
        out_specs=(
            pl.BlockSpec((micros, shard_len, width), lambda p, m: (0, 0, 0)),
            any_space(),
            pl.BlockSpec((pieces, 1, rows, cols), lambda p, m: (0, p, 0, 0)),
            pl.BlockSpec((1, heads, length), lambda p, m: (p, 0, 0)),
            pl.BlockSpec((1, width), lambda p, m: (0, 0)),
            pl.BlockSpec((1, width), lambda p, m: (0, 0)),
        ),
        scratch_shapes=[
            pltpu.VMEM((micros, shard_len, width), F32),
            pltpu.VMEM((micros, members, shard_len, width), BF16),
            pltpu.VMEM((micros, members, shard_len, 2 * cols), BF16),
            pltpu.VMEM((micros, members, shard_len, 2 * cols), BF16),
            pltpu.VMEM((micros, members, shard_len, width), BF16),
            pltpu.VMEM((micros, members, shard_len, width), BF16),
            pltpu.VMEM((micros, members, shard_len, width), F32),
            pltpu.VMEM((micros, half, width), BF16),
            pltpu.VMEM((half, half), BF16),
            pltpu.VMEM((3, half, cols), BF16),
            pltpu.VMEM((length, TILE), F32),
            dma, dma, dma, dma, dma, dma, ride_dma, ride_dma, pltpu.SemaphoreType.DMA,
        ],
        compiler_params=pltpu.CompilerParams(
            vmem_limit_bytes=VMEM_LIMIT, collective_id=6, has_side_effects=True
        ),
        cost_estimate=pl.CostEstimate(
            flops=2 * micros * half * cols * (16 * width + 8 * half),
            bytes_accessed=250000000,
            transcendentals=0,
        ),
        name="attend_back",
    )(*operands)


def closing_kernel(
    pieces_ref, small_ref, y_ref, h1_ref, rows_ref, place_ref, first_h1_ref,
    whole_ref, sum_ref, block_ref,
    y_got, y_send, y_recv, half_got, held_ref, quarter_got, total_ref, moved_ref, moved_got, small_got, line_sum,
    line_got, half_sem, quarter_send, quarter_recv, small_send, small_recv, line_send, line_recv,
    moved_sem, on_send, on_recv, own_sem,
):
    chips = pieces_ref.shape[0]
    devices = 2 * chips
    blocks = line_got.shape[0]
    me = lax.axis_index("expert")
    line = lax.axis_index("hidden")
    chip, core = me // 2, lax.rem(me, 2)
    sibling = partner_of(me, 1, devices)
    along = [lax.rem(line + s, blocks) for s in range(1, blocks)]
    across = lax.rem(line + blocks // 2, blocks)
    greet([(partner_of(me, s, devices), line) for s in range(1, devices)] + [(me, z) for z in along])
    share = y_ref.shape[1] // 2
    turns = (pl.ds(0, share), pl.ds(share, y_ref.shape[1] - share))

    def y_copies(turn):
        rows = turns[turn]
        return [
            remote(
                y_ref.at[z, rows], y_got.at[line, rows], y_send.at[turn, s], y_recv.at[turn, s],
                (me, z),
            )
            for s, z in enumerate(along)
        ]

    halves = remote(
        pieces_ref.at[:, 1 - core], half_got, half_sem.at[0], half_sem.at[1], (sibling, line)
    )
    halves.start()
    for copy in y_copies(0):
        copy.start()
    smalls = [
        remote(
            small_ref, small_got.at[me], small_send.at[s], small_recv.at[s],
            (partner_of(me, s, devices), line),
        )
        for s in range(1, devices)
    ]
    for copy in smalls:
        copy.start()
    small_got[me] = small_ref[...]
    block_ref[0] = (first_h1_ref[...] + collect(rows_ref, place_ref)).astype(BF16)
    halves.wait_recv()
    steps = range(1, chips)

    def quarter(s):
        other = partner_of(chip, s, chips)
        return remote(
            held_ref.at[other], quarter_got.at[s], quarter_send.at[s], quarter_recv.at[s],
            (partner_of(me, 2 * s, devices), line),
        )

    for s in steps:
        other = partner_of(chip, s, chips)
        held = pieces_ref[other, core].astype(F32) + half_got[other].astype(F32)
        held_ref[other] = held.astype(BF16)
        quarter(s).start()
    total_ref[...] = pieces_ref[chip, core].astype(F32) + half_got[chip].astype(F32)
    for copy in smalls:
        copy.wait_recv()
    line_sum[...] = jnp.sum(small_got[...], axis=0)
    lines = [
        remote(line_sum, line_got.at[line], line_send.at[s], line_recv.at[s], (me, z))
        for s, z in enumerate(along)
    ]
    for copy in lines:
        copy.start()
    line_got[line] = line_sum[...]
    for s in steps:
        quarter(s).wait_recv()
        total_ref[...] += quarter_got[s].astype(F32)
    moved_ref[...] = total_ref[1].astype(BF16)
    cross = remote(moved_ref, moved_got, moved_sem.at[0], moved_sem.at[1], (me, across))
    cross.start()
    cross.wait_recv()
    for copy in y_copies(1):
        copy.start()
    whole_ref[chip, core] = (total_ref[0] + moved_got[...].astype(F32)).astype(BF16)
    onward = [
        remote(
            whole_ref.at[chip, core], whole_ref.at[chip, core], on_send.at[s], on_recv.at[s],
            (partner_of(me, 2 * s, devices), line),
        )
        for s in steps
    ]
    for copy in onward:
        copy.start()
    for copy in lines:
        copy.wait_recv()
    sum_ref[...] = jnp.sum(line_got[...], axis=0)
    for copy in onward:
        copy.wait_recv()
    y_got[line] = y_ref[line]
    last = remote(
        whole_ref.at[:, core], whole_ref.at[:, core], on_send.at[0], on_recv.at[0], (sibling, line)
    )
    last.start()
    for copy in y_copies(0) + y_copies(1):
        copy.wait_recv()
    block_ref[1] = (h1_ref[...] + jnp.sum(y_got[...].astype(F32), axis=0)).astype(BF16)
    for copy in y_copies(0) + y_copies(1):
        copy.wait_send()
    halves.wait_send()
    for s in steps:
        quarter(s).wait_send()
    cross.wait_send()
    for copy in smalls + lines + onward:
        copy.wait_send()
    last.wait()


def closing(pieces, small, y, h1, rows_first, place, first_h1):
    devices, both, rows, cols = pieces.shape
    blocks = y.shape[0]
    chips = devices // 2
    vmem = pl.BlockSpec(memory_space=pltpu.VMEM)
    dma = pltpu.SemaphoreType.DMA
    return pl.pallas_call(
        closing_kernel,
        out_shape=(
            jax.ShapeDtypeStruct((chips, 2, rows, cols), BF16),
            jax.ShapeDtypeStruct(small.shape, F32),
            jax.ShapeDtypeStruct((2,) + h1.shape, BF16),
        ),
        in_specs=[vmem] * 7,
        out_specs=(vmem,) * 3,
        scratch_shapes=[
            pltpu.VMEM(y.shape, BF16),
            dma((2, blocks)),
            dma((2, blocks)),
            pltpu.VMEM((chips, both, rows, cols), BF16),
            pltpu.VMEM((chips, both, rows, cols), BF16),
            pltpu.VMEM((chips, both, rows, cols), BF16),
            pltpu.VMEM((both, rows, cols), F32),
            pltpu.VMEM((rows, cols), BF16),
            pltpu.VMEM((rows, cols), BF16),
            pltpu.VMEM((devices,) + small.shape, F32),
            pltpu.VMEM(small.shape, F32),
            pltpu.VMEM((blocks,) + small.shape, F32),
            dma((2,)), dma((chips,)), dma((chips,)), dma((devices,)), dma((devices,)),
            dma((blocks,)), dma((blocks,)), dma((2,)), dma((chips,)), dma((chips,)), dma,
        ],
        compiler_params=pltpu.CompilerParams(
            vmem_limit_bytes=VMEM_LIMIT, collective_id=3, has_side_effects=True
        ),
        cost_estimate=pl.CostEstimate(flops=0, bytes_accessed=160000000, transcendentals=0),
        name="closing",
    )(pieces.reshape(chips, 2, both, rows, cols), small, y, h1, rows_first, place, first_h1)


def spread(rows, place0, place1, count):
    ids = lax.broadcasted_iota(jnp.int32, (count, rows.shape[0]), 0)
    hit = (ids == place0) | (ids == place1)
    return mm(jnp.where(hit, 1.0, 0.0).astype(BF16), rows)


def spread_kernel(rows_ref, place_ref, out_ref):
    experts, _, cap, width = out_ref.shape
    placed = spread(rows_ref[0], place_ref[0:1, :], place_ref[1:2, :], experts * cap)
    out_ref[...] = placed.astype(BF16).reshape(experts, 1, cap, width)


def spread_rows(rows, micro, place, experts, cap, shard_len):
    _, slots, width = rows.shape
    blocks = slots // shard_len
    return pl.pallas_call(
        spread_kernel,
        grid=(blocks,),
        out_shape=jax.ShapeDtypeStruct((experts, blocks, cap, width), BF16),
        in_specs=[
            pl.BlockSpec((1, shard_len, width), lambda b: (micro, b, 0)),
            pl.BlockSpec((2, shard_len), lambda b: (0, b)),
        ],
        out_specs=pl.BlockSpec((experts, 1, cap, width), lambda b: (0, b, 0, 0)),
        compiler_params=pltpu.CompilerParams(vmem_limit_bytes=VMEM_LIMIT),
        cost_estimate=pl.CostEstimate(
            flops=2 * experts * cap * slots * width,
            bytes_accessed=2 * slots * width + 2 * experts * blocks * cap * width,
            transcendentals=0,
        ),
        name="spread_rows",
    )(rows, place)


def collect_kernel(rows_ref, place_ref, out_ref):
    out_ref[...] = collect(rows_ref, place_ref).astype(BF16)


def collect_rows(rows, place, shard_len):
    experts, blocks, cap, width = rows.shape
    slots = blocks * shard_len
    return pl.pallas_call(
        collect_kernel,
        grid=(blocks,),
        out_shape=jax.ShapeDtypeStruct((slots, width), BF16),
        in_specs=[
            pl.BlockSpec((experts, 1, cap, width), lambda b: (0, b, 0, 0)),
            pl.BlockSpec((2, shard_len), lambda b: (0, b)),
        ],
        out_specs=pl.BlockSpec((shard_len, width), lambda b: (b, 0)),
        compiler_params=pltpu.CompilerParams(vmem_limit_bytes=VMEM_LIMIT),
        cost_estimate=pl.CostEstimate(
            flops=2 * experts * cap * slots * width,
            bytes_accessed=2 * slots * width + 2 * experts * blocks * cap * width,
            transcendentals=0,
        ),
        name="collect_rows",
    )(rows, place)


def place_kernel(cap, experts, route_ref, place_ref):
    blocks, micros, _, shard_len = route_ref.shape
    for block in range(blocks):
        for micro in range(micros):
            _, found = places(route_ref, (block, micro), cap, experts)
            for k in range(2):
                lanes = slice(block * shard_len, (block + 1) * shard_len)
                place_ref[micro, k : k + 1, lanes] = found[k]


def find_places(route, experts, cap):
    blocks, micros, _, shard_len = route.shape
    vmem = pl.BlockSpec(memory_space=pltpu.VMEM)
    return pl.pallas_call(
        functools.partial(place_kernel, cap, experts),
        out_shape=jax.ShapeDtypeStruct((micros, 2, blocks * shard_len), jnp.int32),
        in_specs=[vmem],
        out_specs=vmem,
        compiler_params=pltpu.CompilerParams(vmem_limit_bytes=VMEM_LIMIT),
        name="find_places",
    )(route)


def expert_kernel(
    by_block, sent_ref, dy_ref, pair_ref, wr_ref, wg_ref, wu_ref, wd_ref,
    back_ref, y_ref, x_ref, g_ref, hid_ref, dga_ref, dup_ref, dlog_ref,
    got_ref, dx_ref, stage_ref, x_send, x_recv, dx_send, dx_recv, own_sem, stage_sem,
):
    devices, experts, cap, width = sent_ref.shape
    step = pl.program_id(0)
    me = lax.axis_index("expert")
    line = lax.axis_index("hidden")
    first_wave = bits_of(devices)
    rest = [s for s in range(1, devices) if s not in first_wave]
    later_waves = [rest[i : i + 2] for i in range(0, len(rest), 2)]

    def x_copy(s):
        peer = partner_of(me, s, devices)
        return pltpu.make_async_remote_copy(
            src_ref=sent_ref.at[peer], dst_ref=got_ref.at[s], send_sem=x_send.at[s],
            recv_sem=x_recv.at[s], device_id=(peer, line), device_id_type=pl.DeviceIdType.MESH,
        )

    def dx_copy(s):
        peer = partner_of(me, s, devices)
        return pltpu.make_async_remote_copy(
            src_ref=dx_ref.at[s], dst_ref=back_ref.at[me], send_sem=dx_send.at[s],
            recv_sem=dx_recv.at[s], device_id=(peer, line), device_id_type=pl.DeviceIdType.MESH,
        )

    blocks, share = stage_ref.shape[2:4]

    def y_copies(s):
        source = partner_of(me, s, devices)
        slot = lax.rem(s, 2)
        if not by_block[1]:
            return [
                pltpu.make_async_copy(stage_ref.at[slot], y_ref.at[source], stage_sem.at[slot, 0])
            ]
        return [
            pltpu.make_async_copy(
                stage_ref.at[slot, e], y_ref.at[:, source, e], stage_sem.at[slot, e]
            )
            for e in range(experts)
        ]

    def work(s):
        source = partner_of(me, s, devices)
        slot = lax.rem(s, 2)
        for e in range(experts):
            x = got_ref[s, e]
            dy = dy_ref[:, source, e] if by_block[0] else dy_ref[source, e]
            dy = dy.reshape(cap, width).astype(F32)
            pair = pair_ref[source, e].astype(F32)
            margin = jnp.sum(mm_nt(x, wr_ref[...]) * pair, axis=-1, keepdims=True)
            own_gate = 1.0 / (1.0 + jnp.exp(-margin))
            other_gate = 1.0 / (1.0 + jnp.exp(margin))
            g = (own_gate * dy).astype(BF16)
            x_ref[0, e] = x
            g_ref[0, e] = g
            gate = mm_nt(x, wg_ref[e])
            up = mm_nt(x, wu_ref[e])
            square = gate * gate
            bent = jnp.tanh(GELU_C * gate * (1.0 + GELU_A * square))
            half_gate = 0.5 * gate
            gelu = half_gate * (1.0 + bent)
            slope = 0.5 * (1.0 + bent) + half_gate * (1.0 - bent * bent) * (
                GELU_C * (1.0 + 3.0 * GELU_A * square)
            )
            hid = (gelu * up).astype(BF16)
            dhid = mm_nt(g, wd_ref[e])
            dga = (dhid * (up * slope)).astype(BF16)
            dup = (dhid * gelu).astype(BF16)
            hid_ref[0, e] = hid
            dga_ref[0, e] = dga
            dup_ref[0, e] = dup
            y = mm(hid, wd_ref[e])
            dgate = jnp.sum(y * dy, axis=-1, keepdims=True)
            stage_ref[slot, e] = (y * own_gate).astype(BF16).reshape(blocks, share, width)
            dlog = (dgate * own_gate * other_gate * pair).astype(BF16)
            dlog_ref[0, e] = dlog
            dx = mm(dga, wg_ref[e]) + mm(dup, wu_ref[e]) + mm(dlog, wr_ref[...])
            dx_ref[s, e] = dx.astype(BF16)

    @pl.when(step == 0)
    def _():
        barrier = pltpu.get_barrier_semaphore()
        for s in range(1, devices):
            pl.semaphore_signal(
                barrier, inc=1, device_id=(partner_of(me, s, devices), line),
                device_id_type=pl.DeviceIdType.MESH,
            )
        pl.semaphore_wait(barrier, devices - 1)
        for s in first_wave:
            x_copy(s).start()
        own = pltpu.make_async_copy(sent_ref.at[me], got_ref.at[0], own_sem)
        own.start()
        own.wait()

    @pl.when(step > 0)
    def _():
        x_copy(step).wait_recv()

    for index, wave in enumerate(later_waves):

        @pl.when(step == 2 + index)
        def _(wave=wave):
            for s in wave:
                x_copy(s).start()

    @pl.when(step > 1)
    def _():
        for copy in y_copies(step - 2):
            copy.wait()

    work(step)
    for copy in y_copies(step):
        copy.start()

    @pl.when(step > 0)
    def _():
        dx_copy(step).start()

    @pl.when(step == devices - 1)
    def _():
        own = pltpu.make_async_copy(dx_ref.at[0], back_ref.at[me], own_sem)
        own.start()
        own.wait()
        for copy in y_copies(devices - 2) + y_copies(devices - 1):
            copy.wait()
        for s in range(1, devices):
            x_copy(s).wait_send()
            dx_copy(s).wait_send()
            dx_copy(s).wait_recv()


def expert_pass(sent, dy, pair, wr, wg, wu, wd, by_block, identity):
    share = dy.shape[3]
    blocks = sent.shape[2] // share
    devices, experts, cap, width = sent.shape
    hidden = wg.shape[1]
    choices = wr.shape[0]

    def whole(shape):
        return pl.BlockSpec(shape, lambda s: (0,) * len(shape), pipeline_mode=pl.Buffered(1))

    def block(cols):
        return pl.BlockSpec((1, experts, cap, cols), lambda s: (s, 0, 0, 0))

    def kept(cols):
        return jax.ShapeDtypeStruct((devices, experts, cap, cols), BF16)

    y_shape = (blocks, devices, experts, share, width)
    if not by_block[1]:
        y_shape = (devices, experts, blocks, share, width)
    return pl.pallas_call(
        functools.partial(expert_kernel, by_block),
        grid=(devices,),
        out_shape=(
            kept(width), jax.ShapeDtypeStruct(y_shape, BF16), kept(width), kept(width), kept(hidden), kept(hidden),
            kept(hidden), kept(choices),
        ),
        in_specs=[
            any_space(), whole(dy.shape), whole(pair.shape), whole(wr.shape), whole(wg.shape),
            whole(wu.shape), whole(wd.shape),
        ],
        out_specs=(
            any_space(), any_space(), block(width), block(width), block(hidden), block(hidden),
            block(hidden), block(choices),
        ),
        scratch_shapes=[
            pltpu.VMEM((devices, experts, cap, width), BF16),
            pltpu.VMEM((devices, experts, cap, width), BF16),
            pltpu.VMEM((2, experts, blocks, share, width), BF16),
            pltpu.SemaphoreType.DMA((devices,)),
            pltpu.SemaphoreType.DMA((devices,)),
            pltpu.SemaphoreType.DMA((devices,)),
            pltpu.SemaphoreType.DMA((devices,)),
            pltpu.SemaphoreType.DMA,
            pltpu.SemaphoreType.DMA((2, experts)),
        ],
        compiler_params=pltpu.CompilerParams(
            vmem_limit_bytes=VMEM_LIMIT, collective_id=identity, has_side_effects=True
        ),
        cost_estimate=pl.CostEstimate(flops=0, bytes_accessed=490000000, transcendentals=0),
        name="expert_pass",
    )(sent, dy, pair, wr, wg, wu, wd)


def weight_kernel(*refs):
    count = (len(refs) - 4) // 6
    dwr_ref, dwg_ref, dwu_ref, dwd_ref = refs[-4:]
    totals = [0.0, 0.0, 0.0, 0.0]
    for index in range(count):
        blocks = [
            ref[...].reshape(ref.shape[0] * ref.shape[2], ref.shape[3])
            for ref in refs[6 * index : 6 * index + 6]
        ]
        x, g, hid, dga, dup, dlog = blocks
        totals[0] = totals[0] + mm_tn(dlog, x)
        totals[1] = totals[1] + mm_tn(dga, x)
        totals[2] = totals[2] + mm_tn(dup, x)
        totals[3] = totals[3] + mm_tn(hid, g)
    dwr_ref[0] = totals[0]
    dwg_ref[0] = totals[1]
    dwu_ref[0] = totals[2]
    dwd_ref[0] = totals[3]


def weight_pass(kept):
    sources, experts, cap, width = kept[0][0].shape
    hidden = kept[0][2].shape[3]
    choices = kept[0][5].shape[3]
    rows = sources * cap
    block = 256 if width % 256 == 0 else width
    tokens = pl.BlockSpec((sources, 1, cap, block), lambda e, j: (0, e, 0, j))
    acts = pl.BlockSpec((sources, 1, cap, hidden), lambda e, j: (0, e, 0, 0))
    logs = pl.BlockSpec((sources, 1, cap, choices), lambda e, j: (0, e, 0, 0))
    operands = []
    for arrays in kept:
        operands.extend(arrays)
    return pl.pallas_call(
        weight_kernel,
        grid=(experts, width // block),
        out_shape=(
            jax.ShapeDtypeStruct((experts, choices, width), F32),
            jax.ShapeDtypeStruct((experts, hidden, width), F32),
            jax.ShapeDtypeStruct((experts, hidden, width), F32),
            jax.ShapeDtypeStruct((experts, hidden, width), F32),
        ),
        in_specs=[tokens, tokens, acts, acts, acts, logs] * len(kept),
        out_specs=(
            pl.BlockSpec((1, choices, block), lambda e, j: (e, 0, j)),
            pl.BlockSpec((1, hidden, block), lambda e, j: (e, 0, j)),
            pl.BlockSpec((1, hidden, block), lambda e, j: (e, 0, j)),
            pl.BlockSpec((1, hidden, block), lambda e, j: (e, 0, j)),
        ),
        compiler_params=pltpu.CompilerParams(vmem_limit_bytes=VMEM_LIMIT),
        cost_estimate=pl.CostEstimate(
            flops=6 * len(kept) * experts * rows * width * hidden,
            bytes_accessed=len(kept) * experts * rows * (4 * width + 6 * hidden)
            + 12 * experts * width * hidden,
            transcendentals=0,
        ),
        name="weight_pass",
    )(*operands)


def after(values, *others):
    return lax.optimization_barrier((values,) + others)[0]


def shards(
    x_in,
    cotangent,
    segment_ids,
    routes,
    qkv_weight,
    out_weight,
    bias_table,
    attn_gain,
    moe_gain,
    router_weight,
    gate_weight,
    up_weight,
    down_weight,
):
    micro_count, _, shard_len, width = x_in.shape
    slot_count = segment_ids.shape[2]
    head_cols = out_weight.shape[0]
    bucket_count, heads_here = bias_table.shape
    head_size = head_cols // heads_here
    expert_count = router_weight.shape[1]
    experts_here = gate_weight.shape[0]
    devices = expert_count // experts_here
    blocks = slot_count // shard_len
    members = blocks // 2
    half = slot_count // 2
    capacity = max(2, (10 * shard_len + 4 * expert_count - 1) // (4 * expert_count))
    scale = head_size ** (-0.5)
    hidden_index = lax.axis_index("hidden")
    expert_index = lax.axis_index("expert")
    part = hidden_index // members
    attn_gain_f = attn_gain.astype(F32).reshape(1, width)
    moe_gain_f = moe_gain.astype(F32).reshape(1, width)
    token_shape = (devices, experts_here, blocks * capacity, width)
    flat_shape = (devices, experts_here * blocks * capacity, width)
    place_shape = (expert_count, blocks, capacity, width)
    gate_rows = gate_weight.transpose(0, 2, 1)
    up_rows = up_weight.transpose(0, 2, 1)
    router_rows = router_weight.T

    def exchange(buffer):
        return lax.all_to_all(buffer, "expert", split_axis=0, concat_axis=0, tiled=True)

    def gather(values):
        return lax.all_gather(values, "hidden", axis=0, tiled=True)

    def scatter(values):
        return lax.psum_scatter(values, "hidden", scatter_dimension=0, tiled=True)

    states = [dict() for _ in range(micro_count)]
    own_seg = lax.dynamic_slice_in_dim(segment_ids[:, 0], hidden_index * shard_len, shard_len, 1)
    live_routes = jnp.where(own_seg[:, None, :] >= 0, routes[:, 0].transpose(0, 2, 1), -1)
    own_place = find_places(live_routes[None], expert_count, capacity)

    def spread(rows, micro, placed):
        return spread_rows(rows, micro, placed, expert_count, capacity, shard_len)

    *x_all, other_qkv, all_out, all_routes, other_table = opening(
        x_in[:, 0], qkv_weight.reshape(3 * width, head_cols), out_weight,
        live_routes, bias_table.T.astype(F32), devices, blocks, members,
    )
    x_half = [x.reshape(1, half, width) for x in x_all]
    other_qkv = other_qkv.reshape(qkv_weight.shape)
    all_out = all_out.reshape(blocks, head_cols, width)

    own_routes = lax.dynamic_index_in_dim(all_routes, expert_index, 0, keepdims=False)
    place = find_places(own_routes, expert_count, capacity)

    tables = jnp.concatenate([bias_table.T.astype(F32), other_table], axis=0)
    onehot_bucket = bucket_onehot(half, bucket_count)
    bias = position_bias(jnp.einsum("jb,hb->hj", onehot_bucket, tables, precision=PRECISE))
    seg_half = lax.dynamic_slice_in_dim(segment_ids[:, 0], part * half, half, 1)

    def gather_dy(rows):
        whole = gather(rows.reshape(1, devices * experts_here * capacity, width))
        return whole.reshape(blocks, devices, experts_here, capacity, width)

    def experts(micro, kept, *behind):
        sent = spread(kept["xn2_all"][None], 0, place[micro]).reshape(token_shape)
        kept["by_block"] = (micro > 0, micro + 1 < micro_count)
        back, kept["y"], x, g, hid, dga, dup, dlog = expert_pass(
            after(sent, *behind), kept["dy"], pairs[micro], router_rows, gate_rows, up_rows,
            down_weight, kept["by_block"], 4 + micro,
        )
        kept["weights"] = (x, g, hid, dga, dup, dlog)
        kept["back"] = back
        if micro > 0:
            back = after(back, states[micro - 1]["y_own"])
        kept["dx_back"] = back.reshape(place_shape)
        kept["dx_part"] = collect_rows(kept["dx_back"], place[micro], shard_len)
        kept["dxn2"] = scatter(kept["dx_part"])
        if kept["by_block"][1]:
            parts = after(kept["y"], kept["dx_part"]).reshape(blocks, -1, width)
            kept["y_own"] = scatter(parts).reshape(devices, -1, width)

    first, last = states
    first["dy_all"] = gather(after(cotangent[0, 0], all_out))
    pair_shape = (micro_count, devices, experts_here, blocks, capacity, expert_count)
    for micro, state in enumerate(states):
        inputs = (
            attn_gain_f, qkv_weight, other_qkv, bias, seg_half[micro : micro + 1], all_out,
            x_in, moe_gain_f, scale, members, 10 + micro, micro,
        )
        if micro == 0:
            sent = spread(cotangent[:, 0], 1, own_place[1]).reshape(devices, -1, width)
            qkv, prob, heads, h1, xn2, last["dy_here"] = attend(
                after(x_half[0], place), *inputs, sent
            )
        else:
            sent = spread(after(first["dy_all"], xn2)[None], 0, place[0]).reshape(token_shape)
            qkv, prob, heads, h1, xn2, first["dy"], pairs = attend(
                after(x_half[1], xn2), *inputs, sent, all_routes, pair_shape
            )
        state.update(qkv=qkv[0], prob=prob[0], heads=heads[0], h1=h1[0], xn2=xn2[0])
    first["dy"] = first["dy"].reshape(devices, experts_here, blocks, capacity, width)
    pairs = pairs.reshape(micro_count, devices, experts_here, blocks * capacity, expert_count)
    behind = ()
    for micro in range(micro_count):
        state = states[micro]
        state["xn2_all"] = gather(after(state["xn2"], *behind))
        behind = (state["xn2_all"],)
    for micro in range(1, micro_count):
        states[micro]["dy"] = gather_dy(after(states[micro]["dy_here"], states[0]["xn2_all"]))
    behind = ()
    for micro in range(micro_count):
        experts(micro, states[micro], *behind)
        behind = (states[micro]["dx_part"],)
    last_part = states[-1]["dx_part"]
    kept = [state["weights"] for state in states]
    kept[-1] = tuple(after(list(kept[-1]), last_part))
    dwr, dwg, dwu, dwd = weight_pass(kept)
    last["y_rows"] = exchange(after(last["y"], last_part).reshape(flat_shape)).reshape(place_shape)
    x_grad, first_rows, grads, lines, moe_gain_grad, attn_gain_grad = attend_back(
        moe_gain_f, attn_gain_f, all_out, qkv_weight, other_qkv,
        [
            (
                after(state["dxn2"], dwr), state["h1"], cotangent, x_in,
                x_half[micro][0], state["qkv"], state["prob"], state["heads"],
            )
            for micro, state in enumerate(states)
        ],
        first["y_own"], scale, devices, members,
    )
    rows = collect_rows(after(last["y_rows"], grads), place[-1], shard_len)
    rows = rows.reshape(blocks, shard_len, width)
    first_rows = first_rows.reshape(expert_count, 1, capacity, width)
    lines = lines.reshape(2 * heads_here, 2 * half)
    table = jnp.einsum("hj,jb->hb", lines, onehot_bucket, precision=PRECISE)
    table = table.reshape(2, heads_here * bucket_count)
    mine = jnp.arange(blocks, dtype=jnp.int32)[:, None]
    table = jnp.where(mine == hidden_index, table[0], 0.0) + jnp.where(
        mine == (hidden_index + members) % blocks, table[1], 0.0
    )
    small = jnp.concatenate(
        [
            jnp.sum(dwr, axis=0).reshape(-1),
            attn_gain_grad.reshape(-1),
            moe_gain_grad.reshape(-1),
            table.reshape(-1),
        ]
    )
    used = small.shape[0]
    small = jnp.pad(small, (0, -used % 1024)).reshape(-1, 128)
    whole, small, block_out = closing(
        grads, small, rows, last["h1"], first_rows, own_place[0], first["h1"]
    )
    whole = whole.reshape(4 * width, head_cols).astype(F32)
    grad_qkv = whole[: 3 * width].reshape(qkv_weight.shape)
    grad_out = whole[3 * width :].T
    small = small.reshape(-1)
    sizes = (width * expert_count, width, width)
    grad_router = small[: sizes[0]].reshape(expert_count, width).T
    grad_attn_gain = small[sizes[0] : sizes[0] + width]
    grad_moe_gain = small[sizes[0] + width : sizes[0] + 2 * width]
    table = small[sizes[0] + 2 * width : used].reshape(blocks, heads_here, bucket_count)
    grad_table = lax.dynamic_index_in_dim(table, hidden_index, 0, keepdims=False).T
    return (
        block_out[:, None],
        x_grad[:, None],
        grad_qkv,
        grad_out,
        grad_table,
        grad_attn_gain,
        grad_moe_gain,
        grad_router,
        dwg.transpose(0, 2, 1),
        dwu.transpose(0, 2, 1),
        dwd,
    )


def solution(mesh):
    return jax.shard_map(
        shards,
        mesh=mesh,
        in_specs=(
            P(None, "expert", "hidden", None),
            P(None, "expert", "hidden", None),
            P(None, "expert", None),
            P(None, "expert", "hidden", None),
            P(None, None, "hidden"),
            P("hidden", None),
            P(None, "hidden"),
            P(),
            P(),
            P(),
            P("expert", None, "hidden"),
            P("expert", None, "hidden"),
            P("expert", "hidden", None),
        ),
        out_specs=(
            P(None, "expert", "hidden", None),
            P(None, "expert", "hidden", None),
            P(None, None, "hidden"),
            P("hidden", None),
            P(None, "hidden"),
            P(),
            P(),
            P(),
            P("expert", None, "hidden"),
            P("expert", None, "hidden"),
            P("expert", "hidden", None),
        ),
        check_vma=False,
    )
```

```python
import functools

import jax
import jax.numpy as jnp
from jax import lax
from jax.experimental import pallas as pl
from jax.experimental.pallas import tpu as pltpu
from jax.sharding import PartitionSpec as P

EPSILON = 1e-06
PRECISE = lax.Precision.HIGHEST
LIMITS = (12, 16, 23, 32, 46, 64, 91)
MASKED = -1000000000.0
GELU_C = 0.7978845608028654
GELU_A = 0.044715
VMEM_LIMIT = 60 * 1024 * 1024
F32 = jnp.float32
BF16 = jnp.bfloat16


def mm(a, b):
    return lax.dot_general(a, b, (((1,), (0,)), ((), ())), preferred_element_type=F32)


def mm_nt(a, b):
    return lax.dot_general(a, b, (((1,), (1,)), ((), ())), preferred_element_type=F32)


def mm_tn(a, b):
    return lax.dot_general(a, b, (((0,), (0,)), ((), ())), preferred_element_type=F32)


def bucket_of(distance):
    magnitude = jnp.abs(distance)
    far_bucket = jnp.full(magnitude.shape, 8, jnp.int32)
    for threshold in LIMITS:
        far_bucket = far_bucket + (magnitude >= threshold).astype(jnp.int32)
    return jnp.where(magnitude < 8, magnitude, far_bucket) + 16 * (distance > 0).astype(jnp.int32)


def bucket_onehot(half, bucket_count):
    lane = jnp.arange(2 * half, dtype=jnp.int32)
    distance = jnp.where(lane < half, lane, lane - 2 * half)
    return (
        bucket_of(distance)[:, None] == jnp.arange(bucket_count, dtype=jnp.int32)[None, :]
    ).astype(F32)


TILE = 128


def bias_kernel(line_ref, out_ref):
    heads, _, length = out_ref.shape
    row = lax.broadcasted_iota(jnp.int32, (8, length), 0)
    for head in range(heads):
        line = jnp.broadcast_to(line_ref[head : head + 1, :], (8, length))
        sheet = line
        for r in range(1, 8):
            sheet = jnp.where(row == r, pltpu.roll(line, r, 1), sheet)
        while sheet.shape[0] < TILE:
            sheet = jnp.concatenate([sheet, pltpu.roll(sheet, sheet.shape[0], 1)], axis=0)
        out_ref[head] = sheet.astype(out_ref.dtype)


def position_bias(line):
    heads, length = line.shape
    vmem = pl.BlockSpec(memory_space=pltpu.VMEM)
    return pl.pallas_call(
        bias_kernel,
        out_shape=jax.ShapeDtypeStruct((heads, TILE, length), BF16),
        in_specs=[vmem],
        out_specs=vmem,
        compiler_params=pltpu.CompilerParams(vmem_limit_bytes=VMEM_LIMIT),
        name="position_bias",
    )(line)


def unit_rows(x):
    x = x.astype(F32)
    return x * lax.rsqrt(jnp.mean(x * x, axis=-1, keepdims=True) + EPSILON)


def remote(src, dst, send_sem, recv_sem, device):
    return pltpu.make_async_remote_copy(
        src_ref=src, dst_ref=dst, send_sem=send_sem, recv_sem=recv_sem,
        device_id=device, device_id_type=pl.DeviceIdType.MESH,
    )


def greet(devices):
    barrier = pltpu.get_barrier_semaphore()
    for device in devices:
        pl.semaphore_signal(
            barrier, inc=1, device_id=device, device_id_type=pl.DeviceIdType.MESH
        )
    pl.semaphore_wait(barrier, len(devices))


def bits_of(count):
    return [1 << b for b in range(count.bit_length() - 1)]


def partner_of(me, step, count):
    found = 0
    for bit in bits_of(count):
        found = found + bit * lax.rem(me // bit + step // bit, 2)
    return found


def any_space():
    return pl.BlockSpec(memory_space=pl.ANY)


def opening_kernel(
    micros, x_ref, qkv_ref, out_ref, routes_ref, table_ref, *refs,
):
    x_all, refs = refs[:micros], refs[micros:]
    (
        qkv_all, out_all, routes_all, table_all,
        x_send, x_recv, qkv_send, qkv_recv, out_send, out_recv, qkv_on_send, qkv_on_recv,
        out_on_send, out_on_recv, routes_send, routes_recv, routes_on_send, routes_on_recv,
        table_send, table_recv, own_sem,
    ) = refs
    devices, qkv_rows = qkv_all.shape[0] * 2, qkv_all.shape[2]
    blocks, out_rows = out_all.shape[0], out_all.shape[3]
    members = x_all[0].shape[0]
    me = lax.axis_index("expert")
    line = lax.axis_index("hidden")
    chip, core = me // 2, lax.rem(me, 2)
    mine = lax.rem(line, members)
    base = line - mine
    along = [lax.rem(line + s, blocks) for s in range(1, blocks)]
    across = lax.rem(line + members, blocks)
    sibling = partner_of(me, 1, devices)
    greet([(partner_of(me, s, devices), line) for s in range(1, devices)] + [(me, z) for z in along])
    own = [
        pltpu.make_async_copy(
            out_ref.at[pl.ds(me * out_rows, out_rows)], out_all.at[line, chip, core], own_sem.at[0]
        ),
        pltpu.make_async_copy(routes_ref, routes_all.at[me, line], own_sem.at[1]),
    ]
    for micro in range(micros):
        own.append(
            pltpu.make_async_copy(x_ref.at[micro], x_all[micro].at[mine], own_sem.at[2 + micro])
        )
    for copy in own:
        copy.start()
    first_qkv = remote(
        qkv_ref.at[pl.ds(me * qkv_rows, qkv_rows)], qkv_all.at[chip, core], qkv_send, qkv_recv,
        (me, across),
    )
    first_qkv.start()
    first_out, first_routes = [], []
    rest = [remote(table_ref, table_all, table_send, table_recv, (me, across))]
    for s, z in enumerate(along):
        first_out.append(
            remote(
                out_ref.at[pl.ds(me * out_rows, out_rows)], out_all.at[line, chip, core],
                out_send.at[s], out_recv.at[s], (me, z),
            )
        )
        first_routes.append(
            remote(
                routes_ref, routes_all.at[me, line], routes_send.at[s], routes_recv.at[s], (me, z)
            )
        )
    for copy in first_routes + first_out + rest:
        copy.start()
    for micro in range(micros):
        for s in range(1, members):
            peer = base + lax.rem(mine + s, members)
            copy = remote(
                x_ref.at[micro], x_all[micro].at[mine], x_send.at[micro, s], x_recv.at[micro, s],
                (me, peer),
            )
            copy.start()
            rest.append(copy)
    first_qkv.wait_recv()
    qkv_on, out_on = [], []
    for s in range(2, devices, 2):
        copy = remote(
            qkv_all.at[chip, core], qkv_all.at[chip, core], qkv_on_send.at[s], qkv_on_recv.at[s],
            (partner_of(me, s, devices), line),
        )
        copy.start()
        qkv_on.append(copy)
    own[1].wait()
    for copy in first_routes:
        copy.wait_recv()
    for s in range(1, devices):
        copy = remote(
            routes_all.at[me], routes_all.at[me], routes_on_send.at[s], routes_on_recv.at[s],
            (partner_of(me, s, devices), line),
        )
        copy.start()
        rest.append(copy)
    own[0].wait()
    for copy in first_out:
        copy.wait_recv()
    for s in range(2, devices, 2):
        copy = remote(
            out_all.at[:, chip, core], out_all.at[:, chip, core], out_on_send.at[s],
            out_on_recv.at[s], (partner_of(me, s, devices), line),
        )
        copy.start()
        out_on.append(copy)
    for copy in qkv_on:
        copy.wait_recv()
    copy = remote(
        qkv_all.at[:, core], qkv_all.at[:, core], qkv_on_send.at[1], qkv_on_recv.at[1],
        (sibling, line),
    )
    copy.start()
    rest.append(copy)
    for copy in out_on:
        copy.wait_recv()
    copy = remote(
        out_all.at[:, :, core], out_all.at[:, :, core], out_on_send.at[1], out_on_recv.at[1],
        (sibling, line),
    )
    copy.start()
    rest.append(copy)
    for copy in own[2:]:
        copy.wait()
    first_qkv.wait_send()
    for copy in first_out + first_routes + qkv_on + out_on:
        copy.wait_send()
    for copy in rest:
        copy.wait()


def opening(x, qkv, out, routes, table, devices, blocks, members):
    micros, shard_len, width = x.shape
    dma = pltpu.SemaphoreType.DMA
    pair = (devices // 2, 2)
    return pl.pallas_call(
        functools.partial(opening_kernel, micros),
        out_shape=(jax.ShapeDtypeStruct((members, shard_len, width), BF16),) * micros
        + (
            jax.ShapeDtypeStruct(pair + (qkv.shape[0] // devices, qkv.shape[1]), BF16),
            jax.ShapeDtypeStruct((blocks,) + pair + (out.shape[0] // devices, width), BF16),
            jax.ShapeDtypeStruct((devices, blocks) + routes.shape, jnp.int32),
            jax.ShapeDtypeStruct(table.shape, table.dtype),
        ),
        in_specs=[any_space()] * 5,
        out_specs=(any_space(),) * (4 + micros),
        scratch_shapes=[
            dma((micros, members)), dma((micros, members)), dma, dma, dma((blocks,)), dma((blocks,)),
            dma((devices,)), dma((devices,)), dma((devices,)), dma((devices,)), dma((blocks,)),
            dma((blocks,)), dma((devices,)), dma((devices,)), dma, dma, dma((2 + micros,)),
        ],
        compiler_params=pltpu.CompilerParams(collective_id=1, has_side_effects=True),
        cost_estimate=pl.CostEstimate(flops=0, bytes_accessed=200000000, transcendentals=0),
        name="opening",
    )(x, qkv, out, routes, table)


def unit_rows(x):
    x = x.astype(F32)
    return x * lax.rsqrt(jnp.mean(x * x, axis=-1, keepdims=True) + EPSILON)


def places(route_ref, index, cap, experts):
    shard_len = route_ref.shape[-1]
    row = lax.broadcasted_iota(jnp.int32, (shard_len, shard_len), 0)
    col = lax.broadcasted_iota(jnp.int32, (shard_len, shard_len), 1)
    earlier = jnp.where(row < col, 1.0, 0.0).astype(BF16)
    ids = lax.broadcasted_iota(jnp.int32, (experts, shard_len), 0)
    pair = [route_ref[index + (slice(k, k + 1),)] for k in range(2)]
    chosen = (ids == pair[0]) | (ids == pair[1])
    before = mm(jnp.where(chosen, 1.0, 0.0).astype(BF16), earlier)
    found = []
    for route in pair:
        position = jnp.sum(jnp.where(ids == route, before, 0.0), axis=0, keepdims=True)
        found.append(jnp.where(route >= 0, route * cap + position.astype(jnp.int32), -1))
    return pair, found


def fill_pairs(route_ref, pair_ref, source, micro, me):
    _, _, here, blocks, cap, experts = pair_ref.shape
    spots = lax.broadcasted_iota(jnp.int32, (cap, route_ref.shape[-1]), 0)
    ids = lax.broadcasted_iota(jnp.int32, (cap, experts), 1)
    for block in range(blocks):
        pair, place = places(route_ref, (source, block, micro), cap, experts)
        for e in range(here):
            expert = me * here + e
            other = jnp.full((cap, 1), -1, jnp.int32)
            for k in range(2):
                hit = spots + expert * cap == place[k]
                found = jnp.max(jnp.where(hit, pair[1 - k], -1), axis=1, keepdims=True)
                other = jnp.maximum(other, found)
            sign = jnp.where(ids == expert, 1.0, 0.0) - jnp.where(ids == other, 1.0, 0.0)
            pair_ref[micro, source, e, block] = jnp.where(other >= 0, sign, 0.0).astype(BF16)


def collect(rows_ref, place_ref):
    experts, _, cap, width = rows_ref.shape
    tokens = place_ref.shape[1]
    ids = lax.broadcasted_iota(jnp.int32, (experts * cap, tokens), 0)
    hit = (ids == place_ref[0:1, :]) | (ids == place_ref[1:2, :])
    rows = rows_ref[...].reshape(experts * cap, width)
    return mm_tn(jnp.where(hit, 1.0, 0.0).astype(BF16), rows)


def attend_kernel(
    scale, x_ref, gain_ref, own_ref, other_ref, bias_ref, seg_row_ref, seg_col_ref,
    out_ref, x_own_ref, moe_gain_ref, *refs,
):
    sent_ref, refs = refs[0], refs[1:]
    pairing = len(refs) > 14
    if pairing:
        routes_ref, pair_ref = refs[0], refs[7]
        refs = refs[1:7] + refs[8:]
    arrived_ref, ride_send, ride_recv, ride_own = refs[5], *refs[-3:]
    refs = refs[:5] + refs[6:-3]
    qkv_ref, prob_ref, heads_ref, h1_ref, xn2_ref, xn_ref, part_ref, got_ref, send_sem, recv_sem = refs
    micros, members, shard_len, both = got_ref.shape
    cols = both // 2
    heads, length = bias_ref.shape[0], bias_ref.shape[2]
    half = members * shard_len
    size = cols // heads
    micro, group = pl.program_id(0), pl.program_id(1)
    me = lax.axis_index("expert")
    line = lax.axis_index("hidden")
    mine = lax.rem(line, members)
    part = line // members
    base = line - mine

    def swap(m, s):
        peer = lax.rem(mine + s, members)
        return remote(
            part_ref.at[m, peer], got_ref.at[m, mine], send_sem.at[m, s], recv_sem.at[m, s],
            (me, base + peer),
        )

    def ride(s):
        peer = partner_of(me, s, sent_ref.shape[0])
        return remote(
            sent_ref.at[peer], arrived_ref.at[me], ride_send.at[s], ride_recv.at[s], (peer, line)
        )

    def stay():
        return pltpu.make_async_copy(sent_ref.at[me], arrived_ref.at[me], ride_own)

    @pl.when((micro == 0) & (group == 0))
    def _():
        peers = [(me, base + lax.rem(mine + s, members)) for s in range(1, members)]
        devices = sent_ref.shape[0]
        peers += [(partner_of(me, s, devices), line) for s in range(1, devices)]
        greet(peers)
        stay().start()
        for s in range(1, devices):
            ride(s).start()

    @pl.when(group == 0)
    def _():
        xn_ref[...] = (unit_rows(x_ref[0]) * gain_ref[...]).astype(BF16)
        for t in range(3):
            qkv_ref[0, 0, t] = mm(xn_ref[...], own_ref[t]).astype(BF16)

    @pl.when(group > 0)
    def _():
        for t in range(3):
            qkv_ref[0, 0, t] = mm(xn_ref[...], other_ref[t]).astype(BF16)

    seg_row = seg_row_ref[0]
    for head in range(heads):
        inner = slice(head * size, (head + 1) * size)
        keys = qkv_ref[0, 0, 1, :, inner]
        values = qkv_ref[0, 0, 2, :, inner]
        for start in range(0, half, TILE):
            rows = slice(start, start + TILE)
            scores = mm_nt(qkv_ref[0, 0, 0, rows, inner], keys) * scale
            shift = bias_ref[head, :, : half - start]
            if start:
                shift = jnp.concatenate([bias_ref[head, :, length - start :], shift], axis=1)
            scores = scores + shift.astype(F32)
            scores = jnp.where(seg_col_ref[0, rows, :] == seg_row, scores, MASKED)
            top = jnp.max(scores, axis=-1, keepdims=True)
            weights = jnp.exp(scores - top)
            inverse = 1.0 / jnp.sum(weights, axis=-1, keepdims=True)
            prob = (weights * inverse).astype(BF16)
            prob_ref[0, 0, head, :, rows] = prob.T
            heads_ref[0, rows, inner] = mm(prob, values).astype(BF16)

    for g in range(2):

        @pl.when(group == g)
        def _(g=g):
            for member in range(members):
                rows = slice(member * shard_len, (member + 1) * shard_len)
                part_ref[micro, member, :, g * cols : (g + 1) * cols] = heads_ref[0, rows, :]

    @pl.when(group == 1)
    def _():
        got_ref[micro, mine] = part_ref[micro, mine]
        for s in range(1, members):
            swap(micro, s).start()

    @pl.when((micro == micros - 1) & (group == 1))
    def _():
        for m in range(micros):
            for s in range(1, members):
                swap(m, s).wait_recv()
            h1 = x_own_ref[0, 0].astype(F32)
            for member in range(members):
                for j in range(2):
                    index = lax.rem(part + j, 2) * members + member
                    h1 = h1 + mm(got_ref[m, member, :, j * cols : (j + 1) * cols], out_ref[index])
            h1_ref[m] = h1
            xn2_ref[m] = (unit_rows(h1) * moe_gain_ref[...]).astype(BF16)
        for m in range(micros):
            for s in range(1, members):
                swap(m, s).wait_send()
        if pairing:

            @pl.loop(0, routes_ref.shape[0])
            def _(source):
                for m in range(pair_ref.shape[0]):
                    fill_pairs(routes_ref, pair_ref, source, m, me)

        stay().wait()
        for s in range(1, sent_ref.shape[0]):
            ride(s).wait()


def attend(
    x, gain, own_weight, other_weight, bias, seg, out_weight, x_own, moe_gain, scale, members, identity,
    which, rider, routes=None, pair_shape=None,
):
    micros, half, width = x.shape
    cols = own_weight.shape[2]
    heads = bias.shape[0] // 2
    shard_len = half // members
    mine = pl.BlockSpec(
        (1, 1, shard_len, width), lambda m, p: (which, 0, 0, 0), pipeline_mode=pl.Buffered(1)
    )
    riders, ride_specs = [rider], [any_space()]
    ride_out, ride_out_specs = [jax.ShapeDtypeStruct(rider.shape, BF16)], [any_space()]
    if routes is not None:
        riders.append(routes)
        ride_specs.append(pl.BlockSpec(memory_space=pltpu.VMEM))
        ride_out.append(jax.ShapeDtypeStruct(pair_shape, BF16))
        ride_out_specs.append(pl.BlockSpec(memory_space=pltpu.VMEM))
    ride_sems = [pltpu.SemaphoreType.DMA((rider.shape[0],))] * 2 + [pltpu.SemaphoreType.DMA]

    def once(shape):
        return pl.BlockSpec(shape, lambda m, p: (0,) * len(shape), pipeline_mode=pl.Buffered(1))

    return pl.pallas_call(
        functools.partial(attend_kernel, scale),
        grid=(micros, 2),
        out_shape=(
            jax.ShapeDtypeStruct((micros, 2, 3, half, cols), BF16),
            jax.ShapeDtypeStruct((micros, 2, heads, half, half), BF16),
            jax.ShapeDtypeStruct((micros, half, 2 * cols), BF16),
            jax.ShapeDtypeStruct((micros, shard_len, width), F32),
            jax.ShapeDtypeStruct((micros, shard_len, width), BF16),
        )
        + tuple(ride_out),
        in_specs=[
            pl.BlockSpec((1, half, width), lambda m, p: (m, 0, 0)),
            once((1, width)),
            once((3, width, cols)),
            once((3, width, cols)),
            pl.BlockSpec((heads,) + bias.shape[1:], lambda m, p: (p, 0, 0)),
            pl.BlockSpec((1, 1, half), lambda m, p: (m, 0, 0)),
            pl.BlockSpec((1, half, 1), lambda m, p: (m, 0, 0)),
            once(out_weight.shape),
            mine,
            once((1, width)),
        ]
        + ride_specs,
        out_specs=(
            pl.BlockSpec((1, 1, 3, half, cols), lambda m, p: (m, p, 0, 0, 0)),
            pl.BlockSpec((1, 1, heads, half, half), lambda m, p: (m, p, 0, 0, 0)),
            pl.BlockSpec((1, half, cols), lambda m, p: (m, 0, p)),
            pl.BlockSpec((micros, shard_len, width), lambda m, p: (0, 0, 0)),
            pl.BlockSpec((micros, shard_len, width), lambda m, p: (0, 0, 0)),
        )
        + tuple(ride_out_specs),
        scratch_shapes=[
            pltpu.VMEM((half, width), BF16),
            pltpu.VMEM((micros, members, shard_len, 2 * cols), BF16),
            pltpu.VMEM((micros, members, shard_len, 2 * cols), BF16),
            pltpu.SemaphoreType.DMA((micros, members)),
            pltpu.SemaphoreType.DMA((micros, members)),
        ]
        + ride_sems,
        compiler_params=pltpu.CompilerParams(
            vmem_limit_bytes=VMEM_LIMIT, collective_id=identity, has_side_effects=True
        ),
        cost_estimate=pl.CostEstimate(
            flops=micros * 2 * half * cols * (8 * width + 4 * half),
            bytes_accessed=100000000,
            transcendentals=micros * 2 * heads * half * half,
        ),
        name="attend",
    )(
        x, gain, own_weight, other_weight, bias, seg.reshape(micros, 1, half),
        seg.reshape(micros, half, 1), out_weight, x_own, moe_gain, *riders,
    )


def back_kernel(scale, micros, *refs):
    moe_gain_ref, gain_ref, out_ref, own_ref, other_ref = refs[:5]
    inputs = [refs[5 + 8 * m : 13 + 8 * m] for m in range(micros)]
    sent_ref, refs = refs[5 + 8 * micros], refs[6 + 8 * micros :]
    (
        xgrad_ref, arrived_ref, grads_ref, crossed_ref, line_ref, dmoe_ref, dgain_ref,
        far_ref, half_got, held_ref, quarter_got, moved_ref, moved_got, dh1_ref, dattn_all, dheads_part, dheads_all, dxn_part, dxn_got, total_ref, xn_ref, ds_ref,
        dproj_ref, sheet_ref, attn_send, attn_recv, heads_send, heads_recv, dxn_send, dxn_recv,
        ride_send, ride_recv, ride_own, half_sem, quarter_send, quarter_recv, moved_sem,
    ) = refs
    devices = sent_ref.shape[0]
    chips = devices // 2
    _, members, shard_len, width = dattn_all.shape
    cols = dproj_ref.shape[2]
    half = members * shard_len
    length = sheet_ref.shape[0]
    group, micro = pl.program_id(0), pl.program_id(1)
    me = lax.axis_index("expert")
    line = lax.axis_index("hidden")
    mine = lax.rem(line, members)
    part = line // members
    base = line - mine
    steps = range(1, members)

    def peer_of(s):
        return lax.rem(mine + s, members)

    def attn_copy(m, s):
        return remote(
            dattn_all.at[m, mine], dattn_all.at[m, mine], attn_send.at[m, s], attn_recv.at[m, s],
            (me, base + peer_of(s)),
        )

    def heads_copy(m, s):
        return remote(
            dheads_part.at[m, peer_of(s)], dheads_all.at[m, mine], heads_send.at[m, s],
            heads_recv.at[m, s], (me, base + peer_of(s)),
        )

    def dxn_copy(m, s):
        return remote(
            dxn_part.at[m, peer_of(s)], dxn_got.at[m, mine], dxn_send.at[m, s], dxn_recv.at[m, s],
            (me, base + peer_of(s)),
        )

    def ride(s):
        peer = partner_of(me, s, devices)
        return remote(
            sent_ref.at[peer], arrived_ref.at[me], ride_send.at[s], ride_recv.at[s], (peer, line)
        )

    def stay():
        return pltpu.make_async_copy(sent_ref.at[me], arrived_ref.at[me], ride_own)

    chip, core = me // 2, lax.rem(me, 2)
    across = lax.rem(line + members, 2 * members)

    def halves():
        return remote(
            far_ref.at[:, 1 - core], half_got, half_sem.at[0], half_sem.at[1],
            (partner_of(me, 1, devices), line),
        )

    def quarter(s):
        return remote(
            held_ref.at[partner_of(chip, s, chips)], quarter_got.at[s], quarter_send.at[s],
            quarter_recv.at[s], (partner_of(me, 2 * s, devices), line),
        )

    def cross():
        return remote(moved_ref, moved_got, moved_sem.at[0], moved_sem.at[1], (me, across))

    @pl.when((group == 0) & (micro == 0))
    def _():
        peers = [(me, base + peer_of(s)) for s in steps] + [(me, across)]
        greet(peers + [(partner_of(me, s, devices), line) for s in range(1, devices)])
        stay().start()
        for s in range(1, devices):
            ride(s).start()
        dmoe_ref[...] = jnp.zeros_like(dmoe_ref)
        dgain_ref[...] = jnp.zeros_like(dgain_ref)
        for m in range(micros):
            grad_ref, h1_ref, dy_ref = inputs[m][:3]
            grad = grad_ref[...].astype(F32)
            h1 = h1_ref[...]
            r2 = lax.rsqrt(jnp.mean(h1 * h1, axis=-1, keepdims=True) + EPSILON)
            unit = h1 * r2
            dmoe_ref[...] += jnp.sum(grad * unit, axis=0, keepdims=True)
            weighted = grad * moe_gain_ref[...]
            inner = jnp.mean(weighted * unit, axis=-1, keepdims=True)
            dh1 = dy_ref[0, 0].astype(F32) + r2 * (weighted - unit * inner)
            dh1_ref[m] = dh1
            dattn = dh1.astype(BF16)
            dattn_all[m, mine] = dattn
            for member in range(members):
                for j in range(2):
                    index = lax.rem(part + j, 2) * members + member
                    dheads = mm_nt(dattn, out_ref[index]).astype(BF16)
                    dheads_part[m, member, :, j * cols : (j + 1) * cols] = dheads
            for s in steps:
                heads_copy(m, s).start()
            dheads_all[m, mine] = dheads_part[m, mine]
        for m in range(micros):
            xn_ref[m] = (unit_rows(inputs[m][4][...]) * gain_ref[...]).astype(BF16)

    @pl.when((group == 1) & (micro == 0))
    def _():
        halves().wait_recv()
        for s in range(1, chips):
            other = partner_of(chip, s, chips)
            held = far_ref[other, core].astype(F32) + half_got[other].astype(F32)
            held_ref[other] = held.astype(BF16)
            quarter(s).start()

    @pl.when((group == 1) & (micro == micros - 1))
    def _():
        total = far_ref[chip, core].astype(F32) + half_got[chip].astype(F32)
        for s in range(1, chips):
            quarter(s).wait_recv()
            total = total + quarter_got[s].astype(F32)
        moved_ref[...] = total.astype(BF16)
        cross().start()

    def products(weight_ref):
        dxn = mm_nt(dproj_ref[0], weight_ref[0])
        for t in range(1, 3):
            dxn = dxn + mm_nt(dproj_ref[t], weight_ref[t])
        return dxn.reshape(members, shard_len, width)

    span = chips // 4
    for g in range(2):
        for m in range(micros):

            @pl.when((group == g) & (micro == m))
            def _(g=g, m=m):
                x_ref, qkv_ref, prob_ref, heads_ref = inputs[m][4:]
                heads = prob_ref.shape[1]
                size = cols // heads
                if g == 0:
                    for s in steps:
                        heads_copy(m, s).wait_recv()
                    for s in steps:
                        attn_copy(m, s).start()
                for head in range(heads):
                    inner_cols = slice(head * size, (head + 1) * size)
                    outer = (1 - g) * cols + head * size
                    outer_cols = slice(outer, outer + size)
                    values = qkv_ref[0, 2, :, inner_cols]
                    grads = dheads_all[m, :, :, outer_cols].reshape(half, size)
                    sheet_ref[...] = jnp.zeros_like(sheet_ref)
                    for start in range(0, half, TILE):
                        rows = slice(start, start + TILE)
                        prob = prob_ref[0, head, :, rows].astype(F32)
                        dprob = mm_nt(values, grads[rows])
                        inner = jnp.sum(prob * dprob, axis=0, keepdims=True)
                        dscore = (prob * (dprob - inner)).astype(BF16)
                        ds_ref[:, rows] = dscore
                        dscore = dscore.astype(F32)
                        sheet_ref[: half - start, :] += dscore[start:]
                        if start:
                            sheet_ref[length - start :, :] += dscore[:start]
                    dscores = ds_ref[...]
                    keys, queries = qkv_ref[0, 1, :, inner_cols], qkv_ref[0, 0, :, inner_cols]
                    dproj_ref[0, :, inner_cols] = (mm_tn(dscores, keys) * scale).astype(BF16)
                    dproj_ref[1, :, inner_cols] = (mm(dscores, queries) * scale).astype(BF16)
                    dproj_ref[2, :, inner_cols] = mm(prob_ref[0, head], grads).astype(BF16)
                    sheet = sheet_ref[...].T
                    while sheet.shape[0] > 8:
                        upper = sheet.shape[0] // 2
                        sheet = sheet[:upper] + pltpu.roll(sheet[upper:], length - upper, 1)
                    row = lax.broadcasted_iota(jnp.int32, (8, length), 0)
                    found = jnp.zeros((1, length), F32)
                    for r in range(8):
                        moved = pltpu.roll(sheet, length - r, 1) if r else sheet
                        found = found + jnp.sum(
                            jnp.where(row == r, moved, 0.0), axis=0, keepdims=True
                        )
                    if m:
                        found = found + line_ref[0, head : head + 1, :]
                    line_ref[0, head : head + 1, :] = found
                if g == 0:
                    total_ref[m] = products(other_ref)
                    for s in steps:
                        attn_copy(m, s).wait_recv()
                else:
                    total = total_ref[m] + products(own_ref)
                    total_ref[m] = total
                    dxn_part[m] = total.astype(BF16)
                    for s in steps:
                        dxn_copy(m, s).start()
                    total = total.reshape(half, width)
                    dgain_ref[...] += jnp.sum(total * unit_rows(x_ref[...]), axis=0, keepdims=True)
                for t in range(4):
                    if t < 3:
                        found = mm_tn(xn_ref[m], dproj_ref[t])
                    else:
                        found = mm_tn(dattn_all[m].reshape(half, width), heads_ref[...])
                    target = (far_ref, grads_ref)[g]
                    found = found.reshape(span, 2, width // (2 * span), cols)
                    if m:
                        found = found + target[t * span : (t + 1) * span].astype(F32)
                    target[t * span : (t + 1) * span] = found.astype(BF16)
                if g == 0 and m == micros - 1:
                    halves().start()

    @pl.when((group == 1) & (micro == micros - 1))
    def _():
        for m in range(micros):
            x_own = inputs[m][3][0, 0].astype(F32)
            r1 = lax.rsqrt(jnp.mean(x_own * x_own, axis=-1, keepdims=True) + EPSILON)
            unit = x_own * r1
            for s in steps:
                dxn_copy(m, s).wait_recv()
            dxn1 = total_ref[m, mine]
            for s in steps:
                dxn1 = dxn1 + dxn_got[m, lax.rem(mine + members - s, members)].astype(F32)
            weighted = dxn1 * gain_ref[...]
            inner = jnp.mean(weighted * unit, axis=-1, keepdims=True)
            xgrad_ref[m] = (dh1_ref[m] + r1 * (weighted - unit * inner)).astype(BF16)
        for m in range(micros):
            for s in steps:
                heads_copy(m, s).wait_send()
                attn_copy(m, s).wait_send()
                dxn_copy(m, s).wait_send()
        stay().wait()
        for s in range(1, devices):
            ride(s).wait()
        cross().wait_recv()
        crossed_ref[...] = moved_got[...]
        halves().wait_send()
        cross().wait_send()
        for s in range(1, chips):
            quarter(s).wait_send()


def attend_back(
    moe_gain, gain, out_weight, own_weight, other_weight, kept, rider, scale, pieces, members
):
    micros = len(kept)
    _, heads, half = kept[0][6].shape[:3]
    width, cols = own_weight.shape[1:]
    shard_len = half // members
    length = 2 * half
    rows = 4 * width // pieces

    def once(array):
        return pl.BlockSpec(
            array.shape, lambda p, m: (0,) * array.ndim, pipeline_mode=pl.Buffered(1)
        )

    operands = [moe_gain, gain, out_weight, own_weight, other_weight]
    in_specs = [once(array) for array in operands]
    for micro, arrays in enumerate(kept):
        operands.extend(arrays)
        grad, h1, _, _, x_half = [once(array) for array in arrays[:5]]
        mine = pl.BlockSpec(
            (1, 1, shard_len, width), lambda p, m, which=micro: (which, 0, 0, 0),
            pipeline_mode=pl.Buffered(1),
        )
        in_specs += [grad, h1, mine, mine, x_half] + [
            pl.BlockSpec((1, 3, half, cols), lambda p, m: (1 - p, 0, 0, 0)),
            pl.BlockSpec((1, heads, half, half), lambda p, m: (1 - p, 0, 0, 0)),
            pl.BlockSpec((half, cols), lambda p, m: (0, 1 - p)),
        ]
    operands.append(rider)
    in_specs.append(any_space())
    dma = pltpu.SemaphoreType.DMA((micros, members))
    ride_dma = pltpu.SemaphoreType.DMA((rider.shape[0],))
    return pl.pallas_call(
        functools.partial(back_kernel, scale, micros),
        grid=(2, micros),
        out_shape=(
            jax.ShapeDtypeStruct((micros, shard_len, width), BF16),
            jax.ShapeDtypeStruct(rider.shape, BF16),
            jax.ShapeDtypeStruct((pieces // 2, 2, rows, cols), BF16),
            jax.ShapeDtypeStruct((rows, cols), BF16),
            jax.ShapeDtypeStruct((2, heads, length), F32),
            jax.ShapeDtypeStruct((1, width), F32),
            jax.ShapeDtypeStruct((1, width), F32),
        ),
        in_specs=in_specs,
        out_specs=(
            pl.BlockSpec((micros, shard_len, width), lambda p, m: (0, 0, 0)),
            any_space(),
            pl.BlockSpec(
                (pieces // 2, 2, rows, cols), lambda p, m: (0, 0, 0, 0),
                pipeline_mode=pl.Buffered(1),
            ),
            pl.BlockSpec((rows, cols), lambda p, m: (0, 0)),
            pl.BlockSpec((1, heads, length), lambda p, m: (1 - p, 0, 0)),
            pl.BlockSpec((1, width), lambda p, m: (0, 0)),
            pl.BlockSpec((1, width), lambda p, m: (0, 0)),
        ),
        scratch_shapes=[
            pltpu.VMEM((pieces // 2, 2, rows, cols), BF16),
            pltpu.VMEM((pieces // 2, rows, cols), BF16),
            pltpu.VMEM((pieces // 2, rows, cols), BF16),
            pltpu.VMEM((pieces // 2, rows, cols), BF16),
            pltpu.VMEM((rows, cols), BF16),
            pltpu.VMEM((rows, cols), BF16),
            pltpu.VMEM((micros, shard_len, width), F32),
            pltpu.VMEM((micros, members, shard_len, width), BF16),
            pltpu.VMEM((micros, members, shard_len, 2 * cols), BF16),
            pltpu.VMEM((micros, members, shard_len, 2 * cols), BF16),
            pltpu.VMEM((micros, members, shard_len, width), BF16),
            pltpu.VMEM((micros, members, shard_len, width), BF16),
            pltpu.VMEM((micros, members, shard_len, width), F32),
            pltpu.VMEM((micros, half, width), BF16),
            pltpu.VMEM((half, half), BF16),
            pltpu.VMEM((3, half, cols), BF16),
            pltpu.VMEM((length, TILE), F32),
            dma, dma, dma, dma, dma, dma, ride_dma, ride_dma, pltpu.SemaphoreType.DMA,
            pltpu.SemaphoreType.DMA((2,)), ride_dma, ride_dma, pltpu.SemaphoreType.DMA((2,)),
        ],
        compiler_params=pltpu.CompilerParams(
            vmem_limit_bytes=VMEM_LIMIT, collective_id=6, has_side_effects=True
        ),
        cost_estimate=pl.CostEstimate(
            flops=2 * micros * half * cols * (16 * width + 8 * half),
            bytes_accessed=250000000,
            transcendentals=0,
        ),
        name="attend_back",
    )(*operands)


def closing_kernel(
    pieces_ref, crossed_ref, small_ref, rows_ref, place_ref, first_h1_ref,
    whole_ref, sum_ref, block_ref,
    half_got, held_ref, quarter_got, small_got, line_sum, line_got,
    half_sem, quarter_send, quarter_recv, small_send, small_recv, line_send, line_recv,
    on_send, on_recv,
):
    chips = pieces_ref.shape[0]
    devices = 2 * chips
    blocks = line_got.shape[0]
    me = lax.axis_index("expert")
    line = lax.axis_index("hidden")
    chip, core = me // 2, lax.rem(me, 2)
    sibling = partner_of(me, 1, devices)
    along = [lax.rem(line + s, blocks) for s in range(1, blocks)]
    steps = range(1, chips)
    greet([(partner_of(me, s, devices), line) for s in range(1, devices)] + [(me, z) for z in along])
    halves = remote(
        pieces_ref.at[:, 1 - core], half_got, half_sem.at[0], half_sem.at[1], (sibling, line)
    )
    halves.start()
    smalls = [
        remote(
            small_ref, small_got.at[me], small_send.at[s], small_recv.at[s],
            (partner_of(me, s, devices), line),
        )
        for s in range(1, devices)
    ]
    for copy in smalls:
        copy.start()
    small_got[me] = small_ref[...]

    def quarter(s):
        return remote(
            held_ref.at[partner_of(chip, s, chips)], quarter_got.at[s], quarter_send.at[s],
            quarter_recv.at[s], (partner_of(me, 2 * s, devices), line),
        )

    halves.wait_recv()
    for s in steps:
        other = partner_of(chip, s, chips)
        held = pieces_ref[other, core].astype(F32) + half_got[other].astype(F32)
        held_ref[other] = held.astype(BF16)
        quarter(s).start()
    for copy in smalls:
        copy.wait_recv()
    line_sum[...] = jnp.sum(small_got[...], axis=0)
    lines = [
        remote(line_sum, line_got.at[line], line_send.at[s], line_recv.at[s], (me, z))
        for s, z in enumerate(along)
    ]
    for copy in lines:
        copy.start()
    line_got[line] = line_sum[...]
    block_ref[...] = (first_h1_ref[...] + collect(rows_ref, place_ref)).astype(BF16)
    total = pieces_ref[chip, core].astype(F32) + half_got[chip].astype(F32)
    total = total + crossed_ref[...].astype(F32)
    for s in steps:
        quarter(s).wait_recv()
        total = total + quarter_got[s].astype(F32)
    whole_ref[chip, core] = total.astype(BF16)
    onward = [
        remote(
            whole_ref.at[chip, core], whole_ref.at[chip, core], on_send.at[s], on_recv.at[s],
            (partner_of(me, 2 * s, devices), line),
        )
        for s in steps
    ]
    for copy in onward:
        copy.start()
    for copy in onward:
        copy.wait_recv()
    last = remote(
        whole_ref.at[:, core], whole_ref.at[:, core], on_send.at[0], on_recv.at[0], (sibling, line)
    )
    last.start()
    for copy in lines:
        copy.wait_recv()
    sum_ref[...] = jnp.sum(line_got[...], axis=0)
    halves.wait_send()
    for s in steps:
        quarter(s).wait_send()
    for copy in smalls + lines + onward:
        copy.wait_send()
    last.wait()


def closing(pieces, crossed, small, rows_first, place, first_h1, blocks):
    chips, _, rows, cols = pieces.shape
    devices = 2 * chips
    vmem = pl.BlockSpec(memory_space=pltpu.VMEM)
    dma = pltpu.SemaphoreType.DMA
    return pl.pallas_call(
        closing_kernel,
        out_shape=(
            jax.ShapeDtypeStruct((chips, 2, rows, cols), BF16),
            jax.ShapeDtypeStruct(small.shape, F32),
            jax.ShapeDtypeStruct(first_h1.shape, BF16),
        ),
        in_specs=[vmem] * 6,
        out_specs=(vmem,) * 3,
        scratch_shapes=[
            pltpu.VMEM((chips, rows, cols), BF16),
            pltpu.VMEM((chips, rows, cols), BF16),
            pltpu.VMEM((chips, rows, cols), BF16),
            pltpu.VMEM((devices,) + small.shape, F32),
            pltpu.VMEM(small.shape, F32),
            pltpu.VMEM((blocks,) + small.shape, F32),
            dma((2,)), dma((chips,)), dma((chips,)), dma((devices,)), dma((devices,)),
            dma((blocks,)), dma((blocks,)), dma((chips,)), dma((chips,)),
        ],
        compiler_params=pltpu.CompilerParams(
            vmem_limit_bytes=VMEM_LIMIT, collective_id=3, has_side_effects=True
        ),
        cost_estimate=pl.CostEstimate(flops=0, bytes_accessed=160000000, transcendentals=0),
        name="closing",
    )(pieces, crossed, small, rows_first, place, first_h1)


def spread(rows, place0, place1, count):
    ids = lax.broadcasted_iota(jnp.int32, (count, rows.shape[0]), 0)
    hit = (ids == place0) | (ids == place1)
    return mm(jnp.where(hit, 1.0, 0.0).astype(BF16), rows)


def spread_kernel(rows_ref, place_ref, out_ref):
    experts, _, cap, width = out_ref.shape
    placed = spread(rows_ref[0], place_ref[0:1, :], place_ref[1:2, :], experts * cap)
    out_ref[...] = placed.astype(BF16).reshape(experts, 1, cap, width)


def spread_rows(rows, micro, place, experts, cap, shard_len):
    _, slots, width = rows.shape
    blocks = slots // shard_len
    return pl.pallas_call(
        spread_kernel,
        grid=(blocks,),
        out_shape=jax.ShapeDtypeStruct((experts, blocks, cap, width), BF16),
        in_specs=[
            pl.BlockSpec((1, shard_len, width), lambda b: (micro, b, 0)),
            pl.BlockSpec((2, shard_len), lambda b: (0, b)),
        ],
        out_specs=pl.BlockSpec((experts, 1, cap, width), lambda b: (0, b, 0, 0)),
        compiler_params=pltpu.CompilerParams(vmem_limit_bytes=VMEM_LIMIT),
        cost_estimate=pl.CostEstimate(
            flops=2 * experts * cap * slots * width,
            bytes_accessed=2 * slots * width + 2 * experts * blocks * cap * width,
            transcendentals=0,
        ),
        name="spread_rows",
    )(rows, place)


def collect_kernel(rows_ref, place_ref, out_ref):
    out_ref[...] = collect(rows_ref, place_ref).astype(BF16)


def collect_rows(rows, place, shard_len):
    experts, blocks, cap, width = rows.shape
    slots = blocks * shard_len
    return pl.pallas_call(
        collect_kernel,
        grid=(blocks,),
        out_shape=jax.ShapeDtypeStruct((slots, width), BF16),
        in_specs=[
            pl.BlockSpec((experts, 1, cap, width), lambda b: (0, b, 0, 0)),
            pl.BlockSpec((2, shard_len), lambda b: (0, b)),
        ],
        out_specs=pl.BlockSpec((shard_len, width), lambda b: (b, 0)),
        compiler_params=pltpu.CompilerParams(vmem_limit_bytes=VMEM_LIMIT),
        cost_estimate=pl.CostEstimate(
            flops=2 * experts * cap * slots * width,
            bytes_accessed=2 * slots * width + 2 * experts * blocks * cap * width,
            transcendentals=0,
        ),
        name="collect_rows",
    )(rows, place)


def place_kernel(cap, experts, route_ref, place_ref):
    blocks, micros, _, shard_len = route_ref.shape
    for block in range(blocks):
        for micro in range(micros):
            _, found = places(route_ref, (block, micro), cap, experts)
            for k in range(2):
                lanes = slice(block * shard_len, (block + 1) * shard_len)
                place_ref[micro, k : k + 1, lanes] = found[k]


def find_places(route, experts, cap):
    blocks, micros, _, shard_len = route.shape
    vmem = pl.BlockSpec(memory_space=pltpu.VMEM)
    return pl.pallas_call(
        functools.partial(place_kernel, cap, experts),
        out_shape=jax.ShapeDtypeStruct((micros, 2, blocks * shard_len), jnp.int32),
        in_specs=[vmem],
        out_specs=vmem,
        compiler_params=pltpu.CompilerParams(vmem_limit_bytes=VMEM_LIMIT),
        name="find_places",
    )(route)


def expert_kernel(
    by_block, sent_ref, dy_ref, pair_ref, wr_ref, wg_ref, wu_ref, wd_ref,
    back_ref, y_ref, x_ref, g_ref, hid_ref, dga_ref, dup_ref, dlog_ref,
    got_ref, dx_ref, stage_ref, x_send, x_recv, dx_send, dx_recv, own_sem, stage_sem,
):
    devices, experts, cap, width = sent_ref.shape
    step = pl.program_id(0)
    me = lax.axis_index("expert")
    line = lax.axis_index("hidden")
    first_wave = bits_of(devices)
    rest = [s for s in range(1, devices) if s not in first_wave]
    later_waves = [rest[i : i + 2] for i in range(0, len(rest), 2)]

    def x_copy(s):
        peer = partner_of(me, s, devices)
        return pltpu.make_async_remote_copy(
            src_ref=sent_ref.at[peer], dst_ref=got_ref.at[s], send_sem=x_send.at[s],
            recv_sem=x_recv.at[s], device_id=(peer, line), device_id_type=pl.DeviceIdType.MESH,
        )

    def dx_copy(s):
        peer = partner_of(me, s, devices)
        return pltpu.make_async_remote_copy(
            src_ref=dx_ref.at[s], dst_ref=back_ref.at[me], send_sem=dx_send.at[s],
            recv_sem=dx_recv.at[s], device_id=(peer, line), device_id_type=pl.DeviceIdType.MESH,
        )

    blocks, share = stage_ref.shape[2:4]

    def y_copies(s):
        source = partner_of(me, s, devices)
        slot = lax.rem(s, 2)
        if not by_block[1]:
            return [
                pltpu.make_async_copy(stage_ref.at[slot], y_ref.at[source], stage_sem.at[slot, 0])
            ]
        return [
            pltpu.make_async_copy(
                stage_ref.at[slot, e], y_ref.at[:, source, e], stage_sem.at[slot, e]
            )
            for e in range(experts)
        ]

    def work(s):
        source = partner_of(me, s, devices)
        slot = lax.rem(s, 2)
        for e in range(experts):
            x = got_ref[s, e]
            dy = dy_ref[:, source, e] if by_block[0] else dy_ref[source, e]
            dy = dy.reshape(cap, width).astype(F32)
            pair = pair_ref[0, source, e].astype(F32)
            margin = jnp.sum(mm_nt(x, wr_ref[...]) * pair, axis=-1, keepdims=True)
            own_gate = 1.0 / (1.0 + jnp.exp(-margin))
            other_gate = 1.0 / (1.0 + jnp.exp(margin))
            g = (own_gate * dy).astype(BF16)
            x_ref[0, e] = x
            g_ref[0, e] = g
            gate = mm_nt(x, wg_ref[e])
            up = mm_nt(x, wu_ref[e])
            square = gate * gate
            bent = jnp.tanh(GELU_C * gate * (1.0 + GELU_A * square))
            half_gate = 0.5 * gate
            gelu = half_gate * (1.0 + bent)
            slope = 0.5 * (1.0 + bent) + half_gate * (1.0 - bent * bent) * (
                GELU_C * (1.0 + 3.0 * GELU_A * square)
            )
            hid = (gelu * up).astype(BF16)
            dhid = mm_nt(g, wd_ref[e])
            dga = (dhid * (up * slope)).astype(BF16)
            dup = (dhid * gelu).astype(BF16)
            hid_ref[0, e] = hid
            dga_ref[0, e] = dga
            dup_ref[0, e] = dup
            y = mm(hid, wd_ref[e])
            dgate = jnp.sum(y * dy, axis=-1, keepdims=True)
            stage_ref[slot, e] = (y * own_gate).astype(BF16).reshape(blocks, share, width)
            dlog = (dgate * own_gate * other_gate * pair).astype(BF16)
            dlog_ref[0, e] = dlog
            dx = mm(dga, wg_ref[e]) + mm(dup, wu_ref[e]) + mm(dlog, wr_ref[...])
            dx_ref[s, e] = dx.astype(BF16)

    @pl.when(step == 0)
    def _():
        barrier = pltpu.get_barrier_semaphore()
        for s in range(1, devices):
            pl.semaphore_signal(
                barrier, inc=1, device_id=(partner_of(me, s, devices), line),
                device_id_type=pl.DeviceIdType.MESH,
            )
        pl.semaphore_wait(barrier, devices - 1)
        for s in first_wave:
            x_copy(s).start()
        own = pltpu.make_async_copy(sent_ref.at[me], got_ref.at[0], own_sem)
        own.start()
        own.wait()

    @pl.when(step > 0)
    def _():
        x_copy(step).wait_recv()

    for index, wave in enumerate(later_waves):

        @pl.when(step == 2 + index)
        def _(wave=wave):
            for s in wave:
                x_copy(s).start()

    @pl.when(step > 1)
    def _():
        for copy in y_copies(step - 2):
            copy.wait()

    work(step)
    for copy in y_copies(step):
        copy.start()

    @pl.when(step > 0)
    def _():
        dx_copy(step).start()

    @pl.when(step == devices - 1)
    def _():
        own = pltpu.make_async_copy(dx_ref.at[0], back_ref.at[me], own_sem)
        own.start()
        own.wait()
        for copy in y_copies(devices - 2) + y_copies(devices - 1):
            copy.wait()
        for s in range(1, devices):
            x_copy(s).wait_send()
            dx_copy(s).wait_send()
            dx_copy(s).wait_recv()


def expert_pass(sent, dy, pair, which, wr, wg, wu, wd, by_block, identity):
    share = dy.shape[3]
    blocks = sent.shape[2] // share
    devices, experts, cap, width = sent.shape
    hidden = wg.shape[1]
    choices = wr.shape[0]

    def whole(shape):
        return pl.BlockSpec(shape, lambda s: (0,) * len(shape), pipeline_mode=pl.Buffered(1))

    def block(cols):
        return pl.BlockSpec((1, experts, cap, cols), lambda s: (s, 0, 0, 0))

    def kept(cols):
        return jax.ShapeDtypeStruct((devices, experts, cap, cols), BF16)

    pair_spec = pl.BlockSpec(
        (1,) + pair.shape[1:], lambda s: (which, 0, 0, 0, 0), pipeline_mode=pl.Buffered(1)
    )
    y_shape = (blocks, devices, experts, share, width)
    if not by_block[1]:
        y_shape = (devices, experts, blocks, share, width)
    return pl.pallas_call(
        functools.partial(expert_kernel, by_block),
        grid=(devices,),
        out_shape=(
            kept(width), jax.ShapeDtypeStruct(y_shape, BF16), kept(width), kept(width), kept(hidden), kept(hidden),
            kept(hidden), kept(choices),
        ),
        in_specs=[
            any_space(), whole(dy.shape), pair_spec, whole(wr.shape), whole(wg.shape),
            whole(wu.shape), whole(wd.shape),
        ],
        out_specs=(
            any_space(), any_space(), block(width), block(width), block(hidden), block(hidden),
            block(hidden), block(choices),
        ),
        scratch_shapes=[
            pltpu.VMEM((devices, experts, cap, width), BF16),
            pltpu.VMEM((devices, experts, cap, width), BF16),
            pltpu.VMEM((2, experts, blocks, share, width), BF16),
            pltpu.SemaphoreType.DMA((devices,)),
            pltpu.SemaphoreType.DMA((devices,)),
            pltpu.SemaphoreType.DMA((devices,)),
            pltpu.SemaphoreType.DMA((devices,)),
            pltpu.SemaphoreType.DMA,
            pltpu.SemaphoreType.DMA((2, experts)),
        ],
        compiler_params=pltpu.CompilerParams(
            vmem_limit_bytes=VMEM_LIMIT, collective_id=identity, has_side_effects=True
        ),
        cost_estimate=pl.CostEstimate(flops=0, bytes_accessed=490000000, transcendentals=0),
        name="expert_pass",
    )(sent, dy, pair, wr, wg, wu, wd)


def weight_kernel(*refs):
    count = (len(refs) - 4) // 6
    dwr_ref, dwg_ref, dwu_ref, dwd_ref = refs[-4:]
    totals = [0.0, 0.0, 0.0, 0.0]
    for index in range(count):
        blocks = [
            ref[...].reshape(ref.shape[0] * ref.shape[2], ref.shape[3])
            for ref in refs[6 * index : 6 * index + 6]
        ]
        x, g, hid, dga, dup, dlog = blocks
        totals[0] = totals[0] + mm_tn(dlog, x)
        totals[1] = totals[1] + mm_tn(dga, x)
        totals[2] = totals[2] + mm_tn(dup, x)
        totals[3] = totals[3] + mm_tn(hid, g)
    dwr_ref[0] = totals[0]
    dwg_ref[0] = totals[1]
    dwu_ref[0] = totals[2]
    dwd_ref[0] = totals[3]


def weight_pass(kept):
    sources, experts, cap, width = kept[0][0].shape
    hidden = kept[0][2].shape[3]
    choices = kept[0][5].shape[3]
    rows = sources * cap
    block = 256 if width % 256 == 0 else width
    tokens = pl.BlockSpec((sources, 1, cap, block), lambda e, j: (0, e, 0, j))
    acts = pl.BlockSpec((sources, 1, cap, hidden), lambda e, j: (0, e, 0, 0))
    logs = pl.BlockSpec((sources, 1, cap, choices), lambda e, j: (0, e, 0, 0))
    operands = []
    for arrays in kept:
        operands.extend(arrays)
    return pl.pallas_call(
        weight_kernel,
        grid=(experts, width // block),
        out_shape=(
            jax.ShapeDtypeStruct((experts, choices, width), F32),
            jax.ShapeDtypeStruct((experts, hidden, width), F32),
            jax.ShapeDtypeStruct((experts, hidden, width), F32),
            jax.ShapeDtypeStruct((experts, hidden, width), F32),
        ),
        in_specs=[tokens, tokens, acts, acts, acts, logs] * len(kept),
        out_specs=(
            pl.BlockSpec((1, choices, block), lambda e, j: (e, 0, j)),
            pl.BlockSpec((1, hidden, block), lambda e, j: (e, 0, j)),
            pl.BlockSpec((1, hidden, block), lambda e, j: (e, 0, j)),
            pl.BlockSpec((1, hidden, block), lambda e, j: (e, 0, j)),
        ),
        compiler_params=pltpu.CompilerParams(vmem_limit_bytes=VMEM_LIMIT),
        cost_estimate=pl.CostEstimate(
            flops=6 * len(kept) * experts * rows * width * hidden,
            bytes_accessed=len(kept) * experts * rows * (4 * width + 6 * hidden)
            + 12 * experts * width * hidden,
            transcendentals=0,
        ),
        name="weight_pass",
    )(*operands)


def after(values, *others):
    return lax.optimization_barrier((values,) + others)[0]


def shards(
    x_in,
    cotangent,
    segment_ids,
    routes,
    qkv_weight,
    out_weight,
    bias_table,
    attn_gain,
    moe_gain,
    router_weight,
    gate_weight,
    up_weight,
    down_weight,
):
    micro_count, _, shard_len, width = x_in.shape
    slot_count = segment_ids.shape[2]
    head_cols = out_weight.shape[0]
    bucket_count, heads_here = bias_table.shape
    head_size = head_cols // heads_here
    expert_count = router_weight.shape[1]
    experts_here = gate_weight.shape[0]
    devices = expert_count // experts_here
    blocks = slot_count // shard_len
    members = blocks // 2
    half = slot_count // 2
    capacity = max(2, (10 * shard_len + 4 * expert_count - 1) // (4 * expert_count))
    scale = head_size ** (-0.5)
    hidden_index = lax.axis_index("hidden")
    expert_index = lax.axis_index("expert")
    part = hidden_index // members
    attn_gain_f = attn_gain.astype(F32).reshape(1, width)
    moe_gain_f = moe_gain.astype(F32).reshape(1, width)
    token_shape = (devices, experts_here, blocks * capacity, width)
    flat_shape = (devices, experts_here * blocks * capacity, width)
    place_shape = (expert_count, blocks, capacity, width)
    gate_rows = gate_weight.transpose(0, 2, 1)
    up_rows = up_weight.transpose(0, 2, 1)
    router_rows = router_weight.T

    def exchange(buffer):
        return lax.all_to_all(buffer, "expert", split_axis=0, concat_axis=0, tiled=True)

    def gather(values):
        return lax.all_gather(values, "hidden", axis=0, tiled=True)

    def scatter(values):
        return lax.psum_scatter(values, "hidden", scatter_dimension=0, tiled=True)

    states = [dict() for _ in range(micro_count)]
    own_seg = lax.dynamic_slice_in_dim(segment_ids[:, 0], hidden_index * shard_len, shard_len, 1)
    live_routes = jnp.where(own_seg[:, None, :] >= 0, routes[:, 0].transpose(0, 2, 1), -1)
    own_place = find_places(live_routes[None], expert_count, capacity)

    def spread(rows, micro, placed):
        return spread_rows(rows, micro, placed, expert_count, capacity, shard_len)

    *x_all, other_qkv, all_out, all_routes, other_table = opening(
        x_in[:, 0], qkv_weight.reshape(3 * width, head_cols), out_weight,
        live_routes, bias_table.T.astype(F32), devices, blocks, members,
    )
    x_half = [x.reshape(1, half, width) for x in x_all]
    other_qkv = other_qkv.reshape(qkv_weight.shape)
    all_out = all_out.reshape(blocks, head_cols, width)

    own_routes = lax.dynamic_index_in_dim(all_routes, expert_index, 0, keepdims=False)
    place = find_places(own_routes, expert_count, capacity)

    tables = jnp.concatenate([bias_table.T.astype(F32), other_table], axis=0)
    onehot_bucket = bucket_onehot(half, bucket_count)
    bias = position_bias(jnp.einsum("jb,hb->hj", onehot_bucket, tables, precision=PRECISE))
    seg_half = lax.dynamic_slice_in_dim(segment_ids[:, 0], part * half, half, 1)

    def gather_dy(rows):
        whole = gather(rows.reshape(1, devices * experts_here * capacity, width))
        return whole.reshape(blocks, devices, experts_here, capacity, width)

    def experts(micro, kept, *behind):
        sent = spread(kept["xn2_all"][None], 0, place[micro]).reshape(token_shape)
        kept["by_block"] = (micro > 0, micro + 1 < micro_count)
        back, kept["y"], x, g, hid, dga, dup, dlog = expert_pass(
            after(sent, *behind), kept["dy"], pairs, micro, router_rows, gate_rows, up_rows,
            down_weight, kept["by_block"], 4 + micro,
        )
        kept["weights"] = (x, g, hid, dga, dup, dlog)
        kept["back"] = back
        if micro > 0:
            back = after(back, states[micro - 1]["y_own"])
        kept["dx_back"] = back.reshape(place_shape)
        kept["dx_part"] = collect_rows(kept["dx_back"], place[micro], shard_len)
        kept["dxn2"] = scatter(kept["dx_part"])
        if kept["by_block"][1]:
            parts = after(kept["y"], kept["dx_part"]).reshape(blocks, -1, width)
            kept["y_own"] = scatter(parts).reshape(devices, -1, width)

    first, last = states
    first["dy_all"] = gather(after(cotangent[0, 0], all_out))
    pair_shape = (micro_count, devices, experts_here, blocks, capacity, expert_count)
    for micro, state in enumerate(states):
        inputs = (
            attn_gain_f, qkv_weight, other_qkv, bias, seg_half[micro : micro + 1], all_out,
            x_in, moe_gain_f, scale, members, 10 + micro, micro,
        )
        if micro == 0:
            sent = spread(cotangent[:, 0], 1, own_place[1]).reshape(devices, -1, width)
            qkv, prob, heads, h1, xn2, last["dy_here"] = attend(
                after(x_half[0], place), *inputs, sent
            )
        else:
            sent = spread(after(first["dy_all"], xn2)[None], 0, place[0]).reshape(token_shape)
            qkv, prob, heads, h1, xn2, first["dy"], pairs = attend(
                after(x_half[1], xn2), *inputs, sent, all_routes, pair_shape
            )
        state.update(qkv=qkv[0], prob=prob[0], heads=heads[0], h1=h1[0], xn2=xn2[0])
    first["dy"] = first["dy"].reshape(devices, experts_here, blocks, capacity, width)
    pairs = pairs.reshape(micro_count, devices, experts_here, blocks * capacity, expert_count)
    behind = ()
    for micro in range(micro_count):
        state = states[micro]
        state["xn2_all"] = gather(after(state["xn2"], *behind))
        behind = (state["xn2_all"],)
    for micro in range(1, micro_count):
        states[micro]["dy"] = gather_dy(after(states[micro]["dy_here"], states[0]["xn2_all"]))
    behind = ()
    for micro in range(micro_count):
        experts(micro, states[micro], *behind)
        behind = (states[micro]["dx_part"],)
    last_part = states[-1]["dx_part"]
    kept = [state["weights"] for state in states]
    kept[-1] = tuple(after(list(kept[-1]), last_part))
    dwr, dwg, dwu, dwd = weight_pass(kept)
    last["y_rows"] = exchange(after(last["y"], last_part).reshape(flat_shape)).reshape(place_shape)
    x_grad, first_rows, grads, crossed, lines, moe_gain_grad, attn_gain_grad = attend_back(
        moe_gain_f, attn_gain_f, all_out, qkv_weight, other_qkv,
        [
            (
                after(state["dxn2"], dwr), state["h1"], cotangent, x_in,
                x_half[micro][0], state["qkv"], state["prob"], state["heads"],
            )
            for micro, state in enumerate(states)
        ],
        first["y_own"], scale, devices, members,
    )
    rows = collect_rows(after(last["y_rows"], grads), place[-1], shard_len)
    mixed = scatter(rows)
    last_block = (last["h1"] + mixed.astype(F32)).astype(BF16)
    first_rows = first_rows.reshape(expert_count, 1, capacity, width)
    lines = lines.reshape(2 * heads_here, 2 * half)
    table = jnp.einsum("hj,jb->hb", lines, onehot_bucket, precision=PRECISE)
    table = table.reshape(2, heads_here * bucket_count)
    mine = jnp.arange(blocks, dtype=jnp.int32)[:, None]
    table = jnp.where(mine == hidden_index, table[0], 0.0) + jnp.where(
        mine == (hidden_index + members) % blocks, table[1], 0.0
    )
    small = jnp.concatenate(
        [
            jnp.sum(dwr, axis=0).reshape(-1),
            attn_gain_grad.reshape(-1),
            moe_gain_grad.reshape(-1),
            table.reshape(-1),
        ]
    )
    used = small.shape[0]
    small = jnp.pad(small, (0, -used % 1024)).reshape(-1, 128)
    whole, small, first_block = closing(
        grads, crossed, small, first_rows, own_place[0], first["h1"], blocks
    )
    whole = whole.reshape(4 * width, head_cols).astype(F32)
    grad_qkv = whole[: 3 * width].reshape(qkv_weight.shape)
    grad_out = whole[3 * width :].T
    small = small.reshape(-1)
    sizes = (width * expert_count, width, width)
    grad_router = small[: sizes[0]].reshape(expert_count, width).T
    grad_attn_gain = small[sizes[0] : sizes[0] + width]
    grad_moe_gain = small[sizes[0] + width : sizes[0] + 2 * width]
    table = small[sizes[0] + 2 * width : used].reshape(blocks, heads_here, bucket_count)
    grad_table = lax.dynamic_index_in_dim(table, hidden_index, 0, keepdims=False).T
    return (
        jnp.stack([first_block, last_block])[:, None],
        x_grad[:, None],
        grad_qkv,
        grad_out,
        grad_table,
        grad_attn_gain,
        grad_moe_gain,
        grad_router,
        dwg.transpose(0, 2, 1),
        dwu.transpose(0, 2, 1),
        dwd,
    )


def solution(mesh):
    return jax.shard_map(
        shards,
        mesh=mesh,
        in_specs=(
            P(None, "expert", "hidden", None),
            P(None, "expert", "hidden", None),
            P(None, "expert", None),
            P(None, "expert", "hidden", None),
            P(None, None, "hidden"),
            P("hidden", None),
            P(None, "hidden"),
            P(),
            P(),
            P(),
            P("expert", None, "hidden"),
            P("expert", None, "hidden"),
            P("expert", "hidden", None),
        ),
        out_specs=(
            P(None, "expert", "hidden", None),
            P(None, "expert", "hidden", None),
            P(None, None, "hidden"),
            P("hidden", None),
            P(None, "hidden"),
            P(),
            P(),
            P(),
            P("expert", None, "hidden"),
            P("expert", None, "hidden"),
            P("expert", "hidden", None),
        ),
        check_vma=False,
    )
```

```python
import functools

import jax
import jax.numpy as jnp
from jax import lax
from jax.experimental import pallas as pl
from jax.experimental.pallas import tpu as pltpu
from jax.sharding import PartitionSpec as P

EPSILON = 1e-06
PRECISE = lax.Precision.HIGHEST
LIMITS = (12, 16, 23, 32, 46, 64, 91)
MASKED = -1000000000.0
GELU_C = 0.7978845608028654
GELU_A = 0.044715
VMEM_LIMIT = 60 * 1024 * 1024
F32 = jnp.float32
BF16 = jnp.bfloat16


def mm(a, b):
    return lax.dot_general(a, b, (((1,), (0,)), ((), ())), preferred_element_type=F32)


def mm_nt(a, b):
    return lax.dot_general(a, b, (((1,), (1,)), ((), ())), preferred_element_type=F32)


def mm_tn(a, b):
    return lax.dot_general(a, b, (((0,), (0,)), ((), ())), preferred_element_type=F32)


def bucket_of(distance):
    magnitude = jnp.abs(distance)
    far_bucket = jnp.full(magnitude.shape, 8, jnp.int32)
    for threshold in LIMITS:
        far_bucket = far_bucket + (magnitude >= threshold).astype(jnp.int32)
    return jnp.where(magnitude < 8, magnitude, far_bucket) + 16 * (distance > 0).astype(jnp.int32)


def bucket_onehot(half, bucket_count):
    lane = jnp.arange(2 * half, dtype=jnp.int32)
    distance = jnp.where(lane < half, lane, lane - 2 * half)
    return (
        bucket_of(distance)[:, None] == jnp.arange(bucket_count, dtype=jnp.int32)[None, :]
    ).astype(F32)


TILE = 128


def bias_kernel(line_ref, out_ref):
    heads, _, length = out_ref.shape
    row = lax.broadcasted_iota(jnp.int32, (8, length), 0)
    for head in range(heads):
        line = jnp.broadcast_to(line_ref[head : head + 1, :], (8, length))
        sheet = line
        for r in range(1, 8):
            sheet = jnp.where(row == r, pltpu.roll(line, r, 1), sheet)
        while sheet.shape[0] < TILE:
            sheet = jnp.concatenate([sheet, pltpu.roll(sheet, sheet.shape[0], 1)], axis=0)
        out_ref[head] = sheet.astype(out_ref.dtype)


def position_bias(line):
    heads, length = line.shape
    vmem = pl.BlockSpec(memory_space=pltpu.VMEM)
    return pl.pallas_call(
        bias_kernel,
        out_shape=jax.ShapeDtypeStruct((heads, TILE, length), BF16),
        in_specs=[vmem],
        out_specs=vmem,
        compiler_params=pltpu.CompilerParams(vmem_limit_bytes=VMEM_LIMIT),
        name="position_bias",
    )(line)


def unit_rows(x):
    x = x.astype(F32)
    return x * lax.rsqrt(jnp.mean(x * x, axis=-1, keepdims=True) + EPSILON)


def remote(src, dst, send_sem, recv_sem, device):
    return pltpu.make_async_remote_copy(
        src_ref=src, dst_ref=dst, send_sem=send_sem, recv_sem=recv_sem,
        device_id=device, device_id_type=pl.DeviceIdType.MESH,
    )


def greet(devices):
    barrier = pltpu.get_barrier_semaphore()
    for device in devices:
        pl.semaphore_signal(
            barrier, inc=1, device_id=device, device_id_type=pl.DeviceIdType.MESH
        )
    pl.semaphore_wait(barrier, len(devices))


def bits_of(count):
    return [1 << b for b in range(count.bit_length() - 1)]


def partner_of(me, step, count):
    found = 0
    for bit in bits_of(count):
        found = found + bit * lax.rem(me // bit + step // bit, 2)
    return found


def any_space():
    return pl.BlockSpec(memory_space=pl.ANY)


def opening_kernel(
    micros, x_ref, qkv_ref, out_ref, routes_ref, table_ref, *refs,
):
    x_all, refs = refs[:micros], refs[micros:]
    (
        qkv_all, out_all, routes_all, table_all,
        x_send, x_recv, qkv_send, qkv_recv, out_send, out_recv, qkv_on_send, qkv_on_recv,
        out_on_send, out_on_recv, routes_send, routes_recv, routes_on_send, routes_on_recv,
        table_send, table_recv, own_sem,
    ) = refs
    devices, qkv_rows = qkv_all.shape[0] * 2, qkv_all.shape[2]
    blocks, out_rows = out_all.shape[0], out_all.shape[3]
    members = x_all[0].shape[0]
    me = lax.axis_index("expert")
    line = lax.axis_index("hidden")
    chip, core = me // 2, lax.rem(me, 2)
    mine = lax.rem(line, members)
    base = line - mine
    along = [lax.rem(line + s, blocks) for s in range(1, blocks)]
    across = lax.rem(line + members, blocks)
    sibling = partner_of(me, 1, devices)
    greet([(partner_of(me, s, devices), line) for s in range(1, devices)] + [(me, z) for z in along])
    own = [
        pltpu.make_async_copy(
            out_ref.at[pl.ds(me * out_rows, out_rows)], out_all.at[line, chip, core], own_sem.at[0]
        ),
        pltpu.make_async_copy(routes_ref, routes_all.at[me, line], own_sem.at[1]),
    ]
    for micro in range(micros):
        own.append(
            pltpu.make_async_copy(x_ref.at[micro], x_all[micro].at[mine], own_sem.at[2 + micro])
        )
    for copy in own:
        copy.start()
    first_qkv = remote(
        qkv_ref.at[pl.ds(me * qkv_rows, qkv_rows)], qkv_all.at[chip, core], qkv_send, qkv_recv,
        (me, across),
    )
    first_qkv.start()
    first_out, first_routes = [], []
    rest = [remote(table_ref, table_all, table_send, table_recv, (me, across))]
    for s, z in enumerate(along):
        first_out.append(
            remote(
                out_ref.at[pl.ds(me * out_rows, out_rows)], out_all.at[line, chip, core],
                out_send.at[s], out_recv.at[s], (me, z),
            )
        )
        first_routes.append(
            remote(
                routes_ref, routes_all.at[me, line], routes_send.at[s], routes_recv.at[s], (me, z)
            )
        )
    for copy in first_routes + first_out + rest:
        copy.start()
    for micro in range(micros):
        for s in range(1, members):
            peer = base + lax.rem(mine + s, members)
            copy = remote(
                x_ref.at[micro], x_all[micro].at[mine], x_send.at[micro, s], x_recv.at[micro, s],
                (me, peer),
            )
            copy.start()
            rest.append(copy)
    first_qkv.wait_recv()
    qkv_on, out_on = [], []
    for s in range(2, devices, 2):
        copy = remote(
            qkv_all.at[chip, core], qkv_all.at[chip, core], qkv_on_send.at[s], qkv_on_recv.at[s],
            (partner_of(me, s, devices), line),
        )
        copy.start()
        qkv_on.append(copy)
    own[1].wait()
    for copy in first_routes:
        copy.wait_recv()
    for s in range(1, devices):
        copy = remote(
            routes_all.at[me], routes_all.at[me], routes_on_send.at[s], routes_on_recv.at[s],
            (partner_of(me, s, devices), line),
        )
        copy.start()
        rest.append(copy)
    own[0].wait()
    for copy in first_out:
        copy.wait_recv()
    for s in range(2, devices, 2):
        copy = remote(
            out_all.at[:, chip, core], out_all.at[:, chip, core], out_on_send.at[s],
            out_on_recv.at[s], (partner_of(me, s, devices), line),
        )
        copy.start()
        out_on.append(copy)
    for copy in qkv_on:
        copy.wait_recv()
    copy = remote(
        qkv_all.at[:, core], qkv_all.at[:, core], qkv_on_send.at[1], qkv_on_recv.at[1],
        (sibling, line),
    )
    copy.start()
    rest.append(copy)
    for copy in out_on:
        copy.wait_recv()
    copy = remote(
        out_all.at[:, :, core], out_all.at[:, :, core], out_on_send.at[1], out_on_recv.at[1],
        (sibling, line),
    )
    copy.start()
    rest.append(copy)
    for copy in own[2:]:
        copy.wait()
    first_qkv.wait_send()
    for copy in first_out + first_routes + qkv_on + out_on:
        copy.wait_send()
    for copy in rest:
        copy.wait()


def opening(x, qkv, out, routes, table, devices, blocks, members):
    micros, shard_len, width = x.shape
    dma = pltpu.SemaphoreType.DMA
    pair = (devices // 2, 2)
    return pl.pallas_call(
        functools.partial(opening_kernel, micros),
        out_shape=(jax.ShapeDtypeStruct((members, shard_len, width), BF16),) * micros
        + (
            jax.ShapeDtypeStruct(pair + (qkv.shape[0] // devices, qkv.shape[1]), BF16),
            jax.ShapeDtypeStruct((blocks,) + pair + (out.shape[0] // devices, width), BF16),
            jax.ShapeDtypeStruct((devices, blocks) + routes.shape, jnp.int32),
            jax.ShapeDtypeStruct(table.shape, table.dtype),
        ),
        in_specs=[any_space()] * 5,
        out_specs=(any_space(),) * (4 + micros),
        scratch_shapes=[
            dma((micros, members)), dma((micros, members)), dma, dma, dma((blocks,)), dma((blocks,)),
            dma((devices,)), dma((devices,)), dma((devices,)), dma((devices,)), dma((blocks,)),
            dma((blocks,)), dma((devices,)), dma((devices,)), dma, dma, dma((2 + micros,)),
        ],
        compiler_params=pltpu.CompilerParams(collective_id=1, has_side_effects=True),
        cost_estimate=pl.CostEstimate(flops=0, bytes_accessed=200000000, transcendentals=0),
        name="opening",
    )(x, qkv, out, routes, table)


def unit_rows(x):
    x = x.astype(F32)
    return x * lax.rsqrt(jnp.mean(x * x, axis=-1, keepdims=True) + EPSILON)


def places(route_ref, index, cap, experts):
    shard_len = route_ref.shape[-1]
    row = lax.broadcasted_iota(jnp.int32, (shard_len, shard_len), 0)
    col = lax.broadcasted_iota(jnp.int32, (shard_len, shard_len), 1)
    earlier = jnp.where(row < col, 1.0, 0.0).astype(BF16)
    ids = lax.broadcasted_iota(jnp.int32, (experts, shard_len), 0)
    pair = [route_ref[index + (slice(k, k + 1),)] for k in range(2)]
    chosen = (ids == pair[0]) | (ids == pair[1])
    before = mm(jnp.where(chosen, 1.0, 0.0).astype(BF16), earlier)
    found = []
    for route in pair:
        position = jnp.sum(jnp.where(ids == route, before, 0.0), axis=0, keepdims=True)
        found.append(jnp.where(route >= 0, route * cap + position.astype(jnp.int32), -1))
    return pair, found


def fill_pairs(route_ref, pair_ref, source, micro, me):
    _, _, here, blocks, cap, experts = pair_ref.shape
    spots = lax.broadcasted_iota(jnp.int32, (cap, route_ref.shape[-1]), 0)
    ids = lax.broadcasted_iota(jnp.int32, (cap, experts), 1)
    for block in range(blocks):
        pair, place = places(route_ref, (source, block, micro), cap, experts)
        for e in range(here):
            expert = me * here + e
            other = jnp.full((cap, 1), -1, jnp.int32)
            for k in range(2):
                hit = spots + expert * cap == place[k]
                found = jnp.max(jnp.where(hit, pair[1 - k], -1), axis=1, keepdims=True)
                other = jnp.maximum(other, found)
            sign = jnp.where(ids == expert, 1.0, 0.0) - jnp.where(ids == other, 1.0, 0.0)
            pair_ref[micro, source, e, block] = jnp.where(other >= 0, sign, 0.0).astype(BF16)


def collect(rows_ref, place_ref):
    experts, _, cap, width = rows_ref.shape
    tokens = place_ref.shape[1]
    ids = lax.broadcasted_iota(jnp.int32, (experts * cap, tokens), 0)
    hit = (ids == place_ref[0:1, :]) | (ids == place_ref[1:2, :])
    rows = rows_ref[...].reshape(experts * cap, width)
    return mm_tn(jnp.where(hit, 1.0, 0.0).astype(BF16), rows)


def attend_kernel(
    scale, x_ref, gain_ref, own_ref, other_ref, bias_ref, seg_row_ref, seg_col_ref,
    out_ref, x_own_ref, moe_gain_ref, *refs,
):
    sent_ref, refs = refs[0], refs[1:]
    pairing = len(refs) > 14
    if pairing:
        routes_ref, pair_ref = refs[0], refs[7]
        refs = refs[1:7] + refs[8:]
    arrived_ref, ride_send, ride_recv, ride_own = refs[5], *refs[-3:]
    refs = refs[:5] + refs[6:-3]
    qkv_ref, prob_ref, heads_ref, h1_ref, xn2_ref, xn_ref, part_ref, got_ref, send_sem, recv_sem = refs
    micros, members, shard_len, both = got_ref.shape
    cols = both // 2
    heads, length = bias_ref.shape[0], bias_ref.shape[2]
    half = members * shard_len
    size = cols // heads
    micro, group = pl.program_id(0), pl.program_id(1)
    me = lax.axis_index("expert")
    line = lax.axis_index("hidden")
    mine = lax.rem(line, members)
    part = line // members
    base = line - mine

    def swap(m, s):
        peer = lax.rem(mine + s, members)
        return remote(
            part_ref.at[m, peer], got_ref.at[m, mine], send_sem.at[m, s], recv_sem.at[m, s],
            (me, base + peer),
        )

    def ride(s):
        peer = partner_of(me, s, sent_ref.shape[0])
        return remote(
            sent_ref.at[peer], arrived_ref.at[me], ride_send.at[s], ride_recv.at[s], (peer, line)
        )

    def stay():
        return pltpu.make_async_copy(sent_ref.at[me], arrived_ref.at[me], ride_own)

    @pl.when((micro == 0) & (group == 0))
    def _():
        peers = [(me, base + lax.rem(mine + s, members)) for s in range(1, members)]
        devices = sent_ref.shape[0]
        peers += [(partner_of(me, s, devices), line) for s in range(1, devices)]
        greet(peers)
        stay().start()
        for s in range(1, devices):
            ride(s).start()

    @pl.when(group == 0)
    def _():
        xn_ref[...] = (unit_rows(x_ref[0]) * gain_ref[...]).astype(BF16)
        for t in range(3):
            qkv_ref[0, 0, t] = mm(xn_ref[...], own_ref[t]).astype(BF16)

    @pl.when(group > 0)
    def _():
        for t in range(3):
            qkv_ref[0, 0, t] = mm(xn_ref[...], other_ref[t]).astype(BF16)

    seg_row = seg_row_ref[0]
    for head in range(heads):
        inner = slice(head * size, (head + 1) * size)
        keys = qkv_ref[0, 0, 1, :, inner]
        values = qkv_ref[0, 0, 2, :, inner]
        for start in range(0, half, TILE):
            rows = slice(start, start + TILE)
            scores = mm_nt(qkv_ref[0, 0, 0, rows, inner], keys) * scale
            shift = bias_ref[head, :, : half - start]
            if start:
                shift = jnp.concatenate([bias_ref[head, :, length - start :], shift], axis=1)
            scores = scores + shift.astype(F32)
            scores = jnp.where(seg_col_ref[0, rows, :] == seg_row, scores, MASKED)
            top = jnp.max(scores, axis=-1, keepdims=True)
            weights = jnp.exp(scores - top)
            inverse = 1.0 / jnp.sum(weights, axis=-1, keepdims=True)
            prob = (weights * inverse).astype(BF16)
            prob_ref[0, 0, head, :, rows] = prob.T
            heads_ref[0, rows, inner] = mm(prob, values).astype(BF16)

    for g in range(2):

        @pl.when(group == g)
        def _(g=g):
            for member in range(members):
                rows = slice(member * shard_len, (member + 1) * shard_len)
                part_ref[micro, member, :, g * cols : (g + 1) * cols] = heads_ref[0, rows, :]

    @pl.when(group == 1)
    def _():
        got_ref[micro, mine] = part_ref[micro, mine]
        for s in range(1, members):
            swap(micro, s).start()

    @pl.when((micro == micros - 1) & (group == 1))
    def _():
        for m in range(micros):
            for s in range(1, members):
                swap(m, s).wait_recv()
            h1 = x_own_ref[0, 0].astype(F32)
            for member in range(members):
                for j in range(2):
                    index = lax.rem(part + j, 2) * members + member
                    h1 = h1 + mm(got_ref[m, member, :, j * cols : (j + 1) * cols], out_ref[index])
            h1_ref[m] = h1
            xn2_ref[m] = (unit_rows(h1) * moe_gain_ref[...]).astype(BF16)
        for m in range(micros):
            for s in range(1, members):
                swap(m, s).wait_send()
        if pairing:

            @pl.loop(0, routes_ref.shape[0])
            def _(source):
                for m in range(pair_ref.shape[0]):
                    fill_pairs(routes_ref, pair_ref, source, m, me)

        stay().wait()
        for s in range(1, sent_ref.shape[0]):
            ride(s).wait()


def attend(
    x, gain, own_weight, other_weight, bias, seg, out_weight, x_own, moe_gain, scale, members, identity,
    which, rider, routes=None, pair_shape=None,
):
    micros, half, width = x.shape
    cols = own_weight.shape[2]
    heads = bias.shape[0] // 2
    shard_len = half // members
    mine = pl.BlockSpec(
        (1, 1, shard_len, width), lambda m, p: (which, 0, 0, 0), pipeline_mode=pl.Buffered(1)
    )
    riders, ride_specs = [rider], [any_space()]
    ride_out, ride_out_specs = [jax.ShapeDtypeStruct(rider.shape, BF16)], [any_space()]
    if routes is not None:
        riders.append(routes)
        ride_specs.append(pl.BlockSpec(memory_space=pltpu.VMEM))
        ride_out.append(jax.ShapeDtypeStruct(pair_shape, BF16))
        ride_out_specs.append(pl.BlockSpec(memory_space=pltpu.VMEM))
    ride_sems = [pltpu.SemaphoreType.DMA((rider.shape[0],))] * 2 + [pltpu.SemaphoreType.DMA]

    def once(shape):
        return pl.BlockSpec(shape, lambda m, p: (0,) * len(shape), pipeline_mode=pl.Buffered(1))

    return pl.pallas_call(
        functools.partial(attend_kernel, scale),
        grid=(micros, 2),
        out_shape=(
            jax.ShapeDtypeStruct((micros, 2, 3, half, cols), BF16),
            jax.ShapeDtypeStruct((micros, 2, heads, half, half), BF16),
            jax.ShapeDtypeStruct((micros, half, 2 * cols), BF16),
            jax.ShapeDtypeStruct((micros, shard_len, width), F32),
            jax.ShapeDtypeStruct((micros, shard_len, width), BF16),
        )
        + tuple(ride_out),
        in_specs=[
            pl.BlockSpec((1, half, width), lambda m, p: (m, 0, 0)),
            once((1, width)),
            once((3, width, cols)),
            once((3, width, cols)),
            pl.BlockSpec((heads,) + bias.shape[1:], lambda m, p: (p, 0, 0)),
            pl.BlockSpec((1, 1, half), lambda m, p: (m, 0, 0)),
            pl.BlockSpec((1, half, 1), lambda m, p: (m, 0, 0)),
            once(out_weight.shape),
            mine,
            once((1, width)),
        ]
        + ride_specs,
        out_specs=(
            pl.BlockSpec((1, 1, 3, half, cols), lambda m, p: (m, p, 0, 0, 0)),
            pl.BlockSpec((1, 1, heads, half, half), lambda m, p: (m, p, 0, 0, 0)),
            pl.BlockSpec((1, half, cols), lambda m, p: (m, 0, p)),
            pl.BlockSpec((micros, shard_len, width), lambda m, p: (0, 0, 0)),
            pl.BlockSpec((micros, shard_len, width), lambda m, p: (0, 0, 0)),
        )
        + tuple(ride_out_specs),
        scratch_shapes=[
            pltpu.VMEM((half, width), BF16),
            pltpu.VMEM((micros, members, shard_len, 2 * cols), BF16),
            pltpu.VMEM((micros, members, shard_len, 2 * cols), BF16),
            pltpu.SemaphoreType.DMA((micros, members)),
            pltpu.SemaphoreType.DMA((micros, members)),
        ]
        + ride_sems,
        compiler_params=pltpu.CompilerParams(
            vmem_limit_bytes=VMEM_LIMIT, collective_id=identity, has_side_effects=True
        ),
        cost_estimate=pl.CostEstimate(
            flops=micros * 2 * half * cols * (8 * width + 4 * half),
            bytes_accessed=100000000,
            transcendentals=micros * 2 * heads * half * half,
        ),
        name="attend",
    )(
        x, gain, own_weight, other_weight, bias, seg.reshape(micros, 1, half),
        seg.reshape(micros, half, 1), out_weight, x_own, moe_gain, *riders,
    )


def back_kernel(scale, micros, *refs):
    moe_gain_ref, gain_ref, out_ref, own_ref, other_ref = refs[:5]
    inputs = [refs[5 + 8 * m : 13 + 8 * m] for m in range(micros)]
    sent_ref, refs = refs[5 + 8 * micros], refs[6 + 8 * micros :]
    (
        xgrad_ref, arrived_ref, grads_ref, crossed_ref, line_ref, dmoe_ref, dgain_ref,
        far_ref, half_got, held_ref, quarter_got, moved_ref, moved_got, dh1_ref, dattn_all, dheads_part, dheads_all, dxn_part, dxn_got, total_ref, xn_ref, ds_ref,
        dproj_ref, sheet_ref, attn_send, attn_recv, heads_send, heads_recv, dxn_send, dxn_recv,
        ride_send, ride_recv, ride_own, half_sem, quarter_send, quarter_recv, moved_sem,
    ) = refs
    devices = sent_ref.shape[0]
    chips = devices // 2
    _, members, shard_len, width = dattn_all.shape
    cols = dproj_ref.shape[2]
    half = members * shard_len
    length = sheet_ref.shape[0]
    group, micro = pl.program_id(0), pl.program_id(1)
    me = lax.axis_index("expert")
    line = lax.axis_index("hidden")
    mine = lax.rem(line, members)
    part = line // members
    base = line - mine
    steps = range(1, members)

    def peer_of(s):
        return lax.rem(mine + s, members)

    def attn_copy(m, s):
        return remote(
            dattn_all.at[m, mine], dattn_all.at[m, mine], attn_send.at[m, s], attn_recv.at[m, s],
            (me, base + peer_of(s)),
        )

    def heads_copy(m, s):
        return remote(
            dheads_part.at[m, peer_of(s)], dheads_all.at[m, mine], heads_send.at[m, s],
            heads_recv.at[m, s], (me, base + peer_of(s)),
        )

    def dxn_copy(m, s):
        return remote(
            dxn_part.at[m, peer_of(s)], dxn_got.at[m, mine], dxn_send.at[m, s], dxn_recv.at[m, s],
            (me, base + peer_of(s)),
        )

    def ride(s):
        peer = partner_of(me, s, devices)
        return remote(
            sent_ref.at[peer], arrived_ref.at[me], ride_send.at[s], ride_recv.at[s], (peer, line)
        )

    def stay():
        return pltpu.make_async_copy(sent_ref.at[me], arrived_ref.at[me], ride_own)

    chip, core = me // 2, lax.rem(me, 2)
    across = lax.rem(line + members, 2 * members)

    def halves():
        return remote(
            far_ref.at[:, 1 - core], half_got, half_sem.at[0], half_sem.at[1],
            (partner_of(me, 1, devices), line),
        )

    def quarter(s):
        return remote(
            held_ref.at[partner_of(chip, s, chips)], quarter_got.at[s], quarter_send.at[s],
            quarter_recv.at[s], (partner_of(me, 2 * s, devices), line),
        )

    def cross():
        return remote(moved_ref, moved_got, moved_sem.at[0], moved_sem.at[1], (me, across))

    @pl.when((group == 0) & (micro == 0))
    def _():
        peers = [(me, base + peer_of(s)) for s in steps] + [(me, across)]
        greet(peers + [(partner_of(me, s, devices), line) for s in range(1, devices)])
        stay().start()
        for s in range(1, devices):
            ride(s).start()
        dmoe_ref[...] = jnp.zeros_like(dmoe_ref)
        dgain_ref[...] = jnp.zeros_like(dgain_ref)
        for m in range(micros):
            grad_ref, h1_ref, dy_ref = inputs[m][:3]
            grad = grad_ref[...].astype(F32)
            h1 = h1_ref[...]
            r2 = lax.rsqrt(jnp.mean(h1 * h1, axis=-1, keepdims=True) + EPSILON)
            unit = h1 * r2
            dmoe_ref[...] += jnp.sum(grad * unit, axis=0, keepdims=True)
            weighted = grad * moe_gain_ref[...]
            inner = jnp.mean(weighted * unit, axis=-1, keepdims=True)
            dh1 = dy_ref[0, 0].astype(F32) + r2 * (weighted - unit * inner)
            dh1_ref[m] = dh1
            dattn = dh1.astype(BF16)
            dattn_all[m, mine] = dattn
            for member in range(members):
                for j in range(2):
                    index = lax.rem(part + j, 2) * members + member
                    dheads = mm_nt(dattn, out_ref[index]).astype(BF16)
                    dheads_part[m, member, :, j * cols : (j + 1) * cols] = dheads
            for s in steps:
                heads_copy(m, s).start()
            dheads_all[m, mine] = dheads_part[m, mine]
        for m in range(micros):
            xn_ref[m] = (unit_rows(inputs[m][4][...]) * gain_ref[...]).astype(BF16)

    def pass_halves():
        halves().wait_recv()
        for s in range(1, chips):
            other = partner_of(chip, s, chips)
            held = far_ref[other, core].astype(F32) + half_got[other].astype(F32)
            held_ref[other] = held.astype(BF16)
            quarter(s).start()

    def pass_quarters():
        total = far_ref[chip, core].astype(F32) + half_got[chip].astype(F32)
        for s in range(1, chips):
            quarter(s).wait_recv()
            total = total + quarter_got[s].astype(F32)
        moved_ref[...] = total.astype(BF16)
        cross().start()

    def products(weight_ref):
        dxn = mm_nt(dproj_ref[0], weight_ref[0])
        for t in range(1, 3):
            dxn = dxn + mm_nt(dproj_ref[t], weight_ref[t])
        return dxn.reshape(members, shard_len, width)

    span = chips // 4
    for g in range(2):
        for m in range(micros):

            @pl.when((group == g) & (micro == m))
            def _(g=g, m=m):
                x_ref, qkv_ref, prob_ref, heads_ref = inputs[m][4:]
                heads = prob_ref.shape[1]
                size = cols // heads
                if g == 0:
                    for s in steps:
                        heads_copy(m, s).wait_recv()
                    for s in steps:
                        attn_copy(m, s).start()
                for head in range(heads):
                    inner_cols = slice(head * size, (head + 1) * size)
                    outer = (1 - g) * cols + head * size
                    outer_cols = slice(outer, outer + size)
                    values = qkv_ref[0, 2, :, inner_cols]
                    grads = dheads_all[m, :, :, outer_cols].reshape(half, size)
                    sheet_ref[...] = jnp.zeros_like(sheet_ref)
                    for start in range(0, half, TILE):
                        rows = slice(start, start + TILE)
                        prob = prob_ref[0, head, :, rows].astype(F32)
                        dprob = mm_nt(values, grads[rows])
                        inner = jnp.sum(prob * dprob, axis=0, keepdims=True)
                        dscore = (prob * (dprob - inner)).astype(BF16)
                        ds_ref[:, rows] = dscore
                        dscore = dscore.astype(F32)
                        sheet_ref[: half - start, :] += dscore[start:]
                        if start:
                            sheet_ref[length - start :, :] += dscore[:start]
                    dscores = ds_ref[...]
                    keys, queries = qkv_ref[0, 1, :, inner_cols], qkv_ref[0, 0, :, inner_cols]
                    dproj_ref[0, :, inner_cols] = (mm_tn(dscores, keys) * scale).astype(BF16)
                    dproj_ref[1, :, inner_cols] = (mm(dscores, queries) * scale).astype(BF16)
                    dproj_ref[2, :, inner_cols] = mm(prob_ref[0, head], grads).astype(BF16)
                    sheet = sheet_ref[...].T
                    while sheet.shape[0] > 8:
                        upper = sheet.shape[0] // 2
                        sheet = sheet[:upper] + pltpu.roll(sheet[upper:], length - upper, 1)
                    row = lax.broadcasted_iota(jnp.int32, (8, length), 0)
                    found = jnp.zeros((1, length), F32)
                    for r in range(8):
                        moved = pltpu.roll(sheet, length - r, 1) if r else sheet
                        found = found + jnp.sum(
                            jnp.where(row == r, moved, 0.0), axis=0, keepdims=True
                        )
                    if m:
                        found = found + line_ref[0, head : head + 1, :]
                    line_ref[0, head : head + 1, :] = found
                if g == 1 and m == 0:
                    pass_halves()
                if g == 1 and m == micros - 1:
                    pass_quarters()
                if g == 0:
                    total_ref[m] = products(other_ref)
                    for s in steps:
                        attn_copy(m, s).wait_recv()
                else:
                    total = total_ref[m] + products(own_ref)
                    total_ref[m] = total
                    dxn_part[m] = total.astype(BF16)
                    for s in steps:
                        dxn_copy(m, s).start()
                    total = total.reshape(half, width)
                    dgain_ref[...] += jnp.sum(total * unit_rows(x_ref[...]), axis=0, keepdims=True)
                for t in range(4):
                    if t < 3:
                        found = mm_tn(xn_ref[m], dproj_ref[t])
                    else:
                        found = mm_tn(dattn_all[m].reshape(half, width), heads_ref[...])
                    target = (far_ref, grads_ref)[g]
                    found = found.reshape(span, 2, width // (2 * span), cols)
                    if m:
                        found = found + target[t * span : (t + 1) * span].astype(F32)
                    target[t * span : (t + 1) * span] = found.astype(BF16)
                if g == 0 and m == micros - 1:
                    halves().start()

    @pl.when((group == 1) & (micro == micros - 1))
    def _():
        for m in range(micros):
            x_own = inputs[m][3][0, 0].astype(F32)
            r1 = lax.rsqrt(jnp.mean(x_own * x_own, axis=-1, keepdims=True) + EPSILON)
            unit = x_own * r1
            for s in steps:
                dxn_copy(m, s).wait_recv()
            dxn1 = total_ref[m, mine]
            for s in steps:
                dxn1 = dxn1 + dxn_got[m, lax.rem(mine + members - s, members)].astype(F32)
            weighted = dxn1 * gain_ref[...]
            inner = jnp.mean(weighted * unit, axis=-1, keepdims=True)
            xgrad_ref[m] = (dh1_ref[m] + r1 * (weighted - unit * inner)).astype(BF16)
        for m in range(micros):
            for s in steps:
                heads_copy(m, s).wait_send()
                attn_copy(m, s).wait_send()
                dxn_copy(m, s).wait_send()
        stay().wait()
        for s in range(1, devices):
            ride(s).wait()
        cross().wait_recv()
        crossed_ref[...] = moved_got[...]
        halves().wait_send()
        cross().wait_send()
        for s in range(1, chips):
            quarter(s).wait_send()


def attend_back(
    moe_gain, gain, out_weight, own_weight, other_weight, kept, rider, scale, pieces, members
):
    micros = len(kept)
    _, heads, half = kept[0][6].shape[:3]
    width, cols = own_weight.shape[1:]
    shard_len = half // members
    length = 2 * half
    rows = 4 * width // pieces

    def once(array):
        return pl.BlockSpec(
            array.shape, lambda p, m: (0,) * array.ndim, pipeline_mode=pl.Buffered(1)
        )

    operands = [moe_gain, gain, out_weight, own_weight, other_weight]
    in_specs = [once(array) for array in operands]
    for micro, arrays in enumerate(kept):
        operands.extend(arrays)
        grad, h1, _, _, x_half = [once(array) for array in arrays[:5]]
        mine = pl.BlockSpec(
            (1, 1, shard_len, width), lambda p, m, which=micro: (which, 0, 0, 0),
            pipeline_mode=pl.Buffered(1),
        )
        in_specs += [grad, h1, mine, mine, x_half] + [
            pl.BlockSpec((1, 3, half, cols), lambda p, m: (1 - p, 0, 0, 0)),
            pl.BlockSpec((1, heads, half, half), lambda p, m: (1 - p, 0, 0, 0)),
            pl.BlockSpec((half, cols), lambda p, m: (0, 1 - p)),
        ]
    operands.append(rider)
    in_specs.append(any_space())
    dma = pltpu.SemaphoreType.DMA((micros, members))
    ride_dma = pltpu.SemaphoreType.DMA((rider.shape[0],))
    return pl.pallas_call(
        functools.partial(back_kernel, scale, micros),
        grid=(2, micros),
        out_shape=(
            jax.ShapeDtypeStruct((micros, shard_len, width), BF16),
            jax.ShapeDtypeStruct(rider.shape, BF16),
            jax.ShapeDtypeStruct((pieces // 2, 2, rows, cols), BF16),
            jax.ShapeDtypeStruct((rows, cols), BF16),
            jax.ShapeDtypeStruct((2, heads, length), F32),
            jax.ShapeDtypeStruct((1, width), F32),
            jax.ShapeDtypeStruct((1, width), F32),
        ),
        in_specs=in_specs,
        out_specs=(
            pl.BlockSpec((micros, shard_len, width), lambda p, m: (0, 0, 0)),
            any_space(),
            pl.BlockSpec(
                (pieces // 2, 2, rows, cols), lambda p, m: (0, 0, 0, 0),
                pipeline_mode=pl.Buffered(1),
            ),
            pl.BlockSpec((rows, cols), lambda p, m: (0, 0)),
            pl.BlockSpec((1, heads, length), lambda p, m: (1 - p, 0, 0)),
            pl.BlockSpec((1, width), lambda p, m: (0, 0)),
            pl.BlockSpec((1, width), lambda p, m: (0, 0)),
        ),
        scratch_shapes=[
            pltpu.VMEM((pieces // 2, 2, rows, cols), BF16),
            pltpu.VMEM((pieces // 2, rows, cols), BF16),
            pltpu.VMEM((pieces // 2, rows, cols), BF16),
            pltpu.VMEM((pieces // 2, rows, cols), BF16),
            pltpu.VMEM((rows, cols), BF16),
            pltpu.VMEM((rows, cols), BF16),
            pltpu.VMEM((micros, shard_len, width), F32),
            pltpu.VMEM((micros, members, shard_len, width), BF16),
            pltpu.VMEM((micros, members, shard_len, 2 * cols), BF16),
            pltpu.VMEM((micros, members, shard_len, 2 * cols), BF16),
            pltpu.VMEM((micros, members, shard_len, width), BF16),
            pltpu.VMEM((micros, members, shard_len, width), BF16),
            pltpu.VMEM((micros, members, shard_len, width), F32),
            pltpu.VMEM((micros, half, width), BF16),
            pltpu.VMEM((half, half), BF16),
            pltpu.VMEM((3, half, cols), BF16),
            pltpu.VMEM((length, TILE), F32),
            dma, dma, dma, dma, dma, dma, ride_dma, ride_dma, pltpu.SemaphoreType.DMA,
            pltpu.SemaphoreType.DMA((2,)), ride_dma, ride_dma, pltpu.SemaphoreType.DMA((2,)),
        ],
        compiler_params=pltpu.CompilerParams(
            vmem_limit_bytes=VMEM_LIMIT, collective_id=6, has_side_effects=True
        ),
        cost_estimate=pl.CostEstimate(
            flops=2 * micros * half * cols * (16 * width + 8 * half),
            bytes_accessed=250000000,
            transcendentals=0,
        ),
        name="attend_back",
    )(*operands)


def closing_kernel(
    pieces_ref, crossed_ref, small_ref, rows_ref, place_ref, first_h1_ref,
    whole_ref, sum_ref, block_ref,
    half_got, held_ref, quarter_got, small_got, line_sum, line_got,
    half_sem, quarter_send, quarter_recv, small_send, small_recv, line_send, line_recv,
    on_send, on_recv,
):
    chips = pieces_ref.shape[0]
    devices = 2 * chips
    blocks = line_got.shape[0]
    me = lax.axis_index("expert")
    line = lax.axis_index("hidden")
    chip, core = me // 2, lax.rem(me, 2)
    sibling = partner_of(me, 1, devices)
    along = [lax.rem(line + s, blocks) for s in range(1, blocks)]
    steps = range(1, chips)
    greet([(partner_of(me, s, devices), line) for s in range(1, devices)] + [(me, z) for z in along])
    halves = remote(
        pieces_ref.at[:, 1 - core], half_got, half_sem.at[0], half_sem.at[1], (sibling, line)
    )
    halves.start()
    smalls = [
        remote(
            small_ref, small_got.at[me], small_send.at[s], small_recv.at[s],
            (partner_of(me, s, devices), line),
        )
        for s in range(1, devices)
    ]
    for copy in smalls:
        copy.start()
    small_got[me] = small_ref[...]

    def quarter(s):
        return remote(
            held_ref.at[partner_of(chip, s, chips)], quarter_got.at[s], quarter_send.at[s],
            quarter_recv.at[s], (partner_of(me, 2 * s, devices), line),
        )

    halves.wait_recv()
    for s in steps:
        other = partner_of(chip, s, chips)
        held = pieces_ref[other, core].astype(F32) + half_got[other].astype(F32)
        held_ref[other] = held.astype(BF16)
        quarter(s).start()
    for copy in smalls:
        copy.wait_recv()
    line_sum[...] = jnp.sum(small_got[...], axis=0)
    lines = [
        remote(line_sum, line_got.at[line], line_send.at[s], line_recv.at[s], (me, z))
        for s, z in enumerate(along)
    ]
    for copy in lines:
        copy.start()
    line_got[line] = line_sum[...]
    block_ref[...] = (first_h1_ref[...] + collect(rows_ref, place_ref)).astype(BF16)
    total = pieces_ref[chip, core].astype(F32) + half_got[chip].astype(F32)
    total = total + crossed_ref[...].astype(F32)
    for s in steps:
        quarter(s).wait_recv()
        total = total + quarter_got[s].astype(F32)
    whole_ref[chip, core] = total.astype(BF16)
    onward = [
        remote(
            whole_ref.at[chip, core], whole_ref.at[chip, core], on_send.at[s], on_recv.at[s],
            (partner_of(me, 2 * s, devices), line),
        )
        for s in steps
    ]
    for copy in onward:
        copy.start()
    for copy in onward:
        copy.wait_recv()
    last = remote(
        whole_ref.at[:, core], whole_ref.at[:, core], on_send.at[0], on_recv.at[0], (sibling, line)
    )
    last.start()
    for copy in lines:
        copy.wait_recv()
    sum_ref[...] = jnp.sum(line_got[...], axis=0)
    halves.wait_send()
    for s in steps:
        quarter(s).wait_send()
    for copy in smalls + lines + onward:
        copy.wait_send()
    last.wait()


def closing(pieces, crossed, small, rows_first, place, first_h1, blocks):
    chips, _, rows, cols = pieces.shape
    devices = 2 * chips
    vmem = pl.BlockSpec(memory_space=pltpu.VMEM)
    dma = pltpu.SemaphoreType.DMA
    return pl.pallas_call(
        closing_kernel,
        out_shape=(
            jax.ShapeDtypeStruct((chips, 2, rows, cols), BF16),
            jax.ShapeDtypeStruct(small.shape, F32),
            jax.ShapeDtypeStruct(first_h1.shape, BF16),
        ),
        in_specs=[vmem] * 6,
        out_specs=(vmem,) * 3,
        scratch_shapes=[
            pltpu.VMEM((chips, rows, cols), BF16),
            pltpu.VMEM((chips, rows, cols), BF16),
            pltpu.VMEM((chips, rows, cols), BF16),
            pltpu.VMEM((devices,) + small.shape, F32),
            pltpu.VMEM(small.shape, F32),
            pltpu.VMEM((blocks,) + small.shape, F32),
            dma((2,)), dma((chips,)), dma((chips,)), dma((devices,)), dma((devices,)),
            dma((blocks,)), dma((blocks,)), dma((chips,)), dma((chips,)),
        ],
        compiler_params=pltpu.CompilerParams(
            vmem_limit_bytes=VMEM_LIMIT, collective_id=3, has_side_effects=True
        ),
        cost_estimate=pl.CostEstimate(flops=0, bytes_accessed=160000000, transcendentals=0),
        name="closing",
    )(pieces, crossed, small, rows_first, place, first_h1)


def spread(rows, place0, place1, count):
    ids = lax.broadcasted_iota(jnp.int32, (count, rows.shape[0]), 0)
    hit = (ids == place0) | (ids == place1)
    return mm(jnp.where(hit, 1.0, 0.0).astype(BF16), rows)


def spread_kernel(rows_ref, place_ref, out_ref):
    experts, _, cap, width = out_ref.shape
    placed = spread(rows_ref[0], place_ref[0:1, :], place_ref[1:2, :], experts * cap)
    out_ref[...] = placed.astype(BF16).reshape(experts, 1, cap, width)


def spread_rows(rows, micro, place, experts, cap, shard_len):
    _, slots, width = rows.shape
    blocks = slots // shard_len
    return pl.pallas_call(
        spread_kernel,
        grid=(blocks,),
        out_shape=jax.ShapeDtypeStruct((experts, blocks, cap, width), BF16),
        in_specs=[
            pl.BlockSpec((1, shard_len, width), lambda b: (micro, b, 0)),
            pl.BlockSpec((2, shard_len), lambda b: (0, b)),
        ],
        out_specs=pl.BlockSpec((experts, 1, cap, width), lambda b: (0, b, 0, 0)),
        compiler_params=pltpu.CompilerParams(vmem_limit_bytes=VMEM_LIMIT),
        cost_estimate=pl.CostEstimate(
            flops=2 * experts * cap * slots * width,
            bytes_accessed=2 * slots * width + 2 * experts * blocks * cap * width,
            transcendentals=0,
        ),
        name="spread_rows",
    )(rows, place)


def collect_kernel(rows_ref, place_ref, out_ref):
    out_ref[...] = collect(rows_ref, place_ref).astype(BF16)


def collect_rows(rows, place, shard_len):
    experts, blocks, cap, width = rows.shape
    slots = blocks * shard_len
    return pl.pallas_call(
        collect_kernel,
        grid=(blocks,),
        out_shape=jax.ShapeDtypeStruct((slots, width), BF16),
        in_specs=[
            pl.BlockSpec((experts, 1, cap, width), lambda b: (0, b, 0, 0)),
            pl.BlockSpec((2, shard_len), lambda b: (0, b)),
        ],
        out_specs=pl.BlockSpec((shard_len, width), lambda b: (b, 0)),
        compiler_params=pltpu.CompilerParams(vmem_limit_bytes=VMEM_LIMIT),
        cost_estimate=pl.CostEstimate(
            flops=2 * experts * cap * slots * width,
            bytes_accessed=2 * slots * width + 2 * experts * blocks * cap * width,
            transcendentals=0,
        ),
        name="collect_rows",
    )(rows, place)


def place_kernel(cap, experts, route_ref, place_ref):
    blocks, micros, _, shard_len = route_ref.shape
    for block in range(blocks):
        for micro in range(micros):
            _, found = places(route_ref, (block, micro), cap, experts)
            for k in range(2):
                lanes = slice(block * shard_len, (block + 1) * shard_len)
                place_ref[micro, k : k + 1, lanes] = found[k]


def find_places(route, experts, cap):
    blocks, micros, _, shard_len = route.shape
    vmem = pl.BlockSpec(memory_space=pltpu.VMEM)
    return pl.pallas_call(
        functools.partial(place_kernel, cap, experts),
        out_shape=jax.ShapeDtypeStruct((micros, 2, blocks * shard_len), jnp.int32),
        in_specs=[vmem],
        out_specs=vmem,
        compiler_params=pltpu.CompilerParams(vmem_limit_bytes=VMEM_LIMIT),
        name="find_places",
    )(route)


def expert_kernel(
    by_block, sent_ref, dy_ref, pair_ref, wr_ref, wg_ref, wu_ref, wd_ref,
    back_ref, y_ref, x_ref, g_ref, hid_ref, dga_ref, dup_ref, dlog_ref,
    got_ref, dx_ref, stage_ref, x_send, x_recv, dx_send, dx_recv, own_sem, stage_sem,
):
    devices, experts, cap, width = sent_ref.shape
    step = pl.program_id(0)
    me = lax.axis_index("expert")
    line = lax.axis_index("hidden")
    first_wave = bits_of(devices)
    rest = [s for s in range(1, devices) if s not in first_wave]
    later_waves = [rest[i : i + 2] for i in range(0, len(rest), 2)]

    def x_copy(s):
        peer = partner_of(me, s, devices)
        return pltpu.make_async_remote_copy(
            src_ref=sent_ref.at[peer], dst_ref=got_ref.at[s], send_sem=x_send.at[s],
            recv_sem=x_recv.at[s], device_id=(peer, line), device_id_type=pl.DeviceIdType.MESH,
        )

    def dx_copy(s):
        peer = partner_of(me, s, devices)
        return pltpu.make_async_remote_copy(
            src_ref=dx_ref.at[s], dst_ref=back_ref.at[me], send_sem=dx_send.at[s],
            recv_sem=dx_recv.at[s], device_id=(peer, line), device_id_type=pl.DeviceIdType.MESH,
        )

    blocks, share = stage_ref.shape[2:4]

    def y_copies(s):
        source = partner_of(me, s, devices)
        slot = lax.rem(s, 2)
        if not by_block[1]:
            return [
                pltpu.make_async_copy(stage_ref.at[slot], y_ref.at[source], stage_sem.at[slot, 0])
            ]
        return [
            pltpu.make_async_copy(
                stage_ref.at[slot, e], y_ref.at[:, source, e], stage_sem.at[slot, e]
            )
            for e in range(experts)
        ]

    def work(s):
        source = partner_of(me, s, devices)
        slot = lax.rem(s, 2)
        for e in range(experts):
            x = got_ref[s, e]
            dy = dy_ref[:, source, e] if by_block[0] else dy_ref[source, e]
            dy = dy.reshape(cap, width).astype(F32)
            pair = pair_ref[0, source, e].astype(F32)
            margin = jnp.sum(mm_nt(x, wr_ref[...]) * pair, axis=-1, keepdims=True)
            own_gate = 1.0 / (1.0 + jnp.exp(-margin))
            other_gate = 1.0 / (1.0 + jnp.exp(margin))
            g = (own_gate * dy).astype(BF16)
            x_ref[0, e] = x
            g_ref[0, e] = g
            gate = mm_nt(x, wg_ref[e])
            up = mm_nt(x, wu_ref[e])
            square = gate * gate
            bent = jnp.tanh(GELU_C * gate * (1.0 + GELU_A * square))
            half_gate = 0.5 * gate
            gelu = half_gate * (1.0 + bent)
            slope = 0.5 * (1.0 + bent) + half_gate * (1.0 - bent * bent) * (
                GELU_C * (1.0 + 3.0 * GELU_A * square)
            )
            hid = (gelu * up).astype(BF16)
            dhid = mm_nt(g, wd_ref[e])
            dga = (dhid * (up * slope)).astype(BF16)
            dup = (dhid * gelu).astype(BF16)
            hid_ref[0, e] = hid
            dga_ref[0, e] = dga
            dup_ref[0, e] = dup
            y = mm(hid, wd_ref[e])
            dgate = jnp.sum(y * dy, axis=-1, keepdims=True)
            stage_ref[slot, e] = (y * own_gate).astype(BF16).reshape(blocks, share, width)
            dlog = (dgate * own_gate * other_gate * pair).astype(BF16)
            dlog_ref[0, e] = dlog
            dx = mm(dga, wg_ref[e]) + mm(dup, wu_ref[e]) + mm(dlog, wr_ref[...])
            dx_ref[s, e] = dx.astype(BF16)

    @pl.when(step == 0)
    def _():
        barrier = pltpu.get_barrier_semaphore()
        for s in range(1, devices):
            pl.semaphore_signal(
                barrier, inc=1, device_id=(partner_of(me, s, devices), line),
                device_id_type=pl.DeviceIdType.MESH,
            )
        pl.semaphore_wait(barrier, devices - 1)
        for s in first_wave:
            x_copy(s).start()
        own = pltpu.make_async_copy(sent_ref.at[me], got_ref.at[0], own_sem)
        own.start()
        own.wait()

    @pl.when(step > 0)
    def _():
        x_copy(step).wait_recv()

    for index, wave in enumerate(later_waves):

        @pl.when(step == 2 + index)
        def _(wave=wave):
            for s in wave:
                x_copy(s).start()

    @pl.when(step > 1)
    def _():
        for copy in y_copies(step - 2):
            copy.wait()

    work(step)
    for copy in y_copies(step):
        copy.start()

    @pl.when(step > 0)
    def _():
        dx_copy(step).start()

    @pl.when(step == devices - 1)
    def _():
        own = pltpu.make_async_copy(dx_ref.at[0], back_ref.at[me], own_sem)
        own.start()
        own.wait()
        for copy in y_copies(devices - 2) + y_copies(devices - 1):
            copy.wait()
        for s in range(1, devices):
            x_copy(s).wait_send()
            dx_copy(s).wait_send()
            dx_copy(s).wait_recv()


def expert_pass(sent, dy, pair, which, wr, wg, wu, wd, by_block, identity):
    share = dy.shape[3]
    blocks = sent.shape[2] // share
    devices, experts, cap, width = sent.shape
    hidden = wg.shape[1]
    choices = wr.shape[0]

    def whole(shape):
        return pl.BlockSpec(shape, lambda s: (0,) * len(shape), pipeline_mode=pl.Buffered(1))

    def block(cols):
        return pl.BlockSpec((1, experts, cap, cols), lambda s: (s, 0, 0, 0))

    def kept(cols):
        return jax.ShapeDtypeStruct((devices, experts, cap, cols), BF16)

    pair_spec = pl.BlockSpec(
        (1,) + pair.shape[1:], lambda s: (which, 0, 0, 0, 0), pipeline_mode=pl.Buffered(1)
    )
    y_shape = (blocks, devices, experts, share, width)
    if not by_block[1]:
        y_shape = (devices, experts, blocks, share, width)
    return pl.pallas_call(
        functools.partial(expert_kernel, by_block),
        grid=(devices,),
        out_shape=(
            kept(width), jax.ShapeDtypeStruct(y_shape, BF16), kept(width), kept(width), kept(hidden), kept(hidden),
            kept(hidden), kept(choices),
        ),
        in_specs=[
            any_space(), whole(dy.shape), pair_spec, whole(wr.shape), whole(wg.shape),
            whole(wu.shape), whole(wd.shape),
        ],
        out_specs=(
            any_space(), any_space(), block(width), block(width), block(hidden), block(hidden),
            block(hidden), block(choices),
        ),
        scratch_shapes=[
            pltpu.VMEM((devices, experts, cap, width), BF16),
            pltpu.VMEM((devices, experts, cap, width), BF16),
            pltpu.VMEM((2, experts, blocks, share, width), BF16),
            pltpu.SemaphoreType.DMA((devices,)),
            pltpu.SemaphoreType.DMA((devices,)),
            pltpu.SemaphoreType.DMA((devices,)),
            pltpu.SemaphoreType.DMA((devices,)),
            pltpu.SemaphoreType.DMA,
            pltpu.SemaphoreType.DMA((2, experts)),
        ],
        compiler_params=pltpu.CompilerParams(
            vmem_limit_bytes=VMEM_LIMIT, collective_id=identity, has_side_effects=True
        ),
        cost_estimate=pl.CostEstimate(flops=0, bytes_accessed=490000000, transcendentals=0),
        name="expert_pass",
    )(sent, dy, pair, wr, wg, wu, wd)


def weight_kernel(*refs):
    count = (len(refs) - 4) // 6
    dwr_ref, dwg_ref, dwu_ref, dwd_ref = refs[-4:]
    totals = [0.0, 0.0, 0.0, 0.0]
    for index in range(count):
        blocks = [
            ref[...].reshape(ref.shape[0] * ref.shape[2], ref.shape[3])
            for ref in refs[6 * index : 6 * index + 6]
        ]
        x, g, hid, dga, dup, dlog = blocks
        totals[0] = totals[0] + mm_tn(dlog, x)
        totals[1] = totals[1] + mm_tn(dga, x)
        totals[2] = totals[2] + mm_tn(dup, x)
        totals[3] = totals[3] + mm_tn(hid, g)
    dwr_ref[0] = totals[0]
    dwg_ref[0] = totals[1]
    dwu_ref[0] = totals[2]
    dwd_ref[0] = totals[3]


def weight_pass(kept):
    sources, experts, cap, width = kept[0][0].shape
    hidden = kept[0][2].shape[3]
    choices = kept[0][5].shape[3]
    rows = sources * cap
    block = 256 if width % 256 == 0 else width
    tokens = pl.BlockSpec((sources, 1, cap, block), lambda e, j: (0, e, 0, j))
    acts = pl.BlockSpec((sources, 1, cap, hidden), lambda e, j: (0, e, 0, 0))
    logs = pl.BlockSpec((sources, 1, cap, choices), lambda e, j: (0, e, 0, 0))
    operands = []
    for arrays in kept:
        operands.extend(arrays)
    return pl.pallas_call(
        weight_kernel,
        grid=(experts, width // block),
        out_shape=(
            jax.ShapeDtypeStruct((experts, choices, width), F32),
            jax.ShapeDtypeStruct((experts, hidden, width), F32),
            jax.ShapeDtypeStruct((experts, hidden, width), F32),
            jax.ShapeDtypeStruct((experts, hidden, width), F32),
        ),
        in_specs=[tokens, tokens, acts, acts, acts, logs] * len(kept),
        out_specs=(
            pl.BlockSpec((1, choices, block), lambda e, j: (e, 0, j)),
            pl.BlockSpec((1, hidden, block), lambda e, j: (e, 0, j)),
            pl.BlockSpec((1, hidden, block), lambda e, j: (e, 0, j)),
            pl.BlockSpec((1, hidden, block), lambda e, j: (e, 0, j)),
        ),
        compiler_params=pltpu.CompilerParams(vmem_limit_bytes=VMEM_LIMIT),
        cost_estimate=pl.CostEstimate(
            flops=6 * len(kept) * experts * rows * width * hidden,
            bytes_accessed=len(kept) * experts * rows * (4 * width + 6 * hidden)
            + 12 * experts * width * hidden,
            transcendentals=0,
        ),
        name="weight_pass",
    )(*operands)


def after(values, *others):
    return lax.optimization_barrier((values,) + others)[0]


def shards(
    x_in,
    cotangent,
    segment_ids,
    routes,
    qkv_weight,
    out_weight,
    bias_table,
    attn_gain,
    moe_gain,
    router_weight,
    gate_weight,
    up_weight,
    down_weight,
):
    micro_count, _, shard_len, width = x_in.shape
    slot_count = segment_ids.shape[2]
    head_cols = out_weight.shape[0]
    bucket_count, heads_here = bias_table.shape
    head_size = head_cols // heads_here
    expert_count = router_weight.shape[1]
    experts_here = gate_weight.shape[0]
    devices = expert_count // experts_here
    blocks = slot_count // shard_len
    members = blocks // 2
    half = slot_count // 2
    capacity = max(2, (10 * shard_len + 4 * expert_count - 1) // (4 * expert_count))
    scale = head_size ** (-0.5)
    hidden_index = lax.axis_index("hidden")
    expert_index = lax.axis_index("expert")
    part = hidden_index // members
    attn_gain_f = attn_gain.astype(F32).reshape(1, width)
    moe_gain_f = moe_gain.astype(F32).reshape(1, width)
    token_shape = (devices, experts_here, blocks * capacity, width)
    flat_shape = (devices, experts_here * blocks * capacity, width)
    place_shape = (expert_count, blocks, capacity, width)
    gate_rows = gate_weight.transpose(0, 2, 1)
    up_rows = up_weight.transpose(0, 2, 1)
    router_rows = router_weight.T

    def exchange(buffer):
        return lax.all_to_all(buffer, "expert", split_axis=0, concat_axis=0, tiled=True)

    def gather(values):
        return lax.all_gather(values, "hidden", axis=0, tiled=True)

    def scatter(values):
        return lax.psum_scatter(values, "hidden", scatter_dimension=0, tiled=True)

    states = [dict() for _ in range(micro_count)]
    own_seg = lax.dynamic_slice_in_dim(segment_ids[:, 0], hidden_index * shard_len, shard_len, 1)
    live_routes = jnp.where(own_seg[:, None, :] >= 0, routes[:, 0].transpose(0, 2, 1), -1)
    own_place = find_places(live_routes[None], expert_count, capacity)

    def spread(rows, micro, placed):
        return spread_rows(rows, micro, placed, expert_count, capacity, shard_len)

    *x_all, other_qkv, all_out, all_routes, other_table = opening(
        x_in[:, 0], qkv_weight.reshape(3 * width, head_cols), out_weight,
        live_routes, bias_table.T.astype(F32), devices, blocks, members,
    )
    x_half = [x.reshape(1, half, width) for x in x_all]
    other_qkv = other_qkv.reshape(qkv_weight.shape)
    all_out = all_out.reshape(blocks, head_cols, width)

    own_routes = lax.dynamic_index_in_dim(all_routes, expert_index, 0, keepdims=False)
    place = find_places(own_routes, expert_count, capacity)

    tables = jnp.concatenate([bias_table.T.astype(F32), other_table], axis=0)
    onehot_bucket = bucket_onehot(half, bucket_count)
    bias = position_bias(jnp.einsum("jb,hb->hj", onehot_bucket, tables, precision=PRECISE))
    seg_half = lax.dynamic_slice_in_dim(segment_ids[:, 0], part * half, half, 1)

    def gather_dy(rows):
        whole = gather(rows.reshape(1, devices * experts_here * capacity, width))
        return whole.reshape(blocks, devices, experts_here, capacity, width)

    def experts(micro, kept, *behind):
        sent = spread(kept["xn2_all"][None], 0, place[micro]).reshape(token_shape)
        kept["by_block"] = (micro > 0, micro + 1 < micro_count)
        back, kept["y"], x, g, hid, dga, dup, dlog = expert_pass(
            after(sent, *behind), kept["dy"], pairs, micro, router_rows, gate_rows, up_rows,
            down_weight, kept["by_block"], 4 + micro,
        )
        kept["weights"] = (x, g, hid, dga, dup, dlog)
        kept["back"] = back
        if micro > 0:
            back = after(back, states[micro - 1]["y_own"])
        kept["dx_back"] = back.reshape(place_shape)
        kept["dx_part"] = collect_rows(kept["dx_back"], place[micro], shard_len)
        kept["dxn2"] = scatter(kept["dx_part"])
        if kept["by_block"][1]:
            parts = after(kept["y"], kept["dx_part"]).reshape(blocks, -1, width)
            kept["y_own"] = scatter(parts).reshape(devices, -1, width)

    first, last = states
    first["dy_all"] = gather(after(cotangent[0, 0], all_out))
    pair_shape = (micro_count, devices, experts_here, blocks, capacity, expert_count)
    for micro, state in enumerate(states):
        inputs = (
            attn_gain_f, qkv_weight, other_qkv, bias, seg_half[micro : micro + 1], all_out,
            x_in, moe_gain_f, scale, members, 10 + micro, micro,
        )
        if micro == 0:
            sent = spread(cotangent[:, 0], 1, own_place[1]).reshape(devices, -1, width)
            qkv, prob, heads, h1, xn2, last["dy_here"] = attend(
                after(x_half[0], place), *inputs, sent
            )
        else:
            sent = spread(after(first["dy_all"], xn2)[None], 0, place[0]).reshape(token_shape)
            qkv, prob, heads, h1, xn2, first["dy"], pairs = attend(
                after(x_half[1], xn2), *inputs, sent, all_routes, pair_shape
            )
        state.update(qkv=qkv[0], prob=prob[0], heads=heads[0], h1=h1[0], xn2=xn2[0])
    first["dy"] = first["dy"].reshape(devices, experts_here, blocks, capacity, width)
    pairs = pairs.reshape(micro_count, devices, experts_here, blocks * capacity, expert_count)
    behind = ()
    for micro in range(micro_count):
        state = states[micro]
        state["xn2_all"] = gather(after(state["xn2"], *behind))
        behind = (state["xn2_all"],)
    for micro in range(1, micro_count):
        states[micro]["dy"] = gather_dy(after(states[micro]["dy_here"], states[0]["xn2_all"]))
    behind = ()
    for micro in range(micro_count):
        experts(micro, states[micro], *behind)
        behind = (states[micro]["dx_part"],)
    last_part = states[-1]["dx_part"]
    kept = [state["weights"] for state in states]
    kept[-1] = tuple(after(list(kept[-1]), last_part))
    dwr, dwg, dwu, dwd = weight_pass(kept)
    last["y_rows"] = exchange(after(last["y"], last_part).reshape(flat_shape)).reshape(place_shape)
    x_grad, first_rows, grads, crossed, lines, moe_gain_grad, attn_gain_grad = attend_back(
        moe_gain_f, attn_gain_f, all_out, qkv_weight, other_qkv,
        [
            (
                after(state["dxn2"], dwr), state["h1"], cotangent, x_in,
                x_half[micro][0], state["qkv"], state["prob"], state["heads"],
            )
            for micro, state in enumerate(states)
        ],
        first["y_own"], scale, devices, members,
    )
    rows = collect_rows(after(last["y_rows"], grads), place[-1], shard_len)
    mixed = scatter(rows)
    last_block = (last["h1"] + mixed.astype(F32)).astype(BF16)
    first_rows = first_rows.reshape(expert_count, 1, capacity, width)
    lines = lines.reshape(2 * heads_here, 2 * half)
    table = jnp.einsum("hj,jb->hb", lines, onehot_bucket, precision=PRECISE)
    table = table.reshape(2, heads_here * bucket_count)
    mine = jnp.arange(blocks, dtype=jnp.int32)[:, None]
    table = jnp.where(mine == hidden_index, table[0], 0.0) + jnp.where(
        mine == (hidden_index + members) % blocks, table[1], 0.0
    )
    small = jnp.concatenate(
        [
            jnp.sum(dwr, axis=0).reshape(-1),
            attn_gain_grad.reshape(-1),
            moe_gain_grad.reshape(-1),
            table.reshape(-1),
        ]
    )
    used = small.shape[0]
    small = jnp.pad(small, (0, -used % 1024)).reshape(-1, 128)
    whole, small, first_block = closing(
        grads, crossed, small, first_rows, own_place[0], first["h1"], blocks
    )
    whole = whole.reshape(4 * width, head_cols).astype(F32)
    grad_qkv = whole[: 3 * width].reshape(qkv_weight.shape)
    grad_out = whole[3 * width :].T
    small = small.reshape(-1)
    sizes = (width * expert_count, width, width)
    grad_router = small[: sizes[0]].reshape(expert_count, width).T
    grad_attn_gain = small[sizes[0] : sizes[0] + width]
    grad_moe_gain = small[sizes[0] + width : sizes[0] + 2 * width]
    table = small[sizes[0] + 2 * width : used].reshape(blocks, heads_here, bucket_count)
    grad_table = lax.dynamic_index_in_dim(table, hidden_index, 0, keepdims=False).T
    return (
        jnp.stack([first_block, last_block])[:, None],
        x_grad[:, None],
        grad_qkv,
        grad_out,
        grad_table,
        grad_attn_gain,
        grad_moe_gain,
        grad_router,
        dwg.transpose(0, 2, 1),
        dwu.transpose(0, 2, 1),
        dwd,
    )


def solution(mesh):
    return jax.shard_map(
        shards,
        mesh=mesh,
        in_specs=(
            P(None, "expert", "hidden", None),
            P(None, "expert", "hidden", None),
            P(None, "expert", None),
            P(None, "expert", "hidden", None),
            P(None, None, "hidden"),
            P("hidden", None),
            P(None, "hidden"),
            P(),
            P(),
            P(),
            P("expert", None, "hidden"),
            P("expert", None, "hidden"),
            P("expert", "hidden", None),
        ),
        out_specs=(
            P(None, "expert", "hidden", None),
            P(None, "expert", "hidden", None),
            P(None, None, "hidden"),
            P("hidden", None),
            P(None, "hidden"),
            P(),
            P(),
            P(),
            P("expert", None, "hidden"),
            P("expert", None, "hidden"),
            P("expert", "hidden", None),
        ),
        check_vma=False,
    )
```
